32 devices in a mesh: blk: 8 (over z, x), head: 4 (over y, core).
Axes of the slice: x: 2, y: 2, z: 4, core: 2. Of those that a mesh axis runs over, the one named last changes fastest.
Arguments:
- tokens: bfloat16 [16384, 1536], P(('blk', 'head')), may hold values from -6 to 6
- segment: int32 [16384], P('blk'), may hold values from 0 to 15, never falling along the last dimension, each value on 1 to 2000 neighbouring positions
- norm1_gain: float32 [1536], P(('blk', 'head')), may hold values from 0.5 to 1.5
- w_query: float32 [1536, 1536], P(('blk', 'head')), may hold values from -0.15625 to 0.15625
- w_key: float32 [1536, 1536], P(('blk', 'head')), may hold values from -0.15625 to 0.15625
- w_value: float32 [1536, 1536], P(('blk', 'head')), may hold values from -0.15625 to 0.15625
- w_gate_out: float32 [1536, 1536], P(('blk', 'head')), may hold values from -0.15625 to 0.15625
- w_forget: float32 [1536, 24], P(('blk', 'head')), may hold values from -0.15625 to 0.15625
- forget_bias: float32 [24], replicated, may hold values from 3 to 10
- w_output: float32 [1536, 1536], P(('blk', 'head')), may hold values from -1.75 to 1.75
- norm2_gain: float32 [1536], P(('blk', 'head')), may hold values from 0.5 to 1.5
- w_gate: float32 [1536, 4096], P(('blk', 'head')), may hold values from -0.15625 to 0.15625
- w_up: float32 [1536, 4096], P(('blk', 'head')), may hold values from -0.15625 to 0.15625
- w_down: float32 [1536, 4096], P(('blk', 'head')), may hold values from -0.09375 to 0.09375
- cotangent: bfloat16 [16384, 1536], P(('blk', 'head')), may hold values from -6 to 6
Outputs:
- tokens_out: bfloat16 [16384, 1536], P(('blk', 'head'))
- tokens_grad: float32 [16384, 1536], P(('blk', 'head'))
- norm1_gain_grad: float32 [1536], P(('blk', 'head'))
- w_query_grad: float32 [1536, 1536], P(('blk', 'head'))
- w_key_grad: float32 [1536, 1536], P(('blk', 'head'))
- w_value_grad: float32 [1536, 1536], P(('blk', 'head'))
- w_gate_out_grad: float32 [1536, 1536], P(('blk', 'head'))
- w_forget_grad: float32 [1536, 24], P(('blk', 'head'))
- forget_bias_grad: float32 [24], replicated
- w_output_grad: float32 [1536, 1536], P(('blk', 'head'))
- norm2_gain_grad: float32 [1536], P(('blk', 'head'))
- w_gate_grad: float32 [1536, 4096], P(('blk', 'head'))
- w_up_grad: float32 [1536, 4096], P(('blk', 'head'))
- w_down_grad: float32 [1536, 4096], P(('blk', 'head'))
The draws below stay inside these ranges and needn't reach their ends.
Inputs may be any that keep to these rules, and one draw needn't show every extreme that they name: `segment`: segment numbers never fall along the tokens and every number occurs; a document has 1 to 2000 tokens and one has exactly 2000.
All inputs are finite; a program needn't handle non-finite values.
Results may differ from the reference program's by a relative error of at most 0.014.
The reference program's roundings to bfloat16 on the way count: a program that leaves them out, or rounds other values in their place, can miss the bound.
Values may be sent and summed in bfloat16 or wider, within the bound.
A program may use at most 384 MiB of HBM per device.

```python
import math
import jax
import jax.numpy as jnp
import numpy as np
from jax import lax

D = 1536
HEADS = 24
HEAD_DIM = 64
FF = 4096
TOK_DEV = 512
MAXDOC = 2000
TOKENS = 16384
DOCS = 16
N_HEAD = 4


def raised(drawn, rng, source, target, parts, factor):
    def block_of(axis_at):
        return (jnp.arange(drawn.shape[axis_at]) // (drawn.shape[axis_at] // parts)).reshape((-1,) + (1,) * (drawn.ndim - 1 - axis_at))

    one_side = jax.random.permutation(rng, parts)[block_of(target)]
    second = (block_of(target) + parts // 2) % parts
    return jnp.where((block_of(source) == one_side) | (block_of(source) == second), factor * drawn, drawn)


def shard_levels(own_key, shape, pieces, least, top_value):
    loudness, own = 1.0, jax.random.fold_in(own_key, 6)
    for position, blocks in pieces:
        steps = jnp.exp(jax.random.uniform(jax.random.fold_in(own, position), (blocks,), jnp.float32, least / len(pieces), top_value / len(pieces)))
        loudness = loudness * jnp.repeat(steps, shape[position] // blocks).reshape([-1 if axis == position else 1 for axis in range(len(shape))])
    return loudness


def split_up(number_of, total, reach, skew):
    weights = [(1 << 20) // math.isqrt(grade ** skew) + 1 for grade in range(2, number_of + 1)]
    surplus, holding = total - reach - (number_of - 1), [1] * (number_of - 1)
    while surplus > 0:
        candidates = [i for i in range(number_of - 1) if holding[i] < reach]
        whole, remaining = sum([weights[i] for i in candidates]), surplus
        for i in candidates:
            more = min(reach - holding[i], max(1, remaining * weights[i] // whole), surplus)
            holding[i] = holding[i] + more
            surplus = surplus - more
    return np.array([reach] + holding)


def ragged_sizes(rng, amount, total, reach, slope):
    if amount == 2:
        one = jax.random.randint(rng, (), max(1, total - reach), min(reach, total - 1) + 1)
        return jnp.stack([one, total - one])
    sizes = jnp.asarray(split_up(amount, total, reach, slope), jnp.int32)
    pairs = (amount - 1) // 2
    donor, taker = sizes[1:1 + 2 * pairs:2], sizes[2:2 + 2 * pairs:2]
    margin = jnp.minimum(donor - 1, reach - taker)
    moved = jax.random.randint(jax.random.fold_in(rng, 1), (pairs,), 0, 1 << 20) % (margin + 1)
    sizes = sizes.at[1:1 + 2 * pairs:2].set(donor - moved).at[2:2 + 2 * pairs:2].set(taker + moved)
    return sizes[jax.random.permutation(jax.random.fold_in(rng, 2), amount)]


def bell_draw(stream_key, shape, scale, bound, cuts=(), kind=jnp.bfloat16):
    values = scale * jax.random.normal(stream_key, shape, jnp.float32)
    if cuts:
        values = values * shard_levels(stream_key, shape, cuts, -0.22, 0.18)
    return jnp.clip(values, -bound, bound).astype(kind)


def gaussian_with(stream_key, shape, deviation, most, pieces, heavy, kind=jnp.bfloat16):
    entries = deviation * jax.random.normal(stream_key, shape, jnp.float32)
    if pieces:
        entries = entries * shard_levels(stream_key, shape, pieces, -0.22, 0.18)
    return jnp.clip(raised(entries, jax.random.fold_in(stream_key, 3), *heavy), -most, most).astype(kind)


def setup_inputs(seed: int = 0) -> dict:
    key_list = jax.random.split(jax.random.key(seed), 16)
    return {
        "tokens": gaussian_with(key_list[0], (TOKENS, D), 1.0, 6.0, ((0, 32),), (0, 1, 32, 2.75)),
        "segment": jnp.searchsorted(jnp.cumsum(ragged_sizes(key_list[1], DOCS, TOKENS, MAXDOC, 0)), jnp.arange(TOKENS), side="right").astype(jnp.int32),
        "norm1_gain": jnp.clip(1.0 + 0.1 * jax.random.normal(key_list[2], (D,), jnp.float32), 0.5, 1.5),
        "w_query": bell_draw(key_list[3], (D, D), D ** -0.5, 0.15625, ((0, 32),), jnp.float32),
        "w_key": bell_draw(key_list[4], (D, D), D ** -0.5, 0.15625, ((0, 32),), jnp.float32),
        "w_value": bell_draw(key_list[5], (D, D), D ** -0.5, 0.15625, ((0, 32),), jnp.float32),
        "w_gate_out": bell_draw(key_list[6], (D, D), D ** -0.5, 0.15625, ((0, 32),), jnp.float32),
        "w_forget": bell_draw(key_list[7], (D, HEADS), D ** -0.5, 0.15625, ((0, 32),), jnp.float32),
        "forget_bias": jnp.clip(jax.random.uniform(key_list[8], (HEADS,), jnp.float32, 3.0, 10.0), 3.0, 10.0),
        "w_output": bell_draw(key_list[9], (D, D), (max(D // 128, 1)) ** -0.5, 1.75, ((0, 32),), jnp.float32),
        "norm2_gain": jnp.clip(1.0 + 0.1 * jax.random.normal(key_list[10], (D,), jnp.float32), 0.5, 1.5),
        "w_gate": bell_draw(key_list[11], (D, FF), D ** -0.5, 0.15625, ((0, 32),), jnp.float32),
        "w_up": bell_draw(key_list[12], (D, FF), D ** -0.5, 0.15625, ((0, 32),), jnp.float32),
        "w_down": bell_draw(key_list[13], (D, FF), FF ** -0.5, 0.09375, ((0, 32),), jnp.float32),
        "cotangent": gaussian_with(key_list[14], (TOKENS, D), 1.0, 6.0, ((0, 32),), (0, 1, 32, 2.75)),
    }


epsilon = 1e-06
highest = lax.Precision.HIGHEST

@jax.custom_vjp
def low(v):
    return lax.optimization_barrier(v.astype(jnp.bfloat16)).astype(jnp.float32)

@jax.custom_vjp
def low_back(v):
    return v

def low_keep(v):
    return (low(v), None)

def low_pass(kept, grad):
    return (grad,)

def back_keep(v):
    return (v, None)

def back_low(kept, grad):
    return (low(grad),)
low.defvjp(low_keep, low_pass)
low_back.defvjp(back_keep, back_low)

def highest_dot(operand, weight):
    return jnp.dot(operand, weight, precision=highest)

def normalize(hidden):
    return hidden * lax.rsqrt(lax.optimization_barrier(jnp.mean(hidden * hidden, axis=-1, keepdims=True)) + epsilon)

def attention(query, keys, values, logf, segment):
    total_rows = query.shape[0]
    block_rows = TOK_DEV * N_HEAD
    query_rows = min(512, block_rows)
    key_rows = block_rows + query_rows
    block_count = total_rows // query_rows
    scaling = HEAD_DIM ** (-0.5)
    padding = jnp.zeros((block_rows, HEADS, HEAD_DIM), jnp.float32)
    keys_padded = jnp.concatenate([padding, keys], axis=0)
    values_padded = jnp.concatenate([padding, values], axis=0)
    logf_padded = jnp.concatenate([jnp.zeros((block_rows, HEADS), jnp.float32), logf], axis=0)
    segment_padded = jnp.concatenate([jnp.full((block_rows,), -1, jnp.int32), segment.astype(jnp.int32)], axis=0)
    query_place = lax.broadcasted_iota(jnp.int32, (query_rows, key_rows), 0)
    key_place = lax.broadcasted_iota(jnp.int32, (query_rows, key_rows), 1)

    def one_block(number):
        offset = (number * query_rows).astype(jnp.int32)
        query_block = lax.dynamic_slice_in_dim(query, offset, query_rows, 0)
        key_window = lax.dynamic_slice_in_dim(keys_padded, offset, key_rows, 0)
        value_window = lax.dynamic_slice_in_dim(values_padded, offset, key_rows, 0)
        logf_window = lax.dynamic_slice_in_dim(logf_padded, offset, key_rows, 0)
        segment_query = lax.dynamic_slice_in_dim(segment.astype(jnp.int32), offset, query_rows, 0)
        segment_window = lax.dynamic_slice_in_dim(segment_padded, offset, key_rows, 0)
        decay_sums = jnp.cumsum(logf_window, axis=0)
        decays = decay_sums[block_rows:].T[:, :, None] - decay_sums.T[:, None, :]
        logits = low_back(jnp.einsum('qhd,khd->hqk', query_block, key_window, precision=highest) * scaling)
        allowed = (segment_query[:, None] == segment_window[None, :]) & (key_place <= query_place + block_rows)
        scores = jnp.where(allowed[None], logits + decays, -jnp.inf)
        probabilities = jax.nn.softmax(scores, axis=-1)
        return jnp.einsum('hqk,khd->qhd', low(probabilities), value_window, precision=highest)
    blocks = lax.map(jax.checkpoint(one_block), jnp.arange(block_count, dtype=jnp.int32))
    return blocks.reshape(total_rows, HEADS, HEAD_DIM)

def forward(inputs, first_gain, query_weight, key_weight, value_weight, output_gate_weight, forget_weight, forget_bias, output_weight, second_gain, gate_weight, up_weight, down_weight, segment):
    total_rows = inputs.shape[0]
    input1 = low(normalize(inputs) * low(first_gain))
    query = low_back(low(highest_dot(input1, low(query_weight))))
    keys = low_back(low(highest_dot(input1, low(key_weight))))
    values = low_back(low(highest_dot(input1, low(value_weight))))
    gate_pre = low_back(highest_dot(input1, low(output_gate_weight)))
    forget = low_back(low(highest_dot(input1, low(forget_weight)) + forget_bias))
    logf = jax.nn.log_sigmoid(forget)
    heads_out = attention(query.reshape(total_rows, HEADS, HEAD_DIM), keys.reshape(total_rows, HEADS, HEAD_DIM), values.reshape(total_rows, HEADS, HEAD_DIM), logf, segment)
    attended = low_back(low(heads_out.reshape(total_rows, D)))
    gated = low(jax.nn.sigmoid(gate_pre) * attended)
    middle = inputs + low_back(highest_dot(gated, low(output_weight).T))
    input2 = low(normalize(middle) * low(second_gain))
    gate_act = low_back(highest_dot(input2, low(gate_weight)))
    up_act = low_back(highest_dot(input2, low(up_weight)))
    hidden = low(jax.nn.silu(gate_act) * up_act)
    return middle + low_back(highest_dot(hidden, low(down_weight).T))

def reference(tokens, segment, norm1_gain, w_query, w_key, w_value, w_gate_out, w_forget, forget_bias, w_output, norm2_gain, w_gate, w_up, w_down, cotangent):

    def run(inputs, first_gain, query_weight, key_weight, value_weight, output_gate_weight, forget_weight, bias_vector, output_weight, second_gain, gate_weight, up_weight, down_weight):
        return forward(inputs, first_gain, query_weight, key_weight, value_weight, output_gate_weight, forget_weight, bias_vector, output_weight, second_gain, gate_weight, up_weight, down_weight, segment)
    result, pullback = jax.vjp(run, tokens.astype(jnp.float32), norm1_gain, w_query, w_key, w_value, w_gate_out, w_forget, forget_bias, w_output, norm2_gain, w_gate, w_up, w_down)
    grads = pullback(cotangent.astype(jnp.float32))
    return (result.astype(jnp.bfloat16), grads[0], grads[1], grads[2], grads[3], grads[4], grads[5], grads[6], grads[7], grads[8], grads[9], grads[10], grads[11], grads[12])
```

```python
import functools

import jax
import jax.numpy as jnp
from jax import lax
from jax.experimental import pallas as pl
from jax.experimental.pallas import tpu as pltpu
from jax.sharding import PartitionSpec as P

epsilon = 1e-06
LANES = 128
Q_TILE = 512
K_TILE = 256
FAR = -1e30
NT = (((1,), (1,)), ((), ()))
NN = (((1,), (0,)), ((), ()))
bf16 = jnp.bfloat16
f32 = jnp.float32


def dot(a, b, dims=NN, **kw):
    return lax.dot_general(a, b, dims, preferred_element_type=f32, **kw)


def passed_along(array, axis, by):
    peers = lax.axis_size(axis)
    pairs = [(i, i + by) for i in range(peers) if 0 <= i + by < peers]
    return lax.ppermute(array, axis, pairs)


def split3(value):
    high = value.astype(bf16)
    rest = value - high.astype(f32)
    mid = rest.astype(bf16)
    low = (rest - mid.astype(f32)).astype(bf16)
    return high, mid, low


def running(value_of, steps, rows, upper):
    place = lax.broadcasted_iota(jnp.int32, (rows, rows), 0)
    other = lax.broadcasted_iota(jnp.int32, (rows, rows), 1)
    tri = jnp.where((other >= place) if upper else (other <= place), 1.0, 0.0).astype(bf16)
    outs = [None] * steps
    carry = jnp.zeros((1, LANES), f32)
    order = range(steps - 1, -1, -1) if upper else range(steps)
    for n in order:
        block = value_of(n)
        total = sum(dot(tri, part) for part in split3(block)) + carry
        outs[n] = total
        carry = total[0:1] if upper else total[rows - 1 : rows]
    return outs, carry


def decay_kernel(local_heads, logf_ref, own_ref, halo_ref):
    rows = 256
    steps = logf_ref.shape[0] // rows
    lane = lax.broadcasted_iota(jnp.int32, (rows, LANES), 1)

    def value_of(n):
        return jnp.where(lane < local_heads, logf_ref[n * rows : (n + 1) * rows, :], 0.0)

    sums, total = running(value_of, steps, rows, False)
    one = jnp.where(lane == 3 * local_heads, 1.0, 0.0)

    def terms(value):
        high, mid, low = split3(value)
        return (
            high.astype(f32)
            + pltpu.roll(mid.astype(f32), local_heads, 1)
            + pltpu.roll(low.astype(f32), 2 * local_heads, 1)
            + one
        ).astype(bf16)

    for n in range(steps):
        own_ref[n * rows : (n + 1) * rows, :] = terms(sums[n])
        halo_ref[n * rows : (n + 1) * rows, :] = terms(sums[n] - total)


def decay_terms(logf, local_heads):
    shape = jax.ShapeDtypeStruct(logf.shape, bf16)
    return pl.pallas_call(
        functools.partial(decay_kernel, local_heads),
        out_shape=(shape, shape),
        name="decay_terms",
    )(logf)


def decay_back_kernel(own_ref, halo_ref, out_ref):
    rows = 256
    steps = own_ref.shape[0] // rows
    own, _ = running(lambda n: own_ref[n * rows : (n + 1) * rows, :], steps, rows, True)
    halo, _ = running(lambda n: halo_ref[n * rows : (n + 1) * rows, :], steps, rows, False)
    for n in range(steps):
        part = slice(n * rows, (n + 1) * rows)
        out_ref[part, :] = own[n] + (halo[n] - halo_ref[part, :])


def decay_back(own, halo):
    return pl.pallas_call(
        decay_back_kernel,
        out_shape=jax.ShapeDtypeStruct(own.shape, f32),
        name="decay_back",
    )(own, halo)


def placing(pair, local_heads, for_query):
    row = lax.broadcasted_iota(jnp.int32, (LANES, LANES), 0)
    col = lax.broadcasted_iota(jnp.int32, (LANES, LANES), 1)
    head = jnp.where(col < 64, 2 * pair + 1, 2 * pair)
    spot = jnp.where(col < 64, col, col - 64)
    term = jnp.where(for_query, spot, spot - 3)
    is_term = (term >= 0) & (term < 3) & (row == term * local_heads + head)
    ones = jnp.where(for_query, spot - 3, spot)
    is_one = (ones >= 0) & (ones < 3) & (row == 3 * local_heads)
    sign = 1.0 if for_query else -1.0
    return (jnp.where(is_term, sign, 0.0) + jnp.where(is_one, 1.0, 0.0)).astype(bf16)


def allowed_pairs(start, first_key, query_tile, rows, begin_row):
    shape = (K_TILE, Q_TILE)
    key_place = first_key + lax.broadcasted_iota(jnp.int32, shape, 0)
    query_place = rows + query_tile * Q_TILE + lax.broadcasted_iota(jnp.int32, shape, 1)
    return (key_place >= begin_row) & (key_place <= query_place)


def key_loops(ranges_ref, query_tile, rows, step, carry):
    first = ranges_ref[0, query_tile]
    full = ranges_ref[1, query_tile]
    diagonal = (rows + query_tile * Q_TILE) // K_TILE
    full = jnp.minimum(full, diagonal)
    carry = lax.fori_loop(first, full, functools.partial(step, True), carry)
    carry = lax.fori_loop(full, diagonal, functools.partial(step, False), carry)
    return lax.fori_loop(
        diagonal, diagonal + Q_TILE // K_TILE, functools.partial(step, True), carry
    )


def fill_keys(pair, local_heads, sources, keys, chunk):
    place = placing(pair, local_heads, False)
    rows = sources[0][0].shape[0]
    lane = lax.broadcasted_iota(jnp.int32, (chunk, LANES), 1)
    for half, (key_ref, terms_ref) in enumerate(sources):

        def fill(n, carry):
            here = pl.ds(pl.multiple_of(n * chunk, chunk), chunk)
            there = pl.ds(pl.multiple_of(half * rows + n * chunk, chunk), chunk)
            extra = dot(terms_ref[here, :], place).astype(bf16)
            key = key_ref[here, :]
            keys[0][there, :] = jnp.where(lane < 64, key, extra)
            keys[1][there, :] = jnp.where(lane < 64, extra, key)
            return carry

        lax.fori_loop(0, rows // chunk, fill, 0)


def query_tiles(q_ref, terms_ref, place, here, scaling):
    lane = lax.broadcasted_iota(jnp.int32, (Q_TILE, LANES), 1)
    extra = dot(terms_ref[here, :], place).astype(bf16)
    query = (q_ref[here, :].astype(f32) * scaling).astype(bf16)
    return jnp.where(lane < 64, query, extra), jnp.where(lane < 64, extra, query)


def attend_kernel(
    local_heads,
    ranges_ref,
    q_ref,
    k_own_ref,
    v_own_ref,
    k_prev_ref,
    v_prev_ref,
    t_own_ref,
    t_prev_ref,
    begin_ref,
    o_ref,
    lse_ref,
    key0,
    key1,
    values,
    acc0,
    acc1,
):
    pair = pl.program_id(0)
    rows = q_ref.shape[0]
    chunk = 512
    keys, accs = (key0, key1), (acc0, acc1)
    fill_keys(
        pair, local_heads, ((k_prev_ref, t_prev_ref), (k_own_ref, t_own_ref)), keys, chunk
    )
    for half, v_ref in enumerate((v_prev_ref, v_own_ref)):
        for n in range(rows // chunk):
            values[:, half * rows + n * chunk : half * rows + (n + 1) * chunk] = v_ref[
                n * chunk : (n + 1) * chunk, :
            ].T
    place = placing(pair, local_heads, True)

    def query_loop(tile, carry):
        here = pl.ds(pl.multiple_of(tile * Q_TILE, Q_TILE), Q_TILE)
        queries = query_tiles(q_ref, t_own_ref, place, here, 64**-0.5)
        begin_row = begin_ref[0:1, here]
        for acc in accs:
            acc[...] = jnp.zeros_like(acc)

        def step(masked, number, state):
            first_key = pl.multiple_of(number * K_TILE, K_TILE)
            there = pl.ds(first_key, K_TILE)
            fresh = []
            if masked:
                allowed = allowed_pairs(None, first_key, tile, rows, begin_row)
            for h in range(2):
                largest, total = state[2 * h], state[2 * h + 1]
                scores = dot(keys[h][there, :], queries[h], NT)
                if masked:
                    scores = jnp.where(allowed, scores, FAR)
                now = jnp.maximum(largest, jnp.max(scores, axis=0, keepdims=True))
                fade = jnp.exp(largest - now)
                weights = jnp.exp(scores - now)
                total = total * fade + jnp.sum(weights, axis=0, keepdims=True)
                accs[h][...] = accs[h][...] * fade + dot(
                    values[64 * h : 64 * (h + 1), there], weights.astype(bf16)
                )
                fresh += [now, total]
            return tuple(fresh)

        low = jnp.full((1, Q_TILE), FAR, f32)
        zero = jnp.zeros((1, Q_TILE), f32)
        state = key_loops(ranges_ref, tile, rows, step, (low, zero, low, zero))
        mixed = jnp.concatenate(
            [accs[h][...] * (1.0 / state[2 * h + 1]) for h in range(2)], axis=0
        )
        o_ref[here, :] = mixed.T.astype(bf16)
        for h in range(2):
            lse_ref[h : h + 1, here] = state[2 * h] + jnp.log(state[2 * h + 1])
        return carry

    lax.fori_loop(0, rows // Q_TILE, query_loop, 0)


def lane_block(rows, offset):
    return pl.BlockSpec((rows, LANES), lambda p, *_: (0, offset + p))


def fixed(shape):
    return pl.BlockSpec(shape, lambda p, *_: (0, 0))


def attend(ranges, query, key_value, earlier, terms, earlier_terms, begins, local_heads):
    rows = query.shape[0]
    pairs = local_heads // 2
    return pl.pallas_call(
        functools.partial(attend_kernel, local_heads),
        grid_spec=pltpu.PrefetchScalarGridSpec(
            num_scalar_prefetch=1,
            grid=(pairs,),
            in_specs=[
                lane_block(rows, 0),
                lane_block(rows, 0),
                lane_block(rows, pairs),
                lane_block(rows, 0),
                lane_block(rows, pairs),
                fixed((rows, LANES)),
                fixed((rows, LANES)),
                fixed((8, rows)),
            ],
            out_specs=[lane_block(rows, 0), pl.BlockSpec((8, rows), lambda p, *_: (p, 0))],
            scratch_shapes=[
                pltpu.VMEM((2 * rows, LANES), bf16),
                pltpu.VMEM((2 * rows, LANES), bf16),
                pltpu.VMEM((LANES, 2 * rows), bf16),
                pltpu.VMEM((64, Q_TILE), f32),
                pltpu.VMEM((64, Q_TILE), f32),
            ],
        ),
        out_shape=(
            jax.ShapeDtypeStruct((rows, pairs * LANES), bf16),
            jax.ShapeDtypeStruct((8 * pairs, rows), f32),
        ),
        cost_estimate=pl.CostEstimate(
            flops=40_000_000_000, transcendentals=20_000_000, bytes_accessed=12_000_000
        ),
        name="attend",
    )(ranges, query, key_value, key_value, earlier, earlier, terms, earlier_terms, begins)


def attend_back_kernel(
    local_heads,
    ranges_ref,
    q_ref,
    k_own_ref,
    v_own_ref,
    k_prev_ref,
    v_prev_ref,
    t_own_ref,
    t_prev_ref,
    begin_ref,
    grad_ref,
    o_ref,
    lse_ref,
    dq_ref,
    dk_own_ref,
    dv_own_ref,
    dk_prev_ref,
    dv_prev_ref,
    decay_own_ref,
    decay_prev_ref,
    key0,
    key1,
    key_t0,
    key_t1,
    values,
    dk0,
    dk1,
    dv,
    dq0,
    dq1,
):
    pair = pl.program_id(0)
    rows = q_ref.shape[0]
    chunk = 512
    keys, keys_t, dks, dqs = (key0, key1), (key_t0, key_t1), (dk0, dk1), (dq0, dq1)
    fill_keys(
        pair, local_heads, ((k_prev_ref, t_prev_ref), (k_own_ref, t_own_ref)), keys, chunk
    )
    for n in range(2 * rows // chunk):
        part = slice(n * chunk, (n + 1) * chunk)
        for h in range(2):
            keys_t[h][:, part] = keys[h][part, :].T
    values[0:rows, :] = v_prev_ref[...]
    values[rows : 2 * rows, :] = v_own_ref[...]
    for ref in (dk0, dk1, dv):
        ref[...] = jnp.zeros_like(ref)
    place = placing(pair, local_heads, True)
    lane = lax.broadcasted_iota(jnp.int32, (Q_TILE, LANES), 1)
    pick_row = lax.broadcasted_iota(jnp.int32, (8, LANES), 0)
    pick_lane = lax.broadcasted_iota(jnp.int32, (8, LANES), 1)
    pick = jnp.where((pick_lane // 64) == pick_row, 1.0, 0.0)

    @pl.when(pair == 0)
    def _():
        decay_own_ref[...] = jnp.zeros_like(decay_own_ref)
        decay_prev_ref[...] = jnp.zeros_like(decay_prev_ref)

    def query_loop(tile, carry):
        here = pl.ds(pl.multiple_of(tile * Q_TILE, Q_TILE), Q_TILE)
        queries = query_tiles(q_ref, t_own_ref, place, here, 64**-0.5)
        begin_row = begin_ref[0:1, here]
        grad = grad_ref[here, :]
        nothing = jnp.zeros_like(grad)
        grads = (jnp.where(lane < 64, grad, nothing), jnp.where(lane < 64, nothing, grad))
        product = grad.astype(f32) * o_ref[here, :].astype(f32)
        inner = dot(pick, product, NT, precision=lax.Precision.HIGHEST)
        for dq in dqs:
            dq[...] = jnp.zeros_like(dq)

        def step(masked, number, state):
            first_key = pl.multiple_of(number * K_TILE, K_TILE)
            there = pl.ds(first_key, K_TILE)
            if masked:
                allowed = allowed_pairs(None, first_key, tile, rows, begin_row)
            value = values[there, :]
            value_part = 0.0
            for h in range(2):
                scores = dot(keys[h][there, :], queries[h], NT)
                prob = jnp.exp(scores - lse_ref[h : h + 1, here])
                if masked:
                    prob = jnp.where(allowed, prob, 0.0)
                grad_prob = dot(value, grads[h], NT)
                grad_score = (prob * (grad_prob - inner[h : h + 1, :])).astype(bf16)
                value_part = value_part + dot(prob.astype(bf16), grads[h])
                dks[h][there, :] += dot(grad_score, queries[h])
                dqs[h][...] += dot(keys_t[h][:, there], grad_score)
            dv[there, :] += value_part
            return state

        key_loops(ranges_ref, tile, rows, step, 0)
        turned = [dq[...].T for dq in dqs]
        dq_ref[here, :] = (jnp.where(lane < 64, turned[0], turned[1]) * 64**-0.5).astype(bf16)
        decay = decay_own_ref[here, :]
        decay = decay + jnp.where(lane == 2 * pair, turned[0][:, 64:65], 0.0)
        decay = decay + jnp.where(lane == 2 * pair + 1, turned[1][:, 0:1], 0.0)
        decay_own_ref[here, :] = decay
        return carry

    lax.fori_loop(0, rows // Q_TILE, query_loop, 0)

    def finish(n, carry):
        for half, dk_ref, dv_ref, decay_ref, sign in (
            (0, dk_prev_ref, dv_prev_ref, decay_prev_ref, 1.0),
            (1, dk_own_ref, dv_own_ref, decay_own_ref, -1.0),
        ):
            here = pl.ds(pl.multiple_of(n * chunk, chunk), chunk)
            there = pl.ds(pl.multiple_of(half * rows + n * chunk, chunk), chunk)
            first, second = dk0[there, :], dk1[there, :]
            dk_ref[here, :] = jnp.where(lane < 64, first, second).astype(dk_ref.dtype)
            dv_ref[here, :] = dv[there, :].astype(dv_ref.dtype)
            decay = decay_ref[here, :]
            decay = decay + jnp.where(lane == 2 * pair, sign * first[:, 67:68], 0.0)
            decay = decay + jnp.where(lane == 2 * pair + 1, sign * second[:, 3:4], 0.0)
            decay_ref[here, :] = decay
        return carry

    lax.fori_loop(0, rows // chunk, finish, 0)


def attend_back(
    ranges, query, key_value, earlier, terms, earlier_terms, begins, grad, mixed, lse, local_heads
):
    rows = query.shape[0]
    pairs = local_heads // 2
    wide = pairs * LANES
    return pl.pallas_call(
        functools.partial(attend_back_kernel, local_heads),
        grid_spec=pltpu.PrefetchScalarGridSpec(
            num_scalar_prefetch=1,
            grid=(pairs,),
            in_specs=[
                lane_block(rows, 0),
                lane_block(rows, 0),
                lane_block(rows, pairs),
                lane_block(rows, 0),
                lane_block(rows, pairs),
                fixed((rows, LANES)),
                fixed((rows, LANES)),
                fixed((8, rows)),
                lane_block(rows, 0),
                lane_block(rows, 0),
                pl.BlockSpec((8, rows), lambda p, *_: (p, 0)),
            ],
            out_specs=[lane_block(rows, 0)] * 5 + [fixed((rows, LANES))] * 2,
            scratch_shapes=[
                pltpu.VMEM((2 * rows, LANES), bf16),
                pltpu.VMEM((2 * rows, LANES), bf16),
                pltpu.VMEM((LANES, 2 * rows), bf16),
                pltpu.VMEM((LANES, 2 * rows), bf16),
                pltpu.VMEM((2 * rows, LANES), bf16),
                pltpu.VMEM((2 * rows, LANES), f32),
                pltpu.VMEM((2 * rows, LANES), f32),
                pltpu.VMEM((2 * rows, LANES), f32),
                pltpu.VMEM((LANES, Q_TILE), f32),
                pltpu.VMEM((LANES, Q_TILE), f32),
            ],
        ),
        out_shape=(
            jax.ShapeDtypeStruct((rows, wide), bf16),
            jax.ShapeDtypeStruct((rows, wide), f32),
            jax.ShapeDtypeStruct((rows, wide), f32),
            jax.ShapeDtypeStruct((rows, wide), bf16),
            jax.ShapeDtypeStruct((rows, wide), bf16),
            jax.ShapeDtypeStruct((rows, LANES), f32),
            jax.ShapeDtypeStruct((rows, LANES), f32),
        ),
        cost_estimate=pl.CostEstimate(
            flops=80_000_000_000, transcendentals=20_000_000, bytes_accessed=25_000_000
        ),
        name="attend_back",
    )(
        ranges, query, key_value, key_value, earlier, earlier, terms, earlier_terms, begins,
        grad, mixed, lse,
    )


def normalize(hidden):
    factor = lax.rsqrt(jnp.mean(hidden * hidden, axis=1, keepdims=True) + epsilon)
    return (hidden * factor, factor)


def norm_back(grad_hat, normed, factor):
    return factor * (grad_hat - normed * jnp.mean(grad_hat * normed, axis=1, keepdims=True))


def over_tokens(operand, other_side):
    return lax.dot_general(
        operand, other_side, (((0,), (0,)), ((), ())), preferred_element_type=f32
    )


def gathered(pieces, groups):
    packed = jnp.concatenate(
        [piece.reshape(piece.shape[0], groups, -1) for piece in pieces], axis=2
    )
    mine = lax.all_to_all(packed, "head", split_axis=1, concat_axis=0, tiled=True)
    mine = mine.reshape(mine.shape[0], mine.shape[2])
    return lax.all_gather(mine, "blk", axis=0, tiled=True)


def scattered(grad, groups):
    summed = lax.psum_scatter(grad, "blk", scatter_dimension=0, tiled=True)
    rows, columns = summed.shape
    parts = lax.all_to_all(
        summed.reshape(groups, rows // groups, columns), "head", split_axis=0, concat_axis=0
    )
    return jnp.swapaxes(parts, 0, 1).astype(f32)


def body(
    tokens,
    segment,
    norm1_gain,
    w_query,
    w_key,
    w_value,
    w_gate_out,
    w_forget,
    forget_bias,
    w_output,
    norm2_gain,
    w_gate,
    w_up,
    w_down,
    cotangent,
):
    token_rows, model_width = tokens.shape
    groups = lax.axis_size("head")
    head_count = forget_bias.shape[0]
    local_heads = head_count // groups
    local_width = model_width // groups
    hidden_width = w_gate.shape[1] // groups
    rows = token_rows * groups
    share = w_query.shape[0]
    group = lax.axis_index("head")

    low = lambda array: array.astype(bf16)
    spread = lambda gain: jnp.broadcast_to(low(gain)[:, None, None], (share, groups, 1))
    forget_low = low(w_forget).reshape(share, groups, local_heads)
    rest = LANES - local_heads - 2
    small = jnp.concatenate(
        [forget_low, spread(norm1_gain), spread(norm2_gain), jnp.zeros((share, groups, rest), bf16)],
        axis=2,
    )
    first = gathered([low(w_key), low(w_value), low(w_query), low(w_gate_out), small], groups)
    tokens_all = lax.all_gather(tokens, "head", axis=0, tiled=True)
    output_weight = gathered([low(w_output)], groups)
    second = gathered([low(w_gate), low(w_up), low(w_down)], groups)
    cotangent_all = lax.all_gather(cotangent, "head", axis=0, tiled=True)

    segment_plus = segment + 1
    earlier_segment = passed_along(segment_plus, "blk", 1)
    window = jnp.concatenate([earlier_segment, segment_plus])
    begins = jnp.sum(
        (window[:, None] < segment_plus[None, :]).astype(jnp.int32), axis=0
    )
    tiles = begins.reshape(rows // Q_TILE, Q_TILE)
    ranges = jnp.stack([tiles[:, 0] // K_TILE, (tiles[:, -1] + K_TILE - 1) // K_TILE])
    begins = jnp.broadcast_to(begins[None, :], (8, rows))

    gain1 = first[:, 4 * local_width + local_heads].astype(f32)
    gain2 = first[:, 4 * local_width + local_heads + 1].astype(f32)
    normed_all, _ = normalize(tokens_all.astype(f32))
    input1 = (normed_all * gain1).astype(bf16)
    key_value = dot(input1, first[:, : 2 * local_width]).astype(bf16)
    earlier_kv = passed_along(key_value, "blk", 1)
    query = dot(input1, first[:, 2 * local_width : 3 * local_width]).astype(bf16)
    gate_forget = dot(input1, first[:, 3 * local_width :])
    gate_raw = gate_forget[:, :local_width]
    bias = lax.dynamic_slice_in_dim(forget_bias, group * local_heads, local_heads, 0)
    bias = jnp.pad(bias, (0, LANES - local_heads))
    forget = (gate_forget[:, local_width:] + bias[None, :]).astype(bf16).astype(f32)
    terms, halo_terms = decay_terms(jax.nn.log_sigmoid(forget), local_heads)
    earlier_terms = passed_along(halo_terms, "blk", 1)

    attended, lse = attend(
        ranges, query, key_value, earlier_kv, terms, earlier_terms, begins, local_heads
    )
    opened = jax.nn.sigmoid(gate_raw)
    attended_wide = attended.astype(f32)
    gated = (opened * attended_wide).astype(bf16)
    branch = dot(gated, output_weight, NT).astype(bf16)
    inputs = tokens.astype(f32)
    middle = inputs + lax.psum_scatter(branch, "head", scatter_dimension=0, tiled=True).astype(f32)
    normed2, factor2 = normalize(middle)
    input2 = lax.all_gather(
        (normed2 * gain2).astype(bf16), "head", axis=0, tiled=True
    )
    gate_act = dot(input2, second[:, :hidden_width])
    up_act = dot(input2, second[:, hidden_width : 2 * hidden_width])
    opening = jax.nn.sigmoid(gate_act)
    hidden = (gate_act * opening * up_act).astype(bf16)
    down = dot(hidden, second[:, 2 * hidden_width :], NT).astype(bf16)
    grad_hidden = dot(cotangent_all, second[:, 2 * hidden_width :])
    grad_gate_act = (grad_hidden * up_act * opening * (1.0 + gate_act * (1.0 - opening))).astype(
        bf16
    )
    grad_up_act = (grad_hidden * gate_act * opening).astype(bf16)
    grad_act = jnp.concatenate([grad_gate_act, grad_up_act], axis=1)
    grad_input2 = dot(grad_act, second[:, : 2 * hidden_width], NT).astype(bf16)
    grad_input2 = lax.psum_scatter(
        grad_input2, "head", scatter_dimension=0, tiled=True
    ).astype(f32)
    grad_middle = cotangent.astype(f32) + norm_back(grad_input2 * gain2, normed2, factor2)
    grad_branch = lax.all_gather(grad_middle.astype(bf16), "head", axis=0, tiled=True)
    result = (
        middle + lax.psum_scatter(down, "head", scatter_dimension=0, tiled=True).astype(f32)
    ).astype(bf16)
    second_grad = jnp.concatenate(
        [over_tokens(input2, grad_act).astype(bf16), over_tokens(cotangent_all, hidden).astype(bf16)],
        axis=1,
    )
    second_sum = scattered(second_grad, groups)

    grad_gated = dot(grad_branch, output_weight)
    grad_attended = (grad_gated * opened).astype(bf16)
    grad_gate_pre = (grad_gated * attended_wide * opened * (1.0 - opened)).astype(bf16)
    output_sum = scattered(over_tokens(grad_branch, gated).astype(bf16), groups)

    dq, dk_own, dv_own, dk_prev, dv_prev, decay_own, decay_prev = attend_back(
        ranges, query, key_value, earlier_kv, terms, earlier_terms, begins,
        grad_attended, attended, lse, local_heads,
    )
    dk = (dk_own + passed_along(dk_prev, "blk", -1).astype(f32)).astype(bf16)
    dv = (dv_own + passed_along(dv_prev, "blk", -1).astype(f32)).astype(bf16)
    decay_later = passed_along(decay_prev, "blk", -1)
    logf_grad = decay_back(decay_own, decay_later)
    forget_grad = jnp.where(
        jnp.arange(LANES)[None, :] < local_heads, logf_grad * jax.nn.sigmoid(-forget), 0.0
    ).astype(bf16)
    grads = jnp.concatenate([dk, dv, dq, grad_gate_pre, forget_grad], axis=1)
    grad_input1 = dot(grads, first, NT).astype(bf16)
    grad_input1 = lax.psum_scatter(
        grad_input1, "head", scatter_dimension=0, tiled=True
    ).astype(f32)
    normed1, factor1 = normalize(inputs)
    tokens_grad = grad_middle + norm_back(grad_input1 * gain1, normed1, factor1)

    first_grad = over_tokens(input1, grads)
    bias_part = jnp.sum(forget_grad.astype(f32), axis=0)
    row = jnp.arange(model_width)[:, None] % share
    column = jnp.arange(4 * local_width + LANES)[None, :]
    spread_bias = jnp.sum(
        jnp.where(row[:, :, None] == jnp.arange(local_heads)[None, None, :], bias_part[:local_heads], 0.0),
        axis=2,
    )
    first_grad = jnp.where(
        column == 4 * local_width + local_heads, spread_bias, first_grad
    ).astype(bf16)
    first_sum = scattered(first_grad, groups)

    def columns(array, start, width):
        return array[:, :, start : start + width].reshape(share, groups * width)

    key_sum, value_sum, query_sum, gate_out_sum = (
        columns(first_sum, n * local_width, local_width) for n in range(4)
    )
    forget_sum = columns(first_sum, 4 * local_width, local_heads)
    bias_total = first_sum[:local_heads, :, 4 * local_width + local_heads].T.reshape(head_count)
    gate_sum, up_sum, down_sum = (
        columns(second_sum, n * hidden_width, hidden_width) for n in range(3)
    )
    output_total = columns(output_sum, 0, local_width)

    def along(weight, grad):
        return jnp.sum(low(weight).astype(f32) * grad, axis=1)

    gain1_total = (
        along(w_query, query_sum)
        + along(w_key, key_sum)
        + along(w_value, value_sum)
        + along(w_gate_out, gate_out_sum)
        + along(w_forget, forget_sum)
    ) / low(norm1_gain).astype(f32)
    gain2_total = (along(w_gate, gate_sum) + along(w_up, up_sum)) / low(norm2_gain).astype(f32)
    return (
        result,
        tokens_grad,
        gain1_total,
        query_sum,
        key_sum,
        value_sum,
        gate_out_sum,
        forget_sum,
        bias_total,
        output_total,
        gain2_total,
        gate_sum,
        up_sum,
        down_sum,
    )


def solution(mesh):
    both = ("blk", "head")
    matrix, vector = P(both, None), P(both)
    return jax.shard_map(
        body,
        mesh=mesh,
        in_specs=(
            matrix, P("blk"), vector, matrix, matrix, matrix, matrix, matrix, P(), matrix, vector,
            matrix, matrix, matrix, matrix,
        ),
        out_specs=(
            matrix, matrix, vector, matrix, matrix, matrix, matrix, matrix, P(), matrix, vector,
            matrix, matrix, matrix,
        ),
        check_vma=False,
    )
```

```python
import functools

import jax
import jax.numpy as jnp
from jax import lax
from jax.experimental import pallas as pl
from jax.experimental.pallas import tpu as pltpu
from jax.sharding import PartitionSpec as P

epsilon = 1e-06
LANES = 128
Q_TILE = 512
K_TILE = 256
FAR = -1e30
NT = (((1,), (1,)), ((), ()))
NN = (((1,), (0,)), ((), ()))
bf16 = jnp.bfloat16
f32 = jnp.float32


def dot(a, b, dims=NN, **kw):
    return lax.dot_general(a, b, dims, preferred_element_type=f32, **kw)


def passed_along(array, axis, by):
    peers = lax.axis_size(axis)
    pairs = [(i, i + by) for i in range(peers) if 0 <= i + by < peers]
    return lax.ppermute(array, axis, pairs)


def split3(value):
    high = value.astype(bf16)
    rest = value - high.astype(f32)
    mid = rest.astype(bf16)
    low = (rest - mid.astype(f32)).astype(bf16)
    return high, mid, low


def running(value_of, steps, rows, upper):
    place = lax.broadcasted_iota(jnp.int32, (rows, rows), 0)
    other = lax.broadcasted_iota(jnp.int32, (rows, rows), 1)
    tri = jnp.where((other >= place) if upper else (other <= place), 1.0, 0.0).astype(bf16)
    outs = [None] * steps
    carry = jnp.zeros((1, LANES), f32)
    order = range(steps - 1, -1, -1) if upper else range(steps)
    for n in order:
        block = value_of(n)
        total = sum(dot(tri, part) for part in split3(block)) + carry
        outs[n] = total
        carry = total[0:1] if upper else total[rows - 1 : rows]
    return outs, carry


def decay_kernel(local_heads, logf_ref, own_ref, halo_ref):
    rows = 256
    steps = logf_ref.shape[0] // rows
    lane = lax.broadcasted_iota(jnp.int32, (rows, LANES), 1)

    def value_of(n):
        return jnp.where(lane < local_heads, logf_ref[n * rows : (n + 1) * rows, :], 0.0)

    sums, total = running(value_of, steps, rows, False)
    one = jnp.where(lane == 3 * local_heads, 1.0, 0.0)

    def terms(value):
        high, mid, low = split3(value)
        return (
            high.astype(f32)
            + pltpu.roll(mid.astype(f32), local_heads, 1)
            + pltpu.roll(low.astype(f32), 2 * local_heads, 1)
            + one
        ).astype(bf16)

    for n in range(steps):
        own_ref[n * rows : (n + 1) * rows, :] = terms(sums[n])
        halo_ref[n * rows : (n + 1) * rows, :] = terms(sums[n] - total)


def decay_terms(logf, local_heads):
    shape = jax.ShapeDtypeStruct(logf.shape, bf16)
    return pl.pallas_call(
        functools.partial(decay_kernel, local_heads),
        out_shape=(shape, shape),
        name="decay_terms",
    )(logf)


def decay_back_kernel(own_ref, halo_ref, out_ref):
    rows = 256
    steps = own_ref.shape[0] // rows
    own, _ = running(lambda n: own_ref[n * rows : (n + 1) * rows, :], steps, rows, True)
    halo, _ = running(lambda n: halo_ref[n * rows : (n + 1) * rows, :], steps, rows, False)
    for n in range(steps):
        part = slice(n * rows, (n + 1) * rows)
        out_ref[part, :] = own[n] + (halo[n] - halo_ref[part, :])


def decay_back(own, halo):
    return pl.pallas_call(
        decay_back_kernel,
        out_shape=jax.ShapeDtypeStruct(own.shape, f32),
        name="decay_back",
    )(own, halo)


def placing(pair, local_heads, for_query):
    row = lax.broadcasted_iota(jnp.int32, (LANES, LANES), 0)
    col = lax.broadcasted_iota(jnp.int32, (LANES, LANES), 1)
    head = jnp.where(col < 64, 2 * pair + 1, 2 * pair)
    spot = jnp.where(col < 64, col, col - 64)
    term = jnp.where(for_query, spot, spot - 3)
    is_term = (term >= 0) & (term < 3) & (row == term * local_heads + head)
    ones = jnp.where(for_query, spot - 3, spot)
    is_one = (ones >= 0) & (ones < 3) & (row == 3 * local_heads)
    sign = 1.0 if for_query else -1.0
    return (jnp.where(is_term, sign, 0.0) + jnp.where(is_one, 1.0, 0.0)).astype(bf16)


def allowed_pairs(start, first_key, query_tile, rows, begin_row):
    shape = (K_TILE, Q_TILE)
    key_place = first_key + lax.broadcasted_iota(jnp.int32, shape, 0)
    query_place = rows + query_tile * Q_TILE + lax.broadcasted_iota(jnp.int32, shape, 1)
    return (key_place >= begin_row) & (key_place <= query_place)


def key_loops(ranges_ref, query_tile, rows, step, carry):
    first = ranges_ref[0, query_tile]
    full = ranges_ref[1, query_tile]
    diagonal = (rows + query_tile * Q_TILE) // K_TILE
    full = jnp.minimum(full, diagonal)
    carry = lax.fori_loop(first, full, functools.partial(step, True), carry)
    carry = lax.fori_loop(full, diagonal, functools.partial(step, False), carry)
    return lax.fori_loop(
        diagonal, diagonal + Q_TILE // K_TILE, functools.partial(step, True), carry
    )


def fill_keys(pair, local_heads, sources, keys, chunk):
    place = placing(pair, local_heads, False)
    rows = sources[0][0].shape[0]
    lane = lax.broadcasted_iota(jnp.int32, (chunk, LANES), 1)
    for half, (key_ref, terms_ref) in enumerate(sources):

        def fill(n, carry):
            here = pl.ds(pl.multiple_of(n * chunk, chunk), chunk)
            there = pl.ds(pl.multiple_of(half * rows + n * chunk, chunk), chunk)
            extra = dot(terms_ref[here, :], place).astype(bf16)
            key = key_ref[here, :]
            keys[0][there, :] = jnp.where(lane < 64, key, extra)
            keys[1][there, :] = jnp.where(lane < 64, extra, key)
            return carry

        lax.fori_loop(0, rows // chunk, fill, 0)


def query_tiles(q_ref, terms_ref, place, here, scaling):
    lane = lax.broadcasted_iota(jnp.int32, (Q_TILE, LANES), 1)
    extra = dot(terms_ref[here, :], place).astype(bf16)
    query = (q_ref[here, :].astype(f32) * scaling).astype(bf16)
    return jnp.where(lane < 64, query, extra), jnp.where(lane < 64, extra, query)


def attend_kernel(
    local_heads,
    ranges_ref,
    q_ref,
    k_own_ref,
    v_own_ref,
    k_prev_ref,
    v_prev_ref,
    t_own_ref,
    t_prev_ref,
    begin_ref,
    o_ref,
    lse_ref,
    key0,
    key1,
    values,
    acc0,
    acc1,
):
    pair = pl.program_id(0)
    rows = q_ref.shape[0]
    chunk = 512
    keys, accs = (key0, key1), (acc0, acc1)
    fill_keys(
        pair, local_heads, ((k_prev_ref, t_prev_ref), (k_own_ref, t_own_ref)), keys, chunk
    )
    for half, v_ref in enumerate((v_prev_ref, v_own_ref)):
        for n in range(rows // chunk):
            values[:, half * rows + n * chunk : half * rows + (n + 1) * chunk] = v_ref[
                n * chunk : (n + 1) * chunk, :
            ].T
    place = placing(pair, local_heads, True)

    def query_loop(tile, carry):
        here = pl.ds(pl.multiple_of(tile * Q_TILE, Q_TILE), Q_TILE)
        queries = query_tiles(q_ref, t_own_ref, place, here, 64**-0.5)
        begin_row = begin_ref[0:1, here]
        for acc in accs:
            acc[...] = jnp.zeros_like(acc)

        def step(masked, number, state):
            first_key = pl.multiple_of(number * K_TILE, K_TILE)
            there = pl.ds(first_key, K_TILE)
            fresh = []
            if masked:
                allowed = allowed_pairs(None, first_key, tile, rows, begin_row)
            for h in range(2):
                largest, total = state[2 * h], state[2 * h + 1]
                scores = dot(keys[h][there, :], queries[h], NT)
                if masked:
                    scores = jnp.where(allowed, scores, FAR)
                now = jnp.maximum(largest, jnp.max(scores, axis=0, keepdims=True))
                fade = jnp.exp(largest - now)
                weights = jnp.exp(scores - now)
                total = total * fade + jnp.sum(weights, axis=0, keepdims=True)
                accs[h][...] = accs[h][...] * fade + dot(
                    values[64 * h : 64 * (h + 1), there], weights.astype(bf16)
                )
                fresh += [now, total]
            return tuple(fresh)

        low = jnp.full((1, Q_TILE), FAR, f32)
        zero = jnp.zeros((1, Q_TILE), f32)
        state = key_loops(ranges_ref, tile, rows, step, (low, zero, low, zero))
        mixed = jnp.concatenate(
            [accs[h][...] * (1.0 / state[2 * h + 1]) for h in range(2)], axis=0
        )
        o_ref[here, :] = mixed.T.astype(bf16)
        for h in range(2):
            lse_ref[h : h + 1, here] = state[2 * h] + jnp.log(state[2 * h + 1])
        return carry

    lax.fori_loop(0, rows // Q_TILE, query_loop, 0)


def lane_block(rows, offset):
    return pl.BlockSpec((rows, LANES), lambda p, *_: (0, offset + p))


def fixed(shape):
    return pl.BlockSpec(shape, lambda p, *_: (0, 0))


def attend(ranges, query, key_value, earlier, terms, earlier_terms, begins, local_heads):
    rows = query.shape[0]
    pairs = local_heads // 2
    return pl.pallas_call(
        functools.partial(attend_kernel, local_heads),
        grid_spec=pltpu.PrefetchScalarGridSpec(
            num_scalar_prefetch=1,
            grid=(pairs,),
            in_specs=[
                lane_block(rows, 0),
                lane_block(rows, 0),
                lane_block(rows, pairs),
                lane_block(rows, 0),
                lane_block(rows, pairs),
                fixed((rows, LANES)),
                fixed((rows, LANES)),
                fixed((8, rows)),
            ],
            out_specs=[lane_block(rows, 0), pl.BlockSpec((8, rows), lambda p, *_: (p, 0))],
            scratch_shapes=[
                pltpu.VMEM((2 * rows, LANES), bf16),
                pltpu.VMEM((2 * rows, LANES), bf16),
                pltpu.VMEM((LANES, 2 * rows), bf16),
                pltpu.VMEM((64, Q_TILE), f32),
                pltpu.VMEM((64, Q_TILE), f32),
            ],
        ),
        out_shape=(
            jax.ShapeDtypeStruct((rows, pairs * LANES), bf16),
            jax.ShapeDtypeStruct((8 * pairs, rows), f32),
        ),
        cost_estimate=pl.CostEstimate(
            flops=40_000_000_000, transcendentals=20_000_000, bytes_accessed=12_000_000
        ),
        name="attend",
    )(ranges, query, key_value, key_value, earlier, earlier, terms, earlier_terms, begins)


def attend_back_kernel(
    local_heads,
    ranges_ref,
    q_ref,
    k_own_ref,
    v_own_ref,
    k_prev_ref,
    v_prev_ref,
    t_own_ref,
    t_prev_ref,
    begin_ref,
    grad_ref,
    o_ref,
    lse_ref,
    dq_ref,
    dk_own_ref,
    dv_own_ref,
    dk_prev_ref,
    dv_prev_ref,
    decay_own_ref,
    decay_prev_ref,
    key0,
    key1,
    key_t0,
    key_t1,
    values,
    dk0,
    dk1,
    dv,
    dq0,
    dq1,
):
    pair = pl.program_id(0)
    rows = q_ref.shape[0]
    chunk = 512
    keys, keys_t, dks, dqs = (key0, key1), (key_t0, key_t1), (dk0, dk1), (dq0, dq1)
    fill_keys(
        pair, local_heads, ((k_prev_ref, t_prev_ref), (k_own_ref, t_own_ref)), keys, chunk
    )
    for n in range(2 * rows // chunk):
        part = slice(n * chunk, (n + 1) * chunk)
        for h in range(2):
            keys_t[h][:, part] = keys[h][part, :].T
    values[0:rows, :] = v_prev_ref[...]
    values[rows : 2 * rows, :] = v_own_ref[...]
    for ref in (dk0, dk1, dv):
        ref[...] = jnp.zeros_like(ref)
    place = placing(pair, local_heads, True)
    lane = lax.broadcasted_iota(jnp.int32, (Q_TILE, LANES), 1)
    pick_row = lax.broadcasted_iota(jnp.int32, (8, LANES), 0)
    pick_lane = lax.broadcasted_iota(jnp.int32, (8, LANES), 1)
    pick = jnp.where((pick_lane // 64) == pick_row, 1.0, 0.0)

    @pl.when(pair == 0)
    def _():
        decay_own_ref[...] = jnp.zeros_like(decay_own_ref)
        decay_prev_ref[...] = jnp.zeros_like(decay_prev_ref)

    def query_loop(tile, carry):
        here = pl.ds(pl.multiple_of(tile * Q_TILE, Q_TILE), Q_TILE)
        queries = query_tiles(q_ref, t_own_ref, place, here, 64**-0.5)
        begin_row = begin_ref[0:1, here]
        grad = grad_ref[here, :]
        nothing = jnp.zeros_like(grad)
        grads = (jnp.where(lane < 64, grad, nothing), jnp.where(lane < 64, nothing, grad))
        product = grad.astype(f32) * o_ref[here, :].astype(f32)
        inner = dot(pick, product, NT, precision=lax.Precision.HIGHEST)
        for dq in dqs:
            dq[...] = jnp.zeros_like(dq)

        def step(masked, number, state):
            first_key = pl.multiple_of(number * K_TILE, K_TILE)
            there = pl.ds(first_key, K_TILE)
            if masked:
                allowed = allowed_pairs(None, first_key, tile, rows, begin_row)
            value = values[there, :]
            value_part = 0.0
            for h in range(2):
                scores = dot(keys[h][there, :], queries[h], NT)
                prob = jnp.exp(scores - lse_ref[h : h + 1, here])
                if masked:
                    prob = jnp.where(allowed, prob, 0.0)
                grad_prob = dot(value, grads[h], NT)
                grad_score = (prob * (grad_prob - inner[h : h + 1, :])).astype(bf16)
                value_part = value_part + dot(prob.astype(bf16), grads[h])
                dks[h][there, :] += dot(grad_score, queries[h])
                dqs[h][...] += dot(keys_t[h][:, there], grad_score)
            dv[there, :] += value_part
            return state

        key_loops(ranges_ref, tile, rows, step, 0)
        turned = [dq[...].T for dq in dqs]
        dq_ref[here, :] = (jnp.where(lane < 64, turned[0], turned[1]) * 64**-0.5).astype(bf16)
        decay = decay_own_ref[here, :]
        decay = decay + jnp.where(lane == 2 * pair, turned[0][:, 64:65], 0.0)
        decay = decay + jnp.where(lane == 2 * pair + 1, turned[1][:, 0:1], 0.0)
        decay_own_ref[here, :] = decay
        return carry

    lax.fori_loop(0, rows // Q_TILE, query_loop, 0)

    def finish(n, carry):
        for half, dk_ref, dv_ref, decay_ref, sign in (
            (0, dk_prev_ref, dv_prev_ref, decay_prev_ref, 1.0),
            (1, dk_own_ref, dv_own_ref, decay_own_ref, -1.0),
        ):
            here = pl.ds(pl.multiple_of(n * chunk, chunk), chunk)
            there = pl.ds(pl.multiple_of(half * rows + n * chunk, chunk), chunk)
            first, second = dk0[there, :], dk1[there, :]
            dk_ref[here, :] = jnp.where(lane < 64, first, second).astype(dk_ref.dtype)
            dv_ref[here, :] = dv[there, :].astype(dv_ref.dtype)
            decay = decay_ref[here, :]
            decay = decay + jnp.where(lane == 2 * pair, sign * first[:, 67:68], 0.0)
            decay = decay + jnp.where(lane == 2 * pair + 1, sign * second[:, 3:4], 0.0)
            decay_ref[here, :] = decay
        return carry

    lax.fori_loop(0, rows // chunk, finish, 0)


def attend_back(
    ranges, query, key_value, earlier, terms, earlier_terms, begins, grad, mixed, lse, local_heads
):
    rows = query.shape[0]
    pairs = local_heads // 2
    wide = pairs * LANES
    return pl.pallas_call(
        functools.partial(attend_back_kernel, local_heads),
        grid_spec=pltpu.PrefetchScalarGridSpec(
            num_scalar_prefetch=1,
            grid=(pairs,),
            in_specs=[
                lane_block(rows, 0),
                lane_block(rows, 0),
                lane_block(rows, pairs),
                lane_block(rows, 0),
                lane_block(rows, pairs),
                fixed((rows, LANES)),
                fixed((rows, LANES)),
                fixed((8, rows)),
                lane_block(rows, 0),
                lane_block(rows, 0),
                pl.BlockSpec((8, rows), lambda p, *_: (p, 0)),
            ],
            out_specs=[lane_block(rows, 0)] * 5 + [fixed((rows, LANES))] * 2,
            scratch_shapes=[
                pltpu.VMEM((2 * rows, LANES), bf16),
                pltpu.VMEM((2 * rows, LANES), bf16),
                pltpu.VMEM((LANES, 2 * rows), bf16),
                pltpu.VMEM((LANES, 2 * rows), bf16),
                pltpu.VMEM((2 * rows, LANES), bf16),
                pltpu.VMEM((2 * rows, LANES), f32),
                pltpu.VMEM((2 * rows, LANES), f32),
                pltpu.VMEM((2 * rows, LANES), f32),
                pltpu.VMEM((LANES, Q_TILE), f32),
                pltpu.VMEM((LANES, Q_TILE), f32),
            ],
        ),
        out_shape=(
            jax.ShapeDtypeStruct((rows, wide), bf16),
            jax.ShapeDtypeStruct((rows, wide), f32),
            jax.ShapeDtypeStruct((rows, wide), f32),
            jax.ShapeDtypeStruct((rows, wide), bf16),
            jax.ShapeDtypeStruct((rows, wide), bf16),
            jax.ShapeDtypeStruct((rows, LANES), f32),
            jax.ShapeDtypeStruct((rows, LANES), f32),
        ),
        cost_estimate=pl.CostEstimate(
            flops=80_000_000_000, transcendentals=20_000_000, bytes_accessed=25_000_000
        ),
        name="attend_back",
    )(
        ranges, query, key_value, key_value, earlier, earlier, terms, earlier_terms, begins,
        grad, mixed, lse,
    )


PIECES = 4


def partners():
    me = lax.axis_index("head")
    near = me + 1 - 2 * (me % 2)
    far = (me + 2) % 4
    cross = (near + 2) % 4
    return me, near, far, cross


def greet(*others):
    barrier = pltpu.get_barrier_semaphore()
    for other in others:
        pl.semaphore_signal(
            barrier, inc=1, device_id={"head": other}, device_id_type=pl.DeviceIdType.MESH
        )
    pl.semaphore_wait(barrier, len(others))


def remote(source, target, send, receive, other):
    return pltpu.make_async_remote_copy(
        src_ref=source,
        dst_ref=target,
        send_sem=send,
        recv_sem=receive,
        device_id={"head": other},
        device_id_type=pl.DeviceIdType.MESH,
    )


def rows_of(ref, shard, piece, size):
    span = size // PIECES
    start = pl.multiple_of(shard * size + piece * span, span)
    return ref.at[pl.ds(start, span), :]


def spread_piece(source_of, all_ref, size, sems, piece):
    me, near, far, _ = partners()
    far_send, far_recv, near_send, near_recv, _, _, own = sems
    copies = (
        remote(source_of(piece), rows_of(all_ref, me, piece, size), far_send.at[piece], far_recv.at[piece], far),
        remote(source_of(piece), rows_of(all_ref, me, piece, size), near_send.at[piece], near_recv.at[piece], near),
        pltpu.make_async_copy(source_of(piece), rows_of(all_ref, me, piece, size), own.at[piece]),
    )
    for copy in copies:
        copy.start()
    return copies


def hand_on(all_ref, size, sems, sent):
    me, near, far, cross = partners()
    far_send, far_recv, near_send, near_recv, on_send, on_recv, own = sems
    passed = []
    for piece in range(PIECES):
        there = rows_of(all_ref, far, piece, size)
        remote(there, there, far_send.at[piece], far_recv.at[piece], far).wait_recv()
        copy = remote(there, there, on_send.at[piece], on_recv.at[piece], near)
        copy.start()
        passed.append(copy)
    for piece in range(PIECES):
        to_far, to_near, local = sent[piece]
        to_far.wait_send()
        to_near.wait_send()
        local.wait()
        passed[piece].wait_send()
        there = rows_of(all_ref, near, piece, size)
        remote(there, there, near_send.at[piece], near_recv.at[piece], near).wait_recv()
        there = rows_of(all_ref, cross, piece, size)
        remote(there, there, on_send.at[piece], on_recv.at[piece], near).wait_recv()


def gather_sems():
    return [pltpu.SemaphoreType.DMA((PIECES,)) for _ in range(7)]


def gather_kernel(mine_ref, all_ref, *sems):
    size = mine_ref.shape[0]
    _, near, far, _ = partners()
    greet(near, far)
    sent = [
        spread_piece(lambda n: rows_of(mine_ref, 0, n, size), all_ref, size, sems, piece)
        for piece in range(PIECES)
    ]
    hand_on(all_ref, size, sems, sent)


def gather_heads(mine, number):
    rows, width = mine.shape
    return pl.pallas_call(
        gather_kernel,
        in_specs=[pl.BlockSpec(memory_space=pl.ANY)],
        out_specs=pl.BlockSpec(memory_space=pl.ANY),
        out_shape=jax.ShapeDtypeStruct((4 * rows, width), mine.dtype),
        scratch_shapes=gather_sems(),
        compiler_params=pltpu.CompilerParams(collective_id=number, has_side_effects=True),
        cost_estimate=pl.CostEstimate(
            flops=30_000_000_000, transcendentals=0, bytes_accessed=8_000_000
        ),
        name="gather_heads",
    )(mine)


def exchange_kernel(local, extras, gather, *refs):
    part_ref, rest = refs[0], refs[1:]
    extra_refs, rest = rest[:extras], rest[extras:]
    out_ref, rest = rest[0], rest[1:]
    if gather:
        all_ref, rest = rest[0], rest[1:]
    near_buf, turn_buf, far_buf, rest = rest[0], rest[1], rest[2], rest[3:]
    near_send, near_recv, far_send, far_recv = rest[:4]
    if gather:
        payload, sems = rest[4], rest[5:]
    size = out_ref.shape[0]
    span = size // PIECES
    me, near, far, cross = partners()
    greet(near, far)
    near_copies = []
    for which, shard in ((0, cross), (1, near)):
        for piece in range(PIECES):
            copy = remote(
                rows_of(part_ref, shard, piece, size),
                near_buf.at[which, pl.ds(piece * span, span), :],
                near_send.at[which, piece],
                near_recv.at[which, piece],
                near,
            )
            copy.start()
            near_copies.append(copy)
    far_copies = []
    for piece in range(PIECES):
        here = slice(piece * span, (piece + 1) * span)
        near_copies[piece].wait_recv()
        turn_buf[here, :] = (
            rows_of(part_ref, far, piece, size)[...].astype(f32) + near_buf[0, here, :].astype(f32)
        ).astype(bf16)
        copy = remote(
            turn_buf.at[pl.ds(piece * span, span), :],
            far_buf.at[pl.ds(piece * span, span), :],
            far_send.at[piece],
            far_recv.at[piece],
            far,
        )
        copy.start()
        far_copies.append(copy)
    sent = []
    for piece in range(PIECES):
        here = slice(piece * span, (piece + 1) * span)
        near_copies[PIECES + piece].wait_recv()
        far_copies[piece].wait_recv()
        total = (
            rows_of(part_ref, me, piece, size)[...].astype(f32)
            + near_buf[1, here, :].astype(f32)
            + far_buf[here, :].astype(f32)
        )
        result, share = local(total, here, *extra_refs)
        out_ref[here, :] = result.astype(out_ref.dtype)
        if gather:
            payload[here, :] = share.astype(bf16)
            sent.append(
                spread_piece(
                    lambda n: payload.at[pl.ds(n * span, span), :], all_ref, size, sems, piece
                )
            )
    if gather:
        hand_on(all_ref, size, sems, sent)
    for copy in near_copies + far_copies:
        copy.wait_send()


def exchange(local, part, extras, out_type, gather, number, name):
    rows, width = part.shape
    size = rows // 4
    out_shape = [jax.ShapeDtypeStruct((size, width), out_type)]
    out_specs = [pl.BlockSpec(memory_space=pltpu.VMEM)]
    scratch = [
        pltpu.VMEM((2, size, width), bf16),
        pltpu.VMEM((size, width), bf16),
        pltpu.VMEM((size, width), bf16),
        pltpu.SemaphoreType.DMA((2, PIECES)),
        pltpu.SemaphoreType.DMA((2, PIECES)),
        pltpu.SemaphoreType.DMA((PIECES,)),
        pltpu.SemaphoreType.DMA((PIECES,)),
    ]
    if gather:
        out_shape.append(jax.ShapeDtypeStruct((rows, width), bf16))
        out_specs.append(pl.BlockSpec(memory_space=pl.ANY))
        scratch += [pltpu.VMEM((size, width), bf16)] + gather_sems()
    return pl.pallas_call(
        functools.partial(exchange_kernel, local, len(extras), gather),
        in_specs=[pl.BlockSpec(memory_space=pltpu.VMEM)] * (1 + len(extras)),
        out_specs=out_specs,
        out_shape=out_shape,
        scratch_shapes=scratch,
        compiler_params=pltpu.CompilerParams(collective_id=number, has_side_effects=True),
        cost_estimate=pl.CostEstimate(
            flops=60_000_000_000 if gather else 35_000_000_000,
            transcendentals=0,
            bytes_accessed=16_000_000,
        ),
        name=name,
    )(part, *extras)


def inverse_rms(value):
    return lax.rsqrt(jnp.mean(value * value, axis=1, keepdims=True) + epsilon)


def through_norm(grad, value):
    factor = inverse_rms(value)
    normed = value * factor
    return factor * (grad - normed * jnp.mean(grad * normed, axis=1, keepdims=True))


def after_attention(total, here, tokens_ref, gain_ref):
    middle = tokens_ref[here, :].astype(f32) + total
    return middle, middle * inverse_rms(middle) * gain_ref[0:1, :]


def after_hidden(total, here, cotangent_ref, middle_ref, gain_ref):
    grad = cotangent_ref[here, :].astype(f32) + through_norm(
        total * gain_ref[0:1, :], middle_ref[here, :]
    )
    return grad, grad


def after_first(total, here, grad_ref, tokens_ref, gain_ref):
    grad = grad_ref[here, :] + through_norm(
        total * gain_ref[0:1, :], tokens_ref[here, :].astype(f32)
    )
    return grad, None


def after_down(total, here, middle_ref):
    return middle_ref[here, :] + total, None


def over_tokens(operand, other_side):
    return lax.dot_general(
        operand, other_side, (((0,), (0,)), ((), ())), preferred_element_type=f32
    )


def sent_columns(pieces, groups):
    packed = jnp.concatenate(
        [piece.reshape(piece.shape[0], groups, -1) for piece in pieces], axis=2
    )
    mine = lax.all_to_all(packed, "head", split_axis=1, concat_axis=0, tiled=True)
    return mine.reshape(mine.shape[0], mine.shape[2])


def all_rows(mine):
    return lax.all_gather(mine, "blk", axis=0, tiled=True)


def scattered(grad, groups):
    summed = lax.psum_scatter(grad, "blk", scatter_dimension=0, tiled=True)
    rows, columns = summed.shape
    parts = lax.all_to_all(
        summed.reshape(groups, rows // groups, columns), "head", split_axis=0, concat_axis=0
    )
    return jnp.swapaxes(parts, 0, 1).astype(f32)


def body(
    tokens,
    segment,
    norm1_gain,
    w_query,
    w_key,
    w_value,
    w_gate_out,
    w_forget,
    forget_bias,
    w_output,
    norm2_gain,
    w_gate,
    w_up,
    w_down,
    cotangent,
):
    token_rows, model_width = tokens.shape
    groups = lax.axis_size("head")
    head_count = forget_bias.shape[0]
    local_heads = head_count // groups
    local_width = model_width // groups
    hidden_width = w_gate.shape[1] // groups
    rows = token_rows * groups
    share = w_query.shape[0]
    group = lax.axis_index("head")

    low = lambda array: array.astype(bf16)
    spread = lambda gain: jnp.broadcast_to(low(gain)[:, None, None], (share, groups, 1))
    forget_low = low(w_forget).reshape(share, groups, local_heads)
    rest = LANES - local_heads - 2
    small = jnp.concatenate(
        [forget_low, spread(norm1_gain), spread(norm2_gain), jnp.zeros((share, groups, rest), bf16)],
        axis=2,
    )
    mine_kv = sent_columns([low(w_key), low(w_value), small], groups)
    first_kv = all_rows(mine_kv)
    mine_rest = sent_columns(
        [low(w_query), low(w_gate_out), low(w_output), low(w_gate), low(w_up), low(w_down)], groups
    )
    first_q = all_rows(mine_rest[:, : 3 * local_width])
    second = all_rows(mine_rest[:, 3 * local_width :])
    tokens_all = gather_heads(tokens, 0)
    cotangent_all = gather_heads(cotangent, 1)
    output_weight = first_q[:, 2 * local_width :]

    segment_plus = segment + 1
    earlier_segment = passed_along(segment_plus, "blk", 1)
    window = jnp.concatenate([earlier_segment, segment_plus])
    begins = jnp.sum(
        (window[:, None] < segment_plus[None, :]).astype(jnp.int32), axis=0
    )
    tiles = begins.reshape(rows // Q_TILE, Q_TILE)
    ranges = jnp.stack([tiles[:, 0] // K_TILE, (tiles[:, -1] + K_TILE - 1) // K_TILE])
    begins = jnp.broadcast_to(begins[None, :], (8, rows))

    def gain_rows(column):
        gain = first_kv[:, 2 * local_width + local_heads + column].astype(f32)
        return jnp.broadcast_to(gain[None, :], (8, model_width))

    gain1, gain2 = gain_rows(0), gain_rows(1)
    wide_all = tokens_all.astype(f32)
    input1 = (wide_all * inverse_rms(wide_all) * gain1[0:1]).astype(bf16)
    key_value = dot(input1, first_kv[:, : 2 * local_width]).astype(bf16)
    earlier_kv = passed_along(key_value, "blk", 1)
    bias = lax.dynamic_slice_in_dim(forget_bias, group * local_heads, local_heads, 0)
    bias = jnp.pad(bias, (0, LANES - local_heads))
    forget = dot(input1, first_kv[:, 2 * local_width :]) + bias[None, :]
    forget = forget.astype(bf16).astype(f32)
    terms, halo_terms = decay_terms(jax.nn.log_sigmoid(forget), local_heads)
    earlier_terms = passed_along(halo_terms, "blk", 1)
    query = dot(input1, first_q[:, :local_width]).astype(bf16)
    gate_raw = dot(input1, first_q[:, local_width : 2 * local_width])

    attended, lse = attend(
        ranges, query, key_value, earlier_kv, terms, earlier_terms, begins, local_heads
    )
    opened = jax.nn.sigmoid(gate_raw)
    attended_wide = attended.astype(f32)
    gated = (opened * attended_wide).astype(bf16)
    branch = dot(gated, output_weight, NT).astype(bf16)
    middle, input2 = exchange(
        after_attention, branch, [tokens, gain2], f32, True, 2, "exchange_middle"
    )
    gate_act = dot(input2, second[:, :hidden_width])
    up_act = dot(input2, second[:, hidden_width : 2 * hidden_width])
    opening = jax.nn.sigmoid(gate_act)
    hidden = (gate_act * opening * up_act).astype(bf16)
    down = dot(hidden, second[:, 2 * hidden_width :], NT).astype(bf16)
    grad_hidden = dot(cotangent_all, second[:, 2 * hidden_width :])
    grad_gate_act = (grad_hidden * up_act * opening * (1.0 + gate_act * (1.0 - opening))).astype(
        bf16
    )
    grad_up_act = (grad_hidden * gate_act * opening).astype(bf16)
    grad_act = jnp.concatenate([grad_gate_act, grad_up_act], axis=1)
    grad_input2 = dot(grad_act, second[:, : 2 * hidden_width], NT).astype(bf16)
    grad_middle, grad_branch = exchange(
        after_hidden, grad_input2, [cotangent, middle, gain2], f32, True, 3, "exchange_hidden"
    )
    second_grad = jnp.concatenate(
        [over_tokens(input2, grad_act).astype(bf16), over_tokens(cotangent_all, hidden).astype(bf16)],
        axis=1,
    )
    second_sum = scattered(second_grad, groups)

    grad_gated = dot(grad_branch, output_weight)
    grad_attended = (grad_gated * opened).astype(bf16)
    grad_gate_pre = (grad_gated * attended_wide * opened * (1.0 - opened)).astype(bf16)
    early_grad = jnp.concatenate(
        [over_tokens(input1, grad_gate_pre).astype(bf16), over_tokens(grad_branch, gated).astype(bf16)],
        axis=1,
    )
    early_sum = scattered(early_grad, groups)

    dq, dk_own, dv_own, dk_prev, dv_prev, decay_own, decay_prev = attend_back(
        ranges, query, key_value, earlier_kv, terms, earlier_terms, begins,
        grad_attended, attended, lse, local_heads,
    )
    dk = (dk_own + passed_along(dk_prev, "blk", -1).astype(f32)).astype(bf16)
    dv = (dv_own + passed_along(dv_prev, "blk", -1).astype(f32)).astype(bf16)
    decay_later = passed_along(decay_prev, "blk", -1)
    logf_grad = decay_back(decay_own, decay_later)
    forget_grad = jnp.where(
        jnp.arange(LANES)[None, :] < local_heads, logf_grad * jax.nn.sigmoid(-forget), 0.0
    ).astype(bf16)
    grads = jnp.concatenate([dk, dv, forget_grad, dq], axis=1)
    first_grad = over_tokens(input1, grads)
    bias_part = jnp.sum(forget_grad.astype(f32), axis=0)
    row = jnp.arange(model_width)[:, None] % share
    column = jnp.arange(3 * local_width + LANES)[None, :]
    spread_bias = jnp.sum(
        jnp.where(row == jnp.arange(LANES)[None, :], bias_part[None, :], 0.0), axis=1, keepdims=True
    )
    first_grad = jnp.where(
        column == 2 * local_width + local_heads, spread_bias, first_grad
    ).astype(bf16)
    first_sum = scattered(first_grad, groups)
    kv_width = 2 * local_width + LANES
    grad_input1 = (
        dot(grads[:, :kv_width], first_kv, NT)
        + dot(
            jnp.concatenate([dq, grad_gate_pre], axis=1), first_q[:, : 2 * local_width], NT
        )
    ).astype(bf16)
    (tokens_grad,) = exchange(
        after_first, grad_input1, [grad_middle, tokens, gain1], f32, False, 4, "exchange_first"
    )
    (result,) = exchange(after_down, down, [middle], bf16, False, 5, "exchange_down")

    def columns(array, start, width):
        return array[:, :, start : start + width].reshape(share, groups * width)

    key_sum, value_sum = (columns(first_sum, n * local_width, local_width) for n in range(2))
    forget_sum = columns(first_sum, 2 * local_width, local_heads)
    bias_total = first_sum[:local_heads, :, 2 * local_width + local_heads].T.reshape(head_count)
    query_sum = columns(first_sum, kv_width, local_width)
    gate_out_sum, output_total = (
        columns(early_sum, n * local_width, local_width) for n in range(2)
    )
    gate_sum, up_sum, down_sum = (
        columns(second_sum, n * hidden_width, hidden_width) for n in range(3)
    )

    def along(weight, grad):
        return jnp.sum(low(weight).astype(f32) * grad, axis=1)

    gain1_total = (
        along(w_query, query_sum)
        + along(w_key, key_sum)
        + along(w_value, value_sum)
        + along(w_gate_out, gate_out_sum)
        + along(w_forget, forget_sum)
    ) / low(norm1_gain).astype(f32)
    gain2_total = (along(w_gate, gate_sum) + along(w_up, up_sum)) / low(norm2_gain).astype(f32)
    return (
        result,
        tokens_grad,
        gain1_total,
        query_sum,
        key_sum,
        value_sum,
        gate_out_sum,
        forget_sum,
        bias_total,
        output_total,
        gain2_total,
        gate_sum,
        up_sum,
        down_sum,
    )


def solution(mesh):
    both = ("blk", "head")
    matrix, vector = P(both, None), P(both)
    return jax.shard_map(
        body,
        mesh=mesh,
        in_specs=(
            matrix, P("blk"), vector, matrix, matrix, matrix, matrix, matrix, P(), matrix, vector,
            matrix, matrix, matrix, matrix,
        ),
        out_specs=(
            matrix, matrix, vector, matrix, matrix, matrix, matrix, matrix, P(), matrix, vector,
            matrix, matrix, matrix,
        ),
        check_vma=False,
    )
```

```python
import functools

import jax
import jax.numpy as jnp
from jax import lax
from jax.experimental import pallas as pl
from jax.experimental.pallas import tpu as pltpu
from jax.sharding import PartitionSpec as P

epsilon = 1e-06
LANES = 128
Q_TILE = 512
K_TILE = 256
FAR = -1e30
NT = (((1,), (1,)), ((), ()))
NN = (((1,), (0,)), ((), ()))
bf16 = jnp.bfloat16
f32 = jnp.float32


def dot(a, b, dims=NN, **kw):
    return lax.dot_general(a, b, dims, preferred_element_type=f32, **kw)


def passed_along(array, axis, by):
    peers = lax.axis_size(axis)
    pairs = [(i, i + by) for i in range(peers) if 0 <= i + by < peers]
    return lax.ppermute(array, axis, pairs)


def split3(value):
    high = value.astype(bf16)
    rest = value - high.astype(f32)
    mid = rest.astype(bf16)
    low = (rest - mid.astype(f32)).astype(bf16)
    return high, mid, low


def running(value_of, steps, rows, upper):
    place = lax.broadcasted_iota(jnp.int32, (rows, rows), 0)
    other = lax.broadcasted_iota(jnp.int32, (rows, rows), 1)
    tri = jnp.where((other >= place) if upper else (other <= place), 1.0, 0.0).astype(bf16)
    outs = [None] * steps
    carry = jnp.zeros((1, LANES), f32)
    order = range(steps - 1, -1, -1) if upper else range(steps)
    for n in order:
        block = value_of(n)
        total = sum(dot(tri, part) for part in split3(block)) + carry
        outs[n] = total
        carry = total[0:1] if upper else total[rows - 1 : rows]
    return outs, carry


def decay_kernel(local_heads, logf_ref, own_ref, halo_ref):
    rows = 256
    steps = logf_ref.shape[0] // rows
    lane = lax.broadcasted_iota(jnp.int32, (rows, LANES), 1)

    def value_of(n):
        return jnp.where(lane < local_heads, logf_ref[n * rows : (n + 1) * rows, :], 0.0)

    sums, total = running(value_of, steps, rows, False)
    one = jnp.where(lane == 3 * local_heads, 1.0, 0.0)

    def terms(value):
        high, mid, low = split3(value)
        return (
            high.astype(f32)
            + pltpu.roll(mid.astype(f32), local_heads, 1)
            + pltpu.roll(low.astype(f32), 2 * local_heads, 1)
            + one
        ).astype(bf16)

    for n in range(steps):
        own_ref[n * rows : (n + 1) * rows, :] = terms(sums[n])
        halo_ref[n * rows : (n + 1) * rows, :] = terms(sums[n] - total)


def decay_terms(logf, local_heads):
    shape = jax.ShapeDtypeStruct(logf.shape, bf16)
    return pl.pallas_call(
        functools.partial(decay_kernel, local_heads),
        out_shape=(shape, shape),
        name="decay_terms",
    )(logf)


def decay_back_kernel(own_ref, halo_ref, out_ref):
    rows = 256
    steps = own_ref.shape[0] // rows
    own, _ = running(lambda n: own_ref[n * rows : (n + 1) * rows, :], steps, rows, True)
    halo, _ = running(lambda n: halo_ref[n * rows : (n + 1) * rows, :], steps, rows, False)
    for n in range(steps):
        part = slice(n * rows, (n + 1) * rows)
        out_ref[part, :] = own[n] + (halo[n] - halo_ref[part, :])


def decay_back(own, halo):
    return pl.pallas_call(
        decay_back_kernel,
        out_shape=jax.ShapeDtypeStruct(own.shape, f32),
        name="decay_back",
    )(own, halo)


def placing(pair, local_heads, for_query):
    row = lax.broadcasted_iota(jnp.int32, (LANES, LANES), 0)
    col = lax.broadcasted_iota(jnp.int32, (LANES, LANES), 1)
    head = jnp.where(col < 64, 2 * pair + 1, 2 * pair)
    spot = jnp.where(col < 64, col, col - 64)
    term = jnp.where(for_query, spot, spot - 3)
    is_term = (term >= 0) & (term < 3) & (row == term * local_heads + head)
    ones = jnp.where(for_query, spot - 3, spot)
    is_one = (ones >= 0) & (ones < 3) & (row == 3 * local_heads)
    sign = 1.0 if for_query else -1.0
    return (jnp.where(is_term, sign, 0.0) + jnp.where(is_one, 1.0, 0.0)).astype(bf16)


def allowed_pairs(first_key, query_tile, rows, begin_row):
    shape = (K_TILE, Q_TILE)
    key_place = first_key + lax.broadcasted_iota(jnp.int32, shape, 0)
    query_place = rows + query_tile * Q_TILE + lax.broadcasted_iota(jnp.int32, shape, 1)
    return (key_place >= begin_row) & (key_place <= query_place)


def key_range(ranges_ref, query_tile, rows, own):
    count = rows // K_TILE
    base = count if own else 0
    first = jnp.clip(ranges_ref[0, query_tile] - base, 0, count)
    full = jnp.clip(ranges_ref[1, query_tile] - base, first, count)
    return first, full


def key_loops(ranges_ref, query_tile, rows, own, step, carry):
    first, full = key_range(ranges_ref, query_tile, rows, own)
    inside = query_tile * (Q_TILE // K_TILE) if own else rows // K_TILE
    full = jnp.minimum(full, inside)
    carry = lax.fori_loop(first, full, functools.partial(step, True), carry)
    carry = lax.fori_loop(full, inside, functools.partial(step, False), carry)
    if own:
        carry = lax.fori_loop(
            inside, inside + Q_TILE // K_TILE, functools.partial(step, True), carry
        )
    return carry


def tile_of(number, size):
    return pl.ds(pl.multiple_of(number * size, size), size)


def fill_keys(pair, local_heads, first, key_ref, terms_ref, keys):
    place = placing(pair, local_heads, False)
    lane = lax.broadcasted_iota(jnp.int32, (K_TILE, LANES), 1)

    def fill(n, carry):
        here = tile_of(n, K_TILE)
        extra = dot(terms_ref[here, :], place).astype(bf16)
        key = key_ref[here, :]
        keys[0][here, :] = jnp.where(lane < 64, key, extra)
        keys[1][here, :] = jnp.where(lane < 64, extra, key)
        return carry

    lax.fori_loop(first, key_ref.shape[0] // K_TILE, fill, 0)


def query_tiles(q_ref, terms_ref, place, here, scaling):
    lane = lax.broadcasted_iota(jnp.int32, (Q_TILE, LANES), 1)
    extra = dot(terms_ref[here, :], place).astype(bf16)
    query = (q_ref[here, :].astype(f32) * scaling).astype(bf16)
    return jnp.where(lane < 64, query, extra), jnp.where(lane < 64, extra, query)


def attend_kernel(local_heads, own, ranges_ref, q_ref, k_ref, v_ref, t_query_ref, t_key_ref,
                  begin_ref, *refs):
    if own:
        acc_out_ref, state_out_ref, key0, key1, values, acc0, acc1 = refs
    else:
        acc_in_ref, state_in_ref, o_ref, lse_ref, key0, key1, values, acc0, acc1 = refs
    pair = pl.program_id(0)
    rows = q_ref.shape[0]
    base = rows if own else 0
    keys, accs = (key0, key1), (acc0, acc1)
    first, _ = key_range(ranges_ref, 0, rows, own)
    fill_keys(pair, local_heads, first, k_ref, t_key_ref, keys)

    def turn(n, carry):
        values[:, tile_of(n, K_TILE)] = v_ref[tile_of(n, K_TILE), :].T
        return carry

    lax.fori_loop(first, rows // K_TILE, turn, 0)
    place = placing(pair, local_heads, True)

    def query_loop(tile, carry):
        here = tile_of(tile, Q_TILE)
        queries = query_tiles(q_ref, t_query_ref, place, here, 64**-0.5)
        begin_row = begin_ref[0:1, here]
        if own:
            low = jnp.full((1, Q_TILE), FAR, f32)
            zero = jnp.zeros((1, Q_TILE), f32)
            state = (low, zero, low, zero)
            for acc in accs:
                acc[...] = jnp.zeros_like(acc)
        else:
            state = tuple(state_in_ref[n : n + 1, here] for n in range(4))
            for h in range(2):
                accs[h][...] = acc_in_ref[64 * h : 64 * (h + 1), here]

        def step(masked, number, state):
            there = tile_of(number, K_TILE)
            fresh = []
            if masked:
                allowed = allowed_pairs(base + number * K_TILE, tile, rows, begin_row)
            for h in range(2):
                largest, total = state[2 * h], state[2 * h + 1]
                scores = dot(keys[h][there, :], queries[h], NT)
                if masked:
                    scores = jnp.where(allowed, scores, FAR)
                now = jnp.maximum(largest, jnp.max(scores, axis=0, keepdims=True))
                fade = jnp.exp(largest - now)
                weights = jnp.exp(scores - now)
                total = total * fade + jnp.sum(weights, axis=0, keepdims=True)
                accs[h][...] = accs[h][...] * fade + dot(
                    values[64 * h : 64 * (h + 1), there], weights.astype(bf16)
                )
                fresh += [now, total]
            return tuple(fresh)

        state = key_loops(ranges_ref, tile, rows, own, step, state)
        if own:
            for h in range(2):
                acc_out_ref[64 * h : 64 * (h + 1), here] = accs[h][...]
            for n in range(4):
                state_out_ref[n : n + 1, here] = state[n]
        else:
            mixed = jnp.concatenate(
                [accs[h][...] * (1.0 / state[2 * h + 1]) for h in range(2)], axis=0
            )
            o_ref[here, :] = mixed.T.astype(bf16)
            for h in range(2):
                lse_ref[h : h + 1, here] = state[2 * h] + jnp.log(state[2 * h + 1])
        return carry

    lax.fori_loop(0, rows // Q_TILE, query_loop, 0)


def lane_block(rows, offset):
    return pl.BlockSpec((rows, LANES), lambda p, *_: (0, offset + p))


def fixed(shape):
    return pl.BlockSpec(shape, lambda p, *_: (0, 0))


def pair_block(height, rows):
    return pl.BlockSpec((height, rows), lambda p, *_: (p, 0))


def attend(own, ranges, query, key_value, terms, key_terms, begins, local_heads, so_far=()):
    rows = query.shape[0]
    pairs = local_heads // 2
    running_specs = [pair_block(LANES, rows), pair_block(8, rows)]
    running_shape = (
        jax.ShapeDtypeStruct((LANES * pairs, rows), f32),
        jax.ShapeDtypeStruct((8 * pairs, rows), f32),
    )
    final_specs = [lane_block(rows, 0), pair_block(8, rows)]
    final_shape = (
        jax.ShapeDtypeStruct((rows, pairs * LANES), bf16),
        jax.ShapeDtypeStruct((8 * pairs, rows), f32),
    )
    return pl.pallas_call(
        functools.partial(attend_kernel, local_heads, own),
        grid_spec=pltpu.PrefetchScalarGridSpec(
            num_scalar_prefetch=1,
            grid=(pairs,),
            in_specs=[
                lane_block(rows, 0),
                lane_block(rows, 0),
                lane_block(rows, pairs),
                fixed((rows, LANES)),
                fixed((rows, LANES)),
                fixed((8, rows)),
            ]
            + ([] if own else running_specs),
            out_specs=running_specs if own else final_specs,
            scratch_shapes=[
                pltpu.VMEM((rows, LANES), bf16),
                pltpu.VMEM((rows, LANES), bf16),
                pltpu.VMEM((LANES, rows), bf16),
                pltpu.VMEM((64, Q_TILE), f32),
                pltpu.VMEM((64, Q_TILE), f32),
            ],
        ),
        out_shape=running_shape if own else final_shape,
        cost_estimate=pl.CostEstimate(
            flops=40_000_000_000 if own else 10_000_000_000,
            transcendentals=20_000_000,
            bytes_accessed=12_000_000,
        ),
        name="attend_own" if own else "attend_prev",
    )(ranges, query, key_value, key_value, terms, key_terms, begins, *so_far)


def attend_back_kernel(local_heads, own, ranges_ref, q_ref, k_ref, v_ref, t_query_ref, t_key_ref,
                       begin_ref, grad_ref, o_ref, lse_ref, *refs):
    if own:
        dq_in_ref, decay_in_ref, dq_ref, dk_ref, dv_ref, decay_ref = refs[:6]
    else:
        dq_ref, row_decay_ref, dkv_ref, decay_ref = refs[:4]
        dk_ref, dv_ref = dkv_ref.at[0], dkv_ref.at[1]
    key0, key1, key_t0, key_t1, dk0, dk1, dv, dq0, dq1 = refs[-9:]
    pair = pl.program_id(0)
    rows = q_ref.shape[0]
    base = rows if own else 0
    keys, keys_t, dks, dqs = (key0, key1), (key_t0, key_t1), (dk0, dk1), (dq0, dq1)
    first, _ = key_range(ranges_ref, 0, rows, own)
    fill_keys(pair, local_heads, first, k_ref, t_key_ref, keys)

    def turn(n, carry):
        here = tile_of(n, K_TILE)
        for h in range(2):
            keys_t[h][:, here] = keys[h][here, :].T
        return carry

    lax.fori_loop(first, rows // K_TILE, turn, 0)
    for ref in (dk0, dk1, dv):
        ref[...] = jnp.zeros_like(ref)
    place = placing(pair, local_heads, True)
    lane = lax.broadcasted_iota(jnp.int32, (Q_TILE, LANES), 1)
    pick_row = lax.broadcasted_iota(jnp.int32, (8, LANES), 0)
    pick_lane = lax.broadcasted_iota(jnp.int32, (8, LANES), 1)
    pick = jnp.where((pick_lane // 64) == pick_row, 1.0, 0.0)
    sums_ref = decay_ref if own else row_decay_ref

    @pl.when(pair == 0)
    def _():
        if own:
            decay_ref[...] = decay_in_ref[...]
        else:
            decay_ref[...] = jnp.zeros_like(decay_ref)
            row_decay_ref[...] = jnp.zeros_like(row_decay_ref)

    def query_tile(tile):
        here = tile_of(tile, Q_TILE)
        queries = query_tiles(q_ref, t_query_ref, place, here, 64**-0.5)
        begin_row = begin_ref[0:1, here]
        grad = grad_ref[here, :]
        nothing = jnp.zeros_like(grad)
        grads = (jnp.where(lane < 64, grad, nothing), jnp.where(lane < 64, nothing, grad))
        product = grad.astype(f32) * o_ref[here, :].astype(f32)
        inner = dot(pick, product, NT, precision=lax.Precision.HIGHEST)
        for dq in dqs:
            dq[...] = jnp.zeros_like(dq)

        def step(masked, number, state):
            there = tile_of(number, K_TILE)
            if masked:
                allowed = allowed_pairs(base + number * K_TILE, tile, rows, begin_row)
            value = v_ref[there, :]
            value_part = 0.0
            for h in range(2):
                scores = dot(keys[h][there, :], queries[h], NT)
                prob = jnp.exp(scores - lse_ref[h : h + 1, here])
                if masked:
                    prob = jnp.where(allowed, prob, 0.0)
                grad_prob = dot(value, grads[h], NT)
                grad_score = (prob * (grad_prob - inner[h : h + 1, :])).astype(bf16)
                value_part = value_part + dot(prob.astype(bf16), grads[h])
                dks[h][there, :] += dot(grad_score, queries[h])
                dqs[h][...] += dot(keys_t[h][:, there], grad_score)
            dv[there, :] += value_part
            return state

        key_loops(ranges_ref, tile, rows, own, step, 0)
        turned = [dq[...].T for dq in dqs]
        dq_tile = jnp.where(lane < 64, turned[0], turned[1]) * 64**-0.5
        if own:
            dq_tile = dq_tile + dq_in_ref[here, :]
        dq_ref[here, :] = dq_tile.astype(dq_ref.dtype)
        sums = sums_ref[here, :]
        sums = sums + jnp.where(lane == 2 * pair, turned[0][:, 64:65], 0.0)
        sums = sums + jnp.where(lane == 2 * pair + 1, turned[1][:, 0:1], 0.0)
        sums_ref[here, :] = sums

    def query_loop(tile, carry):
        if own:
            query_tile(tile)
        else:
            reaches = key_range(ranges_ref, tile, rows, own)[0] < rows // K_TILE
            pl.when(reaches)(lambda: query_tile(tile))

            @pl.when(jnp.logical_not(reaches))
            def _():
                dq_ref[tile_of(tile, Q_TILE), :] = jnp.zeros((Q_TILE, LANES), dq_ref.dtype)

        return carry

    lax.fori_loop(0, rows // Q_TILE, query_loop, 0)
    sign = -1.0 if own else 1.0

    def finish(n, carry):
        here = tile_of(n, Q_TILE)
        left, right = dk0[here, :], dk1[here, :]
        dk_ref[here, :] = jnp.where(lane < 64, left, right).astype(dk_ref.dtype)
        dv_ref[here, :] = dv[here, :].astype(dv_ref.dtype)
        decay = decay_ref[here, :]
        decay = decay + jnp.where(lane == 2 * pair, sign * left[:, 67:68], 0.0)
        decay = decay + jnp.where(lane == 2 * pair + 1, sign * right[:, 3:4], 0.0)
        decay_ref[here, :] = decay
        return carry

    lax.fori_loop(0, rows // Q_TILE, finish, 0)


def attend_back(
    own, ranges, query, key_value, terms, key_terms, begins, grad, mixed, lse, local_heads,
    so_far=(),
):
    rows = query.shape[0]
    pairs = local_heads // 2
    wide = jax.ShapeDtypeStruct((rows, pairs * LANES), f32)
    sums = jax.ShapeDtypeStruct((rows, LANES), f32)
    if own:
        out_specs = [lane_block(rows, 0)] * 3 + [fixed((rows, LANES))]
        out_shape = (jax.ShapeDtypeStruct(wide.shape, bf16), wide, wide, sums)
    else:
        both = pl.BlockSpec((2, rows, LANES), lambda p, *_: (0, 0, p))
        out_specs = [lane_block(rows, 0), fixed((rows, LANES)), both, fixed((rows, LANES))]
        out_shape = (
            wide, sums, jax.ShapeDtypeStruct((2, rows, pairs * LANES), bf16), sums,
        )
    return pl.pallas_call(
        functools.partial(attend_back_kernel, local_heads, own),
        grid_spec=pltpu.PrefetchScalarGridSpec(
            num_scalar_prefetch=1,
            grid=(pairs,),
            in_specs=[
                lane_block(rows, 0),
                lane_block(rows, 0),
                lane_block(rows, pairs),
                fixed((rows, LANES)),
                fixed((rows, LANES)),
                fixed((8, rows)),
                lane_block(rows, 0),
                lane_block(rows, 0),
                pair_block(8, rows),
            ]
            + ([lane_block(rows, 0), fixed((rows, LANES))] if own else []),
            out_specs=out_specs,
            scratch_shapes=[
                pltpu.VMEM((rows, LANES), bf16),
                pltpu.VMEM((rows, LANES), bf16),
                pltpu.VMEM((LANES, rows), bf16),
                pltpu.VMEM((LANES, rows), bf16),
                pltpu.VMEM((rows, LANES), f32),
                pltpu.VMEM((rows, LANES), f32),
                pltpu.VMEM((rows, LANES), f32),
                pltpu.VMEM((LANES, Q_TILE), f32),
                pltpu.VMEM((LANES, Q_TILE), f32),
            ],
        ),
        out_shape=out_shape,
        cost_estimate=pl.CostEstimate(
            flops=80_000_000_000 if own else 15_000_000_000,
            transcendentals=20_000_000,
            bytes_accessed=25_000_000,
        ),
        name="attend_back_own" if own else "attend_back_prev",
    )(
        ranges, query, key_value, key_value, terms, key_terms, begins, grad, mixed, lse, *so_far
    )


PIECES = 4


def partners():
    me = lax.axis_index("head")
    near = me + 1 - 2 * (me % 2)
    far = (me + 2) % 4
    cross = (near + 2) % 4
    return me, near, far, cross


def greet(*others):
    barrier = pltpu.get_barrier_semaphore()
    for other in others:
        pl.semaphore_signal(
            barrier, inc=1, device_id={"head": other}, device_id_type=pl.DeviceIdType.MESH
        )
    pl.semaphore_wait(barrier, len(others))


def remote(source, target, send, receive, other):
    return pltpu.make_async_remote_copy(
        src_ref=source,
        dst_ref=target,
        send_sem=send,
        recv_sem=receive,
        device_id={"head": other},
        device_id_type=pl.DeviceIdType.MESH,
    )


def rows_of(ref, shard, piece, size):
    span = size // PIECES
    start = pl.multiple_of(shard * size + piece * span, span)
    return ref.at[pl.ds(start, span), :]


def spread_piece(source_of, all_ref, size, sems, piece):
    me, near, far, _ = partners()
    far_send, far_recv, near_send, near_recv, _, _, own = sems
    copies = (
        remote(source_of(piece), rows_of(all_ref, me, piece, size), far_send.at[piece], far_recv.at[piece], far),
        remote(source_of(piece), rows_of(all_ref, me, piece, size), near_send.at[piece], near_recv.at[piece], near),
        pltpu.make_async_copy(source_of(piece), rows_of(all_ref, me, piece, size), own.at[piece]),
    )
    for copy in copies:
        copy.start()
    return copies


def hand_on(all_ref, size, sems, sent):
    me, near, far, cross = partners()
    far_send, far_recv, near_send, near_recv, on_send, on_recv, own = sems
    passed = []
    for piece in range(PIECES):
        there = rows_of(all_ref, far, piece, size)
        remote(there, there, far_send.at[piece], far_recv.at[piece], far).wait_recv()
        copy = remote(there, there, on_send.at[piece], on_recv.at[piece], near)
        copy.start()
        passed.append(copy)
    for piece in range(PIECES):
        to_far, to_near, local = sent[piece]
        to_far.wait_send()
        to_near.wait_send()
        local.wait()
        passed[piece].wait_send()
        there = rows_of(all_ref, near, piece, size)
        remote(there, there, near_send.at[piece], near_recv.at[piece], near).wait_recv()
        there = rows_of(all_ref, cross, piece, size)
        remote(there, there, on_send.at[piece], on_recv.at[piece], near).wait_recv()


def gather_sems():
    return [pltpu.SemaphoreType.DMA((PIECES,)) for _ in range(7)]


def gather_kernel(mine_ref, all_ref, *sems):
    size = mine_ref.shape[0]
    _, near, far, _ = partners()
    greet(near, far)
    sent = [
        spread_piece(lambda n: rows_of(mine_ref, 0, n, size), all_ref, size, sems, piece)
        for piece in range(PIECES)
    ]
    hand_on(all_ref, size, sems, sent)


def gather_heads(mine, number):
    rows, width = mine.shape
    return pl.pallas_call(
        gather_kernel,
        in_specs=[pl.BlockSpec(memory_space=pl.ANY)],
        out_specs=pl.BlockSpec(memory_space=pl.ANY),
        out_shape=jax.ShapeDtypeStruct((4 * rows, width), mine.dtype),
        scratch_shapes=gather_sems(),
        compiler_params=pltpu.CompilerParams(collective_id=number, has_side_effects=True),
        cost_estimate=pl.CostEstimate(
            flops=30_000_000_000, transcendentals=0, bytes_accessed=8_000_000
        ),
        name="gather_heads",
    )(mine)


def exchange_kernel(local, extras, gather, *refs):
    part_ref, rest = refs[0], refs[1:]
    extra_refs, rest = rest[:extras], rest[extras:]
    out_ref, rest = rest[0], rest[1:]
    if gather:
        all_ref, rest = rest[0], rest[1:]
    near_buf, turn_buf, far_buf, rest = rest[0], rest[1], rest[2], rest[3:]
    near_send, near_recv, far_send, far_recv = rest[:4]
    if gather:
        payload, sems = rest[4], rest[5:]
    size = out_ref.shape[0]
    span = size // PIECES
    me, near, far, cross = partners()
    greet(near, far)
    near_copies = []
    for which, shard in ((0, cross), (1, near)):
        for piece in range(PIECES):
            copy = remote(
                rows_of(part_ref, shard, piece, size),
                near_buf.at[which, pl.ds(piece * span, span), :],
                near_send.at[which, piece],
                near_recv.at[which, piece],
                near,
            )
            copy.start()
            near_copies.append(copy)
    far_copies = []
    for piece in range(PIECES):
        here = slice(piece * span, (piece + 1) * span)
        near_copies[piece].wait_recv()
        turn_buf[here, :] = (
            rows_of(part_ref, far, piece, size)[...].astype(f32) + near_buf[0, here, :].astype(f32)
        ).astype(bf16)
        copy = remote(
            turn_buf.at[pl.ds(piece * span, span), :],
            far_buf.at[pl.ds(piece * span, span), :],
            far_send.at[piece],
            far_recv.at[piece],
            far,
        )
        copy.start()
        far_copies.append(copy)
    sent = []
    for piece in range(PIECES):
        here = slice(piece * span, (piece + 1) * span)
        near_copies[PIECES + piece].wait_recv()
        far_copies[piece].wait_recv()
        total = (
            rows_of(part_ref, me, piece, size)[...].astype(f32)
            + near_buf[1, here, :].astype(f32)
            + far_buf[here, :].astype(f32)
        )
        result, share = local(total, here, *extra_refs)
        out_ref[here, :] = result.astype(out_ref.dtype)
        if gather:
            payload[here, :] = share.astype(bf16)
            sent.append(
                spread_piece(
                    lambda n: payload.at[pl.ds(n * span, span), :], all_ref, size, sems, piece
                )
            )
    if gather:
        hand_on(all_ref, size, sems, sent)
    for copy in near_copies + far_copies:
        copy.wait_send()


def exchange(local, part, extras, out_type, gather, number, name):
    rows, width = part.shape
    size = rows // 4
    out_shape = [jax.ShapeDtypeStruct((size, width), out_type)]
    out_specs = [pl.BlockSpec(memory_space=pltpu.VMEM)]
    scratch = [
        pltpu.VMEM((2, size, width), bf16),
        pltpu.VMEM((size, width), bf16),
        pltpu.VMEM((size, width), bf16),
        pltpu.SemaphoreType.DMA((2, PIECES)),
        pltpu.SemaphoreType.DMA((2, PIECES)),
        pltpu.SemaphoreType.DMA((PIECES,)),
        pltpu.SemaphoreType.DMA((PIECES,)),
    ]
    if gather:
        out_shape.append(jax.ShapeDtypeStruct((rows, width), bf16))
        out_specs.append(pl.BlockSpec(memory_space=pl.ANY))
        scratch += [pltpu.VMEM((size, width), bf16)] + gather_sems()
    return pl.pallas_call(
        functools.partial(exchange_kernel, local, len(extras), gather),
        in_specs=[pl.BlockSpec(memory_space=pltpu.VMEM)] * (1 + len(extras)),
        out_specs=out_specs,
        out_shape=out_shape,
        scratch_shapes=scratch,
        compiler_params=pltpu.CompilerParams(collective_id=number, has_side_effects=True),
        cost_estimate=pl.CostEstimate(
            flops=60_000_000_000 if gather else 35_000_000_000,
            transcendentals=0,
            bytes_accessed=16_000_000,
        ),
        name=name,
    )(part, *extras)


def inverse_rms(value):
    return lax.rsqrt(jnp.mean(value * value, axis=1, keepdims=True) + epsilon)


def through_norm(grad, value):
    factor = inverse_rms(value)
    normed = value * factor
    return factor * (grad - normed * jnp.mean(grad * normed, axis=1, keepdims=True))


def after_attention(total, here, tokens_ref, gain_ref):
    middle = tokens_ref[here, :].astype(f32) + total
    return middle, middle * inverse_rms(middle) * gain_ref[0:1, :]


def after_hidden(total, here, cotangent_ref, middle_ref, gain_ref):
    grad = cotangent_ref[here, :].astype(f32) + through_norm(
        total * gain_ref[0:1, :], middle_ref[here, :]
    )
    return grad, grad


def after_first(total, here, grad_ref, tokens_ref, gain_ref):
    grad = grad_ref[here, :] + through_norm(
        total * gain_ref[0:1, :], tokens_ref[here, :].astype(f32)
    )
    return grad, None


def after_down(total, here, middle_ref):
    return middle_ref[here, :] + total, None


def over_tokens(operand, other_side):
    return lax.dot_general(
        operand, other_side, (((0,), (0,)), ((), ())), preferred_element_type=f32
    )


def sent_columns(pieces, groups):
    packed = jnp.concatenate(
        [piece.reshape(piece.shape[0], groups, -1) for piece in pieces], axis=2
    )
    mine = lax.all_to_all(packed, "head", split_axis=1, concat_axis=0, tiled=True)
    return mine.reshape(mine.shape[0], mine.shape[2])


def all_rows(mine):
    return lax.all_gather(mine, "blk", axis=0, tiled=True)


def row_sums(grad):
    return lax.psum_scatter(grad, "blk", scatter_dimension=0, tiled=True)


def own_rows(summed, groups):
    rows, columns = summed.shape
    parts = lax.all_to_all(
        summed.reshape(groups, rows // groups, columns), "head", split_axis=0, concat_axis=0
    )
    return jnp.swapaxes(parts, 0, 1).astype(f32)


def body(
    tokens,
    segment,
    norm1_gain,
    w_query,
    w_key,
    w_value,
    w_gate_out,
    w_forget,
    forget_bias,
    w_output,
    norm2_gain,
    w_gate,
    w_up,
    w_down,
    cotangent,
):
    token_rows, model_width = tokens.shape
    groups = lax.axis_size("head")
    head_count = forget_bias.shape[0]
    local_heads = head_count // groups
    local_width = model_width // groups
    hidden_width = w_gate.shape[1] // groups
    rows = token_rows * groups
    share = w_query.shape[0]
    group = lax.axis_index("head")

    low = lambda array: array.astype(bf16)
    spread = lambda gain: jnp.broadcast_to(low(gain)[:, None, None], (share, groups, 1))
    forget_low = low(w_forget).reshape(share, groups, local_heads)
    rest = LANES - local_heads - 2
    small = jnp.concatenate(
        [forget_low, spread(norm1_gain), spread(norm2_gain), jnp.zeros((share, groups, rest), bf16)],
        axis=2,
    )
    mine_kv = sent_columns([low(w_key), low(w_value), small], groups)
    first_kv = all_rows(mine_kv)
    mine_q = sent_columns([low(w_query), low(w_gate_out), low(w_output)], groups)
    first_q = all_rows(mine_q)
    tokens_all = gather_heads(tokens, 0)
    output_weight = first_q[:, 2 * local_width :]

    segment_plus = segment + 1
    earlier_segment = passed_along(segment_plus, "blk", 1)
    window = jnp.concatenate([earlier_segment, segment_plus])
    begins = jnp.sum(
        (window[:, None] < segment_plus[None, :]).astype(jnp.int32), axis=0
    )
    tiles = begins.reshape(rows // Q_TILE, Q_TILE)
    ranges = jnp.stack([tiles[:, 0] // K_TILE, (tiles[:, -1] + K_TILE - 1) // K_TILE])
    begins = jnp.broadcast_to(begins[None, :], (8, rows))

    def gain_rows(column):
        gain = first_kv[:, 2 * local_width + local_heads + column].astype(f32)
        return jnp.broadcast_to(gain[None, :], (8, model_width))

    gain1, gain2 = gain_rows(0), gain_rows(1)
    wide_all = tokens_all.astype(f32)
    input1 = (wide_all * inverse_rms(wide_all) * gain1[0:1]).astype(bf16)
    key_value = dot(input1, first_kv[:, : 2 * local_width]).astype(bf16)
    earlier_kv = passed_along(key_value, "blk", 1)
    ahead = lax.optimization_barrier((low(w_gate), low(w_up), low(w_down), key_value))
    second = all_rows(sent_columns(ahead[:3], groups))
    bias = lax.dynamic_slice_in_dim(forget_bias, group * local_heads, local_heads, 0)
    bias = jnp.pad(bias, (0, LANES - local_heads))
    forget = dot(input1, first_kv[:, 2 * local_width :]) + bias[None, :]
    forget = forget.astype(bf16).astype(f32)
    terms, halo_terms = decay_terms(jax.nn.log_sigmoid(forget), local_heads)
    earlier_terms = passed_along(halo_terms, "blk", 1)
    query = dot(input1, first_q[:, :local_width]).astype(bf16)
    gate_raw = dot(input1, first_q[:, local_width : 2 * local_width])

    so_far = attend(True, ranges, query, key_value, terms, terms, begins, local_heads)
    attended, lse = attend(
        False, ranges, query, earlier_kv, terms, earlier_terms, begins, local_heads, so_far
    )
    opened = jax.nn.sigmoid(gate_raw)
    attended_wide = attended.astype(f32)
    gated = (opened * attended_wide).astype(bf16)
    branch = dot(gated, output_weight, NT).astype(bf16)
    middle, input2 = exchange(
        after_attention, branch, [tokens, gain2], f32, True, 2, "exchange_middle"
    )
    middle, input2, cotangent_late = lax.optimization_barrier((middle, input2, cotangent))
    cotangent_all = gather_heads(cotangent_late, 1)
    gate_act = dot(input2, second[:, :hidden_width])
    up_act = dot(input2, second[:, hidden_width : 2 * hidden_width])
    opening = jax.nn.sigmoid(gate_act)
    hidden = (gate_act * opening * up_act).astype(bf16)
    down = dot(hidden, second[:, 2 * hidden_width :], NT).astype(bf16)
    grad_hidden = dot(cotangent_all, second[:, 2 * hidden_width :])
    grad_gate_act = (grad_hidden * up_act * opening * (1.0 + gate_act * (1.0 - opening))).astype(
        bf16
    )
    grad_up_act = (grad_hidden * gate_act * opening).astype(bf16)
    grad_act = jnp.concatenate([grad_gate_act, grad_up_act], axis=1)
    grad_input2 = dot(grad_act, second[:, : 2 * hidden_width], NT).astype(bf16)
    second_grad = jnp.concatenate(
        [over_tokens(input2, grad_act).astype(bf16), over_tokens(cotangent_all, hidden).astype(bf16)],
        axis=1,
    )
    second_grad, grad_input2 = lax.optimization_barrier((second_grad, grad_input2))
    second_part = row_sums(second_grad)
    grad_middle, grad_branch = exchange(
        after_hidden, grad_input2, [cotangent, middle, gain2], f32, True, 3, "exchange_hidden"
    )

    grad_gated = dot(grad_branch, output_weight)
    grad_attended = (grad_gated * opened).astype(bf16)
    grad_gate_pre = (grad_gated * attended_wide * opened * (1.0 - opened)).astype(bf16)
    dq_prev, rows_prev, dkv_prev, decay_prev = attend_back(
        False, ranges, query, earlier_kv, terms, earlier_terms, begins, grad_attended, attended,
        lse, local_heads,
    )
    dkv_later = passed_along(dkv_prev, "blk", -1)
    decay_later = passed_along(decay_prev[:, :8], "blk", -1)
    decay_later = jnp.pad(decay_later, ((0, 0), (0, LANES - 8)))
    dq, dk_own, dv_own, decay_own = attend_back(
        True, ranges, query, key_value, terms, terms, begins, grad_attended, attended,
        lse, local_heads, (dq_prev, rows_prev),
    )
    dk = (dk_own + dkv_later[0].astype(f32)).astype(bf16)
    dv = (dv_own + dkv_later[1].astype(f32)).astype(bf16)
    logf_grad = decay_back(decay_own, decay_later)
    forget_grad = jnp.where(
        jnp.arange(LANES)[None, :] < local_heads, logf_grad * jax.nn.sigmoid(-forget), 0.0
    ).astype(bf16)
    grads = jnp.concatenate([dk, dv, forget_grad, dq], axis=1)
    first_grad = over_tokens(input1, grads)
    bias_part = jnp.sum(forget_grad.astype(f32), axis=0)
    row = jnp.arange(model_width)[:, None] % share
    column = jnp.arange(3 * local_width + LANES)[None, :]
    spread_bias = jnp.sum(
        jnp.where(row == jnp.arange(LANES)[None, :], bias_part[None, :], 0.0), axis=1, keepdims=True
    )
    first_grad = jnp.where(column == 2 * local_width + local_heads, spread_bias, first_grad)
    first_grad = jnp.concatenate(
        [
            first_grad.astype(bf16),
            over_tokens(input1, grad_gate_pre).astype(bf16),
            over_tokens(grad_branch, gated).astype(bf16),
        ],
        axis=1,
    )
    first_grad, second_part = lax.optimization_barrier((first_grad, second_part))
    first_sum = own_rows(row_sums(first_grad), groups)
    second_sum = own_rows(second_part, groups)
    kv_width = 2 * local_width + LANES
    grad_input1 = (
        dot(grads[:, :kv_width], first_kv, NT)
        + dot(
            jnp.concatenate([dq, grad_gate_pre], axis=1), first_q[:, : 2 * local_width], NT
        )
    ).astype(bf16)
    (tokens_grad,) = exchange(
        after_first, grad_input1, [grad_middle, tokens, gain1], f32, False, 4, "exchange_first"
    )
    (result,) = exchange(after_down, down, [middle], bf16, False, 5, "exchange_down")

    def columns(array, start, width):
        return array[:, :, start : start + width].reshape(share, groups * width)

    key_sum, value_sum = (columns(first_sum, n * local_width, local_width) for n in range(2))
    forget_sum = columns(first_sum, 2 * local_width, local_heads)
    bias_total = first_sum[:local_heads, :, 2 * local_width + local_heads].T.reshape(head_count)
    query_sum, gate_out_sum, output_total = (
        columns(first_sum, kv_width + n * local_width, local_width) for n in range(3)
    )
    gate_sum, up_sum, down_sum = (
        columns(second_sum, n * hidden_width, hidden_width) for n in range(3)
    )

    def along(weight, grad):
        return jnp.sum(low(weight).astype(f32) * grad, axis=1)

    gain1_total = (
        along(w_query, query_sum)
        + along(w_key, key_sum)
        + along(w_value, value_sum)
        + along(w_gate_out, gate_out_sum)
        + along(w_forget, forget_sum)
    ) / low(norm1_gain).astype(f32)
    gain2_total = (along(w_gate, gate_sum) + along(w_up, up_sum)) / low(norm2_gain).astype(f32)
    return (
        result,
        tokens_grad,
        gain1_total,
        query_sum,
        key_sum,
        value_sum,
        gate_out_sum,
        forget_sum,
        bias_total,
        output_total,
        gain2_total,
        gate_sum,
        up_sum,
        down_sum,
    )


def solution(mesh):
    both = ("blk", "head")
    matrix, vector = P(both, None), P(both)
    return jax.shard_map(
        body,
        mesh=mesh,
        in_specs=(
            matrix, P("blk"), vector, matrix, matrix, matrix, matrix, matrix, P(), matrix, vector,
            matrix, matrix, matrix, matrix,
        ),
        out_specs=(
            matrix, matrix, vector, matrix, matrix, matrix, matrix, matrix, P(), matrix, vector,
            matrix, matrix, matrix,
        ),
        check_vma=False,
    )
```

```python
import functools

import jax
import jax.numpy as jnp
from jax import lax
from jax.experimental import pallas as pl
from jax.experimental.pallas import tpu as pltpu
from jax.sharding import PartitionSpec as P

epsilon = 1e-06
LANES = 128
Q_TILE = 512
K_TILE = 256
FAR = -1e30
NT = (((1,), (1,)), ((), ()))
NN = (((1,), (0,)), ((), ()))
bf16 = jnp.bfloat16
f32 = jnp.float32


def dot(a, b, dims=NN, **kw):
    return lax.dot_general(a, b, dims, preferred_element_type=f32, **kw)


def passed_along(array, axis, by):
    peers = lax.axis_size(axis)
    pairs = [(i, i + by) for i in range(peers) if 0 <= i + by < peers]
    return lax.ppermute(array, axis, pairs)


def split3(value):
    high = value.astype(bf16)
    rest = value - high.astype(f32)
    mid = rest.astype(bf16)
    low = (rest - mid.astype(f32)).astype(bf16)
    return high, mid, low


def running(value_of, steps, rows, upper):
    place = lax.broadcasted_iota(jnp.int32, (rows, rows), 0)
    other = lax.broadcasted_iota(jnp.int32, (rows, rows), 1)
    tri = jnp.where((other >= place) if upper else (other <= place), 1.0, 0.0).astype(bf16)
    outs = [None] * steps
    carry = jnp.zeros((1, LANES), f32)
    order = range(steps - 1, -1, -1) if upper else range(steps)
    for n in order:
        block = value_of(n)
        total = sum(dot(tri, part) for part in split3(block)) + carry
        outs[n] = total
        carry = total[0:1] if upper else total[rows - 1 : rows]
    return outs, carry


def decay_kernel(local_heads, logf_ref, own_ref, halo_ref):
    rows = 256
    steps = logf_ref.shape[0] // rows
    lane = lax.broadcasted_iota(jnp.int32, (rows, LANES), 1)

    def value_of(n):
        return jnp.where(lane < local_heads, logf_ref[n * rows : (n + 1) * rows, :], 0.0)

    sums, total = running(value_of, steps, rows, False)
    one = jnp.where(lane == 3 * local_heads, 1.0, 0.0)

    def terms(value):
        high, mid, low = split3(value)
        return (
            high.astype(f32)
            + pltpu.roll(mid.astype(f32), local_heads, 1)
            + pltpu.roll(low.astype(f32), 2 * local_heads, 1)
            + one
        ).astype(bf16)

    for n in range(steps):
        own_ref[n * rows : (n + 1) * rows, :] = terms(sums[n])
        halo_ref[n * rows : (n + 1) * rows, :] = terms(sums[n] - total)


def decay_terms(logf, local_heads):
    shape = jax.ShapeDtypeStruct(logf.shape, bf16)
    return pl.pallas_call(
        functools.partial(decay_kernel, local_heads),
        out_shape=(shape, shape),
        name="decay_terms",
    )(logf)


def decay_back_kernel(own_ref, halo_ref, out_ref):
    rows = 256
    steps = own_ref.shape[0] // rows
    own, _ = running(lambda n: own_ref[n * rows : (n + 1) * rows, :], steps, rows, True)
    halo, _ = running(lambda n: halo_ref[n * rows : (n + 1) * rows, :], steps, rows, False)
    for n in range(steps):
        part = slice(n * rows, (n + 1) * rows)
        out_ref[part, :] = own[n] + (halo[n] - halo_ref[part, :])


def decay_back(own, halo):
    return pl.pallas_call(
        decay_back_kernel,
        out_shape=jax.ShapeDtypeStruct(own.shape, f32),
        name="decay_back",
    )(own, halo)


def placing(pair, local_heads, for_query):
    row = lax.broadcasted_iota(jnp.int32, (LANES, LANES), 0)
    col = lax.broadcasted_iota(jnp.int32, (LANES, LANES), 1)
    head = jnp.where(col < 64, 2 * pair + 1, 2 * pair)
    spot = jnp.where(col < 64, col, col - 64)
    term = jnp.where(for_query, spot, spot - 3)
    is_term = (term >= 0) & (term < 3) & (row == term * local_heads + head)
    ones = jnp.where(for_query, spot - 3, spot)
    is_one = (ones >= 0) & (ones < 3) & (row == 3 * local_heads)
    sign = 1.0 if for_query else -1.0
    return (jnp.where(is_term, sign, 0.0) + jnp.where(is_one, 1.0, 0.0)).astype(bf16)


def allowed_pairs(first_key, query_tile, rows, begin_row):
    shape = (K_TILE, Q_TILE)
    key_place = first_key + lax.broadcasted_iota(jnp.int32, shape, 0)
    query_place = rows + query_tile * Q_TILE + lax.broadcasted_iota(jnp.int32, shape, 1)
    return (key_place >= begin_row) & (key_place <= query_place)


def key_range(ranges_ref, query_tile, rows, own):
    count = rows // K_TILE
    base = count if own else 0
    first = jnp.clip(ranges_ref[0, query_tile] - base, 0, count)
    full = jnp.clip(ranges_ref[1, query_tile] - base, first, count)
    return first, full


def key_loops(ranges_ref, query_tile, rows, own, step, carry):
    first, full = key_range(ranges_ref, query_tile, rows, own)
    inside = query_tile * (Q_TILE // K_TILE) if own else rows // K_TILE
    full = jnp.minimum(full, inside)
    carry = lax.fori_loop(first, full, functools.partial(step, True), carry)
    carry = lax.fori_loop(full, inside, functools.partial(step, False), carry)
    if own:
        carry = lax.fori_loop(
            inside, inside + Q_TILE // K_TILE, functools.partial(step, True), carry
        )
    return carry


def tile_of(number, size):
    return pl.ds(pl.multiple_of(number * size, size), size)


def fill_keys(pair, local_heads, first, key_ref, terms_ref, keys):
    place = placing(pair, local_heads, False)
    lane = lax.broadcasted_iota(jnp.int32, (K_TILE, LANES), 1)

    def fill(n, carry):
        here = tile_of(n, K_TILE)
        extra = dot(terms_ref[here, :], place).astype(bf16)
        key = key_ref[here, :]
        keys[0][here, :] = jnp.where(lane < 64, key, extra)
        keys[1][here, :] = jnp.where(lane < 64, extra, key)
        return carry

    lax.fori_loop(first, key_ref.shape[0] // K_TILE, fill, 0)


def query_tiles(q_ref, terms_ref, place, here, scaling):
    lane = lax.broadcasted_iota(jnp.int32, (Q_TILE, LANES), 1)
    extra = dot(terms_ref[here, :], place).astype(bf16)
    query = (q_ref[here, :].astype(f32) * scaling).astype(bf16)
    return jnp.where(lane < 64, query, extra), jnp.where(lane < 64, extra, query)


def attend_kernel(local_heads, own, ranges_ref, q_ref, k_ref, v_ref, t_query_ref, t_key_ref,
                  begin_ref, *refs):
    if own:
        acc_out_ref, state_out_ref, key0, key1, values, acc0, acc1 = refs
    else:
        acc_in_ref, state_in_ref, o_ref, lse_ref, key0, key1, values, acc0, acc1 = refs
    pair = pl.program_id(0)
    rows = q_ref.shape[0]
    base = rows if own else 0
    keys, accs = (key0, key1), (acc0, acc1)
    first, _ = key_range(ranges_ref, 0, rows, own)
    fill_keys(pair, local_heads, first, k_ref, t_key_ref, keys)

    def turn(n, carry):
        values[:, tile_of(n, K_TILE)] = v_ref[tile_of(n, K_TILE), :].T
        return carry

    lax.fori_loop(first, rows // K_TILE, turn, 0)
    place = placing(pair, local_heads, True)

    def query_loop(tile, carry):
        here = tile_of(tile, Q_TILE)
        queries = query_tiles(q_ref, t_query_ref, place, here, 64**-0.5)
        begin_row = begin_ref[0:1, here]
        if own:
            low = jnp.full((1, Q_TILE), FAR, f32)
            zero = jnp.zeros((1, Q_TILE), f32)
            state = (low, zero, low, zero)
            for acc in accs:
                acc[...] = jnp.zeros_like(acc)
        else:
            state = tuple(state_in_ref[n : n + 1, here] for n in range(4))
            for h in range(2):
                accs[h][...] = acc_in_ref[64 * h : 64 * (h + 1), here]

        def step(masked, number, state):
            there = tile_of(number, K_TILE)
            fresh = []
            if masked:
                allowed = allowed_pairs(base + number * K_TILE, tile, rows, begin_row)
            for h in range(2):
                largest, total = state[2 * h], state[2 * h + 1]
                scores = dot(keys[h][there, :], queries[h], NT)
                if masked:
                    scores = jnp.where(allowed, scores, FAR)
                now = jnp.maximum(largest, jnp.max(scores, axis=0, keepdims=True))
                fade = jnp.exp(largest - now)
                weights = jnp.exp(scores - now)
                total = total * fade + jnp.sum(weights, axis=0, keepdims=True)
                accs[h][...] = accs[h][...] * fade + dot(
                    values[64 * h : 64 * (h + 1), there], weights.astype(bf16)
                )
                fresh += [now, total]
            return tuple(fresh)

        state = key_loops(ranges_ref, tile, rows, own, step, state)
        if own:
            for h in range(2):
                acc_out_ref[64 * h : 64 * (h + 1), here] = accs[h][...]
            for n in range(4):
                state_out_ref[n : n + 1, here] = state[n]
        else:
            mixed = jnp.concatenate(
                [accs[h][...] * (1.0 / state[2 * h + 1]) for h in range(2)], axis=0
            )
            o_ref[here, :] = mixed.T.astype(bf16)
            for h in range(2):
                lse_ref[h : h + 1, here] = state[2 * h] + jnp.log(state[2 * h + 1])
        return carry

    lax.fori_loop(0, rows // Q_TILE, query_loop, 0)


def lane_block(rows, offset):
    return pl.BlockSpec((rows, LANES), lambda p, *_: (0, offset + p))


def fixed(shape):
    return pl.BlockSpec(shape, lambda p, *_: (0, 0))


def pair_block(height, rows):
    return pl.BlockSpec((height, rows), lambda p, *_: (p, 0))


def attend(own, ranges, query, key_value, terms, key_terms, begins, local_heads, so_far=()):
    rows = query.shape[0]
    pairs = local_heads // 2
    running_specs = [pair_block(LANES, rows), pair_block(8, rows)]
    running_shape = (
        jax.ShapeDtypeStruct((LANES * pairs, rows), f32),
        jax.ShapeDtypeStruct((8 * pairs, rows), f32),
    )
    final_specs = [lane_block(rows, 0), pair_block(8, rows)]
    final_shape = (
        jax.ShapeDtypeStruct((rows, pairs * LANES), bf16),
        jax.ShapeDtypeStruct((8 * pairs, rows), f32),
    )
    return pl.pallas_call(
        functools.partial(attend_kernel, local_heads, own),
        grid_spec=pltpu.PrefetchScalarGridSpec(
            num_scalar_prefetch=1,
            grid=(pairs,),
            in_specs=[
                lane_block(rows, 0),
                lane_block(rows, 0),
                lane_block(rows, pairs),
                fixed((rows, LANES)),
                fixed((rows, LANES)),
                fixed((8, rows)),
            ]
            + ([] if own else running_specs),
            out_specs=running_specs if own else final_specs,
            scratch_shapes=[
                pltpu.VMEM((rows, LANES), bf16),
                pltpu.VMEM((rows, LANES), bf16),
                pltpu.VMEM((LANES, rows), bf16),
                pltpu.VMEM((64, Q_TILE), f32),
                pltpu.VMEM((64, Q_TILE), f32),
            ],
        ),
        out_shape=running_shape if own else final_shape,
        cost_estimate=pl.CostEstimate(
            flops=40_000_000_000 if own else 10_000_000_000,
            transcendentals=20_000_000,
            bytes_accessed=12_000_000,
        ),
        name="attend_own" if own else "attend_prev",
    )(ranges, query, key_value, key_value, terms, key_terms, begins, *so_far)


def attend_back_kernel(local_heads, own, ranges_ref, q_ref, k_ref, v_ref, t_query_ref, t_key_ref,
                       begin_ref, grad_ref, o_ref, lse_ref, *refs):
    if own:
        dq_in_ref, decay_in_ref, dq_ref, dk_ref, dv_ref, decay_ref = refs[:6]
    else:
        dq_ref, row_decay_ref, dkv_ref, decay_ref = refs[:4]
        dk_ref, dv_ref = dkv_ref.at[0], dkv_ref.at[1]
    key0, key1, key_t0, key_t1, dk0, dk1, dv, dq0, dq1 = refs[-9:]
    pair = pl.program_id(0)
    rows = q_ref.shape[0]
    base = rows if own else 0
    keys, keys_t, dks, dqs = (key0, key1), (key_t0, key_t1), (dk0, dk1), (dq0, dq1)
    first, _ = key_range(ranges_ref, 0, rows, own)
    fill_keys(pair, local_heads, first, k_ref, t_key_ref, keys)

    def turn(n, carry):
        here = tile_of(n, K_TILE)
        for h in range(2):
            keys_t[h][:, here] = keys[h][here, :].T
        return carry

    lax.fori_loop(first, rows // K_TILE, turn, 0)
    for ref in (dk0, dk1, dv):
        ref[...] = jnp.zeros_like(ref)
    place = placing(pair, local_heads, True)
    lane = lax.broadcasted_iota(jnp.int32, (Q_TILE, LANES), 1)
    pick_row = lax.broadcasted_iota(jnp.int32, (8, LANES), 0)
    pick_lane = lax.broadcasted_iota(jnp.int32, (8, LANES), 1)
    pick = jnp.where((pick_lane // 64) == pick_row, 1.0, 0.0)
    sums_ref = decay_ref if own else row_decay_ref

    @pl.when(pair == 0)
    def _():
        if own:
            decay_ref[...] = decay_in_ref[...]
        else:
            decay_ref[...] = jnp.zeros_like(decay_ref)
            row_decay_ref[...] = jnp.zeros_like(row_decay_ref)

    def query_tile(tile):
        here = tile_of(tile, Q_TILE)
        queries = query_tiles(q_ref, t_query_ref, place, here, 64**-0.5)
        begin_row = begin_ref[0:1, here]
        grad = grad_ref[here, :]
        nothing = jnp.zeros_like(grad)
        grads = (jnp.where(lane < 64, grad, nothing), jnp.where(lane < 64, nothing, grad))
        product = grad.astype(f32) * o_ref[here, :].astype(f32)
        inner = dot(pick, product, NT, precision=lax.Precision.HIGHEST)
        for dq in dqs:
            dq[...] = jnp.zeros_like(dq)

        def step(masked, number, state):
            there = tile_of(number, K_TILE)
            if masked:
                allowed = allowed_pairs(base + number * K_TILE, tile, rows, begin_row)
            value = v_ref[there, :]
            value_part = 0.0
            for h in range(2):
                scores = dot(keys[h][there, :], queries[h], NT)
                prob = jnp.exp(scores - lse_ref[h : h + 1, here])
                if masked:
                    prob = jnp.where(allowed, prob, 0.0)
                grad_prob = dot(value, grads[h], NT)
                grad_score = (prob * (grad_prob - inner[h : h + 1, :])).astype(bf16)
                value_part = value_part + dot(prob.astype(bf16), grads[h])
                dks[h][there, :] += dot(grad_score, queries[h])
                dqs[h][...] += dot(keys_t[h][:, there], grad_score)
            dv[there, :] += value_part
            return state

        key_loops(ranges_ref, tile, rows, own, step, 0)
        turned = [dq[...].T for dq in dqs]
        dq_tile = jnp.where(lane < 64, turned[0], turned[1]) * 64**-0.5
        if own:
            dq_tile = dq_tile + dq_in_ref[here, :]
        dq_ref[here, :] = dq_tile.astype(dq_ref.dtype)
        sums = sums_ref[here, :]
        sums = sums + jnp.where(lane == 2 * pair, turned[0][:, 64:65], 0.0)
        sums = sums + jnp.where(lane == 2 * pair + 1, turned[1][:, 0:1], 0.0)
        sums_ref[here, :] = sums

    def query_loop(tile, carry):
        if own:
            query_tile(tile)
        else:
            reaches = key_range(ranges_ref, tile, rows, own)[0] < rows // K_TILE
            pl.when(reaches)(lambda: query_tile(tile))

            @pl.when(jnp.logical_not(reaches))
            def _():
                dq_ref[tile_of(tile, Q_TILE), :] = jnp.zeros((Q_TILE, LANES), dq_ref.dtype)

        return carry

    lax.fori_loop(0, rows // Q_TILE, query_loop, 0)
    sign = -1.0 if own else 1.0

    def finish(n, carry):
        here = tile_of(n, Q_TILE)
        left, right = dk0[here, :], dk1[here, :]
        dk_ref[here, :] = jnp.where(lane < 64, left, right).astype(dk_ref.dtype)
        dv_ref[here, :] = dv[here, :].astype(dv_ref.dtype)
        decay = decay_ref[here, :]
        decay = decay + jnp.where(lane == 2 * pair, sign * left[:, 67:68], 0.0)
        decay = decay + jnp.where(lane == 2 * pair + 1, sign * right[:, 3:4], 0.0)
        decay_ref[here, :] = decay
        return carry

    lax.fori_loop(0, rows // Q_TILE, finish, 0)


def attend_back(
    own, ranges, query, key_value, terms, key_terms, begins, grad, mixed, lse, local_heads,
    so_far=(),
):
    rows = query.shape[0]
    pairs = local_heads // 2
    wide = jax.ShapeDtypeStruct((rows, pairs * LANES), f32)
    sums = jax.ShapeDtypeStruct((rows, LANES), f32)
    if own:
        out_specs = [lane_block(rows, 0)] * 3 + [fixed((rows, LANES))]
        out_shape = (jax.ShapeDtypeStruct(wide.shape, bf16), wide, wide, sums)
    else:
        both = pl.BlockSpec((2, rows, LANES), lambda p, *_: (0, 0, p))
        out_specs = [lane_block(rows, 0), fixed((rows, LANES)), both, fixed((rows, LANES))]
        out_shape = (
            wide, sums, jax.ShapeDtypeStruct((2, rows, pairs * LANES), bf16), sums,
        )
    return pl.pallas_call(
        functools.partial(attend_back_kernel, local_heads, own),
        grid_spec=pltpu.PrefetchScalarGridSpec(
            num_scalar_prefetch=1,
            grid=(pairs,),
            in_specs=[
                lane_block(rows, 0),
                lane_block(rows, 0),
                lane_block(rows, pairs),
                fixed((rows, LANES)),
                fixed((rows, LANES)),
                fixed((8, rows)),
                lane_block(rows, 0),
                lane_block(rows, 0),
                pair_block(8, rows),
            ]
            + ([lane_block(rows, 0), fixed((rows, LANES))] if own else []),
            out_specs=out_specs,
            scratch_shapes=[
                pltpu.VMEM((rows, LANES), bf16),
                pltpu.VMEM((rows, LANES), bf16),
                pltpu.VMEM((LANES, rows), bf16),
                pltpu.VMEM((LANES, rows), bf16),
                pltpu.VMEM((rows, LANES), f32),
                pltpu.VMEM((rows, LANES), f32),
                pltpu.VMEM((rows, LANES), f32),
                pltpu.VMEM((LANES, Q_TILE), f32),
                pltpu.VMEM((LANES, Q_TILE), f32),
            ],
        ),
        out_shape=out_shape,
        cost_estimate=pl.CostEstimate(
            flops=80_000_000_000 if own else 15_000_000_000,
            transcendentals=20_000_000,
            bytes_accessed=25_000_000,
        ),
        name="attend_back_own" if own else "attend_back_prev",
    )(
        ranges, query, key_value, key_value, terms, key_terms, begins, grad, mixed, lse, *so_far
    )


PIECES = 4


def partners():
    me = lax.axis_index("head")
    near = me + 1 - 2 * (me % 2)
    far = (me + 2) % 4
    cross = (near + 2) % 4
    return me, near, far, cross


def signal(other):
    pl.semaphore_signal(
        pltpu.get_barrier_semaphore(), inc=1, device_id=other, device_id_type=pl.DeviceIdType.MESH
    )


def greet(others):
    for other in others:
        signal(other)
    pl.semaphore_wait(pltpu.get_barrier_semaphore(), len(others))


def remote(source, target, send, receive, other):
    return pltpu.make_async_remote_copy(
        src_ref=source,
        dst_ref=target,
        send_sem=send,
        recv_sem=receive,
        device_id=other,
        device_id_type=pl.DeviceIdType.MESH,
    )


def on_head(index):
    return {"head": index}


def on_blk(index):
    return {"blk": index}


def rows_of(ref, shard, piece, size):
    span = size // PIECES
    start = pl.multiple_of(shard * size + piece * span, span)
    return ref.at[pl.ds(start, span), :]


def spread_piece(source, all_ref, size, sems, piece):
    me, near, far, _ = partners()
    far_send, far_recv, near_send, near_recv, _, _, own = sems
    place = rows_of(all_ref, me, piece, size)
    copies = (
        remote(source, place, far_send.at[piece], far_recv.at[piece], on_head(far)),
        remote(source, place, near_send.at[piece], near_recv.at[piece], on_head(near)),
        pltpu.make_async_copy(source, place, own.at[piece]),
    )
    for copy in copies:
        copy.start()
    return copies


def hand_on(all_ref, size, sems, sent):
    me, near, far, cross = partners()
    far_send, far_recv, near_send, near_recv, on_send, on_recv, own = sems
    passed = []
    for piece in range(PIECES):
        there = rows_of(all_ref, far, piece, size)
        remote(there, there, far_send.at[piece], far_recv.at[piece], on_head(far)).wait_recv()
        copy = remote(there, there, on_send.at[piece], on_recv.at[piece], on_head(near))
        copy.start()
        passed.append(copy)

    def finish():
        for piece in range(PIECES):
            to_far, to_near, local = sent[piece]
            to_far.wait_send()
            to_near.wait_send()
            local.wait()
            passed[piece].wait_send()
            there = rows_of(all_ref, near, piece, size)
            remote(there, there, near_send.at[piece], near_recv.at[piece], on_head(near)).wait_recv()
            there = rows_of(all_ref, cross, piece, size)
            remote(there, there, on_send.at[piece], on_recv.at[piece], on_head(near)).wait_recv()

    return finish


def gather_sems():
    return [pltpu.SemaphoreType.DMA((PIECES,)) for _ in range(7)]


def blk_peers():
    here = lax.axis_index("blk")
    half = lax.axis_size("blk") // 2
    low, high = here % 2, here // 2
    partner = here + 1 - 2 * low
    after = [((high + t) % half) * 2 + low for t in range(half)]
    before = [((high + half - t) % half) * 2 + low for t in range(half)]
    return here, partner, after, before


def gather_first_kernel(pack_ref, tokens_ref, cotangent_ref, pack_all, tokens_all, cotangent_all,
                        *sems):
    (swap_send, swap_recv, swap_own, line_send, line_recv, pair_send, pair_recv) = sems[:7]
    token_sems, cotangent_sems = sems[7:14], sems[14:21]
    me, near, far, cross = partners()
    here, partner, after, before = blk_peers()
    steps = len(after)
    greet(
        [on_head(near), on_head(far), on_head(cross), on_blk(partner)]
        + [on_blk(peer) for peer in after[1:]]
    )
    swaps = [pltpu.make_async_copy(pack_ref.at[me], pack_all.at[here, me], swap_own)]
    for kind, other in enumerate((near, far, cross)):
        swaps.append(
            remote(
                pack_ref.at[other],
                pack_all.at[here, me],
                swap_send.at[kind],
                swap_recv.at[kind],
                on_head(other),
            )
        )
    for swap in swaps:
        swap.start()
    size = tokens_ref.shape[0]
    span = size // PIECES

    def spread_all(ref, all_ref, some):
        return [
            spread_piece(ref.at[pl.ds(piece * span, span), :], all_ref, size, some, piece)
            for piece in range(PIECES)
        ]

    tokens_sent = spread_all(tokens_ref, tokens_all, token_sems)
    sources = (me, near, far, cross)
    waiting = []
    for kind, source in enumerate(sources):
        block = pack_all.at[here, source]
        if kind == 0:
            swaps[0].wait()
        else:
            remote(
                block, block, swap_send.at[kind - 1], swap_recv.at[kind - 1], on_head(source)
            ).wait_recv()
        for t in range(steps):
            if t == 0:
                copy = remote(
                    block, block, pair_send.at[kind, 0], pair_recv.at[kind, 0], on_blk(partner)
                )
            else:
                copy = remote(
                    block, block, line_send.at[kind, t], line_recv.at[kind, t], on_blk(after[t])
                )
            copy.start()
            waiting.append(copy)
    cotangent_sent = spread_all(cotangent_ref, cotangent_all, cotangent_sems)
    finish_tokens = finish_cotangent = None
    for t in range(1, steps):
        for kind, source in enumerate(sources):
            block = pack_all.at[before[t], source]
            remote(
                block, block, line_send.at[kind, t], line_recv.at[kind, t], on_blk(after[t])
            ).wait_recv()
            copy = remote(
                block, block, pair_send.at[kind, t], pair_recv.at[kind, t], on_blk(partner)
            )
            copy.start()
            waiting.append(copy)
        if t == min(2, steps - 1):
            finish_tokens = hand_on(tokens_all, size, token_sems, tokens_sent)
    finish_cotangent = hand_on(cotangent_all, size, cotangent_sems, cotangent_sent)
    for swap in swaps[1:]:
        swap.wait_send()
    for copy in waiting:
        copy.wait_send()
    for t in range(steps):
        for kind, source in enumerate(sources):
            block = pack_all.at[before[t] + partner - here, source]
            remote(
                block, block, pair_send.at[kind, t], pair_recv.at[kind, t], on_blk(partner)
            ).wait_recv()
    finish_tokens()
    finish_cotangent()


def gather_first(pack, tokens, cotangent, number):
    groups, share, columns = pack.shape
    peers = lax.axis_size("blk")
    rows, width = tokens.shape
    whole = jax.ShapeDtypeStruct((groups * rows, width), bf16)
    vmem, anywhere = pl.BlockSpec(memory_space=pltpu.VMEM), pl.BlockSpec(memory_space=pl.ANY)
    all_pack, all_tokens, all_cotangent = pl.pallas_call(
        gather_first_kernel,
        in_specs=[vmem] * 3,
        out_specs=[anywhere] * 3,
        out_shape=[jax.ShapeDtypeStruct((peers, groups, share, columns), bf16), whole, whole],
        scratch_shapes=[
            pltpu.SemaphoreType.DMA((3,)),
            pltpu.SemaphoreType.DMA((3,)),
            pltpu.SemaphoreType.DMA,
        ]
        + [pltpu.SemaphoreType.DMA((4, peers // 2)) for _ in range(4)]
        + gather_sems()
        + gather_sems(),
        compiler_params=pltpu.CompilerParams(collective_id=number, has_side_effects=True),
        cost_estimate=pl.CostEstimate(
            flops=70_000_000_000, transcendentals=0, bytes_accessed=30_000_000
        ),
        name="gather_first",
    )(pack, tokens, cotangent)
    return all_pack.reshape(peers * groups * share, columns), all_tokens, all_cotangent


class Sum:
    def __init__(self, part_ref, buffers, sems, size):
        self.part_ref, self.size, self.span = part_ref, size, size // PIECES
        self.near_buf, self.turn_buf, self.far_buf = buffers
        self.near_send, self.near_recv, self.far_send, self.far_recv = sems
        self.near_copies, self.far_copies = [], []

    def piece(self, n):
        return slice(n * self.span, (n + 1) * self.span)

    def start(self):
        me, near, far, cross = partners()
        for which, shard in ((0, cross), (1, near)):
            for n in range(PIECES):
                copy = remote(
                    rows_of(self.part_ref, shard, n, self.size),
                    self.near_buf.at[which, pl.ds(n * self.span, self.span), :],
                    self.near_send.at[which, n],
                    self.near_recv.at[which, n],
                    on_head(near),
                )
                copy.start()
                self.near_copies.append(copy)

    def turn(self):
        me, near, far, cross = partners()
        for n in range(PIECES):
            here = self.piece(n)
            self.near_copies[n].wait_recv()
            self.turn_buf[here, :] = (
                rows_of(self.part_ref, far, n, self.size)[...].astype(f32)
                + self.near_buf[0, here, :].astype(f32)
            ).astype(bf16)
            copy = remote(
                self.turn_buf.at[pl.ds(n * self.span, self.span), :],
                self.far_buf.at[pl.ds(n * self.span, self.span), :],
                self.far_send.at[n],
                self.far_recv.at[n],
                on_head(far),
            )
            copy.start()
            self.far_copies.append(copy)

    def total(self, n):
        me = lax.axis_index("head")
        self.near_copies[PIECES + n].wait_recv()
        self.far_copies[n].wait_recv()
        here = self.piece(n)
        return (
            rows_of(self.part_ref, me, n, self.size)[...].astype(f32)
            + self.near_buf[1, here, :].astype(f32)
            + self.far_buf[here, :].astype(f32)
        )

    def finish(self):
        for copy in self.near_copies + self.far_copies:
            copy.wait_send()


def sum_buffers(size, width):
    return [
        pltpu.VMEM((2, size, width), bf16),
        pltpu.VMEM((size, width), bf16),
        pltpu.VMEM((size, width), bf16),
    ]


def sum_sems():
    return [
        pltpu.SemaphoreType.DMA((2, PIECES)),
        pltpu.SemaphoreType.DMA((2, PIECES)),
        pltpu.SemaphoreType.DMA((PIECES,)),
        pltpu.SemaphoreType.DMA((PIECES,)),
    ]


def exchange_kernel(local, extras, *refs):
    part_ref, extra_refs = refs[0], refs[1 : 1 + extras]
    out_ref, all_ref, near_buf, turn_buf, far_buf, payload = refs[1 + extras : 7 + extras]
    sems = refs[7 + extras :]
    size = out_ref.shape[0]
    _, near, far, _ = partners()
    greet([on_head(near), on_head(far)])
    shares = Sum(part_ref, (near_buf, turn_buf, far_buf), sems[:4], size)
    shares.start()
    shares.turn()
    sent = []
    for piece in range(PIECES):
        here = shares.piece(piece)
        result, share = local(shares.total(piece), here, *extra_refs)
        out_ref[here, :] = result.astype(out_ref.dtype)
        payload[here, :] = share.astype(bf16)
        source = payload.at[pl.ds(piece * shares.span, shares.span), :]
        sent.append(spread_piece(source, all_ref, size, sems[4:], piece))
    hand_on(all_ref, size, sems[4:], sent)()
    shares.finish()


def exchange(local, part, extras, number, name):
    rows, width = part.shape
    size = rows // 4
    vmem = pl.BlockSpec(memory_space=pltpu.VMEM)
    return pl.pallas_call(
        functools.partial(exchange_kernel, local, len(extras)),
        in_specs=[vmem] * (1 + len(extras)),
        out_specs=[vmem, pl.BlockSpec(memory_space=pl.ANY)],
        out_shape=[
            jax.ShapeDtypeStruct((size, width), f32),
            jax.ShapeDtypeStruct((rows, width), bf16),
        ],
        scratch_shapes=sum_buffers(size, width)
        + [pltpu.VMEM((size, width), bf16)]
        + sum_sems()
        + gather_sems(),
        compiler_params=pltpu.CompilerParams(collective_id=number, has_side_effects=True),
        cost_estimate=pl.CostEstimate(
            flops=70_000_000_000, transcendentals=0, bytes_accessed=16_000_000
        ),
        name=name,
    )(part, *extras)


def finish_last_kernel(grad_ref, first_ref, down_ref, grad_middle_ref, tokens_ref, gain_ref,
                       middle_ref, weights_ref, tokens_grad_ref, result_ref, pair_buf, turn_buf,
                       line_buf, row_buf, near1, turn1, far1, near2, turn2, far2, *sems):
    pair_send, pair_recv, line_send, line_recv, swap_send, swap_recv = sems[:6]
    me, near, far, cross = partners()
    here, partner, after, before = blk_peers()
    steps = len(after)
    groups = grad_ref.shape[1]
    greet(
        [on_head(near), on_head(far), on_head(cross), on_blk(partner)]
        + [on_blk(peer) for peer in after[1:]]
    )
    size = result_ref.shape[0]
    first = Sum(first_ref, (near1, turn1, far1), sems[6:10], size)
    down = Sum(down_ref, (near2, turn2, far2), sems[10:14], size)
    first.start()
    order = list(range(1, steps)) + [0]
    pair_copies = {}
    for t in order:
        copy = remote(
            grad_ref.at[after[t] + partner - here],
            pair_buf.at[t],
            pair_send.at[t],
            pair_recv.at[t],
            on_blk(partner),
        )
        copy.start()
        pair_copies[t] = copy
    first.turn()
    down.start()
    down.turn()
    line_copies = {}

    def pass_on(t):
        pair_copies[t].wait_recv()

        def add(group, carry):
            turn_buf[t, group] = (
                grad_ref[after[t], group].astype(f32) + pair_buf[t, group].astype(f32)
            ).astype(bf16)
            return carry

        lax.fori_loop(0, groups, add, 0)
        copy = remote(
            turn_buf.at[t], line_buf.at[t], line_send.at[t], line_recv.at[t], on_blk(after[t])
        )
        copy.start()
        line_copies[t] = copy

    def put(shares, local, out_ref, extra_refs):
        for piece in range(PIECES):
            rows = shares.piece(piece)
            value, _ = local(shares.total(piece), rows, *extra_refs)
            out_ref[rows, :] = value.astype(out_ref.dtype)

    for t in range(1, steps):
        pass_on(t)
        if t == min(2, steps - 1):
            put(first, after_first, tokens_grad_ref, (grad_middle_ref, tokens_ref, gain_ref))
    pair_copies[0].wait_recv()
    for t in range(1, steps):
        line_copies[t].wait_recv()

    def add_all(group, carry):
        total = grad_ref[here, group].astype(f32) + pair_buf[0, group].astype(f32)
        for t in range(1, steps):
            total = total + line_buf[t, group].astype(f32)
        row_buf[group] = total.astype(bf16)
        return carry

    lax.fori_loop(0, groups, add_all, 0)
    swaps = []
    for kind, other in enumerate((near, far, cross)):
        copy = remote(
            row_buf.at[other],
            weights_ref.at[me],
            swap_send.at[kind],
            swap_recv.at[kind],
            on_head(other),
        )
        copy.start()
        swaps.append(copy)
    weights_ref[me] = row_buf[me]
    put(down, after_down, result_ref, (middle_ref,))
    for kind, other in enumerate((near, far, cross)):
        block = weights_ref.at[other]
        remote(block, block, swap_send.at[kind], swap_recv.at[kind], on_head(other)).wait_recv()
        swaps[kind].wait_send()
    for copy in list(pair_copies.values()) + list(line_copies.values()):
        copy.wait_send()
    first.finish()
    down.finish()


def finish_last(grad, groups, part_first, part_down, grad_middle, tokens, gain, middle, number):
    peers = lax.axis_size("blk")
    all_rows, columns = grad.shape
    share = all_rows // (peers * groups)
    rows, width = tokens.shape
    vmem = pl.BlockSpec(memory_space=pltpu.VMEM)
    half = peers // 2
    return pl.pallas_call(
        finish_last_kernel,
        in_specs=[vmem] * 7,
        out_specs=[vmem] * 3,
        out_shape=[
            jax.ShapeDtypeStruct((groups, share, columns), bf16),
            jax.ShapeDtypeStruct((rows, width), f32),
            jax.ShapeDtypeStruct((rows, width), bf16),
        ],
        scratch_shapes=[pltpu.VMEM((half, groups, share, columns), bf16) for _ in range(3)]
        + [pltpu.VMEM((groups, share, columns), bf16)]
        + sum_buffers(rows, width)
        + sum_buffers(rows, width)
        + [pltpu.SemaphoreType.DMA((half,)) for _ in range(4)]
        + [pltpu.SemaphoreType.DMA((3,)) for _ in range(2)]
        + sum_sems()
        + sum_sems(),
        compiler_params=pltpu.CompilerParams(
            collective_id=number, has_side_effects=True, vmem_limit_bytes=60 << 20
        ),
        cost_estimate=pl.CostEstimate(
            flops=80_000_000_000, transcendentals=0, bytes_accessed=40_000_000
        ),
        name="finish_last",
    )(
        grad.reshape(peers, groups, share, columns), part_first, part_down, grad_middle, tokens,
        gain, middle,
    )


def inverse_rms(value):
    return lax.rsqrt(jnp.mean(value * value, axis=1, keepdims=True) + epsilon)


def through_norm(grad, value):
    factor = inverse_rms(value)
    normed = value * factor
    return factor * (grad - normed * jnp.mean(grad * normed, axis=1, keepdims=True))


def after_attention(total, here, tokens_ref, gain_ref):
    middle = tokens_ref[here, :].astype(f32) + total
    return middle, middle * inverse_rms(middle) * gain_ref[0:1, :]


def after_hidden(total, here, cotangent_ref, middle_ref, gain_ref):
    grad = cotangent_ref[here, :].astype(f32) + through_norm(
        total * gain_ref[0:1, :], middle_ref[here, :]
    )
    return grad, grad


def after_first(total, here, grad_ref, tokens_ref, gain_ref):
    grad = grad_ref[here, :] + through_norm(
        total * gain_ref[0:1, :], tokens_ref[here, :].astype(f32)
    )
    return grad, None


def after_down(total, here, middle_ref):
    return middle_ref[here, :] + total, None


def over_tokens(operand, other_side):
    return lax.dot_general(
        operand, other_side, (((0,), (0,)), ((), ())), preferred_element_type=f32
    )


def sent_columns(pieces, groups):
    packed = jnp.concatenate(
        [piece.reshape(piece.shape[0], groups, -1) for piece in pieces], axis=2
    )
    mine = lax.all_to_all(packed, "head", split_axis=1, concat_axis=0, tiled=True)
    return mine.reshape(mine.shape[0], mine.shape[2])


def all_rows(mine):
    return lax.all_gather(mine, "blk", axis=0, tiled=True)


def row_sums(grad):
    return lax.psum_scatter(grad, "blk", scatter_dimension=0, tiled=True)


def own_rows(summed, groups):
    rows, columns = summed.shape
    parts = lax.all_to_all(
        summed.reshape(groups, rows // groups, columns), "head", split_axis=0, concat_axis=0
    )
    return jnp.swapaxes(parts, 0, 1).astype(f32)


def body(
    tokens,
    segment,
    norm1_gain,
    w_query,
    w_key,
    w_value,
    w_gate_out,
    w_forget,
    forget_bias,
    w_output,
    norm2_gain,
    w_gate,
    w_up,
    w_down,
    cotangent,
):
    token_rows, model_width = tokens.shape
    groups = lax.axis_size("head")
    head_count = forget_bias.shape[0]
    local_heads = head_count // groups
    local_width = model_width // groups
    hidden_width = w_gate.shape[1] // groups
    rows = token_rows * groups
    share = w_query.shape[0]
    group = lax.axis_index("head")

    low = lambda array: array.astype(bf16)
    spread = lambda gain: jnp.broadcast_to(low(gain)[:, None, None], (share, groups, 1))
    forget_low = low(w_forget).reshape(share, groups, local_heads)
    rest = LANES - local_heads - 2
    small = jnp.concatenate(
        [forget_low, spread(norm1_gain), spread(norm2_gain), jnp.zeros((share, groups, rest), bf16)],
        axis=2,
    )
    pack = jnp.concatenate(
        [
            low(piece).reshape(share, groups, -1)
            for piece in (w_key, w_value, small, w_query, w_gate_out, w_output)
        ],
        axis=2,
    )
    first, tokens_all, cotangent_all = gather_first(
        jnp.swapaxes(pack, 0, 1), tokens, cotangent, 0
    )
    kv_width = 2 * local_width + LANES
    output_weight = first[:, kv_width + 2 * local_width :]

    segment_plus = segment + 1
    earlier_segment = passed_along(segment_plus, "blk", 1)
    window = jnp.concatenate([earlier_segment, segment_plus])
    begins = jnp.sum(
        (window[:, None] < segment_plus[None, :]).astype(jnp.int32), axis=0
    )
    tiles = begins.reshape(rows // Q_TILE, Q_TILE)
    ranges = jnp.stack([tiles[:, 0] // K_TILE, (tiles[:, -1] + K_TILE - 1) // K_TILE])
    begins = jnp.broadcast_to(begins[None, :], (8, rows))

    def gain_rows(column):
        gain = first[:, 2 * local_width + local_heads + column].astype(f32)
        return jnp.broadcast_to(gain[None, :], (8, model_width))

    gain1, gain2 = gain_rows(0), gain_rows(1)
    wide_all = tokens_all.astype(f32)
    input1 = (wide_all * inverse_rms(wide_all) * gain1[0:1]).astype(bf16)
    key_value = dot(input1, first[:, : 2 * local_width]).astype(bf16)
    earlier_kv = passed_along(key_value, "blk", 1)
    bias = lax.dynamic_slice_in_dim(forget_bias, group * local_heads, local_heads, 0)
    bias = jnp.pad(bias, (0, LANES - local_heads))
    forget = dot(input1, first[:, 2 * local_width : kv_width]) + bias[None, :]
    forget = forget.astype(bf16).astype(f32)
    terms, halo_terms = decay_terms(jax.nn.log_sigmoid(forget), local_heads)
    earlier_terms = passed_along(halo_terms, "blk", 1)
    query = dot(input1, first[:, kv_width : kv_width + local_width]).astype(bf16)
    gate_raw = dot(
        input1, first[:, kv_width + local_width : kv_width + 2 * local_width]
    )

    so_far = attend(True, ranges, query, key_value, terms, terms, begins, local_heads)
    mine = sent_columns([low(w_gate), low(w_up), low(w_down)], groups)
    mine, earlier_kv, so_far = lax.optimization_barrier((mine, earlier_kv, so_far))
    second = all_rows(mine)
    attended, lse = attend(
        False, ranges, query, earlier_kv, terms, earlier_terms, begins, local_heads, so_far
    )
    opened = jax.nn.sigmoid(gate_raw)
    attended_wide = attended.astype(f32)
    gated = (opened * attended_wide).astype(bf16)
    branch = dot(gated, output_weight, NT).astype(bf16)
    middle, input2 = exchange(after_attention, branch, [tokens, gain2], 1, "exchange_middle")
    gate_act = dot(input2, second[:, :hidden_width])
    up_act = dot(input2, second[:, hidden_width : 2 * hidden_width])
    opening = jax.nn.sigmoid(gate_act)
    hidden = (gate_act * opening * up_act).astype(bf16)
    down = dot(hidden, second[:, 2 * hidden_width :], NT).astype(bf16)
    grad_hidden = dot(cotangent_all, second[:, 2 * hidden_width :])
    grad_gate_act = (grad_hidden * up_act * opening * (1.0 + gate_act * (1.0 - opening))).astype(
        bf16
    )
    grad_up_act = (grad_hidden * gate_act * opening).astype(bf16)
    grad_act = jnp.concatenate([grad_gate_act, grad_up_act], axis=1)
    grad_input2 = dot(grad_act, second[:, : 2 * hidden_width], NT).astype(bf16)
    second_grad = jnp.concatenate(
        [over_tokens(input2, grad_act).astype(bf16), over_tokens(cotangent_all, hidden).astype(bf16)],
        axis=1,
    )
    second_grad, grad_input2 = lax.optimization_barrier((second_grad, grad_input2))
    second_part = row_sums(second_grad)
    grad_middle, grad_branch = exchange(
        after_hidden, grad_input2, [cotangent, middle, gain2], 2, "exchange_hidden"
    )

    grad_gated = dot(grad_branch, output_weight)
    grad_attended = (grad_gated * opened).astype(bf16)
    grad_gate_pre = (grad_gated * attended_wide * opened * (1.0 - opened)).astype(bf16)
    dq_prev, rows_prev, dkv_prev, decay_prev = attend_back(
        False, ranges, query, earlier_kv, terms, earlier_terms, begins, grad_attended, attended,
        lse, local_heads,
    )
    dkv_later = passed_along(dkv_prev, "blk", -1)
    decay_later = passed_along(decay_prev[:, :8], "blk", -1)
    decay_later = jnp.pad(decay_later, ((0, 0), (0, LANES - 8)))
    dq, dk_own, dv_own, decay_own = attend_back(
        True, ranges, query, key_value, terms, terms, begins, grad_attended, attended,
        lse, local_heads, (dq_prev, rows_prev),
    )
    dk = (dk_own + dkv_later[0].astype(f32)).astype(bf16)
    dv = (dv_own + dkv_later[1].astype(f32)).astype(bf16)
    logf_grad = decay_back(decay_own, decay_later)
    forget_grad = jnp.where(
        jnp.arange(LANES)[None, :] < local_heads, logf_grad * jax.nn.sigmoid(-forget), 0.0
    ).astype(bf16)
    grads = jnp.concatenate([dk, dv, forget_grad, dq], axis=1)
    first_grad = over_tokens(input1, grads)
    bias_part = jnp.sum(forget_grad.astype(f32), axis=0)
    row = jnp.arange(model_width)[:, None] % share
    column = jnp.arange(3 * local_width + LANES)[None, :]
    spread_bias = jnp.sum(
        jnp.where(row == jnp.arange(LANES)[None, :], bias_part[None, :], 0.0), axis=1, keepdims=True
    )
    first_grad = jnp.where(column == 2 * local_width + local_heads, spread_bias, first_grad)
    first_grad = jnp.concatenate(
        [
            first_grad.astype(bf16),
            over_tokens(input1, grad_gate_pre).astype(bf16),
            over_tokens(grad_branch, gated).astype(bf16),
        ],
        axis=1,
    )
    grad_input1 = (
        dot(grads, first[:, : kv_width + local_width], NT)
        + dot(
            grad_gate_pre, first[:, kv_width + local_width : kv_width + 2 * local_width], NT
        )
    ).astype(bf16)
    first_sum, tokens_grad, result = finish_last(
        first_grad, groups, grad_input1, down, grad_middle, tokens, gain1, middle, 3
    )
    first_sum = jnp.swapaxes(first_sum, 0, 1).astype(f32)
    second_sum = own_rows(second_part, groups)

    def columns(array, start, width):
        return array[:, :, start : start + width].reshape(share, groups * width)

    key_sum, value_sum = (columns(first_sum, n * local_width, local_width) for n in range(2))
    forget_sum = columns(first_sum, 2 * local_width, local_heads)
    bias_total = first_sum[:local_heads, :, 2 * local_width + local_heads].T.reshape(head_count)
    query_sum, gate_out_sum, output_total = (
        columns(first_sum, kv_width + n * local_width, local_width) for n in range(3)
    )
    gate_sum, up_sum, down_sum = (
        columns(second_sum, n * hidden_width, hidden_width) for n in range(3)
    )

    def along(weight, grad):
        return jnp.sum(low(weight).astype(f32) * grad, axis=1)

    gain1_total = (
        along(w_query, query_sum)
        + along(w_key, key_sum)
        + along(w_value, value_sum)
        + along(w_gate_out, gate_out_sum)
        + along(w_forget, forget_sum)
    ) / low(norm1_gain).astype(f32)
    gain2_total = (along(w_gate, gate_sum) + along(w_up, up_sum)) / low(norm2_gain).astype(f32)
    return (
        result,
        tokens_grad,
        gain1_total,
        query_sum,
        key_sum,
        value_sum,
        gate_out_sum,
        forget_sum,
        bias_total,
        output_total,
        gain2_total,
        gate_sum,
        up_sum,
        down_sum,
    )


def solution(mesh):
    both = ("blk", "head")
    matrix, vector = P(both, None), P(both)
    return jax.shard_map(
        body,
        mesh=mesh,
        in_specs=(
            matrix, P("blk"), vector, matrix, matrix, matrix, matrix, matrix, P(), matrix, vector,
            matrix, matrix, matrix, matrix,
        ),
        out_specs=(
            matrix, matrix, vector, matrix, matrix, matrix, matrix, matrix, P(), matrix, vector,
            matrix, matrix, matrix,
        ),
        check_vma=False,
    )
```

```python
import functools

import jax
import jax.numpy as jnp
from jax import lax
from jax.experimental import pallas as pl
from jax.experimental.pallas import tpu as pltpu
from jax.sharding import PartitionSpec as P

epsilon = 1e-06
LANES = 128
Q_TILE = 512
K_TILE = 512
FAR = -1e30
NT = (((1,), (1,)), ((), ()))
NN = (((1,), (0,)), ((), ()))
bf16 = jnp.bfloat16
f32 = jnp.float32


def dot(a, b, dims=NN, **kw):
    return lax.dot_general(a, b, dims, preferred_element_type=f32, **kw)


def passed_along(array, axis, by):
    peers = lax.axis_size(axis)
    pairs = [(i, i + by) for i in range(peers) if 0 <= i + by < peers]
    return lax.ppermute(array, axis, pairs)


def split3(value):
    high = value.astype(bf16)
    rest = value - high.astype(f32)
    mid = rest.astype(bf16)
    low = (rest - mid.astype(f32)).astype(bf16)
    return high, mid, low


def running(value_of, steps, rows, upper):
    place = lax.broadcasted_iota(jnp.int32, (rows, rows), 0)
    other = lax.broadcasted_iota(jnp.int32, (rows, rows), 1)
    tri = jnp.where((other >= place) if upper else (other <= place), 1.0, 0.0).astype(bf16)
    outs = [None] * steps
    carry = jnp.zeros((1, LANES), f32)
    order = range(steps - 1, -1, -1) if upper else range(steps)
    for n in order:
        block = value_of(n)
        total = sum(dot(tri, part) for part in split3(block)) + carry
        outs[n] = total
        carry = total[0:1] if upper else total[rows - 1 : rows]
    return outs, carry


def decay_kernel(local_heads, logf_ref, own_ref, halo_ref):
    rows = 256
    steps = logf_ref.shape[0] // rows
    lane = lax.broadcasted_iota(jnp.int32, (rows, LANES), 1)

    def value_of(n):
        return jnp.where(lane < local_heads, logf_ref[n * rows : (n + 1) * rows, :], 0.0)

    sums, total = running(value_of, steps, rows, False)
    one = jnp.where(lane == 3 * local_heads, 1.0, 0.0)

    def terms(value):
        high, mid, low = split3(value)
        return (
            high.astype(f32)
            + pltpu.roll(mid.astype(f32), local_heads, 1)
            + pltpu.roll(low.astype(f32), 2 * local_heads, 1)
            + one
        ).astype(bf16)

    for n in range(steps):
        own_ref[n * rows : (n + 1) * rows, :] = terms(sums[n])
        halo_ref[n * rows : (n + 1) * rows, :] = terms(sums[n] - total)


def decay_terms(logf, local_heads):
    shape = jax.ShapeDtypeStruct(logf.shape, bf16)
    return pl.pallas_call(
        functools.partial(decay_kernel, local_heads),
        out_shape=(shape, shape),
        name="decay_terms",
    )(logf)


def decay_back_kernel(own_ref, halo_ref, out_ref):
    rows = 256
    steps = own_ref.shape[0] // rows
    own, _ = running(lambda n: own_ref[n * rows : (n + 1) * rows, :], steps, rows, True)
    halo, _ = running(lambda n: halo_ref[n * rows : (n + 1) * rows, :], steps, rows, False)
    for n in range(steps):
        part = slice(n * rows, (n + 1) * rows)
        out_ref[part, :] = own[n] + (halo[n] - halo_ref[part, :])


def decay_back(own, halo):
    return pl.pallas_call(
        decay_back_kernel,
        out_shape=jax.ShapeDtypeStruct(own.shape, f32),
        name="decay_back",
    )(own, halo)


def placing(pair, local_heads, for_query):
    row = lax.broadcasted_iota(jnp.int32, (LANES, LANES), 0)
    col = lax.broadcasted_iota(jnp.int32, (LANES, LANES), 1)
    head = jnp.where(col < 64, 2 * pair + 1, 2 * pair)
    spot = jnp.where(col < 64, col, col - 64)
    term = jnp.where(for_query, spot, spot - 3)
    is_term = (term >= 0) & (term < 3) & (row == term * local_heads + head)
    ones = jnp.where(for_query, spot - 3, spot)
    is_one = (ones >= 0) & (ones < 3) & (row == 3 * local_heads)
    sign = 1.0 if for_query else -1.0
    return (jnp.where(is_term, sign, 0.0) + jnp.where(is_one, 1.0, 0.0)).astype(bf16)


def allowed_pairs(first_key, query_tile, rows, begin_row):
    shape = (K_TILE, Q_TILE)
    key_place = first_key + lax.broadcasted_iota(jnp.int32, shape, 0)
    query_place = rows + query_tile * Q_TILE + lax.broadcasted_iota(jnp.int32, shape, 1)
    return (key_place >= begin_row) & (key_place <= query_place)


def key_range(ranges_ref, query_tile, rows, own):
    count = rows // K_TILE
    base = count if own else 0
    first = jnp.clip(ranges_ref[0, query_tile] - base, 0, count)
    full = jnp.clip(ranges_ref[1, query_tile] - base, first, count)
    return first, full


def key_loops(ranges_ref, query_tile, rows, own, step, carry):
    first, full = key_range(ranges_ref, query_tile, rows, own)
    inside = query_tile * (Q_TILE // K_TILE) if own else rows // K_TILE
    full = jnp.minimum(full, inside)
    carry = lax.fori_loop(first, full, functools.partial(step, True), carry)
    carry = lax.fori_loop(full, inside, functools.partial(step, False), carry)
    if own:
        carry = lax.fori_loop(
            inside, inside + Q_TILE // K_TILE, functools.partial(step, True), carry
        )
    return carry


def tile_of(number, size):
    return pl.ds(pl.multiple_of(number * size, size), size)


def fill_keys(pair, local_heads, first, key_ref, terms_ref, keys):
    place = placing(pair, local_heads, False)
    lane = lax.broadcasted_iota(jnp.int32, (K_TILE, LANES), 1)

    def fill(n, carry):
        here = tile_of(n, K_TILE)
        extra = dot(terms_ref[here, :], place).astype(bf16)
        key = key_ref[here, :]
        keys[0][here, :] = jnp.where(lane < 64, key, extra)
        keys[1][here, :] = jnp.where(lane < 64, extra, key)
        return carry

    lax.fori_loop(first, key_ref.shape[0] // K_TILE, fill, 0)


def query_tiles(q_ref, terms_ref, place, here, scaling):
    lane = lax.broadcasted_iota(jnp.int32, (Q_TILE, LANES), 1)
    extra = dot(terms_ref[here, :], place).astype(bf16)
    query = (q_ref[here, :].astype(f32) * scaling).astype(bf16)
    return jnp.where(lane < 64, query, extra), jnp.where(lane < 64, extra, query)


def attend_kernel(local_heads, own, ranges_ref, q_ref, k_ref, v_ref, t_query_ref, t_key_ref,
                  begin_ref, *refs):
    if own:
        acc_out_ref, state_out_ref, key0, key1, values, acc0, acc1 = refs
    else:
        acc_in_ref, state_in_ref, o_ref, lse_ref, key0, key1, values, acc0, acc1 = refs
    pair = pl.program_id(0)
    rows = q_ref.shape[0]
    base = rows if own else 0
    keys, accs = (key0, key1), (acc0, acc1)
    first, _ = key_range(ranges_ref, 0, rows, own)
    fill_keys(pair, local_heads, first, k_ref, t_key_ref, keys)

    def turn(n, carry):
        values[:, tile_of(n, K_TILE)] = v_ref[tile_of(n, K_TILE), :].T
        return carry

    lax.fori_loop(first, rows // K_TILE, turn, 0)
    place = placing(pair, local_heads, True)

    def query_loop(tile, carry):
        here = tile_of(tile, Q_TILE)
        queries = query_tiles(q_ref, t_query_ref, place, here, 64**-0.5)
        begin_row = begin_ref[0:1, here]
        if own:
            low = jnp.full((1, Q_TILE), FAR, f32)
            zero = jnp.zeros((1, Q_TILE), f32)
            state = (low, zero, low, zero)
            for acc in accs:
                acc[...] = jnp.zeros_like(acc)
        else:
            state = tuple(state_in_ref[n : n + 1, here] for n in range(4))
            for h in range(2):
                accs[h][...] = acc_in_ref[64 * h : 64 * (h + 1), here]

        def step(masked, number, state):
            there = tile_of(number, K_TILE)
            fresh = []
            if masked:
                allowed = allowed_pairs(base + number * K_TILE, tile, rows, begin_row)
            for h in range(2):
                largest, total = state[2 * h], state[2 * h + 1]
                scores = dot(keys[h][there, :], queries[h], NT)
                if masked:
                    scores = jnp.where(allowed, scores, FAR)
                now = jnp.maximum(largest, jnp.max(scores, axis=0, keepdims=True))
                fade = jnp.exp(largest - now)
                weights = jnp.exp(scores - now)
                total = total * fade + jnp.sum(weights, axis=0, keepdims=True)
                accs[h][...] = accs[h][...] * fade + dot(
                    values[64 * h : 64 * (h + 1), there], weights.astype(bf16)
                )
                fresh += [now, total]
            return tuple(fresh)

        state = key_loops(ranges_ref, tile, rows, own, step, state)
        if own:
            for h in range(2):
                acc_out_ref[64 * h : 64 * (h + 1), here] = accs[h][...]
            for n in range(4):
                state_out_ref[n : n + 1, here] = state[n]
        else:
            mixed = jnp.concatenate(
                [accs[h][...] * (1.0 / state[2 * h + 1]) for h in range(2)], axis=0
            )
            o_ref[here, :] = mixed.T.astype(bf16)
            for h in range(2):
                lse_ref[h : h + 1, here] = state[2 * h] + jnp.log(state[2 * h + 1])
        return carry

    lax.fori_loop(0, rows // Q_TILE, query_loop, 0)


def lane_block(rows, offset):
    return pl.BlockSpec((rows, LANES), lambda p, *_: (0, offset + p))


def fixed(shape):
    return pl.BlockSpec(shape, lambda p, *_: (0, 0))


def pair_block(height, rows):
    return pl.BlockSpec((height, rows), lambda p, *_: (p, 0))


def terms_block(own, rows, pairs):
    return pl.BlockSpec((rows, LANES), lambda p, *_: (0, 0 if own else 2 * pairs))


def attend(own, ranges, query, key_value, terms, key_terms, begins, local_heads, so_far=()):
    rows = query.shape[0]
    pairs = local_heads // 2
    running_specs = [pair_block(LANES, rows), pair_block(8, rows)]
    running_shape = (
        jax.ShapeDtypeStruct((LANES * pairs, rows), f32),
        jax.ShapeDtypeStruct((8 * pairs, rows), f32),
    )
    final_specs = [lane_block(rows, 0), pair_block(8, rows)]
    final_shape = (
        jax.ShapeDtypeStruct((rows, pairs * LANES), bf16),
        jax.ShapeDtypeStruct((8 * pairs, rows), f32),
    )
    return pl.pallas_call(
        functools.partial(attend_kernel, local_heads, own),
        grid_spec=pltpu.PrefetchScalarGridSpec(
            num_scalar_prefetch=1,
            grid=(pairs,),
            in_specs=[
                lane_block(rows, 0),
                lane_block(rows, 0),
                lane_block(rows, pairs),
                fixed((rows, LANES)),
                terms_block(own, rows, pairs),
                fixed((8, rows)),
            ]
            + ([] if own else running_specs),
            out_specs=running_specs if own else final_specs,
            scratch_shapes=[
                pltpu.VMEM((rows, LANES), bf16),
                pltpu.VMEM((rows, LANES), bf16),
                pltpu.VMEM((LANES, rows), bf16),
                pltpu.VMEM((64, Q_TILE), f32),
                pltpu.VMEM((64, Q_TILE), f32),
            ],
        ),
        out_shape=running_shape if own else final_shape,
        cost_estimate=pl.CostEstimate(
            flops=40_000_000_000 if own else 10_000_000_000,
            transcendentals=20_000_000,
            bytes_accessed=12_000_000,
        ),
        name="attend_own" if own else "attend_prev",
    )(ranges, query, key_value, key_value, terms, key_terms, begins, *so_far)


def attend_back_kernel(local_heads, own, ranges_ref, q_ref, k_ref, v_ref, t_query_ref, t_key_ref,
                       begin_ref, grad_ref, o_ref, lse_ref, *refs):
    if own:
        dq_in_ref, decay_in_ref, dq_ref, dk_ref, dv_ref, decay_ref = refs[:6]
    else:
        dq_ref, row_decay_ref, dkv_ref, decay_ref = refs[:4]
        dk_ref, dv_ref = dkv_ref.at[0], dkv_ref.at[1]
    key0, key1, key_t0, key_t1, dk0, dk1, dv, dq0, dq1 = refs[-9:]
    pair = pl.program_id(0)
    rows = q_ref.shape[0]
    base = rows if own else 0
    keys, keys_t, dks, dqs = (key0, key1), (key_t0, key_t1), (dk0, dk1), (dq0, dq1)
    first, _ = key_range(ranges_ref, 0, rows, own)
    fill_keys(pair, local_heads, first, k_ref, t_key_ref, keys)

    def turn(n, carry):
        here = tile_of(n, K_TILE)
        for h in range(2):
            keys_t[h][:, here] = keys[h][here, :].T
        return carry

    lax.fori_loop(first, rows // K_TILE, turn, 0)
    for ref in (dk0, dk1, dv):
        ref[...] = jnp.zeros_like(ref)
    place = placing(pair, local_heads, True)
    lane = lax.broadcasted_iota(jnp.int32, (Q_TILE, LANES), 1)
    pick_row = lax.broadcasted_iota(jnp.int32, (8, LANES), 0)
    pick_lane = lax.broadcasted_iota(jnp.int32, (8, LANES), 1)
    pick = jnp.where((pick_lane // 64) == pick_row, 1.0, 0.0)
    sums_ref = decay_ref if own else row_decay_ref

    @pl.when(pair == 0)
    def _():
        if own:
            decay_ref[...] = decay_in_ref[...]
        else:
            decay_ref[...] = jnp.zeros_like(decay_ref)
            row_decay_ref[...] = jnp.zeros_like(row_decay_ref)

    def query_tile(tile):
        here = tile_of(tile, Q_TILE)
        queries = query_tiles(q_ref, t_query_ref, place, here, 64**-0.5)
        begin_row = begin_ref[0:1, here]
        grad = grad_ref[here, :]
        nothing = jnp.zeros_like(grad)
        grads = (jnp.where(lane < 64, grad, nothing), jnp.where(lane < 64, nothing, grad))
        product = grad.astype(f32) * o_ref[here, :].astype(f32)
        inner = dot(pick, product, NT, precision=lax.Precision.HIGHEST)
        for dq in dqs:
            dq[...] = jnp.zeros_like(dq)

        def step(masked, number, state):
            there = tile_of(number, K_TILE)
            if masked:
                allowed = allowed_pairs(base + number * K_TILE, tile, rows, begin_row)
            value = v_ref[there, :]
            value_part = 0.0
            for h in range(2):
                scores = dot(keys[h][there, :], queries[h], NT)
                prob = jnp.exp(scores - lse_ref[h : h + 1, here])
                if masked:
                    prob = jnp.where(allowed, prob, 0.0)
                grad_prob = dot(value, grads[h], NT)
                grad_score = (prob * (grad_prob - inner[h : h + 1, :])).astype(bf16)
                value_part = value_part + dot(prob.astype(bf16), grads[h])
                dks[h][there, :] += dot(grad_score, queries[h])
                dqs[h][...] += dot(keys_t[h][:, there], grad_score)
            dv[there, :] += value_part
            return state

        key_loops(ranges_ref, tile, rows, own, step, 0)
        turned = [dq[...].T for dq in dqs]
        dq_tile = jnp.where(lane < 64, turned[0], turned[1]) * 64**-0.5
        if own:
            dq_tile = dq_tile + dq_in_ref[here, :]
        dq_ref[here, :] = dq_tile.astype(dq_ref.dtype)
        sums = sums_ref[here, :]
        sums = sums + jnp.where(lane == 2 * pair, turned[0][:, 64:65], 0.0)
        sums = sums + jnp.where(lane == 2 * pair + 1, turned[1][:, 0:1], 0.0)
        sums_ref[here, :] = sums

    def query_loop(tile, carry):
        if own:
            query_tile(tile)
        else:
            reaches = key_range(ranges_ref, tile, rows, own)[0] < rows // K_TILE
            pl.when(reaches)(lambda: query_tile(tile))

            @pl.when(jnp.logical_not(reaches))
            def _():
                dq_ref[tile_of(tile, Q_TILE), :] = jnp.zeros((Q_TILE, LANES), dq_ref.dtype)

        return carry

    lax.fori_loop(0, rows // Q_TILE, query_loop, 0)
    sign = -1.0 if own else 1.0

    def finish(n, carry):
        here = tile_of(n, Q_TILE)
        left, right = dk0[here, :], dk1[here, :]
        dk_ref[here, :] = jnp.where(lane < 64, left, right).astype(dk_ref.dtype)
        dv_ref[here, :] = dv[here, :].astype(dv_ref.dtype)
        decay = decay_ref[here, :]
        decay = decay + jnp.where(lane == 2 * pair, sign * left[:, 67:68], 0.0)
        decay = decay + jnp.where(lane == 2 * pair + 1, sign * right[:, 3:4], 0.0)
        decay_ref[here, :] = decay
        return carry

    lax.fori_loop(0, rows // Q_TILE, finish, 0)


def attend_back(
    own, ranges, query, key_value, terms, key_terms, begins, grad, mixed, lse, local_heads,
    so_far=(),
):
    rows = query.shape[0]
    pairs = local_heads // 2
    wide = jax.ShapeDtypeStruct((rows, pairs * LANES), f32)
    sums = jax.ShapeDtypeStruct((rows, LANES), f32)
    if own:
        out_specs = [lane_block(rows, 0)] * 3 + [fixed((rows, LANES))]
        out_shape = (jax.ShapeDtypeStruct(wide.shape, bf16), wide, wide, sums)
    else:
        both = pl.BlockSpec((2, rows, LANES), lambda p, *_: (0, 0, p))
        out_specs = [lane_block(rows, 0), fixed((rows, LANES)), both, fixed((rows, LANES))]
        out_shape = (
            wide, sums, jax.ShapeDtypeStruct((2, rows, pairs * LANES), bf16), sums,
        )
    return pl.pallas_call(
        functools.partial(attend_back_kernel, local_heads, own),
        grid_spec=pltpu.PrefetchScalarGridSpec(
            num_scalar_prefetch=1,
            grid=(pairs,),
            in_specs=[
                lane_block(rows, 0),
                lane_block(rows, 0),
                lane_block(rows, pairs),
                fixed((rows, LANES)),
                terms_block(own, rows, pairs),
                fixed((8, rows)),
                lane_block(rows, 0),
                lane_block(rows, 0),
                pair_block(8, rows),
            ]
            + ([lane_block(rows, 0), fixed((rows, LANES))] if own else []),
            out_specs=out_specs,
            scratch_shapes=[
                pltpu.VMEM((rows, LANES), bf16),
                pltpu.VMEM((rows, LANES), bf16),
                pltpu.VMEM((LANES, rows), bf16),
                pltpu.VMEM((LANES, rows), bf16),
                pltpu.VMEM((rows, LANES), f32),
                pltpu.VMEM((rows, LANES), f32),
                pltpu.VMEM((rows, LANES), f32),
                pltpu.VMEM((LANES, Q_TILE), f32),
                pltpu.VMEM((LANES, Q_TILE), f32),
            ],
        ),
        out_shape=out_shape,
        cost_estimate=pl.CostEstimate(
            flops=80_000_000_000 if own else 15_000_000_000,
            transcendentals=20_000_000,
            bytes_accessed=25_000_000,
        ),
        name="attend_back_own" if own else "attend_back_prev",
    )(
        ranges, query, key_value, key_value, terms, key_terms, begins, grad, mixed, lse, *so_far
    )


PIECES = 4


def partners():
    me = lax.axis_index("head")
    near = me + 1 - 2 * (me % 2)
    far = (me + 2) % 4
    cross = (near + 2) % 4
    return me, near, far, cross


def signal(other):
    pl.semaphore_signal(
        pltpu.get_barrier_semaphore(), inc=1, device_id=other, device_id_type=pl.DeviceIdType.MESH
    )


def greet(others):
    for other in others:
        signal(other)
    pl.semaphore_wait(pltpu.get_barrier_semaphore(), len(others))


def remote(source, target, send, receive, other):
    return pltpu.make_async_remote_copy(
        src_ref=source,
        dst_ref=target,
        send_sem=send,
        recv_sem=receive,
        device_id=other,
        device_id_type=pl.DeviceIdType.MESH,
    )


def on_head(index):
    return {"head": index}


def on_blk(index):
    return {"blk": index}


def rows_of(ref, shard, piece, size):
    span = size // PIECES
    start = pl.multiple_of(shard * size + piece * span, span)
    return ref.at[pl.ds(start, span), :]


def spread_piece(source, all_ref, size, sems, piece):
    me, near, far, _ = partners()
    far_send, far_recv, near_send, near_recv, _, _, own = sems
    place = rows_of(all_ref, me, piece, size)
    copies = (
        remote(source, place, far_send.at[piece], far_recv.at[piece], on_head(far)),
        remote(source, place, near_send.at[piece], near_recv.at[piece], on_head(near)),
        pltpu.make_async_copy(source, place, own.at[piece]),
    )
    for copy in copies:
        copy.start()
    return copies


def hand_on(all_ref, size, sems, sent):
    me, near, far, cross = partners()
    far_send, far_recv, near_send, near_recv, on_send, on_recv, own = sems
    passed = []
    for piece in range(PIECES):
        there = rows_of(all_ref, far, piece, size)
        remote(there, there, far_send.at[piece], far_recv.at[piece], on_head(far)).wait_recv()
        copy = remote(there, there, on_send.at[piece], on_recv.at[piece], on_head(near))
        copy.start()
        passed.append(copy)

    def finish():
        for piece in range(PIECES):
            to_far, to_near, local = sent[piece]
            to_far.wait_send()
            to_near.wait_send()
            local.wait()
            passed[piece].wait_send()
            there = rows_of(all_ref, near, piece, size)
            remote(there, there, near_send.at[piece], near_recv.at[piece], on_head(near)).wait_recv()
            there = rows_of(all_ref, cross, piece, size)
            remote(there, there, on_send.at[piece], on_recv.at[piece], on_head(near)).wait_recv()

    return finish


def gather_sems():
    return [pltpu.SemaphoreType.DMA((PIECES,)) for _ in range(7)]


def blk_peers():
    here = lax.axis_index("blk")
    half = lax.axis_size("blk") // 2
    low, high = here % 2, here // 2
    partner = here + 1 - 2 * low
    after = [((high + t) % half) * 2 + low for t in range(half)]
    return here, partner, after


class Line:
    def __init__(self, block_of, kinds, sems):
        self.block_of, self.kinds = block_of, kinds
        self.pair_send, self.pair_recv, self.up_send, self.up_recv, self.down_send, self.down_recv = sems
        here = lax.axis_index("blk")
        self.half = lax.axis_size("blk") // 2
        self.low, self.high = here % 2, here // 2
        self.partner = here + 1 - 2 * self.low
        self.has_up, self.has_down = self.high < self.half - 1, self.high > 0

    def greet(self, others):
        greet_sum = len(others) + 1
        for other in others + [on_blk(self.partner)]:
            signal(other)
        pl.when(self.has_up)(lambda: signal(on_blk(self.at(self.high + 1))))
        pl.when(self.has_down)(lambda: signal(on_blk(self.at(self.high - 1))))
        ends = (self.high == 0).astype(jnp.int32) + (self.high == self.half - 1).astype(jnp.int32)
        pl.semaphore_wait(pltpu.get_barrier_semaphore(), greet_sum + 2 - ends)

    def at(self, high):
        return high * 2 + self.low

    def pair_copy(self, kind, high, low):
        block = self.block_of(kind, high * 2 + low)
        return remote(
            block, block, self.pair_send.at[kind, high], self.pair_recv.at[kind, high],
            on_blk(self.partner),
        )

    def up_copy(self, kind, high):
        block = self.block_of(kind, self.at(high))
        return remote(
            block, block, self.up_send.at[kind, high], self.up_recv.at[kind, high],
            on_blk(self.at(jnp.minimum(self.high + 1, self.half - 1))),
        )

    def down_copy(self, kind, high):
        block = self.block_of(kind, self.at(high))
        return remote(
            block, block, self.down_send.at[kind, high], self.down_recv.at[kind, high],
            on_blk(self.at(jnp.maximum(self.high - 1, 0))),
        )

    def launch(self, kind):
        self.pair_copy(kind, self.high, self.low).start()
        pl.when(self.has_up)(lambda: self.up_copy(kind, self.high).start())
        pl.when(self.has_down)(lambda: self.down_copy(kind, self.high).start())

    def step(self, t):
        for kind in range(self.kinds):
            below, above = self.high - t, self.high + t

            @pl.when(below >= 0)
            def _():
                self.up_copy(kind, below).wait_recv()
                self.pair_copy(kind, below, self.low).start()
                pl.when(self.has_up)(lambda: self.up_copy(kind, below).start())

            @pl.when(above < self.half)
            def _():
                self.down_copy(kind, above).wait_recv()
                self.pair_copy(kind, above, self.low).start()
                pl.when(self.has_down)(lambda: self.down_copy(kind, above).start())

    def finish(self):
        for kind in range(self.kinds):

            def wait(high, carry):
                self.pair_copy(kind, high, self.low).wait_send()
                self.pair_copy(kind, high, 1 - self.low).wait_recv()

                @pl.when((high <= self.high) & self.has_up)
                def _():
                    self.up_copy(kind, high).wait_send()

                @pl.when((high >= self.high) & self.has_down)
                def _():
                    self.down_copy(kind, high).wait_send()

                return carry

            lax.fori_loop(0, self.half, wait, 0)


def gather_first_kernel(pack_ref, tokens_ref, cotangent_ref, pack_all, tokens_all, cotangent_all,
                        *sems):
    swap_send, swap_recv, swap_own = sems[:3]
    token_sems, cotangent_sems = sems[9:16], sems[16:23]
    me, near, far, cross = partners()
    sources = (me, near, far, cross)
    line = Line(lambda kind, blk: pack_all.at[blk, sources[kind]], 4, sems[3:9])
    here = lax.axis_index("blk")
    line.greet([on_head(near), on_head(far), on_head(cross)])
    swaps = [pltpu.make_async_copy(pack_ref.at[me], pack_all.at[here, me], swap_own)]
    for kind, other in enumerate((near, far, cross)):
        swaps.append(
            remote(
                pack_ref.at[other],
                pack_all.at[here, me],
                swap_send.at[kind],
                swap_recv.at[kind],
                on_head(other),
            )
        )
    for swap in swaps:
        swap.start()
    size = tokens_ref.shape[0]
    span = size // PIECES

    def spread_all(ref, all_ref, some):
        return [
            spread_piece(ref.at[pl.ds(piece * span, span), :], all_ref, size, some, piece)
            for piece in range(PIECES)
        ]

    tokens_sent = spread_all(tokens_ref, tokens_all, token_sems)
    swaps[0].wait()
    line.launch(0)
    for kind, source in enumerate((near, far, cross)):
        block = pack_all.at[here, source]
        remote(
            block, block, swap_send.at[kind], swap_recv.at[kind], on_head(source)
        ).wait_recv()
        line.launch(kind + 1)
    cotangent_sent = spread_all(cotangent_ref, cotangent_all, cotangent_sems)
    for t in range(1, line.half):
        line.step(t)
    finish_tokens = hand_on(tokens_all, size, token_sems, tokens_sent)
    finish_cotangent = hand_on(cotangent_all, size, cotangent_sems, cotangent_sent)
    for swap in swaps[1:]:
        swap.wait_send()
    line.finish()
    finish_tokens()
    finish_cotangent()


def gather_first(pack, tokens, cotangent, number):
    groups, share, columns = pack.shape
    peers = lax.axis_size("blk")
    rows, width = tokens.shape
    whole = jax.ShapeDtypeStruct((groups * rows, width), bf16)
    vmem, anywhere = pl.BlockSpec(memory_space=pltpu.VMEM), pl.BlockSpec(memory_space=pl.ANY)
    all_pack, all_tokens, all_cotangent = pl.pallas_call(
        gather_first_kernel,
        in_specs=[vmem] * 3,
        out_specs=[anywhere] * 3,
        out_shape=[jax.ShapeDtypeStruct((peers, groups, share, columns), bf16), whole, whole],
        scratch_shapes=[
            pltpu.SemaphoreType.DMA((3,)),
            pltpu.SemaphoreType.DMA((3,)),
            pltpu.SemaphoreType.DMA,
        ]
        + [pltpu.SemaphoreType.DMA((4, peers // 2)) for _ in range(6)]
        + gather_sems()
        + gather_sems(),
        compiler_params=pltpu.CompilerParams(collective_id=number, has_side_effects=True),
        cost_estimate=pl.CostEstimate(
            flops=70_000_000_000, transcendentals=0, bytes_accessed=30_000_000
        ),
        name="gather_first",
    )(pack, tokens, cotangent)
    return all_pack.reshape(peers * groups * share, columns), all_tokens, all_cotangent


class Sum:
    def __init__(self, part_ref, buffers, sems, size):
        self.part_ref, self.size, self.span = part_ref, size, size // PIECES
        self.near_buf, self.turn_buf, self.far_buf = buffers
        self.near_send, self.near_recv, self.far_send, self.far_recv = sems
        self.near_copies, self.far_copies = [], []

    def piece(self, n):
        return slice(n * self.span, (n + 1) * self.span)

    def start(self):
        me, near, far, cross = partners()
        for which, shard in ((0, cross), (1, near)):
            for n in range(PIECES):
                copy = remote(
                    rows_of(self.part_ref, shard, n, self.size),
                    self.near_buf.at[which, pl.ds(n * self.span, self.span), :],
                    self.near_send.at[which, n],
                    self.near_recv.at[which, n],
                    on_head(near),
                )
                copy.start()
                self.near_copies.append(copy)

    def turn(self):
        me, near, far, cross = partners()
        for n in range(PIECES):
            here = self.piece(n)
            self.near_copies[n].wait_recv()
            self.turn_buf[here, :] = (
                rows_of(self.part_ref, far, n, self.size)[...].astype(f32)
                + self.near_buf[0, here, :].astype(f32)
            ).astype(bf16)
            copy = remote(
                self.turn_buf.at[pl.ds(n * self.span, self.span), :],
                self.far_buf.at[pl.ds(n * self.span, self.span), :],
                self.far_send.at[n],
                self.far_recv.at[n],
                on_head(far),
            )
            copy.start()
            self.far_copies.append(copy)

    def total(self, n):
        me = lax.axis_index("head")
        self.near_copies[PIECES + n].wait_recv()
        self.far_copies[n].wait_recv()
        here = self.piece(n)
        return (
            rows_of(self.part_ref, me, n, self.size)[...].astype(f32)
            + self.near_buf[1, here, :].astype(f32)
            + self.far_buf[here, :].astype(f32)
        )

    def finish(self):
        for copy in self.near_copies + self.far_copies:
            copy.wait_send()


def sum_buffers(size, width):
    return [
        pltpu.VMEM((2, size, width), bf16),
        pltpu.VMEM((size, width), bf16),
        pltpu.VMEM((size, width), bf16),
    ]


def sum_sems():
    return [
        pltpu.SemaphoreType.DMA((2, PIECES)),
        pltpu.SemaphoreType.DMA((2, PIECES)),
        pltpu.SemaphoreType.DMA((PIECES,)),
        pltpu.SemaphoreType.DMA((PIECES,)),
    ]


def exchange_kernel(local, extras, *refs):
    part_ref, extra_refs = refs[0], refs[1 : 1 + extras]
    out_ref, all_ref, near_buf, turn_buf, far_buf, payload = refs[1 + extras : 7 + extras]
    sems = refs[7 + extras :]
    size = out_ref.shape[0]
    _, near, far, _ = partners()
    greet([on_head(near), on_head(far)])
    shares = Sum(part_ref, (near_buf, turn_buf, far_buf), sems[:4], size)
    shares.start()
    shares.turn()
    sent = []
    for piece in range(PIECES):
        here = shares.piece(piece)
        result, share = local(shares.total(piece), here, *extra_refs)
        out_ref[here, :] = result.astype(out_ref.dtype)
        payload[here, :] = share.astype(bf16)
        source = payload.at[pl.ds(piece * shares.span, shares.span), :]
        sent.append(spread_piece(source, all_ref, size, sems[4:], piece))
    hand_on(all_ref, size, sems[4:], sent)()
    shares.finish()


def exchange(local, part, extras, number, name):
    rows, width = part.shape
    size = rows // 4
    vmem = pl.BlockSpec(memory_space=pltpu.VMEM)
    return pl.pallas_call(
        functools.partial(exchange_kernel, local, len(extras)),
        in_specs=[vmem] * (1 + len(extras)),
        out_specs=[vmem, pl.BlockSpec(memory_space=pl.ANY)],
        out_shape=[
            jax.ShapeDtypeStruct((size, width), f32),
            jax.ShapeDtypeStruct((rows, width), bf16),
        ],
        scratch_shapes=sum_buffers(size, width)
        + [pltpu.VMEM((size, width), bf16)]
        + sum_sems()
        + gather_sems(),
        compiler_params=pltpu.CompilerParams(collective_id=number, has_side_effects=True),
        cost_estimate=pl.CostEstimate(
            flops=70_000_000_000, transcendentals=0, bytes_accessed=16_000_000
        ),
        name=name,
    )(part, *extras)


def finish_last_kernel(grad_ref, output_grad_ref, first_ref, down_ref, grad_middle_ref, tokens_ref,
                       gain_ref, middle_ref, weights_ref, output_ref, tokens_grad_ref, result_ref,
                       *refs):
    buffers, (near1, turn1, far1, near2, turn2, far2) = refs[:8], refs[8:14]
    sems = refs[14:]
    me, near, far, cross = partners()
    here, partner, after = blk_peers()
    steps = len(after)
    greet(
        [on_head(near), on_head(far), on_head(cross), on_blk(partner)]
        + [on_blk(peer) for peer in after[1:]]
    )
    size = result_ref.shape[0]
    first = Sum(first_ref, (near1, turn1, far1), sems[12:16], size)
    down = Sum(down_ref, (near2, turn2, far2), sems[16:20], size)
    sums = (
        (grad_ref, weights_ref, buffers[:4], sems[:6]),
        (output_grad_ref, output_ref, buffers[4:], sems[6:12]),
    )
    first.start()
    sent = []
    for t in list(range(1, steps)) + [0]:
        for ref, _, (pair_buf, _, _, _), (pair_send, pair_recv, *_) in sums:
            copy = remote(
                ref.at[after[t] + partner - here],
                pair_buf.at[t],
                pair_send.at[t],
                pair_recv.at[t],
                on_blk(partner),
            )
            copy.start()
            sent.append(copy)
    first.turn()
    down.start()
    down.turn()
    lines = []
    for t in range(1, steps):
        for ref, _, (pair_buf, turn_buf, line_buf, _), some in sums:
            pair_send, pair_recv, line_send, line_recv = some[:4]
            remote(
                pair_buf.at[t], pair_buf.at[t], pair_send.at[t], pair_recv.at[t], on_blk(partner)
            ).wait_recv()

            def add(group, carry):
                turn_buf[t, group] = (
                    ref[after[t], group].astype(f32) + pair_buf[t, group].astype(f32)
                ).astype(bf16)
                return carry

            lax.fori_loop(0, ref.shape[1], add, 0)
            copy = remote(
                turn_buf.at[t], line_buf.at[t], line_send.at[t], line_recv.at[t], on_blk(after[t])
            )
            copy.start()
            lines.append(copy)

    def put(shares, local, out_ref, extra_refs):
        for piece in range(PIECES):
            rows = shares.piece(piece)
            value, _ = local(shares.total(piece), rows, *extra_refs)
            out_ref[rows, :] = value.astype(out_ref.dtype)

    put(first, after_first, tokens_grad_ref, (grad_middle_ref, tokens_ref, gain_ref))
    swaps = []
    for ref, out_ref, (pair_buf, _, line_buf, row_buf), some in sums:
        pair_send, pair_recv, line_send, line_recv, swap_send, swap_recv = some
        remote(
            pair_buf.at[0], pair_buf.at[0], pair_send.at[0], pair_recv.at[0], on_blk(partner)
        ).wait_recv()
        for t in range(1, steps):
            remote(
                line_buf.at[t], line_buf.at[t], line_send.at[t], line_recv.at[t], on_blk(after[t])
            ).wait_recv()

        def add_all(group, carry):
            total = ref[here, group].astype(f32) + pair_buf[0, group].astype(f32)
            for t in range(1, steps):
                total = total + line_buf[t, group].astype(f32)
            row_buf[group] = total.astype(bf16)
            return carry

        lax.fori_loop(0, ref.shape[1], add_all, 0)
        for kind, other in enumerate((near, far, cross)):
            copy = remote(
                row_buf.at[other],
                out_ref.at[me],
                swap_send.at[kind],
                swap_recv.at[kind],
                on_head(other),
            )
            copy.start()
            swaps.append(copy)
        out_ref[me] = row_buf[me]
    put(down, after_down, result_ref, (middle_ref,))
    for _, out_ref, _, some in sums:
        for kind, other in enumerate((near, far, cross)):
            block = out_ref.at[other]
            remote(
                block, block, some[4].at[kind], some[5].at[kind], on_head(other)
            ).wait_recv()
    for copy in sent + lines + swaps:
        copy.wait_send()
    first.finish()
    down.finish()


def finish_last(grad, output_grad, groups, part_first, part_down, grad_middle, tokens, gain, middle,
                number):
    peers = lax.axis_size("blk")
    share = grad.shape[0] // (peers * groups)
    rows, width = tokens.shape
    vmem = pl.BlockSpec(memory_space=pltpu.VMEM)
    half = peers // 2
    widths = (grad.shape[1], output_grad.shape[1])

    def blocks(columns):
        return [pltpu.VMEM((half, groups, share, columns), bf16) for _ in range(3)] + [
            pltpu.VMEM((groups, share, columns), bf16)
        ]

    swap_sems = [pltpu.SemaphoreType.DMA((half,)) for _ in range(4)] + [
        pltpu.SemaphoreType.DMA((3,)) for _ in range(2)
    ]
    return pl.pallas_call(
        finish_last_kernel,
        in_specs=[vmem] * 8,
        out_specs=[vmem] * 4,
        out_shape=[
            jax.ShapeDtypeStruct((groups, share, columns), bf16) for columns in widths
        ]
        + [
            jax.ShapeDtypeStruct((rows, width), f32),
            jax.ShapeDtypeStruct((rows, width), bf16),
        ],
        scratch_shapes=blocks(widths[0])
        + blocks(widths[1])
        + sum_buffers(rows, width)
        + sum_buffers(rows, width)
        + swap_sems
        + swap_sems
        + sum_sems()
        + sum_sems(),
        compiler_params=pltpu.CompilerParams(
            collective_id=number, has_side_effects=True, vmem_limit_bytes=60 << 20
        ),
        cost_estimate=pl.CostEstimate(
            flops=80_000_000_000, transcendentals=0, bytes_accessed=40_000_000
        ),
        name="finish_last",
    )(
        grad.reshape(peers, groups, share, widths[0]),
        output_grad.reshape(peers, groups, share, widths[1]),
        part_first, part_down, grad_middle, tokens, gain, middle,
    )


def inverse_rms(value):
    return lax.rsqrt(jnp.mean(value * value, axis=1, keepdims=True) + epsilon)


def through_norm(grad, value):
    factor = inverse_rms(value)
    normed = value * factor
    return factor * (grad - normed * jnp.mean(grad * normed, axis=1, keepdims=True))


def after_attention(total, here, tokens_ref, gain_ref):
    middle = tokens_ref[here, :].astype(f32) + total
    return middle, middle * inverse_rms(middle) * gain_ref[0:1, :]


def after_hidden(total, here, cotangent_ref, middle_ref, gain_ref):
    grad = cotangent_ref[here, :].astype(f32) + through_norm(
        total * gain_ref[0:1, :], middle_ref[here, :]
    )
    return grad, grad


def after_first(total, here, grad_ref, tokens_ref, gain_ref):
    grad = grad_ref[here, :] + through_norm(
        total * gain_ref[0:1, :], tokens_ref[here, :].astype(f32)
    )
    return grad, None


def after_down(total, here, middle_ref):
    return middle_ref[here, :] + total, None


FEED_TILE = 256
FEED_COLUMNS = 512


def feed_kernel(input_ref, cotangent_ref, weight_ref, down_ref, grad_input_ref, grad_ref, total,
                down_sum, input_sum, turned):
    step = pl.program_id(0)
    width = input_ref.shape[1]
    hidden_width = weight_ref.shape[1] // 3
    inputs, cotangent = input_ref[...], cotangent_ref[...]
    turned[0] = inputs.T
    turned[1] = cotangent.T

    def columns(which, n):
        return pl.ds(pl.multiple_of(which * hidden_width + n * FEED_COLUMNS, FEED_COLUMNS), FEED_COLUMNS)

    def chunk(n, carry):
        gate_at, up_at, down_at = columns(0, n), columns(1, n), columns(2, n)
        gate = dot(inputs, weight_ref[:, gate_at])
        up = dot(inputs, weight_ref[:, up_at])
        grad_hidden = dot(cotangent, weight_ref[:, down_at])
        opening = jax.nn.sigmoid(gate)
        active = gate * opening
        hidden = (active * up).astype(bf16)
        grad_gate = (grad_hidden * up * opening * (1.0 + gate * (1.0 - opening))).astype(bf16)
        grad_up = (grad_hidden * active).astype(bf16)
        down = dot(hidden, weight_ref[:, down_at], NT)
        back = dot(grad_gate, weight_ref[:, gate_at], NT) + dot(grad_up, weight_ref[:, up_at], NT)

        @pl.when(n == 0)
        def _():
            down_sum[...] = down
            input_sum[...] = back

        @pl.when(n > 0)
        def _():
            down_sum[...] += down
            input_sum[...] += back

        for at, side, grad in ((gate_at, 0, grad_gate), (up_at, 0, grad_up), (down_at, 1, hidden)):

            @pl.when(step == 0)
            def _():
                total[:, at] = dot(turned[side], grad)

            @pl.when(step > 0)
            def _():
                total[:, at] += dot(turned[side], grad)

        return carry

    lax.fori_loop(0, hidden_width // FEED_COLUMNS, chunk, 0)
    down_ref[...] = down_sum[...].astype(bf16)
    grad_input_ref[...] = input_sum[...].astype(bf16)

    @pl.when(step == pl.num_programs(0) - 1)
    def _():
        def store(n, carry):
            at = pl.ds(pl.multiple_of(n * 128, 128), 128)
            grad_ref[at, :] = total[at, :].astype(bf16)
            return carry

        lax.fori_loop(0, width // 128, store, 0)


def feed(inputs, cotangent, weight):
    rows, width = inputs.shape
    columns = weight.shape[1]
    tile = pl.BlockSpec((FEED_TILE, width), lambda n: (n, 0))
    whole = pl.BlockSpec((width, columns), lambda n: (0, 0), pipeline_mode=pl.Buffered(1))
    return pl.pallas_call(
        feed_kernel,
        grid=(rows // FEED_TILE,),
        in_specs=[tile, tile, whole],
        out_specs=[tile, tile, whole],
        out_shape=[
            jax.ShapeDtypeStruct((rows, width), bf16),
            jax.ShapeDtypeStruct((rows, width), bf16),
            jax.ShapeDtypeStruct((width, columns), bf16),
        ],
        scratch_shapes=[
            pltpu.VMEM((width, columns), f32),
            pltpu.VMEM((FEED_TILE, width), f32),
            pltpu.VMEM((FEED_TILE, width), f32),
            pltpu.VMEM((2, width, FEED_TILE), bf16),
        ],
        compiler_params=pltpu.CompilerParams(vmem_limit_bytes=60 << 20),
        cost_estimate=pl.CostEstimate(
            flops=6 * rows * width * columns, transcendentals=rows * columns // 3,
            bytes_accessed=45_000_000,
        ),
        name="feed",
    )(inputs, cotangent, weight)


def over_tokens(operand, other_side):
    return lax.dot_general(
        operand, other_side, (((0,), (0,)), ((), ())), preferred_element_type=f32
    )


def sent_columns(pieces, groups):
    packed = jnp.concatenate(
        [piece.reshape(piece.shape[0], groups, -1) for piece in pieces], axis=2
    )
    mine = lax.all_to_all(packed, "head", split_axis=1, concat_axis=0, tiled=True)
    return mine.reshape(mine.shape[0], mine.shape[2])


def all_rows(mine):
    return lax.all_gather(mine, "blk", axis=0, tiled=True)


def row_sums(grad):
    return lax.psum_scatter(grad, "blk", scatter_dimension=0, tiled=True)


def own_rows(summed, groups):
    rows, columns = summed.shape
    parts = lax.all_to_all(
        summed.reshape(groups, rows // groups, columns), "head", split_axis=0, concat_axis=0
    )
    return jnp.swapaxes(parts, 0, 1).astype(f32)


def body(
    tokens,
    segment,
    norm1_gain,
    w_query,
    w_key,
    w_value,
    w_gate_out,
    w_forget,
    forget_bias,
    w_output,
    norm2_gain,
    w_gate,
    w_up,
    w_down,
    cotangent,
):
    token_rows, model_width = tokens.shape
    groups = lax.axis_size("head")
    head_count = forget_bias.shape[0]
    local_heads = head_count // groups
    local_width = model_width // groups
    hidden_width = w_gate.shape[1] // groups
    rows = token_rows * groups
    share = w_query.shape[0]
    group = lax.axis_index("head")

    low = lambda array: array.astype(bf16)
    spread = lambda gain: jnp.broadcast_to(low(gain)[:, None, None], (share, groups, 1))
    forget_low = low(w_forget).reshape(share, groups, local_heads)
    rest = LANES - local_heads - 2
    small = jnp.concatenate(
        [forget_low, spread(norm1_gain), spread(norm2_gain), jnp.zeros((share, groups, rest), bf16)],
        axis=2,
    )
    pack = jnp.concatenate(
        [
            low(piece).reshape(share, groups, -1)
            for piece in (w_key, w_value, small, w_query, w_gate_out, w_output)
        ],
        axis=2,
    )
    first, tokens_all, cotangent_all = gather_first(
        jnp.swapaxes(pack, 0, 1), tokens, cotangent, 0
    )
    kv_width = 2 * local_width + LANES
    output_weight = first[:, kv_width + 2 * local_width :]

    segment_plus = segment + 1
    earlier_segment = passed_along(segment_plus, "blk", 1)
    window = jnp.concatenate([earlier_segment, segment_plus])
    begins = jnp.sum(
        (window[:, None] < segment_plus[None, :]).astype(jnp.int32), axis=0
    )
    tiles = begins.reshape(rows // Q_TILE, Q_TILE)
    ranges = jnp.stack([tiles[:, 0] // K_TILE, (tiles[:, -1] + K_TILE - 1) // K_TILE])
    begins = jnp.broadcast_to(begins[None, :], (8, rows))

    def gain_rows(column):
        gain = first[:, 2 * local_width + local_heads + column].astype(f32)
        return jnp.broadcast_to(gain[None, :], (8, model_width))

    gain1, gain2 = gain_rows(0), gain_rows(1)
    wide_all = tokens_all.astype(f32)
    input1 = lax.optimization_barrier(
        (wide_all * inverse_rms(wide_all) * gain1[0:1]).astype(bf16)
    )
    key_value = dot(input1, first[:, : 2 * local_width]).astype(bf16)
    bias = lax.dynamic_slice_in_dim(forget_bias, group * local_heads, local_heads, 0)
    bias = jnp.pad(bias, (0, LANES - local_heads))
    forget = dot(input1, first[:, 2 * local_width : kv_width]) + bias[None, :]
    forget = forget.astype(bf16).astype(f32)
    terms, halo_terms = decay_terms(jax.nn.log_sigmoid(forget), local_heads)
    earlier_kv = passed_along(jnp.concatenate([key_value, halo_terms], axis=1), "blk", 1)
    query = dot(input1, first[:, kv_width : kv_width + local_width]).astype(bf16)
    gate_raw = dot(
        input1, first[:, kv_width + local_width : kv_width + 2 * local_width]
    )

    so_far = attend(True, ranges, query, key_value, terms, terms, begins, local_heads)
    mine = sent_columns([low(w_gate), low(w_up), low(w_down)], groups)
    mine, earlier_kv, so_far = lax.optimization_barrier((mine, earlier_kv, so_far))
    second = all_rows(mine)
    attended, lse = attend(
        False, ranges, query, earlier_kv, terms, earlier_kv, begins, local_heads, so_far
    )
    opened = jax.nn.sigmoid(gate_raw)
    attended_wide = attended.astype(f32)
    gated = (opened * attended_wide).astype(bf16)
    branch = dot(gated, output_weight, NT).astype(bf16)
    middle, input2 = exchange(after_attention, branch, [tokens, gain2], 1, "exchange_middle")
    down, grad_input2, second_grad = feed(input2, cotangent_all, second)
    second_part = row_sums(second_grad)
    grad_middle, grad_branch = exchange(
        after_hidden, grad_input2, [cotangent, middle, gain2], 2, "exchange_hidden"
    )

    grad_gated = dot(grad_branch, output_weight)
    grad_attended = (grad_gated * opened).astype(bf16)
    grad_gate_pre = (grad_gated * attended_wide * opened * (1.0 - opened)).astype(bf16)
    dq_prev, rows_prev, dkv_prev, decay_prev = attend_back(
        False, ranges, query, earlier_kv, terms, earlier_kv, begins, grad_attended, attended,
        lse, local_heads,
    )
    dkv_later = passed_along(dkv_prev, "blk", -1)
    decay_later = passed_along(decay_prev[:, :8], "blk", -1)
    decay_later = jnp.pad(decay_later, ((0, 0), (0, LANES - 8)))
    dq, dk_own, dv_own, decay_own = attend_back(
        True, ranges, query, key_value, terms, terms, begins, grad_attended, attended,
        lse, local_heads, (dq_prev, rows_prev),
    )
    dk = (dk_own + dkv_later[0].astype(f32)).astype(bf16)
    dv = (dv_own + dkv_later[1].astype(f32)).astype(bf16)
    logf_grad = decay_back(decay_own, decay_later)
    forget_grad = jnp.where(
        jnp.arange(LANES)[None, :] < local_heads, logf_grad * jax.nn.sigmoid(-forget), 0.0
    ).astype(bf16)
    grads = jnp.concatenate([dk, dv, forget_grad, dq, grad_gate_pre], axis=1)
    first_grad = over_tokens(input1, grads)
    bias_part = jnp.sum(forget_grad.astype(f32), axis=0)
    row = jnp.arange(model_width)[:, None] % share
    column = jnp.arange(kv_width + 2 * local_width)[None, :]
    spread_bias = jnp.sum(
        jnp.where(row == jnp.arange(LANES)[None, :], bias_part[None, :], 0.0), axis=1, keepdims=True
    )
    first_grad = jnp.where(
        column == 2 * local_width + local_heads, spread_bias, first_grad
    ).astype(bf16)
    output_grad = over_tokens(grad_branch, gated).astype(bf16)
    grad_input1 = dot(grads, first[:, : kv_width + 2 * local_width], NT).astype(bf16)
    second_sum = own_rows(second_part, groups)
    grad_input1, second_sum = lax.optimization_barrier((grad_input1, second_sum))
    first_sum, output_sum, tokens_grad, result = finish_last(
        first_grad, output_grad, groups, grad_input1, down, grad_middle, tokens, gain1, middle, 3
    )
    first_sum = jnp.swapaxes(first_sum, 0, 1).astype(f32)
    output_sum = jnp.swapaxes(output_sum, 0, 1).astype(f32)

    def columns(array, start, width):
        return array[:, :, start : start + width].reshape(share, groups * width)

    key_sum, value_sum = (columns(first_sum, n * local_width, local_width) for n in range(2))
    forget_sum = columns(first_sum, 2 * local_width, local_heads)
    bias_total = first_sum[:local_heads, :, 2 * local_width + local_heads].T.reshape(head_count)
    query_sum, gate_out_sum = (
        columns(first_sum, kv_width + n * local_width, local_width) for n in range(2)
    )
    output_total = columns(output_sum, 0, local_width)
    gate_sum, up_sum, down_sum = (
        columns(second_sum, n * hidden_width, hidden_width) for n in range(3)
    )

    def along(weight, grad):
        return jnp.sum(low(weight).astype(f32) * grad, axis=1)

    gain1_total = (
        along(w_query, query_sum)
        + along(w_key, key_sum)
        + along(w_value, value_sum)
        + along(w_gate_out, gate_out_sum)
        + along(w_forget, forget_sum)
    ) / low(norm1_gain).astype(f32)
    gain2_total = (along(w_gate, gate_sum) + along(w_up, up_sum)) / low(norm2_gain).astype(f32)
    return (
        result,
        tokens_grad,
        gain1_total,
        query_sum,
        key_sum,
        value_sum,
        gate_out_sum,
        forget_sum,
        bias_total,
        output_total,
        gain2_total,
        gate_sum,
        up_sum,
        down_sum,
    )


def solution(mesh):
    both = ("blk", "head")
    matrix, vector = P(both, None), P(both)
    return jax.shard_map(
        body,
        mesh=mesh,
        in_specs=(
            matrix, P("blk"), vector, matrix, matrix, matrix, matrix, matrix, P(), matrix, vector,
            matrix, matrix, matrix, matrix,
        ),
        out_specs=(
            matrix, matrix, vector, matrix, matrix, matrix, matrix, matrix, P(), matrix, vector,
            matrix, matrix, matrix,
        ),
        check_vma=False,
    )
```

```python
import functools

import jax
import jax.numpy as jnp
from jax import lax
from jax.experimental import pallas as pl
from jax.experimental.pallas import tpu as pltpu
from jax.sharding import PartitionSpec as P

epsilon = 1e-06
LANES = 128
Q_TILE = 512
K_TILE = 512
FAR = -1e30
NT = (((1,), (1,)), ((), ()))
NN = (((1,), (0,)), ((), ()))
bf16 = jnp.bfloat16
f32 = jnp.float32


def dot(a, b, dims=NN, **kw):
    return lax.dot_general(a, b, dims, preferred_element_type=f32, **kw)


def passed_along(array, axis, by):
    peers = lax.axis_size(axis)
    pairs = [(i, i + by) for i in range(peers) if 0 <= i + by < peers]
    return lax.ppermute(array, axis, pairs)


def split3(value):
    high = value.astype(bf16)
    rest = value - high.astype(f32)
    mid = rest.astype(bf16)
    low = (rest - mid.astype(f32)).astype(bf16)
    return high, mid, low


def running(value_of, steps, rows, upper):
    place = lax.broadcasted_iota(jnp.int32, (rows, rows), 0)
    other = lax.broadcasted_iota(jnp.int32, (rows, rows), 1)
    tri = jnp.where((other >= place) if upper else (other <= place), 1.0, 0.0).astype(bf16)
    outs = [None] * steps
    carry = jnp.zeros((1, LANES), f32)
    order = range(steps - 1, -1, -1) if upper else range(steps)
    for n in order:
        block = value_of(n)
        total = sum(dot(tri, part) for part in split3(block)) + carry
        outs[n] = total
        carry = total[0:1] if upper else total[rows - 1 : rows]
    return outs, carry


PROJECT_TILE = 256


def project_kernel(local_heads, tokens_ref, gain_ref, weight_ref, bias_ref, input_ref, out_ref,
                   forget_ref, carry_ref):
    rows = tokens_ref.shape[0]
    wide = weight_ref.shape[1] - LANES

    @pl.when(pl.program_id(0) == 0)
    def _():
        carry_ref[...] = jnp.zeros_like(carry_ref)

    tokens = tokens_ref[...].astype(f32)
    input1 = (tokens * inverse_rms(tokens) * gain_ref[0:1, :]).astype(bf16)
    input_ref[...] = input1
    raw = dot(input1, weight_ref[...])
    out_ref[:, :wide] = raw[:, :wide].astype(bf16)
    forget = (raw[:, wide:] + bias_ref[0:1, :]).astype(bf16).astype(f32)
    forget_ref[...] = forget
    lane = lax.broadcasted_iota(jnp.int32, (rows, LANES), 1)
    logf = jnp.minimum(forget, 0.0) - jnp.log1p(jnp.exp(-jnp.abs(forget)))
    logf = jnp.where(lane < local_heads, logf, 0.0)
    place = lax.broadcasted_iota(jnp.int32, (rows, rows), 0)
    other = lax.broadcasted_iota(jnp.int32, (rows, rows), 1)
    tri = jnp.where(other <= place, 1.0, 0.0).astype(bf16)
    sums = sum(dot(tri, part) for part in split3(logf)) + carry_ref[0:1, :]
    carry_ref[0:1, :] = sums[rows - 1 : rows, :]
    high, mid, low = split3(sums)
    out_ref[:, wide:] = (
        high.astype(f32)
        + pltpu.roll(mid.astype(f32), local_heads, 1)
        + pltpu.roll(low.astype(f32), 2 * local_heads, 1)
        + jnp.where(lane == 3 * local_heads, 1.0, 0.0)
    ).astype(bf16)


def project(tokens, gain, weight, bias, wide, local_heads):
    rows, width = tokens.shape

    def tile(columns):
        return pl.BlockSpec((PROJECT_TILE, columns), lambda n: (n, 0))

    def whole(*shape):
        return pl.BlockSpec(shape, lambda n: (0, 0))

    return pl.pallas_call(
        functools.partial(project_kernel, local_heads),
        grid=(rows // PROJECT_TILE,),
        in_specs=[tile(width), whole(8, width), whole(width, wide + LANES), whole(8, LANES)],
        out_specs=[tile(width), tile(wide + LANES), tile(LANES)],
        out_shape=[
            jax.ShapeDtypeStruct((rows, width), bf16),
            jax.ShapeDtypeStruct((rows, wide + LANES), bf16),
            jax.ShapeDtypeStruct((rows, LANES), f32),
        ],
        scratch_shapes=[pltpu.VMEM((8, LANES), f32)],
        cost_estimate=pl.CostEstimate(
            flops=2 * rows * width * (wide + LANES), transcendentals=rows * LANES,
            bytes_accessed=20_000_000,
        ),
        name="project",
    )(tokens, gain, weight, bias)


def decay_back_kernel(own_ref, halo_ref, out_ref):
    rows = 256
    steps = own_ref.shape[0] // rows
    own, _ = running(lambda n: own_ref[n * rows : (n + 1) * rows, :], steps, rows, True)
    halo, _ = running(lambda n: halo_ref[n * rows : (n + 1) * rows, :], steps, rows, False)
    for n in range(steps):
        part = slice(n * rows, (n + 1) * rows)
        out_ref[part, :] = own[n] + (halo[n] - halo_ref[part, :])


def decay_back(own, halo):
    return pl.pallas_call(
        decay_back_kernel,
        out_shape=jax.ShapeDtypeStruct(own.shape, f32),
        name="decay_back",
    )(own, halo)


QUERY, KEY, TOTAL = range(3)


def placing(pair, local_heads, role):
    row = lax.broadcasted_iota(jnp.int32, (LANES, LANES), 0)
    col = lax.broadcasted_iota(jnp.int32, (LANES, LANES), 1)
    head = jnp.where(col < 64, 2 * pair + 1, 2 * pair)
    spot = jnp.where(col < 64, col, col - 64)
    term = spot - 3 * role
    is_term = (term >= 0) & (term < 3) & (row == term * local_heads + head)
    if role == QUERY:
        ones = (spot >= 3) & (spot < 9)
    else:
        ones = (spot < 3) & (role == KEY)
    is_one = ones & (row == 3 * local_heads)
    sign = -1.0 if role == KEY else 1.0
    return (jnp.where(is_term, sign, 0.0) + jnp.where(is_one, 1.0, 0.0)).astype(bf16)


def allowed_pairs(first_key, query_tile, rows, begin_row):
    shape = (K_TILE, Q_TILE)
    key_place = first_key + lax.broadcasted_iota(jnp.int32, shape, 0)
    query_place = rows + query_tile * Q_TILE + lax.broadcasted_iota(jnp.int32, shape, 1)
    return (key_place >= begin_row) & (key_place <= query_place)


def key_range(ranges_ref, query_tile, rows, own):
    count = rows // K_TILE
    base = count if own else 0
    first = jnp.clip(ranges_ref[0, query_tile] - base, 0, count)
    full = jnp.clip(ranges_ref[1, query_tile] - base, first, count)
    return first, full


def key_loops(ranges_ref, query_tile, rows, own, step, carry):
    first, full = key_range(ranges_ref, query_tile, rows, own)
    inside = query_tile * (Q_TILE // K_TILE) if own else rows // K_TILE
    full = jnp.minimum(full, inside)
    carry = lax.fori_loop(first, full, functools.partial(step, True), carry)
    carry = lax.fori_loop(full, inside, functools.partial(step, False), carry)
    if own:
        carry = lax.fori_loop(
            inside, inside + Q_TILE // K_TILE, functools.partial(step, True), carry
        )
    return carry


def tile_of(number, size):
    return pl.ds(pl.multiple_of(number * size, size), size)


def fill_keys(pair, local_heads, own, first, key_ref, terms_ref, keys):
    place = placing(pair, local_heads, KEY)
    lane = lax.broadcasted_iota(jnp.int32, (K_TILE, LANES), 1)
    rows = key_ref.shape[0]
    total = 0.0
    if not own:
        last = dot(terms_ref[rows - 16 : rows, :], placing(pair, local_heads, TOTAL))
        total = last[15:16, :]

    def fill(n, carry):
        here = tile_of(n, K_TILE)
        extra = (dot(terms_ref[here, :], place) + total).astype(bf16)
        key = key_ref[here, :]
        keys[0][here, :] = jnp.where(lane < 64, key, extra)
        keys[1][here, :] = jnp.where(lane < 64, extra, key)
        return carry

    lax.fori_loop(first, rows // K_TILE, fill, 0)


def query_tiles(q_ref, terms_ref, place, here, scaling):
    lane = lax.broadcasted_iota(jnp.int32, (Q_TILE, LANES), 1)
    extra = dot(terms_ref[here, :], place).astype(bf16)
    query = (q_ref[here, :].astype(f32) * scaling).astype(bf16)
    return jnp.where(lane < 64, query, extra), jnp.where(lane < 64, extra, query)


def attend_kernel(local_heads, own, ranges_ref, q_ref, k_ref, v_ref, t_query_ref, t_key_ref,
                  begin_ref, *refs):
    if own:
        acc_out_ref, state_out_ref, key0, key1, values, acc0, acc1 = refs
    else:
        acc_in_ref, state_in_ref, o_ref, lse_ref, key0, key1, values, acc0, acc1 = refs
    pair = pl.program_id(0)
    rows = q_ref.shape[0]
    base = rows if own else 0
    keys, accs = (key0, key1), (acc0, acc1)
    first, _ = key_range(ranges_ref, 0, rows, own)
    fill_keys(pair, local_heads, own, first, k_ref, t_key_ref, keys)

    def turn(n, carry):
        values[:, tile_of(n, K_TILE)] = v_ref[tile_of(n, K_TILE), :].T
        return carry

    lax.fori_loop(first, rows // K_TILE, turn, 0)
    place = placing(pair, local_heads, QUERY)

    def query_loop(tile, carry):
        here = tile_of(tile, Q_TILE)
        queries = query_tiles(q_ref, t_query_ref, place, here, 64**-0.5)
        begin_row = begin_ref[0:1, here]
        if own:
            low = jnp.full((1, Q_TILE), FAR, f32)
            zero = jnp.zeros((1, Q_TILE), f32)
            state = (low, zero, low, zero)
            for acc in accs:
                acc[...] = jnp.zeros_like(acc)
        else:
            state = tuple(state_in_ref[n : n + 1, here] for n in range(4))
            for h in range(2):
                accs[h][...] = acc_in_ref[64 * h : 64 * (h + 1), here]

        def step(masked, number, state):
            there = tile_of(number, K_TILE)
            fresh = []
            if masked:
                allowed = allowed_pairs(base + number * K_TILE, tile, rows, begin_row)
            for h in range(2):
                largest, total = state[2 * h], state[2 * h + 1]
                scores = dot(keys[h][there, :], queries[h], NT)
                if masked:
                    scores = jnp.where(allowed, scores, FAR)
                now = jnp.maximum(largest, jnp.max(scores, axis=0, keepdims=True))
                fade = jnp.exp(largest - now)
                weights = jnp.exp(scores - now)
                total = total * fade + jnp.sum(weights, axis=0, keepdims=True)
                accs[h][...] = accs[h][...] * fade + dot(
                    values[64 * h : 64 * (h + 1), there], weights.astype(bf16)
                )
                fresh += [now, total]
            return tuple(fresh)

        state = key_loops(ranges_ref, tile, rows, own, step, state)
        if own:
            for h in range(2):
                acc_out_ref[64 * h : 64 * (h + 1), here] = accs[h][...]
            for n in range(4):
                state_out_ref[n : n + 1, here] = state[n]
        else:
            mixed = jnp.concatenate(
                [accs[h][...] * (1.0 / state[2 * h + 1]) for h in range(2)], axis=0
            )
            o_ref[here, :] = mixed.T.astype(bf16)
            for h in range(2):
                lse_ref[h : h + 1, here] = state[2 * h] + jnp.log(state[2 * h + 1])
        return carry

    lax.fori_loop(0, rows // Q_TILE, query_loop, 0)


def lane_block(rows, offset):
    return pl.BlockSpec((rows, LANES), lambda p, *_: (0, offset + p))


def fixed(shape):
    return pl.BlockSpec(shape, lambda p, *_: (0, 0))


def pair_block(height, rows):
    return pl.BlockSpec((height, rows), lambda p, *_: (p, 0))


def terms_block(rows, pairs):
    return pl.BlockSpec((rows, LANES), lambda p, *_: (0, 2 * pairs))


def attend(own, ranges, query, key_value, own_terms, begins, local_heads, so_far=()):
    rows = query.shape[0]
    pairs = local_heads // 2
    running_specs = [pair_block(LANES, rows), pair_block(8, rows)]
    running_shape = (
        jax.ShapeDtypeStruct((LANES * pairs, rows), f32),
        jax.ShapeDtypeStruct((8 * pairs, rows), f32),
    )
    final_specs = [lane_block(rows, 0), pair_block(8, rows)]
    final_shape = (
        jax.ShapeDtypeStruct((rows, pairs * LANES), bf16),
        jax.ShapeDtypeStruct((8 * pairs, rows), f32),
    )
    return pl.pallas_call(
        functools.partial(attend_kernel, local_heads, own),
        grid_spec=pltpu.PrefetchScalarGridSpec(
            num_scalar_prefetch=1,
            grid=(pairs,),
            in_specs=[
                lane_block(rows, 0),
                lane_block(rows, 0),
                lane_block(rows, pairs),
                terms_block(rows, pairs),
                terms_block(rows, pairs),
                fixed((8, rows)),
            ]
            + ([] if own else running_specs),
            out_specs=running_specs if own else final_specs,
            scratch_shapes=[
                pltpu.VMEM((rows, LANES), bf16),
                pltpu.VMEM((rows, LANES), bf16),
                pltpu.VMEM((LANES, rows), bf16),
                pltpu.VMEM((64, Q_TILE), f32),
                pltpu.VMEM((64, Q_TILE), f32),
            ],
        ),
        out_shape=running_shape if own else final_shape,
        cost_estimate=pl.CostEstimate(
            flops=40_000_000_000 if own else 10_000_000_000,
            transcendentals=20_000_000,
            bytes_accessed=12_000_000,
        ),
        name="attend_own" if own else "attend_prev",
    )(ranges, query, key_value, key_value, own_terms, key_value, begins, *so_far)


def attend_back_kernel(local_heads, own, ranges_ref, q_ref, k_ref, v_ref, t_query_ref, t_key_ref,
                       begin_ref, grad_ref, o_ref, lse_ref, *refs):
    if own:
        dq_in_ref, decay_in_ref, dq_ref, dk_ref, dv_ref, decay_ref = refs[:6]
    else:
        dq_ref, row_decay_ref, dkv_ref, decay_ref = refs[:4]
        dk_ref, dv_ref = dkv_ref.at[0], dkv_ref.at[1]
    key0, key1, key_t0, key_t1, dk0, dk1, dv, dq0, dq1 = refs[-9:]
    pair = pl.program_id(0)
    rows = q_ref.shape[0]
    base = rows if own else 0
    keys, keys_t, dks, dqs = (key0, key1), (key_t0, key_t1), (dk0, dk1), (dq0, dq1)
    first, _ = key_range(ranges_ref, 0, rows, own)
    fill_keys(pair, local_heads, own, first, k_ref, t_key_ref, keys)

    def turn(n, carry):
        here = tile_of(n, K_TILE)
        for h in range(2):
            keys_t[h][:, here] = keys[h][here, :].T
        return carry

    lax.fori_loop(first, rows // K_TILE, turn, 0)
    for ref in (dk0, dk1, dv):
        ref[...] = jnp.zeros_like(ref)
    place = placing(pair, local_heads, QUERY)
    lane = lax.broadcasted_iota(jnp.int32, (Q_TILE, LANES), 1)
    pick_row = lax.broadcasted_iota(jnp.int32, (8, LANES), 0)
    pick_lane = lax.broadcasted_iota(jnp.int32, (8, LANES), 1)
    pick = jnp.where((pick_lane // 64) == pick_row, 1.0, 0.0)
    sums_ref = decay_ref if own else row_decay_ref

    @pl.when(pair == 0)
    def _():
        if own:
            decay_ref[...] = decay_in_ref[...]
        else:
            decay_ref[...] = jnp.zeros_like(decay_ref)
            row_decay_ref[...] = jnp.zeros_like(row_decay_ref)

    def query_tile(tile):
        here = tile_of(tile, Q_TILE)
        queries = query_tiles(q_ref, t_query_ref, place, here, 64**-0.5)
        begin_row = begin_ref[0:1, here]
        grad = grad_ref[here, :]
        nothing = jnp.zeros_like(grad)
        grads = (jnp.where(lane < 64, grad, nothing), jnp.where(lane < 64, nothing, grad))
        product = grad.astype(f32) * o_ref[here, :].astype(f32)
        inner = dot(pick, product, NT, precision=lax.Precision.HIGHEST)
        for dq in dqs:
            dq[...] = jnp.zeros_like(dq)

        def step(masked, number, state):
            there = tile_of(number, K_TILE)
            if masked:
                allowed = allowed_pairs(base + number * K_TILE, tile, rows, begin_row)
            value = v_ref[there, :]
            value_part = 0.0
            for h in range(2):
                scores = dot(keys[h][there, :], queries[h], NT)
                prob = jnp.exp(scores - lse_ref[h : h + 1, here])
                if masked:
                    prob = jnp.where(allowed, prob, 0.0)
                grad_prob = dot(value, grads[h], NT)
                grad_score = (prob * (grad_prob - inner[h : h + 1, :])).astype(bf16)
                value_part = value_part + dot(prob.astype(bf16), grads[h])
                dks[h][there, :] += dot(grad_score, queries[h])
                dqs[h][...] += dot(keys_t[h][:, there], grad_score)
            dv[there, :] += value_part
            return state

        key_loops(ranges_ref, tile, rows, own, step, 0)
        turned = [dq[...].T for dq in dqs]
        dq_tile = jnp.where(lane < 64, turned[0], turned[1]) * 64**-0.5
        if own:
            dq_tile = dq_tile + dq_in_ref[here, :]
        dq_ref[here, :] = dq_tile.astype(dq_ref.dtype)
        sums = sums_ref[here, :]
        sums = sums + jnp.where(lane == 2 * pair, turned[0][:, 64:65], 0.0)
        sums = sums + jnp.where(lane == 2 * pair + 1, turned[1][:, 0:1], 0.0)
        sums_ref[here, :] = sums

    def query_loop(tile, carry):
        if own:
            query_tile(tile)
        else:
            reaches = key_range(ranges_ref, tile, rows, own)[0] < rows // K_TILE
            pl.when(reaches)(lambda: query_tile(tile))

            @pl.when(jnp.logical_not(reaches))
            def _():
                dq_ref[tile_of(tile, Q_TILE), :] = jnp.zeros((Q_TILE, LANES), dq_ref.dtype)

        return carry

    lax.fori_loop(0, rows // Q_TILE, query_loop, 0)
    sign = -1.0 if own else 1.0

    def finish(n, carry):
        here = tile_of(n, Q_TILE)
        left, right = dk0[here, :], dk1[here, :]
        dk_ref[here, :] = jnp.where(lane < 64, left, right).astype(dk_ref.dtype)
        dv_ref[here, :] = dv[here, :].astype(dv_ref.dtype)
        decay = decay_ref[here, :]
        decay = decay + jnp.where(lane == 2 * pair, sign * left[:, 67:68], 0.0)
        decay = decay + jnp.where(lane == 2 * pair + 1, sign * right[:, 3:4], 0.0)
        decay_ref[here, :] = decay
        return carry

    lax.fori_loop(0, rows // Q_TILE, finish, 0)


def attend_back(
    own, ranges, query, key_value, own_terms, begins, grad, mixed, lse, local_heads,
    so_far=(),
):
    rows = query.shape[0]
    pairs = local_heads // 2
    wide = jax.ShapeDtypeStruct((rows, pairs * LANES), f32)
    sums = jax.ShapeDtypeStruct((rows, LANES), f32)
    if own:
        out_specs = [lane_block(rows, 0)] * 3 + [fixed((rows, LANES))]
        out_shape = (jax.ShapeDtypeStruct(wide.shape, bf16), wide, wide, sums)
    else:
        both = pl.BlockSpec((2, rows, LANES), lambda p, *_: (0, 0, p))
        out_specs = [lane_block(rows, 0), fixed((rows, LANES)), both, fixed((rows, LANES))]
        out_shape = (
            wide, sums, jax.ShapeDtypeStruct((2, rows, pairs * LANES), bf16), sums,
        )
    return pl.pallas_call(
        functools.partial(attend_back_kernel, local_heads, own),
        grid_spec=pltpu.PrefetchScalarGridSpec(
            num_scalar_prefetch=1,
            grid=(pairs,),
            in_specs=[
                lane_block(rows, 0),
                lane_block(rows, 0),
                lane_block(rows, pairs),
                terms_block(rows, pairs),
                terms_block(rows, pairs),
                fixed((8, rows)),
                lane_block(rows, 0),
                lane_block(rows, 0),
                pair_block(8, rows),
            ]
            + ([lane_block(rows, 0), fixed((rows, LANES))] if own else []),
            out_specs=out_specs,
            scratch_shapes=[
                pltpu.VMEM((rows, LANES), bf16),
                pltpu.VMEM((rows, LANES), bf16),
                pltpu.VMEM((LANES, rows), bf16),
                pltpu.VMEM((LANES, rows), bf16),
                pltpu.VMEM((rows, LANES), f32),
                pltpu.VMEM((rows, LANES), f32),
                pltpu.VMEM((rows, LANES), f32),
                pltpu.VMEM((LANES, Q_TILE), f32),
                pltpu.VMEM((LANES, Q_TILE), f32),
            ],
        ),
        out_shape=out_shape,
        cost_estimate=pl.CostEstimate(
            flops=80_000_000_000 if own else 15_000_000_000,
            transcendentals=20_000_000,
            bytes_accessed=25_000_000,
        ),
        name="attend_back_own" if own else "attend_back_prev",
    )(
        ranges, query, key_value, key_value, own_terms, key_value, begins, grad, mixed, lse, *so_far
    )


PIECES = 4


def partners():
    me = lax.axis_index("head")
    near = me + 1 - 2 * (me % 2)
    far = (me + 2) % 4
    cross = (near + 2) % 4
    return me, near, far, cross


def signal(other):
    pl.semaphore_signal(
        pltpu.get_barrier_semaphore(), inc=1, device_id=other, device_id_type=pl.DeviceIdType.MESH
    )


def greet(others):
    for other in others:
        signal(other)
    pl.semaphore_wait(pltpu.get_barrier_semaphore(), len(others))


def remote(source, target, send, receive, other):
    return pltpu.make_async_remote_copy(
        src_ref=source,
        dst_ref=target,
        send_sem=send,
        recv_sem=receive,
        device_id=other,
        device_id_type=pl.DeviceIdType.MESH,
    )


def on_head(index):
    return {"head": index}


def on_blk(index):
    return {"blk": index}


def piece_at(ref, slot, piece, size):
    span = size // PIECES
    return ref.at[pl.ds(pl.multiple_of(slot * size + piece * span, span), span), :]


class Slots:
    def __init__(self, by_device):
        me, near, far, cross = partners()
        if by_device:
            self.own = self.sent_near = self.sent_far = me
            self.near, self.far, self.cross = near, far, cross
            self.passed = far
        else:
            self.own, self.sent_near, self.sent_far = 3, 2, 1
            self.near, self.far, self.cross = 2, 1, 0
            self.passed = 0


def spread_piece(source, all_ref, size, sems, piece, slots):
    me, near, far, _ = partners()
    far_send, far_recv, near_send, near_recv, _, _, own = sems
    copies = (
        remote(source, piece_at(all_ref, slots.sent_far, piece, size), far_send.at[piece],
               far_recv.at[piece], on_head(far)),
        remote(source, piece_at(all_ref, slots.sent_near, piece, size), near_send.at[piece],
               near_recv.at[piece], on_head(near)),
        pltpu.make_async_copy(source, piece_at(all_ref, slots.own, piece, size), own.at[piece]),
    )
    for copy in copies:
        copy.start()
    return copies


def hand_on(all_ref, size, sems, sent, slots):
    me, near, far, cross = partners()
    far_send, far_recv, near_send, near_recv, on_send, on_recv, own = sems
    passed = []
    for piece in range(PIECES):
        there = piece_at(all_ref, slots.far, piece, size)
        remote(there, there, far_send.at[piece], far_recv.at[piece], on_head(far)).wait_recv()
        copy = remote(
            there, piece_at(all_ref, slots.passed, piece, size), on_send.at[piece],
            on_recv.at[piece], on_head(near),
        )
        copy.start()
        passed.append(copy)

    def finish():
        for piece in range(PIECES):
            to_far, to_near, local = sent[piece]
            to_far.wait_send()
            to_near.wait_send()
            local.wait()
            passed[piece].wait_send()
            there = piece_at(all_ref, slots.near, piece, size)
            remote(there, there, near_send.at[piece], near_recv.at[piece], on_head(near)).wait_recv()
            there = piece_at(all_ref, slots.cross, piece, size)
            remote(there, there, on_send.at[piece], on_recv.at[piece], on_head(near)).wait_recv()

    return finish


def gather_sems():
    return [pltpu.SemaphoreType.DMA((PIECES,)) for _ in range(7)]


def blk_peers():
    here = lax.axis_index("blk")
    half = lax.axis_size("blk") // 2
    low, high = here % 2, here // 2
    partner = here + 1 - 2 * low
    after = [((high + t) % half) * 2 + low for t in range(half)]
    return here, partner, after


class Line:
    def __init__(self, block_of, kinds, sems):
        self.block_of, self.kinds = block_of, kinds
        self.pair_send, self.pair_recv, self.up_send, self.up_recv, self.down_send, self.down_recv = sems
        here = lax.axis_index("blk")
        self.half = lax.axis_size("blk") // 2
        self.low, self.high = here % 2, here // 2
        self.partner = here + 1 - 2 * self.low
        self.has_up, self.has_down = self.high < self.half - 1, self.high > 0

    def greet(self, others):
        greet_sum = len(others) + 1
        for other in others + [on_blk(self.partner)]:
            signal(other)
        pl.when(self.has_up)(lambda: signal(on_blk(self.at(self.high + 1))))
        pl.when(self.has_down)(lambda: signal(on_blk(self.at(self.high - 1))))
        ends = (self.high == 0).astype(jnp.int32) + (self.high == self.half - 1).astype(jnp.int32)
        pl.semaphore_wait(pltpu.get_barrier_semaphore(), greet_sum + 2 - ends)

    def at(self, high):
        return high * 2 + self.low

    def pair_copy(self, kind, high, low):
        block = self.block_of(kind, high * 2 + low)
        return remote(
            block, block, self.pair_send.at[kind, high], self.pair_recv.at[kind, high],
            on_blk(self.partner),
        )

    def up_copy(self, kind, high):
        block = self.block_of(kind, self.at(high))
        return remote(
            block, block, self.up_send.at[kind, high], self.up_recv.at[kind, high],
            on_blk(self.at(jnp.minimum(self.high + 1, self.half - 1))),
        )

    def down_copy(self, kind, high):
        block = self.block_of(kind, self.at(high))
        return remote(
            block, block, self.down_send.at[kind, high], self.down_recv.at[kind, high],
            on_blk(self.at(jnp.maximum(self.high - 1, 0))),
        )

    def launch(self, kind):
        self.pair_copy(kind, self.high, self.low).start()
        pl.when(self.has_up)(lambda: self.up_copy(kind, self.high).start())
        pl.when(self.has_down)(lambda: self.down_copy(kind, self.high).start())

    def step(self, t):
        for kind in range(self.kinds):
            below, above = self.high - t, self.high + t

            @pl.when(below >= 0)
            def _():
                self.up_copy(kind, below).wait_recv()
                self.pair_copy(kind, below, self.low).start()
                pl.when(self.has_up)(lambda: self.up_copy(kind, below).start())

            @pl.when(above < self.half)
            def _():
                self.down_copy(kind, above).wait_recv()
                self.pair_copy(kind, above, self.low).start()
                pl.when(self.has_down)(lambda: self.down_copy(kind, above).start())

    def finish(self):
        for kind in range(self.kinds):

            def wait(high, carry):
                self.pair_copy(kind, high, self.low).wait_send()
                self.pair_copy(kind, high, 1 - self.low).wait_recv()

                @pl.when((high <= self.high) & self.has_up)
                def _():
                    self.up_copy(kind, high).wait_send()

                @pl.when((high >= self.high) & self.has_down)
                def _():
                    self.down_copy(kind, high).wait_send()

                return carry

            lax.fori_loop(0, self.half, wait, 0)


def gather_first_kernel(pack_ref, tokens_ref, cotangent_ref, pack_all, tokens_all, cotangent_all,
                        *sems):
    swap_send, swap_recv, swap_own = sems[:3]
    token_sems, cotangent_sems = sems[9:16], sems[16:23]
    me, near, far, cross = partners()
    sources = (me, near, far, cross)
    line = Line(lambda kind, blk: pack_all.at[blk, sources[kind]], 4, sems[3:9])
    here = lax.axis_index("blk")
    line.greet([on_head(near), on_head(far), on_head(cross)])
    swaps = [pltpu.make_async_copy(pack_ref.at[me], pack_all.at[here, me], swap_own)]
    for kind, other in enumerate((near, far, cross)):
        swaps.append(
            remote(
                pack_ref.at[other],
                pack_all.at[here, me],
                swap_send.at[kind],
                swap_recv.at[kind],
                on_head(other),
            )
        )
    for swap in swaps:
        swap.start()
    size = tokens_ref.shape[0]
    span = size // PIECES

    def spread_all(ref, all_ref, some, slots):
        return [
            spread_piece(ref.at[pl.ds(piece * span, span), :], all_ref, size, some, piece, slots)
            for piece in range(PIECES)
        ]

    by_device, crossing = Slots(True), Slots(False)
    tokens_sent = spread_all(tokens_ref, tokens_all, token_sems, by_device)
    swaps[0].wait()
    line.launch(0)
    for kind, source in enumerate((near, far, cross)):
        block = pack_all.at[here, source]
        remote(
            block, block, swap_send.at[kind], swap_recv.at[kind], on_head(source)
        ).wait_recv()
        line.launch(kind + 1)
    cotangent_sent = spread_all(cotangent_ref, cotangent_all, cotangent_sems, crossing)
    for t in range(1, line.half):
        line.step(t)
    finish_tokens = hand_on(tokens_all, size, token_sems, tokens_sent, by_device)
    finish_cotangent = hand_on(cotangent_all, size, cotangent_sems, cotangent_sent, crossing)
    for swap in swaps[1:]:
        swap.wait_send()
    line.finish()
    finish_tokens()
    finish_cotangent()


def gather_first(pack, tokens, cotangent, number):
    groups, share, columns = pack.shape
    peers = lax.axis_size("blk")
    rows, width = tokens.shape
    whole = jax.ShapeDtypeStruct((groups * rows, width), bf16)
    vmem, anywhere = pl.BlockSpec(memory_space=pltpu.VMEM), pl.BlockSpec(memory_space=pl.ANY)
    all_pack, all_tokens, all_cotangent = pl.pallas_call(
        gather_first_kernel,
        in_specs=[vmem] * 3,
        out_specs=[anywhere] * 3,
        out_shape=[jax.ShapeDtypeStruct((peers, groups, share, columns), bf16), whole, whole],
        scratch_shapes=[
            pltpu.SemaphoreType.DMA((3,)),
            pltpu.SemaphoreType.DMA((3,)),
            pltpu.SemaphoreType.DMA,
        ]
        + [pltpu.SemaphoreType.DMA((4, peers // 2)) for _ in range(6)]
        + gather_sems()
        + gather_sems(),
        compiler_params=pltpu.CompilerParams(collective_id=number, has_side_effects=True),
        cost_estimate=pl.CostEstimate(
            flops=70_000_000_000, transcendentals=0, bytes_accessed=30_000_000
        ),
        name="gather_first",
    )(pack, tokens, cotangent)
    return all_pack.reshape(peers * groups * share, columns), all_tokens, all_cotangent


class Sum:
    def __init__(self, part_ref, buffers, sems, size, by_device):
        self.part_ref, self.size, self.span = part_ref, size, size // PIECES
        self.slots = Slots(by_device)
        self.near_buf, self.turn_buf, self.far_buf = buffers
        self.near_send, self.near_recv, self.far_send, self.far_recv = sems
        self.near_copies, self.far_copies = [], []

    def piece(self, n):
        return slice(n * self.span, (n + 1) * self.span)

    def start(self):
        me, near, far, cross = partners()
        for which, shard in ((0, self.slots.cross), (1, self.slots.near)):
            for n in range(PIECES):
                copy = remote(
                    piece_at(self.part_ref, shard, n, self.size),
                    self.near_buf.at[which, pl.ds(n * self.span, self.span), :],
                    self.near_send.at[which, n],
                    self.near_recv.at[which, n],
                    on_head(near),
                )
                copy.start()
                self.near_copies.append(copy)

    def turn(self):
        me, near, far, cross = partners()
        for n in range(PIECES):
            here = self.piece(n)
            self.near_copies[n].wait_recv()
            self.turn_buf[here, :] = (
                piece_at(self.part_ref, self.slots.far, n, self.size)[...].astype(f32)
                + self.near_buf[0, here, :].astype(f32)
            ).astype(bf16)
            copy = remote(
                self.turn_buf.at[pl.ds(n * self.span, self.span), :],
                self.far_buf.at[pl.ds(n * self.span, self.span), :],
                self.far_send.at[n],
                self.far_recv.at[n],
                on_head(far),
            )
            copy.start()
            self.far_copies.append(copy)

    def total(self, n):
        self.near_copies[PIECES + n].wait_recv()
        self.far_copies[n].wait_recv()
        here = self.piece(n)
        return (
            piece_at(self.part_ref, self.slots.own, n, self.size)[...].astype(f32)
            + self.near_buf[1, here, :].astype(f32)
            + self.far_buf[here, :].astype(f32)
        )

    def finish(self):
        for copy in self.near_copies + self.far_copies:
            copy.wait_send()


def sum_buffers(size, width):
    return [
        pltpu.VMEM((2, size, width), bf16),
        pltpu.VMEM((size, width), bf16),
        pltpu.VMEM((size, width), bf16),
    ]


def sum_sems():
    return [
        pltpu.SemaphoreType.DMA((2, PIECES)),
        pltpu.SemaphoreType.DMA((2, PIECES)),
        pltpu.SemaphoreType.DMA((PIECES,)),
        pltpu.SemaphoreType.DMA((PIECES,)),
    ]


def exchange_kernel(local, extras, summed, *refs):
    part_ref, extra_refs = refs[0], refs[1 : 1 + extras]
    out_ref, all_ref, payload = refs[1 + extras : 4 + extras]
    sems = refs[4 + extras :]
    size = out_ref.shape[0]
    span = size // PIECES
    _, near, far, _ = partners()
    greet([on_head(near), on_head(far)])
    slots = Slots(summed)
    if not summed:
        shares = Sum(part_ref, sems[7:10], sems[10:], size, True)
        shares.start()
        shares.turn()
    sent = []
    for piece in range(PIECES):
        here = slice(piece * span, (piece + 1) * span)
        total = part_ref[here, :] if summed else shares.total(piece)
        result, share = local(total, here, *extra_refs)
        out_ref[here, :] = result.astype(out_ref.dtype)
        payload[here, :] = share.astype(bf16)
        source = payload.at[pl.ds(piece * span, span), :]
        sent.append(spread_piece(source, all_ref, size, sems[:7], piece, slots))
    hand_on(all_ref, size, sems[:7], sent, slots)()
    if not summed:
        shares.finish()


def exchange(local, part, extras, summed, number, name):
    rows, width = part.shape
    size = rows if summed else rows // 4
    vmem = pl.BlockSpec(memory_space=pltpu.VMEM)
    return pl.pallas_call(
        functools.partial(exchange_kernel, local, len(extras), summed),
        in_specs=[vmem] * (1 + len(extras)),
        out_specs=[vmem, pl.BlockSpec(memory_space=pl.ANY)],
        out_shape=[
            jax.ShapeDtypeStruct((size, width), f32),
            jax.ShapeDtypeStruct((4 * size, width), bf16),
        ],
        scratch_shapes=[pltpu.VMEM((size, width), bf16)]
        + gather_sems()
        + ([] if summed else sum_buffers(size, width) + sum_sems()),
        compiler_params=pltpu.CompilerParams(collective_id=number, has_side_effects=True),
        cost_estimate=pl.CostEstimate(
            flops=40_000_000_000 if summed else 70_000_000_000,
            transcendentals=0,
            bytes_accessed=16_000_000,
        ),
        name=name,
    )(part, *extras)


def finish_last_kernel(grad_ref, output_grad_ref, first_ref, down_ref, grad_middle_ref, tokens_ref,
                       gain_ref, middle_ref, weights_ref, output_ref, tokens_grad_ref, result_ref,
                       *refs):
    buffers, (near1, turn1, far1, near2, turn2, far2) = refs[:8], refs[8:14]
    sems = refs[14:]
    me, near, far, cross = partners()
    here, partner, after = blk_peers()
    steps = len(after)
    greet(
        [on_head(near), on_head(far), on_head(cross), on_blk(partner)]
        + [on_blk(peer) for peer in after[1:]]
    )
    size = result_ref.shape[0]
    first = Sum(first_ref, (near1, turn1, far1), sems[12:16], size, True)
    down = Sum(down_ref, (near2, turn2, far2), sems[16:20], size, False)
    sums = (
        (grad_ref, weights_ref, buffers[:4], sems[:6]),
        (output_grad_ref, output_ref, buffers[4:], sems[6:12]),
    )
    first.start()
    sent = []
    for t in list(range(1, steps)) + [0]:
        for ref, _, (pair_buf, _, _, _), (pair_send, pair_recv, *_) in sums:
            copy = remote(
                ref.at[after[t] + partner - here],
                pair_buf.at[t],
                pair_send.at[t],
                pair_recv.at[t],
                on_blk(partner),
            )
            copy.start()
            sent.append(copy)
    first.turn()
    down.start()
    down.turn()
    lines = []
    for t in range(1, steps):
        for ref, _, (pair_buf, turn_buf, line_buf, _), some in sums:
            pair_send, pair_recv, line_send, line_recv = some[:4]
            remote(
                pair_buf.at[t], pair_buf.at[t], pair_send.at[t], pair_recv.at[t], on_blk(partner)
            ).wait_recv()

            def add(group, carry):
                turn_buf[t, group] = (
                    ref[after[t], group].astype(f32) + pair_buf[t, group].astype(f32)
                ).astype(bf16)
                return carry

            lax.fori_loop(0, ref.shape[1], add, 0)
            copy = remote(
                turn_buf.at[t], line_buf.at[t], line_send.at[t], line_recv.at[t], on_blk(after[t])
            )
            copy.start()
            lines.append(copy)

    def put(shares, local, out_ref, extra_refs):
        for piece in range(PIECES):
            rows = shares.piece(piece)
            value, _ = local(shares.total(piece), rows, *extra_refs)
            out_ref[rows, :] = value.astype(out_ref.dtype)

    put(first, after_first, tokens_grad_ref, (grad_middle_ref, tokens_ref, gain_ref))
    swaps = []
    for ref, out_ref, (pair_buf, _, line_buf, row_buf), some in sums:
        pair_send, pair_recv, line_send, line_recv, swap_send, swap_recv = some
        remote(
            pair_buf.at[0], pair_buf.at[0], pair_send.at[0], pair_recv.at[0], on_blk(partner)
        ).wait_recv()
        for t in range(1, steps):
            remote(
                line_buf.at[t], line_buf.at[t], line_send.at[t], line_recv.at[t], on_blk(after[t])
            ).wait_recv()

        def add_all(group, carry):
            total = ref[here, group].astype(f32) + pair_buf[0, group].astype(f32)
            for t in range(1, steps):
                total = total + line_buf[t, group].astype(f32)
            row_buf[group] = total.astype(bf16)
            return carry

        lax.fori_loop(0, ref.shape[1], add_all, 0)
        for kind, other in enumerate((near, far, cross)):
            copy = remote(
                row_buf.at[other],
                out_ref.at[me],
                swap_send.at[kind],
                swap_recv.at[kind],
                on_head(other),
            )
            copy.start()
            swaps.append(copy)
        out_ref[me] = row_buf[me]
    put(down, after_down, result_ref, (middle_ref,))
    for _, out_ref, _, some in sums:
        for kind, other in enumerate((near, far, cross)):
            block = out_ref.at[other]
            remote(
                block, block, some[4].at[kind], some[5].at[kind], on_head(other)
            ).wait_recv()
    for copy in sent + lines + swaps:
        copy.wait_send()
    first.finish()
    down.finish()


def finish_last(grad, output_grad, groups, part_first, part_down, grad_middle, tokens, gain, middle,
                number):
    peers = lax.axis_size("blk")
    share = grad.shape[0] // (peers * groups)
    rows, width = tokens.shape
    vmem = pl.BlockSpec(memory_space=pltpu.VMEM)
    half = peers // 2
    widths = (grad.shape[1], output_grad.shape[1])

    def blocks(columns):
        return [pltpu.VMEM((half, groups, share, columns), bf16) for _ in range(3)] + [
            pltpu.VMEM((groups, share, columns), bf16)
        ]

    swap_sems = [pltpu.SemaphoreType.DMA((half,)) for _ in range(4)] + [
        pltpu.SemaphoreType.DMA((3,)) for _ in range(2)
    ]
    return pl.pallas_call(
        finish_last_kernel,
        in_specs=[vmem] * 8,
        out_specs=[vmem] * 4,
        out_shape=[
            jax.ShapeDtypeStruct((groups, share, columns), bf16) for columns in widths
        ]
        + [
            jax.ShapeDtypeStruct((rows, width), f32),
            jax.ShapeDtypeStruct((rows, width), bf16),
        ],
        scratch_shapes=blocks(widths[0])
        + blocks(widths[1])
        + sum_buffers(rows, width)
        + sum_buffers(rows, width)
        + swap_sems
        + swap_sems
        + sum_sems()
        + sum_sems(),
        compiler_params=pltpu.CompilerParams(
            collective_id=number, has_side_effects=True, vmem_limit_bytes=60 << 20
        ),
        cost_estimate=pl.CostEstimate(
            flops=80_000_000_000, transcendentals=0, bytes_accessed=40_000_000
        ),
        name="finish_last",
    )(
        grad.reshape(peers, groups, share, widths[0]),
        output_grad.reshape(peers, groups, share, widths[1]),
        part_first, part_down, grad_middle, tokens, gain, middle,
    )


def inverse_rms(value):
    return lax.rsqrt(jnp.mean(value * value, axis=1, keepdims=True) + epsilon)


def through_norm(grad, value):
    factor = inverse_rms(value)
    normed = value * factor
    return factor * (grad - normed * jnp.mean(grad * normed, axis=1, keepdims=True))


def after_attention(total, here, tokens_ref, gain_ref):
    middle = tokens_ref[here, :].astype(f32) + total
    return middle, middle * inverse_rms(middle) * gain_ref[0:1, :]


def after_hidden(total, here, cotangent_ref, middle_ref, gain_ref):
    grad = cotangent_ref[here, :].astype(f32) + through_norm(
        total * gain_ref[0:1, :], middle_ref[here, :]
    )
    return grad, grad


def after_first(total, here, grad_ref, tokens_ref, gain_ref):
    grad = grad_ref[here, :] + through_norm(
        total * gain_ref[0:1, :], tokens_ref[here, :].astype(f32)
    )
    return grad, None


def after_down(total, here, middle_ref):
    return middle_ref[here, :] + total, None


FEED_TILE = 256
FEED_COLUMNS = 512


def feed_kernel(input_ref, cotangent_ref, weight_ref, down_ref, grad_ref, total_ref, acts, turned0,
                turned1, stage, near_buf, far_buf, near_send, near_recv, far_send, far_recv):
    step = pl.program_id(0)
    hidden_width = weight_ref.shape[1] // 3
    size = total_ref.shape[0]
    per = size // FEED_TILE
    tiles = 4 * per
    _, near, far, _ = partners()

    @pl.when(step == 0)
    def _():
        greet([on_head(near), on_head(far)])

    def to_near(which, piece):
        return remote(
            stage.at[which * per + piece],
            near_buf.at[which, piece],
            near_send.at[which, piece],
            near_recv.at[which, piece],
            on_head(near),
        )

    def to_far(piece):
        return remote(
            near_buf.at[0, piece], far_buf.at[piece], far_send.at[piece], far_recv.at[piece],
            on_head(far),
        )

    @pl.when(step < tiles)
    def _():
        here = tile_of(step, FEED_TILE)
        inputs, cotangent = input_ref[...], cotangent_ref[...]
        turned0[:, here] = inputs.T
        turned1[:, here] = cotangent.T
        gate_at, up_at, down_at = (
            slice(n * hidden_width, (n + 1) * hidden_width) for n in range(3)
        )
        gate = dot(inputs, weight_ref[:, gate_at])
        up = dot(inputs, weight_ref[:, up_at])
        grad_hidden = dot(cotangent, weight_ref[:, down_at])
        opening = jax.nn.sigmoid(gate)
        active = gate * opening
        hidden = (active * up).astype(bf16)
        grad_gate = (grad_hidden * up * opening * (1.0 + gate * (1.0 - opening))).astype(bf16)
        grad_up = (grad_hidden * active).astype(bf16)
        acts[here, gate_at] = grad_gate
        acts[here, up_at] = grad_up
        acts[here, down_at] = hidden
        down_ref[...] = dot(hidden, weight_ref[:, down_at], NT).astype(bf16)
        back = dot(grad_gate, weight_ref[:, gate_at], NT) + dot(
            grad_up, weight_ref[:, up_at], NT
        )
        for piece in range(per):
            for which, first in ((0, 0), (1, 2 * per)):

                @pl.when(step == first + piece)
                def _():
                    stage[which * per + piece] = back.astype(bf16)
                    to_near(which, piece).start()

            @pl.when(step == per + piece)
            def _():
                to_near(0, piece).wait_recv()
                near_buf[0, piece] = (back + near_buf[0, piece].astype(f32)).astype(bf16)
                to_far(piece).start()

            @pl.when(step == 3 * per + piece)
            def _():
                total_ref[piece * FEED_TILE : (piece + 1) * FEED_TILE, :] = back

    @pl.when(step >= tiles)
    def _():
        at = tile_of(step - tiles, FEED_COLUMNS)
        from_input = (step - tiles) * FEED_COLUMNS < 2 * hidden_width

        @pl.when(from_input)
        def _():
            grad_ref[...] = dot(turned0[...], acts[:, at]).astype(bf16)

        @pl.when(jnp.logical_not(from_input))
        def _():
            grad_ref[...] = dot(turned1[...], acts[:, at]).astype(bf16)

    @pl.when(step == pl.num_programs(0) - 1)
    def _():
        for piece in range(per):
            here = slice(piece * FEED_TILE, (piece + 1) * FEED_TILE)
            to_near(1, piece).wait_recv()
            to_far(piece).wait_recv()
            total_ref[here, :] += near_buf[1, piece].astype(f32) + far_buf[piece].astype(f32)
            to_near(0, piece).wait_send()
            to_near(1, piece).wait_send()
            to_far(piece).wait_send()


def feed(inputs, cotangent, weight, number):
    rows, width = inputs.shape
    columns = weight.shape[1]
    size = rows // 4
    tiles, per = rows // FEED_TILE, size // FEED_TILE
    tile = pl.BlockSpec((FEED_TILE, width), lambda n: (jnp.minimum(n, tiles - 1), 0))

    def whole(shape):
        return pl.BlockSpec(shape, lambda n: (0, 0), pipeline_mode=pl.Buffered(1))

    return pl.pallas_call(
        feed_kernel,
        grid=(tiles + columns // FEED_COLUMNS,),
        in_specs=[tile, tile, whole((width, columns))],
        out_specs=[
            tile,
            pl.BlockSpec((width, FEED_COLUMNS), lambda n: (0, jnp.maximum(n - tiles, 0))),
            whole((size, width)),
        ],
        out_shape=[
            jax.ShapeDtypeStruct((rows, width), bf16),
            jax.ShapeDtypeStruct((width, columns), bf16),
            jax.ShapeDtypeStruct((size, width), f32),
        ],
        scratch_shapes=[
            pltpu.VMEM((rows, columns), bf16),
            pltpu.VMEM((width, rows), bf16),
            pltpu.VMEM((width, rows), bf16),
            pltpu.VMEM((2 * per, FEED_TILE, width), bf16),
            pltpu.VMEM((2, per, FEED_TILE, width), bf16),
            pltpu.VMEM((per, FEED_TILE, width), bf16),
            pltpu.SemaphoreType.DMA((2, per)),
            pltpu.SemaphoreType.DMA((2, per)),
            pltpu.SemaphoreType.DMA((per,)),
            pltpu.SemaphoreType.DMA((per,)),
        ],
        compiler_params=pltpu.CompilerParams(
            collective_id=number, has_side_effects=True, vmem_limit_bytes=63 << 20
        ),
        cost_estimate=pl.CostEstimate(
            flops=6 * rows * width * columns, transcendentals=rows * columns // 3,
            bytes_accessed=45_000_000,
        ),
        name="feed",
    )(inputs, cotangent, weight)


def over_tokens(operand, other_side):
    return lax.dot_general(
        operand, other_side, (((0,), (0,)), ((), ())), preferred_element_type=f32
    )


def sent_columns(pieces, groups):
    packed = jnp.concatenate(
        [piece.reshape(piece.shape[0], groups, -1) for piece in pieces], axis=2
    )
    mine = lax.all_to_all(packed, "head", split_axis=1, concat_axis=0, tiled=True)
    return mine.reshape(mine.shape[0], mine.shape[2])


def all_rows(mine):
    return lax.all_gather(mine, "blk", axis=0, tiled=True)


def row_sums(grad):
    return lax.psum_scatter(grad, "blk", scatter_dimension=0, tiled=True)


def own_rows(summed, groups):
    rows, columns = summed.shape
    parts = lax.all_to_all(
        summed.reshape(groups, rows // groups, columns), "head", split_axis=0, concat_axis=0
    )
    return jnp.swapaxes(parts, 0, 1).astype(f32)


def body(
    tokens,
    segment,
    norm1_gain,
    w_query,
    w_key,
    w_value,
    w_gate_out,
    w_forget,
    forget_bias,
    w_output,
    norm2_gain,
    w_gate,
    w_up,
    w_down,
    cotangent,
):
    token_rows, model_width = tokens.shape
    groups = lax.axis_size("head")
    head_count = forget_bias.shape[0]
    local_heads = head_count // groups
    local_width = model_width // groups
    hidden_width = w_gate.shape[1] // groups
    rows = token_rows * groups
    share = w_query.shape[0]
    group = lax.axis_index("head")

    low = lambda array: array.astype(bf16)
    spread = lambda gain: jnp.broadcast_to(low(gain)[:, None, None], (share, groups, 1))
    forget_low = low(w_forget).reshape(share, groups, local_heads)
    rest = LANES - local_heads - 2
    small = jnp.concatenate(
        [forget_low, spread(norm1_gain), spread(norm2_gain), jnp.zeros((share, groups, rest), bf16)],
        axis=2,
    )
    pack = jnp.concatenate(
        [
            low(piece).reshape(share, groups, -1)
            for piece in (w_key, w_value, small, w_query, w_gate_out, w_output)
        ],
        axis=2,
    )
    first, tokens_all, cotangent_all = gather_first(
        jnp.swapaxes(pack, 0, 1), tokens, cotangent, 0
    )
    kv_width = 2 * local_width + LANES
    output_weight = first[:, kv_width + 2 * local_width :]

    segment_plus = segment + 1
    earlier_segment = passed_along(segment_plus, "blk", 1)
    window = jnp.concatenate([earlier_segment, segment_plus])
    begins = jnp.sum(
        (window[:, None] < segment_plus[None, :]).astype(jnp.int32), axis=0
    )
    tiles = begins.reshape(rows // Q_TILE, Q_TILE)
    ranges = jnp.stack([tiles[:, 0] // K_TILE, (tiles[:, -1] + K_TILE - 1) // K_TILE])
    begins = jnp.broadcast_to(begins[None, :], (8, rows))

    def gain_rows(column):
        gain = first[:, 2 * local_width + local_heads + column].astype(f32)
        return jnp.broadcast_to(gain[None, :], (8, model_width))

    gain1, gain2 = gain_rows(0), gain_rows(1)
    bias = lax.dynamic_slice_in_dim(forget_bias, group * local_heads, local_heads, 0)
    bias = jnp.broadcast_to(jnp.pad(bias, (0, LANES - local_heads))[None, :], (8, LANES))
    input1, key_value, forget = project(
        tokens_all, gain1, first, bias, 2 * local_width, local_heads
    )
    earlier_kv = passed_along(key_value, "blk", 1)
    query = dot(input1, first[:, kv_width : kv_width + local_width]).astype(bf16)
    gate_raw = dot(
        input1, first[:, kv_width + local_width : kv_width + 2 * local_width]
    )

    so_far = attend(True, ranges, query, key_value, key_value, begins, local_heads)
    mine = sent_columns([low(w_gate), low(w_up), low(w_down)], groups)
    mine, earlier_kv, so_far = lax.optimization_barrier((mine, earlier_kv, so_far))
    second = all_rows(mine)
    attended, lse = attend(
        False, ranges, query, earlier_kv, key_value, begins, local_heads, so_far
    )
    opened = jax.nn.sigmoid(gate_raw)
    attended_wide = attended.astype(f32)
    gated = (opened * attended_wide).astype(bf16)
    branch = dot(gated, output_weight, NT).astype(bf16)
    middle, input2 = exchange(
        after_attention, branch, [tokens, gain2], False, 1, "exchange_middle"
    )
    down, second_grad, grad_input2 = feed(input2, cotangent_all, second, 4)
    second_part = row_sums(second_grad)
    grad_middle, grad_branch = exchange(
        after_hidden, grad_input2, [cotangent, middle, gain2], True, 2, "exchange_hidden"
    )

    grad_gated = dot(grad_branch, output_weight)
    grad_attended = (grad_gated * opened).astype(bf16)
    grad_gate_pre = (grad_gated * attended_wide * opened * (1.0 - opened)).astype(bf16)
    dq_prev, rows_prev, dkv_prev, decay_prev = attend_back(
        False, ranges, query, earlier_kv, key_value, begins, grad_attended, attended,
        lse, local_heads,
    )
    dkv_later = passed_along(dkv_prev, "blk", -1)
    decay_later = passed_along(decay_prev[:, :8], "blk", -1)
    decay_later = jnp.pad(decay_later, ((0, 0), (0, LANES - 8)))
    dq, dk_own, dv_own, decay_own = attend_back(
        True, ranges, query, key_value, key_value, begins, grad_attended, attended,
        lse, local_heads, (dq_prev, rows_prev),
    )
    dk = (dk_own + dkv_later[0].astype(f32)).astype(bf16)
    dv = (dv_own + dkv_later[1].astype(f32)).astype(bf16)
    logf_grad = decay_back(decay_own, decay_later)
    forget_grad = jnp.where(
        jnp.arange(LANES)[None, :] < local_heads, logf_grad * jax.nn.sigmoid(-forget), 0.0
    ).astype(bf16)
    grads = jnp.concatenate([dk, dv, forget_grad, dq, grad_gate_pre], axis=1)
    first_grad = over_tokens(input1, grads)
    bias_part = jnp.sum(forget_grad.astype(f32), axis=0)
    row = jnp.arange(model_width)[:, None] % share
    column = jnp.arange(kv_width + 2 * local_width)[None, :]
    spread_bias = jnp.sum(
        jnp.where(row == jnp.arange(LANES)[None, :], bias_part[None, :], 0.0), axis=1, keepdims=True
    )
    first_grad = jnp.where(
        column == 2 * local_width + local_heads, spread_bias, first_grad
    ).astype(bf16)
    output_grad = over_tokens(grad_branch, gated).astype(bf16)
    grad_input1 = dot(grads, first[:, : kv_width + 2 * local_width], NT).astype(bf16)
    second_sum = own_rows(second_part, groups)
    grad_input1, second_sum = lax.optimization_barrier((grad_input1, second_sum))
    first_sum, output_sum, tokens_grad, result = finish_last(
        first_grad, output_grad, groups, grad_input1, down, grad_middle, tokens, gain1, middle, 3
    )
    first_sum = jnp.swapaxes(first_sum, 0, 1).astype(f32)
    output_sum = jnp.swapaxes(output_sum, 0, 1).astype(f32)

    def columns(array, start, width):
        return array[:, :, start : start + width].reshape(share, groups * width)

    key_sum, value_sum = (columns(first_sum, n * local_width, local_width) for n in range(2))
    forget_sum = columns(first_sum, 2 * local_width, local_heads)
    bias_total = first_sum[:local_heads, :, 2 * local_width + local_heads].T.reshape(head_count)
    query_sum, gate_out_sum = (
        columns(first_sum, kv_width + n * local_width, local_width) for n in range(2)
    )
    output_total = columns(output_sum, 0, local_width)
    gate_sum, up_sum, down_sum = (
        columns(second_sum, n * hidden_width, hidden_width) for n in range(3)
    )

    def along(weight, grad):
        return jnp.sum(low(weight).astype(f32) * grad, axis=1)

    gain1_total = (
        along(w_query, query_sum)
        + along(w_key, key_sum)
        + along(w_value, value_sum)
        + along(w_gate_out, gate_out_sum)
        + along(w_forget, forget_sum)
    ) / low(norm1_gain).astype(f32)
    gain2_total = (along(w_gate, gate_sum) + along(w_up, up_sum)) / low(norm2_gain).astype(f32)
    return (
        result,
        tokens_grad,
        gain1_total,
        query_sum,
        key_sum,
        value_sum,
        gate_out_sum,
        forget_sum,
        bias_total,
        output_total,
        gain2_total,
        gate_sum,
        up_sum,
        down_sum,
    )


def solution(mesh):
    both = ("blk", "head")
    matrix, vector = P(both, None), P(both)
    return jax.shard_map(
        body,
        mesh=mesh,
        in_specs=(
            matrix, P("blk"), vector, matrix, matrix, matrix, matrix, matrix, P(), matrix, vector,
            matrix, matrix, matrix, matrix,
        ),
        out_specs=(
            matrix, matrix, vector, matrix, matrix, matrix, matrix, matrix, P(), matrix, vector,
            matrix, matrix, matrix,
        ),
        check_vma=False,
    )
```

```python
import functools

import jax
import jax.numpy as jnp
from jax import lax
from jax.experimental import pallas as pl
from jax.experimental.pallas import tpu as pltpu
from jax.sharding import PartitionSpec as P

epsilon = 1e-06
LANES = 128
Q_TILE = 512
K_TILE = 512
FAR = -1e30
NT = (((1,), (1,)), ((), ()))
NN = (((1,), (0,)), ((), ()))
bf16 = jnp.bfloat16
f32 = jnp.float32


def dot(a, b, dims=NN, **kw):
    return lax.dot_general(a, b, dims, preferred_element_type=f32, **kw)


def passed_along(array, axis, by):
    peers = lax.axis_size(axis)
    pairs = [(i, i + by) for i in range(peers) if 0 <= i + by < peers]
    return lax.ppermute(array, axis, pairs)


def split3(value):
    high = value.astype(bf16)
    rest = value - high.astype(f32)
    mid = rest.astype(bf16)
    low = (rest - mid.astype(f32)).astype(bf16)
    return high, mid, low


def running(value_of, steps, rows, upper):
    place = lax.broadcasted_iota(jnp.int32, (rows, rows), 0)
    other = lax.broadcasted_iota(jnp.int32, (rows, rows), 1)
    tri = jnp.where((other >= place) if upper else (other <= place), 1.0, 0.0).astype(bf16)
    outs = [None] * steps
    carry = jnp.zeros((1, LANES), f32)
    order = range(steps - 1, -1, -1) if upper else range(steps)
    for n in order:
        block = value_of(n)
        total = sum(dot(tri, part) for part in split3(block)) + carry
        outs[n] = total
        carry = total[0:1] if upper else total[rows - 1 : rows]
    return outs, carry


PROJECT_TILE = 256
TERM_ROWS = 32


def project_kernel(local_heads, tokens_ref, gain_ref, weight_ref, bias_ref, input_ref, out_ref,
                   terms_ref, turned_ref, forget_ref, carry_ref):
    rows = tokens_ref.shape[0]
    wide = weight_ref.shape[1] - LANES

    @pl.when(pl.program_id(0) == 0)
    def _():
        carry_ref[...] = jnp.zeros_like(carry_ref)

    tokens = tokens_ref[...].astype(f32)
    input1 = (tokens * inverse_rms(tokens) * gain_ref[0:1, :]).astype(bf16)
    input_ref[...] = input1
    raw = dot(input1, weight_ref[...])
    out_ref[...] = raw[:, :wide].astype(bf16)
    forget = (raw[:, wide:] + bias_ref[0:1, :]).astype(bf16).astype(f32)
    forget_ref[...] = forget
    lane = lax.broadcasted_iota(jnp.int32, (rows, LANES), 1)
    logf = jnp.minimum(forget, 0.0) - jnp.log1p(jnp.exp(-jnp.abs(forget)))
    logf = jnp.where(lane < local_heads, logf, 0.0)
    place = lax.broadcasted_iota(jnp.int32, (rows, rows), 0)
    other = lax.broadcasted_iota(jnp.int32, (rows, rows), 1)
    tri = jnp.where(other <= place, 1.0, 0.0).astype(bf16)
    sums = sum(dot(tri, part) for part in split3(logf)) + carry_ref[0:1, :]
    carry_ref[0:1, :] = sums[rows - 1 : rows, :]
    high, mid, low = split3(sums)
    terms = (
        high.astype(f32)
        + pltpu.roll(mid.astype(f32), local_heads, 1)
        + pltpu.roll(low.astype(f32), 2 * local_heads, 1)
        + jnp.where(lane == 3 * local_heads, 1.0, 0.0)
    ).astype(bf16)
    terms_ref[...] = terms
    turned_ref[...] = terms.T[0:TERM_ROWS, :]


def project(tokens, gain, weight, bias, wide, local_heads):
    rows, width = tokens.shape

    def tile(columns):
        return pl.BlockSpec((PROJECT_TILE, columns), lambda n: (n, 0))

    def whole(*shape):
        return pl.BlockSpec(shape, lambda n: (0, 0))

    return pl.pallas_call(
        functools.partial(project_kernel, local_heads),
        grid=(rows // PROJECT_TILE,),
        in_specs=[tile(width), whole(8, width), whole(width, wide + LANES), whole(8, LANES)],
        out_specs=[
            tile(width),
            tile(wide),
            tile(LANES),
            pl.BlockSpec((TERM_ROWS, PROJECT_TILE), lambda n: (0, n)),
            tile(LANES),
        ],
        out_shape=[
            jax.ShapeDtypeStruct((rows, width), bf16),
            jax.ShapeDtypeStruct((rows, wide), bf16),
            jax.ShapeDtypeStruct((rows, LANES), bf16),
            jax.ShapeDtypeStruct((TERM_ROWS, rows), bf16),
            jax.ShapeDtypeStruct((rows, LANES), f32),
        ],
        scratch_shapes=[pltpu.VMEM((8, LANES), f32)],
        cost_estimate=pl.CostEstimate(
            flops=2 * rows * width * (wide + LANES), transcendentals=rows * LANES,
            bytes_accessed=20_000_000,
        ),
        name="project",
    )(tokens, gain, weight, bias)


def decay_back_kernel(own_ref, halo_ref, out_ref):
    rows = 256
    steps = own_ref.shape[0] // rows
    own, _ = running(lambda n: own_ref[n * rows : (n + 1) * rows, :], steps, rows, True)
    halo, _ = running(lambda n: halo_ref[n * rows : (n + 1) * rows, :], steps, rows, False)
    for n in range(steps):
        part = slice(n * rows, (n + 1) * rows)
        out_ref[part, :] = own[n] + (halo[n] - halo_ref[part, :])


def decay_back(own, halo):
    return pl.pallas_call(
        decay_back_kernel,
        out_shape=jax.ShapeDtypeStruct(own.shape, f32),
        name="decay_back",
    )(own, halo)


QUERY, KEY, TOTAL = range(3)


def placing(pair, local_heads, role):
    row = lax.broadcasted_iota(jnp.int32, (LANES, LANES), 0)
    col = lax.broadcasted_iota(jnp.int32, (LANES, LANES), 1)
    head = jnp.where(col < 64, 2 * pair + 1, 2 * pair)
    spot = jnp.where(col < 64, col, col - 64)
    term = spot - 3 * role
    is_term = (term >= 0) & (term < 3) & (row == term * local_heads + head)
    if role == QUERY:
        ones = (spot >= 3) & (spot < 9)
    else:
        ones = (spot < 3) & (role == KEY)
    is_one = ones & (row == 3 * local_heads)
    sign = -1.0 if role == KEY else 1.0
    return (jnp.where(is_term, sign, 0.0) + jnp.where(is_one, 1.0, 0.0)).astype(bf16)


def allowed_pairs(first_key, query_tile, rows, begin_row):
    shape = (K_TILE, Q_TILE)
    key_place = first_key + lax.broadcasted_iota(jnp.int32, shape, 0)
    query_place = rows + query_tile * Q_TILE + lax.broadcasted_iota(jnp.int32, shape, 1)
    return (key_place >= begin_row) & (key_place <= query_place)


def key_range(ranges_ref, query_tile, rows, own):
    count = rows // K_TILE
    base = count if own else 0
    first = jnp.clip(ranges_ref[0, query_tile] - base, 0, count)
    full = jnp.clip(ranges_ref[1, query_tile] - base, first, count)
    return first, full


def key_loops(ranges_ref, query_tile, rows, own, step, carry):
    first, full = key_range(ranges_ref, query_tile, rows, own)
    inside = query_tile * (Q_TILE // K_TILE) if own else rows // K_TILE
    full = jnp.minimum(full, inside)
    carry = lax.fori_loop(first, full, functools.partial(step, True), carry)
    carry = lax.fori_loop(full, inside, functools.partial(step, False), carry)
    if own:
        carry = lax.fori_loop(
            inside, inside + Q_TILE // K_TILE, functools.partial(step, True), carry
        )
    return carry


def tile_of(number, size):
    return pl.ds(pl.multiple_of(number * size, size), size)


def fill_keys(pair, local_heads, own, first, key_ref, terms_ref, keys):
    place = placing(pair, local_heads, KEY)
    lane = lax.broadcasted_iota(jnp.int32, (K_TILE, LANES), 1)
    rows = key_ref.shape[0]
    if not own:
        last = terms_ref[:, rows - LANES : rows].T
        total = dot(last, placing(pair, local_heads, TOTAL)[0:TERM_ROWS, :])[LANES - 1 : LANES, :]

    def fill(n, carry):
        here = tile_of(n, K_TILE)
        if own:
            extra = dot(terms_ref[here, :], place).astype(bf16)
        else:
            extra = dot(terms_ref[:, here].T, place[0:TERM_ROWS, :])
            extra = (extra + total).astype(bf16)
        key = key_ref[here, :]
        keys[0][here, :] = jnp.where(lane < 64, key, extra)
        keys[1][here, :] = jnp.where(lane < 64, extra, key)
        return carry

    lax.fori_loop(first, rows // K_TILE, fill, 0)


def query_tiles(q_ref, terms_ref, place, here, scaling):
    lane = lax.broadcasted_iota(jnp.int32, (Q_TILE, LANES), 1)
    extra = dot(terms_ref[here, :], place).astype(bf16)
    query = (q_ref[here, :].astype(f32) * scaling).astype(bf16)
    return jnp.where(lane < 64, query, extra), jnp.where(lane < 64, extra, query)


def attend_kernel(local_heads, own, ranges_ref, q_ref, k_ref, v_ref, t_query_ref, t_key_ref,
                  begin_ref, *refs):
    if own:
        acc_out_ref, state_out_ref, key0, key1, values, acc0, acc1 = refs
    else:
        acc_in_ref, state_in_ref, o_ref, lse_ref, key0, key1, values, acc0, acc1 = refs
    pair = pl.program_id(0)
    rows = q_ref.shape[0]
    base = rows if own else 0
    keys, accs = (key0, key1), (acc0, acc1)
    first, _ = key_range(ranges_ref, 0, rows, own)
    fill_keys(pair, local_heads, own, first, k_ref, t_key_ref, keys)

    def turn(n, carry):
        values[:, tile_of(n, K_TILE)] = v_ref[tile_of(n, K_TILE), :].T
        return carry

    lax.fori_loop(first, rows // K_TILE, turn, 0)
    place = placing(pair, local_heads, QUERY)

    def query_loop(tile, carry):
        here = tile_of(tile, Q_TILE)
        queries = query_tiles(q_ref, t_query_ref, place, here, 64**-0.5)
        begin_row = begin_ref[0:1, here]
        if own:
            low = jnp.full((1, Q_TILE), FAR, f32)
            zero = jnp.zeros((1, Q_TILE), f32)
            state = (low, zero, low, zero)
            for acc in accs:
                acc[...] = jnp.zeros_like(acc)
        else:
            state = tuple(state_in_ref[n : n + 1, here] for n in range(4))
            for h in range(2):
                accs[h][...] = acc_in_ref[64 * h : 64 * (h + 1), here]

        def step(masked, number, state):
            there = tile_of(number, K_TILE)
            fresh = []
            if masked:
                allowed = allowed_pairs(base + number * K_TILE, tile, rows, begin_row)
            for h in range(2):
                largest, total = state[2 * h], state[2 * h + 1]
                scores = dot(keys[h][there, :], queries[h], NT)
                if masked:
                    scores = jnp.where(allowed, scores, FAR)
                now = jnp.maximum(largest, jnp.max(scores, axis=0, keepdims=True))
                fade = jnp.exp(largest - now)
                weights = jnp.exp(scores - now)
                total = total * fade + jnp.sum(weights, axis=0, keepdims=True)
                accs[h][...] = accs[h][...] * fade + dot(
                    values[64 * h : 64 * (h + 1), there], weights.astype(bf16)
                )
                fresh += [now, total]
            return tuple(fresh)

        state = key_loops(ranges_ref, tile, rows, own, step, state)
        if own:
            for h in range(2):
                acc_out_ref[64 * h : 64 * (h + 1), here] = accs[h][...]
            for n in range(4):
                state_out_ref[n : n + 1, here] = state[n]
        else:
            mixed = jnp.concatenate(
                [accs[h][...] * (1.0 / state[2 * h + 1]) for h in range(2)], axis=0
            )
            o_ref[here, :] = mixed.T.astype(bf16)
            for h in range(2):
                lse_ref[h : h + 1, here] = state[2 * h] + jnp.log(state[2 * h + 1])
        return carry

    lax.fori_loop(0, rows // Q_TILE, query_loop, 0)


def lane_block(rows, offset):
    return pl.BlockSpec((rows, LANES), lambda p, *_: (0, offset + p))


def fixed(shape):
    return pl.BlockSpec(shape, lambda p, *_: (0, 0))


def pair_block(height, rows):
    return pl.BlockSpec((height, rows), lambda p, *_: (p, 0))


def attend(own, ranges, query, key_value, terms, key_terms, begins, local_heads, so_far=()):
    rows = query.shape[0]
    pairs = local_heads // 2
    running_specs = [pair_block(LANES, rows), pair_block(8, rows)]
    running_shape = (
        jax.ShapeDtypeStruct((LANES * pairs, rows), f32),
        jax.ShapeDtypeStruct((8 * pairs, rows), f32),
    )
    final_specs = [lane_block(rows, 0), pair_block(8, rows)]
    final_shape = (
        jax.ShapeDtypeStruct((rows, pairs * LANES), bf16),
        jax.ShapeDtypeStruct((8 * pairs, rows), f32),
    )
    return pl.pallas_call(
        functools.partial(attend_kernel, local_heads, own),
        grid_spec=pltpu.PrefetchScalarGridSpec(
            num_scalar_prefetch=1,
            grid=(pairs,),
            in_specs=[
                lane_block(rows, 0),
                lane_block(rows, 0),
                lane_block(rows, pairs),
                fixed((rows, LANES)),
                fixed((rows, LANES) if own else (TERM_ROWS, rows)),
                fixed((8, rows)),
            ]
            + ([] if own else running_specs),
            out_specs=running_specs if own else final_specs,
            scratch_shapes=[
                pltpu.VMEM((rows, LANES), bf16),
                pltpu.VMEM((rows, LANES), bf16),
                pltpu.VMEM((LANES, rows), bf16),
                pltpu.VMEM((64, Q_TILE), f32),
                pltpu.VMEM((64, Q_TILE), f32),
            ],
        ),
        out_shape=running_shape if own else final_shape,
        cost_estimate=pl.CostEstimate(
            flops=40_000_000_000 if own else 10_000_000_000,
            transcendentals=20_000_000,
            bytes_accessed=12_000_000,
        ),
        name="attend_own" if own else "attend_prev",
    )(ranges, query, key_value, key_value, terms, key_terms, begins, *so_far)


def attend_back_kernel(local_heads, own, ranges_ref, q_ref, k_ref, v_ref, t_query_ref, t_key_ref,
                       begin_ref, grad_ref, o_ref, lse_ref, *refs):
    if own:
        dq_in_ref, decay_in_ref, dq_ref, dk_ref, dv_ref, decay_ref = refs[:6]
    else:
        dq_ref, row_decay_ref, dkv_ref, decay_ref = refs[:4]
        dk_ref, dv_ref = dkv_ref.at[0], dkv_ref.at[1]
    key0, key1, key_t0, key_t1, dk0, dk1, dv, dq0, dq1 = refs[-9:]
    pair = pl.program_id(0)
    rows = q_ref.shape[0]
    base = rows if own else 0
    keys, keys_t, dks, dqs = (key0, key1), (key_t0, key_t1), (dk0, dk1), (dq0, dq1)
    first, _ = key_range(ranges_ref, 0, rows, own)
    fill_keys(pair, local_heads, own, first, k_ref, t_key_ref, keys)

    def turn(n, carry):
        here = tile_of(n, K_TILE)
        for h in range(2):
            keys_t[h][:, here] = keys[h][here, :].T
        return carry

    lax.fori_loop(first, rows // K_TILE, turn, 0)
    for ref in (dk0, dk1, dv):
        ref[...] = jnp.zeros_like(ref)
    place = placing(pair, local_heads, QUERY)
    lane = lax.broadcasted_iota(jnp.int32, (Q_TILE, LANES), 1)
    pick_row = lax.broadcasted_iota(jnp.int32, (8, LANES), 0)
    pick_lane = lax.broadcasted_iota(jnp.int32, (8, LANES), 1)
    pick = jnp.where((pick_lane // 64) == pick_row, 1.0, 0.0)
    sums_ref = decay_ref if own else row_decay_ref

    @pl.when(pair == 0)
    def _():
        if own:
            decay_ref[...] = decay_in_ref[...]
        else:
            decay_ref[...] = jnp.zeros_like(decay_ref)
            row_decay_ref[...] = jnp.zeros_like(row_decay_ref)

    def query_tile(tile):
        here = tile_of(tile, Q_TILE)
        queries = query_tiles(q_ref, t_query_ref, place, here, 64**-0.5)
        begin_row = begin_ref[0:1, here]
        grad = grad_ref[here, :]
        nothing = jnp.zeros_like(grad)
        grads = (jnp.where(lane < 64, grad, nothing), jnp.where(lane < 64, nothing, grad))
        product = grad.astype(f32) * o_ref[here, :].astype(f32)
        inner = dot(pick, product, NT, precision=lax.Precision.HIGHEST)
        for dq in dqs:
            dq[...] = jnp.zeros_like(dq)

        def step(masked, number, state):
            there = tile_of(number, K_TILE)
            if masked:
                allowed = allowed_pairs(base + number * K_TILE, tile, rows, begin_row)
            value = v_ref[there, :]
            value_part = 0.0
            for h in range(2):
                scores = dot(keys[h][there, :], queries[h], NT)
                prob = jnp.exp(scores - lse_ref[h : h + 1, here])
                if masked:
                    prob = jnp.where(allowed, prob, 0.0)
                grad_prob = dot(value, grads[h], NT)
                grad_score = (prob * (grad_prob - inner[h : h + 1, :])).astype(bf16)
                value_part = value_part + dot(prob.astype(bf16), grads[h])
                dks[h][there, :] += dot(grad_score, queries[h])
                dqs[h][...] += dot(keys_t[h][:, there], grad_score)
            dv[there, :] += value_part
            return state

        key_loops(ranges_ref, tile, rows, own, step, 0)
        turned = [dq[...].T for dq in dqs]
        dq_tile = jnp.where(lane < 64, turned[0], turned[1]) * 64**-0.5
        if own:
            dq_tile = dq_tile + dq_in_ref[here, :]
        dq_ref[here, :] = dq_tile.astype(dq_ref.dtype)
        sums = sums_ref[here, :]
        sums = sums + jnp.where(lane == 2 * pair, turned[0][:, 64:65], 0.0)
        sums = sums + jnp.where(lane == 2 * pair + 1, turned[1][:, 0:1], 0.0)
        sums_ref[here, :] = sums

    def query_loop(tile, carry):
        if own:
            query_tile(tile)
        else:
            reaches = key_range(ranges_ref, tile, rows, own)[0] < rows // K_TILE
            pl.when(reaches)(lambda: query_tile(tile))

            @pl.when(jnp.logical_not(reaches))
            def _():
                dq_ref[tile_of(tile, Q_TILE), :] = jnp.zeros((Q_TILE, LANES), dq_ref.dtype)

        return carry

    lax.fori_loop(0, rows // Q_TILE, query_loop, 0)
    sign = -1.0 if own else 1.0

    def finish(n, carry):
        here = tile_of(n, Q_TILE)
        left, right = dk0[here, :], dk1[here, :]
        dk_ref[here, :] = jnp.where(lane < 64, left, right).astype(dk_ref.dtype)
        dv_ref[here, :] = dv[here, :].astype(dv_ref.dtype)
        decay = decay_ref[here, :]
        decay = decay + jnp.where(lane == 2 * pair, sign * left[:, 67:68], 0.0)
        decay = decay + jnp.where(lane == 2 * pair + 1, sign * right[:, 3:4], 0.0)
        decay_ref[here, :] = decay
        return carry

    lax.fori_loop(0, rows // Q_TILE, finish, 0)


def attend_back(
    own, ranges, query, key_value, terms, key_terms, begins, grad, mixed, lse, local_heads,
    so_far=(),
):
    rows = query.shape[0]
    pairs = local_heads // 2
    wide = jax.ShapeDtypeStruct((rows, pairs * LANES), f32)
    sums = jax.ShapeDtypeStruct((rows, LANES), f32)
    if own:
        out_specs = [lane_block(rows, 0)] * 3 + [fixed((rows, LANES))]
        out_shape = (jax.ShapeDtypeStruct(wide.shape, bf16), wide, wide, sums)
    else:
        both = pl.BlockSpec((2, rows, LANES), lambda p, *_: (0, 0, p))
        out_specs = [lane_block(rows, 0), fixed((rows, LANES)), both, fixed((rows, LANES))]
        out_shape = (
            wide, sums, jax.ShapeDtypeStruct((2, rows, pairs * LANES), bf16), sums,
        )
    return pl.pallas_call(
        functools.partial(attend_back_kernel, local_heads, own),
        grid_spec=pltpu.PrefetchScalarGridSpec(
            num_scalar_prefetch=1,
            grid=(pairs,),
            in_specs=[
                lane_block(rows, 0),
                lane_block(rows, 0),
                lane_block(rows, pairs),
                fixed((rows, LANES)),
                fixed((rows, LANES) if own else (TERM_ROWS, rows)),
                fixed((8, rows)),
                lane_block(rows, 0),
                lane_block(rows, 0),
                pair_block(8, rows),
            ]
            + ([lane_block(rows, 0), fixed((rows, LANES))] if own else []),
            out_specs=out_specs,
            scratch_shapes=[
                pltpu.VMEM((rows, LANES), bf16),
                pltpu.VMEM((rows, LANES), bf16),
                pltpu.VMEM((LANES, rows), bf16),
                pltpu.VMEM((LANES, rows), bf16),
                pltpu.VMEM((rows, LANES), f32),
                pltpu.VMEM((rows, LANES), f32),
                pltpu.VMEM((rows, LANES), f32),
                pltpu.VMEM((LANES, Q_TILE), f32),
                pltpu.VMEM((LANES, Q_TILE), f32),
            ],
        ),
        out_shape=out_shape,
        cost_estimate=pl.CostEstimate(
            flops=80_000_000_000 if own else 15_000_000_000,
            transcendentals=20_000_000,
            bytes_accessed=25_000_000,
        ),
        name="attend_back_own" if own else "attend_back_prev",
    )(
        ranges, query, key_value, key_value, terms, key_terms, begins, grad, mixed, lse, *so_far
    )


PIECES = 4


def partners():
    me = lax.axis_index("head")
    near = me + 1 - 2 * (me % 2)
    far = (me + 2) % 4
    cross = (near + 2) % 4
    return me, near, far, cross


def signal(other):
    pl.semaphore_signal(
        pltpu.get_barrier_semaphore(), inc=1, device_id=other, device_id_type=pl.DeviceIdType.MESH
    )


def greet(others):
    for other in others:
        signal(other)
    pl.semaphore_wait(pltpu.get_barrier_semaphore(), len(others))


def remote(source, target, send, receive, other):
    return pltpu.make_async_remote_copy(
        src_ref=source,
        dst_ref=target,
        send_sem=send,
        recv_sem=receive,
        device_id=other,
        device_id_type=pl.DeviceIdType.MESH,
    )


def on_head(index):
    return {"head": index}


def on_blk(index):
    return {"blk": index}


def piece_at(ref, slot, piece, size):
    span = size // PIECES
    return ref.at[pl.ds(pl.multiple_of(slot * size + piece * span, span), span), :]


class Slots:
    def __init__(self, by_device):
        me, near, far, cross = partners()
        if by_device:
            self.own = self.sent_near = self.sent_far = me
            self.near, self.far, self.cross = near, far, cross
            self.passed = far
        else:
            self.own, self.sent_near, self.sent_far = 3, 2, 1
            self.near, self.far, self.cross = 2, 1, 0
            self.passed = 0


def spread_piece(source, all_ref, size, sems, piece, slots):
    me, near, far, _ = partners()
    far_send, far_recv, near_send, near_recv, _, _, own = sems
    copies = (
        remote(source, piece_at(all_ref, slots.sent_far, piece, size), far_send.at[piece],
               far_recv.at[piece], on_head(far)),
        remote(source, piece_at(all_ref, slots.sent_near, piece, size), near_send.at[piece],
               near_recv.at[piece], on_head(near)),
        pltpu.make_async_copy(source, piece_at(all_ref, slots.own, piece, size), own.at[piece]),
    )
    for copy in copies:
        copy.start()
    return copies


def hand_on(all_ref, size, sems, sent, slots):
    me, near, far, cross = partners()
    far_send, far_recv, near_send, near_recv, on_send, on_recv, own = sems
    passed = []
    for piece in range(PIECES):
        there = piece_at(all_ref, slots.far, piece, size)
        remote(there, there, far_send.at[piece], far_recv.at[piece], on_head(far)).wait_recv()
        copy = remote(
            there, piece_at(all_ref, slots.passed, piece, size), on_send.at[piece],
            on_recv.at[piece], on_head(near),
        )
        copy.start()
        passed.append(copy)

    def finish():
        for piece in range(PIECES):
            to_far, to_near, local = sent[piece]
            to_far.wait_send()
            to_near.wait_send()
            local.wait()
            passed[piece].wait_send()
            there = piece_at(all_ref, slots.near, piece, size)
            remote(there, there, near_send.at[piece], near_recv.at[piece], on_head(near)).wait_recv()
            there = piece_at(all_ref, slots.cross, piece, size)
            remote(there, there, on_send.at[piece], on_recv.at[piece], on_head(near)).wait_recv()

    return finish


def gather_sems():
    return [pltpu.SemaphoreType.DMA((PIECES,)) for _ in range(7)]


def blk_peers():
    here = lax.axis_index("blk")
    half = lax.axis_size("blk") // 2
    low, high = here % 2, here // 2
    partner = here + 1 - 2 * low
    after = [((high + t) % half) * 2 + low for t in range(half)]
    return here, partner, after


class Line:
    def __init__(self, block_of, kinds, sems):
        self.block_of, self.kinds = block_of, kinds
        self.pair_send, self.pair_recv, self.up_send, self.up_recv, self.down_send, self.down_recv = sems
        here = lax.axis_index("blk")
        self.half = lax.axis_size("blk") // 2
        self.low, self.high = here % 2, here // 2
        self.partner = here + 1 - 2 * self.low
        self.has_up, self.has_down = self.high < self.half - 1, self.high > 0

    def greet(self, others):
        greet_sum = len(others) + 1
        for other in others + [on_blk(self.partner)]:
            signal(other)
        pl.when(self.has_up)(lambda: signal(on_blk(self.at(self.high + 1))))
        pl.when(self.has_down)(lambda: signal(on_blk(self.at(self.high - 1))))
        ends = (self.high == 0).astype(jnp.int32) + (self.high == self.half - 1).astype(jnp.int32)
        pl.semaphore_wait(pltpu.get_barrier_semaphore(), greet_sum + 2 - ends)

    def at(self, high):
        return high * 2 + self.low

    def pair_copy(self, kind, high, low):
        block = self.block_of(kind, high * 2 + low)
        return remote(
            block, block, self.pair_send.at[kind, high], self.pair_recv.at[kind, high],
            on_blk(self.partner),
        )

    def up_copy(self, kind, high):
        block = self.block_of(kind, self.at(high))
        return remote(
            block, block, self.up_send.at[kind, high], self.up_recv.at[kind, high],
            on_blk(self.at(jnp.minimum(self.high + 1, self.half - 1))),
        )

    def down_copy(self, kind, high):
        block = self.block_of(kind, self.at(high))
        return remote(
            block, block, self.down_send.at[kind, high], self.down_recv.at[kind, high],
            on_blk(self.at(jnp.maximum(self.high - 1, 0))),
        )

    def launch(self, kind):
        self.pair_copy(kind, self.high, self.low).start()
        pl.when(self.has_up)(lambda: self.up_copy(kind, self.high).start())
        pl.when(self.has_down)(lambda: self.down_copy(kind, self.high).start())

    def step(self, t):
        for kind in range(self.kinds):
            below, above = self.high - t, self.high + t

            @pl.when(below >= 0)
            def _():
                self.up_copy(kind, below).wait_recv()
                self.pair_copy(kind, below, self.low).start()
                pl.when(self.has_up)(lambda: self.up_copy(kind, below).start())

            @pl.when(above < self.half)
            def _():
                self.down_copy(kind, above).wait_recv()
                self.pair_copy(kind, above, self.low).start()
                pl.when(self.has_down)(lambda: self.down_copy(kind, above).start())

    def finish(self):
        for kind in range(self.kinds):

            def wait(high, carry):
                self.pair_copy(kind, high, self.low).wait_send()
                self.pair_copy(kind, high, 1 - self.low).wait_recv()

                @pl.when((high <= self.high) & self.has_up)
                def _():
                    self.up_copy(kind, high).wait_send()

                @pl.when((high >= self.high) & self.has_down)
                def _():
                    self.down_copy(kind, high).wait_send()

                return carry

            lax.fori_loop(0, self.half, wait, 0)


def gather_first_kernel(pack_ref, tokens_ref, cotangent_ref, pack_all, tokens_all, cotangent_all,
                        *sems):
    swap_send, swap_recv, swap_own = sems[:3]
    token_sems, cotangent_sems = sems[9:16], sems[16:23]
    me, near, far, cross = partners()
    sources = (me, near, far, cross)
    line = Line(lambda kind, blk: pack_all.at[blk, sources[kind]], 4, sems[3:9])
    here = lax.axis_index("blk")
    line.greet([on_head(near), on_head(far), on_head(cross)])
    swaps = [pltpu.make_async_copy(pack_ref.at[me], pack_all.at[here, me], swap_own)]
    for kind, other in enumerate((near, far, cross)):
        swaps.append(
            remote(
                pack_ref.at[other],
                pack_all.at[here, me],
                swap_send.at[kind],
                swap_recv.at[kind],
                on_head(other),
            )
        )
    for swap in swaps:
        swap.start()
    size = tokens_ref.shape[0]
    span = size // PIECES

    def spread_all(ref, all_ref, some, slots):
        return [
            spread_piece(ref.at[pl.ds(piece * span, span), :], all_ref, size, some, piece, slots)
            for piece in range(PIECES)
        ]

    by_device, crossing = Slots(True), Slots(False)
    tokens_sent = spread_all(tokens_ref, tokens_all, token_sems, by_device)
    swaps[0].wait()
    line.launch(0)
    for kind, source in enumerate((near, far, cross)):
        block = pack_all.at[here, source]
        remote(
            block, block, swap_send.at[kind], swap_recv.at[kind], on_head(source)
        ).wait_recv()
        line.launch(kind + 1)
    cotangent_sent = spread_all(cotangent_ref, cotangent_all, cotangent_sems, crossing)
    for t in range(1, line.half):
        line.step(t)
    finish_tokens = hand_on(tokens_all, size, token_sems, tokens_sent, by_device)
    finish_cotangent = hand_on(cotangent_all, size, cotangent_sems, cotangent_sent, crossing)
    for swap in swaps[1:]:
        swap.wait_send()
    line.finish()
    finish_tokens()
    finish_cotangent()


def gather_first(pack, tokens, cotangent, number):
    groups, share, columns = pack.shape
    peers = lax.axis_size("blk")
    rows, width = tokens.shape
    whole = jax.ShapeDtypeStruct((groups * rows, width), bf16)
    vmem, anywhere = pl.BlockSpec(memory_space=pltpu.VMEM), pl.BlockSpec(memory_space=pl.ANY)
    all_pack, all_tokens, all_cotangent = pl.pallas_call(
        gather_first_kernel,
        in_specs=[vmem] * 3,
        out_specs=[anywhere] * 3,
        out_shape=[jax.ShapeDtypeStruct((peers, groups, share, columns), bf16), whole, whole],
        scratch_shapes=[
            pltpu.SemaphoreType.DMA((3,)),
            pltpu.SemaphoreType.DMA((3,)),
            pltpu.SemaphoreType.DMA,
        ]
        + [pltpu.SemaphoreType.DMA((4, peers // 2)) for _ in range(6)]
        + gather_sems()
        + gather_sems(),
        compiler_params=pltpu.CompilerParams(collective_id=number, has_side_effects=True),
        cost_estimate=pl.CostEstimate(
            flops=70_000_000_000, transcendentals=0, bytes_accessed=30_000_000
        ),
        name="gather_first",
    )(pack, tokens, cotangent)
    return all_pack.reshape(peers * groups * share, columns), all_tokens, all_cotangent


class Sum:
    def __init__(self, part_ref, buffers, sems, size, by_device):
        self.part_ref, self.size, self.span = part_ref, size, size // PIECES
        self.slots = Slots(by_device)
        self.near_buf, self.turn_buf, self.far_buf = buffers
        self.near_send, self.near_recv, self.far_send, self.far_recv = sems
        self.near_copies, self.far_copies = [], []

    def piece(self, n):
        return slice(n * self.span, (n + 1) * self.span)

    def start(self):
        me, near, far, cross = partners()
        for which, shard in ((0, self.slots.cross), (1, self.slots.near)):
            for n in range(PIECES):
                copy = remote(
                    piece_at(self.part_ref, shard, n, self.size),
                    self.near_buf.at[which, pl.ds(n * self.span, self.span), :],
                    self.near_send.at[which, n],
                    self.near_recv.at[which, n],
                    on_head(near),
                )
                copy.start()
                self.near_copies.append(copy)

    def turn(self):
        me, near, far, cross = partners()
        for n in range(PIECES):
            here = self.piece(n)
            self.near_copies[n].wait_recv()
            self.turn_buf[here, :] = (
                piece_at(self.part_ref, self.slots.far, n, self.size)[...].astype(f32)
                + self.near_buf[0, here, :].astype(f32)
            ).astype(bf16)
            copy = remote(
                self.turn_buf.at[pl.ds(n * self.span, self.span), :],
                self.far_buf.at[pl.ds(n * self.span, self.span), :],
                self.far_send.at[n],
                self.far_recv.at[n],
                on_head(far),
            )
            copy.start()
            self.far_copies.append(copy)

    def total(self, n):
        self.near_copies[PIECES + n].wait_recv()
        self.far_copies[n].wait_recv()
        here = self.piece(n)
        return (
            piece_at(self.part_ref, self.slots.own, n, self.size)[...].astype(f32)
            + self.near_buf[1, here, :].astype(f32)
            + self.far_buf[here, :].astype(f32)
        )

    def finish(self):
        for copy in self.near_copies + self.far_copies:
            copy.wait_send()


def sum_buffers(size, width):
    return [
        pltpu.VMEM((2, size, width), bf16),
        pltpu.VMEM((size, width), bf16),
        pltpu.VMEM((size, width), bf16),
    ]


def sum_sems():
    return [
        pltpu.SemaphoreType.DMA((2, PIECES)),
        pltpu.SemaphoreType.DMA((2, PIECES)),
        pltpu.SemaphoreType.DMA((PIECES,)),
        pltpu.SemaphoreType.DMA((PIECES,)),
    ]


def exchange_kernel(local, extras, summed, *refs):
    part_ref, extra_refs = refs[0], refs[1 : 1 + extras]
    out_ref, all_ref, payload = refs[1 + extras : 4 + extras]
    sems = refs[4 + extras :]
    size = out_ref.shape[0]
    span = size // PIECES
    _, near, far, _ = partners()
    greet([on_head(near), on_head(far)])
    slots = Slots(summed)
    if not summed:
        shares = Sum(part_ref, sems[7:10], sems[10:], size, True)
        shares.start()
        shares.turn()
    sent = []
    for piece in range(PIECES):
        here = slice(piece * span, (piece + 1) * span)
        total = part_ref[here, :] if summed else shares.total(piece)
        result, share = local(total, here, *extra_refs)
        out_ref[here, :] = result.astype(out_ref.dtype)
        payload[here, :] = share.astype(bf16)
        source = payload.at[pl.ds(piece * span, span), :]
        sent.append(spread_piece(source, all_ref, size, sems[:7], piece, slots))
    hand_on(all_ref, size, sems[:7], sent, slots)()
    if not summed:
        shares.finish()


def exchange(local, part, extras, summed, number, name):
    rows, width = part.shape
    size = rows if summed else rows // 4
    vmem = pl.BlockSpec(memory_space=pltpu.VMEM)
    return pl.pallas_call(
        functools.partial(exchange_kernel, local, len(extras), summed),
        in_specs=[vmem] * (1 + len(extras)),
        out_specs=[vmem, pl.BlockSpec(memory_space=pl.ANY)],
        out_shape=[
            jax.ShapeDtypeStruct((size, width), f32),
            jax.ShapeDtypeStruct((4 * size, width), bf16),
        ],
        scratch_shapes=[pltpu.VMEM((size, width), bf16)]
        + gather_sems()
        + ([] if summed else sum_buffers(size, width) + sum_sems()),
        compiler_params=pltpu.CompilerParams(collective_id=number, has_side_effects=True),
        cost_estimate=pl.CostEstimate(
            flops=40_000_000_000 if summed else 70_000_000_000,
            transcendentals=0,
            bytes_accessed=16_000_000,
        ),
        name=name,
    )(part, *extras)


def column_chunks(width):
    count = max(width // 512, 1)
    first = width - 512 * (count - 1)
    return [(0, first)] + [(first + 512 * n, 512) for n in range(count - 1)]


def finish_last_kernel(grad_ref, output_grad_ref, second_ref, first_ref, down_ref, grad_middle_ref,
                       tokens_ref, gain_ref, middle_ref, weights_ref, output_ref, second_out_ref,
                       tokens_grad_ref, result_ref, *refs):
    buffers = (refs[0:3], refs[3:6])
    first_buffers, down_buffers = refs[6:9], refs[9:12]
    pair_send, pair_recv, line_send, line_recv, swap_send, swap_recv = refs[12:18]
    first_sems, down_sems = refs[18:22], refs[22:26]
    me, near, far, cross = partners()
    others = (near, far, cross)
    here, partner, after = blk_peers()
    steps = len(after)
    greet(
        [on_head(other) for other in others]
        + [on_blk(partner)]
        + [on_blk(peer) for peer in after[1:]]
    )
    size = result_ref.shape[0]
    first = Sum(first_ref, first_buffers, first_sems, size, True)
    down = Sum(down_ref, down_buffers, down_sems, size, False)
    chunks = []
    for ref, out_ref, some in (
        (grad_ref, weights_ref, buffers[0]), (output_grad_ref, output_ref, buffers[1])
    ):
        for start, wide in column_chunks(ref.shape[3]):
            chunks.append((ref, out_ref, some, pl.ds(start, wide)))
    groups = grad_ref.shape[1]
    first.start()
    sent = []
    for c, (ref, _, (pair_buf, _, _), at) in enumerate(chunks):
        for t in list(range(1, steps)) + [0]:
            copy = remote(
                ref.at[after[t] + partner - here, :, :, at],
                pair_buf.at[t, :, :, at],
                pair_send.at[c, t],
                pair_recv.at[c, t],
                on_blk(partner),
            )
            copy.start()
            sent.append(copy)
    first.turn()

    def swap(source_ref, out_ref, c):
        for kind, other in enumerate(others):
            copy = remote(
                source_ref.at[other], out_ref.at[me], swap_send.at[c, kind],
                swap_recv.at[c, kind], on_head(other),
            )
            copy.start()
            sent.append(copy)

    swap(second_ref, second_out_ref, len(chunks))
    down.start()
    down.turn()

    def add_up(c):
        ref, out_ref, (pair_buf, line_buf, row_buf), at = chunks[c]
        block = pair_buf.at[0, :, :, at]
        remote(block, block, pair_send.at[c, 0], pair_recv.at[c, 0], on_blk(partner)).wait_recv()
        for t in range(1, steps):
            block = line_buf.at[t, :, :, at]
            remote(
                block, block, line_send.at[c, t], line_recv.at[c, t], on_blk(after[t])
            ).wait_recv()

        def add_all(group, carry):
            total = ref[here, group, :, at].astype(f32) + pair_buf[0, group, :, at].astype(f32)
            for t in range(1, steps):
                total = total + line_buf[t, group, :, at].astype(f32)
            row_buf[group, :, at] = total.astype(bf16)
            return carry

        lax.fori_loop(0, groups, add_all, 0)
        out_ref[me, :, at] = row_buf[me, :, at]
        swap(row_buf.at[:, :, at], out_ref.at[:, :, at], c)

    def put(shares, local, out_ref, extra_refs):
        for piece in range(PIECES):
            rows = shares.piece(piece)
            value, _ = local(shares.total(piece), rows, *extra_refs)
            out_ref[rows, :] = value.astype(out_ref.dtype)

    for c, (ref, _, (pair_buf, line_buf, _), at) in enumerate(chunks):
        for t in range(1, steps):
            block = pair_buf.at[t, :, :, at]
            remote(
                block, block, pair_send.at[c, t], pair_recv.at[c, t], on_blk(partner)
            ).wait_recv()

            def add(group, carry):
                pair_buf[t, group, :, at] = (
                    ref[after[t], group, :, at].astype(f32)
                    + pair_buf[t, group, :, at].astype(f32)
                ).astype(bf16)
                return carry

            lax.fori_loop(0, groups, add, 0)
            copy = remote(
                block, line_buf.at[t, :, :, at], line_send.at[c, t], line_recv.at[c, t],
                on_blk(after[t]),
            )
            copy.start()
            sent.append(copy)
        if c > 0:
            add_up(c - 1)
    put(first, after_first, tokens_grad_ref, (grad_middle_ref, tokens_ref, gain_ref))
    add_up(len(chunks) - 1)
    put(down, after_down, result_ref, (middle_ref,))
    second_out_ref[me] = second_ref[me]
    for c in range(len(chunks) + 1):
        if c < len(chunks):
            _, out_ref, _, at = chunks[c]
            out_ref = out_ref.at[:, :, at]
        else:
            out_ref = second_out_ref
        for kind, other in enumerate(others):
            block = out_ref.at[other]
            remote(
                block, block, swap_send.at[c, kind], swap_recv.at[c, kind], on_head(other)
            ).wait_recv()
    for copy in sent:
        copy.wait_send()
    first.finish()
    down.finish()


def finish_last(grad, output_grad, second, groups, part_first, part_down, grad_middle, tokens, gain,
                middle, number):
    peers = lax.axis_size("blk")
    share = grad.shape[0] // (peers * groups)
    rows, width = tokens.shape
    vmem = pl.BlockSpec(memory_space=pltpu.VMEM)
    half = peers // 2
    widths = (grad.shape[1], output_grad.shape[1])
    chunks = sum(len(column_chunks(width)) for width in widths)

    def blocks(columns):
        return [pltpu.VMEM((half, groups, share, columns), bf16) for _ in range(2)] + [
            pltpu.VMEM((groups, share, columns), bf16)
        ]

    return pl.pallas_call(
        finish_last_kernel,
        in_specs=[vmem] * 9,
        out_specs=[vmem] * 5,
        out_shape=[
            jax.ShapeDtypeStruct((groups, share, columns), bf16)
            for columns in widths + (second.shape[1],)
        ]
        + [
            jax.ShapeDtypeStruct((rows, width), f32),
            jax.ShapeDtypeStruct((rows, width), bf16),
        ],
        scratch_shapes=blocks(widths[0])
        + blocks(widths[1])
        + sum_buffers(rows, width)
        + sum_buffers(rows, width)
        + [pltpu.SemaphoreType.DMA((chunks, half)) for _ in range(4)]
        + [pltpu.SemaphoreType.DMA((chunks + 1, 3)) for _ in range(2)]
        + sum_sems()
        + sum_sems(),
        compiler_params=pltpu.CompilerParams(
            collective_id=number, has_side_effects=True, vmem_limit_bytes=60 << 20
        ),
        cost_estimate=pl.CostEstimate(
            flops=80_000_000_000, transcendentals=0, bytes_accessed=40_000_000
        ),
        name="finish_last",
    )(
        grad.reshape(peers, groups, share, widths[0]),
        output_grad.reshape(peers, groups, share, widths[1]),
        second.reshape(groups, share, second.shape[1]),
        part_first, part_down, grad_middle, tokens, gain, middle,
    )


def inverse_rms(value):
    return lax.rsqrt(jnp.mean(value * value, axis=1, keepdims=True) + epsilon)


def through_norm(grad, value):
    factor = inverse_rms(value)
    normed = value * factor
    return factor * (grad - normed * jnp.mean(grad * normed, axis=1, keepdims=True))


def after_attention(total, here, tokens_ref, gain_ref):
    middle = tokens_ref[here, :].astype(f32) + total
    return middle, middle * inverse_rms(middle) * gain_ref[0:1, :]


def after_hidden(total, here, cotangent_ref, middle_ref, gain_ref):
    grad = cotangent_ref[here, :].astype(f32) + through_norm(
        total * gain_ref[0:1, :], middle_ref[here, :]
    )
    return grad, grad


def after_first(total, here, grad_ref, tokens_ref, gain_ref):
    grad = grad_ref[here, :] + through_norm(
        total * gain_ref[0:1, :], tokens_ref[here, :].astype(f32)
    )
    return grad, None


def after_down(total, here, middle_ref):
    return middle_ref[here, :] + total, None


FEED_TILE = 256
FEED_COLUMNS = 512


def feed_kernel(input_ref, cotangent_ref, weight_ref, down_ref, grad_ref, total_ref, acts, turned0,
                turned1, stage, near_buf, far_buf, near_send, near_recv, far_send, far_recv):
    step = pl.program_id(0)
    hidden_width = weight_ref.shape[1] // 3
    size = total_ref.shape[0]
    per = size // FEED_TILE
    tiles = 4 * per
    _, near, far, _ = partners()

    @pl.when(step == 0)
    def _():
        greet([on_head(near), on_head(far)])

    def to_near(which, piece):
        return remote(
            stage.at[which * per + piece],
            near_buf.at[which, piece],
            near_send.at[which, piece],
            near_recv.at[which, piece],
            on_head(near),
        )

    def to_far(piece):
        return remote(
            near_buf.at[0, piece], far_buf.at[piece], far_send.at[piece], far_recv.at[piece],
            on_head(far),
        )

    @pl.when(step < tiles)
    def _():
        here = tile_of(step, FEED_TILE)
        inputs, cotangent = input_ref[...], cotangent_ref[...]
        turned0[:, here] = inputs.T
        turned1[:, here] = cotangent.T
        gate_at, up_at, down_at = (
            slice(n * hidden_width, (n + 1) * hidden_width) for n in range(3)
        )
        gate = dot(inputs, weight_ref[:, gate_at])
        up = dot(inputs, weight_ref[:, up_at])
        grad_hidden = dot(cotangent, weight_ref[:, down_at])
        opening = jax.nn.sigmoid(gate)
        active = gate * opening
        hidden = (active * up).astype(bf16)
        grad_gate = (grad_hidden * up * opening * (1.0 + gate * (1.0 - opening))).astype(bf16)
        grad_up = (grad_hidden * active).astype(bf16)
        acts[here, gate_at] = grad_gate
        acts[here, up_at] = grad_up
        acts[here, down_at] = hidden
        down_ref[...] = dot(hidden, weight_ref[:, down_at], NT).astype(bf16)
        back = dot(grad_gate, weight_ref[:, gate_at], NT) + dot(
            grad_up, weight_ref[:, up_at], NT
        )
        for piece in range(per):
            for which, first in ((0, 0), (1, 2 * per)):

                @pl.when(step == first + piece)
                def _():
                    stage[which * per + piece] = back.astype(bf16)
                    to_near(which, piece).start()

            @pl.when(step == per + piece)
            def _():
                to_near(0, piece).wait_recv()
                near_buf[0, piece] = (back + near_buf[0, piece].astype(f32)).astype(bf16)
                to_far(piece).start()

            @pl.when(step == 3 * per + piece)
            def _():
                total_ref[piece * FEED_TILE : (piece + 1) * FEED_TILE, :] = back

    @pl.when(step >= tiles)
    def _():
        at = tile_of(step - tiles, FEED_COLUMNS)
        from_input = (step - tiles) * FEED_COLUMNS < 2 * hidden_width

        @pl.when(from_input)
        def _():
            grad_ref[...] = dot(turned0[...], acts[:, at]).astype(bf16)

        @pl.when(jnp.logical_not(from_input))
        def _():
            grad_ref[...] = dot(turned1[...], acts[:, at]).astype(bf16)

    @pl.when(step == pl.num_programs(0) - 1)
    def _():
        for piece in range(per):
            here = slice(piece * FEED_TILE, (piece + 1) * FEED_TILE)
            to_near(1, piece).wait_recv()
            to_far(piece).wait_recv()
            total_ref[here, :] += near_buf[1, piece].astype(f32) + far_buf[piece].astype(f32)
            to_near(0, piece).wait_send()
            to_near(1, piece).wait_send()
            to_far(piece).wait_send()


def feed(inputs, cotangent, weight, number):
    rows, width = inputs.shape
    columns = weight.shape[1]
    size = rows // 4
    tiles, per = rows // FEED_TILE, size // FEED_TILE
    tile = pl.BlockSpec((FEED_TILE, width), lambda n: (jnp.minimum(n, tiles - 1), 0))

    def whole(shape):
        return pl.BlockSpec(shape, lambda n: (0, 0), pipeline_mode=pl.Buffered(1))

    return pl.pallas_call(
        feed_kernel,
        grid=(tiles + columns // FEED_COLUMNS,),
        in_specs=[tile, tile, whole((width, columns))],
        out_specs=[
            tile,
            pl.BlockSpec((width, FEED_COLUMNS), lambda n: (0, jnp.maximum(n - tiles, 0))),
            whole((size, width)),
        ],
        out_shape=[
            jax.ShapeDtypeStruct((rows, width), bf16),
            jax.ShapeDtypeStruct((width, columns), bf16),
            jax.ShapeDtypeStruct((size, width), f32),
        ],
        scratch_shapes=[
            pltpu.VMEM((rows, columns), bf16),
            pltpu.VMEM((width, rows), bf16),
            pltpu.VMEM((width, rows), bf16),
            pltpu.VMEM((2 * per, FEED_TILE, width), bf16),
            pltpu.VMEM((2, per, FEED_TILE, width), bf16),
            pltpu.VMEM((per, FEED_TILE, width), bf16),
            pltpu.SemaphoreType.DMA((2, per)),
            pltpu.SemaphoreType.DMA((2, per)),
            pltpu.SemaphoreType.DMA((per,)),
            pltpu.SemaphoreType.DMA((per,)),
        ],
        compiler_params=pltpu.CompilerParams(
            collective_id=number, has_side_effects=True, vmem_limit_bytes=63 << 20
        ),
        cost_estimate=pl.CostEstimate(
            flops=6 * rows * width * columns, transcendentals=rows * columns // 3,
            bytes_accessed=45_000_000,
        ),
        name="feed",
    )(inputs, cotangent, weight)


def over_tokens(operand, other_side):
    return lax.dot_general(
        operand, other_side, (((0,), (0,)), ((), ())), preferred_element_type=f32
    )


def sent_columns(pieces, groups):
    packed = jnp.concatenate(
        [piece.reshape(piece.shape[0], groups, -1) for piece in pieces], axis=2
    )
    mine = lax.all_to_all(packed, "head", split_axis=1, concat_axis=0, tiled=True)
    return mine.reshape(mine.shape[0], mine.shape[2])


def all_rows(mine):
    return lax.all_gather(mine, "blk", axis=0, tiled=True)


def row_sums(grad):
    return lax.psum_scatter(grad, "blk", scatter_dimension=0, tiled=True)


def body(
    tokens,
    segment,
    norm1_gain,
    w_query,
    w_key,
    w_value,
    w_gate_out,
    w_forget,
    forget_bias,
    w_output,
    norm2_gain,
    w_gate,
    w_up,
    w_down,
    cotangent,
):
    token_rows, model_width = tokens.shape
    groups = lax.axis_size("head")
    head_count = forget_bias.shape[0]
    local_heads = head_count // groups
    local_width = model_width // groups
    hidden_width = w_gate.shape[1] // groups
    rows = token_rows * groups
    share = w_query.shape[0]
    group = lax.axis_index("head")

    low = lambda array: array.astype(bf16)
    spread = lambda gain: jnp.broadcast_to(low(gain)[:, None, None], (share, groups, 1))
    forget_low = low(w_forget).reshape(share, groups, local_heads)
    rest = LANES - local_heads - 2
    small = jnp.concatenate(
        [forget_low, spread(norm1_gain), spread(norm2_gain), jnp.zeros((share, groups, rest), bf16)],
        axis=2,
    )
    pack = jnp.concatenate(
        [
            low(piece).reshape(share, groups, -1)
            for piece in (w_key, w_value, small, w_query, w_gate_out, w_output)
        ],
        axis=2,
    )
    first, tokens_all, cotangent_all = gather_first(
        jnp.swapaxes(pack, 0, 1), tokens, cotangent, 0
    )
    kv_width = 2 * local_width + LANES
    output_weight = first[:, kv_width + 2 * local_width :]

    segment_plus = segment + 1
    earlier_segment = passed_along(segment_plus, "blk", 1)
    window = jnp.concatenate([earlier_segment, segment_plus])
    begins = jnp.sum(
        (window[:, None] < segment_plus[None, :]).astype(jnp.int32), axis=0
    )
    tiles = begins.reshape(rows // Q_TILE, Q_TILE)
    ranges = jnp.stack([tiles[:, 0] // K_TILE, (tiles[:, -1] + K_TILE - 1) // K_TILE])
    begins = jnp.broadcast_to(begins[None, :], (8, rows))

    def gain_rows(column):
        gain = first[:, 2 * local_width + local_heads + column].astype(f32)
        return jnp.broadcast_to(gain[None, :], (8, model_width))

    gain1, gain2 = gain_rows(0), gain_rows(1)
    bias = lax.dynamic_slice_in_dim(forget_bias, group * local_heads, local_heads, 0)
    bias = jnp.broadcast_to(jnp.pad(bias, (0, LANES - local_heads))[None, :], (8, LANES))
    input1, key_value, terms, turned_terms, forget = project(
        tokens_all, gain1, first, bias, 2 * local_width, local_heads
    )
    earlier_kv = passed_along(key_value, "blk", 1)
    earlier_terms = passed_along(turned_terms, "blk", 1)
    query = dot(input1, first[:, kv_width : kv_width + local_width]).astype(bf16)
    gate_raw = dot(
        input1, first[:, kv_width + local_width : kv_width + 2 * local_width]
    )

    so_far = attend(True, ranges, query, key_value, terms, terms, begins, local_heads)
    later = lax.optimization_barrier((low(w_gate), low(w_up), low(w_down), key_value))
    mine = sent_columns(later[:3], groups)
    mine, earlier_kv, earlier_terms, so_far = lax.optimization_barrier(
        (mine, earlier_kv, earlier_terms, so_far)
    )
    second = all_rows(mine)
    attended, lse = attend(
        False, ranges, query, earlier_kv, terms, earlier_terms, begins, local_heads, so_far
    )
    opened = jax.nn.sigmoid(gate_raw)
    attended_wide = attended.astype(f32)
    gated = (opened * attended_wide).astype(bf16)
    branch = dot(gated, output_weight, NT).astype(bf16)
    middle, input2 = exchange(
        after_attention, branch, [tokens, gain2], False, 1, "exchange_middle"
    )
    down, second_grad, grad_input2 = feed(input2, cotangent_all, second, 4)
    second_part = row_sums(second_grad)
    grad_middle, grad_branch = exchange(
        after_hidden, grad_input2, [cotangent, middle, gain2], True, 2, "exchange_hidden"
    )

    grad_gated = dot(grad_branch, output_weight)
    grad_attended = (grad_gated * opened).astype(bf16)
    grad_gate_pre = (grad_gated * attended_wide * opened * (1.0 - opened)).astype(bf16)
    dq_prev, rows_prev, dkv_prev, decay_prev = attend_back(
        False, ranges, query, earlier_kv, terms, earlier_terms, begins, grad_attended, attended,
        lse, local_heads,
    )
    dkv_later = passed_along(dkv_prev, "blk", -1)
    decay_later = passed_along(decay_prev[:, :8], "blk", -1)
    decay_later = jnp.pad(decay_later, ((0, 0), (0, LANES - 8)))
    dq, dk_own, dv_own, decay_own = attend_back(
        True, ranges, query, key_value, terms, terms, begins, grad_attended, attended,
        lse, local_heads, (dq_prev, rows_prev),
    )
    dk = (dk_own + dkv_later[0].astype(f32)).astype(bf16)
    dv = (dv_own + dkv_later[1].astype(f32)).astype(bf16)
    logf_grad = decay_back(decay_own, decay_later)
    forget_grad = jnp.where(
        jnp.arange(LANES)[None, :] < local_heads, logf_grad * jax.nn.sigmoid(-forget), 0.0
    ).astype(bf16)
    grads = jnp.concatenate([dk, dv, forget_grad, dq, grad_gate_pre], axis=1)
    first_grad = over_tokens(input1, grads)
    bias_part = jnp.sum(forget_grad.astype(f32), axis=0)
    row = jnp.arange(model_width)[:, None] % share
    column = jnp.arange(kv_width + 2 * local_width)[None, :]
    spread_bias = jnp.sum(
        jnp.where(row == jnp.arange(LANES)[None, :], bias_part[None, :], 0.0), axis=1, keepdims=True
    )
    first_grad = jnp.where(
        column == 2 * local_width + local_heads, spread_bias, first_grad
    ).astype(bf16)
    output_grad = over_tokens(grad_branch, gated).astype(bf16)
    grad_input1 = dot(grads, first[:, : kv_width + 2 * local_width], NT).astype(bf16)
    first_sum, output_sum, second_sum, tokens_grad, result = finish_last(
        first_grad, output_grad, second_part, groups, grad_input1, down, grad_middle, tokens,
        gain1, middle, 3,
    )
    first_sum, output_sum, second_sum = (
        jnp.swapaxes(array, 0, 1).astype(f32) for array in (first_sum, output_sum, second_sum)
    )

    def columns(array, start, width):
        return array[:, :, start : start + width].reshape(share, groups * width)

    key_sum, value_sum = (columns(first_sum, n * local_width, local_width) for n in range(2))
    forget_sum = columns(first_sum, 2 * local_width, local_heads)
    bias_total = first_sum[:local_heads, :, 2 * local_width + local_heads].T.reshape(head_count)
    query_sum, gate_out_sum = (
        columns(first_sum, kv_width + n * local_width, local_width) for n in range(2)
    )
    output_total = columns(output_sum, 0, local_width)
    gate_sum, up_sum, down_sum = (
        columns(second_sum, n * hidden_width, hidden_width) for n in range(3)
    )

    def along(weight, grad):
        return jnp.sum(low(weight).astype(f32) * grad, axis=1)

    gain1_total = (
        along(w_query, query_sum)
        + along(w_key, key_sum)
        + along(w_value, value_sum)
        + along(w_gate_out, gate_out_sum)
        + along(w_forget, forget_sum)
    ) / low(norm1_gain).astype(f32)
    gain2_total = (along(w_gate, gate_sum) + along(w_up, up_sum)) / low(norm2_gain).astype(f32)
    return (
        result,
        tokens_grad,
        gain1_total,
        query_sum,
        key_sum,
        value_sum,
        gate_out_sum,
        forget_sum,
        bias_total,
        output_total,
        gain2_total,
        gate_sum,
        up_sum,
        down_sum,
    )


def solution(mesh):
    both = ("blk", "head")
    matrix, vector = P(both, None), P(both)
    return jax.shard_map(
        body,
        mesh=mesh,
        in_specs=(
            matrix, P("blk"), vector, matrix, matrix, matrix, matrix, matrix, P(), matrix, vector,
            matrix, matrix, matrix, matrix,
        ),
        out_specs=(
            matrix, matrix, vector, matrix, matrix, matrix, matrix, matrix, P(), matrix, vector,
            matrix, matrix, matrix,
        ),
        check_vma=False,
    )
```

```python
import functools

import jax
import jax.numpy as jnp
from jax import lax
from jax.experimental import pallas as pl
from jax.experimental.pallas import tpu as pltpu
from jax.sharding import PartitionSpec as P

epsilon = 1e-06
LANES = 128
Q_TILE = 512
K_TILE = 512
FAR = -1e30
NT = (((1,), (1,)), ((), ()))
NN = (((1,), (0,)), ((), ()))
bf16 = jnp.bfloat16
f32 = jnp.float32


def dot(a, b, dims=NN, **kw):
    return lax.dot_general(a, b, dims, preferred_element_type=f32, **kw)


def passed_along(array, axis, by):
    peers = lax.axis_size(axis)
    pairs = [(i, i + by) for i in range(peers) if 0 <= i + by < peers]
    return lax.ppermute(array, axis, pairs)


def split3(value):
    high = value.astype(bf16)
    rest = value - high.astype(f32)
    mid = rest.astype(bf16)
    low = (rest - mid.astype(f32)).astype(bf16)
    return high, mid, low


def running(value_of, steps, rows, upper):
    place = lax.broadcasted_iota(jnp.int32, (rows, rows), 0)
    other = lax.broadcasted_iota(jnp.int32, (rows, rows), 1)
    tri = jnp.where((other >= place) if upper else (other <= place), 1.0, 0.0).astype(bf16)
    outs = [None] * steps
    carry = jnp.zeros((1, LANES), f32)
    order = range(steps - 1, -1, -1) if upper else range(steps)
    for n in order:
        block = value_of(n)
        total = sum(dot(tri, part) for part in split3(block)) + carry
        outs[n] = total
        carry = total[0:1] if upper else total[rows - 1 : rows]
    return outs, carry


PROJECT_TILE = 256
TERM_ROWS = 32


def project_kernel(local_heads, tokens_ref, gain_ref, weight_ref, bias_ref, input_ref, out_ref,
                   terms_ref, turned_ref, forget_ref, carry_ref):
    rows = tokens_ref.shape[0]
    wide = weight_ref.shape[1] - LANES

    @pl.when(pl.program_id(0) == 0)
    def _():
        carry_ref[...] = jnp.zeros_like(carry_ref)

    tokens = tokens_ref[...].astype(f32)
    input1 = (tokens * inverse_rms(tokens) * gain_ref[0:1, :]).astype(bf16)
    input_ref[...] = input1
    raw = dot(input1, weight_ref[...])
    out_ref[...] = raw[:, :wide].astype(bf16)
    forget = (raw[:, wide:] + bias_ref[0:1, :]).astype(bf16).astype(f32)
    forget_ref[...] = forget
    lane = lax.broadcasted_iota(jnp.int32, (rows, LANES), 1)
    logf = jnp.minimum(forget, 0.0) - jnp.log1p(jnp.exp(-jnp.abs(forget)))
    logf = jnp.where(lane < local_heads, logf, 0.0)
    place = lax.broadcasted_iota(jnp.int32, (rows, rows), 0)
    other = lax.broadcasted_iota(jnp.int32, (rows, rows), 1)
    tri = jnp.where(other <= place, 1.0, 0.0).astype(bf16)
    sums = sum(dot(tri, part) for part in split3(logf)) + carry_ref[0:1, :]
    carry_ref[0:1, :] = sums[rows - 1 : rows, :]
    high, mid, low = split3(sums)
    terms = (
        high.astype(f32)
        + pltpu.roll(mid.astype(f32), local_heads, 1)
        + pltpu.roll(low.astype(f32), 2 * local_heads, 1)
        + jnp.where(lane == 3 * local_heads, 1.0, 0.0)
    ).astype(bf16)
    terms_ref[...] = terms
    turned_ref[...] = terms.T[0:TERM_ROWS, :]


def project(tokens, gain, weight, bias, wide, local_heads):
    rows, width = tokens.shape

    def tile(columns):
        return pl.BlockSpec((PROJECT_TILE, columns), lambda n: (n, 0))

    def whole(*shape):
        return pl.BlockSpec(shape, lambda n: (0, 0))

    return pl.pallas_call(
        functools.partial(project_kernel, local_heads),
        grid=(rows // PROJECT_TILE,),
        in_specs=[tile(width), whole(8, width), whole(width, wide + LANES), whole(8, LANES)],
        out_specs=[
            tile(width),
            tile(wide),
            tile(LANES),
            pl.BlockSpec((TERM_ROWS, PROJECT_TILE), lambda n: (0, n)),
            tile(LANES),
        ],
        out_shape=[
            jax.ShapeDtypeStruct((rows, width), bf16),
            jax.ShapeDtypeStruct((rows, wide), bf16),
            jax.ShapeDtypeStruct((rows, LANES), bf16),
            jax.ShapeDtypeStruct((TERM_ROWS, rows), bf16),
            jax.ShapeDtypeStruct((rows, LANES), f32),
        ],
        scratch_shapes=[pltpu.VMEM((8, LANES), f32)],
        cost_estimate=pl.CostEstimate(
            flops=2 * rows * width * (wide + LANES), transcendentals=rows * LANES,
            bytes_accessed=20_000_000,
        ),
        name="project",
    )(tokens, gain, weight, bias)


def decay_back_kernel(own_ref, halo_ref, out_ref):
    rows = 256
    steps = own_ref.shape[0] // rows
    own, _ = running(lambda n: own_ref[n * rows : (n + 1) * rows, :], steps, rows, True)
    halo, _ = running(lambda n: halo_ref[n * rows : (n + 1) * rows, :], steps, rows, False)
    for n in range(steps):
        part = slice(n * rows, (n + 1) * rows)
        out_ref[part, :] = own[n] + (halo[n] - halo_ref[part, :])


def decay_back(own, halo):
    return pl.pallas_call(
        decay_back_kernel,
        out_shape=jax.ShapeDtypeStruct(own.shape, f32),
        name="decay_back",
    )(own, halo)


QUERY, KEY, TOTAL = range(3)


def placing(pair, local_heads, role):
    row = lax.broadcasted_iota(jnp.int32, (LANES, LANES), 0)
    col = lax.broadcasted_iota(jnp.int32, (LANES, LANES), 1)
    head = jnp.where(col < 64, 2 * pair + 1, 2 * pair)
    spot = jnp.where(col < 64, col, col - 64)
    term = spot - 3 * role
    is_term = (term >= 0) & (term < 3) & (row == term * local_heads + head)
    if role == QUERY:
        ones = (spot >= 3) & (spot < 9)
    else:
        ones = (spot < 3) & (role == KEY)
    is_one = ones & (row == 3 * local_heads)
    sign = -1.0 if role == KEY else 1.0
    return (jnp.where(is_term, sign, 0.0) + jnp.where(is_one, 1.0, 0.0)).astype(bf16)


def allowed_pairs(first_key, query_tile, rows, begin_row):
    shape = (K_TILE, Q_TILE)
    key_place = first_key + lax.broadcasted_iota(jnp.int32, shape, 0)
    query_place = rows + query_tile * Q_TILE + lax.broadcasted_iota(jnp.int32, shape, 1)
    return (key_place >= begin_row) & (key_place <= query_place)


def key_range(ranges_ref, query_tile, rows, own):
    count = rows // K_TILE
    base = count if own else 0
    first = jnp.clip(ranges_ref[0, query_tile] - base, 0, count)
    full = jnp.clip(ranges_ref[1, query_tile] - base, first, count)
    return first, full


def key_loops(ranges_ref, query_tile, rows, own, step, carry):
    first, full = key_range(ranges_ref, query_tile, rows, own)
    inside = query_tile * (Q_TILE // K_TILE) if own else rows // K_TILE
    full = jnp.minimum(full, inside)
    carry = lax.fori_loop(first, full, functools.partial(step, True), carry)
    carry = lax.fori_loop(full, inside, functools.partial(step, False), carry)
    if own:
        carry = lax.fori_loop(
            inside, inside + Q_TILE // K_TILE, functools.partial(step, True), carry
        )
    return carry


def tile_of(number, size):
    return pl.ds(pl.multiple_of(number * size, size), size)


def fill_keys(pair, local_heads, own, first, key_ref, terms_ref, keys):
    place = placing(pair, local_heads, KEY)
    lane = lax.broadcasted_iota(jnp.int32, (K_TILE, LANES), 1)
    rows = key_ref.shape[0]
    if not own:
        last = terms_ref[:, rows - LANES : rows].T
        total = dot(last, placing(pair, local_heads, TOTAL)[0:TERM_ROWS, :])[LANES - 1 : LANES, :]

    def fill(n, carry):
        here = tile_of(n, K_TILE)
        if own:
            extra = dot(terms_ref[here, :], place).astype(bf16)
        else:
            extra = dot(terms_ref[:, here].T, place[0:TERM_ROWS, :])
            extra = (extra + total).astype(bf16)
        key = key_ref[here, :]
        keys[0][here, :] = jnp.where(lane < 64, key, extra)
        keys[1][here, :] = jnp.where(lane < 64, extra, key)
        return carry

    lax.fori_loop(first, rows // K_TILE, fill, 0)


def query_tiles(q_ref, terms_ref, place, here, scaling):
    lane = lax.broadcasted_iota(jnp.int32, (Q_TILE, LANES), 1)
    extra = dot(terms_ref[here, :], place).astype(bf16)
    query = (q_ref[here, :].astype(f32) * scaling).astype(bf16)
    return jnp.where(lane < 64, query, extra), jnp.where(lane < 64, extra, query)


def attend_kernel(local_heads, own, ranges_ref, q_ref, k_ref, v_ref, t_query_ref, t_key_ref,
                  begin_ref, *refs):
    if own:
        acc_out_ref, state_out_ref, key0, key1, values, acc0, acc1 = refs
    else:
        acc_in_ref, state_in_ref, o_ref, lse_ref, key0, key1, values, acc0, acc1 = refs
    pair = pl.program_id(0)
    rows = q_ref.shape[0]
    base = rows if own else 0
    keys, accs = (key0, key1), (acc0, acc1)
    first, _ = key_range(ranges_ref, 0, rows, own)
    fill_keys(pair, local_heads, own, first, k_ref, t_key_ref, keys)

    def turn(n, carry):
        values[:, tile_of(n, K_TILE)] = v_ref[tile_of(n, K_TILE), :].T
        return carry

    lax.fori_loop(first, rows // K_TILE, turn, 0)
    place = placing(pair, local_heads, QUERY)

    def query_loop(tile, carry):
        here = tile_of(tile, Q_TILE)
        queries = query_tiles(q_ref, t_query_ref, place, here, 64**-0.5)
        begin_row = begin_ref[0:1, here]
        if own:
            low = jnp.full((1, Q_TILE), FAR, f32)
            zero = jnp.zeros((1, Q_TILE), f32)
            state = (low, zero, low, zero)
            for acc in accs:
                acc[...] = jnp.zeros_like(acc)
        else:
            state = tuple(state_in_ref[n : n + 1, here] for n in range(4))
            for h in range(2):
                accs[h][...] = acc_in_ref[64 * h : 64 * (h + 1), here]

        def step(masked, number, state):
            there = tile_of(number, K_TILE)
            fresh = []
            if masked:
                allowed = allowed_pairs(base + number * K_TILE, tile, rows, begin_row)
            for h in range(2):
                largest, total = state[2 * h], state[2 * h + 1]
                scores = dot(keys[h][there, :], queries[h], NT)
                if masked:
                    scores = jnp.where(allowed, scores, FAR)
                now = jnp.maximum(largest, jnp.max(scores, axis=0, keepdims=True))
                fade = jnp.exp(largest - now)
                weights = jnp.exp(scores - now)
                total = total * fade + jnp.sum(weights, axis=0, keepdims=True)
                accs[h][...] = accs[h][...] * fade + dot(
                    values[64 * h : 64 * (h + 1), there], weights.astype(bf16)
                )
                fresh += [now, total]
            return tuple(fresh)

        state = key_loops(ranges_ref, tile, rows, own, step, state)
        if own:
            for h in range(2):
                acc_out_ref[64 * h : 64 * (h + 1), here] = accs[h][...]
            for n in range(4):
                state_out_ref[n : n + 1, here] = state[n]
        else:
            mixed = jnp.concatenate(
                [accs[h][...] * (1.0 / state[2 * h + 1]) for h in range(2)], axis=0
            )
            o_ref[here, :] = mixed.T.astype(bf16)
            for h in range(2):
                lse_ref[h : h + 1, here] = state[2 * h] + jnp.log(state[2 * h + 1])
        return carry

    lax.fori_loop(0, rows // Q_TILE, query_loop, 0)


def lane_block(rows, offset):
    return pl.BlockSpec((rows, LANES), lambda p, *_: (0, offset + p))


def fixed(shape):
    return pl.BlockSpec(shape, lambda p, *_: (0, 0))


def pair_block(height, rows):
    return pl.BlockSpec((height, rows), lambda p, *_: (p, 0))


def attend(own, ranges, query, key_value, terms, key_terms, begins, local_heads, so_far=()):
    rows = query.shape[0]
    pairs = local_heads // 2
    running_specs = [pair_block(LANES, rows), pair_block(8, rows)]
    running_shape = (
        jax.ShapeDtypeStruct((LANES * pairs, rows), f32),
        jax.ShapeDtypeStruct((8 * pairs, rows), f32),
    )
    final_specs = [lane_block(rows, 0), pair_block(8, rows)]
    final_shape = (
        jax.ShapeDtypeStruct((rows, pairs * LANES), bf16),
        jax.ShapeDtypeStruct((8 * pairs, rows), f32),
    )
    return pl.pallas_call(
        functools.partial(attend_kernel, local_heads, own),
        grid_spec=pltpu.PrefetchScalarGridSpec(
            num_scalar_prefetch=1,
            grid=(pairs,),
            in_specs=[
                lane_block(rows, 0),
                lane_block(rows, 0),
                lane_block(rows, pairs),
                fixed((rows, LANES)),
                fixed((rows, LANES) if own else (TERM_ROWS, rows)),
                fixed((8, rows)),
            ]
            + ([] if own else running_specs),
            out_specs=running_specs if own else final_specs,
            scratch_shapes=[
                pltpu.VMEM((rows, LANES), bf16),
                pltpu.VMEM((rows, LANES), bf16),
                pltpu.VMEM((LANES, rows), bf16),
                pltpu.VMEM((64, Q_TILE), f32),
                pltpu.VMEM((64, Q_TILE), f32),
            ],
        ),
        out_shape=running_shape if own else final_shape,
        cost_estimate=pl.CostEstimate(
            flops=40_000_000_000 if own else 10_000_000_000,
            transcendentals=20_000_000,
            bytes_accessed=12_000_000,
        ),
        name="attend_own" if own else "attend_prev",
    )(ranges, query, key_value, key_value, terms, key_terms, begins, *so_far)


def attend_back_kernel(local_heads, own, ranges_ref, q_ref, k_ref, v_ref, t_query_ref, t_key_ref,
                       begin_ref, grad_ref, o_ref, lse_ref, *refs):
    if own:
        dq_in_ref, decay_in_ref, dq_ref, dk_ref, dv_ref, decay_ref = refs[:6]
    else:
        dq_ref, row_decay_ref, dkv_ref, decay_ref = refs[:4]
        dk_ref, dv_ref = dkv_ref.at[0], dkv_ref.at[1]
    key0, key1, key_t0, key_t1, dk0, dk1, dv, dq0, dq1 = refs[-9:]
    pair = pl.program_id(0)
    rows = q_ref.shape[0]
    base = rows if own else 0
    keys, keys_t, dks, dqs = (key0, key1), (key_t0, key_t1), (dk0, dk1), (dq0, dq1)
    first, _ = key_range(ranges_ref, 0, rows, own)
    fill_keys(pair, local_heads, own, first, k_ref, t_key_ref, keys)

    def turn(n, carry):
        here = tile_of(n, K_TILE)
        for h in range(2):
            keys_t[h][:, here] = keys[h][here, :].T
        return carry

    lax.fori_loop(first, rows // K_TILE, turn, 0)
    for ref in (dk0, dk1, dv):
        ref[...] = jnp.zeros_like(ref)
    place = placing(pair, local_heads, QUERY)
    lane = lax.broadcasted_iota(jnp.int32, (Q_TILE, LANES), 1)
    pick_row = lax.broadcasted_iota(jnp.int32, (8, LANES), 0)
    pick_lane = lax.broadcasted_iota(jnp.int32, (8, LANES), 1)
    pick = jnp.where((pick_lane // 64) == pick_row, 1.0, 0.0)
    sums_ref = decay_ref if own else row_decay_ref

    @pl.when(pair == 0)
    def _():
        if own:
            decay_ref[...] = decay_in_ref[...]
        else:
            decay_ref[...] = jnp.zeros_like(decay_ref)
            row_decay_ref[...] = jnp.zeros_like(row_decay_ref)

    def query_tile(tile):
        here = tile_of(tile, Q_TILE)
        queries = query_tiles(q_ref, t_query_ref, place, here, 64**-0.5)
        begin_row = begin_ref[0:1, here]
        grad = grad_ref[here, :]
        nothing = jnp.zeros_like(grad)
        grads = (jnp.where(lane < 64, grad, nothing), jnp.where(lane < 64, nothing, grad))
        product = grad.astype(f32) * o_ref[here, :].astype(f32)
        inner = dot(pick, product, NT, precision=lax.Precision.HIGHEST)
        for dq in dqs:
            dq[...] = jnp.zeros_like(dq)

        def step(masked, number, state):
            there = tile_of(number, K_TILE)
            if masked:
                allowed = allowed_pairs(base + number * K_TILE, tile, rows, begin_row)
            value = v_ref[there, :]
            value_part = 0.0
            for h in range(2):
                scores = dot(keys[h][there, :], queries[h], NT)
                prob = jnp.exp(scores - lse_ref[h : h + 1, here])
                if masked:
                    prob = jnp.where(allowed, prob, 0.0)
                grad_prob = dot(value, grads[h], NT)
                grad_score = (prob * (grad_prob - inner[h : h + 1, :])).astype(bf16)
                value_part = value_part + dot(prob.astype(bf16), grads[h])
                dks[h][there, :] += dot(grad_score, queries[h])
                dqs[h][...] += dot(keys_t[h][:, there], grad_score)
            dv[there, :] += value_part
            return state

        key_loops(ranges_ref, tile, rows, own, step, 0)
        turned = [dq[...].T for dq in dqs]
        dq_tile = jnp.where(lane < 64, turned[0], turned[1]) * 64**-0.5
        if own:
            dq_tile = dq_tile + dq_in_ref[here, :]
        dq_ref[here, :] = dq_tile.astype(dq_ref.dtype)
        sums = sums_ref[here, :]
        sums = sums + jnp.where(lane == 2 * pair, turned[0][:, 64:65], 0.0)
        sums = sums + jnp.where(lane == 2 * pair + 1, turned[1][:, 0:1], 0.0)
        sums_ref[here, :] = sums

    def query_loop(tile, carry):
        if own:
            query_tile(tile)
        else:
            reaches = key_range(ranges_ref, tile, rows, own)[0] < rows // K_TILE
            pl.when(reaches)(lambda: query_tile(tile))

            @pl.when(jnp.logical_not(reaches))
            def _():
                dq_ref[tile_of(tile, Q_TILE), :] = jnp.zeros((Q_TILE, LANES), dq_ref.dtype)

        return carry

    lax.fori_loop(0, rows // Q_TILE, query_loop, 0)
    sign = -1.0 if own else 1.0

    def finish(n, carry):
        here = tile_of(n, Q_TILE)
        left, right = dk0[here, :], dk1[here, :]
        dk_ref[here, :] = jnp.where(lane < 64, left, right).astype(dk_ref.dtype)
        dv_ref[here, :] = dv[here, :].astype(dv_ref.dtype)
        decay = decay_ref[here, :]
        decay = decay + jnp.where(lane == 2 * pair, sign * left[:, 67:68], 0.0)
        decay = decay + jnp.where(lane == 2 * pair + 1, sign * right[:, 3:4], 0.0)
        decay_ref[here, :] = decay
        return carry

    lax.fori_loop(0, rows // Q_TILE, finish, 0)


def attend_back(
    own, ranges, query, key_value, terms, key_terms, begins, grad, mixed, lse, local_heads,
    so_far=(),
):
    rows = query.shape[0]
    pairs = local_heads // 2
    wide = jax.ShapeDtypeStruct((rows, pairs * LANES), f32)
    sums = jax.ShapeDtypeStruct((rows, LANES), f32)
    if own:
        out_specs = [lane_block(rows, 0)] * 3 + [fixed((rows, LANES))]
        out_shape = (jax.ShapeDtypeStruct(wide.shape, bf16), wide, wide, sums)
    else:
        both = pl.BlockSpec((2, rows, LANES), lambda p, *_: (0, 0, p))
        out_specs = [lane_block(rows, 0), fixed((rows, LANES)), both, fixed((rows, LANES))]
        out_shape = (
            wide, sums, jax.ShapeDtypeStruct((2, rows, pairs * LANES), bf16), sums,
        )
    return pl.pallas_call(
        functools.partial(attend_back_kernel, local_heads, own),
        grid_spec=pltpu.PrefetchScalarGridSpec(
            num_scalar_prefetch=1,
            grid=(pairs,),
            in_specs=[
                lane_block(rows, 0),
                lane_block(rows, 0),
                lane_block(rows, pairs),
                fixed((rows, LANES)),
                fixed((rows, LANES) if own else (TERM_ROWS, rows)),
                fixed((8, rows)),
                lane_block(rows, 0),
                lane_block(rows, 0),
                pair_block(8, rows),
            ]
            + ([lane_block(rows, 0), fixed((rows, LANES))] if own else []),
            out_specs=out_specs,
            scratch_shapes=[
                pltpu.VMEM((rows, LANES), bf16),
                pltpu.VMEM((rows, LANES), bf16),
                pltpu.VMEM((LANES, rows), bf16),
                pltpu.VMEM((LANES, rows), bf16),
                pltpu.VMEM((rows, LANES), f32),
                pltpu.VMEM((rows, LANES), f32),
                pltpu.VMEM((rows, LANES), f32),
                pltpu.VMEM((LANES, Q_TILE), f32),
                pltpu.VMEM((LANES, Q_TILE), f32),
            ],
        ),
        out_shape=out_shape,
        cost_estimate=pl.CostEstimate(
            flops=80_000_000_000 if own else 15_000_000_000,
            transcendentals=20_000_000,
            bytes_accessed=25_000_000,
        ),
        name="attend_back_own" if own else "attend_back_prev",
    )(
        ranges, query, key_value, key_value, terms, key_terms, begins, grad, mixed, lse, *so_far
    )


PIECES = 4


def partners():
    me = lax.axis_index("head")
    near = me + 1 - 2 * (me % 2)
    far = (me + 2) % 4
    cross = (near + 2) % 4
    return me, near, far, cross


def signal(other):
    pl.semaphore_signal(
        pltpu.get_barrier_semaphore(), inc=1, device_id=other, device_id_type=pl.DeviceIdType.MESH
    )


def greet(others):
    for other in others:
        signal(other)
    pl.semaphore_wait(pltpu.get_barrier_semaphore(), len(others))


def remote(source, target, send, receive, other):
    return pltpu.make_async_remote_copy(
        src_ref=source,
        dst_ref=target,
        send_sem=send,
        recv_sem=receive,
        device_id=other,
        device_id_type=pl.DeviceIdType.MESH,
    )


def on_head(index):
    return {"head": index}


def on_blk(index):
    return {"blk": index}


def piece_at(ref, slot, piece, size):
    span = size // PIECES
    return ref.at[pl.ds(pl.multiple_of(slot * size + piece * span, span), span), :]


class Slots:
    def __init__(self, by_device):
        me, near, far, cross = partners()
        if by_device:
            self.own = self.sent_near = self.sent_far = me
            self.near, self.far, self.cross = near, far, cross
            self.passed = far
        else:
            self.own, self.sent_near, self.sent_far = 3, 2, 1
            self.near, self.far, self.cross = 2, 1, 0
            self.passed = 0


def spread_piece(source, all_ref, size, sems, piece, slots):
    me, near, far, _ = partners()
    far_send, far_recv, near_send, near_recv, _, _, own = sems
    copies = (
        remote(source, piece_at(all_ref, slots.sent_far, piece, size), far_send.at[piece],
               far_recv.at[piece], on_head(far)),
        remote(source, piece_at(all_ref, slots.sent_near, piece, size), near_send.at[piece],
               near_recv.at[piece], on_head(near)),
        pltpu.make_async_copy(source, piece_at(all_ref, slots.own, piece, size), own.at[piece]),
    )
    for copy in copies:
        copy.start()
    return copies


def hand_on(all_ref, size, sems, sent, slots):
    me, near, far, cross = partners()
    far_send, far_recv, near_send, near_recv, on_send, on_recv, own = sems
    passed = []
    for piece in range(PIECES):
        there = piece_at(all_ref, slots.far, piece, size)
        remote(there, there, far_send.at[piece], far_recv.at[piece], on_head(far)).wait_recv()
        copy = remote(
            there, piece_at(all_ref, slots.passed, piece, size), on_send.at[piece],
            on_recv.at[piece], on_head(near),
        )
        copy.start()
        passed.append(copy)

    def finish():
        for piece in range(PIECES):
            to_far, to_near, local = sent[piece]
            to_far.wait_send()
            to_near.wait_send()
            local.wait()
            passed[piece].wait_send()
            there = piece_at(all_ref, slots.near, piece, size)
            remote(there, there, near_send.at[piece], near_recv.at[piece], on_head(near)).wait_recv()
            there = piece_at(all_ref, slots.cross, piece, size)
            remote(there, there, on_send.at[piece], on_recv.at[piece], on_head(near)).wait_recv()

    return finish


def gather_sems():
    return [pltpu.SemaphoreType.DMA((PIECES,)) for _ in range(7)]


def blk_peers():
    here = lax.axis_index("blk")
    half = lax.axis_size("blk") // 2
    low, high = here % 2, here // 2
    partner = here + 1 - 2 * low
    after = [((high + t) % half) * 2 + low for t in range(half)]
    return here, partner, after


class Line:
    def __init__(self, block_of, kinds, sems):
        self.block_of, self.kinds = block_of, kinds
        self.pair_send, self.pair_recv, self.up_send, self.up_recv, self.down_send, self.down_recv = sems
        here = lax.axis_index("blk")
        self.half = lax.axis_size("blk") // 2
        self.low, self.high = here % 2, here // 2
        self.partner = here + 1 - 2 * self.low
        self.has_up, self.has_down = self.high < self.half - 1, self.high > 0

    def greet(self, others):
        greet_sum = len(others) + 1
        for other in others + [on_blk(self.partner)]:
            signal(other)
        pl.when(self.has_up)(lambda: signal(on_blk(self.at(self.high + 1))))
        pl.when(self.has_down)(lambda: signal(on_blk(self.at(self.high - 1))))
        ends = (self.high == 0).astype(jnp.int32) + (self.high == self.half - 1).astype(jnp.int32)
        pl.semaphore_wait(pltpu.get_barrier_semaphore(), greet_sum + 2 - ends)

    def at(self, high):
        return high * 2 + self.low

    def pair_copy(self, kind, high, low):
        block = self.block_of(kind, high * 2 + low)
        return remote(
            block, block, self.pair_send.at[kind, high], self.pair_recv.at[kind, high],
            on_blk(self.partner),
        )

    def up_copy(self, kind, high):
        block = self.block_of(kind, self.at(high))
        return remote(
            block, block, self.up_send.at[kind, high], self.up_recv.at[kind, high],
            on_blk(self.at(jnp.minimum(self.high + 1, self.half - 1))),
        )

    def down_copy(self, kind, high):
        block = self.block_of(kind, self.at(high))
        return remote(
            block, block, self.down_send.at[kind, high], self.down_recv.at[kind, high],
            on_blk(self.at(jnp.maximum(self.high - 1, 0))),
        )

    def launch(self, kind):
        self.pair_copy(kind, self.high, self.low).start()
        pl.when(self.has_up)(lambda: self.up_copy(kind, self.high).start())
        pl.when(self.has_down)(lambda: self.down_copy(kind, self.high).start())

    def step(self, t):
        for kind in range(self.kinds):
            below, above = self.high - t, self.high + t

            @pl.when(below >= 0)
            def _():
                self.up_copy(kind, below).wait_recv()
                self.pair_copy(kind, below, self.low).start()
                pl.when(self.has_up)(lambda: self.up_copy(kind, below).start())

            @pl.when(above < self.half)
            def _():
                self.down_copy(kind, above).wait_recv()
                self.pair_copy(kind, above, self.low).start()
                pl.when(self.has_down)(lambda: self.down_copy(kind, above).start())

    def finish(self):
        for kind in range(self.kinds):

            def wait(high, carry):
                self.pair_copy(kind, high, self.low).wait_send()
                self.pair_copy(kind, high, 1 - self.low).wait_recv()

                @pl.when((high <= self.high) & self.has_up)
                def _():
                    self.up_copy(kind, high).wait_send()

                @pl.when((high >= self.high) & self.has_down)
                def _():
                    self.down_copy(kind, high).wait_send()

                return carry

            lax.fori_loop(0, self.half, wait, 0)


def gather_first_kernel(pack_ref, tokens_ref, cotangent_ref, pack_all, tokens_all, cotangent_all,
                        *sems):
    swap_send, swap_recv, swap_own = sems[:3]
    token_sems, cotangent_sems = sems[9:16], sems[16:23]
    me, near, far, cross = partners()
    sources = (me, near, far, cross)
    line = Line(lambda kind, blk: pack_all.at[blk, sources[kind]], 4, sems[3:9])
    here = lax.axis_index("blk")
    line.greet([on_head(near), on_head(far), on_head(cross)])
    swaps = [pltpu.make_async_copy(pack_ref.at[me], pack_all.at[here, me], swap_own)]
    for kind, other in enumerate((near, far, cross)):
        swaps.append(
            remote(
                pack_ref.at[other],
                pack_all.at[here, me],
                swap_send.at[kind],
                swap_recv.at[kind],
                on_head(other),
            )
        )
    for swap in swaps:
        swap.start()
    size = tokens_ref.shape[0]
    span = size // PIECES

    def spread_all(ref, all_ref, some, slots):
        return [
            spread_piece(ref.at[pl.ds(piece * span, span), :], all_ref, size, some, piece, slots)
            for piece in range(PIECES)
        ]

    by_device, crossing = Slots(True), Slots(False)
    tokens_sent = spread_all(tokens_ref, tokens_all, token_sems, by_device)
    swaps[0].wait()
    line.launch(0)
    for kind, source in enumerate((near, far, cross)):
        block = pack_all.at[here, source]
        remote(
            block, block, swap_send.at[kind], swap_recv.at[kind], on_head(source)
        ).wait_recv()
        line.launch(kind + 1)
    cotangent_sent = spread_all(cotangent_ref, cotangent_all, cotangent_sems, crossing)
    for t in range(1, line.half):
        line.step(t)
    finish_tokens = hand_on(tokens_all, size, token_sems, tokens_sent, by_device)
    finish_cotangent = hand_on(cotangent_all, size, cotangent_sems, cotangent_sent, crossing)
    for swap in swaps[1:]:
        swap.wait_send()
    line.finish()
    finish_tokens()
    finish_cotangent()


def gather_first(pack, tokens, cotangent, number):
    groups, share, columns = pack.shape
    peers = lax.axis_size("blk")
    rows, width = tokens.shape
    whole = jax.ShapeDtypeStruct((groups * rows, width), bf16)
    vmem, anywhere = pl.BlockSpec(memory_space=pltpu.VMEM), pl.BlockSpec(memory_space=pl.ANY)
    all_pack, all_tokens, all_cotangent = pl.pallas_call(
        gather_first_kernel,
        in_specs=[vmem] * 3,
        out_specs=[anywhere] * 3,
        out_shape=[jax.ShapeDtypeStruct((peers, groups, share, columns), bf16), whole, whole],
        scratch_shapes=[
            pltpu.SemaphoreType.DMA((3,)),
            pltpu.SemaphoreType.DMA((3,)),
            pltpu.SemaphoreType.DMA,
        ]
        + [pltpu.SemaphoreType.DMA((4, peers // 2)) for _ in range(6)]
        + gather_sems()
        + gather_sems(),
        compiler_params=pltpu.CompilerParams(collective_id=number, has_side_effects=True),
        cost_estimate=pl.CostEstimate(
            flops=70_000_000_000, transcendentals=0, bytes_accessed=30_000_000
        ),
        name="gather_first",
    )(pack, tokens, cotangent)
    return all_pack.reshape(peers * groups * share, columns), all_tokens, all_cotangent


class Sum:
    def __init__(self, part_ref, buffers, sems, size, by_device):
        self.part_ref, self.size, self.span = part_ref, size, size // PIECES
        self.slots = Slots(by_device)
        self.near_buf, self.turn_buf, self.far_buf = buffers
        self.near_send, self.near_recv, self.far_send, self.far_recv = sems
        self.near_copies, self.far_copies = [], []

    def piece(self, n):
        return slice(n * self.span, (n + 1) * self.span)

    def start(self):
        me, near, far, cross = partners()
        for which, shard in ((0, self.slots.cross), (1, self.slots.near)):
            for n in range(PIECES):
                copy = remote(
                    piece_at(self.part_ref, shard, n, self.size),
                    self.near_buf.at[which, pl.ds(n * self.span, self.span), :],
                    self.near_send.at[which, n],
                    self.near_recv.at[which, n],
                    on_head(near),
                )
                copy.start()
                self.near_copies.append(copy)

    def turn(self):
        me, near, far, cross = partners()
        for n in range(PIECES):
            here = self.piece(n)
            self.near_copies[n].wait_recv()
            self.turn_buf[here, :] = (
                piece_at(self.part_ref, self.slots.far, n, self.size)[...].astype(f32)
                + self.near_buf[0, here, :].astype(f32)
            ).astype(bf16)
            copy = remote(
                self.turn_buf.at[pl.ds(n * self.span, self.span), :],
                self.far_buf.at[pl.ds(n * self.span, self.span), :],
                self.far_send.at[n],
                self.far_recv.at[n],
                on_head(far),
            )
            copy.start()
            self.far_copies.append(copy)

    def total(self, n):
        self.near_copies[PIECES + n].wait_recv()
        self.far_copies[n].wait_recv()
        here = self.piece(n)
        return (
            piece_at(self.part_ref, self.slots.own, n, self.size)[...].astype(f32)
            + self.near_buf[1, here, :].astype(f32)
            + self.far_buf[here, :].astype(f32)
        )

    def finish(self):
        for copy in self.near_copies + self.far_copies:
            copy.wait_send()


def sum_buffers(size, width):
    return [
        pltpu.VMEM((2, size, width), bf16),
        pltpu.VMEM((size, width), bf16),
        pltpu.VMEM((size, width), bf16),
    ]


def sum_sems():
    return [
        pltpu.SemaphoreType.DMA((2, PIECES)),
        pltpu.SemaphoreType.DMA((2, PIECES)),
        pltpu.SemaphoreType.DMA((PIECES,)),
        pltpu.SemaphoreType.DMA((PIECES,)),
    ]


def exchange_kernel(local, extras, summed, weights, *refs):
    part_ref, extra_refs = refs[0], refs[1 : 1 + extras]
    refs = refs[1 + extras :]
    if weights:
        mine_ref, refs = refs[0], refs[1:]
    out_ref, all_ref, refs = refs[0], refs[1], refs[2:]
    if weights:
        weight_ref, refs = refs[0], refs[1:]
    payload, sems = refs[0], refs[1:]
    size = out_ref.shape[0]
    span = size // PIECES
    _, near, far, _ = partners()
    if weights:
        kinds = mine_ref.shape[0]
        line = Line(lambda kind, blk: weight_ref.at[blk, kind], kinds, sems[-7:-1])
        own = pltpu.make_async_copy(mine_ref, weight_ref.at[lax.axis_index("blk")], sems[-1])
        own.start()
        line.greet([on_head(near), on_head(far)])
    else:
        greet([on_head(near), on_head(far)])
    slots = Slots(summed)
    if not summed:
        shares = Sum(part_ref, sems[7:10], sems[10:14], size, True)
        shares.start()
    if weights:
        own.wait()
        for kind in range(kinds):
            line.launch(kind)
    if not summed:
        shares.turn()
    sent = []
    for piece in range(PIECES):
        if weights and piece != 2:
            hop = {0: 1, 1: 2, 3: 3}[piece]
            for t in range(hop, line.half if piece == 3 else min(hop + 1, line.half)):
                line.step(t)
        here = slice(piece * span, (piece + 1) * span)
        total = part_ref[here, :] if summed else shares.total(piece)
        result, share = local(total, here, *extra_refs)
        out_ref[here, :] = result.astype(out_ref.dtype)
        payload[here, :] = share.astype(bf16)
        source = payload.at[pl.ds(piece * span, span), :]
        sent.append(spread_piece(source, all_ref, size, sems[:7], piece, slots))
    hand_on(all_ref, size, sems[:7], sent, slots)()
    if not summed:
        shares.finish()
    if weights:
        line.finish()


def exchange(local, part, extras, summed, number, name, mine=None):
    rows, width = part.shape
    size = rows if summed else rows // 4
    vmem, anywhere = pl.BlockSpec(memory_space=pltpu.VMEM), pl.BlockSpec(memory_space=pl.ANY)
    weights = mine is not None
    inputs = [part, *extras]
    out_specs = [vmem, anywhere]
    out_shape = [
        jax.ShapeDtypeStruct((size, width), f32),
        jax.ShapeDtypeStruct((4 * size, width), bf16),
    ]
    scratch = [pltpu.VMEM((size, width), bf16)] + gather_sems()
    if not summed:
        scratch += sum_buffers(size, width) + sum_sems()
    if weights:
        peers = lax.axis_size("blk")
        inputs.append(mine)
        out_specs.append(anywhere)
        out_shape.append(jax.ShapeDtypeStruct((peers,) + mine.shape, bf16))
        scratch += [pltpu.SemaphoreType.DMA((mine.shape[0], peers // 2)) for _ in range(6)]
        scratch.append(pltpu.SemaphoreType.DMA)
    return pl.pallas_call(
        functools.partial(exchange_kernel, local, len(extras), summed, weights),
        in_specs=[vmem] * len(inputs),
        out_specs=out_specs,
        out_shape=out_shape,
        scratch_shapes=scratch,
        compiler_params=pltpu.CompilerParams(collective_id=number, has_side_effects=True),
        cost_estimate=pl.CostEstimate(
            flops=40_000_000_000 if summed else 70_000_000_000,
            transcendentals=0,
            bytes_accessed=16_000_000,
        ),
        name=name,
    )(*inputs)


def column_chunks(width):
    count = max(width // 512, 1)
    first = width - 512 * (count - 1)
    return [(0, first)] + [(first + 512 * n, 512) for n in range(count - 1)]


def finish_last_kernel(grad_ref, output_grad_ref, second_ref, first_ref, down_ref, grad_middle_ref,
                       tokens_ref, gain_ref, middle_ref, weights_ref, output_ref, second_out_ref,
                       tokens_grad_ref, result_ref, *refs):
    buffers = (refs[0:3], refs[3:6])
    first_buffers, down_buffers = refs[6:9], refs[9:12]
    pair_send, pair_recv, line_send, line_recv, swap_send, swap_recv = refs[12:18]
    first_sems, down_sems = refs[18:22], refs[22:26]
    me, near, far, cross = partners()
    others = (near, far, cross)
    here, partner, after = blk_peers()
    steps = len(after)
    greet(
        [on_head(other) for other in others]
        + [on_blk(partner)]
        + [on_blk(peer) for peer in after[1:]]
    )
    size = result_ref.shape[0]
    first = Sum(first_ref, first_buffers, first_sems, size, True)
    down = Sum(down_ref, down_buffers, down_sems, size, False)
    chunks = []
    for ref, out_ref, some in (
        (grad_ref, weights_ref, buffers[0]), (output_grad_ref, output_ref, buffers[1])
    ):
        for start, wide in column_chunks(ref.shape[3]):
            chunks.append((ref, out_ref, some, pl.ds(start, wide)))
    groups = grad_ref.shape[1]
    first.start()
    sent = []
    for c, (ref, _, (pair_buf, _, _), at) in enumerate(chunks):
        for t in list(range(1, steps)) + [0]:
            copy = remote(
                ref.at[after[t] + partner - here, :, :, at],
                pair_buf.at[t, :, :, at],
                pair_send.at[c, t],
                pair_recv.at[c, t],
                on_blk(partner),
            )
            copy.start()
            sent.append(copy)
    first.turn()

    def swap(source_ref, out_ref, c):
        for kind, other in enumerate(others):
            copy = remote(
                source_ref.at[other], out_ref.at[me], swap_send.at[c, kind],
                swap_recv.at[c, kind], on_head(other),
            )
            copy.start()
            sent.append(copy)

    swap(second_ref, second_out_ref, len(chunks))
    down.start()
    down.turn()

    def add_up(c):
        ref, out_ref, (pair_buf, line_buf, row_buf), at = chunks[c]
        block = pair_buf.at[0, :, :, at]
        remote(block, block, pair_send.at[c, 0], pair_recv.at[c, 0], on_blk(partner)).wait_recv()
        for t in range(1, steps):
            block = line_buf.at[t, :, :, at]
            remote(
                block, block, line_send.at[c, t], line_recv.at[c, t], on_blk(after[t])
            ).wait_recv()

        def add_all(group, carry):
            total = ref[here, group, :, at].astype(f32) + pair_buf[0, group, :, at].astype(f32)
            for t in range(1, steps):
                total = total + line_buf[t, group, :, at].astype(f32)
            row_buf[group, :, at] = total.astype(bf16)
            return carry

        lax.fori_loop(0, groups, add_all, 0)
        out_ref[me, :, at] = row_buf[me, :, at]
        swap(row_buf.at[:, :, at], out_ref.at[:, :, at], c)

    def put(shares, local, out_ref, extra_refs):
        for piece in range(PIECES):
            rows = shares.piece(piece)
            value, _ = local(shares.total(piece), rows, *extra_refs)
            out_ref[rows, :] = value.astype(out_ref.dtype)

    for c, (ref, _, (pair_buf, line_buf, _), at) in enumerate(chunks):
        for t in range(1, steps):
            block = pair_buf.at[t, :, :, at]
            remote(
                block, block, pair_send.at[c, t], pair_recv.at[c, t], on_blk(partner)
            ).wait_recv()

            def add(group, carry):
                pair_buf[t, group, :, at] = (
                    ref[after[t], group, :, at].astype(f32)
                    + pair_buf[t, group, :, at].astype(f32)
                ).astype(bf16)
                return carry

            lax.fori_loop(0, groups, add, 0)
            copy = remote(
                block, line_buf.at[t, :, :, at], line_send.at[c, t], line_recv.at[c, t],
                on_blk(after[t]),
            )
            copy.start()
            sent.append(copy)
        if c > 0:
            add_up(c - 1)
    put(first, after_first, tokens_grad_ref, (grad_middle_ref, tokens_ref, gain_ref))
    add_up(len(chunks) - 1)
    put(down, after_down, result_ref, (middle_ref,))
    second_out_ref[me] = second_ref[me]
    for c in range(len(chunks) + 1):
        if c < len(chunks):
            _, out_ref, _, at = chunks[c]
            out_ref = out_ref.at[:, :, at]
        else:
            out_ref = second_out_ref
        for kind, other in enumerate(others):
            block = out_ref.at[other]
            remote(
                block, block, swap_send.at[c, kind], swap_recv.at[c, kind], on_head(other)
            ).wait_recv()
    for copy in sent:
        copy.wait_send()
    first.finish()
    down.finish()


def finish_last(grad, output_grad, second, groups, part_first, part_down, grad_middle, tokens, gain,
                middle, number):
    peers = lax.axis_size("blk")
    share = grad.shape[0] // (peers * groups)
    rows, width = tokens.shape
    vmem = pl.BlockSpec(memory_space=pltpu.VMEM)
    half = peers // 2
    widths = (grad.shape[1], output_grad.shape[1])
    chunks = sum(len(column_chunks(width)) for width in widths)

    def blocks(columns):
        return [pltpu.VMEM((half, groups, share, columns), bf16) for _ in range(2)] + [
            pltpu.VMEM((groups, share, columns), bf16)
        ]

    return pl.pallas_call(
        finish_last_kernel,
        in_specs=[vmem] * 9,
        out_specs=[vmem] * 5,
        out_shape=[
            jax.ShapeDtypeStruct((groups, share, columns), bf16)
            for columns in widths + (second.shape[1],)
        ]
        + [
            jax.ShapeDtypeStruct((rows, width), f32),
            jax.ShapeDtypeStruct((rows, width), bf16),
        ],
        scratch_shapes=blocks(widths[0])
        + blocks(widths[1])
        + sum_buffers(rows, width)
        + sum_buffers(rows, width)
        + [pltpu.SemaphoreType.DMA((chunks, half)) for _ in range(4)]
        + [pltpu.SemaphoreType.DMA((chunks + 1, 3)) for _ in range(2)]
        + sum_sems()
        + sum_sems(),
        compiler_params=pltpu.CompilerParams(
            collective_id=number, has_side_effects=True, vmem_limit_bytes=60 << 20
        ),
        cost_estimate=pl.CostEstimate(
            flops=80_000_000_000, transcendentals=0, bytes_accessed=40_000_000
        ),
        name="finish_last",
    )(
        grad.reshape(peers, groups, share, widths[0]),
        output_grad.reshape(peers, groups, share, widths[1]),
        second.reshape(groups, share, second.shape[1]),
        part_first, part_down, grad_middle, tokens, gain, middle,
    )


def inverse_rms(value):
    return lax.rsqrt(jnp.mean(value * value, axis=1, keepdims=True) + epsilon)


def through_norm(grad, value):
    factor = inverse_rms(value)
    normed = value * factor
    return factor * (grad - normed * jnp.mean(grad * normed, axis=1, keepdims=True))


def after_attention(total, here, tokens_ref, gain_ref):
    middle = tokens_ref[here, :].astype(f32) + total
    return middle, middle * inverse_rms(middle) * gain_ref[0:1, :]


def after_hidden(total, here, cotangent_ref, middle_ref, gain_ref):
    grad = cotangent_ref[here, :].astype(f32) + through_norm(
        total * gain_ref[0:1, :], middle_ref[here, :]
    )
    return grad, grad


def after_first(total, here, grad_ref, tokens_ref, gain_ref):
    grad = grad_ref[here, :] + through_norm(
        total * gain_ref[0:1, :], tokens_ref[here, :].astype(f32)
    )
    return grad, None


def after_down(total, here, middle_ref):
    return middle_ref[here, :] + total, None


FEED_TILE = 256
FEED_COLUMNS = 512


def feed_kernel(input_ref, cotangent_ref, weight_ref, down_weight_ref, down_ref, grad_ref, total_ref,
                acts, turned0, turned1, stage, near_buf, far_buf, near_send, near_recv, far_send, far_recv):
    step = pl.program_id(0)
    hidden_width = down_weight_ref.shape[1]
    size = total_ref.shape[0]
    per = size // FEED_TILE
    tiles = 4 * per
    _, near, far, _ = partners()

    @pl.when(step == 0)
    def _():
        greet([on_head(near), on_head(far)])

    def to_near(which, piece):
        return remote(
            stage.at[which * per + piece],
            near_buf.at[which, piece],
            near_send.at[which, piece],
            near_recv.at[which, piece],
            on_head(near),
        )

    def to_far(piece):
        return remote(
            near_buf.at[0, piece], far_buf.at[piece], far_send.at[piece], far_recv.at[piece],
            on_head(far),
        )

    @pl.when(step < tiles)
    def _():
        here = tile_of(step, FEED_TILE)
        inputs, cotangent = input_ref[...], cotangent_ref[...]
        turned0[:, here] = inputs.T
        turned1[:, here] = cotangent.T
        gate_at, up_at, down_at = (
            slice(n * hidden_width, (n + 1) * hidden_width) for n in range(3)
        )
        gate = dot(inputs, weight_ref[:, gate_at])
        up = dot(inputs, weight_ref[:, up_at])
        grad_hidden = dot(cotangent, down_weight_ref[...])
        opening = jax.nn.sigmoid(gate)
        active = gate * opening
        hidden = (active * up).astype(bf16)
        grad_gate = (grad_hidden * up * opening * (1.0 + gate * (1.0 - opening))).astype(bf16)
        grad_up = (grad_hidden * active).astype(bf16)
        acts[here, gate_at] = grad_gate
        acts[here, up_at] = grad_up
        acts[here, down_at] = hidden
        down_ref[...] = dot(hidden, down_weight_ref[...], NT).astype(bf16)
        back = dot(grad_gate, weight_ref[:, gate_at], NT) + dot(
            grad_up, weight_ref[:, up_at], NT
        )
        for piece in range(per):
            for which, first in ((0, 0), (1, 2 * per)):

                @pl.when(step == first + piece)
                def _():
                    stage[which * per + piece] = back.astype(bf16)
                    to_near(which, piece).start()

            @pl.when(step == per + piece)
            def _():
                to_near(0, piece).wait_recv()
                near_buf[0, piece] = (back + near_buf[0, piece].astype(f32)).astype(bf16)
                to_far(piece).start()

            @pl.when(step == 3 * per + piece)
            def _():
                total_ref[piece * FEED_TILE : (piece + 1) * FEED_TILE, :] = back

    @pl.when(step >= tiles)
    def _():
        at = tile_of(step - tiles, FEED_COLUMNS)
        from_input = (step - tiles) * FEED_COLUMNS < 2 * hidden_width

        @pl.when(from_input)
        def _():
            grad_ref[...] = dot(turned0[...], acts[:, at]).astype(bf16)

        @pl.when(jnp.logical_not(from_input))
        def _():
            grad_ref[...] = dot(turned1[...], acts[:, at]).astype(bf16)

    @pl.when(step == pl.num_programs(0) - 1)
    def _():
        for piece in range(per):
            here = slice(piece * FEED_TILE, (piece + 1) * FEED_TILE)
            to_near(1, piece).wait_recv()
            to_far(piece).wait_recv()
            total_ref[here, :] += near_buf[1, piece].astype(f32) + far_buf[piece].astype(f32)
            to_near(0, piece).wait_send()
            to_near(1, piece).wait_send()
            to_far(piece).wait_send()


def feed(inputs, cotangent, weight, down_weight, number):
    rows, width = inputs.shape
    columns = weight.shape[1] + down_weight.shape[1]
    size = rows // 4
    tiles, per = rows // FEED_TILE, size // FEED_TILE
    tile = pl.BlockSpec((FEED_TILE, width), lambda n: (jnp.minimum(n, tiles - 1), 0))

    def whole(shape):
        return pl.BlockSpec(shape, lambda n: (0, 0), pipeline_mode=pl.Buffered(1))

    return pl.pallas_call(
        feed_kernel,
        grid=(tiles + columns // FEED_COLUMNS,),
        in_specs=[tile, tile, whole(weight.shape), whole(down_weight.shape)],
        out_specs=[
            tile,
            pl.BlockSpec((width, FEED_COLUMNS), lambda n: (0, jnp.maximum(n - tiles, 0))),
            whole((size, width)),
        ],
        out_shape=[
            jax.ShapeDtypeStruct((rows, width), bf16),
            jax.ShapeDtypeStruct((width, columns), bf16),
            jax.ShapeDtypeStruct((size, width), f32),
        ],
        scratch_shapes=[
            pltpu.VMEM((rows, columns), bf16),
            pltpu.VMEM((width, rows), bf16),
            pltpu.VMEM((width, rows), bf16),
            pltpu.VMEM((2 * per, FEED_TILE, width), bf16),
            pltpu.VMEM((2, per, FEED_TILE, width), bf16),
            pltpu.VMEM((per, FEED_TILE, width), bf16),
            pltpu.SemaphoreType.DMA((2, per)),
            pltpu.SemaphoreType.DMA((2, per)),
            pltpu.SemaphoreType.DMA((per,)),
            pltpu.SemaphoreType.DMA((per,)),
        ],
        compiler_params=pltpu.CompilerParams(
            collective_id=number, has_side_effects=True, vmem_limit_bytes=63 << 20
        ),
        cost_estimate=pl.CostEstimate(
            flops=6 * rows * width * columns, transcendentals=rows * columns // 3,
            bytes_accessed=45_000_000,
        ),
        name="feed",
    )(inputs, cotangent, weight, down_weight)


def over_tokens(operand, other_side):
    return lax.dot_general(
        operand, other_side, (((0,), (0,)), ((), ())), preferred_element_type=f32
    )


def sent_columns(pieces, groups):
    packed = jnp.concatenate(
        [piece.reshape(piece.shape[0], groups, -1) for piece in pieces], axis=2
    )
    mine = lax.all_to_all(packed, "head", split_axis=1, concat_axis=0, tiled=True)
    return mine.reshape(mine.shape[0], mine.shape[2])


def all_rows(mine):
    return lax.all_gather(mine, "blk", axis=0, tiled=True)


def row_sums(grad):
    return lax.psum_scatter(grad, "blk", scatter_dimension=0, tiled=True)


def body(
    tokens,
    segment,
    norm1_gain,
    w_query,
    w_key,
    w_value,
    w_gate_out,
    w_forget,
    forget_bias,
    w_output,
    norm2_gain,
    w_gate,
    w_up,
    w_down,
    cotangent,
):
    token_rows, model_width = tokens.shape
    groups = lax.axis_size("head")
    head_count = forget_bias.shape[0]
    local_heads = head_count // groups
    local_width = model_width // groups
    hidden_width = w_gate.shape[1] // groups
    rows = token_rows * groups
    share = w_query.shape[0]
    group = lax.axis_index("head")

    low = lambda array: array.astype(bf16)
    spread = lambda gain: jnp.broadcast_to(low(gain)[:, None, None], (share, groups, 1))
    forget_low = low(w_forget).reshape(share, groups, local_heads)
    rest = LANES - local_heads - 2
    small = jnp.concatenate(
        [forget_low, spread(norm1_gain), spread(norm2_gain), jnp.zeros((share, groups, rest), bf16)],
        axis=2,
    )
    pack = jnp.concatenate(
        [
            low(piece).reshape(share, groups, -1)
            for piece in (w_key, w_value, small, w_query, w_gate_out, w_output)
        ],
        axis=2,
    )
    first, tokens_all, cotangent_all = gather_first(
        jnp.swapaxes(pack, 0, 1), tokens, cotangent, 0
    )
    kv_width = 2 * local_width + LANES
    output_weight = first[:, kv_width + 2 * local_width :]

    segment_plus = segment + 1
    earlier_segment = passed_along(segment_plus, "blk", 1)
    window = jnp.concatenate([earlier_segment, segment_plus])
    begins = jnp.sum(
        (window[:, None] < segment_plus[None, :]).astype(jnp.int32), axis=0
    )
    tiles = begins.reshape(rows // Q_TILE, Q_TILE)
    ranges = jnp.stack([tiles[:, 0] // K_TILE, (tiles[:, -1] + K_TILE - 1) // K_TILE])
    begins = jnp.broadcast_to(begins[None, :], (8, rows))

    def gain_rows(column):
        gain = first[:, 2 * local_width + local_heads + column].astype(f32)
        return jnp.broadcast_to(gain[None, :], (8, model_width))

    gain1, gain2 = gain_rows(0), gain_rows(1)
    bias = lax.dynamic_slice_in_dim(forget_bias, group * local_heads, local_heads, 0)
    bias = jnp.broadcast_to(jnp.pad(bias, (0, LANES - local_heads))[None, :], (8, LANES))
    input1, key_value, terms, turned_terms, forget = project(
        tokens_all, gain1, first, bias, 2 * local_width, local_heads
    )
    earlier_kv = passed_along(key_value, "blk", 1)
    earlier_terms = passed_along(turned_terms, "blk", 1)
    query = dot(input1, first[:, kv_width : kv_width + local_width]).astype(bf16)
    gate_raw = dot(
        input1, first[:, kv_width + local_width : kv_width + 2 * local_width]
    )

    so_far = attend(True, ranges, query, key_value, terms, terms, begins, local_heads)
    later = lax.optimization_barrier((low(w_gate), low(w_up), low(w_down), key_value))
    mine = sent_columns(later[:3], groups)
    mine, earlier_kv, earlier_terms, so_far = lax.optimization_barrier(
        (mine, earlier_kv, earlier_terms, so_far)
    )
    second = all_rows(mine[:, : 2 * hidden_width])
    mine_down = mine[:, 2 * hidden_width :].reshape(groups, share, hidden_width)
    attended, lse = attend(
        False, ranges, query, earlier_kv, terms, earlier_terms, begins, local_heads, so_far
    )
    opened = jax.nn.sigmoid(gate_raw)
    attended_wide = attended.astype(f32)
    gated = (opened * attended_wide).astype(bf16)
    branch = dot(gated, output_weight, NT).astype(bf16)
    middle, input2, down_weight = exchange(
        after_attention, branch, [tokens, gain2], False, 1, "exchange_middle", mine_down
    )
    down_weight = down_weight.reshape(model_width, hidden_width)
    down, second_grad, grad_input2 = feed(input2, cotangent_all, second, down_weight, 4)
    second_part = row_sums(second_grad)
    grad_middle, grad_branch = exchange(
        after_hidden, grad_input2, [cotangent, middle, gain2], True, 2, "exchange_hidden"
    )

    grad_gated = dot(grad_branch, output_weight)
    grad_attended = (grad_gated * opened).astype(bf16)
    grad_gate_pre = (grad_gated * attended_wide * opened * (1.0 - opened)).astype(bf16)
    dq_prev, rows_prev, dkv_prev, decay_prev = attend_back(
        False, ranges, query, earlier_kv, terms, earlier_terms, begins, grad_attended, attended,
        lse, local_heads,
    )
    dkv_later = passed_along(dkv_prev, "blk", -1)
    decay_later = passed_along(decay_prev[:, :8], "blk", -1)
    decay_later = jnp.pad(decay_later, ((0, 0), (0, LANES - 8)))
    dq, dk_own, dv_own, decay_own = attend_back(
        True, ranges, query, key_value, terms, terms, begins, grad_attended, attended,
        lse, local_heads, (dq_prev, rows_prev),
    )
    dk = (dk_own + dkv_later[0].astype(f32)).astype(bf16)
    dv = (dv_own + dkv_later[1].astype(f32)).astype(bf16)
    logf_grad = decay_back(decay_own, decay_later)
    forget_grad = jnp.where(
        jnp.arange(LANES)[None, :] < local_heads, logf_grad * jax.nn.sigmoid(-forget), 0.0
    ).astype(bf16)
    grads = jnp.concatenate([dk, dv, forget_grad, dq, grad_gate_pre], axis=1)
    first_grad = over_tokens(input1, grads)
    bias_part = jnp.sum(forget_grad.astype(f32), axis=0)
    row = jnp.arange(model_width)[:, None] % share
    column = jnp.arange(kv_width + 2 * local_width)[None, :]
    spread_bias = jnp.sum(
        jnp.where(row == jnp.arange(LANES)[None, :], bias_part[None, :], 0.0), axis=1, keepdims=True
    )
    first_grad = jnp.where(
        column == 2 * local_width + local_heads, spread_bias, first_grad
    ).astype(bf16)
    output_grad = over_tokens(grad_branch, gated).astype(bf16)
    grad_input1 = dot(grads, first[:, : kv_width + 2 * local_width], NT).astype(bf16)
    first_sum, output_sum, second_sum, tokens_grad, result = finish_last(
        first_grad, output_grad, second_part, groups, grad_input1, down, grad_middle, tokens,
        gain1, middle, 3,
    )
    first_sum, output_sum, second_sum = (
        jnp.swapaxes(array, 0, 1).astype(f32) for array in (first_sum, output_sum, second_sum)
    )

    def columns(array, start, width):
        return array[:, :, start : start + width].reshape(share, groups * width)

    key_sum, value_sum = (columns(first_sum, n * local_width, local_width) for n in range(2))
    forget_sum = columns(first_sum, 2 * local_width, local_heads)
    bias_total = first_sum[:local_heads, :, 2 * local_width + local_heads].T.reshape(head_count)
    query_sum, gate_out_sum = (
        columns(first_sum, kv_width + n * local_width, local_width) for n in range(2)
    )
    output_total = columns(output_sum, 0, local_width)
    gate_sum, up_sum, down_sum = (
        columns(second_sum, n * hidden_width, hidden_width) for n in range(3)
    )

    def along(weight, grad):
        return jnp.sum(low(weight).astype(f32) * grad, axis=1)

    gain1_total = (
        along(w_query, query_sum)
        + along(w_key, key_sum)
        + along(w_value, value_sum)
        + along(w_gate_out, gate_out_sum)
        + along(w_forget, forget_sum)
    ) / low(norm1_gain).astype(f32)
    gain2_total = (along(w_gate, gate_sum) + along(w_up, up_sum)) / low(norm2_gain).astype(f32)
    return (
        result,
        tokens_grad,
        gain1_total,
        query_sum,
        key_sum,
        value_sum,
        gate_out_sum,
        forget_sum,
        bias_total,
        output_total,
        gain2_total,
        gate_sum,
        up_sum,
        down_sum,
    )


def solution(mesh):
    both = ("blk", "head")
    matrix, vector = P(both, None), P(both)
    return jax.shard_map(
        body,
        mesh=mesh,
        in_specs=(
            matrix, P("blk"), vector, matrix, matrix, matrix, matrix, matrix, P(), matrix, vector,
            matrix, matrix, matrix, matrix,
        ),
        out_specs=(
            matrix, matrix, vector, matrix, matrix, matrix, matrix, matrix, P(), matrix, vector,
            matrix, matrix, matrix,
        ),
        check_vma=False,
    )
```

```python
import functools

import jax
import jax.numpy as jnp
from jax import lax
from jax.experimental import pallas as pl
from jax.experimental.pallas import tpu as pltpu
from jax.sharding import PartitionSpec as P

epsilon = 1e-06
LANES = 128
Q_TILE = 512
K_TILE = 512
FAR = -1e30
NT = (((1,), (1,)), ((), ()))
NN = (((1,), (0,)), ((), ()))
bf16 = jnp.bfloat16
f32 = jnp.float32


def dot(a, b, dims=NN, **kw):
    return lax.dot_general(a, b, dims, preferred_element_type=f32, **kw)


def passed_along(array, axis, by):
    peers = lax.axis_size(axis)
    pairs = [(i, i + by) for i in range(peers) if 0 <= i + by < peers]
    return lax.ppermute(array, axis, pairs)


def split3(value):
    high = value.astype(bf16)
    rest = value - high.astype(f32)
    mid = rest.astype(bf16)
    low = (rest - mid.astype(f32)).astype(bf16)
    return high, mid, low


def running(value_of, steps, rows, upper):
    place = lax.broadcasted_iota(jnp.int32, (rows, rows), 0)
    other = lax.broadcasted_iota(jnp.int32, (rows, rows), 1)
    tri = jnp.where((other >= place) if upper else (other <= place), 1.0, 0.0).astype(bf16)
    outs = [None] * steps
    carry = jnp.zeros((1, LANES), f32)
    order = range(steps - 1, -1, -1) if upper else range(steps)
    for n in order:
        block = value_of(n)
        total = sum(dot(tri, part) for part in split3(block)) + carry
        outs[n] = total
        carry = total[0:1] if upper else total[rows - 1 : rows]
    return outs, carry


PROJECT_TILE = 256
TERM_ROWS = 32


def project_kernel(local_heads, tokens_ref, gain_ref, weight_ref, bias_ref, input_ref, out_ref,
                   terms_ref, turned_ref, forget_ref, carry_ref):
    rows = tokens_ref.shape[0]
    wide = weight_ref.shape[1] - LANES

    @pl.when(pl.program_id(0) == 0)
    def _():
        carry_ref[...] = jnp.zeros_like(carry_ref)

    tokens = tokens_ref[...].astype(f32)
    input1 = (tokens * inverse_rms(tokens) * gain_ref[0:1, :]).astype(bf16)
    input_ref[...] = input1
    raw = dot(input1, weight_ref[...])
    out_ref[...] = raw[:, :wide].astype(bf16)
    forget = (raw[:, wide:] + bias_ref[0:1, :]).astype(bf16).astype(f32)
    forget_ref[...] = forget
    lane = lax.broadcasted_iota(jnp.int32, (rows, LANES), 1)
    logf = jnp.minimum(forget, 0.0) - jnp.log1p(jnp.exp(-jnp.abs(forget)))
    logf = jnp.where(lane < local_heads, logf, 0.0)
    place = lax.broadcasted_iota(jnp.int32, (rows, rows), 0)
    other = lax.broadcasted_iota(jnp.int32, (rows, rows), 1)
    tri = jnp.where(other <= place, 1.0, 0.0).astype(bf16)
    sums = sum(dot(tri, part) for part in split3(logf)) + carry_ref[0:1, :]
    carry_ref[0:1, :] = sums[rows - 1 : rows, :]
    high, mid, low = split3(sums)
    terms = (
        high.astype(f32)
        + pltpu.roll(mid.astype(f32), local_heads, 1)
        + pltpu.roll(low.astype(f32), 2 * local_heads, 1)
        + jnp.where(lane == 3 * local_heads, 1.0, 0.0)
    ).astype(bf16)
    terms_ref[...] = terms
    turned_ref[...] = terms.T[0:TERM_ROWS, :]


def project(tokens, gain, weight, bias, wide, local_heads):
    rows, width = tokens.shape

    def tile(columns):
        return pl.BlockSpec((PROJECT_TILE, columns), lambda n: (n, 0))

    def whole(*shape):
        return pl.BlockSpec(shape, lambda n: (0, 0))

    return pl.pallas_call(
        functools.partial(project_kernel, local_heads),
        grid=(rows // PROJECT_TILE,),
        in_specs=[tile(width), whole(8, width), whole(width, wide + LANES), whole(8, LANES)],
        out_specs=[
            tile(width),
            tile(wide),
            tile(LANES),
            pl.BlockSpec((TERM_ROWS, PROJECT_TILE), lambda n: (0, n)),
            tile(LANES),
        ],
        out_shape=[
            jax.ShapeDtypeStruct((rows, width), bf16),
            jax.ShapeDtypeStruct((rows, wide), bf16),
            jax.ShapeDtypeStruct((rows, LANES), bf16),
            jax.ShapeDtypeStruct((TERM_ROWS, rows), bf16),
            jax.ShapeDtypeStruct((rows, LANES), f32),
        ],
        scratch_shapes=[pltpu.VMEM((8, LANES), f32)],
        cost_estimate=pl.CostEstimate(
            flops=2 * rows * width * (wide + LANES), transcendentals=rows * LANES,
            bytes_accessed=20_000_000,
        ),
        name="project",
    )(tokens, gain, weight, bias)


def decay_back_kernel(own_ref, halo_ref, out_ref):
    rows = 256
    steps = own_ref.shape[0] // rows
    own, _ = running(lambda n: own_ref[n * rows : (n + 1) * rows, :], steps, rows, True)
    halo, _ = running(lambda n: halo_ref[n * rows : (n + 1) * rows, :], steps, rows, False)
    for n in range(steps):
        part = slice(n * rows, (n + 1) * rows)
        out_ref[part, :] = own[n] + (halo[n] - halo_ref[part, :])


def decay_back(own, halo):
    return pl.pallas_call(
        decay_back_kernel,
        out_shape=jax.ShapeDtypeStruct(own.shape, f32),
        name="decay_back",
    )(own, halo)


QUERY, KEY, TOTAL = range(3)


def placing(pair, local_heads, role):
    row = lax.broadcasted_iota(jnp.int32, (LANES, LANES), 0)
    col = lax.broadcasted_iota(jnp.int32, (LANES, LANES), 1)
    head = jnp.where(col < 64, 2 * pair + 1, 2 * pair)
    spot = jnp.where(col < 64, col, col - 64)
    term = spot - 3 * role
    is_term = (term >= 0) & (term < 3) & (row == term * local_heads + head)
    if role == QUERY:
        ones = (spot >= 3) & (spot < 9)
    else:
        ones = (spot < 3) & (role == KEY)
    is_one = ones & (row == 3 * local_heads)
    sign = -1.0 if role == KEY else 1.0
    return (jnp.where(is_term, sign, 0.0) + jnp.where(is_one, 1.0, 0.0)).astype(bf16)


def allowed_pairs(first_key, query_tile, rows, begin_row):
    shape = (K_TILE, Q_TILE)
    key_place = first_key + lax.broadcasted_iota(jnp.int32, shape, 0)
    query_place = rows + query_tile * Q_TILE + lax.broadcasted_iota(jnp.int32, shape, 1)
    return (key_place >= begin_row) & (key_place <= query_place)


def key_range(ranges_ref, query_tile, rows, own):
    count = rows // K_TILE
    base = count if own else 0
    first = jnp.clip(ranges_ref[0, query_tile] - base, 0, count)
    full = jnp.clip(ranges_ref[1, query_tile] - base, first, count)
    return first, full


def key_loops(ranges_ref, query_tile, rows, own, step, carry):
    first, full = key_range(ranges_ref, query_tile, rows, own)
    inside = query_tile * (Q_TILE // K_TILE) if own else rows // K_TILE
    full = jnp.minimum(full, inside)
    carry = lax.fori_loop(first, full, functools.partial(step, True), carry)
    carry = lax.fori_loop(full, inside, functools.partial(step, False), carry)
    if own:
        carry = lax.fori_loop(
            inside, inside + Q_TILE // K_TILE, functools.partial(step, True), carry
        )
    return carry


def tile_of(number, size):
    return pl.ds(pl.multiple_of(number * size, size), size)


def fill_keys(pair, local_heads, own, first, key_ref, terms_ref, keys):
    place = placing(pair, local_heads, KEY)
    lane = lax.broadcasted_iota(jnp.int32, (K_TILE, LANES), 1)
    rows = key_ref.shape[0]
    if not own:
        last = terms_ref[:, rows - LANES : rows].T
        total = dot(last, placing(pair, local_heads, TOTAL)[0:TERM_ROWS, :])[LANES - 1 : LANES, :]

    def fill(n, carry):
        here = tile_of(n, K_TILE)
        if own:
            extra = dot(terms_ref[here, :], place).astype(bf16)
        else:
            extra = dot(terms_ref[:, here].T, place[0:TERM_ROWS, :])
            extra = (extra + total).astype(bf16)
        key = key_ref[here, :]
        keys[0][here, :] = jnp.where(lane < 64, key, extra)
        keys[1][here, :] = jnp.where(lane < 64, extra, key)
        return carry

    lax.fori_loop(first, rows // K_TILE, fill, 0)


def query_tiles(q_ref, terms_ref, place, here, scaling):
    lane = lax.broadcasted_iota(jnp.int32, (Q_TILE, LANES), 1)
    extra = dot(terms_ref[here, :], place).astype(bf16)
    query = (q_ref[here, :].astype(f32) * scaling).astype(bf16)
    return jnp.where(lane < 64, query, extra), jnp.where(lane < 64, extra, query)


def attend_kernel(local_heads, own, ranges_ref, q_ref, k_ref, v_ref, t_query_ref, t_key_ref,
                  begin_ref, *refs):
    if own:
        acc_out_ref, state_out_ref, key0, key1, values, acc0, acc1 = refs
    else:
        acc_in_ref, state_in_ref, o_ref, lse_ref, key0, key1, values, acc0, acc1 = refs
    pair = pl.program_id(0)
    rows = q_ref.shape[0]
    base = rows if own else 0
    keys, accs = (key0, key1), (acc0, acc1)
    first, _ = key_range(ranges_ref, 0, rows, own)
    fill_keys(pair, local_heads, own, first, k_ref, t_key_ref, keys)

    def turn(n, carry):
        values[:, tile_of(n, K_TILE)] = v_ref[tile_of(n, K_TILE), :].T
        return carry

    lax.fori_loop(first, rows // K_TILE, turn, 0)
    place = placing(pair, local_heads, QUERY)

    def query_loop(tile, carry):
        here = tile_of(tile, Q_TILE)
        queries = query_tiles(q_ref, t_query_ref, place, here, 64**-0.5)
        begin_row = begin_ref[0:1, here]
        if own:
            low = jnp.full((1, Q_TILE), FAR, f32)
            zero = jnp.zeros((1, Q_TILE), f32)
            state = (low, zero, low, zero)
            for acc in accs:
                acc[...] = jnp.zeros_like(acc)
        else:
            state = tuple(state_in_ref[n : n + 1, here] for n in range(4))
            for h in range(2):
                accs[h][...] = acc_in_ref[64 * h : 64 * (h + 1), here]

        def step(masked, number, state):
            there = tile_of(number, K_TILE)
            fresh = []
            if masked:
                allowed = allowed_pairs(base + number * K_TILE, tile, rows, begin_row)
            for h in range(2):
                largest, total = state[2 * h], state[2 * h + 1]
                scores = dot(keys[h][there, :], queries[h], NT)
                if masked:
                    scores = jnp.where(allowed, scores, FAR)
                now = jnp.maximum(largest, jnp.max(scores, axis=0, keepdims=True))
                fade = jnp.exp(largest - now)
                weights = jnp.exp(scores - now)
                total = total * fade + jnp.sum(weights, axis=0, keepdims=True)
                accs[h][...] = accs[h][...] * fade + dot(
                    values[64 * h : 64 * (h + 1), there], weights.astype(bf16)
                )
                fresh += [now, total]
            return tuple(fresh)

        state = key_loops(ranges_ref, tile, rows, own, step, state)
        if own:
            for h in range(2):
                acc_out_ref[64 * h : 64 * (h + 1), here] = accs[h][...]
            for n in range(4):
                state_out_ref[n : n + 1, here] = state[n]
        else:
            mixed = jnp.concatenate(
                [accs[h][...] * (1.0 / state[2 * h + 1]) for h in range(2)], axis=0
            )
            o_ref[here, :] = mixed.T.astype(bf16)
            for h in range(2):
                lse_ref[h : h + 1, here] = state[2 * h] + jnp.log(state[2 * h + 1])
        return carry

    lax.fori_loop(0, rows // Q_TILE, query_loop, 0)


def lane_block(rows, offset):
    return pl.BlockSpec((rows, LANES), lambda p, *_: (0, offset + p))


def fixed(shape):
    return pl.BlockSpec(shape, lambda p, *_: (0, 0))


def pair_block(height, rows):
    return pl.BlockSpec((height, rows), lambda p, *_: (p, 0))


def attend(own, ranges, query, key_value, terms, key_terms, begins, local_heads, so_far=()):
    rows = query.shape[0]
    pairs = local_heads // 2
    running_specs = [pair_block(LANES, rows), pair_block(8, rows)]
    running_shape = (
        jax.ShapeDtypeStruct((LANES * pairs, rows), f32),
        jax.ShapeDtypeStruct((8 * pairs, rows), f32),
    )
    final_specs = [lane_block(rows, 0), pair_block(8, rows)]
    final_shape = (
        jax.ShapeDtypeStruct((rows, pairs * LANES), bf16),
        jax.ShapeDtypeStruct((8 * pairs, rows), f32),
    )
    return pl.pallas_call(
        functools.partial(attend_kernel, local_heads, own),
        grid_spec=pltpu.PrefetchScalarGridSpec(
            num_scalar_prefetch=1,
            grid=(pairs,),
            in_specs=[
                lane_block(rows, 0),
                lane_block(rows, 0),
                lane_block(rows, pairs),
                fixed((rows, LANES)),
                fixed((rows, LANES) if own else (TERM_ROWS, rows)),
                fixed((8, rows)),
            ]
            + ([] if own else running_specs),
            out_specs=running_specs if own else final_specs,
            scratch_shapes=[
                pltpu.VMEM((rows, LANES), bf16),
                pltpu.VMEM((rows, LANES), bf16),
                pltpu.VMEM((LANES, rows), bf16),
                pltpu.VMEM((64, Q_TILE), f32),
                pltpu.VMEM((64, Q_TILE), f32),
            ],
        ),
        out_shape=running_shape if own else final_shape,
        cost_estimate=pl.CostEstimate(
            flops=40_000_000_000 if own else 10_000_000_000,
            transcendentals=20_000_000,
            bytes_accessed=12_000_000,
        ),
        name="attend_own" if own else "attend_prev",
    )(ranges, query, key_value, key_value, terms, key_terms, begins, *so_far)


def attend_back_kernel(local_heads, own, ranges_ref, q_ref, k_ref, v_ref, t_query_ref, t_key_ref,
                       begin_ref, grad_ref, o_ref, lse_ref, *refs):
    if own:
        dq_in_ref, decay_in_ref, dq_ref, dk_ref, dv_ref, decay_ref = refs[:6]
    else:
        dq_ref, row_decay_ref, dkv_ref, decay_ref = refs[:4]
        dk_ref, dv_ref = dkv_ref.at[0], dkv_ref.at[1]
    key0, key1, key_t0, key_t1, dk0, dk1, dv, dq0, dq1 = refs[-9:]
    pair = pl.program_id(0)
    rows = q_ref.shape[0]
    base = rows if own else 0
    keys, keys_t, dks, dqs = (key0, key1), (key_t0, key_t1), (dk0, dk1), (dq0, dq1)
    first, _ = key_range(ranges_ref, 0, rows, own)
    fill_keys(pair, local_heads, own, first, k_ref, t_key_ref, keys)

    def turn(n, carry):
        here = tile_of(n, K_TILE)
        for h in range(2):
            keys_t[h][:, here] = keys[h][here, :].T
        return carry

    lax.fori_loop(first, rows // K_TILE, turn, 0)
    for ref in (dk0, dk1, dv):
        ref[...] = jnp.zeros_like(ref)
    place = placing(pair, local_heads, QUERY)
    lane = lax.broadcasted_iota(jnp.int32, (Q_TILE, LANES), 1)
    pick_row = lax.broadcasted_iota(jnp.int32, (8, LANES), 0)
    pick_lane = lax.broadcasted_iota(jnp.int32, (8, LANES), 1)
    pick = jnp.where((pick_lane // 64) == pick_row, 1.0, 0.0)
    sums_ref = decay_ref if own else row_decay_ref

    @pl.when(pair == 0)
    def _():
        if own:
            decay_ref[...] = decay_in_ref[...]
        else:
            decay_ref[...] = jnp.zeros_like(decay_ref)
            row_decay_ref[...] = jnp.zeros_like(row_decay_ref)

    def query_tile(tile):
        here = tile_of(tile, Q_TILE)
        queries = query_tiles(q_ref, t_query_ref, place, here, 64**-0.5)
        begin_row = begin_ref[0:1, here]
        grad = grad_ref[here, :]
        nothing = jnp.zeros_like(grad)
        grads = (jnp.where(lane < 64, grad, nothing), jnp.where(lane < 64, nothing, grad))
        product = grad.astype(f32) * o_ref[here, :].astype(f32)
        inner = dot(pick, product, NT, precision=lax.Precision.HIGHEST)
        for dq in dqs:
            dq[...] = jnp.zeros_like(dq)

        def step(masked, number, state):
            there = tile_of(number, K_TILE)
            if masked:
                allowed = allowed_pairs(base + number * K_TILE, tile, rows, begin_row)
            value = v_ref[there, :]
            value_part = 0.0
            for h in range(2):
                scores = dot(keys[h][there, :], queries[h], NT)
                prob = jnp.exp(scores - lse_ref[h : h + 1, here])
                if masked:
                    prob = jnp.where(allowed, prob, 0.0)
                grad_prob = dot(value, grads[h], NT)
                grad_score = (prob * (grad_prob - inner[h : h + 1, :])).astype(bf16)
                value_part = value_part + dot(prob.astype(bf16), grads[h])
                dks[h][there, :] += dot(grad_score, queries[h])
                dqs[h][...] += dot(keys_t[h][:, there], grad_score)
            dv[there, :] += value_part
            return state

        key_loops(ranges_ref, tile, rows, own, step, 0)
        turned = [dq[...].T for dq in dqs]
        dq_tile = jnp.where(lane < 64, turned[0], turned[1]) * 64**-0.5
        if own:
            dq_tile = dq_tile + dq_in_ref[here, :]
        dq_ref[here, :] = dq_tile.astype(dq_ref.dtype)
        sums = sums_ref[here, :]
        sums = sums + jnp.where(lane == 2 * pair, turned[0][:, 64:65], 0.0)
        sums = sums + jnp.where(lane == 2 * pair + 1, turned[1][:, 0:1], 0.0)
        sums_ref[here, :] = sums

    def query_loop(tile, carry):
        if own:
            query_tile(tile)
        else:
            reaches = key_range(ranges_ref, tile, rows, own)[0] < rows // K_TILE
            pl.when(reaches)(lambda: query_tile(tile))

            @pl.when(jnp.logical_not(reaches))
            def _():
                dq_ref[tile_of(tile, Q_TILE), :] = jnp.zeros((Q_TILE, LANES), dq_ref.dtype)

        return carry

    lax.fori_loop(0, rows // Q_TILE, query_loop, 0)
    sign = -1.0 if own else 1.0

    def finish(n, carry):
        here = tile_of(n, Q_TILE)
        left, right = dk0[here, :], dk1[here, :]
        dk_ref[here, :] = jnp.where(lane < 64, left, right).astype(dk_ref.dtype)
        dv_ref[here, :] = dv[here, :].astype(dv_ref.dtype)
        decay = decay_ref[here, :]
        decay = decay + jnp.where(lane == 2 * pair, sign * left[:, 67:68], 0.0)
        decay = decay + jnp.where(lane == 2 * pair + 1, sign * right[:, 3:4], 0.0)
        decay_ref[here, :] = decay
        return carry

    lax.fori_loop(0, rows // Q_TILE, finish, 0)


def attend_back(
    own, ranges, query, key_value, terms, key_terms, begins, grad, mixed, lse, local_heads,
    so_far=(),
):
    rows = query.shape[0]
    pairs = local_heads // 2
    wide = jax.ShapeDtypeStruct((rows, pairs * LANES), f32)
    sums = jax.ShapeDtypeStruct((rows, LANES), f32)
    if own:
        out_specs = [lane_block(rows, 0)] * 3 + [fixed((rows, LANES))]
        out_shape = (jax.ShapeDtypeStruct(wide.shape, bf16), wide, wide, sums)
    else:
        both = pl.BlockSpec((2, rows, LANES), lambda p, *_: (0, 0, p))
        out_specs = [lane_block(rows, 0), fixed((rows, LANES)), both, fixed((rows, LANES))]
        out_shape = (
            wide, sums, jax.ShapeDtypeStruct((2, rows, pairs * LANES), bf16), sums,
        )
    return pl.pallas_call(
        functools.partial(attend_back_kernel, local_heads, own),
        grid_spec=pltpu.PrefetchScalarGridSpec(
            num_scalar_prefetch=1,
            grid=(pairs,),
            in_specs=[
                lane_block(rows, 0),
                lane_block(rows, 0),
                lane_block(rows, pairs),
                fixed((rows, LANES)),
                fixed((rows, LANES) if own else (TERM_ROWS, rows)),
                fixed((8, rows)),
                lane_block(rows, 0),
                lane_block(rows, 0),
                pair_block(8, rows),
            ]
            + ([lane_block(rows, 0), fixed((rows, LANES))] if own else []),
            out_specs=out_specs,
            scratch_shapes=[
                pltpu.VMEM((rows, LANES), bf16),
                pltpu.VMEM((rows, LANES), bf16),
                pltpu.VMEM((LANES, rows), bf16),
                pltpu.VMEM((LANES, rows), bf16),
                pltpu.VMEM((rows, LANES), f32),
                pltpu.VMEM((rows, LANES), f32),
                pltpu.VMEM((rows, LANES), f32),
                pltpu.VMEM((LANES, Q_TILE), f32),
                pltpu.VMEM((LANES, Q_TILE), f32),
            ],
        ),
        out_shape=out_shape,
        cost_estimate=pl.CostEstimate(
            flops=80_000_000_000 if own else 15_000_000_000,
            transcendentals=20_000_000,
            bytes_accessed=25_000_000,
        ),
        name="attend_back_own" if own else "attend_back_prev",
    )(
        ranges, query, key_value, key_value, terms, key_terms, begins, grad, mixed, lse, *so_far
    )


PIECES = 4


def partners():
    me = lax.axis_index("head")
    near = me + 1 - 2 * (me % 2)
    far = (me + 2) % 4
    cross = (near + 2) % 4
    return me, near, far, cross


def signal(other):
    pl.semaphore_signal(
        pltpu.get_barrier_semaphore(), inc=1, device_id=other, device_id_type=pl.DeviceIdType.MESH
    )


def greet(others):
    for other in others:
        signal(other)
    pl.semaphore_wait(pltpu.get_barrier_semaphore(), len(others))


def remote(source, target, send, receive, other):
    return pltpu.make_async_remote_copy(
        src_ref=source,
        dst_ref=target,
        send_sem=send,
        recv_sem=receive,
        device_id=other,
        device_id_type=pl.DeviceIdType.MESH,
    )


def on_head(index):
    return {"head": index}


def on_blk(index):
    return {"blk": index}


def piece_at(ref, slot, piece, size):
    span = size // PIECES
    return ref.at[pl.ds(pl.multiple_of(slot * size + piece * span, span), span), :]


class Slots:
    def __init__(self, by_device):
        me, near, far, cross = partners()
        if by_device:
            self.own = self.sent_near = self.sent_far = me
            self.near, self.far, self.cross = near, far, cross
            self.passed = far
        else:
            self.own, self.sent_near, self.sent_far = 3, 2, 1
            self.near, self.far, self.cross = 2, 1, 0
            self.passed = 0


def spread_piece(source, all_ref, size, sems, piece, slots):
    me, near, far, _ = partners()
    far_send, far_recv, near_send, near_recv, _, _, own = sems
    copies = (
        remote(source, piece_at(all_ref, slots.sent_far, piece, size), far_send.at[piece],
               far_recv.at[piece], on_head(far)),
        remote(source, piece_at(all_ref, slots.sent_near, piece, size), near_send.at[piece],
               near_recv.at[piece], on_head(near)),
        pltpu.make_async_copy(source, piece_at(all_ref, slots.own, piece, size), own.at[piece]),
    )
    for copy in copies:
        copy.start()
    return copies


def hand_on(all_ref, size, sems, sent, slots):
    me, near, far, cross = partners()
    far_send, far_recv, near_send, near_recv, on_send, on_recv, own = sems
    passed = []
    for piece in range(PIECES):
        there = piece_at(all_ref, slots.far, piece, size)
        remote(there, there, far_send.at[piece], far_recv.at[piece], on_head(far)).wait_recv()
        copy = remote(
            there, piece_at(all_ref, slots.passed, piece, size), on_send.at[piece],
            on_recv.at[piece], on_head(near),
        )
        copy.start()
        passed.append(copy)

    def finish():
        for piece in range(PIECES):
            to_far, to_near, local = sent[piece]
            to_far.wait_send()
            to_near.wait_send()
            local.wait()
            passed[piece].wait_send()
            there = piece_at(all_ref, slots.near, piece, size)
            remote(there, there, near_send.at[piece], near_recv.at[piece], on_head(near)).wait_recv()
            there = piece_at(all_ref, slots.cross, piece, size)
            remote(there, there, on_send.at[piece], on_recv.at[piece], on_head(near)).wait_recv()

    return finish


def gather_sems():
    return [pltpu.SemaphoreType.DMA((PIECES,)) for _ in range(7)]


def blk_peers():
    here = lax.axis_index("blk")
    half = lax.axis_size("blk") // 2
    low, high = here % 2, here // 2
    partner = here + 1 - 2 * low
    after = [((high + t) % half) * 2 + low for t in range(half)]
    return here, partner, after


class Line:
    def __init__(self, block_of, kinds, sems):
        self.block_of, self.kinds = block_of, kinds
        self.pair_send, self.pair_recv, self.up_send, self.up_recv, self.down_send, self.down_recv = sems
        here = lax.axis_index("blk")
        self.half = lax.axis_size("blk") // 2
        self.low, self.high = here % 2, here // 2
        self.partner = here + 1 - 2 * self.low
        self.has_up, self.has_down = self.high < self.half - 1, self.high > 0

    def greet(self, others):
        greet_sum = len(others) + 1
        for other in others + [on_blk(self.partner)]:
            signal(other)
        pl.when(self.has_up)(lambda: signal(on_blk(self.at(self.high + 1))))
        pl.when(self.has_down)(lambda: signal(on_blk(self.at(self.high - 1))))
        ends = (self.high == 0).astype(jnp.int32) + (self.high == self.half - 1).astype(jnp.int32)
        pl.semaphore_wait(pltpu.get_barrier_semaphore(), greet_sum + 2 - ends)

    def at(self, high):
        return high * 2 + self.low

    def pair_copy(self, kind, high, low):
        block = self.block_of(kind, high * 2 + low)
        return remote(
            block, block, self.pair_send.at[kind, high], self.pair_recv.at[kind, high],
            on_blk(self.partner),
        )

    def up_copy(self, kind, high):
        block = self.block_of(kind, self.at(high))
        return remote(
            block, block, self.up_send.at[kind, high], self.up_recv.at[kind, high],
            on_blk(self.at(jnp.minimum(self.high + 1, self.half - 1))),
        )

    def down_copy(self, kind, high):
        block = self.block_of(kind, self.at(high))
        return remote(
            block, block, self.down_send.at[kind, high], self.down_recv.at[kind, high],
            on_blk(self.at(jnp.maximum(self.high - 1, 0))),
        )

    def launch(self, kind):
        self.pair_copy(kind, self.high, self.low).start()
        pl.when(self.has_up)(lambda: self.up_copy(kind, self.high).start())
        pl.when(self.has_down)(lambda: self.down_copy(kind, self.high).start())

    def step(self, t):
        for kind in range(self.kinds):
            below, above = self.high - t, self.high + t

            @pl.when(below >= 0)
            def _():
                self.up_copy(kind, below).wait_recv()
                self.pair_copy(kind, below, self.low).start()
                pl.when(self.has_up)(lambda: self.up_copy(kind, below).start())

            @pl.when(above < self.half)
            def _():
                self.down_copy(kind, above).wait_recv()
                self.pair_copy(kind, above, self.low).start()
                pl.when(self.has_down)(lambda: self.down_copy(kind, above).start())

    def finish(self):
        for kind in range(self.kinds):

            def wait(high, carry):
                self.pair_copy(kind, high, self.low).wait_send()
                self.pair_copy(kind, high, 1 - self.low).wait_recv()

                @pl.when((high <= self.high) & self.has_up)
                def _():
                    self.up_copy(kind, high).wait_send()

                @pl.when((high >= self.high) & self.has_down)
                def _():
                    self.down_copy(kind, high).wait_send()

                return carry

            lax.fori_loop(0, self.half, wait, 0)


def gather_first_kernel(pack_ref, tokens_ref, cotangent_ref, pack_all, tokens_all, cotangent_all,
                        *sems):
    swap_send, swap_recv, swap_own = sems[:3]
    token_sems, cotangent_sems = sems[9:16], sems[16:23]
    me, near, far, cross = partners()
    sources = (me, near, far, cross)
    line = Line(lambda kind, blk: pack_all.at[blk, sources[kind]], 4, sems[3:9])
    here = lax.axis_index("blk")
    line.greet([on_head(near), on_head(far), on_head(cross)])
    swaps = [pltpu.make_async_copy(pack_ref.at[me], pack_all.at[here, me], swap_own)]
    for kind, other in enumerate((near, far, cross)):
        swaps.append(
            remote(
                pack_ref.at[other],
                pack_all.at[here, me],
                swap_send.at[kind],
                swap_recv.at[kind],
                on_head(other),
            )
        )
    for swap in swaps:
        swap.start()
    size = tokens_ref.shape[0]
    span = size // PIECES

    def spread_all(ref, all_ref, some, slots):
        return [
            spread_piece(ref.at[pl.ds(piece * span, span), :], all_ref, size, some, piece, slots)
            for piece in range(PIECES)
        ]

    by_device, crossing = Slots(True), Slots(False)
    tokens_sent = spread_all(tokens_ref, tokens_all, token_sems, by_device)
    swaps[0].wait()
    line.launch(0)
    for kind, source in enumerate((near, far, cross)):
        block = pack_all.at[here, source]
        remote(
            block, block, swap_send.at[kind], swap_recv.at[kind], on_head(source)
        ).wait_recv()
        line.launch(kind + 1)
    cotangent_sent = spread_all(cotangent_ref, cotangent_all, cotangent_sems, crossing)
    for t in range(1, line.half):
        line.step(t)
    finish_tokens = hand_on(tokens_all, size, token_sems, tokens_sent, by_device)
    finish_cotangent = hand_on(cotangent_all, size, cotangent_sems, cotangent_sent, crossing)
    for swap in swaps[1:]:
        swap.wait_send()
    line.finish()
    finish_tokens()
    finish_cotangent()


def gather_first(pack, tokens, cotangent, number):
    groups, share, columns = pack.shape
    peers = lax.axis_size("blk")
    rows, width = tokens.shape
    whole = jax.ShapeDtypeStruct((groups * rows, width), bf16)
    vmem, anywhere = pl.BlockSpec(memory_space=pltpu.VMEM), pl.BlockSpec(memory_space=pl.ANY)
    all_pack, all_tokens, all_cotangent = pl.pallas_call(
        gather_first_kernel,
        in_specs=[vmem] * 3,
        out_specs=[anywhere] * 3,
        out_shape=[jax.ShapeDtypeStruct((peers, groups, share, columns), bf16), whole, whole],
        scratch_shapes=[
            pltpu.SemaphoreType.DMA((3,)),
            pltpu.SemaphoreType.DMA((3,)),
            pltpu.SemaphoreType.DMA,
        ]
        + [pltpu.SemaphoreType.DMA((4, peers // 2)) for _ in range(6)]
        + gather_sems()
        + gather_sems(),
        compiler_params=pltpu.CompilerParams(collective_id=number, has_side_effects=True),
        cost_estimate=pl.CostEstimate(
            flops=70_000_000_000, transcendentals=0, bytes_accessed=30_000_000
        ),
        name="gather_first",
    )(pack, tokens, cotangent)
    return all_pack.reshape(peers * groups * share, columns), all_tokens, all_cotangent


class Sum:
    def __init__(self, part_ref, buffers, sems, size, by_device):
        self.part_ref, self.size, self.span = part_ref, size, size // PIECES
        self.slots = Slots(by_device)
        self.near_buf, self.turn_buf, self.far_buf = buffers
        self.near_send, self.near_recv, self.far_send, self.far_recv = sems
        self.near_copies, self.far_copies = [], []

    def piece(self, n):
        return slice(n * self.span, (n + 1) * self.span)

    def start(self):
        me, near, far, cross = partners()
        for which, shard in ((0, self.slots.cross), (1, self.slots.near)):
            for n in range(PIECES):
                copy = remote(
                    piece_at(self.part_ref, shard, n, self.size),
                    self.near_buf.at[which, pl.ds(n * self.span, self.span), :],
                    self.near_send.at[which, n],
                    self.near_recv.at[which, n],
                    on_head(near),
                )
                copy.start()
                self.near_copies.append(copy)

    def turn(self):
        me, near, far, cross = partners()
        for n in range(PIECES):
            here = self.piece(n)
            self.near_copies[n].wait_recv()
            self.turn_buf[here, :] = (
                piece_at(self.part_ref, self.slots.far, n, self.size)[...].astype(f32)
                + self.near_buf[0, here, :].astype(f32)
            ).astype(bf16)
            copy = remote(
                self.turn_buf.at[pl.ds(n * self.span, self.span), :],
                self.far_buf.at[pl.ds(n * self.span, self.span), :],
                self.far_send.at[n],
                self.far_recv.at[n],
                on_head(far),
            )
            copy.start()
            self.far_copies.append(copy)

    def total(self, n):
        self.near_copies[PIECES + n].wait_recv()
        self.far_copies[n].wait_recv()
        here = self.piece(n)
        return (
            piece_at(self.part_ref, self.slots.own, n, self.size)[...].astype(f32)
            + self.near_buf[1, here, :].astype(f32)
            + self.far_buf[here, :].astype(f32)
        )

    def finish(self):
        for copy in self.near_copies + self.far_copies:
            copy.wait_send()


def sum_buffers(size, width):
    return [
        pltpu.VMEM((2, size, width), bf16),
        pltpu.VMEM((size, width), bf16),
        pltpu.VMEM((size, width), bf16),
    ]


def sum_sems():
    return [
        pltpu.SemaphoreType.DMA((2, PIECES)),
        pltpu.SemaphoreType.DMA((2, PIECES)),
        pltpu.SemaphoreType.DMA((PIECES,)),
        pltpu.SemaphoreType.DMA((PIECES,)),
    ]


def column_chunks(width):
    count = max(width // 512, 1)
    first = width - 512 * (count - 1)
    return [(0, first)] + [(first + 512 * n, 512) for n in range(count - 1)]


class RowSums:
    def __init__(self, arrays, sems):
        self.pair_send, self.pair_recv, self.line_send, self.line_recv = sems
        self.here, self.partner, self.after = blk_peers()
        self.steps = len(self.after)
        self.chunks = [
            array + (pl.ds(start, wide),)
            for array in arrays
            for start, wide in column_chunks(array[0].shape[3])
        ]
        self.sent = []

    def others(self):
        return [on_blk(self.partner)] + [on_blk(peer) for peer in self.after[1:]]

    def pair_wait(self, c, t):
        _, pair_buf, _, _, at = self.chunks[c]
        block = pair_buf.at[t, :, :, at]
        remote(
            block, block, self.pair_send.at[c, t], self.pair_recv.at[c, t], on_blk(self.partner)
        ).wait_recv()

    def start(self):
        for c, (ref, pair_buf, _, _, at) in enumerate(self.chunks):
            for t in list(range(1, self.steps)) + [0]:
                copy = remote(
                    ref.at[self.after[t] + self.partner - self.here, :, :, at],
                    pair_buf.at[t, :, :, at],
                    self.pair_send.at[c, t],
                    self.pair_recv.at[c, t],
                    on_blk(self.partner),
                )
                copy.start()
                self.sent.append(copy)

    def pass_on(self, c):
        ref, pair_buf, line_buf, _, at = self.chunks[c]
        for t in range(1, self.steps):
            self.pair_wait(c, t)

            def add(group, carry):
                pair_buf[t, group, :, at] = (
                    ref[self.after[t], group, :, at].astype(f32)
                    + pair_buf[t, group, :, at].astype(f32)
                ).astype(bf16)
                return carry

            lax.fori_loop(0, ref.shape[1], add, 0)
            copy = remote(
                pair_buf.at[t, :, :, at], line_buf.at[t, :, :, at], self.line_send.at[c, t],
                self.line_recv.at[c, t], on_blk(self.after[t]),
            )
            copy.start()
            self.sent.append(copy)

    def add_up(self, c):
        ref, pair_buf, line_buf, out_ref, at = self.chunks[c]
        self.pair_wait(c, 0)
        for t in range(1, self.steps):
            block = line_buf.at[t, :, :, at]
            remote(
                block, block, self.line_send.at[c, t], self.line_recv.at[c, t],
                on_blk(self.after[t]),
            ).wait_recv()

        def add_all(group, carry):
            total = ref[self.here, group, :, at].astype(f32)
            total = total + pair_buf[0, group, :, at].astype(f32)
            for t in range(1, self.steps):
                total = total + line_buf[t, group, :, at].astype(f32)
            out_ref[group, :, at] = total.astype(bf16)
            return carry

        lax.fori_loop(0, ref.shape[1], add_all, 0)

    def finish(self):
        for copy in self.sent:
            copy.wait_send()


def row_sum_buffers(half, groups, share, columns):
    return [pltpu.VMEM((half, groups, share, columns), bf16) for _ in range(2)]


def row_sum_sems(chunks, half):
    return [pltpu.SemaphoreType.DMA((chunks, half)) for _ in range(4)]


def exchange_kernel(local, extras, summed, *refs):
    part_ref, extra_refs, mine_ref = refs[0], refs[1 : 1 + extras], refs[1 + extras]
    out_ref, all_ref, weight_ref, payload = refs[2 + extras : 6 + extras]
    sems = refs[6 + extras :]
    size = out_ref.shape[0]
    span = size // PIECES
    _, near, far, _ = partners()
    slots = Slots(summed)
    if summed:
        beside = RowSums([(mine_ref, sems[7], sems[8], weight_ref)], sems[9:13])
        greet([on_head(near), on_head(far)] + beside.others())
        beside.start()
    else:
        kinds = mine_ref.shape[0]
        beside = Line(lambda kind, blk: weight_ref.at[blk, kind], kinds, sems[-7:-1])
        own = pltpu.make_async_copy(mine_ref, weight_ref.at[lax.axis_index("blk")], sems[-1])
        own.start()
        beside.greet([on_head(near), on_head(far)])
        shares = Sum(part_ref, sems[7:10], sems[10:14], size, True)
        shares.start()
        own.wait()
        for kind in range(kinds):
            beside.launch(kind)
        shares.turn()
    sent = []
    for piece in range(PIECES):
        if not summed and piece != 2:
            hop = {0: 1, 1: 2, 3: 3}[piece]
            for t in range(hop, beside.half if piece == 3 else min(hop + 1, beside.half)):
                beside.step(t)
        here = slice(piece * span, (piece + 1) * span)
        total = part_ref[here, :] if summed else shares.total(piece)
        result, share = local(total, here, *extra_refs)
        out_ref[here, :] = result.astype(out_ref.dtype)
        payload[here, :] = share.astype(bf16)
        source = payload.at[pl.ds(piece * span, span), :]
        sent.append(spread_piece(source, all_ref, size, sems[:7], piece, slots))
    if summed:
        for c in range(len(beside.chunks)):
            beside.pass_on(c)
    finish_rows = hand_on(all_ref, size, sems[:7], sent, slots)
    if summed:
        for c in range(len(beside.chunks)):
            beside.add_up(c)
    finish_rows()
    if not summed:
        shares.finish()
    beside.finish()


def exchange(local, part, extras, summed, number, name, mine):
    rows, width = part.shape
    size = rows if summed else rows // 4
    peers = lax.axis_size("blk")
    vmem, anywhere = pl.BlockSpec(memory_space=pltpu.VMEM), pl.BlockSpec(memory_space=pl.ANY)
    scratch = [pltpu.VMEM((size, width), bf16)] + gather_sems()
    if summed:
        beside = mine.shape[1:]
        scratch += row_sum_buffers(peers // 2, *beside)
        scratch += row_sum_sems(len(column_chunks(beside[2])), peers // 2)
    else:
        beside = (peers,) + mine.shape
        scratch += sum_buffers(size, width) + sum_sems()
        scratch += [pltpu.SemaphoreType.DMA((mine.shape[0], peers // 2)) for _ in range(6)]
        scratch.append(pltpu.SemaphoreType.DMA)
    return pl.pallas_call(
        functools.partial(exchange_kernel, local, len(extras), summed),
        in_specs=[vmem] * (2 + len(extras)),
        out_specs=[vmem, anywhere, vmem if summed else anywhere],
        out_shape=[
            jax.ShapeDtypeStruct((size, width), f32),
            jax.ShapeDtypeStruct((4 * size, width), bf16),
            jax.ShapeDtypeStruct(beside, bf16),
        ],
        scratch_shapes=scratch,
        compiler_params=pltpu.CompilerParams(collective_id=number, has_side_effects=True),
        cost_estimate=pl.CostEstimate(
            flops=60_000_000_000 if summed else 80_000_000_000,
            transcendentals=0,
            bytes_accessed=16_000_000,
        ),
        name=name,
    )(part, *extras, mine)


def finish_last_kernel(grads_ref, first_ref, grad_ref, output_grad_ref, second_ref, second_down_ref,
                       grad_middle_ref, tokens_ref, gain_ref, weights_ref, output_ref,
                       second_out_ref, second_down_out_ref, tokens_grad_ref, part_buf, *refs):
    pair0, line0, pair1, line1, row0, row1 = refs[:6]
    swap_send, swap_recv = refs[10:12]
    me, near, far, cross = partners()
    others = (near, far, cross)
    sums = RowSums(
        [(grad_ref, pair0, line0, row0), (output_grad_ref, pair1, line1, row1)], refs[6:10]
    )
    outs = {id(row0): weights_ref, id(row1): output_ref}
    greet([on_head(other) for other in others] + sums.others())
    size = tokens_grad_ref.shape[0]
    first = Sum(part_buf, refs[12:15], refs[15:19], size, True)
    sums.start()
    sent = []

    def swap(source_ref, out_ref, c):
        for kind, other in enumerate(others):
            copy = remote(
                source_ref.at[other], out_ref.at[me], swap_send.at[c, kind],
                swap_recv.at[c, kind], on_head(other),
            )
            copy.start()
            sent.append(copy)

    count = len(sums.chunks)
    swap(second_ref, second_out_ref, count)
    swap(second_down_ref, second_down_out_ref, count + 1)
    columns = grads_ref.shape[1]
    tiles = part_buf.shape[0] // 256

    def multiply(n, carry):
        here = tile_of(n, 256)
        part_buf[here, :] = dot(grads_ref[here, :], first_ref[:, :columns], NT).astype(bf16)
        return carry

    lax.fori_loop(0, tiles // 4, multiply, 0)
    sums.pass_on(0)
    lax.fori_loop(tiles // 4, tiles, multiply, 0)
    first.start()

    def add_up(c):
        sums.add_up(c)
        _, _, _, row_ref, at = sums.chunks[c]
        out_ref = outs[id(row_ref)]
        out_ref[me, :, at] = row_ref[me, :, at]
        swap(row_ref.at[:, :, at], out_ref.at[:, :, at], c)

    for c in range(1, count):
        sums.pass_on(c)
        if c == 1:
            first.turn()
        add_up(c - 1)
    for piece in range(PIECES):
        rows = first.piece(piece)
        tokens_grad_ref[rows, :], _ = after_first(
            first.total(piece), rows, grad_middle_ref, tokens_ref, gain_ref
        )
    add_up(count - 1)
    second_out_ref[me] = second_ref[me]
    second_down_out_ref[me] = second_down_ref[me]
    for c in range(count + 2):
        if c < count:
            _, _, _, row_ref, at = sums.chunks[c]
            out_ref = outs[id(row_ref)].at[:, :, at]
        else:
            out_ref = second_out_ref if c == count else second_down_out_ref
        for kind, other in enumerate(others):
            block = out_ref.at[other]
            remote(
                block, block, swap_send.at[c, kind], swap_recv.at[c, kind], on_head(other)
            ).wait_recv()
    for copy in sent:
        copy.wait_send()
    sums.finish()
    first.finish()


def finish_last(grads, first, grad, output_grad, second, second_down, grad_middle, tokens, gain,
                number):
    peers = lax.axis_size("blk")
    groups, share, down_columns = second_down.shape
    rows, width = tokens.shape
    vmem = pl.BlockSpec(memory_space=pltpu.VMEM)
    half = peers // 2
    widths = (grad.shape[1], output_grad.shape[1])
    chunks = sum(len(column_chunks(columns)) for columns in widths)
    return pl.pallas_call(
        finish_last_kernel,
        in_specs=[vmem] * 9,
        out_specs=[vmem] * 5,
        out_shape=[
            jax.ShapeDtypeStruct((groups, share, columns), bf16)
            for columns in widths + (second.shape[1], down_columns)
        ]
        + [jax.ShapeDtypeStruct((rows, width), f32)],
        scratch_shapes=[pltpu.VMEM((4 * rows, width), bf16)]
        + row_sum_buffers(half, groups, share, widths[0])
        + row_sum_buffers(half, groups, share, widths[1])
        + [pltpu.VMEM((groups, share, columns), bf16) for columns in widths]
        + row_sum_sems(chunks, half)
        + [pltpu.SemaphoreType.DMA((chunks + 2, 3)) for _ in range(2)]
        + sum_buffers(rows, width)
        + sum_sems(),
        compiler_params=pltpu.CompilerParams(
            collective_id=number, has_side_effects=True, vmem_limit_bytes=62 << 20
        ),
        cost_estimate=pl.CostEstimate(
            flops=90_000_000_000, transcendentals=0, bytes_accessed=40_000_000
        ),
        name="finish_last",
    )(
        grads,
        first,
        grad.reshape(peers, groups, share, widths[0]),
        output_grad.reshape(peers, groups, share, widths[1]),
        second.reshape(groups, share, second.shape[1]),
        second_down,
        grad_middle, tokens, gain,
    )


def inverse_rms(value):
    return lax.rsqrt(jnp.mean(value * value, axis=1, keepdims=True) + epsilon)


def through_norm(grad, value):
    factor = inverse_rms(value)
    normed = value * factor
    return factor * (grad - normed * jnp.mean(grad * normed, axis=1, keepdims=True))


def after_attention(total, here, tokens_ref, gain_ref):
    middle = tokens_ref[here, :].astype(f32) + total
    return middle, middle * inverse_rms(middle) * gain_ref[0:1, :]


def after_hidden(total, here, cotangent_ref, middle_ref, gain_ref):
    grad = cotangent_ref[here, :].astype(f32) + through_norm(
        total * gain_ref[0:1, :], middle_ref[here, :]
    )
    return grad, grad


def after_first(total, here, grad_ref, tokens_ref, gain_ref):
    grad = grad_ref[here, :] + through_norm(
        total * gain_ref[0:1, :], tokens_ref[here, :].astype(f32)
    )
    return grad, None


FEED_TILE = 256
FEED_COLUMNS = 512


def feed_kernel(input_ref, cotangent_ref, weight_ref, down_weight_ref, down_ref, grad_ref, grad_down_ref,
                total_ref, acts, turned0, turned1, stage, near_buf, far_buf, down_stage, near_send,
                near_recv, far_send, far_recv, down_sems):
    step = pl.program_id(0)
    hidden_width = down_weight_ref.shape[1]
    size = total_ref.shape[0]
    per = size // FEED_TILE
    tiles = 4 * per
    me, near, far, cross = partners()

    @pl.when(step == 0)
    def _():
        greet([on_head(near), on_head(far)])

    def down_copy(at):
        shard = sum(jnp.where(at // per == n, s, 0) for n, s in enumerate((cross, far, near, me)))
        row = pl.multiple_of(shard * size + (at % per) * FEED_TILE, FEED_TILE)
        return pltpu.make_async_copy(
            down_stage.at[at % 2], down_ref.at[pl.ds(row, FEED_TILE), :], down_sems.at[at % 2]
        )

    def to_near(which, piece):
        return remote(
            stage.at[which * per + piece],
            near_buf.at[which, piece],
            near_send.at[which, piece],
            near_recv.at[which, piece],
            on_head(near),
        )

    def to_far(piece):
        return remote(
            near_buf.at[0, piece], far_buf.at[piece], far_send.at[piece], far_recv.at[piece],
            on_head(far),
        )

    @pl.when(step < tiles)
    def _():
        here = tile_of(step, FEED_TILE)
        inputs, cotangent = input_ref[...], cotangent_ref[...]
        turned0[:, here] = inputs.T
        turned1[:, here] = cotangent.T
        gate_at, up_at, down_at = (
            slice(n * hidden_width, (n + 1) * hidden_width) for n in range(3)
        )
        gate = dot(inputs, weight_ref[:, gate_at])
        up = dot(inputs, weight_ref[:, up_at])
        grad_hidden = dot(cotangent, down_weight_ref[...])
        opening = jax.nn.sigmoid(gate)
        active = gate * opening
        hidden = (active * up).astype(bf16)
        grad_gate = (grad_hidden * up * opening * (1.0 + gate * (1.0 - opening))).astype(bf16)
        grad_up = (grad_hidden * active).astype(bf16)
        acts[here, gate_at] = grad_gate
        acts[here, up_at] = grad_up
        acts[here, down_at] = hidden
        pl.when(step >= 2)(lambda: down_copy(step - 2).wait())
        down_stage[step % 2] = dot(hidden, down_weight_ref[...], NT).astype(bf16)
        down_copy(step).start()
        back = dot(grad_gate, weight_ref[:, gate_at], NT) + dot(
            grad_up, weight_ref[:, up_at], NT
        )
        for piece in range(per):
            for which, first in ((0, 0), (1, 2 * per)):

                @pl.when(step == first + piece)
                def _():
                    stage[which * per + piece] = back.astype(bf16)
                    to_near(which, piece).start()

            @pl.when(step == per + piece)
            def _():
                to_near(0, piece).wait_recv()
                near_buf[0, piece] = (back + near_buf[0, piece].astype(f32)).astype(bf16)
                to_far(piece).start()

            @pl.when(step == 3 * per + piece)
            def _():
                total_ref[piece * FEED_TILE : (piece + 1) * FEED_TILE, :] = back

    @pl.when(step >= tiles)
    def _():
        at = tile_of(step - tiles, FEED_COLUMNS)
        from_input = (step - tiles) * FEED_COLUMNS < 2 * hidden_width

        @pl.when(from_input)
        def _():
            grad_ref[...] = dot(turned0[...], acts[:, at]).astype(bf16)

        @pl.when(jnp.logical_not(from_input))
        def _():
            grad_down_ref[...] = dot(turned1[...], acts[:, at]).astype(bf16)

    @pl.when(step == pl.num_programs(0) - 1)
    def _():
        down_copy(tiles - 2).wait()
        down_copy(tiles - 1).wait()
        for piece in range(per):
            here = slice(piece * FEED_TILE, (piece + 1) * FEED_TILE)
            to_near(1, piece).wait_recv()
            to_far(piece).wait_recv()
            total_ref[here, :] += near_buf[1, piece].astype(f32) + far_buf[piece].astype(f32)
            to_near(0, piece).wait_send()
            to_near(1, piece).wait_send()
            to_far(piece).wait_send()


def feed(inputs, cotangent, weight, down_weight, number):
    rows, width = inputs.shape
    columns = weight.shape[1] + down_weight.shape[1]
    size = rows // 4
    tiles, per = rows // FEED_TILE, size // FEED_TILE
    wide = weight.shape[1] // FEED_COLUMNS
    tile = pl.BlockSpec((FEED_TILE, width), lambda n: (jnp.minimum(n, tiles - 1), 0))

    def whole(shape):
        return pl.BlockSpec(shape, lambda n: (0, 0), pipeline_mode=pl.Buffered(1))

    return pl.pallas_call(
        feed_kernel,
        grid=(tiles + columns // FEED_COLUMNS,),
        in_specs=[tile, tile, whole(weight.shape), whole(down_weight.shape)],
        out_specs=[
            pl.BlockSpec(memory_space=pl.ANY),
            pl.BlockSpec((width, FEED_COLUMNS), lambda n: (0, jnp.clip(n - tiles, 0, wide - 1))),
            pl.BlockSpec((width, FEED_COLUMNS), lambda n: (0, jnp.maximum(n - tiles - wide, 0))),
            whole((size, width)),
        ],
        out_shape=[
            jax.ShapeDtypeStruct((rows, width), bf16),
            jax.ShapeDtypeStruct((width, weight.shape[1]), bf16),
            jax.ShapeDtypeStruct((width, down_weight.shape[1]), bf16),
            jax.ShapeDtypeStruct((size, width), f32),
        ],
        scratch_shapes=[
            pltpu.VMEM((rows, columns), bf16),
            pltpu.VMEM((width, rows), bf16),
            pltpu.VMEM((width, rows), bf16),
            pltpu.VMEM((2 * per, FEED_TILE, width), bf16),
            pltpu.VMEM((2, per, FEED_TILE, width), bf16),
            pltpu.VMEM((per, FEED_TILE, width), bf16),
            pltpu.VMEM((2, FEED_TILE, width), bf16),
            pltpu.SemaphoreType.DMA((2, per)),
            pltpu.SemaphoreType.DMA((2, per)),
            pltpu.SemaphoreType.DMA((per,)),
            pltpu.SemaphoreType.DMA((per,)),
            pltpu.SemaphoreType.DMA((2,)),
        ],
        compiler_params=pltpu.CompilerParams(
            collective_id=number, has_side_effects=True, vmem_limit_bytes=63 << 20
        ),
        cost_estimate=pl.CostEstimate(
            flops=6 * rows * width * columns, transcendentals=rows * columns // 3,
            bytes_accessed=45_000_000,
        ),
        name="feed",
    )(inputs, cotangent, weight, down_weight)


def over_tokens(operand, other_side):
    return lax.dot_general(
        operand, other_side, (((0,), (0,)), ((), ())), preferred_element_type=f32
    )


def sent_columns(pieces, groups):
    packed = jnp.concatenate(
        [piece.reshape(piece.shape[0], groups, -1) for piece in pieces], axis=2
    )
    mine = lax.all_to_all(packed, "head", split_axis=1, concat_axis=0, tiled=True)
    return mine.reshape(mine.shape[0], mine.shape[2])


def all_rows(mine):
    return lax.all_gather(mine, "blk", axis=0, tiled=True)


def row_sums(grad):
    return lax.psum_scatter(grad, "blk", scatter_dimension=0, tiled=True)


def body(
    tokens,
    segment,
    norm1_gain,
    w_query,
    w_key,
    w_value,
    w_gate_out,
    w_forget,
    forget_bias,
    w_output,
    norm2_gain,
    w_gate,
    w_up,
    w_down,
    cotangent,
):
    token_rows, model_width = tokens.shape
    groups = lax.axis_size("head")
    head_count = forget_bias.shape[0]
    local_heads = head_count // groups
    local_width = model_width // groups
    hidden_width = w_gate.shape[1] // groups
    rows = token_rows * groups
    share = w_query.shape[0]
    group = lax.axis_index("head")

    low = lambda array: array.astype(bf16)
    spread = lambda gain: jnp.broadcast_to(low(gain)[:, None, None], (share, groups, 1))
    forget_low = low(w_forget).reshape(share, groups, local_heads)
    rest = LANES - local_heads - 2
    small = jnp.concatenate(
        [forget_low, spread(norm1_gain), spread(norm2_gain), jnp.zeros((share, groups, rest), bf16)],
        axis=2,
    )
    pack = jnp.concatenate(
        [
            low(piece).reshape(share, groups, -1)
            for piece in (w_key, w_value, small, w_query, w_gate_out, w_output)
        ],
        axis=2,
    )
    first, tokens_all, cotangent_all = gather_first(
        jnp.swapaxes(pack, 0, 1), tokens, cotangent, 0
    )
    kv_width = 2 * local_width + LANES
    output_weight = first[:, kv_width + 2 * local_width :]

    segment_plus = segment + 1
    earlier_segment = passed_along(segment_plus, "blk", 1)
    window = jnp.concatenate([earlier_segment, segment_plus])
    begins = jnp.sum(
        (window[:, None] < segment_plus[None, :]).astype(jnp.int32), axis=0
    )
    tiles = begins.reshape(rows // Q_TILE, Q_TILE)
    ranges = jnp.stack([tiles[:, 0] // K_TILE, (tiles[:, -1] + K_TILE - 1) // K_TILE])
    begins = jnp.broadcast_to(begins[None, :], (8, rows))

    def gain_rows(column):
        gain = first[:, 2 * local_width + local_heads + column].astype(f32)
        return jnp.broadcast_to(gain[None, :], (8, model_width))

    gain1, gain2 = gain_rows(0), gain_rows(1)
    bias = lax.dynamic_slice_in_dim(forget_bias, group * local_heads, local_heads, 0)
    bias = jnp.broadcast_to(jnp.pad(bias, (0, LANES - local_heads))[None, :], (8, LANES))
    input1, key_value, terms, turned_terms, forget = project(
        tokens_all, gain1, first, bias, 2 * local_width, local_heads
    )
    earlier_kv = passed_along(key_value, "blk", 1)
    earlier_terms = passed_along(turned_terms, "blk", 1)
    query = dot(input1, first[:, kv_width : kv_width + local_width]).astype(bf16)
    gate_raw = dot(
        input1, first[:, kv_width + local_width : kv_width + 2 * local_width]
    )

    so_far = attend(True, ranges, query, key_value, terms, terms, begins, local_heads)
    later = lax.optimization_barrier((low(w_gate), low(w_up), low(w_down), key_value))
    mine = sent_columns(later[:3], groups)
    mine, earlier_kv, earlier_terms, so_far = lax.optimization_barrier(
        (mine, earlier_kv, earlier_terms, so_far)
    )
    second = all_rows(mine[:, : 2 * hidden_width])
    mine_down = mine[:, 2 * hidden_width :].reshape(groups, share, hidden_width)
    attended, lse = attend(
        False, ranges, query, earlier_kv, terms, earlier_terms, begins, local_heads, so_far
    )
    opened = jax.nn.sigmoid(gate_raw)
    attended_wide = attended.astype(f32)
    gated = (opened * attended_wide).astype(bf16)
    branch = dot(gated, output_weight, NT).astype(bf16)
    middle, input2, down_weight = exchange(
        after_attention, branch, [tokens, gain2], False, 1, "exchange_middle", mine_down
    )
    down_weight = down_weight.reshape(model_width, hidden_width)
    down, second_grad, down_grad, grad_input2 = feed(
        input2, cotangent_all, second, down_weight, 4
    )
    second_part = row_sums(second_grad)
    grad_middle, grad_branch, down_part = exchange(
        after_hidden, grad_input2, [cotangent, middle, gain2], True, 2, "exchange_hidden",
        down_grad.reshape(-1, groups, share, hidden_width),
    )

    grad_gated = dot(grad_branch, output_weight)
    grad_attended = (grad_gated * opened).astype(bf16)
    grad_gate_pre = (grad_gated * attended_wide * opened * (1.0 - opened)).astype(bf16)
    dq_prev, rows_prev, dkv_prev, decay_prev = attend_back(
        False, ranges, query, earlier_kv, terms, earlier_terms, begins, grad_attended, attended,
        lse, local_heads,
    )
    dkv_later = passed_along(dkv_prev, "blk", -1)
    decay_later = passed_along(decay_prev[:, :8], "blk", -1)
    decay_later = jnp.pad(decay_later, ((0, 0), (0, LANES - 8)))
    dq, dk_own, dv_own, decay_own = attend_back(
        True, ranges, query, key_value, terms, terms, begins, grad_attended, attended,
        lse, local_heads, (dq_prev, rows_prev),
    )
    dk = (dk_own + dkv_later[0].astype(f32)).astype(bf16)
    dv = (dv_own + dkv_later[1].astype(f32)).astype(bf16)
    logf_grad = decay_back(decay_own, decay_later)
    forget_grad = jnp.where(
        jnp.arange(LANES)[None, :] < local_heads, logf_grad * jax.nn.sigmoid(-forget), 0.0
    ).astype(bf16)
    grads = jnp.concatenate([dk, dv, forget_grad, dq, grad_gate_pre], axis=1)
    first_grad = over_tokens(input1, grads)
    bias_part = jnp.sum(forget_grad.astype(f32), axis=0)
    row = jnp.arange(model_width)[:, None] % share
    column = jnp.arange(kv_width + 2 * local_width)[None, :]
    spread_bias = jnp.sum(
        jnp.where(row == jnp.arange(LANES)[None, :], bias_part[None, :], 0.0), axis=1, keepdims=True
    )
    first_grad = jnp.where(
        column == 2 * local_width + local_heads, spread_bias, first_grad
    ).astype(bf16)
    output_grad = over_tokens(grad_branch, gated).astype(bf16)
    down, second_part, first_grad = lax.optimization_barrier((down, second_part, first_grad))
    first_sum, output_sum, second_sum, down_sum, tokens_grad = finish_last(
        grads, first, first_grad, output_grad, second_part, down_part, grad_middle, tokens, gain1, 3
    )
    down = lax.psum_scatter(down, "head", scatter_dimension=0, tiled=True)
    result = (middle + down.astype(f32)).astype(bf16)
    first_sum, output_sum, second_sum, down_sum = (
        jnp.swapaxes(array, 0, 1).astype(f32)
        for array in (first_sum, output_sum, second_sum, down_sum)
    )

    def columns(array, start, width):
        return array[:, :, start : start + width].reshape(share, groups * width)

    key_sum, value_sum = (columns(first_sum, n * local_width, local_width) for n in range(2))
    forget_sum = columns(first_sum, 2 * local_width, local_heads)
    bias_total = first_sum[:local_heads, :, 2 * local_width + local_heads].T.reshape(head_count)
    query_sum, gate_out_sum = (
        columns(first_sum, kv_width + n * local_width, local_width) for n in range(2)
    )
    output_total = columns(output_sum, 0, local_width)
    gate_sum, up_sum = (
        columns(second_sum, n * hidden_width, hidden_width) for n in range(2)
    )
    down_sum = columns(down_sum, 0, hidden_width)

    def along(weight, grad):
        return jnp.sum(low(weight).astype(f32) * grad, axis=1)

    gain1_total = (
        along(w_query, query_sum)
        + along(w_key, key_sum)
        + along(w_value, value_sum)
        + along(w_gate_out, gate_out_sum)
        + along(w_forget, forget_sum)
    ) / low(norm1_gain).astype(f32)
    gain2_total = (along(w_gate, gate_sum) + along(w_up, up_sum)) / low(norm2_gain).astype(f32)
    return (
        result,
        tokens_grad,
        gain1_total,
        query_sum,
        key_sum,
        value_sum,
        gate_out_sum,
        forget_sum,
        bias_total,
        output_total,
        gain2_total,
        gate_sum,
        up_sum,
        down_sum,
    )


def solution(mesh):
    both = ("blk", "head")
    matrix, vector = P(both, None), P(both)
    return jax.shard_map(
        body,
        mesh=mesh,
        in_specs=(
            matrix, P("blk"), vector, matrix, matrix, matrix, matrix, matrix, P(), matrix, vector,
            matrix, matrix, matrix, matrix,
        ),
        out_specs=(
            matrix, matrix, vector, matrix, matrix, matrix, matrix, matrix, P(), matrix, vector,
            matrix, matrix, matrix,
        ),
        check_vma=False,
    )
```

```python
import functools

import jax
import jax.numpy as jnp
from jax import lax
from jax.experimental import pallas as pl
from jax.experimental.pallas import tpu as pltpu
from jax.sharding import PartitionSpec as P

epsilon = 1e-06
LANES = 128
Q_TILE = 512
K_TILE = 512
FAR = -1e30
NT = (((1,), (1,)), ((), ()))
NN = (((1,), (0,)), ((), ()))
bf16 = jnp.bfloat16
f32 = jnp.float32


def dot(a, b, dims=NN, **kw):
    return lax.dot_general(a, b, dims, preferred_element_type=f32, **kw)


def passed_along(array, axis, by):
    peers = lax.axis_size(axis)
    pairs = [(i, i + by) for i in range(peers) if 0 <= i + by < peers]
    return lax.ppermute(array, axis, pairs)


def split3(value):
    high = value.astype(bf16)
    rest = value - high.astype(f32)
    mid = rest.astype(bf16)
    low = (rest - mid.astype(f32)).astype(bf16)
    return high, mid, low


def running(value_of, steps, rows, upper):
    place = lax.broadcasted_iota(jnp.int32, (rows, rows), 0)
    other = lax.broadcasted_iota(jnp.int32, (rows, rows), 1)
    tri = jnp.where((other >= place) if upper else (other <= place), 1.0, 0.0).astype(bf16)
    outs = [None] * steps
    carry = jnp.zeros((1, LANES), f32)
    order = range(steps - 1, -1, -1) if upper else range(steps)
    for n in order:
        block = value_of(n)
        total = sum(dot(tri, part) for part in split3(block)) + carry
        outs[n] = total
        carry = total[0:1] if upper else total[rows - 1 : rows]
    return outs, carry


PROJECT_TILE = 256
TERM_ROWS = 32


def project_kernel(local_heads, tokens_ref, gain_ref, weight_ref, bias_ref, input_ref, out_ref,
                   terms_ref, turned_ref, forget_ref, carry_ref):
    rows = tokens_ref.shape[0]
    wide = weight_ref.shape[1] - LANES

    @pl.when(pl.program_id(0) == 0)
    def _():
        carry_ref[...] = jnp.zeros_like(carry_ref)

    tokens = tokens_ref[...].astype(f32)
    input1 = (tokens * inverse_rms(tokens) * gain_ref[0:1, :]).astype(bf16)
    input_ref[...] = input1
    raw = dot(input1, weight_ref[...])
    out_ref[...] = raw[:, :wide].astype(bf16)
    forget = (raw[:, wide:] + bias_ref[0:1, :]).astype(bf16).astype(f32)
    forget_ref[...] = forget
    lane = lax.broadcasted_iota(jnp.int32, (rows, LANES), 1)
    logf = jnp.minimum(forget, 0.0) - jnp.log1p(jnp.exp(-jnp.abs(forget)))
    logf = jnp.where(lane < local_heads, logf, 0.0)
    place = lax.broadcasted_iota(jnp.int32, (rows, rows), 0)
    other = lax.broadcasted_iota(jnp.int32, (rows, rows), 1)
    tri = jnp.where(other <= place, 1.0, 0.0).astype(bf16)
    sums = sum(dot(tri, part) for part in split3(logf)) + carry_ref[0:1, :]
    carry_ref[0:1, :] = sums[rows - 1 : rows, :]
    high, mid, low = split3(sums)
    terms = (
        high.astype(f32)
        + pltpu.roll(mid.astype(f32), local_heads, 1)
        + pltpu.roll(low.astype(f32), 2 * local_heads, 1)
        + jnp.where(lane == 3 * local_heads, 1.0, 0.0)
    ).astype(bf16)
    terms_ref[...] = terms
    turned_ref[...] = terms.T[0:TERM_ROWS, :]


def project(tokens, gain, weight, bias, wide, local_heads):
    rows, width = tokens.shape

    def tile(columns):
        return pl.BlockSpec((PROJECT_TILE, columns), lambda n: (n, 0))

    def whole(*shape):
        return pl.BlockSpec(shape, lambda n: (0, 0))

    return pl.pallas_call(
        functools.partial(project_kernel, local_heads),
        grid=(rows // PROJECT_TILE,),
        in_specs=[tile(width), whole(8, width), whole(width, wide + LANES), whole(8, LANES)],
        out_specs=[
            tile(width),
            tile(wide),
            tile(LANES),
            pl.BlockSpec((TERM_ROWS, PROJECT_TILE), lambda n: (0, n)),
            tile(LANES),
        ],
        out_shape=[
            jax.ShapeDtypeStruct((rows, width), bf16),
            jax.ShapeDtypeStruct((rows, wide), bf16),
            jax.ShapeDtypeStruct((rows, LANES), bf16),
            jax.ShapeDtypeStruct((TERM_ROWS, rows), bf16),
            jax.ShapeDtypeStruct((rows, LANES), f32),
        ],
        scratch_shapes=[pltpu.VMEM((8, LANES), f32)],
        cost_estimate=pl.CostEstimate(
            flops=2 * rows * width * (wide + LANES), transcendentals=rows * LANES,
            bytes_accessed=20_000_000,
        ),
        name="project",
    )(tokens, gain, weight, bias)


def decay_back_kernel(own_ref, halo_ref, out_ref):
    rows = 256
    steps = own_ref.shape[0] // rows
    own, _ = running(lambda n: own_ref[n * rows : (n + 1) * rows, :], steps, rows, True)
    halo, _ = running(lambda n: halo_ref[n * rows : (n + 1) * rows, :], steps, rows, False)
    for n in range(steps):
        part = slice(n * rows, (n + 1) * rows)
        out_ref[part, :] = own[n] + (halo[n] - halo_ref[part, :])


def decay_back(own, halo):
    return pl.pallas_call(
        decay_back_kernel,
        out_shape=jax.ShapeDtypeStruct(own.shape, f32),
        name="decay_back",
    )(own, halo)


QUERY, KEY, TOTAL = range(3)


def placing(pair, local_heads, role):
    row = lax.broadcasted_iota(jnp.int32, (LANES, LANES), 0)
    col = lax.broadcasted_iota(jnp.int32, (LANES, LANES), 1)
    head = jnp.where(col < 64, 2 * pair + 1, 2 * pair)
    spot = jnp.where(col < 64, col, col - 64)
    term = spot - 3 * role
    is_term = (term >= 0) & (term < 3) & (row == term * local_heads + head)
    if role == QUERY:
        ones = (spot >= 3) & (spot < 9)
    else:
        ones = (spot < 3) & (role == KEY)
    is_one = ones & (row == 3 * local_heads)
    sign = -1.0 if role == KEY else 1.0
    return (jnp.where(is_term, sign, 0.0) + jnp.where(is_one, 1.0, 0.0)).astype(bf16)


def allowed_pairs(first_key, query_tile, rows, begin_row):
    shape = (K_TILE, Q_TILE)
    key_place = first_key + lax.broadcasted_iota(jnp.int32, shape, 0)
    query_place = rows + query_tile * Q_TILE + lax.broadcasted_iota(jnp.int32, shape, 1)
    return (key_place >= begin_row) & (key_place <= query_place)


def key_range(ranges_ref, query_tile, rows, own):
    count = rows // K_TILE
    base = count if own else 0
    first = jnp.clip(ranges_ref[0, query_tile] - base, 0, count)
    full = jnp.clip(ranges_ref[1, query_tile] - base, first, count)
    return first, full


def key_loops(ranges_ref, query_tile, rows, own, step, carry):
    first, full = key_range(ranges_ref, query_tile, rows, own)
    inside = query_tile * (Q_TILE // K_TILE) if own else rows // K_TILE
    full = jnp.minimum(full, inside)
    carry = lax.fori_loop(first, full, functools.partial(step, True), carry)
    carry = lax.fori_loop(full, inside, functools.partial(step, False), carry)
    if own:
        carry = lax.fori_loop(
            inside, inside + Q_TILE // K_TILE, functools.partial(step, True), carry
        )
    return carry


def tile_of(number, size):
    return pl.ds(pl.multiple_of(number * size, size), size)


def fill_keys(pair, local_heads, own, first, key_ref, terms_ref, keys):
    place = placing(pair, local_heads, KEY)
    lane = lax.broadcasted_iota(jnp.int32, (K_TILE, LANES), 1)
    rows = key_ref.shape[0]
    if not own:
        last = terms_ref[:, rows - LANES : rows].T
        total = dot(last, placing(pair, local_heads, TOTAL)[0:TERM_ROWS, :])[LANES - 1 : LANES, :]

    def fill(n, carry):
        here = tile_of(n, K_TILE)
        if own:
            extra = dot(terms_ref[here, :], place).astype(bf16)
        else:
            extra = dot(terms_ref[:, here].T, place[0:TERM_ROWS, :])
            extra = (extra + total).astype(bf16)
        key = key_ref[here, :]
        keys[0][here, :] = jnp.where(lane < 64, key, extra)
        keys[1][here, :] = jnp.where(lane < 64, extra, key)
        return carry

    lax.fori_loop(first, rows // K_TILE, fill, 0)


def query_tiles(q_ref, terms_ref, place, here, scaling):
    lane = lax.broadcasted_iota(jnp.int32, (Q_TILE, LANES), 1)
    extra = dot(terms_ref[here, :], place).astype(bf16)
    query = (q_ref[here, :].astype(f32) * scaling).astype(bf16)
    return jnp.where(lane < 64, query, extra), jnp.where(lane < 64, extra, query)


def attend_kernel(local_heads, own, ranges_ref, q_ref, k_ref, v_ref, t_query_ref, t_key_ref,
                  begin_ref, *refs):
    if own:
        acc_out_ref, state_out_ref, key0, key1, values, acc0, acc1 = refs
    else:
        acc_in_ref, state_in_ref, o_ref, lse_ref, key0, key1, values, acc0, acc1 = refs
    pair = pl.program_id(0)
    rows = q_ref.shape[0]
    base = rows if own else 0
    keys, accs = (key0, key1), (acc0, acc1)
    first, _ = key_range(ranges_ref, 0, rows, own)
    fill_keys(pair, local_heads, own, first, k_ref, t_key_ref, keys)

    def turn(n, carry):
        values[:, tile_of(n, K_TILE)] = v_ref[tile_of(n, K_TILE), :].T
        return carry

    lax.fori_loop(first, rows // K_TILE, turn, 0)
    place = placing(pair, local_heads, QUERY)

    def query_loop(tile, carry):
        here = tile_of(tile, Q_TILE)
        queries = query_tiles(q_ref, t_query_ref, place, here, 64**-0.5)
        begin_row = begin_ref[0:1, here]
        if own:
            low = jnp.full((1, Q_TILE), FAR, f32)
            zero = jnp.zeros((1, Q_TILE), f32)
            state = (low, zero, low, zero)
            for acc in accs:
                acc[...] = jnp.zeros_like(acc)
        else:
            state = tuple(state_in_ref[n : n + 1, here] for n in range(4))
            for h in range(2):
                accs[h][...] = acc_in_ref[64 * h : 64 * (h + 1), here]

        def step(masked, number, state):
            there = tile_of(number, K_TILE)
            fresh = []
            if masked:
                allowed = allowed_pairs(base + number * K_TILE, tile, rows, begin_row)
            for h in range(2):
                largest, total = state[2 * h], state[2 * h + 1]
                scores = dot(keys[h][there, :], queries[h], NT)
                if masked:
                    scores = jnp.where(allowed, scores, FAR)
                now = jnp.maximum(largest, jnp.max(scores, axis=0, keepdims=True))
                fade = jnp.exp(largest - now)
                weights = jnp.exp(scores - now)
                total = total * fade + jnp.sum(weights, axis=0, keepdims=True)
                accs[h][...] = accs[h][...] * fade + dot(
                    values[64 * h : 64 * (h + 1), there], weights.astype(bf16)
                )
                fresh += [now, total]
            return tuple(fresh)

        state = key_loops(ranges_ref, tile, rows, own, step, state)
        if own:
            for h in range(2):
                acc_out_ref[64 * h : 64 * (h + 1), here] = accs[h][...]
            for n in range(4):
                state_out_ref[n : n + 1, here] = state[n]
        else:
            mixed = jnp.concatenate(
                [accs[h][...] * (1.0 / state[2 * h + 1]) for h in range(2)], axis=0
            )
            o_ref[here, :] = mixed.T.astype(bf16)
            for h in range(2):
                lse_ref[h : h + 1, here] = state[2 * h] + jnp.log(state[2 * h + 1])
        return carry

    lax.fori_loop(0, rows // Q_TILE, query_loop, 0)


def lane_block(rows, offset):
    return pl.BlockSpec((rows, LANES), lambda p, *_: (0, offset + p))


def fixed(shape):
    return pl.BlockSpec(shape, lambda p, *_: (0, 0))


def pair_block(height, rows):
    return pl.BlockSpec((height, rows), lambda p, *_: (p, 0))


def attend(own, ranges, query, key_value, terms, key_terms, begins, local_heads, so_far=()):
    rows = query.shape[0]
    pairs = local_heads // 2
    running_specs = [pair_block(LANES, rows), pair_block(8, rows)]
    running_shape = (
        jax.ShapeDtypeStruct((LANES * pairs, rows), f32),
        jax.ShapeDtypeStruct((8 * pairs, rows), f32),
    )
    final_specs = [lane_block(rows, 0), pair_block(8, rows)]
    final_shape = (
        jax.ShapeDtypeStruct((rows, pairs * LANES), bf16),
        jax.ShapeDtypeStruct((8 * pairs, rows), f32),
    )
    return pl.pallas_call(
        functools.partial(attend_kernel, local_heads, own),
        grid_spec=pltpu.PrefetchScalarGridSpec(
            num_scalar_prefetch=1,
            grid=(pairs,),
            in_specs=[
                lane_block(rows, 0),
                lane_block(rows, 0),
                lane_block(rows, pairs),
                fixed((rows, LANES)),
                fixed((rows, LANES) if own else (TERM_ROWS, rows)),
                fixed((8, rows)),
            ]
            + ([] if own else running_specs),
            out_specs=running_specs if own else final_specs,
            scratch_shapes=[
                pltpu.VMEM((rows, LANES), bf16),
                pltpu.VMEM((rows, LANES), bf16),
                pltpu.VMEM((LANES, rows), bf16),
                pltpu.VMEM((64, Q_TILE), f32),
                pltpu.VMEM((64, Q_TILE), f32),
            ],
        ),
        out_shape=running_shape if own else final_shape,
        cost_estimate=pl.CostEstimate(
            flops=40_000_000_000 if own else 10_000_000_000,
            transcendentals=20_000_000,
            bytes_accessed=12_000_000,
        ),
        name="attend_own" if own else "attend_prev",
    )(ranges, query, key_value, key_value, terms, key_terms, begins, *so_far)


def attend_back_kernel(local_heads, own, ranges_ref, q_ref, k_ref, v_ref, t_query_ref, t_key_ref,
                       begin_ref, grad_ref, o_ref, lse_ref, *refs):
    if own:
        dq_in_ref, decay_in_ref, dq_ref, dk_ref, dv_ref, decay_ref = refs[:6]
    else:
        dq_ref, row_decay_ref, dkv_ref, decay_ref = refs[:4]
        dk_ref, dv_ref = dkv_ref.at[0], dkv_ref.at[1]
    key0, key1, key_t0, key_t1, dk0, dk1, dv, dq0, dq1 = refs[-9:]
    pair = pl.program_id(0)
    rows = q_ref.shape[0]
    base = rows if own else 0
    keys, keys_t, dks, dqs = (key0, key1), (key_t0, key_t1), (dk0, dk1), (dq0, dq1)
    first, _ = key_range(ranges_ref, 0, rows, own)
    fill_keys(pair, local_heads, own, first, k_ref, t_key_ref, keys)

    def turn(n, carry):
        here = tile_of(n, K_TILE)
        for h in range(2):
            keys_t[h][:, here] = keys[h][here, :].T
        return carry

    lax.fori_loop(first, rows // K_TILE, turn, 0)
    for ref in (dk0, dk1, dv):
        ref[...] = jnp.zeros_like(ref)
    place = placing(pair, local_heads, QUERY)
    lane = lax.broadcasted_iota(jnp.int32, (Q_TILE, LANES), 1)
    pick_row = lax.broadcasted_iota(jnp.int32, (8, LANES), 0)
    pick_lane = lax.broadcasted_iota(jnp.int32, (8, LANES), 1)
    pick = jnp.where((pick_lane // 64) == pick_row, 1.0, 0.0)
    sums_ref = decay_ref if own else row_decay_ref

    @pl.when(pair == 0)
    def _():
        if own:
            decay_ref[...] = decay_in_ref[...]
        else:
            decay_ref[...] = jnp.zeros_like(decay_ref)
            row_decay_ref[...] = jnp.zeros_like(row_decay_ref)

    def query_tile(tile):
        here = tile_of(tile, Q_TILE)
        queries = query_tiles(q_ref, t_query_ref, place, here, 64**-0.5)
        begin_row = begin_ref[0:1, here]
        grad = grad_ref[here, :]
        nothing = jnp.zeros_like(grad)
        grads = (jnp.where(lane < 64, grad, nothing), jnp.where(lane < 64, nothing, grad))
        product = grad.astype(f32) * o_ref[here, :].astype(f32)
        inner = dot(pick, product, NT, precision=lax.Precision.HIGHEST)
        for dq in dqs:
            dq[...] = jnp.zeros_like(dq)

        def step(masked, number, state):
            there = tile_of(number, K_TILE)
            if masked:
                allowed = allowed_pairs(base + number * K_TILE, tile, rows, begin_row)
            value = v_ref[there, :]
            value_part = 0.0
            for h in range(2):
                scores = dot(keys[h][there, :], queries[h], NT)
                prob = jnp.exp(scores - lse_ref[h : h + 1, here])
                if masked:
                    prob = jnp.where(allowed, prob, 0.0)
                grad_prob = dot(value, grads[h], NT)
                grad_score = (prob * (grad_prob - inner[h : h + 1, :])).astype(bf16)
                value_part = value_part + dot(prob.astype(bf16), grads[h])
                dks[h][there, :] += dot(grad_score, queries[h])
                dqs[h][...] += dot(keys_t[h][:, there], grad_score)
            dv[there, :] += value_part
            return state

        key_loops(ranges_ref, tile, rows, own, step, 0)
        turned = [dq[...].T for dq in dqs]
        dq_tile = jnp.where(lane < 64, turned[0], turned[1]) * 64**-0.5
        if own:
            dq_tile = dq_tile + dq_in_ref[here, :]
        dq_ref[here, :] = dq_tile.astype(dq_ref.dtype)
        sums = sums_ref[here, :]
        sums = sums + jnp.where(lane == 2 * pair, turned[0][:, 64:65], 0.0)
        sums = sums + jnp.where(lane == 2 * pair + 1, turned[1][:, 0:1], 0.0)
        sums_ref[here, :] = sums

    def query_loop(tile, carry):
        if own:
            query_tile(tile)
        else:
            reaches = key_range(ranges_ref, tile, rows, own)[0] < rows // K_TILE
            pl.when(reaches)(lambda: query_tile(tile))

            @pl.when(jnp.logical_not(reaches))
            def _():
                dq_ref[tile_of(tile, Q_TILE), :] = jnp.zeros((Q_TILE, LANES), dq_ref.dtype)

        return carry

    lax.fori_loop(0, rows // Q_TILE, query_loop, 0)
    sign = -1.0 if own else 1.0

    def finish(n, carry):
        here = tile_of(n, Q_TILE)
        left, right = dk0[here, :], dk1[here, :]
        dk_ref[here, :] = jnp.where(lane < 64, left, right).astype(dk_ref.dtype)
        dv_ref[here, :] = dv[here, :].astype(dv_ref.dtype)
        decay = decay_ref[here, :]
        decay = decay + jnp.where(lane == 2 * pair, sign * left[:, 67:68], 0.0)
        decay = decay + jnp.where(lane == 2 * pair + 1, sign * right[:, 3:4], 0.0)
        decay_ref[here, :] = decay
        return carry

    lax.fori_loop(0, rows // Q_TILE, finish, 0)


def attend_back(
    own, ranges, query, key_value, terms, key_terms, begins, grad, mixed, lse, local_heads,
    so_far=(),
):
    rows = query.shape[0]
    pairs = local_heads // 2
    wide = jax.ShapeDtypeStruct((rows, pairs * LANES), f32)
    sums = jax.ShapeDtypeStruct((rows, LANES), f32)
    if own:
        out_specs = [lane_block(rows, 0)] * 3 + [fixed((rows, LANES))]
        out_shape = (jax.ShapeDtypeStruct(wide.shape, bf16), wide, wide, sums)
    else:
        both = pl.BlockSpec((2, rows, LANES), lambda p, *_: (0, 0, p))
        out_specs = [lane_block(rows, 0), fixed((rows, LANES)), both, fixed((rows, LANES))]
        out_shape = (
            wide, sums, jax.ShapeDtypeStruct((2, rows, pairs * LANES), bf16), sums,
        )
    return pl.pallas_call(
        functools.partial(attend_back_kernel, local_heads, own),
        grid_spec=pltpu.PrefetchScalarGridSpec(
            num_scalar_prefetch=1,
            grid=(pairs,),
            in_specs=[
                lane_block(rows, 0),
                lane_block(rows, 0),
                lane_block(rows, pairs),
                fixed((rows, LANES)),
                fixed((rows, LANES) if own else (TERM_ROWS, rows)),
                fixed((8, rows)),
                lane_block(rows, 0),
                lane_block(rows, 0),
                pair_block(8, rows),
            ]
            + ([lane_block(rows, 0), fixed((rows, LANES))] if own else []),
            out_specs=out_specs,
            scratch_shapes=[
                pltpu.VMEM((rows, LANES), bf16),
                pltpu.VMEM((rows, LANES), bf16),
                pltpu.VMEM((LANES, rows), bf16),
                pltpu.VMEM((LANES, rows), bf16),
                pltpu.VMEM((rows, LANES), f32),
                pltpu.VMEM((rows, LANES), f32),
                pltpu.VMEM((rows, LANES), f32),
                pltpu.VMEM((LANES, Q_TILE), f32),
                pltpu.VMEM((LANES, Q_TILE), f32),
            ],
        ),
        out_shape=out_shape,
        cost_estimate=pl.CostEstimate(
            flops=80_000_000_000 if own else 15_000_000_000,
            transcendentals=20_000_000,
            bytes_accessed=25_000_000,
        ),
        name="attend_back_own" if own else "attend_back_prev",
    )(
        ranges, query, key_value, key_value, terms, key_terms, begins, grad, mixed, lse, *so_far
    )


PIECES = 4


def partners():
    me = lax.axis_index("head")
    near = me + 1 - 2 * (me % 2)
    far = (me + 2) % 4
    cross = (near + 2) % 4
    return me, near, far, cross


def signal(other):
    pl.semaphore_signal(
        pltpu.get_barrier_semaphore(), inc=1, device_id=other, device_id_type=pl.DeviceIdType.MESH
    )


def greet(others):
    for other in others:
        signal(other)
    pl.semaphore_wait(pltpu.get_barrier_semaphore(), len(others))


def remote(source, target, send, receive, other):
    return pltpu.make_async_remote_copy(
        src_ref=source,
        dst_ref=target,
        send_sem=send,
        recv_sem=receive,
        device_id=other,
        device_id_type=pl.DeviceIdType.MESH,
    )


def on_head(index):
    return {"head": index}


def on_blk(index):
    return {"blk": index}


def piece_at(ref, slot, piece, size):
    span = size // PIECES
    return ref.at[pl.ds(pl.multiple_of(slot * size + piece * span, span), span), :]


class Slots:
    def __init__(self, by_device):
        me, near, far, cross = partners()
        if by_device:
            self.own = self.sent_near = self.sent_far = me
            self.near, self.far, self.cross = near, far, cross
            self.passed = far
        else:
            self.own, self.sent_near, self.sent_far = 3, 2, 1
            self.near, self.far, self.cross = 2, 1, 0
            self.passed = 0


def spread_piece(source, all_ref, size, sems, piece, slots):
    me, near, far, _ = partners()
    far_send, far_recv, near_send, near_recv, _, _, own = sems
    copies = (
        remote(source, piece_at(all_ref, slots.sent_far, piece, size), far_send.at[piece],
               far_recv.at[piece], on_head(far)),
        remote(source, piece_at(all_ref, slots.sent_near, piece, size), near_send.at[piece],
               near_recv.at[piece], on_head(near)),
        pltpu.make_async_copy(source, piece_at(all_ref, slots.own, piece, size), own.at[piece]),
    )
    for copy in copies:
        copy.start()
    return copies


def hand_on(all_ref, size, sems, sent, slots):
    me, near, far, cross = partners()
    far_send, far_recv, near_send, near_recv, on_send, on_recv, own = sems
    passed = []
    for piece in range(PIECES):
        there = piece_at(all_ref, slots.far, piece, size)
        remote(there, there, far_send.at[piece], far_recv.at[piece], on_head(far)).wait_recv()
        copy = remote(
            there, piece_at(all_ref, slots.passed, piece, size), on_send.at[piece],
            on_recv.at[piece], on_head(near),
        )
        copy.start()
        passed.append(copy)

    def finish():
        for piece in range(PIECES):
            to_far, to_near, local = sent[piece]
            to_far.wait_send()
            to_near.wait_send()
            local.wait()
            passed[piece].wait_send()
            there = piece_at(all_ref, slots.near, piece, size)
            remote(there, there, near_send.at[piece], near_recv.at[piece], on_head(near)).wait_recv()
            there = piece_at(all_ref, slots.cross, piece, size)
            remote(there, there, on_send.at[piece], on_recv.at[piece], on_head(near)).wait_recv()

    return finish


def gather_sems():
    return [pltpu.SemaphoreType.DMA((PIECES,)) for _ in range(7)]


def blk_peers():
    here = lax.axis_index("blk")
    half = lax.axis_size("blk") // 2
    low, high = here % 2, here // 2
    partner = here + 1 - 2 * low
    after = [((high + t) % half) * 2 + low for t in range(half)]
    return here, partner, after


class Line:
    def __init__(self, block_of, kinds, sems):
        self.block_of, self.kinds = block_of, kinds
        self.pair_send, self.pair_recv, self.up_send, self.up_recv, self.down_send, self.down_recv = sems
        here = lax.axis_index("blk")
        self.half = lax.axis_size("blk") // 2
        self.low, self.high = here % 2, here // 2
        self.partner = here + 1 - 2 * self.low
        self.has_up, self.has_down = self.high < self.half - 1, self.high > 0

    def greet(self, others):
        greet_sum = len(others) + 1
        for other in others + [on_blk(self.partner)]:
            signal(other)
        pl.when(self.has_up)(lambda: signal(on_blk(self.at(self.high + 1))))
        pl.when(self.has_down)(lambda: signal(on_blk(self.at(self.high - 1))))
        ends = (self.high == 0).astype(jnp.int32) + (self.high == self.half - 1).astype(jnp.int32)
        pl.semaphore_wait(pltpu.get_barrier_semaphore(), greet_sum + 2 - ends)

    def at(self, high):
        return high * 2 + self.low

    def pair_copy(self, kind, high, low):
        block = self.block_of(kind, high * 2 + low)
        return remote(
            block, block, self.pair_send.at[kind, high], self.pair_recv.at[kind, high],
            on_blk(self.partner),
        )

    def up_copy(self, kind, high):
        block = self.block_of(kind, self.at(high))
        return remote(
            block, block, self.up_send.at[kind, high], self.up_recv.at[kind, high],
            on_blk(self.at(jnp.minimum(self.high + 1, self.half - 1))),
        )

    def down_copy(self, kind, high):
        block = self.block_of(kind, self.at(high))
        return remote(
            block, block, self.down_send.at[kind, high], self.down_recv.at[kind, high],
            on_blk(self.at(jnp.maximum(self.high - 1, 0))),
        )

    def launch(self, kind):
        self.pair_copy(kind, self.high, self.low).start()
        pl.when(self.has_up)(lambda: self.up_copy(kind, self.high).start())
        pl.when(self.has_down)(lambda: self.down_copy(kind, self.high).start())

    def step(self, t):
        for kind in range(self.kinds):
            below, above = self.high - t, self.high + t

            @pl.when(below >= 0)
            def _():
                self.up_copy(kind, below).wait_recv()
                self.pair_copy(kind, below, self.low).start()
                pl.when(self.has_up)(lambda: self.up_copy(kind, below).start())

            @pl.when(above < self.half)
            def _():
                self.down_copy(kind, above).wait_recv()
                self.pair_copy(kind, above, self.low).start()
                pl.when(self.has_down)(lambda: self.down_copy(kind, above).start())

    def finish(self):
        for kind in range(self.kinds):

            def wait(high, carry):
                self.pair_copy(kind, high, self.low).wait_send()
                self.pair_copy(kind, high, 1 - self.low).wait_recv()

                @pl.when((high <= self.high) & self.has_up)
                def _():
                    self.up_copy(kind, high).wait_send()

                @pl.when((high >= self.high) & self.has_down)
                def _():
                    self.down_copy(kind, high).wait_send()

                return carry

            lax.fori_loop(0, self.half, wait, 0)


def gather_first_kernel(pack_ref, tokens_ref, cotangent_ref, pack_all, tokens_all, cotangent_all,
                        *sems):
    swap_send, swap_recv, swap_own = sems[:3]
    token_sems, cotangent_sems = sems[9:16], sems[16:23]
    me, near, far, cross = partners()
    sources = (me, near, far, cross)
    line = Line(lambda kind, blk: pack_all.at[blk, sources[kind]], 4, sems[3:9])
    here = lax.axis_index("blk")
    line.greet([on_head(near), on_head(far), on_head(cross)])
    swaps = [pltpu.make_async_copy(pack_ref.at[me], pack_all.at[here, me], swap_own)]
    for kind, other in enumerate((near, far, cross)):
        swaps.append(
            remote(
                pack_ref.at[other],
                pack_all.at[here, me],
                swap_send.at[kind],
                swap_recv.at[kind],
                on_head(other),
            )
        )
    for swap in swaps:
        swap.start()
    size = tokens_ref.shape[0]
    span = size // PIECES

    def spread_all(ref, all_ref, some, slots):
        return [
            spread_piece(ref.at[pl.ds(piece * span, span), :], all_ref, size, some, piece, slots)
            for piece in range(PIECES)
        ]

    by_device, crossing = Slots(True), Slots(False)
    tokens_sent = spread_all(tokens_ref, tokens_all, token_sems, by_device)
    swaps[0].wait()
    line.launch(0)
    for kind, source in enumerate((near, far, cross)):
        block = pack_all.at[here, source]
        remote(
            block, block, swap_send.at[kind], swap_recv.at[kind], on_head(source)
        ).wait_recv()
        line.launch(kind + 1)
    cotangent_sent = spread_all(cotangent_ref, cotangent_all, cotangent_sems, crossing)
    for t in range(1, line.half):
        line.step(t)
    finish_tokens = hand_on(tokens_all, size, token_sems, tokens_sent, by_device)
    finish_cotangent = hand_on(cotangent_all, size, cotangent_sems, cotangent_sent, crossing)
    for swap in swaps[1:]:
        swap.wait_send()
    line.finish()
    finish_tokens()
    finish_cotangent()


def gather_first(pack, tokens, cotangent, number):
    groups, share, columns = pack.shape
    peers = lax.axis_size("blk")
    rows, width = tokens.shape
    whole = jax.ShapeDtypeStruct((groups * rows, width), bf16)
    vmem, anywhere = pl.BlockSpec(memory_space=pltpu.VMEM), pl.BlockSpec(memory_space=pl.ANY)
    all_pack, all_tokens, all_cotangent = pl.pallas_call(
        gather_first_kernel,
        in_specs=[vmem] * 3,
        out_specs=[anywhere] * 3,
        out_shape=[jax.ShapeDtypeStruct((peers, groups, share, columns), bf16), whole, whole],
        scratch_shapes=[
            pltpu.SemaphoreType.DMA((3,)),
            pltpu.SemaphoreType.DMA((3,)),
            pltpu.SemaphoreType.DMA,
        ]
        + [pltpu.SemaphoreType.DMA((4, peers // 2)) for _ in range(6)]
        + gather_sems()
        + gather_sems(),
        compiler_params=pltpu.CompilerParams(collective_id=number, has_side_effects=True),
        cost_estimate=pl.CostEstimate(
            flops=70_000_000_000, transcendentals=0, bytes_accessed=30_000_000
        ),
        name="gather_first",
    )(pack, tokens, cotangent)
    return all_pack.reshape(peers * groups * share, columns), all_tokens, all_cotangent


class Sum:
    def __init__(self, part_ref, buffers, sems, size, by_device):
        self.part_ref, self.size, self.span = part_ref, size, size // PIECES
        self.slots = Slots(by_device)
        self.near_buf, self.turn_buf, self.far_buf = buffers
        self.near_send, self.near_recv, self.far_send, self.far_recv = sems
        self.near_copies, self.far_copies = [], []

    def piece(self, n):
        return slice(n * self.span, (n + 1) * self.span)

    def start(self):
        me, near, far, cross = partners()
        for which, shard in ((0, self.slots.cross), (1, self.slots.near)):
            for n in range(PIECES):
                copy = remote(
                    piece_at(self.part_ref, shard, n, self.size),
                    self.near_buf.at[which, pl.ds(n * self.span, self.span), :],
                    self.near_send.at[which, n],
                    self.near_recv.at[which, n],
                    on_head(near),
                )
                copy.start()
                self.near_copies.append(copy)

    def turn(self):
        me, near, far, cross = partners()
        for n in range(PIECES):
            here = self.piece(n)
            self.near_copies[n].wait_recv()
            self.turn_buf[here, :] = (
                piece_at(self.part_ref, self.slots.far, n, self.size)[...].astype(f32)
                + self.near_buf[0, here, :].astype(f32)
            ).astype(bf16)
            copy = remote(
                self.turn_buf.at[pl.ds(n * self.span, self.span), :],
                self.far_buf.at[pl.ds(n * self.span, self.span), :],
                self.far_send.at[n],
                self.far_recv.at[n],
                on_head(far),
            )
            copy.start()
            self.far_copies.append(copy)

    def total(self, n):
        self.near_copies[PIECES + n].wait_recv()
        self.far_copies[n].wait_recv()
        here = self.piece(n)
        return (
            piece_at(self.part_ref, self.slots.own, n, self.size)[...].astype(f32)
            + self.near_buf[1, here, :].astype(f32)
            + self.far_buf[here, :].astype(f32)
        )

    def finish(self):
        for copy in self.near_copies + self.far_copies:
            copy.wait_send()


def sum_buffers(size, width):
    return [
        pltpu.VMEM((2, size, width), bf16),
        pltpu.VMEM((size, width), bf16),
        pltpu.VMEM((size, width), bf16),
    ]


def sum_sems():
    return [
        pltpu.SemaphoreType.DMA((2, PIECES)),
        pltpu.SemaphoreType.DMA((2, PIECES)),
        pltpu.SemaphoreType.DMA((PIECES,)),
        pltpu.SemaphoreType.DMA((PIECES,)),
    ]


def column_chunks(width):
    count = max(width // 512, 1)
    first = width - 512 * (count - 1)
    return [(0, first)] + [(first + 512 * n, 512) for n in range(count - 1)]


class RowSums:
    def __init__(self, arrays, sems):
        self.pair_send, self.pair_recv, self.line_send, self.line_recv = sems
        self.here, self.partner, self.after = blk_peers()
        self.steps = len(self.after)
        self.chunks = [
            array + (pl.ds(start, wide),)
            for array in arrays
            for start, wide in column_chunks(array[0].shape[3])
        ]
        self.sent = []

    def others(self):
        return [on_blk(self.partner)] + [on_blk(peer) for peer in self.after[1:]]

    def pair_wait(self, c, t):
        _, pair_buf, _, _, at = self.chunks[c]
        block = pair_buf.at[t, :, :, at]
        remote(
            block, block, self.pair_send.at[c, t], self.pair_recv.at[c, t], on_blk(self.partner)
        ).wait_recv()

    def start(self):
        for c, (ref, pair_buf, _, _, at) in enumerate(self.chunks):
            for t in list(range(1, self.steps)) + [0]:
                copy = remote(
                    ref.at[self.after[t] + self.partner - self.here, :, :, at],
                    pair_buf.at[t, :, :, at],
                    self.pair_send.at[c, t],
                    self.pair_recv.at[c, t],
                    on_blk(self.partner),
                )
                copy.start()
                self.sent.append(copy)

    def pass_on(self, c):
        ref, pair_buf, line_buf, _, at = self.chunks[c]
        for t in range(1, self.steps):
            self.pair_wait(c, t)

            def add(group, carry):
                pair_buf[t, group, :, at] = (
                    ref[self.after[t], group, :, at].astype(f32)
                    + pair_buf[t, group, :, at].astype(f32)
                ).astype(bf16)
                return carry

            lax.fori_loop(0, ref.shape[1], add, 0)
            copy = remote(
                pair_buf.at[t, :, :, at], line_buf.at[t, :, :, at], self.line_send.at[c, t],
                self.line_recv.at[c, t], on_blk(self.after[t]),
            )
            copy.start()
            self.sent.append(copy)

    def add_up(self, c):
        ref, pair_buf, line_buf, out_ref, at = self.chunks[c]
        self.pair_wait(c, 0)
        for t in range(1, self.steps):
            block = line_buf.at[t, :, :, at]
            remote(
                block, block, self.line_send.at[c, t], self.line_recv.at[c, t],
                on_blk(self.after[t]),
            ).wait_recv()

        def add_all(group, carry):
            total = ref[self.here, group, :, at].astype(f32)
            total = total + pair_buf[0, group, :, at].astype(f32)
            for t in range(1, self.steps):
                total = total + line_buf[t, group, :, at].astype(f32)
            out_ref[group, :, at] = total.astype(bf16)
            return carry

        lax.fori_loop(0, ref.shape[1], add_all, 0)

    def finish(self):
        for copy in self.sent:
            copy.wait_send()


def row_sum_buffers(half, groups, share, columns):
    return [pltpu.VMEM((half, groups, share, columns), bf16) for _ in range(2)]


def row_sum_sems(chunks, half):
    return [pltpu.SemaphoreType.DMA((chunks, half)) for _ in range(4)]


def exchange_kernel(local, extras, summed, *refs):
    part_ref, extra_refs, refs = refs[0], refs[1 : 1 + extras], refs[1 + extras :]
    if summed:
        out_ref, all_ref, payload, *sems = refs
    else:
        mine_ref, out_ref, all_ref, weight_ref, payload, *sems = refs
    size = out_ref.shape[0]
    span = size // PIECES
    _, near, far, _ = partners()
    slots = Slots(summed)
    if summed:
        greet([on_head(near), on_head(far)])
    else:
        kinds = mine_ref.shape[0]
        beside = Line(lambda kind, blk: weight_ref.at[blk, kind], kinds, sems[-7:-1])
        own = pltpu.make_async_copy(mine_ref, weight_ref.at[lax.axis_index("blk")], sems[-1])
        own.start()
        beside.greet([on_head(near), on_head(far)])
        shares = Sum(part_ref, sems[7:10], sems[10:14], size, True)
        shares.start()
        own.wait()
        for kind in range(kinds):
            beside.launch(kind)
        shares.turn()
    sent = []
    for piece in range(PIECES):
        if not summed and piece != 2:
            hop = {0: 1, 1: 2, 3: 3}[piece]
            for t in range(hop, beside.half if piece == 3 else min(hop + 1, beside.half)):
                beside.step(t)
        here = slice(piece * span, (piece + 1) * span)
        total = part_ref[here, :] if summed else shares.total(piece)
        result, share = local(total, here, *extra_refs)
        out_ref[here, :] = result.astype(out_ref.dtype)
        payload[here, :] = share.astype(bf16)
        source = payload.at[pl.ds(piece * span, span), :]
        sent.append(spread_piece(source, all_ref, size, sems[:7], piece, slots))
    hand_on(all_ref, size, sems[:7], sent, slots)()
    if not summed:
        shares.finish()
        beside.finish()


def exchange(local, part, extras, summed, number, name, mine=None):
    rows, width = part.shape
    size = rows if summed else rows // 4
    peers = lax.axis_size("blk")
    vmem, anywhere = pl.BlockSpec(memory_space=pltpu.VMEM), pl.BlockSpec(memory_space=pl.ANY)
    inputs = [part, *extras]
    out_specs = [vmem, anywhere]
    out_shape = [
        jax.ShapeDtypeStruct((size, width), f32),
        jax.ShapeDtypeStruct((4 * size, width), bf16),
    ]
    scratch = [pltpu.VMEM((size, width), bf16)] + gather_sems()
    if not summed:
        inputs.append(mine)
        out_specs.append(anywhere)
        out_shape.append(jax.ShapeDtypeStruct((peers,) + mine.shape, bf16))
        scratch += sum_buffers(size, width) + sum_sems()
        scratch += [pltpu.SemaphoreType.DMA((mine.shape[0], peers // 2)) for _ in range(6)]
        scratch.append(pltpu.SemaphoreType.DMA)
    return pl.pallas_call(
        functools.partial(exchange_kernel, local, len(extras), summed),
        in_specs=[vmem] * len(inputs),
        out_specs=out_specs,
        out_shape=out_shape,
        scratch_shapes=scratch,
        compiler_params=pltpu.CompilerParams(collective_id=number, has_side_effects=True),
        cost_estimate=pl.CostEstimate(
            flops=40_000_000_000 if summed else 80_000_000_000,
            transcendentals=0,
            bytes_accessed=16_000_000,
        ),
        name=name,
    )(*inputs)


def finish_last_kernel(grads_ref, first_ref, grad_ref, output_grad_ref, down_grad_ref, second_ref,
                       grad_middle_ref, tokens_ref, gain_ref, weights_ref, output_ref, down_ref,
                       second_out_ref, tokens_grad_ref, part_buf, *refs):
    swap_send, swap_recv = refs[13:15]
    me, near, far, cross = partners()
    others = (near, far, cross)
    arrays = (down_grad_ref, grad_ref, output_grad_ref)
    sums = RowSums([(array,) + refs[3 * n : 3 * n + 3] for n, array in enumerate(arrays)], refs[9:13])
    outs = [
        out_ref
        for array, out_ref in zip(arrays, (down_ref, weights_ref, output_ref))
        for _ in column_chunks(array.shape[3])
    ]
    greet([on_head(other) for other in others] + sums.others())
    size = tokens_grad_ref.shape[0]
    first = Sum(part_buf, refs[15:18], refs[18:22], size, True)
    sums.start()
    sent = []

    def swap(source_ref, out_ref, c):
        for kind, other in enumerate(others):
            copy = remote(
                source_ref.at[other], out_ref.at[me], swap_send.at[c, kind],
                swap_recv.at[c, kind], on_head(other),
            )
            copy.start()
            sent.append(copy)

    count = len(sums.chunks)
    swap(second_ref, second_out_ref, count)
    columns = grads_ref.shape[1]
    tiles = part_buf.shape[0] // 256

    def multiply(n, carry):
        here = tile_of(n, 256)
        part_buf[here, :] = dot(grads_ref[here, :], first_ref[:, :columns], NT).astype(bf16)
        return carry

    def add_up(c):
        sums.add_up(c)
        _, _, _, row_ref, at = sums.chunks[c]
        outs[c][me, :, at] = row_ref[me, :, at]
        swap(row_ref.at[:, :, at], outs[c].at[:, :, at], c)

    lax.fori_loop(0, tiles // 2, multiply, 0)
    sums.pass_on(0)
    lax.fori_loop(tiles // 2, tiles, multiply, 0)
    first.start()
    for c in range(1, count):
        sums.pass_on(c)
        if c == 1:
            first.turn()
        add_up(c - 1)
    for piece in range(PIECES):
        rows = first.piece(piece)
        tokens_grad_ref[rows, :], _ = after_first(
            first.total(piece), rows, grad_middle_ref, tokens_ref, gain_ref
        )
    add_up(count - 1)
    second_out_ref[me] = second_ref[me]
    for c in range(count + 1):
        if c < count:
            out_ref = outs[c].at[:, :, sums.chunks[c][4]]
        else:
            out_ref = second_out_ref
        for kind, other in enumerate(others):
            block = out_ref.at[other]
            remote(
                block, block, swap_send.at[c, kind], swap_recv.at[c, kind], on_head(other)
            ).wait_recv()
    for copy in sent:
        copy.wait_send()
    sums.finish()
    first.finish()


def finish_last(grads, first, grad, output_grad, down_grad, second, groups, grad_middle, tokens,
                gain, number):
    peers = lax.axis_size("blk")
    share = grad.shape[0] // (peers * groups)
    rows, width = tokens.shape
    vmem = pl.BlockSpec(memory_space=pltpu.VMEM)
    half = peers // 2
    arrays = (down_grad, grad, output_grad)
    chunks = sum(len(column_chunks(array.shape[1])) for array in arrays)

    def blocks(array):
        return array.reshape(peers, groups, share, array.shape[1])

    def parts(array):
        return jax.ShapeDtypeStruct((groups, share, array.shape[1]), bf16)

    row_sum_scratch = []
    for array in arrays:
        row_sum_scratch += row_sum_buffers(half, groups, share, array.shape[1])
        row_sum_scratch.append(pltpu.VMEM((groups, share, array.shape[1]), bf16))
    return pl.pallas_call(
        finish_last_kernel,
        in_specs=[vmem] * 9,
        out_specs=[vmem] * 5,
        out_shape=[
            parts(grad), parts(output_grad), parts(down_grad), parts(second),
            jax.ShapeDtypeStruct((rows, width), f32),
        ],
        scratch_shapes=[pltpu.VMEM((4 * rows, width), bf16)]
        + row_sum_scratch
        + row_sum_sems(chunks, half)
        + [pltpu.SemaphoreType.DMA((chunks + 1, 3)) for _ in range(2)]
        + sum_buffers(rows, width)
        + sum_sems(),
        compiler_params=pltpu.CompilerParams(
            collective_id=number, has_side_effects=True, vmem_limit_bytes=63 << 20
        ),
        cost_estimate=pl.CostEstimate(
            flops=110_000_000_000, transcendentals=0, bytes_accessed=40_000_000
        ),
        name="finish_last",
    )(
        grads, first, blocks(grad), blocks(output_grad), blocks(down_grad),
        second.reshape(groups, share, second.shape[1]), grad_middle, tokens, gain,
    )


def inverse_rms(value):
    return lax.rsqrt(jnp.mean(value * value, axis=1, keepdims=True) + epsilon)


def through_norm(grad, value):
    factor = inverse_rms(value)
    normed = value * factor
    return factor * (grad - normed * jnp.mean(grad * normed, axis=1, keepdims=True))


def after_attention(total, here, tokens_ref, gain_ref):
    middle = tokens_ref[here, :].astype(f32) + total
    return middle, middle * inverse_rms(middle) * gain_ref[0:1, :]


def after_hidden(total, here, cotangent_ref, middle_ref, gain_ref):
    grad = cotangent_ref[here, :].astype(f32) + through_norm(
        total * gain_ref[0:1, :], middle_ref[here, :]
    )
    return grad, grad


def after_first(total, here, grad_ref, tokens_ref, gain_ref):
    grad = grad_ref[here, :] + through_norm(
        total * gain_ref[0:1, :], tokens_ref[here, :].astype(f32)
    )
    return grad, None


FEED_TILE = 256
FEED_COLUMNS = 512


def feed_kernel(input_ref, cotangent_ref, weight_ref, down_weight_ref, down_ref, grad_ref, grad_down_ref,
                total_ref, acts, turned0, turned1, stage, near_buf, far_buf, down_stage, near_send,
                near_recv, far_send, far_recv, down_sems):
    step = pl.program_id(0)
    hidden_width = down_weight_ref.shape[1]
    size = total_ref.shape[0]
    per = size // FEED_TILE
    tiles = 4 * per
    me, near, far, cross = partners()

    @pl.when(step == 0)
    def _():
        greet([on_head(near), on_head(far)])

    def down_copy(at):
        shard = sum(jnp.where(at // per == n, s, 0) for n, s in enumerate((cross, far, near, me)))
        row = pl.multiple_of(shard * size + (at % per) * FEED_TILE, FEED_TILE)
        return pltpu.make_async_copy(
            down_stage.at[at % 2], down_ref.at[pl.ds(row, FEED_TILE), :], down_sems.at[at % 2]
        )

    def to_near(which, piece):
        return remote(
            stage.at[which * per + piece],
            near_buf.at[which, piece],
            near_send.at[which, piece],
            near_recv.at[which, piece],
            on_head(near),
        )

    def to_far(piece):
        return remote(
            near_buf.at[0, piece], far_buf.at[piece], far_send.at[piece], far_recv.at[piece],
            on_head(far),
        )

    @pl.when(step < tiles)
    def _():
        here = tile_of(step, FEED_TILE)
        inputs, cotangent = input_ref[...], cotangent_ref[...]
        turned0[:, here] = inputs.T
        turned1[:, here] = cotangent.T
        gate_at, up_at, down_at = (
            slice(n * hidden_width, (n + 1) * hidden_width) for n in range(3)
        )
        gate = dot(inputs, weight_ref[:, gate_at])
        up = dot(inputs, weight_ref[:, up_at])
        grad_hidden = dot(cotangent, down_weight_ref[...])
        opening = jax.nn.sigmoid(gate)
        active = gate * opening
        hidden = (active * up).astype(bf16)
        grad_gate = (grad_hidden * up * opening * (1.0 + gate * (1.0 - opening))).astype(bf16)
        grad_up = (grad_hidden * active).astype(bf16)
        acts[here, gate_at] = grad_gate
        acts[here, up_at] = grad_up
        acts[here, down_at] = hidden
        pl.when(step >= 2)(lambda: down_copy(step - 2).wait())
        down_stage[step % 2] = dot(hidden, down_weight_ref[...], NT).astype(bf16)
        down_copy(step).start()
        back = dot(grad_gate, weight_ref[:, gate_at], NT) + dot(
            grad_up, weight_ref[:, up_at], NT
        )
        for piece in range(per):
            for which, first in ((0, 0), (1, 2 * per)):

                @pl.when(step == first + piece)
                def _():
                    stage[which * per + piece] = back.astype(bf16)
                    to_near(which, piece).start()

            @pl.when(step == per + piece)
            def _():
                to_near(0, piece).wait_recv()
                near_buf[0, piece] = (back + near_buf[0, piece].astype(f32)).astype(bf16)
                to_far(piece).start()

            @pl.when(step == 3 * per + piece)
            def _():
                total_ref[piece * FEED_TILE : (piece + 1) * FEED_TILE, :] = back

    @pl.when(step >= tiles)
    def _():
        at = tile_of(step - tiles, FEED_COLUMNS)
        from_input = (step - tiles) * FEED_COLUMNS < 2 * hidden_width

        @pl.when(from_input)
        def _():
            grad_ref[...] = dot(turned0[...], acts[:, at]).astype(bf16)

        @pl.when(jnp.logical_not(from_input))
        def _():
            grad_down_ref[...] = dot(turned1[...], acts[:, at]).astype(bf16)

    @pl.when(step == pl.num_programs(0) - 1)
    def _():
        down_copy(tiles - 2).wait()
        down_copy(tiles - 1).wait()
        for piece in range(per):
            here = slice(piece * FEED_TILE, (piece + 1) * FEED_TILE)
            to_near(1, piece).wait_recv()
            to_far(piece).wait_recv()
            total_ref[here, :] += near_buf[1, piece].astype(f32) + far_buf[piece].astype(f32)
            to_near(0, piece).wait_send()
            to_near(1, piece).wait_send()
            to_far(piece).wait_send()


def feed(inputs, cotangent, weight, down_weight, number):
    rows, width = inputs.shape
    columns = weight.shape[1] + down_weight.shape[1]
    size = rows // 4
    tiles, per = rows // FEED_TILE, size // FEED_TILE
    wide = weight.shape[1] // FEED_COLUMNS
    tile = pl.BlockSpec((FEED_TILE, width), lambda n: (jnp.minimum(n, tiles - 1), 0))

    def whole(shape):
        return pl.BlockSpec(shape, lambda n: (0, 0), pipeline_mode=pl.Buffered(1))

    return pl.pallas_call(
        feed_kernel,
        grid=(tiles + columns // FEED_COLUMNS,),
        in_specs=[tile, tile, whole(weight.shape), whole(down_weight.shape)],
        out_specs=[
            pl.BlockSpec(memory_space=pl.ANY),
            pl.BlockSpec((width, FEED_COLUMNS), lambda n: (0, jnp.clip(n - tiles, 0, wide - 1))),
            pl.BlockSpec((width, FEED_COLUMNS), lambda n: (0, jnp.maximum(n - tiles - wide, 0))),
            whole((size, width)),
        ],
        out_shape=[
            jax.ShapeDtypeStruct((rows, width), bf16),
            jax.ShapeDtypeStruct((width, weight.shape[1]), bf16),
            jax.ShapeDtypeStruct((width, down_weight.shape[1]), bf16),
            jax.ShapeDtypeStruct((size, width), f32),
        ],
        scratch_shapes=[
            pltpu.VMEM((rows, columns), bf16),
            pltpu.VMEM((width, rows), bf16),
            pltpu.VMEM((width, rows), bf16),
            pltpu.VMEM((2 * per, FEED_TILE, width), bf16),
            pltpu.VMEM((2, per, FEED_TILE, width), bf16),
            pltpu.VMEM((per, FEED_TILE, width), bf16),
            pltpu.VMEM((2, FEED_TILE, width), bf16),
            pltpu.SemaphoreType.DMA((2, per)),
            pltpu.SemaphoreType.DMA((2, per)),
            pltpu.SemaphoreType.DMA((per,)),
            pltpu.SemaphoreType.DMA((per,)),
            pltpu.SemaphoreType.DMA((2,)),
        ],
        compiler_params=pltpu.CompilerParams(
            collective_id=number, has_side_effects=True, vmem_limit_bytes=63 << 20
        ),
        cost_estimate=pl.CostEstimate(
            flops=6 * rows * width * columns, transcendentals=rows * columns // 3,
            bytes_accessed=45_000_000,
        ),
        name="feed",
    )(inputs, cotangent, weight, down_weight)


def over_tokens(operand, other_side):
    return lax.dot_general(
        operand, other_side, (((0,), (0,)), ((), ())), preferred_element_type=f32
    )


def sent_columns(pieces, groups):
    packed = jnp.concatenate(
        [piece.reshape(piece.shape[0], groups, -1) for piece in pieces], axis=2
    )
    mine = lax.all_to_all(packed, "head", split_axis=1, concat_axis=0, tiled=True)
    return mine.reshape(mine.shape[0], mine.shape[2])


def all_rows(mine):
    return lax.all_gather(mine, "blk", axis=0, tiled=True)


def row_sums(grad):
    return lax.psum_scatter(grad, "blk", scatter_dimension=0, tiled=True)


def body(
    tokens,
    segment,
    norm1_gain,
    w_query,
    w_key,
    w_value,
    w_gate_out,
    w_forget,
    forget_bias,
    w_output,
    norm2_gain,
    w_gate,
    w_up,
    w_down,
    cotangent,
):
    token_rows, model_width = tokens.shape
    groups = lax.axis_size("head")
    head_count = forget_bias.shape[0]
    local_heads = head_count // groups
    local_width = model_width // groups
    hidden_width = w_gate.shape[1] // groups
    rows = token_rows * groups
    share = w_query.shape[0]
    group = lax.axis_index("head")

    low = lambda array: array.astype(bf16)
    spread = lambda gain: jnp.broadcast_to(low(gain)[:, None, None], (share, groups, 1))
    forget_low = low(w_forget).reshape(share, groups, local_heads)
    rest = LANES - local_heads - 2
    small = jnp.concatenate(
        [forget_low, spread(norm1_gain), spread(norm2_gain), jnp.zeros((share, groups, rest), bf16)],
        axis=2,
    )
    pack = jnp.concatenate(
        [
            low(piece).reshape(share, groups, -1)
            for piece in (w_key, w_value, small, w_query, w_gate_out, w_output)
        ],
        axis=2,
    )
    first, tokens_all, cotangent_all = gather_first(
        jnp.swapaxes(pack, 0, 1), tokens, cotangent, 0
    )
    kv_width = 2 * local_width + LANES
    output_weight = first[:, kv_width + 2 * local_width :]

    segment_plus = segment + 1
    earlier_segment = passed_along(segment_plus, "blk", 1)
    window = jnp.concatenate([earlier_segment, segment_plus])
    begins = jnp.sum(
        (window[:, None] < segment_plus[None, :]).astype(jnp.int32), axis=0
    )
    tiles = begins.reshape(rows // Q_TILE, Q_TILE)
    ranges = jnp.stack([tiles[:, 0] // K_TILE, (tiles[:, -1] + K_TILE - 1) // K_TILE])
    begins = jnp.broadcast_to(begins[None, :], (8, rows))

    def gain_rows(column):
        gain = first[:, 2 * local_width + local_heads + column].astype(f32)
        return jnp.broadcast_to(gain[None, :], (8, model_width))

    gain1, gain2 = gain_rows(0), gain_rows(1)
    bias = lax.dynamic_slice_in_dim(forget_bias, group * local_heads, local_heads, 0)
    bias = jnp.broadcast_to(jnp.pad(bias, (0, LANES - local_heads))[None, :], (8, LANES))
    input1, key_value, terms, turned_terms, forget = project(
        tokens_all, gain1, first, bias, 2 * local_width, local_heads
    )
    earlier_kv = passed_along(key_value, "blk", 1)
    earlier_terms = passed_along(turned_terms, "blk", 1)
    query = dot(input1, first[:, kv_width : kv_width + local_width]).astype(bf16)
    gate_raw = dot(
        input1, first[:, kv_width + local_width : kv_width + 2 * local_width]
    )

    so_far = attend(True, ranges, query, key_value, terms, terms, begins, local_heads)
    later = lax.optimization_barrier((low(w_gate), low(w_up), low(w_down), key_value))
    mine = sent_columns(later[:3], groups)
    mine, earlier_kv, earlier_terms, so_far = lax.optimization_barrier(
        (mine, earlier_kv, earlier_terms, so_far)
    )
    second = all_rows(mine[:, : 2 * hidden_width])
    mine_down = mine[:, 2 * hidden_width :].reshape(groups, share, hidden_width)
    attended, lse = attend(
        False, ranges, query, earlier_kv, terms, earlier_terms, begins, local_heads, so_far
    )
    opened = jax.nn.sigmoid(gate_raw)
    attended_wide = attended.astype(f32)
    gated = (opened * attended_wide).astype(bf16)
    branch = dot(gated, output_weight, NT).astype(bf16)
    middle, input2, down_weight = exchange(
        after_attention, branch, [tokens, gain2], False, 1, "exchange_middle", mine_down
    )
    down_weight = down_weight.reshape(model_width, hidden_width)
    down, second_grad, down_grad, grad_input2 = feed(
        input2, cotangent_all, second, down_weight, 4
    )
    second_part = row_sums(second_grad)
    grad_middle, grad_branch = exchange(
        after_hidden, grad_input2, [cotangent, middle, gain2], True, 2, "exchange_hidden"
    )

    grad_gated = dot(grad_branch, output_weight)
    grad_attended = (grad_gated * opened).astype(bf16)
    grad_gate_pre = (grad_gated * attended_wide * opened * (1.0 - opened)).astype(bf16)
    dq_prev, rows_prev, dkv_prev, decay_prev = attend_back(
        False, ranges, query, earlier_kv, terms, earlier_terms, begins, grad_attended, attended,
        lse, local_heads,
    )
    dkv_later = passed_along(dkv_prev, "blk", -1)
    decay_later = passed_along(decay_prev[:, :8], "blk", -1)
    decay_later = jnp.pad(decay_later, ((0, 0), (0, LANES - 8)))
    dq, dk_own, dv_own, decay_own = attend_back(
        True, ranges, query, key_value, terms, terms, begins, grad_attended, attended,
        lse, local_heads, (dq_prev, rows_prev),
    )
    dk = (dk_own + dkv_later[0].astype(f32)).astype(bf16)
    dv = (dv_own + dkv_later[1].astype(f32)).astype(bf16)
    logf_grad = decay_back(decay_own, decay_later)
    forget_grad = jnp.where(
        jnp.arange(LANES)[None, :] < local_heads, logf_grad * jax.nn.sigmoid(-forget), 0.0
    ).astype(bf16)
    grads = jnp.concatenate([dk, dv, forget_grad, dq, grad_gate_pre], axis=1)
    first_grad = over_tokens(input1, grads)
    bias_part = jnp.sum(forget_grad.astype(f32), axis=0)
    row = jnp.arange(model_width)[:, None] % share
    column = jnp.arange(kv_width + 2 * local_width)[None, :]
    spread_bias = jnp.sum(
        jnp.where(row == jnp.arange(LANES)[None, :], bias_part[None, :], 0.0), axis=1, keepdims=True
    )
    first_grad = jnp.where(
        column == 2 * local_width + local_heads, spread_bias, first_grad
    ).astype(bf16)
    output_grad = over_tokens(grad_branch, gated).astype(bf16)
    down, second_part = lax.optimization_barrier((down, second_part))
    first_sum, output_sum, down_sum, second_sum, tokens_grad = finish_last(
        grads, first, first_grad, output_grad, down_grad, second_part, groups, grad_middle, tokens,
        gain1, 3,
    )
    down = lax.psum_scatter(down, "head", scatter_dimension=0, tiled=True)
    result = (middle + down.astype(f32)).astype(bf16)
    first_sum, output_sum, second_sum, down_sum = (
        jnp.swapaxes(array, 0, 1).astype(f32)
        for array in (first_sum, output_sum, second_sum, down_sum)
    )

    def columns(array, start, width):
        return array[:, :, start : start + width].reshape(share, groups * width)

    key_sum, value_sum = (columns(first_sum, n * local_width, local_width) for n in range(2))
    forget_sum = columns(first_sum, 2 * local_width, local_heads)
    bias_total = first_sum[:local_heads, :, 2 * local_width + local_heads].T.reshape(head_count)
    query_sum, gate_out_sum = (
        columns(first_sum, kv_width + n * local_width, local_width) for n in range(2)
    )
    output_total = columns(output_sum, 0, local_width)
    gate_sum, up_sum = (
        columns(second_sum, n * hidden_width, hidden_width) for n in range(2)
    )
    down_sum = columns(down_sum, 0, hidden_width)

    def along(weight, grad):
        return jnp.sum(low(weight).astype(f32) * grad, axis=1)

    gain1_total = (
        along(w_query, query_sum)
        + along(w_key, key_sum)
        + along(w_value, value_sum)
        + along(w_gate_out, gate_out_sum)
        + along(w_forget, forget_sum)
    ) / low(norm1_gain).astype(f32)
    gain2_total = (along(w_gate, gate_sum) + along(w_up, up_sum)) / low(norm2_gain).astype(f32)
    return (
        result,
        tokens_grad,
        gain1_total,
        query_sum,
        key_sum,
        value_sum,
        gate_out_sum,
        forget_sum,
        bias_total,
        output_total,
        gain2_total,
        gate_sum,
        up_sum,
        down_sum,
    )


def solution(mesh):
    both = ("blk", "head")
    matrix, vector = P(both, None), P(both)
    return jax.shard_map(
        body,
        mesh=mesh,
        in_specs=(
            matrix, P("blk"), vector, matrix, matrix, matrix, matrix, matrix, P(), matrix, vector,
            matrix, matrix, matrix, matrix,
        ),
        out_specs=(
            matrix, matrix, vector, matrix, matrix, matrix, matrix, matrix, P(), matrix, vector,
            matrix, matrix, matrix,
        ),
        check_vma=False,
    )
```

```python
import functools

import jax
import jax.numpy as jnp
from jax import lax
from jax.experimental import pallas as pl
from jax.experimental.pallas import tpu as pltpu
from jax.sharding import PartitionSpec as P

epsilon = 1e-06
LANES = 128
Q_TILE = 512
K_TILE = 512
FAR = -1e30
NT = (((1,), (1,)), ((), ()))
NN = (((1,), (0,)), ((), ()))
bf16 = jnp.bfloat16
f32 = jnp.float32


def dot(a, b, dims=NN, **kw):
    return lax.dot_general(a, b, dims, preferred_element_type=f32, **kw)


def passed_along(array, axis, by):
    peers = lax.axis_size(axis)
    pairs = [(i, i + by) for i in range(peers) if 0 <= i + by < peers]
    return lax.ppermute(array, axis, pairs)


def split3(value):
    high = value.astype(bf16)
    rest = value - high.astype(f32)
    mid = rest.astype(bf16)
    low = (rest - mid.astype(f32)).astype(bf16)
    return high, mid, low


def running(value_of, steps, rows, upper):
    place = lax.broadcasted_iota(jnp.int32, (rows, rows), 0)
    other = lax.broadcasted_iota(jnp.int32, (rows, rows), 1)
    tri = jnp.where((other >= place) if upper else (other <= place), 1.0, 0.0).astype(bf16)
    outs = [None] * steps
    carry = jnp.zeros((1, LANES), f32)
    order = range(steps - 1, -1, -1) if upper else range(steps)
    for n in order:
        block = value_of(n)
        total = sum(dot(tri, part) for part in split3(block)) + carry
        outs[n] = total
        carry = total[0:1] if upper else total[rows - 1 : rows]
    return outs, carry


PROJECT_TILE = 256
TERM_ROWS = 32


def project_kernel(local_heads, tokens_ref, gain_ref, weight_ref, bias_ref, input_ref, out_ref,
                   terms_ref, turned_ref, forget_ref, carry_ref):
    rows = tokens_ref.shape[0]
    wide = weight_ref.shape[1] - LANES

    @pl.when(pl.program_id(0) == 0)
    def _():
        carry_ref[...] = jnp.zeros_like(carry_ref)

    tokens = tokens_ref[...].astype(f32)
    input1 = (tokens * inverse_rms(tokens) * gain_ref[0:1, :]).astype(bf16)
    input_ref[...] = input1
    raw = dot(input1, weight_ref[...])
    out_ref[...] = raw[:, :wide].astype(bf16)
    forget = (raw[:, wide:] + bias_ref[0:1, :]).astype(bf16).astype(f32)
    forget_ref[...] = forget
    lane = lax.broadcasted_iota(jnp.int32, (rows, LANES), 1)
    logf = jnp.minimum(forget, 0.0) - jnp.log1p(jnp.exp(-jnp.abs(forget)))
    logf = jnp.where(lane < local_heads, logf, 0.0)
    place = lax.broadcasted_iota(jnp.int32, (rows, rows), 0)
    other = lax.broadcasted_iota(jnp.int32, (rows, rows), 1)
    tri = jnp.where(other <= place, 1.0, 0.0).astype(bf16)
    sums = sum(dot(tri, part) for part in split3(logf)) + carry_ref[0:1, :]
    carry_ref[0:1, :] = sums[rows - 1 : rows, :]
    high, mid, low = split3(sums)
    terms = (
        high.astype(f32)
        + pltpu.roll(mid.astype(f32), local_heads, 1)
        + pltpu.roll(low.astype(f32), 2 * local_heads, 1)
        + jnp.where(lane == 3 * local_heads, 1.0, 0.0)
    ).astype(bf16)
    terms_ref[...] = terms
    turned_ref[...] = terms.T[0:TERM_ROWS, :]


def project(tokens, gain, weight, bias, wide, local_heads):
    rows, width = tokens.shape

    def tile(columns):
        return pl.BlockSpec((PROJECT_TILE, columns), lambda n: (n, 0))

    def whole(*shape):
        return pl.BlockSpec(shape, lambda n: (0, 0))

    return pl.pallas_call(
        functools.partial(project_kernel, local_heads),
        grid=(rows // PROJECT_TILE,),
        in_specs=[tile(width), whole(8, width), whole(width, wide + LANES), whole(8, LANES)],
        out_specs=[
            tile(width),
            tile(wide),
            tile(LANES),
            pl.BlockSpec((TERM_ROWS, PROJECT_TILE), lambda n: (0, n)),
            tile(LANES),
        ],
        out_shape=[
            jax.ShapeDtypeStruct((rows, width), bf16),
            jax.ShapeDtypeStruct((rows, wide), bf16),
            jax.ShapeDtypeStruct((rows, LANES), bf16),
            jax.ShapeDtypeStruct((TERM_ROWS, rows), bf16),
            jax.ShapeDtypeStruct((rows, LANES), f32),
        ],
        scratch_shapes=[pltpu.VMEM((8, LANES), f32)],
        cost_estimate=pl.CostEstimate(
            flops=2 * rows * width * (wide + LANES), transcendentals=rows * LANES,
            bytes_accessed=20_000_000,
        ),
        name="project",
    )(tokens, gain, weight, bias)


def decay_back_kernel(own_ref, halo_ref, out_ref):
    rows = 256
    steps = own_ref.shape[0] // rows
    own, _ = running(lambda n: own_ref[n * rows : (n + 1) * rows, :], steps, rows, True)
    halo, _ = running(lambda n: halo_ref[n * rows : (n + 1) * rows, :], steps, rows, False)
    for n in range(steps):
        part = slice(n * rows, (n + 1) * rows)
        out_ref[part, :] = own[n] + (halo[n] - halo_ref[part, :])


def decay_back(own, halo):
    return pl.pallas_call(
        decay_back_kernel,
        out_shape=jax.ShapeDtypeStruct(own.shape, f32),
        name="decay_back",
    )(own, halo)


QUERY, KEY, TOTAL = range(3)


def placing(pair, local_heads, role):
    row = lax.broadcasted_iota(jnp.int32, (LANES, LANES), 0)
    col = lax.broadcasted_iota(jnp.int32, (LANES, LANES), 1)
    head = jnp.where(col < 64, 2 * pair + 1, 2 * pair)
    spot = jnp.where(col < 64, col, col - 64)
    term = spot - 3 * role
    is_term = (term >= 0) & (term < 3) & (row == term * local_heads + head)
    if role == QUERY:
        ones = (spot >= 3) & (spot < 9)
    else:
        ones = (spot < 3) & (role == KEY)
    is_one = ones & (row == 3 * local_heads)
    sign = -1.0 if role == KEY else 1.0
    return (jnp.where(is_term, sign, 0.0) + jnp.where(is_one, 1.0, 0.0)).astype(bf16)


def allowed_pairs(first_key, query_tile, rows, begin_row):
    shape = (K_TILE, Q_TILE)
    key_place = first_key + lax.broadcasted_iota(jnp.int32, shape, 0)
    query_place = rows + query_tile * Q_TILE + lax.broadcasted_iota(jnp.int32, shape, 1)
    return (key_place >= begin_row) & (key_place <= query_place)


def key_range(ranges_ref, query_tile, rows, own):
    count = rows // K_TILE
    base = count if own else 0
    first = jnp.clip(ranges_ref[0, query_tile] - base, 0, count)
    full = jnp.clip(ranges_ref[1, query_tile] - base, first, count)
    return first, full


def key_loops(ranges_ref, query_tile, rows, own, step, carry):
    first, full = key_range(ranges_ref, query_tile, rows, own)
    inside = query_tile * (Q_TILE // K_TILE) if own else rows // K_TILE
    full = jnp.minimum(full, inside)
    carry = lax.fori_loop(first, full, functools.partial(step, True), carry)
    carry = lax.fori_loop(full, inside, functools.partial(step, False), carry)
    if own:
        carry = lax.fori_loop(
            inside, inside + Q_TILE // K_TILE, functools.partial(step, True), carry
        )
    return carry


def tile_of(number, size):
    return pl.ds(pl.multiple_of(number * size, size), size)


def fill_keys(pair, local_heads, own, first, key_ref, terms_ref, keys):
    place = placing(pair, local_heads, KEY)
    lane = lax.broadcasted_iota(jnp.int32, (K_TILE, LANES), 1)
    rows = key_ref.shape[0]
    if not own:
        last = terms_ref[:, rows - LANES : rows].T
        total = dot(last, placing(pair, local_heads, TOTAL)[0:TERM_ROWS, :])[LANES - 1 : LANES, :]

    def fill(n, carry):
        here = tile_of(n, K_TILE)
        if own:
            extra = dot(terms_ref[here, :], place).astype(bf16)
        else:
            extra = dot(terms_ref[:, here].T, place[0:TERM_ROWS, :])
            extra = (extra + total).astype(bf16)
        key = key_ref[here, :]
        keys[0][here, :] = jnp.where(lane < 64, key, extra)
        keys[1][here, :] = jnp.where(lane < 64, extra, key)
        return carry

    lax.fori_loop(first, rows // K_TILE, fill, 0)


def query_tiles(q_ref, terms_ref, place, here, scaling):
    lane = lax.broadcasted_iota(jnp.int32, (Q_TILE, LANES), 1)
    extra = dot(terms_ref[here, :], place).astype(bf16)
    query = (q_ref[here, :].astype(f32) * scaling).astype(bf16)
    return jnp.where(lane < 64, query, extra), jnp.where(lane < 64, extra, query)


def attend_kernel(local_heads, own, ranges_ref, q_ref, k_ref, v_ref, t_query_ref, t_key_ref,
                  begin_ref, *refs):
    if own:
        acc_out_ref, state_out_ref, key0, key1, values, acc0, acc1 = refs
    else:
        acc_in_ref, state_in_ref, o_ref, lse_ref, key0, key1, values, acc0, acc1 = refs
    pair = pl.program_id(0)
    rows = q_ref.shape[0]
    base = rows if own else 0
    keys, accs = (key0, key1), (acc0, acc1)
    first, _ = key_range(ranges_ref, 0, rows, own)
    fill_keys(pair, local_heads, own, first, k_ref, t_key_ref, keys)

    def turn(n, carry):
        values[:, tile_of(n, K_TILE)] = v_ref[tile_of(n, K_TILE), :].T
        return carry

    lax.fori_loop(first, rows // K_TILE, turn, 0)
    place = placing(pair, local_heads, QUERY)

    def query_loop(tile, carry):
        here = tile_of(tile, Q_TILE)
        queries = query_tiles(q_ref, t_query_ref, place, here, 64**-0.5)
        begin_row = begin_ref[0:1, here]
        if own:
            low = jnp.full((1, Q_TILE), FAR, f32)
            zero = jnp.zeros((1, Q_TILE), f32)
            state = (low, zero, low, zero)
            for acc in accs:
                acc[...] = jnp.zeros_like(acc)
        else:
            state = tuple(state_in_ref[n : n + 1, here] for n in range(4))
            for h in range(2):
                accs[h][...] = acc_in_ref[64 * h : 64 * (h + 1), here]

        def step(masked, number, state):
            there = tile_of(number, K_TILE)
            fresh = []
            if masked:
                allowed = allowed_pairs(base + number * K_TILE, tile, rows, begin_row)
            for h in range(2):
                largest, total = state[2 * h], state[2 * h + 1]
                scores = dot(keys[h][there, :], queries[h], NT)
                if masked:
                    scores = jnp.where(allowed, scores, FAR)
                now = jnp.maximum(largest, jnp.max(scores, axis=0, keepdims=True))
                fade = jnp.exp(largest - now)
                weights = jnp.exp(scores - now)
                total = total * fade + jnp.sum(weights, axis=0, keepdims=True)
                accs[h][...] = accs[h][...] * fade + dot(
                    values[64 * h : 64 * (h + 1), there], weights.astype(bf16)
                )
                fresh += [now, total]
            return tuple(fresh)

        state = key_loops(ranges_ref, tile, rows, own, step, state)
        if own:
            for h in range(2):
                acc_out_ref[64 * h : 64 * (h + 1), here] = accs[h][...]
            for n in range(4):
                state_out_ref[n : n + 1, here] = state[n]
        else:
            mixed = jnp.concatenate(
                [accs[h][...] * (1.0 / state[2 * h + 1]) for h in range(2)], axis=0
            )
            o_ref[here, :] = mixed.T.astype(bf16)
            for h in range(2):
                lse_ref[h : h + 1, here] = state[2 * h] + jnp.log(state[2 * h + 1])
        return carry

    lax.fori_loop(0, rows // Q_TILE, query_loop, 0)


def lane_block(rows, offset):
    return pl.BlockSpec((rows, LANES), lambda p, *_: (0, offset + p))


def fixed(shape):
    return pl.BlockSpec(shape, lambda p, *_: (0, 0))


def pair_block(height, rows):
    return pl.BlockSpec((height, rows), lambda p, *_: (p, 0))


def attend(own, ranges, query, key_value, terms, key_terms, begins, local_heads, so_far=()):
    rows = query.shape[0]
    pairs = local_heads // 2
    running_specs = [pair_block(LANES, rows), pair_block(8, rows)]
    running_shape = (
        jax.ShapeDtypeStruct((LANES * pairs, rows), f32),
        jax.ShapeDtypeStruct((8 * pairs, rows), f32),
    )
    final_specs = [lane_block(rows, 0), pair_block(8, rows)]
    final_shape = (
        jax.ShapeDtypeStruct((rows, pairs * LANES), bf16),
        jax.ShapeDtypeStruct((8 * pairs, rows), f32),
    )
    return pl.pallas_call(
        functools.partial(attend_kernel, local_heads, own),
        grid_spec=pltpu.PrefetchScalarGridSpec(
            num_scalar_prefetch=1,
            grid=(pairs,),
            in_specs=[
                lane_block(rows, 0),
                lane_block(rows, 0),
                lane_block(rows, pairs),
                fixed((rows, LANES)),
                fixed((rows, LANES) if own else (TERM_ROWS, rows)),
                fixed((8, rows)),
            ]
            + ([] if own else running_specs),
            out_specs=running_specs if own else final_specs,
            scratch_shapes=[
                pltpu.VMEM((rows, LANES), bf16),
                pltpu.VMEM((rows, LANES), bf16),
                pltpu.VMEM((LANES, rows), bf16),
                pltpu.VMEM((64, Q_TILE), f32),
                pltpu.VMEM((64, Q_TILE), f32),
            ],
        ),
        out_shape=running_shape if own else final_shape,
        cost_estimate=pl.CostEstimate(
            flops=40_000_000_000 if own else 10_000_000_000,
            transcendentals=20_000_000,
            bytes_accessed=12_000_000,
        ),
        name="attend_own" if own else "attend_prev",
    )(ranges, query, key_value, key_value, terms, key_terms, begins, *so_far)


def attend_back_kernel(local_heads, own, ranges_ref, q_ref, k_ref, v_ref, t_query_ref, t_key_ref,
                       begin_ref, grad_ref, o_ref, lse_ref, *refs):
    if own:
        dq_in_ref, decay_in_ref, dq_ref, dk_ref, dv_ref, decay_ref = refs[:6]
    else:
        dq_ref, row_decay_ref, dkv_ref, decay_ref = refs[:4]
        dk_ref, dv_ref = dkv_ref.at[0], dkv_ref.at[1]
    key0, key1, key_t0, key_t1, dk0, dk1, dv, dq0, dq1 = refs[-9:]
    pair = pl.program_id(0)
    rows = q_ref.shape[0]
    base = rows if own else 0
    keys, keys_t, dks, dqs = (key0, key1), (key_t0, key_t1), (dk0, dk1), (dq0, dq1)
    first, _ = key_range(ranges_ref, 0, rows, own)
    fill_keys(pair, local_heads, own, first, k_ref, t_key_ref, keys)

    def turn(n, carry):
        here = tile_of(n, K_TILE)
        for h in range(2):
            keys_t[h][:, here] = keys[h][here, :].T
        return carry

    lax.fori_loop(first, rows // K_TILE, turn, 0)
    for ref in (dk0, dk1, dv):
        ref[...] = jnp.zeros_like(ref)
    place = placing(pair, local_heads, QUERY)
    lane = lax.broadcasted_iota(jnp.int32, (Q_TILE, LANES), 1)
    pick_row = lax.broadcasted_iota(jnp.int32, (8, LANES), 0)
    pick_lane = lax.broadcasted_iota(jnp.int32, (8, LANES), 1)
    pick = jnp.where((pick_lane // 64) == pick_row, 1.0, 0.0)
    sums_ref = decay_ref if own else row_decay_ref

    @pl.when(pair == 0)
    def _():
        if own:
            decay_ref[...] = decay_in_ref[...]
        else:
            decay_ref[...] = jnp.zeros_like(decay_ref)
            row_decay_ref[...] = jnp.zeros_like(row_decay_ref)

    def query_tile(tile):
        here = tile_of(tile, Q_TILE)
        queries = query_tiles(q_ref, t_query_ref, place, here, 64**-0.5)
        begin_row = begin_ref[0:1, here]
        grad = grad_ref[here, :]
        nothing = jnp.zeros_like(grad)
        grads = (jnp.where(lane < 64, grad, nothing), jnp.where(lane < 64, nothing, grad))
        product = grad.astype(f32) * o_ref[here, :].astype(f32)
        inner = dot(pick, product, NT, precision=lax.Precision.HIGHEST)
        for dq in dqs:
            dq[...] = jnp.zeros_like(dq)

        def step(masked, number, state):
            there = tile_of(number, K_TILE)
            if masked:
                allowed = allowed_pairs(base + number * K_TILE, tile, rows, begin_row)
            value = v_ref[there, :]
            value_part = 0.0
            for h in range(2):
                scores = dot(keys[h][there, :], queries[h], NT)
                prob = jnp.exp(scores - lse_ref[h : h + 1, here])
                if masked:
                    prob = jnp.where(allowed, prob, 0.0)
                grad_prob = dot(value, grads[h], NT)
                grad_score = (prob * (grad_prob - inner[h : h + 1, :])).astype(bf16)
                value_part = value_part + dot(prob.astype(bf16), grads[h])
                dks[h][there, :] += dot(grad_score, queries[h])
                dqs[h][...] += dot(keys_t[h][:, there], grad_score)
            dv[there, :] += value_part
            return state

        key_loops(ranges_ref, tile, rows, own, step, 0)
        turned = [dq[...].T for dq in dqs]
        dq_tile = jnp.where(lane < 64, turned[0], turned[1]) * 64**-0.5
        if own:
            dq_tile = dq_tile + dq_in_ref[here, :]
        dq_ref[here, :] = dq_tile.astype(dq_ref.dtype)
        sums = sums_ref[here, :]
        sums = sums + jnp.where(lane == 2 * pair, turned[0][:, 64:65], 0.0)
        sums = sums + jnp.where(lane == 2 * pair + 1, turned[1][:, 0:1], 0.0)
        sums_ref[here, :] = sums

    def query_loop(tile, carry):
        if own:
            query_tile(tile)
        else:
            reaches = key_range(ranges_ref, tile, rows, own)[0] < rows // K_TILE
            pl.when(reaches)(lambda: query_tile(tile))

            @pl.when(jnp.logical_not(reaches))
            def _():
                dq_ref[tile_of(tile, Q_TILE), :] = jnp.zeros((Q_TILE, LANES), dq_ref.dtype)

        return carry

    lax.fori_loop(0, rows // Q_TILE, query_loop, 0)
    sign = -1.0 if own else 1.0

    def finish(n, carry):
        here = tile_of(n, Q_TILE)
        left, right = dk0[here, :], dk1[here, :]
        dk_ref[here, :] = jnp.where(lane < 64, left, right).astype(dk_ref.dtype)
        dv_ref[here, :] = dv[here, :].astype(dv_ref.dtype)
        decay = decay_ref[here, :]
        decay = decay + jnp.where(lane == 2 * pair, sign * left[:, 67:68], 0.0)
        decay = decay + jnp.where(lane == 2 * pair + 1, sign * right[:, 3:4], 0.0)
        decay_ref[here, :] = decay
        return carry

    lax.fori_loop(0, rows // Q_TILE, finish, 0)


def attend_back(
    own, ranges, query, key_value, terms, key_terms, begins, grad, mixed, lse, local_heads,
    so_far=(),
):
    rows = query.shape[0]
    pairs = local_heads // 2
    wide = jax.ShapeDtypeStruct((rows, pairs * LANES), f32)
    sums = jax.ShapeDtypeStruct((rows, LANES), f32)
    if own:
        out_specs = [lane_block(rows, 0)] * 3 + [fixed((rows, LANES))]
        out_shape = (jax.ShapeDtypeStruct(wide.shape, bf16), wide, wide, sums)
    else:
        both = pl.BlockSpec((2, rows, LANES), lambda p, *_: (0, 0, p))
        out_specs = [lane_block(rows, 0), fixed((rows, LANES)), both, fixed((rows, LANES))]
        out_shape = (
            wide, sums, jax.ShapeDtypeStruct((2, rows, pairs * LANES), bf16), sums,
        )
    return pl.pallas_call(
        functools.partial(attend_back_kernel, local_heads, own),
        grid_spec=pltpu.PrefetchScalarGridSpec(
            num_scalar_prefetch=1,
            grid=(pairs,),
            in_specs=[
                lane_block(rows, 0),
                lane_block(rows, 0),
                lane_block(rows, pairs),
                fixed((rows, LANES)),
                fixed((rows, LANES) if own else (TERM_ROWS, rows)),
                fixed((8, rows)),
                lane_block(rows, 0),
                lane_block(rows, 0),
                pair_block(8, rows),
            ]
            + ([lane_block(rows, 0), fixed((rows, LANES))] if own else []),
            out_specs=out_specs,
            scratch_shapes=[
                pltpu.VMEM((rows, LANES), bf16),
                pltpu.VMEM((rows, LANES), bf16),
                pltpu.VMEM((LANES, rows), bf16),
                pltpu.VMEM((LANES, rows), bf16),
                pltpu.VMEM((rows, LANES), f32),
                pltpu.VMEM((rows, LANES), f32),
                pltpu.VMEM((rows, LANES), f32),
                pltpu.VMEM((LANES, Q_TILE), f32),
                pltpu.VMEM((LANES, Q_TILE), f32),
            ],
        ),
        out_shape=out_shape,
        cost_estimate=pl.CostEstimate(
            flops=20_000_000_000 if own else 10_000_000_000,
            transcendentals=20_000_000,
            bytes_accessed=25_000_000,
        ),
        name="attend_back_own" if own else "attend_back_prev",
    )(
        ranges, query, key_value, key_value, terms, key_terms, begins, grad, mixed, lse, *so_far
    )


PIECES = 4


def partners():
    me = lax.axis_index("head")
    near = me + 1 - 2 * (me % 2)
    far = (me + 2) % 4
    cross = (near + 2) % 4
    return me, near, far, cross


def signal(other):
    pl.semaphore_signal(
        pltpu.get_barrier_semaphore(), inc=1, device_id=other, device_id_type=pl.DeviceIdType.MESH
    )


def greet(others):
    for other in others:
        signal(other)
    pl.semaphore_wait(pltpu.get_barrier_semaphore(), len(others))


def remote(source, target, send, receive, other):
    return pltpu.make_async_remote_copy(
        src_ref=source,
        dst_ref=target,
        send_sem=send,
        recv_sem=receive,
        device_id=other,
        device_id_type=pl.DeviceIdType.MESH,
    )


def on_head(index):
    return {"head": index}


def on_blk(index):
    return {"blk": index}


def piece_at(ref, slot, piece, size):
    span = size // PIECES
    return ref.at[pl.ds(pl.multiple_of(slot * size + piece * span, span), span), :]


class Slots:
    def __init__(self, by_device):
        me, near, far, cross = partners()
        if by_device:
            self.own = self.sent_near = self.sent_far = me
            self.near, self.far, self.cross = near, far, cross
            self.passed = far
        else:
            self.own, self.sent_near, self.sent_far = 3, 2, 1
            self.near, self.far, self.cross = 2, 1, 0
            self.passed = 0


def spread_piece(source, all_ref, size, sems, piece, slots):
    me, near, far, _ = partners()
    far_send, far_recv, near_send, near_recv, _, _, own = sems
    copies = (
        remote(source, piece_at(all_ref, slots.sent_far, piece, size), far_send.at[piece],
               far_recv.at[piece], on_head(far)),
        remote(source, piece_at(all_ref, slots.sent_near, piece, size), near_send.at[piece],
               near_recv.at[piece], on_head(near)),
        pltpu.make_async_copy(source, piece_at(all_ref, slots.own, piece, size), own.at[piece]),
    )
    for copy in copies:
        copy.start()
    return copies


def hand_on(all_ref, size, sems, sent, slots):
    me, near, far, cross = partners()
    far_send, far_recv, near_send, near_recv, on_send, on_recv, own = sems
    passed = []
    for piece in range(PIECES):
        there = piece_at(all_ref, slots.far, piece, size)
        remote(there, there, far_send.at[piece], far_recv.at[piece], on_head(far)).wait_recv()
        copy = remote(
            there, piece_at(all_ref, slots.passed, piece, size), on_send.at[piece],
            on_recv.at[piece], on_head(near),
        )
        copy.start()
        passed.append(copy)

    def finish():
        for piece in range(PIECES):
            to_far, to_near, local = sent[piece]
            to_far.wait_send()
            to_near.wait_send()
            local.wait()
            passed[piece].wait_send()
            there = piece_at(all_ref, slots.near, piece, size)
            remote(there, there, near_send.at[piece], near_recv.at[piece], on_head(near)).wait_recv()
            there = piece_at(all_ref, slots.cross, piece, size)
            remote(there, there, on_send.at[piece], on_recv.at[piece], on_head(near)).wait_recv()

    return finish


def gather_sems():
    return [pltpu.SemaphoreType.DMA((PIECES,)) for _ in range(7)]


def blk_peers():
    here = lax.axis_index("blk")
    half = lax.axis_size("blk") // 2
    low, high = here % 2, here // 2
    partner = here + 1 - 2 * low
    after = [((high + t) % half) * 2 + low for t in range(half)]
    return here, partner, after


class Line:
    def __init__(self, block_of, kinds, sems):
        self.block_of, self.kinds = block_of, kinds
        self.pair_send, self.pair_recv, self.up_send, self.up_recv, self.down_send, self.down_recv = sems
        here = lax.axis_index("blk")
        self.half = lax.axis_size("blk") // 2
        self.low, self.high = here % 2, here // 2
        self.partner = here + 1 - 2 * self.low
        self.has_up, self.has_down = self.high < self.half - 1, self.high > 0

    def greet(self, others):
        greet_sum = len(others) + 1
        for other in others + [on_blk(self.partner)]:
            signal(other)
        pl.when(self.has_up)(lambda: signal(on_blk(self.at(self.high + 1))))
        pl.when(self.has_down)(lambda: signal(on_blk(self.at(self.high - 1))))
        ends = (self.high == 0).astype(jnp.int32) + (self.high == self.half - 1).astype(jnp.int32)
        pl.semaphore_wait(pltpu.get_barrier_semaphore(), greet_sum + 2 - ends)

    def at(self, high):
        return high * 2 + self.low

    def pair_copy(self, kind, high, low):
        block = self.block_of(kind, high * 2 + low)
        return remote(
            block, block, self.pair_send.at[kind, high], self.pair_recv.at[kind, high],
            on_blk(self.partner),
        )

    def up_copy(self, kind, high):
        block = self.block_of(kind, self.at(high))
        return remote(
            block, block, self.up_send.at[kind, high], self.up_recv.at[kind, high],
            on_blk(self.at(jnp.minimum(self.high + 1, self.half - 1))),
        )

    def down_copy(self, kind, high):
        block = self.block_of(kind, self.at(high))
        return remote(
            block, block, self.down_send.at[kind, high], self.down_recv.at[kind, high],
            on_blk(self.at(jnp.maximum(self.high - 1, 0))),
        )

    def launch(self, kind):
        self.pair_copy(kind, self.high, self.low).start()
        pl.when(self.has_up)(lambda: self.up_copy(kind, self.high).start())
        pl.when(self.has_down)(lambda: self.down_copy(kind, self.high).start())

    def step(self, t):
        for kind in range(self.kinds):
            below, above = self.high - t, self.high + t

            @pl.when(below >= 0)
            def _():
                self.up_copy(kind, below).wait_recv()
                self.pair_copy(kind, below, self.low).start()
                pl.when(self.has_up)(lambda: self.up_copy(kind, below).start())

            @pl.when(above < self.half)
            def _():
                self.down_copy(kind, above).wait_recv()
                self.pair_copy(kind, above, self.low).start()
                pl.when(self.has_down)(lambda: self.down_copy(kind, above).start())

    def finish(self):
        for kind in range(self.kinds):

            def wait(high, carry):
                self.pair_copy(kind, high, self.low).wait_send()
                self.pair_copy(kind, high, 1 - self.low).wait_recv()

                @pl.when((high <= self.high) & self.has_up)
                def _():
                    self.up_copy(kind, high).wait_send()

                @pl.when((high >= self.high) & self.has_down)
                def _():
                    self.down_copy(kind, high).wait_send()

                return carry

            lax.fori_loop(0, self.half, wait, 0)


def gather_first_kernel(before, after, *refs):
    small_ref, weight_refs = refs[0], refs[1 : 1 + before + after]
    tokens_ref, cotangent_ref, pack_all, tokens_all, cotangent_all, pack_ref = refs[
        1 + before + after : 7 + before + after
    ]
    sems = refs[7 + before + after :]
    groups = pack_ref.shape[0]
    start = 0
    for n, ref in enumerate(weight_refs):
        if n == before:
            pack_ref[:, :, start : start + LANES] = small_ref[...]
            start += LANES
        wide = ref.shape[1] // groups
        for group in range(groups):
            pack_ref[group, :, start : start + wide] = ref[
                :, group * wide : (group + 1) * wide
            ].astype(bf16)
        start += wide
    swap_send, swap_recv, swap_own = sems[:3]
    token_sems, cotangent_sems = sems[9:16], sems[16:23]
    me, near, far, cross = partners()
    sources = (me, near, far, cross)
    line = Line(lambda kind, blk: pack_all.at[blk, sources[kind]], 4, sems[3:9])
    here = lax.axis_index("blk")
    line.greet([on_head(near), on_head(far), on_head(cross)])
    swaps = [pltpu.make_async_copy(pack_ref.at[me], pack_all.at[here, me], swap_own)]
    for kind, other in enumerate((near, far, cross)):
        swaps.append(
            remote(
                pack_ref.at[other],
                pack_all.at[here, me],
                swap_send.at[kind],
                swap_recv.at[kind],
                on_head(other),
            )
        )
    for swap in swaps:
        swap.start()
    size = tokens_ref.shape[0]
    span = size // PIECES

    def spread_all(ref, all_ref, some, slots):
        return [
            spread_piece(ref.at[pl.ds(piece * span, span), :], all_ref, size, some, piece, slots)
            for piece in range(PIECES)
        ]

    by_device, crossing = Slots(True), Slots(False)
    tokens_sent = spread_all(tokens_ref, tokens_all, token_sems, by_device)
    swaps[0].wait()
    line.launch(0)
    for kind, source in enumerate((near, far, cross)):
        block = pack_all.at[here, source]
        remote(
            block, block, swap_send.at[kind], swap_recv.at[kind], on_head(source)
        ).wait_recv()
        line.launch(kind + 1)
    cotangent_sent = spread_all(cotangent_ref, cotangent_all, cotangent_sems, crossing)
    for t in range(1, line.half):
        line.step(t)
    finish_tokens = hand_on(tokens_all, size, token_sems, tokens_sent, by_device)
    finish_cotangent = hand_on(cotangent_all, size, cotangent_sems, cotangent_sent, crossing)
    for swap in swaps[1:]:
        swap.wait_send()
    line.finish()
    finish_tokens()
    finish_cotangent()


def gather_first(before, small, after, tokens, cotangent, number):
    groups, share, _ = small.shape
    weights = [*before, *after]
    columns = LANES + sum(weight.shape[1] // groups for weight in weights)
    peers = lax.axis_size("blk")
    rows, width = tokens.shape
    whole = jax.ShapeDtypeStruct((groups * rows, width), bf16)
    vmem, anywhere = pl.BlockSpec(memory_space=pltpu.VMEM), pl.BlockSpec(memory_space=pl.ANY)
    all_pack, all_tokens, all_cotangent = pl.pallas_call(
        functools.partial(gather_first_kernel, len(before), len(after)),
        in_specs=[vmem] * (3 + len(weights)),
        out_specs=[anywhere] * 3,
        out_shape=[jax.ShapeDtypeStruct((peers, groups, share, columns), bf16), whole, whole],
        scratch_shapes=[
            pltpu.VMEM((groups, share, columns), bf16),
            pltpu.SemaphoreType.DMA((3,)),
            pltpu.SemaphoreType.DMA((3,)),
            pltpu.SemaphoreType.DMA,
        ]
        + [pltpu.SemaphoreType.DMA((4, peers // 2)) for _ in range(6)]
        + gather_sems()
        + gather_sems(),
        compiler_params=pltpu.CompilerParams(collective_id=number, has_side_effects=True),
        cost_estimate=pl.CostEstimate(
            flops=70_000_000_000, transcendentals=0, bytes_accessed=30_000_000
        ),
        name="gather_first",
    )(small, *weights, tokens, cotangent)
    return all_pack.reshape(peers * groups * share, columns), all_tokens, all_cotangent


class Sum:
    def __init__(self, part_ref, buffers, sems, size, by_device):
        self.part_ref, self.size, self.span = part_ref, size, size // PIECES
        self.slots = Slots(by_device)
        self.near_buf, self.turn_buf, self.far_buf = buffers
        self.near_send, self.near_recv, self.far_send, self.far_recv = sems
        self.near_copies, self.far_copies = [], []

    def piece(self, n):
        return slice(n * self.span, (n + 1) * self.span)

    def start(self):
        me, near, far, cross = partners()
        for which, shard in ((0, self.slots.cross), (1, self.slots.near)):
            for n in range(PIECES):
                copy = remote(
                    piece_at(self.part_ref, shard, n, self.size),
                    self.near_buf.at[which, pl.ds(n * self.span, self.span), :],
                    self.near_send.at[which, n],
                    self.near_recv.at[which, n],
                    on_head(near),
                )
                copy.start()
                self.near_copies.append(copy)

    def turn(self):
        me, near, far, cross = partners()
        for n in range(PIECES):
            here = self.piece(n)
            self.near_copies[n].wait_recv()
            self.turn_buf[here, :] = (
                piece_at(self.part_ref, self.slots.far, n, self.size)[...].astype(f32)
                + self.near_buf[0, here, :].astype(f32)
            ).astype(bf16)
            copy = remote(
                self.turn_buf.at[pl.ds(n * self.span, self.span), :],
                self.far_buf.at[pl.ds(n * self.span, self.span), :],
                self.far_send.at[n],
                self.far_recv.at[n],
                on_head(far),
            )
            copy.start()
            self.far_copies.append(copy)

    def total(self, n):
        self.near_copies[PIECES + n].wait_recv()
        self.far_copies[n].wait_recv()
        here = self.piece(n)
        return (
            piece_at(self.part_ref, self.slots.own, n, self.size)[...].astype(f32)
            + self.near_buf[1, here, :].astype(f32)
            + self.far_buf[here, :].astype(f32)
        )

    def finish(self):
        for copy in self.near_copies + self.far_copies:
            copy.wait_send()


def sum_buffers(size, width):
    return [
        pltpu.VMEM((2, size, width), bf16),
        pltpu.VMEM((size, width), bf16),
        pltpu.VMEM((size, width), bf16),
    ]


def sum_sems():
    return [
        pltpu.SemaphoreType.DMA((2, PIECES)),
        pltpu.SemaphoreType.DMA((2, PIECES)),
        pltpu.SemaphoreType.DMA((PIECES,)),
        pltpu.SemaphoreType.DMA((PIECES,)),
    ]


def exchange_kernel(local, extras, summed, weights, *refs):
    part_ref, extra_refs = refs[0], refs[1 : 1 + extras]
    refs = refs[1 + extras :]
    if weights:
        mine_ref, refs = refs[0], refs[1:]
    out_ref, all_ref, refs = refs[0], refs[1], refs[2:]
    if weights:
        weight_ref, refs = refs[0], refs[1:]
    payload, sems = refs[0], refs[1:]
    size = out_ref.shape[0]
    span = size // PIECES
    _, near, far, _ = partners()
    if weights:
        kinds = mine_ref.shape[0]
        line = Line(lambda kind, blk: weight_ref.at[blk, kind], kinds, sems[-7:-1])
        own = pltpu.make_async_copy(mine_ref, weight_ref.at[lax.axis_index("blk")], sems[-1])
        own.start()
        line.greet([on_head(near), on_head(far)])
    else:
        greet([on_head(near), on_head(far)])
    slots = Slots(summed)
    if not summed:
        shares = Sum(part_ref, sems[7:10], sems[10:14], size, True)
        shares.start()
    if weights:
        own.wait()
        for kind in range(kinds):
            line.launch(kind)
    if not summed:
        shares.turn()
    sent = []
    for piece in range(PIECES):
        if weights and piece != 2:
            hop = {0: 1, 1: 2, 3: 3}[piece]
            for t in range(hop, line.half if piece == 3 else min(hop + 1, line.half)):
                line.step(t)
        here = slice(piece * span, (piece + 1) * span)
        total = part_ref[here, :] if summed else shares.total(piece)
        result, share = local(total, here, *extra_refs)
        out_ref[here, :] = result.astype(out_ref.dtype)
        payload[here, :] = share.astype(bf16)
        source = payload.at[pl.ds(piece * span, span), :]
        sent.append(spread_piece(source, all_ref, size, sems[:7], piece, slots))
    hand_on(all_ref, size, sems[:7], sent, slots)()
    if not summed:
        shares.finish()
    if weights:
        line.finish()


def exchange(local, part, extras, summed, number, name, mine=None):
    rows, width = part.shape
    size = rows if summed else rows // 4
    vmem, anywhere = pl.BlockSpec(memory_space=pltpu.VMEM), pl.BlockSpec(memory_space=pl.ANY)
    weights = mine is not None
    inputs = [part, *extras]
    out_specs = [vmem, anywhere]
    out_shape = [
        jax.ShapeDtypeStruct((size, width), f32),
        jax.ShapeDtypeStruct((4 * size, width), bf16),
    ]
    scratch = [pltpu.VMEM((size, width), bf16)] + gather_sems()
    if not summed:
        scratch += sum_buffers(size, width) + sum_sems()
    if weights:
        peers = lax.axis_size("blk")
        inputs.append(mine)
        out_specs.append(anywhere)
        out_shape.append(jax.ShapeDtypeStruct((peers,) + mine.shape, bf16))
        scratch += [pltpu.SemaphoreType.DMA((mine.shape[0], peers // 2)) for _ in range(6)]
        scratch.append(pltpu.SemaphoreType.DMA)
    return pl.pallas_call(
        functools.partial(exchange_kernel, local, len(extras), summed, weights),
        in_specs=[vmem] * len(inputs),
        out_specs=out_specs,
        out_shape=out_shape,
        scratch_shapes=scratch,
        compiler_params=pltpu.CompilerParams(collective_id=number, has_side_effects=True),
        cost_estimate=pl.CostEstimate(
            flops=10_000_000_000 if summed else 70_000_000_000,
            transcendentals=0,
            bytes_accessed=16_000_000,
        ),
        name=name,
    )(*inputs)


def column_chunks(width):
    count = max(width // 512, 1)
    first = width - 512 * (count - 1)
    return [(0, first)] + [(first + 512 * n, 512) for n in range(count - 1)]


def finish_last_kernel(grad_ref, output_grad_ref, second_ref, first_ref, grad_middle_ref, tokens_ref,
                       gain_ref, weights_ref, output_ref, second_out_ref, tokens_grad_ref, *refs):
    buffers = (refs[0:3], refs[3:6])
    first_buffers = refs[6:9]
    pair_send, pair_recv, line_send, line_recv, swap_send, swap_recv = refs[9:15]
    first_sems = refs[15:19]
    me, near, far, cross = partners()
    others = (near, far, cross)
    here, partner, after = blk_peers()
    steps = len(after)
    greet(
        [on_head(other) for other in others]
        + [on_blk(partner)]
        + [on_blk(peer) for peer in after[1:]]
    )
    size = tokens_grad_ref.shape[0]
    first = Sum(first_ref, first_buffers, first_sems, size, True)
    chunks = []
    for ref, out_ref, some in (
        (grad_ref, weights_ref, buffers[0]), (output_grad_ref, output_ref, buffers[1])
    ):
        for start, wide in column_chunks(ref.shape[3]):
            chunks.append((ref, out_ref, some, pl.ds(start, wide)))
    groups = grad_ref.shape[1]
    first.start()
    sent = []
    for c, (ref, _, (pair_buf, _, _), at) in enumerate(chunks):
        for t in list(range(1, steps)) + [0]:
            copy = remote(
                ref.at[after[t] + partner - here, :, :, at],
                pair_buf.at[t, :, :, at],
                pair_send.at[c, t],
                pair_recv.at[c, t],
                on_blk(partner),
            )
            copy.start()
            sent.append(copy)
    first.turn()

    def swap(source_ref, out_ref, c):
        for kind, other in enumerate(others):
            copy = remote(
                source_ref.at[other], out_ref.at[me], swap_send.at[c, kind],
                swap_recv.at[c, kind], on_head(other),
            )
            copy.start()
            sent.append(copy)

    swap(second_ref, second_out_ref, len(chunks))

    def add_up(c):
        ref, out_ref, (pair_buf, line_buf, row_buf), at = chunks[c]
        block = pair_buf.at[0, :, :, at]
        remote(block, block, pair_send.at[c, 0], pair_recv.at[c, 0], on_blk(partner)).wait_recv()
        for t in range(1, steps):
            block = line_buf.at[t, :, :, at]
            remote(
                block, block, line_send.at[c, t], line_recv.at[c, t], on_blk(after[t])
            ).wait_recv()

        def add_all(group, carry):
            total = ref[here, group, :, at].astype(f32) + pair_buf[0, group, :, at].astype(f32)
            for t in range(1, steps):
                total = total + line_buf[t, group, :, at].astype(f32)
            row_buf[group, :, at] = total.astype(bf16)
            return carry

        lax.fori_loop(0, groups, add_all, 0)
        out_ref[me, :, at] = row_buf[me, :, at]
        swap(row_buf.at[:, :, at], out_ref.at[:, :, at], c)

    for c, (ref, _, (pair_buf, line_buf, _), at) in enumerate(chunks):
        for t in range(1, steps):
            block = pair_buf.at[t, :, :, at]
            remote(
                block, block, pair_send.at[c, t], pair_recv.at[c, t], on_blk(partner)
            ).wait_recv()

            def add(group, carry):
                pair_buf[t, group, :, at] = (
                    ref[after[t], group, :, at].astype(f32)
                    + pair_buf[t, group, :, at].astype(f32)
                ).astype(bf16)
                return carry

            lax.fori_loop(0, groups, add, 0)
            copy = remote(
                block, line_buf.at[t, :, :, at], line_send.at[c, t], line_recv.at[c, t],
                on_blk(after[t]),
            )
            copy.start()
            sent.append(copy)
        if c > 0:
            add_up(c - 1)
    for piece in range(PIECES):
        rows = first.piece(piece)
        tokens_grad_ref[rows, :], _ = after_first(
            first.total(piece), rows, grad_middle_ref, tokens_ref, gain_ref
        )
    add_up(len(chunks) - 1)
    second_out_ref[me] = second_ref[me]
    for c in range(len(chunks) + 1):
        if c < len(chunks):
            _, out_ref, _, at = chunks[c]
            out_ref = out_ref.at[:, :, at]
        else:
            out_ref = second_out_ref
        for kind, other in enumerate(others):
            block = out_ref.at[other]
            remote(
                block, block, swap_send.at[c, kind], swap_recv.at[c, kind], on_head(other)
            ).wait_recv()
    for copy in sent:
        copy.wait_send()
    first.finish()


def finish_last(grad, output_grad, second, groups, part_first, grad_middle, tokens, gain, number):
    peers = lax.axis_size("blk")
    share = grad.shape[0] // (peers * groups)
    rows, width = tokens.shape
    vmem = pl.BlockSpec(memory_space=pltpu.VMEM)
    half = peers // 2
    widths = (grad.shape[1], output_grad.shape[1])
    chunks = sum(len(column_chunks(width)) for width in widths)

    def blocks(columns):
        return [pltpu.VMEM((half, groups, share, columns), bf16) for _ in range(2)] + [
            pltpu.VMEM((groups, share, columns), bf16)
        ]

    return pl.pallas_call(
        finish_last_kernel,
        in_specs=[vmem] * 7,
        out_specs=[vmem] * 4,
        out_shape=[
            jax.ShapeDtypeStruct((groups, share, columns), bf16)
            for columns in widths + (second.shape[1],)
        ]
        + [jax.ShapeDtypeStruct((rows, width), f32)],
        scratch_shapes=blocks(widths[0])
        + blocks(widths[1])
        + sum_buffers(rows, width)
        + [pltpu.SemaphoreType.DMA((chunks, half)) for _ in range(4)]
        + [pltpu.SemaphoreType.DMA((chunks + 1, 3)) for _ in range(2)]
        + sum_sems(),
        compiler_params=pltpu.CompilerParams(
            collective_id=number, has_side_effects=True, vmem_limit_bytes=60 << 20
        ),
        cost_estimate=pl.CostEstimate(
            flops=80_000_000_000, transcendentals=0, bytes_accessed=40_000_000
        ),
        name="finish_last",
    )(
        grad.reshape(peers, groups, share, widths[0]),
        output_grad.reshape(peers, groups, share, widths[1]),
        second.reshape(groups, share, second.shape[1]),
        part_first, grad_middle, tokens, gain,
    )


def inverse_rms(value):
    return lax.rsqrt(jnp.mean(value * value, axis=1, keepdims=True) + epsilon)


def through_norm(grad, value):
    factor = inverse_rms(value)
    normed = value * factor
    return factor * (grad - normed * jnp.mean(grad * normed, axis=1, keepdims=True))


def after_attention(total, here, tokens_ref, gain_ref):
    middle = tokens_ref[here, :].astype(f32) + total
    return middle, middle * inverse_rms(middle) * gain_ref[0:1, :]


def after_hidden(total, here, cotangent_ref, middle_ref, gain_ref):
    grad = cotangent_ref[here, :].astype(f32) + through_norm(
        total * gain_ref[0:1, :], middle_ref[here, :]
    )
    return grad, grad


def after_first(total, here, grad_ref, tokens_ref, gain_ref):
    grad = grad_ref[here, :] + through_norm(
        total * gain_ref[0:1, :], tokens_ref[here, :].astype(f32)
    )
    return grad, None


FEED_TILE = 256
FEED_COLUMNS = 512


def feed_kernel(input_ref, cotangent_ref, weight_ref, down_weight_ref, down_ref, grad_ref, total_ref,
                acts, turned0, turned1, stage, near_buf, far_buf, near_send, near_recv, far_send, far_recv):
    step = pl.program_id(0)
    hidden_width = down_weight_ref.shape[1]
    size = total_ref.shape[0]
    per = size // FEED_TILE
    tiles = 4 * per
    _, near, far, _ = partners()

    @pl.when(step == 0)
    def _():
        greet([on_head(near), on_head(far)])

    def to_near(which, piece):
        return remote(
            stage.at[which * per + piece],
            near_buf.at[which, piece],
            near_send.at[which, piece],
            near_recv.at[which, piece],
            on_head(near),
        )

    def to_far(piece):
        return remote(
            near_buf.at[0, piece], far_buf.at[piece], far_send.at[piece], far_recv.at[piece],
            on_head(far),
        )

    @pl.when(step < tiles)
    def _():
        here = tile_of(step, FEED_TILE)
        inputs, cotangent = input_ref[...], cotangent_ref[...]
        turned0[:, here] = inputs.T
        turned1[:, here] = cotangent.T
        gate_at, up_at, down_at = (
            slice(n * hidden_width, (n + 1) * hidden_width) for n in range(3)
        )
        gate = dot(inputs, weight_ref[:, gate_at])
        up = dot(inputs, weight_ref[:, up_at])
        grad_hidden = dot(cotangent, down_weight_ref[...])
        opening = jax.nn.sigmoid(gate)
        active = gate * opening
        hidden = (active * up).astype(bf16)
        grad_gate = (grad_hidden * up * opening * (1.0 + gate * (1.0 - opening))).astype(bf16)
        grad_up = (grad_hidden * active).astype(bf16)
        acts[here, gate_at] = grad_gate
        acts[here, up_at] = grad_up
        acts[here, down_at] = hidden
        down_ref[...] = dot(hidden, down_weight_ref[...], NT).astype(bf16)
        back = dot(grad_gate, weight_ref[:, gate_at], NT) + dot(
            grad_up, weight_ref[:, up_at], NT
        )
        for piece in range(per):
            for which, first in ((0, 0), (1, 2 * per)):

                @pl.when(step == first + piece)
                def _():
                    stage[which * per + piece] = back.astype(bf16)
                    to_near(which, piece).start()

            @pl.when(step == per + piece)
            def _():
                to_near(0, piece).wait_recv()
                near_buf[0, piece] = (back + near_buf[0, piece].astype(f32)).astype(bf16)
                to_far(piece).start()

            @pl.when(step == 3 * per + piece)
            def _():
                total_ref[piece * FEED_TILE : (piece + 1) * FEED_TILE, :] = back

    @pl.when(step >= tiles)
    def _():
        at = tile_of(step - tiles, FEED_COLUMNS)
        from_input = (step - tiles) * FEED_COLUMNS < 2 * hidden_width

        @pl.when(from_input)
        def _():
            grad_ref[...] = dot(turned0[...], acts[:, at]).astype(bf16)

        @pl.when(jnp.logical_not(from_input))
        def _():
            grad_ref[...] = dot(turned1[...], acts[:, at]).astype(bf16)

    @pl.when(step == pl.num_programs(0) - 1)
    def _():
        for piece in range(per):
            here = slice(piece * FEED_TILE, (piece + 1) * FEED_TILE)
            to_near(1, piece).wait_recv()
            to_far(piece).wait_recv()
            total_ref[here, :] += near_buf[1, piece].astype(f32) + far_buf[piece].astype(f32)
            to_near(0, piece).wait_send()
            to_near(1, piece).wait_send()
            to_far(piece).wait_send()


def feed(inputs, cotangent, weight, down_weight, number):
    rows, width = inputs.shape
    columns = weight.shape[1] + down_weight.shape[1]
    size = rows // 4
    tiles, per = rows // FEED_TILE, size // FEED_TILE
    tile = pl.BlockSpec((FEED_TILE, width), lambda n: (jnp.minimum(n, tiles - 1), 0))

    def whole(shape):
        return pl.BlockSpec(shape, lambda n: (0, 0), pipeline_mode=pl.Buffered(1))

    return pl.pallas_call(
        feed_kernel,
        grid=(tiles + columns // FEED_COLUMNS,),
        in_specs=[tile, tile, whole(weight.shape), whole(down_weight.shape)],
        out_specs=[
            tile,
            pl.BlockSpec((width, FEED_COLUMNS), lambda n: (0, jnp.maximum(n - tiles, 0))),
            whole((size, width)),
        ],
        out_shape=[
            jax.ShapeDtypeStruct((rows, width), bf16),
            jax.ShapeDtypeStruct((width, columns), bf16),
            jax.ShapeDtypeStruct((size, width), f32),
        ],
        scratch_shapes=[
            pltpu.VMEM((rows, columns), bf16),
            pltpu.VMEM((width, rows), bf16),
            pltpu.VMEM((width, rows), bf16),
            pltpu.VMEM((2 * per, FEED_TILE, width), bf16),
            pltpu.VMEM((2, per, FEED_TILE, width), bf16),
            pltpu.VMEM((per, FEED_TILE, width), bf16),
            pltpu.SemaphoreType.DMA((2, per)),
            pltpu.SemaphoreType.DMA((2, per)),
            pltpu.SemaphoreType.DMA((per,)),
            pltpu.SemaphoreType.DMA((per,)),
        ],
        compiler_params=pltpu.CompilerParams(
            collective_id=number, has_side_effects=True, vmem_limit_bytes=63 << 20
        ),
        cost_estimate=pl.CostEstimate(
            flops=6 * rows * width * columns, transcendentals=rows * columns // 3,
            bytes_accessed=45_000_000,
        ),
        name="feed",
    )(inputs, cotangent, weight, down_weight)


def over_tokens(operand, other_side):
    return lax.dot_general(
        operand, other_side, (((0,), (0,)), ((), ())), preferred_element_type=f32
    )


def sent_columns(pieces, groups):
    packed = jnp.concatenate(
        [piece.reshape(piece.shape[0], groups, -1) for piece in pieces], axis=2
    )
    mine = lax.all_to_all(packed, "head", split_axis=1, concat_axis=0, tiled=True)
    return mine.reshape(mine.shape[0], mine.shape[2])


def all_rows(mine):
    return lax.all_gather(mine, "blk", axis=0, tiled=True)


def row_sums(grad):
    return lax.psum_scatter(grad, "blk", scatter_dimension=0, tiled=True)


def crossing_sum(part):
    cross, far, near, own = (piece.astype(f32) for piece in jnp.split(part, 4))
    members = range(lax.axis_size("head"))
    got = lax.ppermute(
        jnp.concatenate([cross, near]).astype(bf16), "head",
        [(n, n + 1 - 2 * (n % 2)) for n in members],
    )
    of_far, of_own = jnp.split(got.astype(f32), 2)
    back = lax.ppermute(
        (far + of_far).astype(bf16), "head", [(n, (n + 2) % 4) for n in members]
    )
    return own + of_own + back.astype(f32)


def body(
    tokens,
    segment,
    norm1_gain,
    w_query,
    w_key,
    w_value,
    w_gate_out,
    w_forget,
    forget_bias,
    w_output,
    norm2_gain,
    w_gate,
    w_up,
    w_down,
    cotangent,
):
    token_rows, model_width = tokens.shape
    groups = lax.axis_size("head")
    head_count = forget_bias.shape[0]
    local_heads = head_count // groups
    local_width = model_width // groups
    hidden_width = w_gate.shape[1] // groups
    rows = token_rows * groups
    share = w_query.shape[0]
    group = lax.axis_index("head")

    low = lambda array: array.astype(bf16)
    spread = lambda gain: jnp.broadcast_to(low(gain)[:, None, None], (share, groups, 1))
    forget_low = low(w_forget).reshape(share, groups, local_heads)
    rest = LANES - local_heads - 2
    small = jnp.concatenate(
        [forget_low, spread(norm1_gain), spread(norm2_gain), jnp.zeros((share, groups, rest), bf16)],
        axis=2,
    )
    first, tokens_all, cotangent_all = gather_first(
        (w_key, w_value), jnp.swapaxes(small, 0, 1), (w_query, w_gate_out, w_output), tokens,
        cotangent, 0,
    )
    kv_width = 2 * local_width + LANES
    output_weight = first[:, kv_width + 2 * local_width :]

    def gain_rows(column):
        gain = first[:, 2 * local_width + local_heads + column].astype(f32)
        return jnp.broadcast_to(gain[None, :], (8, model_width))

    gain1, gain2 = gain_rows(0), gain_rows(1)
    bias = lax.dynamic_slice_in_dim(forget_bias, group * local_heads, local_heads, 0)
    bias = jnp.broadcast_to(jnp.pad(bias, (0, LANES - local_heads))[None, :], (8, LANES))
    input1, key_value, terms, turned_terms, forget = project(
        tokens_all, gain1, first, bias, 2 * local_width, local_heads
    )
    earlier_kv = passed_along(key_value, "blk", 1)
    earlier_terms = passed_along(turned_terms, "blk", 1)
    query = dot(input1, first[:, kv_width : kv_width + local_width]).astype(bf16)
    gate_raw = dot(
        input1, first[:, kv_width + local_width : kv_width + 2 * local_width]
    )

    segment_plus, _ = lax.optimization_barrier((segment + 1, key_value))
    earlier_segment = passed_along(segment_plus, "blk", 1)
    window = jnp.concatenate([earlier_segment, segment_plus])
    begins = jnp.sum(
        (window[:, None] < segment_plus[None, :]).astype(jnp.int32), axis=0
    )
    tiles = begins.reshape(rows // Q_TILE, Q_TILE)
    ranges = jnp.stack([tiles[:, 0] // K_TILE, (tiles[:, -1] + K_TILE - 1) // K_TILE])
    begins = jnp.broadcast_to(begins[None, :], (8, rows))

    so_far = attend(True, ranges, query, key_value, terms, terms, begins, local_heads)
    later = lax.optimization_barrier((w_gate, w_up, w_down, key_value))
    mine = sent_columns([low(weight) for weight in later[:3]], groups)
    mine, earlier_kv, earlier_terms, so_far = lax.optimization_barrier(
        (mine, earlier_kv, earlier_terms, so_far)
    )
    second = all_rows(mine[:, : 2 * hidden_width])
    mine_down = mine[:, 2 * hidden_width :].reshape(groups, share, hidden_width)
    attended, lse = attend(
        False, ranges, query, earlier_kv, terms, earlier_terms, begins, local_heads, so_far
    )
    opened = jax.nn.sigmoid(gate_raw)
    attended_wide = attended.astype(f32)
    gated = (opened * attended_wide).astype(bf16)
    branch = dot(gated, output_weight, NT).astype(bf16)
    middle, input2, down_weight = exchange(
        after_attention, branch, [tokens, gain2], False, 1, "exchange_middle", mine_down
    )
    down_weight = down_weight.reshape(model_width, hidden_width)
    down, second_grad, grad_input2 = feed(input2, cotangent_all, second, down_weight, 4)
    second_part = row_sums(second_grad)
    grad_middle, grad_branch = exchange(
        after_hidden, grad_input2, [cotangent, middle, gain2], True, 2, "exchange_hidden"
    )

    down, grad_branch = lax.optimization_barrier((down, grad_branch))
    result = (middle + crossing_sum(down)).astype(bf16)
    grad_gated = dot(grad_branch, output_weight)
    grad_attended = (grad_gated * opened).astype(bf16)
    grad_gate_pre = (grad_gated * attended_wide * opened * (1.0 - opened)).astype(bf16)
    dq_prev, rows_prev, dkv_prev, decay_prev = attend_back(
        False, ranges, query, earlier_kv, terms, earlier_terms, begins, grad_attended, attended,
        lse, local_heads,
    )
    dkv_later = passed_along(dkv_prev, "blk", -1)
    decay_later = passed_along(decay_prev[:, :8], "blk", -1)
    decay_later = jnp.pad(decay_later, ((0, 0), (0, LANES - 8)))
    dq, dk_own, dv_own, decay_own = attend_back(
        True, ranges, query, key_value, terms, terms, begins, grad_attended, attended,
        lse, local_heads, (dq_prev, rows_prev),
    )
    dk = (dk_own + dkv_later[0].astype(f32)).astype(bf16)
    dv = (dv_own + dkv_later[1].astype(f32)).astype(bf16)
    logf_grad = decay_back(decay_own, decay_later)
    forget_grad = jnp.where(
        jnp.arange(LANES)[None, :] < local_heads, logf_grad * jax.nn.sigmoid(-forget), 0.0
    ).astype(bf16)
    grads = jnp.concatenate([dk, dv, forget_grad, dq, grad_gate_pre], axis=1)
    first_grad = over_tokens(input1, grads)
    bias_part = jnp.sum(forget_grad.astype(f32), axis=0)
    row = jnp.arange(model_width)[:, None] % share
    column = jnp.arange(kv_width + 2 * local_width)[None, :]
    spread_bias = jnp.sum(
        jnp.where(row == jnp.arange(LANES)[None, :], bias_part[None, :], 0.0), axis=1, keepdims=True
    )
    first_grad = jnp.where(
        column == 2 * local_width + local_heads, spread_bias, first_grad
    ).astype(bf16)
    output_grad = over_tokens(grad_branch, gated).astype(bf16)
    grad_input1 = dot(grads, first[:, : kv_width + 2 * local_width], NT).astype(bf16)
    first_sum, output_sum, second_sum, tokens_grad = finish_last(
        first_grad, output_grad, second_part, groups, grad_input1, grad_middle, tokens, gain1, 3
    )
    first_sum, output_sum, second_sum = (
        jnp.swapaxes(array, 0, 1).astype(f32) for array in (first_sum, output_sum, second_sum)
    )

    def columns(array, start, width):
        return array[:, :, start : start + width].reshape(share, groups * width)

    key_sum, value_sum = (columns(first_sum, n * local_width, local_width) for n in range(2))
    forget_sum = columns(first_sum, 2 * local_width, local_heads)
    bias_total = first_sum[:local_heads, :, 2 * local_width + local_heads].T.reshape(head_count)
    query_sum, gate_out_sum = (
        columns(first_sum, kv_width + n * local_width, local_width) for n in range(2)
    )
    output_total = columns(output_sum, 0, local_width)
    gate_sum, up_sum, down_sum = (
        columns(second_sum, n * hidden_width, hidden_width) for n in range(3)
    )

    def along(weight, grad):
        return jnp.sum(low(weight).astype(f32) * grad, axis=1)

    gain1_total = (
        along(w_query, query_sum)
        + along(w_key, key_sum)
        + along(w_value, value_sum)
        + along(w_gate_out, gate_out_sum)
        + along(w_forget, forget_sum)
    ) / low(norm1_gain).astype(f32)
    gain2_total = (along(w_gate, gate_sum) + along(w_up, up_sum)) / low(norm2_gain).astype(f32)
    return (
        result,
        tokens_grad,
        gain1_total,
        query_sum,
        key_sum,
        value_sum,
        gate_out_sum,
        forget_sum,
        bias_total,
        output_total,
        gain2_total,
        gate_sum,
        up_sum,
        down_sum,
    )


def solution(mesh):
    both = ("blk", "head")
    matrix, vector = P(both, None), P(both)
    return jax.shard_map(
        body,
        mesh=mesh,
        in_specs=(
            matrix, P("blk"), vector, matrix, matrix, matrix, matrix, matrix, P(), matrix, vector,
            matrix, matrix, matrix, matrix,
        ),
        out_specs=(
            matrix, matrix, vector, matrix, matrix, matrix, matrix, matrix, P(), matrix, vector,
            matrix, matrix, matrix,
        ),
        check_vma=False,
    )
```

```python
import functools

import jax
import jax.numpy as jnp
from jax import lax
from jax.experimental import pallas as pl
from jax.experimental.pallas import tpu as pltpu
from jax.sharding import PartitionSpec as P

epsilon = 1e-06
LANES = 128
Q_TILE = 512
K_TILE = 512
FAR = -1e30
NT = (((1,), (1,)), ((), ()))
NN = (((1,), (0,)), ((), ()))
bf16 = jnp.bfloat16
f32 = jnp.float32


def dot(a, b, dims=NN, **kw):
    return lax.dot_general(a, b, dims, preferred_element_type=f32, **kw)


def passed_along(array, axis, by):
    peers = lax.axis_size(axis)
    pairs = [(i, i + by) for i in range(peers) if 0 <= i + by < peers]
    return lax.ppermute(array, axis, pairs)


def split3(value):
    high = value.astype(bf16)
    rest = value - high.astype(f32)
    mid = rest.astype(bf16)
    low = (rest - mid.astype(f32)).astype(bf16)
    return high, mid, low


def running(value_of, steps, rows, upper):
    place = lax.broadcasted_iota(jnp.int32, (rows, rows), 0)
    other = lax.broadcasted_iota(jnp.int32, (rows, rows), 1)
    tri = jnp.where((other >= place) if upper else (other <= place), 1.0, 0.0).astype(bf16)
    outs = [None] * steps
    carry = jnp.zeros((1, LANES), f32)
    order = range(steps - 1, -1, -1) if upper else range(steps)
    for n in order:
        block = value_of(n)
        total = sum(dot(tri, part) for part in split3(block)) + carry
        outs[n] = total
        carry = total[0:1] if upper else total[rows - 1 : rows]
    return outs, carry


PROJECT_TILE = 256
TERM_ROWS = 32


def project_kernel(local_heads, tokens_ref, gain_ref, weight_ref, bias_ref, input_ref, out_ref,
                   terms_ref, turned_ref, forget_ref, carry_ref):
    rows = tokens_ref.shape[0]
    wide = weight_ref.shape[1] - LANES

    @pl.when(pl.program_id(0) == 0)
    def _():
        carry_ref[...] = jnp.zeros_like(carry_ref)

    tokens = tokens_ref[...].astype(f32)
    input1 = (tokens * inverse_rms(tokens) * gain_ref[0:1, :]).astype(bf16)
    input_ref[...] = input1
    raw = dot(input1, weight_ref[...])
    out_ref[...] = raw[:, :wide].astype(bf16)
    forget = (raw[:, wide:] + bias_ref[0:1, :]).astype(bf16).astype(f32)
    forget_ref[...] = forget
    lane = lax.broadcasted_iota(jnp.int32, (rows, LANES), 1)
    logf = jnp.minimum(forget, 0.0) - jnp.log1p(jnp.exp(-jnp.abs(forget)))
    logf = jnp.where(lane < local_heads, logf, 0.0)
    place = lax.broadcasted_iota(jnp.int32, (rows, rows), 0)
    other = lax.broadcasted_iota(jnp.int32, (rows, rows), 1)
    tri = jnp.where(other <= place, 1.0, 0.0).astype(bf16)
    sums = sum(dot(tri, part) for part in split3(logf)) + carry_ref[0:1, :]
    carry_ref[0:1, :] = sums[rows - 1 : rows, :]
    high, mid, low = split3(sums)
    terms = (
        high.astype(f32)
        + pltpu.roll(mid.astype(f32), local_heads, 1)
        + pltpu.roll(low.astype(f32), 2 * local_heads, 1)
        + jnp.where(lane == 3 * local_heads, 1.0, 0.0)
    ).astype(bf16)
    terms_ref[...] = terms
    turned_ref[...] = terms.T[0:TERM_ROWS, :]


def project(tokens, gain, weight, bias, wide, local_heads):
    rows, width = tokens.shape

    def tile(columns):
        return pl.BlockSpec((PROJECT_TILE, columns), lambda n: (n, 0))

    def whole(*shape):
        return pl.BlockSpec(shape, lambda n: (0, 0))

    return pl.pallas_call(
        functools.partial(project_kernel, local_heads),
        grid=(rows // PROJECT_TILE,),
        in_specs=[tile(width), whole(8, width), whole(width, wide + LANES), whole(8, LANES)],
        out_specs=[
            tile(width),
            tile(wide),
            tile(LANES),
            pl.BlockSpec((TERM_ROWS, PROJECT_TILE), lambda n: (0, n)),
            tile(LANES),
        ],
        out_shape=[
            jax.ShapeDtypeStruct((rows, width), bf16),
            jax.ShapeDtypeStruct((rows, wide), bf16),
            jax.ShapeDtypeStruct((rows, LANES), bf16),
            jax.ShapeDtypeStruct((TERM_ROWS, rows), bf16),
            jax.ShapeDtypeStruct((rows, LANES), f32),
        ],
        scratch_shapes=[pltpu.VMEM((8, LANES), f32)],
        cost_estimate=pl.CostEstimate(
            flops=2 * rows * width * (wide + LANES), transcendentals=rows * LANES,
            bytes_accessed=20_000_000,
        ),
        name="project",
    )(tokens, gain, weight, bias)


def decay_back_kernel(own_ref, halo_ref, out_ref):
    rows = 256
    steps = own_ref.shape[0] // rows
    own, _ = running(lambda n: own_ref[n * rows : (n + 1) * rows, :], steps, rows, True)
    halo, _ = running(lambda n: halo_ref[n * rows : (n + 1) * rows, :], steps, rows, False)
    for n in range(steps):
        part = slice(n * rows, (n + 1) * rows)
        out_ref[part, :] = own[n] + (halo[n] - halo_ref[part, :])


def decay_back(own, halo):
    return pl.pallas_call(
        decay_back_kernel,
        out_shape=jax.ShapeDtypeStruct(own.shape, f32),
        name="decay_back",
    )(own, halo)


QUERY, KEY, TOTAL = range(3)


def placing(pair, local_heads, role):
    row = lax.broadcasted_iota(jnp.int32, (LANES, LANES), 0)
    col = lax.broadcasted_iota(jnp.int32, (LANES, LANES), 1)
    head = jnp.where(col < 64, 2 * pair + 1, 2 * pair)
    spot = jnp.where(col < 64, col, col - 64)
    term = spot - 3 * role
    is_term = (term >= 0) & (term < 3) & (row == term * local_heads + head)
    if role == QUERY:
        ones = (spot >= 3) & (spot < 9)
    else:
        ones = (spot < 3) & (role == KEY)
    is_one = ones & (row == 3 * local_heads)
    sign = -1.0 if role == KEY else 1.0
    return (jnp.where(is_term, sign, 0.0) + jnp.where(is_one, 1.0, 0.0)).astype(bf16)


def allowed_pairs(first_key, query_tile, rows, begin_row):
    shape = (K_TILE, Q_TILE)
    key_place = first_key + lax.broadcasted_iota(jnp.int32, shape, 0)
    query_place = rows + query_tile * Q_TILE + lax.broadcasted_iota(jnp.int32, shape, 1)
    return (key_place >= begin_row) & (key_place <= query_place)


def key_range(ranges_ref, query_tile, rows, own):
    count = rows // K_TILE
    base = count if own else 0
    first = jnp.clip(ranges_ref[0, query_tile] - base, 0, count)
    full = jnp.clip(ranges_ref[1, query_tile] - base, first, count)
    return first, full


def key_loops(ranges_ref, query_tile, rows, own, step, carry):
    first, full = key_range(ranges_ref, query_tile, rows, own)
    inside = query_tile * (Q_TILE // K_TILE) if own else rows // K_TILE
    full = jnp.minimum(full, inside)
    carry = lax.fori_loop(first, full, functools.partial(step, True), carry)
    carry = lax.fori_loop(full, inside, functools.partial(step, False), carry)
    if own:
        carry = lax.fori_loop(
            inside, inside + Q_TILE // K_TILE, functools.partial(step, True), carry
        )
    return carry


def tile_of(number, size):
    return pl.ds(pl.multiple_of(number * size, size), size)


def fill_keys(pair, local_heads, own, first, key_ref, terms_ref, keys):
    place = placing(pair, local_heads, KEY)
    lane = lax.broadcasted_iota(jnp.int32, (K_TILE, LANES), 1)
    rows = key_ref.shape[0]
    if not own:
        last = terms_ref[:, rows - LANES : rows].T
        total = dot(last, placing(pair, local_heads, TOTAL)[0:TERM_ROWS, :])[LANES - 1 : LANES, :]

    def fill(n, carry):
        here = tile_of(n, K_TILE)
        if own:
            extra = dot(terms_ref[here, :], place).astype(bf16)
        else:
            extra = dot(terms_ref[:, here].T, place[0:TERM_ROWS, :])
            extra = (extra + total).astype(bf16)
        key = key_ref[here, :]
        keys[0][here, :] = jnp.where(lane < 64, key, extra)
        keys[1][here, :] = jnp.where(lane < 64, extra, key)
        return carry

    lax.fori_loop(first, rows // K_TILE, fill, 0)


def query_tiles(q_ref, terms_ref, place, here, scaling):
    lane = lax.broadcasted_iota(jnp.int32, (Q_TILE, LANES), 1)
    extra = dot(terms_ref[here, :], place).astype(bf16)
    query = (q_ref[here, :].astype(f32) * scaling).astype(bf16)
    return jnp.where(lane < 64, query, extra), jnp.where(lane < 64, extra, query)


def attend_kernel(local_heads, own, ranges_ref, q_ref, k_ref, v_ref, t_query_ref, t_key_ref,
                  begin_ref, *refs):
    if own:
        acc_out_ref, state_out_ref, key0, key1, values, acc0, acc1 = refs
    else:
        acc_in_ref, state_in_ref, o_ref, lse_ref, key0, key1, values, acc0, acc1 = refs
    pair = pl.program_id(0)
    rows = q_ref.shape[0]
    base = rows if own else 0
    keys, accs = (key0, key1), (acc0, acc1)
    first, _ = key_range(ranges_ref, 0, rows, own)
    fill_keys(pair, local_heads, own, first, k_ref, t_key_ref, keys)

    def turn(n, carry):
        values[:, tile_of(n, K_TILE)] = v_ref[tile_of(n, K_TILE), :].T
        return carry

    lax.fori_loop(first, rows // K_TILE, turn, 0)
    place = placing(pair, local_heads, QUERY)

    def query_loop(tile, carry):
        here = tile_of(tile, Q_TILE)
        queries = query_tiles(q_ref, t_query_ref, place, here, 64**-0.5)
        begin_row = begin_ref[0:1, here]
        if own:
            low = jnp.full((1, Q_TILE), FAR, f32)
            zero = jnp.zeros((1, Q_TILE), f32)
            state = (low, zero, low, zero)
            for acc in accs:
                acc[...] = jnp.zeros_like(acc)
        else:
            state = tuple(state_in_ref[n : n + 1, here] for n in range(4))
            for h in range(2):
                accs[h][...] = acc_in_ref[64 * h : 64 * (h + 1), here]

        def step(masked, number, state):
            there = tile_of(number, K_TILE)
            fresh = []
            if masked:
                allowed = allowed_pairs(base + number * K_TILE, tile, rows, begin_row)
            for h in range(2):
                largest, total = state[2 * h], state[2 * h + 1]
                scores = dot(keys[h][there, :], queries[h], NT)
                if masked:
                    scores = jnp.where(allowed, scores, FAR)
                now = jnp.maximum(largest, jnp.max(scores, axis=0, keepdims=True))
                fade = jnp.exp(largest - now)
                weights = jnp.exp(scores - now)
                total = total * fade + jnp.sum(weights, axis=0, keepdims=True)
                accs[h][...] = accs[h][...] * fade + dot(
                    values[64 * h : 64 * (h + 1), there], weights.astype(bf16)
                )
                fresh += [now, total]
            return tuple(fresh)

        state = key_loops(ranges_ref, tile, rows, own, step, state)
        if own:
            for h in range(2):
                acc_out_ref[64 * h : 64 * (h + 1), here] = accs[h][...]
            for n in range(4):
                state_out_ref[n : n + 1, here] = state[n]
        else:
            mixed = jnp.concatenate(
                [accs[h][...] * (1.0 / state[2 * h + 1]) for h in range(2)], axis=0
            )
            o_ref[here, :] = mixed.T.astype(bf16)
            for h in range(2):
                lse_ref[h : h + 1, here] = state[2 * h] + jnp.log(state[2 * h + 1])
        return carry

    lax.fori_loop(0, rows // Q_TILE, query_loop, 0)


def lane_block(rows, offset):
    return pl.BlockSpec((rows, LANES), lambda p, *_: (0, offset + p))


def fixed(shape):
    return pl.BlockSpec(shape, lambda p, *_: (0, 0))


def pair_block(height, rows):
    return pl.BlockSpec((height, rows), lambda p, *_: (p, 0))


def attend(own, ranges, query, key_value, terms, key_terms, begins, local_heads, so_far=()):
    rows = query.shape[0]
    pairs = local_heads // 2
    running_specs = [pair_block(LANES, rows), pair_block(8, rows)]
    running_shape = (
        jax.ShapeDtypeStruct((LANES * pairs, rows), f32),
        jax.ShapeDtypeStruct((8 * pairs, rows), f32),
    )
    final_specs = [lane_block(rows, 0), pair_block(8, rows)]
    final_shape = (
        jax.ShapeDtypeStruct((rows, pairs * LANES), bf16),
        jax.ShapeDtypeStruct((8 * pairs, rows), f32),
    )
    return pl.pallas_call(
        functools.partial(attend_kernel, local_heads, own),
        grid_spec=pltpu.PrefetchScalarGridSpec(
            num_scalar_prefetch=1,
            grid=(pairs,),
            in_specs=[
                lane_block(rows, 0),
                lane_block(rows, 0),
                lane_block(rows, pairs),
                fixed((rows, LANES)),
                fixed((rows, LANES) if own else (TERM_ROWS, rows)),
                fixed((8, rows)),
            ]
            + ([] if own else running_specs),
            out_specs=running_specs if own else final_specs,
            scratch_shapes=[
                pltpu.VMEM((rows, LANES), bf16),
                pltpu.VMEM((rows, LANES), bf16),
                pltpu.VMEM((LANES, rows), bf16),
                pltpu.VMEM((64, Q_TILE), f32),
                pltpu.VMEM((64, Q_TILE), f32),
            ],
        ),
        out_shape=running_shape if own else final_shape,
        cost_estimate=pl.CostEstimate(
            flops=40_000_000_000 if own else 10_000_000_000,
            transcendentals=20_000_000,
            bytes_accessed=12_000_000,
        ),
        name="attend_own" if own else "attend_prev",
    )(ranges, query, key_value, key_value, terms, key_terms, begins, *so_far)


def attend_back_kernel(local_heads, own, ranges_ref, q_ref, k_ref, v_ref, t_query_ref, t_key_ref,
                       begin_ref, grad_ref, o_ref, lse_ref, *refs):
    if own:
        dq_in_ref, decay_in_ref, dq_ref, dk_ref, dv_ref, decay_ref = refs[:6]
    else:
        dq_ref, row_decay_ref, dkv_ref, decay_ref = refs[:4]
        dk_ref, dv_ref = dkv_ref.at[0], dkv_ref.at[1]
    key0, key1, key_t0, key_t1, dk0, dk1, dv, dq0, dq1 = refs[-9:]
    pair = pl.program_id(0)
    rows = q_ref.shape[0]
    base = rows if own else 0
    keys, keys_t, dks, dqs = (key0, key1), (key_t0, key_t1), (dk0, dk1), (dq0, dq1)
    first, _ = key_range(ranges_ref, 0, rows, own)
    fill_keys(pair, local_heads, own, first, k_ref, t_key_ref, keys)

    def turn(n, carry):
        here = tile_of(n, K_TILE)
        for h in range(2):
            keys_t[h][:, here] = keys[h][here, :].T
        return carry

    lax.fori_loop(first, rows // K_TILE, turn, 0)
    for ref in (dk0, dk1, dv):
        ref[...] = jnp.zeros_like(ref)
    place = placing(pair, local_heads, QUERY)
    lane = lax.broadcasted_iota(jnp.int32, (Q_TILE, LANES), 1)
    pick_row = lax.broadcasted_iota(jnp.int32, (8, LANES), 0)
    pick_lane = lax.broadcasted_iota(jnp.int32, (8, LANES), 1)
    pick = jnp.where((pick_lane // 64) == pick_row, 1.0, 0.0)
    sums_ref = decay_ref if own else row_decay_ref

    @pl.when(pair == 0)
    def _():
        if own:
            decay_ref[...] = decay_in_ref[...]
        else:
            decay_ref[...] = jnp.zeros_like(decay_ref)
            row_decay_ref[...] = jnp.zeros_like(row_decay_ref)

    def query_tile(tile):
        here = tile_of(tile, Q_TILE)
        queries = query_tiles(q_ref, t_query_ref, place, here, 64**-0.5)
        begin_row = begin_ref[0:1, here]
        grad = grad_ref[here, :]
        nothing = jnp.zeros_like(grad)
        grads = (jnp.where(lane < 64, grad, nothing), jnp.where(lane < 64, nothing, grad))
        product = grad.astype(f32) * o_ref[here, :].astype(f32)
        inner = dot(pick, product, NT, precision=lax.Precision.HIGHEST)
        for dq in dqs:
            dq[...] = jnp.zeros_like(dq)

        def step(masked, number, state):
            there = tile_of(number, K_TILE)
            if masked:
                allowed = allowed_pairs(base + number * K_TILE, tile, rows, begin_row)
            value = v_ref[there, :]
            value_part = 0.0
            for h in range(2):
                scores = dot(keys[h][there, :], queries[h], NT)
                prob = jnp.exp(scores - lse_ref[h : h + 1, here])
                if masked:
                    prob = jnp.where(allowed, prob, 0.0)
                grad_prob = dot(value, grads[h], NT)
                grad_score = (prob * (grad_prob - inner[h : h + 1, :])).astype(bf16)
                value_part = value_part + dot(prob.astype(bf16), grads[h])
                dks[h][there, :] += dot(grad_score, queries[h])
                dqs[h][...] += dot(keys_t[h][:, there], grad_score)
            dv[there, :] += value_part
            return state

        key_loops(ranges_ref, tile, rows, own, step, 0)
        turned = [dq[...].T for dq in dqs]
        dq_tile = jnp.where(lane < 64, turned[0], turned[1]) * 64**-0.5
        if own:
            dq_tile = dq_tile + dq_in_ref[here, :]
        dq_ref[here, :] = dq_tile.astype(dq_ref.dtype)
        sums = sums_ref[here, :]
        sums = sums + jnp.where(lane == 2 * pair, turned[0][:, 64:65], 0.0)
        sums = sums + jnp.where(lane == 2 * pair + 1, turned[1][:, 0:1], 0.0)
        sums_ref[here, :] = sums

    def query_loop(tile, carry):
        if own:
            query_tile(tile)
        else:
            reaches = key_range(ranges_ref, tile, rows, own)[0] < rows // K_TILE
            pl.when(reaches)(lambda: query_tile(tile))

            @pl.when(jnp.logical_not(reaches))
            def _():
                dq_ref[tile_of(tile, Q_TILE), :] = jnp.zeros((Q_TILE, LANES), dq_ref.dtype)

        return carry

    lax.fori_loop(0, rows // Q_TILE, query_loop, 0)
    sign = -1.0 if own else 1.0

    def finish(n, carry):
        here = tile_of(n, Q_TILE)
        left, right = dk0[here, :], dk1[here, :]
        dk_ref[here, :] = jnp.where(lane < 64, left, right).astype(dk_ref.dtype)
        dv_ref[here, :] = dv[here, :].astype(dv_ref.dtype)
        decay = decay_ref[here, :]
        decay = decay + jnp.where(lane == 2 * pair, sign * left[:, 67:68], 0.0)
        decay = decay + jnp.where(lane == 2 * pair + 1, sign * right[:, 3:4], 0.0)
        decay_ref[here, :] = decay
        return carry

    lax.fori_loop(0, rows // Q_TILE, finish, 0)


def attend_back(
    own, ranges, query, key_value, terms, key_terms, begins, grad, mixed, lse, local_heads,
    so_far=(),
):
    rows = query.shape[0]
    pairs = local_heads // 2
    wide = jax.ShapeDtypeStruct((rows, pairs * LANES), f32)
    sums = jax.ShapeDtypeStruct((rows, LANES), f32)
    if own:
        out_specs = [lane_block(rows, 0)] * 3 + [fixed((rows, LANES))]
        out_shape = (jax.ShapeDtypeStruct(wide.shape, bf16), wide, wide, sums)
    else:
        both = pl.BlockSpec((2, rows, LANES), lambda p, *_: (0, 0, p))
        out_specs = [lane_block(rows, 0), fixed((rows, LANES)), both, fixed((rows, LANES))]
        out_shape = (
            wide, sums, jax.ShapeDtypeStruct((2, rows, pairs * LANES), bf16), sums,
        )
    return pl.pallas_call(
        functools.partial(attend_back_kernel, local_heads, own),
        grid_spec=pltpu.PrefetchScalarGridSpec(
            num_scalar_prefetch=1,
            grid=(pairs,),
            in_specs=[
                lane_block(rows, 0),
                lane_block(rows, 0),
                lane_block(rows, pairs),
                fixed((rows, LANES)),
                fixed((rows, LANES) if own else (TERM_ROWS, rows)),
                fixed((8, rows)),
                lane_block(rows, 0),
                lane_block(rows, 0),
                pair_block(8, rows),
            ]
            + ([lane_block(rows, 0), fixed((rows, LANES))] if own else []),
            out_specs=out_specs,
            scratch_shapes=[
                pltpu.VMEM((rows, LANES), bf16),
                pltpu.VMEM((rows, LANES), bf16),
                pltpu.VMEM((LANES, rows), bf16),
                pltpu.VMEM((LANES, rows), bf16),
                pltpu.VMEM((rows, LANES), f32),
                pltpu.VMEM((rows, LANES), f32),
                pltpu.VMEM((rows, LANES), f32),
                pltpu.VMEM((LANES, Q_TILE), f32),
                pltpu.VMEM((LANES, Q_TILE), f32),
            ],
        ),
        out_shape=out_shape,
        cost_estimate=pl.CostEstimate(
            flops=20_000_000_000 if own else 10_000_000_000,
            transcendentals=20_000_000,
            bytes_accessed=25_000_000,
        ),
        name="attend_back_own" if own else "attend_back_prev",
    )(
        ranges, query, key_value, key_value, terms, key_terms, begins, grad, mixed, lse, *so_far
    )


PIECES = 4


def partners():
    me = lax.axis_index("head")
    near = me + 1 - 2 * (me % 2)
    far = (me + 2) % 4
    cross = (near + 2) % 4
    return me, near, far, cross


def signal(other):
    pl.semaphore_signal(
        pltpu.get_barrier_semaphore(), inc=1, device_id=other, device_id_type=pl.DeviceIdType.MESH
    )


def greet(others):
    for other in others:
        signal(other)
    pl.semaphore_wait(pltpu.get_barrier_semaphore(), len(others))


def remote(source, target, send, receive, other):
    return pltpu.make_async_remote_copy(
        src_ref=source,
        dst_ref=target,
        send_sem=send,
        recv_sem=receive,
        device_id=other,
        device_id_type=pl.DeviceIdType.MESH,
    )


def on_head(index):
    return {"head": index}


def on_blk(index):
    return {"blk": index}


def piece_at(ref, slot, piece, size):
    span = size // PIECES
    return ref.at[pl.ds(pl.multiple_of(slot * size + piece * span, span), span), :]


class Slots:
    def __init__(self, by_device):
        me, near, far, cross = partners()
        if by_device:
            self.own = self.sent_near = self.sent_far = me
            self.near, self.far, self.cross = near, far, cross
            self.passed = far
        else:
            self.own, self.sent_near, self.sent_far = 3, 2, 1
            self.near, self.far, self.cross = 2, 1, 0
            self.passed = 0


def spread_piece(source, all_ref, size, sems, piece, slots):
    me, near, far, _ = partners()
    far_send, far_recv, near_send, near_recv, _, _, own = sems
    copies = (
        remote(source, piece_at(all_ref, slots.sent_far, piece, size), far_send.at[piece],
               far_recv.at[piece], on_head(far)),
        remote(source, piece_at(all_ref, slots.sent_near, piece, size), near_send.at[piece],
               near_recv.at[piece], on_head(near)),
        pltpu.make_async_copy(source, piece_at(all_ref, slots.own, piece, size), own.at[piece]),
    )
    for copy in copies:
        copy.start()
    return copies


def hand_on(all_ref, size, sems, sent, slots):
    me, near, far, cross = partners()
    far_send, far_recv, near_send, near_recv, on_send, on_recv, own = sems
    passed = []
    for piece in range(PIECES):
        there = piece_at(all_ref, slots.far, piece, size)
        remote(there, there, far_send.at[piece], far_recv.at[piece], on_head(far)).wait_recv()
        copy = remote(
            there, piece_at(all_ref, slots.passed, piece, size), on_send.at[piece],
            on_recv.at[piece], on_head(near),
        )
        copy.start()
        passed.append(copy)

    def finish():
        for piece in range(PIECES):
            to_far, to_near, local = sent[piece]
            to_far.wait_send()
            to_near.wait_send()
            local.wait()
            passed[piece].wait_send()
            there = piece_at(all_ref, slots.near, piece, size)
            remote(there, there, near_send.at[piece], near_recv.at[piece], on_head(near)).wait_recv()
            there = piece_at(all_ref, slots.cross, piece, size)
            remote(there, there, on_send.at[piece], on_recv.at[piece], on_head(near)).wait_recv()

    return finish


def gather_sems():
    return [pltpu.SemaphoreType.DMA((PIECES,)) for _ in range(7)]


def blk_peers():
    here = lax.axis_index("blk")
    half = lax.axis_size("blk") // 2
    low, high = here % 2, here // 2
    partner = here + 1 - 2 * low
    after = [((high + t) % half) * 2 + low for t in range(half)]
    return here, partner, after


class Line:
    def __init__(self, block_of, kinds, sems):
        self.block_of, self.kinds = block_of, kinds
        self.pair_send, self.pair_recv, self.up_send, self.up_recv, self.down_send, self.down_recv = sems
        here = lax.axis_index("blk")
        self.half = lax.axis_size("blk") // 2
        self.low, self.high = here % 2, here // 2
        self.partner = here + 1 - 2 * self.low
        self.has_up, self.has_down = self.high < self.half - 1, self.high > 0

    def greet(self, others):
        greet_sum = len(others) + 1
        for other in others + [on_blk(self.partner)]:
            signal(other)
        pl.when(self.has_up)(lambda: signal(on_blk(self.at(self.high + 1))))
        pl.when(self.has_down)(lambda: signal(on_blk(self.at(self.high - 1))))
        ends = (self.high == 0).astype(jnp.int32) + (self.high == self.half - 1).astype(jnp.int32)
        pl.semaphore_wait(pltpu.get_barrier_semaphore(), greet_sum + 2 - ends)

    def at(self, high):
        return high * 2 + self.low

    def pair_copy(self, kind, high, low):
        block = self.block_of(kind, high * 2 + low)
        return remote(
            block, block, self.pair_send.at[kind, high], self.pair_recv.at[kind, high],
            on_blk(self.partner),
        )

    def up_copy(self, kind, high):
        block = self.block_of(kind, self.at(high))
        return remote(
            block, block, self.up_send.at[kind, high], self.up_recv.at[kind, high],
            on_blk(self.at(jnp.minimum(self.high + 1, self.half - 1))),
        )

    def down_copy(self, kind, high):
        block = self.block_of(kind, self.at(high))
        return remote(
            block, block, self.down_send.at[kind, high], self.down_recv.at[kind, high],
            on_blk(self.at(jnp.maximum(self.high - 1, 0))),
        )

    def launch(self, kind):
        self.pair_copy(kind, self.high, self.low).start()
        pl.when(self.has_up)(lambda: self.up_copy(kind, self.high).start())
        pl.when(self.has_down)(lambda: self.down_copy(kind, self.high).start())

    def step(self, t):
        for kind in range(self.kinds):
            below, above = self.high - t, self.high + t

            @pl.when(below >= 0)
            def _():
                self.up_copy(kind, below).wait_recv()
                self.pair_copy(kind, below, self.low).start()
                pl.when(self.has_up)(lambda: self.up_copy(kind, below).start())

            @pl.when(above < self.half)
            def _():
                self.down_copy(kind, above).wait_recv()
                self.pair_copy(kind, above, self.low).start()
                pl.when(self.has_down)(lambda: self.down_copy(kind, above).start())

    def finish(self):
        for kind in range(self.kinds):

            def wait(high, carry):
                self.pair_copy(kind, high, self.low).wait_send()
                self.pair_copy(kind, high, 1 - self.low).wait_recv()

                @pl.when((high <= self.high) & self.has_up)
                def _():
                    self.up_copy(kind, high).wait_send()

                @pl.when((high >= self.high) & self.has_down)
                def _():
                    self.down_copy(kind, high).wait_send()

                return carry

            lax.fori_loop(0, self.half, wait, 0)


def gather_first_kernel(before, after, *refs):
    small_ref, weight_refs = refs[0], refs[1 : 1 + before + after]
    tokens_ref, cotangent_ref, pack_all, tokens_all, cotangent_all, pack_ref = refs[
        1 + before + after : 7 + before + after
    ]
    sems = refs[7 + before + after :]
    groups = pack_ref.shape[0]
    start = 0
    for n, ref in enumerate(weight_refs):
        if n == before:
            pack_ref[:, :, start : start + LANES] = small_ref[...]
            start += LANES
        wide = ref.shape[1] // groups
        for group in range(groups):
            pack_ref[group, :, start : start + wide] = ref[
                :, group * wide : (group + 1) * wide
            ].astype(bf16)
        start += wide
    swap_send, swap_recv, swap_own = sems[:3]
    token_sems, cotangent_sems = sems[9:16], sems[16:23]
    me, near, far, cross = partners()
    sources = (me, near, far, cross)
    line = Line(lambda kind, blk: pack_all.at[blk, sources[kind]], 4, sems[3:9])
    here = lax.axis_index("blk")
    line.greet([on_head(near), on_head(far), on_head(cross)])
    swaps = [pltpu.make_async_copy(pack_ref.at[me], pack_all.at[here, me], swap_own)]
    for kind, other in enumerate((near, far, cross)):
        swaps.append(
            remote(
                pack_ref.at[other],
                pack_all.at[here, me],
                swap_send.at[kind],
                swap_recv.at[kind],
                on_head(other),
            )
        )
    for swap in swaps:
        swap.start()
    size = tokens_ref.shape[0]
    span = size // PIECES

    def spread_all(ref, all_ref, some, slots):
        return [
            spread_piece(ref.at[pl.ds(piece * span, span), :], all_ref, size, some, piece, slots)
            for piece in range(PIECES)
        ]

    by_device, crossing = Slots(True), Slots(False)
    tokens_sent = spread_all(tokens_ref, tokens_all, token_sems, by_device)
    swaps[0].wait()
    line.launch(0)
    for kind, source in enumerate((near, far, cross)):
        block = pack_all.at[here, source]
        remote(
            block, block, swap_send.at[kind], swap_recv.at[kind], on_head(source)
        ).wait_recv()
        line.launch(kind + 1)
    cotangent_sent = spread_all(cotangent_ref, cotangent_all, cotangent_sems, crossing)
    for t in range(1, line.half):
        line.step(t)
    finish_tokens = hand_on(tokens_all, size, token_sems, tokens_sent, by_device)
    finish_cotangent = hand_on(cotangent_all, size, cotangent_sems, cotangent_sent, crossing)
    for swap in swaps[1:]:
        swap.wait_send()
    line.finish()
    finish_tokens()
    finish_cotangent()


def gather_first(before, small, after, tokens, cotangent, number):
    groups, share, _ = small.shape
    weights = [*before, *after]
    columns = LANES + sum(weight.shape[1] // groups for weight in weights)
    peers = lax.axis_size("blk")
    rows, width = tokens.shape
    whole = jax.ShapeDtypeStruct((groups * rows, width), bf16)
    vmem, anywhere = pl.BlockSpec(memory_space=pltpu.VMEM), pl.BlockSpec(memory_space=pl.ANY)
    all_pack, all_tokens, all_cotangent = pl.pallas_call(
        functools.partial(gather_first_kernel, len(before), len(after)),
        in_specs=[vmem] * (3 + len(weights)),
        out_specs=[anywhere] * 3,
        out_shape=[jax.ShapeDtypeStruct((peers, groups, share, columns), bf16), whole, whole],
        scratch_shapes=[
            pltpu.VMEM((groups, share, columns), bf16),
            pltpu.SemaphoreType.DMA((3,)),
            pltpu.SemaphoreType.DMA((3,)),
            pltpu.SemaphoreType.DMA,
        ]
        + [pltpu.SemaphoreType.DMA((4, peers // 2)) for _ in range(6)]
        + gather_sems()
        + gather_sems(),
        compiler_params=pltpu.CompilerParams(collective_id=number, has_side_effects=True),
        cost_estimate=pl.CostEstimate(
            flops=70_000_000_000, transcendentals=0, bytes_accessed=30_000_000
        ),
        name="gather_first",
    )(small, *weights, tokens, cotangent)
    return all_pack.reshape(peers * groups * share, columns), all_tokens, all_cotangent


class Sum:
    def __init__(self, part_ref, buffers, sems, size, by_device):
        self.part_ref, self.size, self.span = part_ref, size, size // PIECES
        self.slots = Slots(by_device)
        self.near_buf, self.turn_buf, self.far_buf = buffers
        self.near_send, self.near_recv, self.far_send, self.far_recv = sems
        self.near_copies, self.far_copies = [], []

    def piece(self, n):
        return slice(n * self.span, (n + 1) * self.span)

    def start(self):
        me, near, far, cross = partners()
        for which, shard in ((0, self.slots.cross), (1, self.slots.near)):
            for n in range(PIECES):
                copy = remote(
                    piece_at(self.part_ref, shard, n, self.size),
                    self.near_buf.at[which, pl.ds(n * self.span, self.span), :],
                    self.near_send.at[which, n],
                    self.near_recv.at[which, n],
                    on_head(near),
                )
                copy.start()
                self.near_copies.append(copy)

    def turn(self):
        me, near, far, cross = partners()
        for n in range(PIECES):
            here = self.piece(n)
            self.near_copies[n].wait_recv()
            self.turn_buf[here, :] = (
                piece_at(self.part_ref, self.slots.far, n, self.size)[...].astype(f32)
                + self.near_buf[0, here, :].astype(f32)
            ).astype(bf16)
            copy = remote(
                self.turn_buf.at[pl.ds(n * self.span, self.span), :],
                self.far_buf.at[pl.ds(n * self.span, self.span), :],
                self.far_send.at[n],
                self.far_recv.at[n],
                on_head(far),
            )
            copy.start()
            self.far_copies.append(copy)

    def total(self, n):
        self.near_copies[PIECES + n].wait_recv()
        self.far_copies[n].wait_recv()
        here = self.piece(n)
        return (
            piece_at(self.part_ref, self.slots.own, n, self.size)[...].astype(f32)
            + self.near_buf[1, here, :].astype(f32)
            + self.far_buf[here, :].astype(f32)
        )

    def finish(self):
        for copy in self.near_copies + self.far_copies:
            copy.wait_send()


def sum_buffers(size, width):
    return [
        pltpu.VMEM((2, size, width), bf16),
        pltpu.VMEM((size, width), bf16),
        pltpu.VMEM((size, width), bf16),
    ]


def sum_sems():
    return [
        pltpu.SemaphoreType.DMA((2, PIECES)),
        pltpu.SemaphoreType.DMA((2, PIECES)),
        pltpu.SemaphoreType.DMA((PIECES,)),
        pltpu.SemaphoreType.DMA((PIECES,)),
    ]


def exchange_kernel(local, extras, summed, weights, *refs):
    part_ref, extra_refs = refs[0], refs[1 : 1 + extras]
    refs = refs[1 + extras :]
    if weights:
        mine_ref, refs = refs[0], refs[1:]
    out_ref, all_ref, refs = refs[0], refs[1], refs[2:]
    if weights:
        weight_ref, refs = refs[0], refs[1:]
    payload, sems = refs[0], refs[1:]
    size = out_ref.shape[0]
    span = size // PIECES
    _, near, far, _ = partners()
    if weights:
        kinds = mine_ref.shape[0]
        line = Line(lambda kind, blk: weight_ref.at[blk, kind], kinds, sems[-7:-1])
        own = pltpu.make_async_copy(mine_ref, weight_ref.at[lax.axis_index("blk")], sems[-1])
        own.start()
        line.greet([on_head(near), on_head(far)])
    else:
        greet([on_head(near), on_head(far)])
    slots = Slots(summed)
    if not summed:
        shares = Sum(part_ref, sems[7:10], sems[10:14], size, True)
        shares.start()
    if weights:
        own.wait()
        for kind in range(kinds):
            line.launch(kind)
    if not summed:
        shares.turn()
    sent = []
    for piece in range(PIECES):
        if weights and piece != 2:
            hop = {0: 1, 1: 2, 3: 3}[piece]
            for t in range(hop, line.half if piece == 3 else min(hop + 1, line.half)):
                line.step(t)
        here = slice(piece * span, (piece + 1) * span)
        total = part_ref[here, :] if summed else shares.total(piece)
        result, share = local(total, here, *extra_refs)
        out_ref[here, :] = result.astype(out_ref.dtype)
        payload[here, :] = share.astype(bf16)
        source = payload.at[pl.ds(piece * span, span), :]
        sent.append(spread_piece(source, all_ref, size, sems[:7], piece, slots))
    hand_on(all_ref, size, sems[:7], sent, slots)()
    if not summed:
        shares.finish()
    if weights:
        line.finish()


def exchange(local, part, extras, summed, number, name, mine=None):
    rows, width = part.shape
    size = rows if summed else rows // 4
    vmem, anywhere = pl.BlockSpec(memory_space=pltpu.VMEM), pl.BlockSpec(memory_space=pl.ANY)
    weights = mine is not None
    inputs = [part, *extras]
    out_specs = [vmem, anywhere]
    out_shape = [
        jax.ShapeDtypeStruct((size, width), f32),
        jax.ShapeDtypeStruct((4 * size, width), bf16),
    ]
    scratch = [pltpu.VMEM((size, width), bf16)] + gather_sems()
    if not summed:
        scratch += sum_buffers(size, width) + sum_sems()
    if weights:
        peers = lax.axis_size("blk")
        inputs.append(mine)
        out_specs.append(anywhere)
        out_shape.append(jax.ShapeDtypeStruct((peers,) + mine.shape, bf16))
        scratch += [pltpu.SemaphoreType.DMA((mine.shape[0], peers // 2)) for _ in range(6)]
        scratch.append(pltpu.SemaphoreType.DMA)
    return pl.pallas_call(
        functools.partial(exchange_kernel, local, len(extras), summed, weights),
        in_specs=[vmem] * len(inputs),
        out_specs=out_specs,
        out_shape=out_shape,
        scratch_shapes=scratch,
        compiler_params=pltpu.CompilerParams(collective_id=number, has_side_effects=True),
        cost_estimate=pl.CostEstimate(
            flops=10_000_000_000 if summed else 70_000_000_000,
            transcendentals=0,
            bytes_accessed=16_000_000,
        ),
        name=name,
    )(*inputs)


def column_chunks(width):
    count = max(width // 512, 1)
    first = width - 512 * (count - 1)
    return [(0, first)] + [(first + 512 * n, 512) for n in range(count - 1)]


def finish_last_kernel(grad_ref, output_grad_ref, second_ref, first_ref, grad_middle_ref, tokens_ref,
                       gain_ref, weights_ref, output_ref, second_out_ref, tokens_grad_ref, *refs):
    buffers = (refs[0:3], refs[3:6])
    first_buffers = refs[6:9]
    pair_send, pair_recv, line_send, line_recv, swap_send, swap_recv = refs[9:15]
    first_sems = refs[15:19]
    me, near, far, cross = partners()
    others = (near, far, cross)
    here, partner, after = blk_peers()
    steps = len(after)
    greet(
        [on_head(other) for other in others]
        + [on_blk(partner)]
        + [on_blk(peer) for peer in after[1:]]
    )
    size = tokens_grad_ref.shape[0]
    first = Sum(first_ref, first_buffers, first_sems, size, True)
    chunks = []
    for ref, out_ref, some in (
        (grad_ref, weights_ref, buffers[0]), (output_grad_ref, output_ref, buffers[1])
    ):
        for start, wide in column_chunks(ref.shape[3]):
            chunks.append((ref, out_ref, some, pl.ds(start, wide)))
    groups = grad_ref.shape[1]
    first.start()
    sent = []
    for c, (ref, _, (pair_buf, _, _), at) in enumerate(chunks):
        for t in list(range(1, steps)) + [0]:
            copy = remote(
                ref.at[after[t] + partner - here, :, :, at],
                pair_buf.at[t, :, :, at],
                pair_send.at[c, t],
                pair_recv.at[c, t],
                on_blk(partner),
            )
            copy.start()
            sent.append(copy)
    first.turn()

    def swap(source_ref, out_ref, c):
        for kind, other in enumerate(others):
            copy = remote(
                source_ref.at[other], out_ref.at[me], swap_send.at[c, kind],
                swap_recv.at[c, kind], on_head(other),
            )
            copy.start()
            sent.append(copy)

    swap(second_ref, second_out_ref, len(chunks))

    def add_up(c):
        ref, out_ref, (pair_buf, line_buf, row_buf), at = chunks[c]
        block = pair_buf.at[0, :, :, at]
        remote(block, block, pair_send.at[c, 0], pair_recv.at[c, 0], on_blk(partner)).wait_recv()
        for t in range(1, steps):
            block = line_buf.at[t, :, :, at]
            remote(
                block, block, line_send.at[c, t], line_recv.at[c, t], on_blk(after[t])
            ).wait_recv()

        def add_all(group, carry):
            total = ref[here, group, :, at].astype(f32) + pair_buf[0, group, :, at].astype(f32)
            for t in range(1, steps):
                total = total + line_buf[t, group, :, at].astype(f32)
            row_buf[group, :, at] = total.astype(bf16)
            return carry

        lax.fori_loop(0, groups, add_all, 0)
        out_ref[me, :, at] = row_buf[me, :, at]
        swap(row_buf.at[:, :, at], out_ref.at[:, :, at], c)

    for c, (ref, _, (pair_buf, line_buf, _), at) in enumerate(chunks):
        for t in range(1, steps):
            block = pair_buf.at[t, :, :, at]
            remote(
                block, block, pair_send.at[c, t], pair_recv.at[c, t], on_blk(partner)
            ).wait_recv()

            def add(group, carry):
                pair_buf[t, group, :, at] = (
                    ref[after[t], group, :, at].astype(f32)
                    + pair_buf[t, group, :, at].astype(f32)
                ).astype(bf16)
                return carry

            lax.fori_loop(0, groups, add, 0)
            copy = remote(
                block, line_buf.at[t, :, :, at], line_send.at[c, t], line_recv.at[c, t],
                on_blk(after[t]),
            )
            copy.start()
            sent.append(copy)
        if c > 0:
            add_up(c - 1)
    for piece in range(PIECES):
        rows = first.piece(piece)
        tokens_grad_ref[rows, :], _ = after_first(
            first.total(piece), rows, grad_middle_ref, tokens_ref, gain_ref
        )
    add_up(len(chunks) - 1)
    second_out_ref[me] = second_ref[me]
    for c in range(len(chunks) + 1):
        if c < len(chunks):
            _, out_ref, _, at = chunks[c]
            out_ref = out_ref.at[:, :, at]
        else:
            out_ref = second_out_ref
        for kind, other in enumerate(others):
            block = out_ref.at[other]
            remote(
                block, block, swap_send.at[c, kind], swap_recv.at[c, kind], on_head(other)
            ).wait_recv()
    for copy in sent:
        copy.wait_send()
    first.finish()


def finish_last(grad, output_grad, second, groups, part_first, grad_middle, tokens, gain, number):
    peers = lax.axis_size("blk")
    share = grad.shape[0] // (peers * groups)
    rows, width = tokens.shape
    vmem = pl.BlockSpec(memory_space=pltpu.VMEM)
    half = peers // 2
    widths = (grad.shape[1], output_grad.shape[1])
    chunks = sum(len(column_chunks(width)) for width in widths)

    def blocks(columns):
        return [pltpu.VMEM((half, groups, share, columns), bf16) for _ in range(2)] + [
            pltpu.VMEM((groups, share, columns), bf16)
        ]

    return pl.pallas_call(
        finish_last_kernel,
        in_specs=[vmem] * 7,
        out_specs=[vmem] * 4,
        out_shape=[
            jax.ShapeDtypeStruct((groups, share, columns), bf16)
            for columns in widths + (second.shape[1],)
        ]
        + [jax.ShapeDtypeStruct((rows, width), f32)],
        scratch_shapes=blocks(widths[0])
        + blocks(widths[1])
        + sum_buffers(rows, width)
        + [pltpu.SemaphoreType.DMA((chunks, half)) for _ in range(4)]
        + [pltpu.SemaphoreType.DMA((chunks + 1, 3)) for _ in range(2)]
        + sum_sems(),
        compiler_params=pltpu.CompilerParams(
            collective_id=number, has_side_effects=True, vmem_limit_bytes=60 << 20
        ),
        cost_estimate=pl.CostEstimate(
            flops=80_000_000_000, transcendentals=0, bytes_accessed=40_000_000
        ),
        name="finish_last",
    )(
        grad.reshape(peers, groups, share, widths[0]),
        output_grad.reshape(peers, groups, share, widths[1]),
        second.reshape(groups, share, second.shape[1]),
        part_first, grad_middle, tokens, gain,
    )


def inverse_rms(value):
    return lax.rsqrt(jnp.mean(value * value, axis=1, keepdims=True) + epsilon)


def through_norm(grad, value):
    factor = inverse_rms(value)
    normed = value * factor
    return factor * (grad - normed * jnp.mean(grad * normed, axis=1, keepdims=True))


def after_attention(total, here, tokens_ref, gain_ref):
    middle = tokens_ref[here, :].astype(f32) + total
    return middle, middle * inverse_rms(middle) * gain_ref[0:1, :]


def after_hidden(total, here, cotangent_ref, middle_ref, gain_ref):
    grad = cotangent_ref[here, :].astype(f32) + through_norm(
        total * gain_ref[0:1, :], middle_ref[here, :]
    )
    return grad, grad


def after_first(total, here, grad_ref, tokens_ref, gain_ref):
    grad = grad_ref[here, :] + through_norm(
        total * gain_ref[0:1, :], tokens_ref[here, :].astype(f32)
    )
    return grad, None


FEED_TILE = 256
FEED_COLUMNS = 512


def feed_kernel(input_ref, cotangent_ref, weight_ref, down_weight_ref, down_ref, grad_ref, total_ref,
                acts, turned0, turned1, stage, near_buf, far_buf, near_send, near_recv, far_send, far_recv):
    step = pl.program_id(0)
    hidden_width = down_weight_ref.shape[1]
    size = total_ref.shape[0]
    per = size // FEED_TILE
    tiles = 4 * per
    _, near, far, _ = partners()

    @pl.when(step == 0)
    def _():
        greet([on_head(near), on_head(far)])

    def to_near(which, piece):
        return remote(
            stage.at[which * per + piece],
            near_buf.at[which, piece],
            near_send.at[which, piece],
            near_recv.at[which, piece],
            on_head(near),
        )

    def to_far(piece):
        return remote(
            near_buf.at[0, piece], far_buf.at[piece], far_send.at[piece], far_recv.at[piece],
            on_head(far),
        )

    @pl.when(step < tiles)
    def _():
        here = tile_of(step, FEED_TILE)
        inputs, cotangent = input_ref[...], cotangent_ref[...]
        turned0[:, here] = inputs.T
        turned1[:, here] = cotangent.T
        gate_at, up_at, down_at = (
            slice(n * hidden_width, (n + 1) * hidden_width) for n in range(3)
        )
        gate = dot(inputs, weight_ref[:, gate_at])
        up = dot(inputs, weight_ref[:, up_at])
        grad_hidden = dot(cotangent, down_weight_ref[...])
        opening = jax.nn.sigmoid(gate)
        active = gate * opening
        hidden = (active * up).astype(bf16)
        grad_gate = (grad_hidden * up * opening * (1.0 + gate * (1.0 - opening))).astype(bf16)
        grad_up = (grad_hidden * active).astype(bf16)
        acts[here, gate_at] = grad_gate
        acts[here, up_at] = grad_up
        acts[here, down_at] = hidden
        down_ref[...] = dot(hidden, down_weight_ref[...], NT).astype(bf16)
        back = dot(grad_gate, weight_ref[:, gate_at], NT) + dot(
            grad_up, weight_ref[:, up_at], NT
        )
        for piece in range(per):
            for which, first in ((0, 0), (1, 2 * per)):

                @pl.when(step == first + piece)
                def _():
                    stage[which * per + piece] = back.astype(bf16)
                    to_near(which, piece).start()

            @pl.when(step == per + piece)
            def _():
                to_near(0, piece).wait_recv()
                near_buf[0, piece] = (back + near_buf[0, piece].astype(f32)).astype(bf16)
                to_far(piece).start()

            @pl.when(step == 3 * per + piece)
            def _():
                total_ref[piece * FEED_TILE : (piece + 1) * FEED_TILE, :] = back

    @pl.when(step >= tiles)
    def _():
        at = tile_of(step - tiles, FEED_COLUMNS)
        from_input = (step - tiles) * FEED_COLUMNS < 2 * hidden_width

        @pl.when(from_input)
        def _():
            grad_ref[...] = dot(turned0[...], acts[:, at]).astype(bf16)

        @pl.when(jnp.logical_not(from_input))
        def _():
            grad_ref[...] = dot(turned1[...], acts[:, at]).astype(bf16)

    @pl.when(step == pl.num_programs(0) - 1)
    def _():
        for piece in range(per):
            here = slice(piece * FEED_TILE, (piece + 1) * FEED_TILE)
            to_near(1, piece).wait_recv()
            to_far(piece).wait_recv()
            total_ref[here, :] += near_buf[1, piece].astype(f32) + far_buf[piece].astype(f32)
            to_near(0, piece).wait_send()
            to_near(1, piece).wait_send()
            to_far(piece).wait_send()


def feed(inputs, cotangent, weight, down_weight, number):
    rows, width = inputs.shape
    columns = weight.shape[1] + down_weight.shape[1]
    size = rows // 4
    tiles, per = rows // FEED_TILE, size // FEED_TILE
    tile = pl.BlockSpec((FEED_TILE, width), lambda n: (jnp.minimum(n, tiles - 1), 0))

    def whole(shape):
        return pl.BlockSpec(shape, lambda n: (0, 0), pipeline_mode=pl.Buffered(1))

    return pl.pallas_call(
        feed_kernel,
        grid=(tiles + columns // FEED_COLUMNS,),
        in_specs=[tile, tile, whole(weight.shape), whole(down_weight.shape)],
        out_specs=[
            tile,
            pl.BlockSpec((width, FEED_COLUMNS), lambda n: (0, jnp.maximum(n - tiles, 0))),
            whole((size, width)),
        ],
        out_shape=[
            jax.ShapeDtypeStruct((rows, width), bf16),
            jax.ShapeDtypeStruct((width, columns), bf16),
            jax.ShapeDtypeStruct((size, width), f32),
        ],
        scratch_shapes=[
            pltpu.VMEM((rows, columns), bf16),
            pltpu.VMEM((width, rows), bf16),
            pltpu.VMEM((width, rows), bf16),
            pltpu.VMEM((2 * per, FEED_TILE, width), bf16),
            pltpu.VMEM((2, per, FEED_TILE, width), bf16),
            pltpu.VMEM((per, FEED_TILE, width), bf16),
            pltpu.SemaphoreType.DMA((2, per)),
            pltpu.SemaphoreType.DMA((2, per)),
            pltpu.SemaphoreType.DMA((per,)),
            pltpu.SemaphoreType.DMA((per,)),
        ],
        compiler_params=pltpu.CompilerParams(
            collective_id=number, has_side_effects=True, vmem_limit_bytes=63 << 20
        ),
        cost_estimate=pl.CostEstimate(
            flops=6 * rows * width * columns, transcendentals=rows * columns // 3,
            bytes_accessed=45_000_000,
        ),
        name="feed",
    )(inputs, cotangent, weight, down_weight)


def over_tokens(operand, other_side):
    return lax.dot_general(
        operand, other_side, (((0,), (0,)), ((), ())), preferred_element_type=f32
    )


def sent_columns(pieces, groups):
    packed = jnp.concatenate(
        [piece.reshape(piece.shape[0], groups, -1) for piece in pieces], axis=2
    )
    mine = lax.all_to_all(packed, "head", split_axis=1, concat_axis=0, tiled=True)
    return mine.reshape(mine.shape[0], mine.shape[2])


def all_rows(mine):
    return lax.all_gather(mine, "blk", axis=0, tiled=True)


def row_sums(grad):
    return lax.psum_scatter(grad, "blk", scatter_dimension=0, tiled=True)


def crossing_sum(part):
    cross, far, near, own = (piece.astype(f32) for piece in jnp.split(part, 4))
    members = range(lax.axis_size("head"))
    got = lax.ppermute(
        jnp.concatenate([cross, near]).astype(bf16), "head",
        [(n, n + 1 - 2 * (n % 2)) for n in members],
    )
    of_far, of_own = jnp.split(got.astype(f32), 2)
    back = lax.ppermute(
        (far + of_far).astype(bf16), "head", [(n, (n + 2) % 4) for n in members]
    )
    return own + of_own + back.astype(f32)


def body(
    tokens,
    segment,
    norm1_gain,
    w_query,
    w_key,
    w_value,
    w_gate_out,
    w_forget,
    forget_bias,
    w_output,
    norm2_gain,
    w_gate,
    w_up,
    w_down,
    cotangent,
):
    token_rows, model_width = tokens.shape
    groups = lax.axis_size("head")
    head_count = forget_bias.shape[0]
    local_heads = head_count // groups
    local_width = model_width // groups
    hidden_width = w_gate.shape[1] // groups
    rows = token_rows * groups
    share = w_query.shape[0]
    group = lax.axis_index("head")

    low = lambda array: array.astype(bf16)
    spread = lambda gain: jnp.broadcast_to(low(gain)[:, None, None], (share, groups, 1))
    forget_low = low(w_forget).reshape(share, groups, local_heads)
    rest = LANES - local_heads - 2
    small = jnp.concatenate(
        [forget_low, spread(norm1_gain), spread(norm2_gain), jnp.zeros((share, groups, rest), bf16)],
        axis=2,
    )
    first, tokens_all, cotangent_all = gather_first(
        (w_key, w_value), jnp.swapaxes(small, 0, 1), (w_query, w_gate_out, w_output), tokens,
        cotangent, 0,
    )
    kv_width = 2 * local_width + LANES
    output_weight = first[:, kv_width + 2 * local_width :]

    def gain_rows(column):
        gain = first[:, 2 * local_width + local_heads + column].astype(f32)
        return jnp.broadcast_to(gain[None, :], (8, model_width))

    gain1, gain2 = gain_rows(0), gain_rows(1)
    bias = lax.dynamic_slice_in_dim(forget_bias, group * local_heads, local_heads, 0)
    bias = jnp.broadcast_to(jnp.pad(bias, (0, LANES - local_heads))[None, :], (8, LANES))
    input1, key_value, terms, turned_terms, forget = project(
        tokens_all, gain1, first, bias, 2 * local_width, local_heads
    )
    earlier_kv = passed_along(key_value, "blk", 1)
    earlier_terms = passed_along(turned_terms, "blk", 1)
    query = dot(input1, first[:, kv_width : kv_width + local_width]).astype(bf16)
    gate_raw = dot(
        input1, first[:, kv_width + local_width : kv_width + 2 * local_width]
    )

    segment_plus = segment + 1
    earlier_segment = passed_along(segment_plus, "blk", 1)
    window = jnp.concatenate([earlier_segment, segment_plus])
    begins = jnp.sum(
        (window[:, None] < segment_plus[None, :]).astype(jnp.int32), axis=0
    )
    tiles = begins.reshape(rows // Q_TILE, Q_TILE)
    ranges = jnp.stack([tiles[:, 0] // K_TILE, (tiles[:, -1] + K_TILE - 1) // K_TILE])
    begins = jnp.broadcast_to(begins[None, :], (8, rows))

    so_far = attend(True, ranges, query, key_value, terms, terms, begins, local_heads)
    later = lax.optimization_barrier((w_gate, w_up, w_down, key_value))
    mine = sent_columns([low(weight) for weight in later[:3]], groups)
    mine, earlier_kv, earlier_terms, so_far = lax.optimization_barrier(
        (mine, earlier_kv, earlier_terms, so_far)
    )
    second = all_rows(mine[:, : 2 * hidden_width])
    mine_down = mine[:, 2 * hidden_width :].reshape(groups, share, hidden_width)
    attended, lse = attend(
        False, ranges, query, earlier_kv, terms, earlier_terms, begins, local_heads, so_far
    )
    opened = jax.nn.sigmoid(gate_raw)
    attended_wide = attended.astype(f32)
    gated = (opened * attended_wide).astype(bf16)
    branch = dot(gated, output_weight, NT).astype(bf16)
    middle, input2, down_weight = exchange(
        after_attention, branch, [tokens, gain2], False, 1, "exchange_middle", mine_down
    )
    down_weight = down_weight.reshape(model_width, hidden_width)
    down, second_grad, grad_input2 = feed(input2, cotangent_all, second, down_weight, 4)
    second_part = row_sums(second_grad)
    grad_middle, grad_branch = exchange(
        after_hidden, grad_input2, [cotangent, middle, gain2], True, 2, "exchange_hidden"
    )

    down, grad_branch = lax.optimization_barrier((down, grad_branch))
    result = (middle + crossing_sum(down)).astype(bf16)
    grad_gated = dot(grad_branch, output_weight)
    grad_attended = (grad_gated * opened).astype(bf16)
    grad_gate_pre = (grad_gated * attended_wide * opened * (1.0 - opened)).astype(bf16)
    dq_prev, rows_prev, dkv_prev, decay_prev = attend_back(
        False, ranges, query, earlier_kv, terms, earlier_terms, begins, grad_attended, attended,
        lse, local_heads,
    )
    dkv_later = passed_along(dkv_prev, "blk", -1)
    decay_later = passed_along(decay_prev[:, :8], "blk", -1)
    decay_later = jnp.pad(decay_later, ((0, 0), (0, LANES - 8)))
    dq, dk_own, dv_own, decay_own = attend_back(
        True, ranges, query, key_value, terms, terms, begins, grad_attended, attended,
        lse, local_heads, (dq_prev, rows_prev),
    )
    dk = (dk_own + dkv_later[0].astype(f32)).astype(bf16)
    dv = (dv_own + dkv_later[1].astype(f32)).astype(bf16)
    logf_grad = decay_back(decay_own, decay_later)
    forget_grad = jnp.where(
        jnp.arange(LANES)[None, :] < local_heads, logf_grad * jax.nn.sigmoid(-forget), 0.0
    ).astype(bf16)
    grads = jnp.concatenate([dk, dv, forget_grad, dq, grad_gate_pre], axis=1)
    first_grad = over_tokens(input1, grads)
    bias_part = jnp.sum(forget_grad.astype(f32), axis=0)
    row = jnp.arange(model_width)[:, None] % share
    column = jnp.arange(kv_width + 2 * local_width)[None, :]
    spread_bias = jnp.sum(
        jnp.where(row == jnp.arange(LANES)[None, :], bias_part[None, :], 0.0), axis=1, keepdims=True
    )
    first_grad = jnp.where(
        column == 2 * local_width + local_heads, spread_bias, first_grad
    ).astype(bf16)
    output_grad = over_tokens(grad_branch, gated).astype(bf16)
    grad_input1 = dot(grads, first[:, : kv_width + 2 * local_width], NT).astype(bf16)
    first_sum, output_sum, second_sum, tokens_grad = finish_last(
        first_grad, output_grad, second_part, groups, grad_input1, grad_middle, tokens, gain1, 3
    )
    first_sum, output_sum, second_sum = (
        jnp.swapaxes(array, 0, 1).astype(f32) for array in (first_sum, output_sum, second_sum)
    )

    def columns(array, start, width):
        return array[:, :, start : start + width].reshape(share, groups * width)

    key_sum, value_sum = (columns(first_sum, n * local_width, local_width) for n in range(2))
    forget_sum = columns(first_sum, 2 * local_width, local_heads)
    bias_total = first_sum[:local_heads, :, 2 * local_width + local_heads].T.reshape(head_count)
    query_sum, gate_out_sum = (
        columns(first_sum, kv_width + n * local_width, local_width) for n in range(2)
    )
    output_total = columns(output_sum, 0, local_width)
    gate_sum, up_sum, down_sum = (
        columns(second_sum, n * hidden_width, hidden_width) for n in range(3)
    )

    def along(weight, grad):
        return jnp.sum(low(weight).astype(f32) * grad, axis=1)

    gain1_total = (
        along(w_query, query_sum)
        + along(w_key, key_sum)
        + along(w_value, value_sum)
        + along(w_gate_out, gate_out_sum)
        + along(w_forget, forget_sum)
    ) / low(norm1_gain).astype(f32)
    gain2_total = (along(w_gate, gate_sum) + along(w_up, up_sum)) / low(norm2_gain).astype(f32)
    return (
        result,
        tokens_grad,
        gain1_total,
        query_sum,
        key_sum,
        value_sum,
        gate_out_sum,
        forget_sum,
        bias_total,
        output_total,
        gain2_total,
        gate_sum,
        up_sum,
        down_sum,
    )


def solution(mesh):
    both = ("blk", "head")
    matrix, vector = P(both, None), P(both)
    return jax.shard_map(
        body,
        mesh=mesh,
        in_specs=(
            matrix, P("blk"), vector, matrix, matrix, matrix, matrix, matrix, P(), matrix, vector,
            matrix, matrix, matrix, matrix,
        ),
        out_specs=(
            matrix, matrix, vector, matrix, matrix, matrix, matrix, matrix, P(), matrix, vector,
            matrix, matrix, matrix,
        ),
        check_vma=False,
    )
```

```python
import functools

import jax
import jax.numpy as jnp
from jax import lax
from jax.experimental import pallas as pl
from jax.experimental.pallas import tpu as pltpu
from jax.sharding import PartitionSpec as P

epsilon = 1e-06
LANES = 128
Q_TILE = 512
K_TILE = 512
FAR = -1e30
NT = (((1,), (1,)), ((), ()))
NN = (((1,), (0,)), ((), ()))
bf16 = jnp.bfloat16
f32 = jnp.float32


def dot(a, b, dims=NN, **kw):
    return lax.dot_general(a, b, dims, preferred_element_type=f32, **kw)


def passed_along(array, axis, by):
    peers = lax.axis_size(axis)
    pairs = [(i, i + by) for i in range(peers) if 0 <= i + by < peers]
    return lax.ppermute(array, axis, pairs)


def split3(value):
    high = value.astype(bf16)
    rest = value - high.astype(f32)
    mid = rest.astype(bf16)
    low = (rest - mid.astype(f32)).astype(bf16)
    return high, mid, low


def running(value_of, steps, rows, upper):
    place = lax.broadcasted_iota(jnp.int32, (rows, rows), 0)
    other = lax.broadcasted_iota(jnp.int32, (rows, rows), 1)
    tri = jnp.where((other >= place) if upper else (other <= place), 1.0, 0.0).astype(bf16)
    outs = [None] * steps
    carry = jnp.zeros((1, LANES), f32)
    order = range(steps - 1, -1, -1) if upper else range(steps)
    for n in order:
        block = value_of(n)
        total = sum(dot(tri, part) for part in split3(block)) + carry
        outs[n] = total
        carry = total[0:1] if upper else total[rows - 1 : rows]
    return outs, carry


PROJECT_TILE = 256
TERM_ROWS = 32


def project_kernel(local_heads, tokens_ref, gain_ref, weight_ref, bias_ref, input_ref, out_ref,
                   terms_ref, turned_ref, forget_ref, carry_ref):
    rows = tokens_ref.shape[0]
    wide = weight_ref.shape[1] - LANES

    @pl.when(pl.program_id(0) == 0)
    def _():
        carry_ref[...] = jnp.zeros_like(carry_ref)

    tokens = tokens_ref[...].astype(f32)
    input1 = (tokens * inverse_rms(tokens) * gain_ref[0:1, :]).astype(bf16)
    input_ref[...] = input1
    raw = dot(input1, weight_ref[...])
    out_ref[...] = raw[:, :wide].astype(bf16)
    forget = (raw[:, wide:] + bias_ref[0:1, :]).astype(bf16).astype(f32)
    forget_ref[...] = forget
    lane = lax.broadcasted_iota(jnp.int32, (rows, LANES), 1)
    logf = jnp.minimum(forget, 0.0) - jnp.log1p(jnp.exp(-jnp.abs(forget)))
    logf = jnp.where(lane < local_heads, logf, 0.0)
    place = lax.broadcasted_iota(jnp.int32, (rows, rows), 0)
    other = lax.broadcasted_iota(jnp.int32, (rows, rows), 1)
    tri = jnp.where(other <= place, 1.0, 0.0).astype(bf16)
    sums = sum(dot(tri, part) for part in split3(logf)) + carry_ref[0:1, :]
    carry_ref[0:1, :] = sums[rows - 1 : rows, :]
    high, mid, low = split3(sums)
    terms = (
        high.astype(f32)
        + pltpu.roll(mid.astype(f32), local_heads, 1)
        + pltpu.roll(low.astype(f32), 2 * local_heads, 1)
        + jnp.where(lane == 3 * local_heads, 1.0, 0.0)
    ).astype(bf16)
    terms_ref[...] = terms
    turned_ref[...] = terms.T[0:TERM_ROWS, :]


def project(tokens, gain, weight, bias, wide, local_heads):
    rows, width = tokens.shape

    def tile(columns):
        return pl.BlockSpec((PROJECT_TILE, columns), lambda n: (n, 0))

    def whole(*shape):
        return pl.BlockSpec(shape, lambda n: (0, 0))

    return pl.pallas_call(
        functools.partial(project_kernel, local_heads),
        grid=(rows // PROJECT_TILE,),
        in_specs=[tile(width), whole(8, width), whole(width, wide + LANES), whole(8, LANES)],
        out_specs=[
            tile(width),
            tile(wide),
            tile(LANES),
            pl.BlockSpec((TERM_ROWS, PROJECT_TILE), lambda n: (0, n)),
            tile(LANES),
        ],
        out_shape=[
            jax.ShapeDtypeStruct((rows, width), bf16),
            jax.ShapeDtypeStruct((rows, wide), bf16),
            jax.ShapeDtypeStruct((rows, LANES), bf16),
            jax.ShapeDtypeStruct((TERM_ROWS, rows), bf16),
            jax.ShapeDtypeStruct((rows, LANES), f32),
        ],
        scratch_shapes=[pltpu.VMEM((8, LANES), f32)],
        cost_estimate=pl.CostEstimate(
            flops=2 * rows * width * (wide + LANES), transcendentals=rows * LANES,
            bytes_accessed=20_000_000,
        ),
        name="project",
    )(tokens, gain, weight, bias)


def decay_back_kernel(own_ref, halo_ref, out_ref):
    rows = 256
    steps = own_ref.shape[0] // rows
    own, _ = running(lambda n: own_ref[n * rows : (n + 1) * rows, :], steps, rows, True)
    halo, _ = running(lambda n: halo_ref[n * rows : (n + 1) * rows, :], steps, rows, False)
    for n in range(steps):
        part = slice(n * rows, (n + 1) * rows)
        out_ref[part, :] = own[n] + (halo[n] - halo_ref[part, :])


def decay_back(own, halo):
    return pl.pallas_call(
        decay_back_kernel,
        out_shape=jax.ShapeDtypeStruct(own.shape, f32),
        name="decay_back",
    )(own, halo)


QUERY, KEY, TOTAL = range(3)


def placing(pair, local_heads, role):
    row = lax.broadcasted_iota(jnp.int32, (LANES, LANES), 0)
    col = lax.broadcasted_iota(jnp.int32, (LANES, LANES), 1)
    head = jnp.where(col < 64, 2 * pair + 1, 2 * pair)
    spot = jnp.where(col < 64, col, col - 64)
    term = spot - 3 * role
    is_term = (term >= 0) & (term < 3) & (row == term * local_heads + head)
    if role == QUERY:
        ones = (spot >= 3) & (spot < 9)
    else:
        ones = (spot < 3) & (role == KEY)
    is_one = ones & (row == 3 * local_heads)
    sign = -1.0 if role == KEY else 1.0
    return (jnp.where(is_term, sign, 0.0) + jnp.where(is_one, 1.0, 0.0)).astype(bf16)


def allowed_pairs(first_key, query_tile, rows, begin_row):
    shape = (K_TILE, Q_TILE)
    key_place = first_key + lax.broadcasted_iota(jnp.int32, shape, 0)
    query_place = rows + query_tile * Q_TILE + lax.broadcasted_iota(jnp.int32, shape, 1)
    return (key_place >= begin_row) & (key_place <= query_place)


def key_range(ranges_ref, query_tile, rows, own):
    count = rows // K_TILE
    base = count if own else 0
    first = jnp.clip(ranges_ref[0, query_tile] - base, 0, count)
    full = jnp.clip(ranges_ref[1, query_tile] - base, first, count)
    return first, full


def key_loops(ranges_ref, query_tile, rows, own, step, carry):
    first, full = key_range(ranges_ref, query_tile, rows, own)
    inside = query_tile * (Q_TILE // K_TILE) if own else rows // K_TILE
    full = jnp.minimum(full, inside)
    carry = lax.fori_loop(first, full, functools.partial(step, True), carry)
    carry = lax.fori_loop(full, inside, functools.partial(step, False), carry)
    if own:
        carry = lax.fori_loop(
            inside, inside + Q_TILE // K_TILE, functools.partial(step, True), carry
        )
    return carry


def tile_of(number, size):
    return pl.ds(pl.multiple_of(number * size, size), size)


def fill_keys(pair, local_heads, own, first, key_ref, terms_ref, keys):
    place = placing(pair, local_heads, KEY)
    lane = lax.broadcasted_iota(jnp.int32, (K_TILE, LANES), 1)
    rows = key_ref.shape[0]
    if not own:
        last = terms_ref[:, rows - LANES : rows].T
        total = dot(last, placing(pair, local_heads, TOTAL)[0:TERM_ROWS, :])[LANES - 1 : LANES, :]

    def fill(n, carry):
        here = tile_of(n, K_TILE)
        if own:
            extra = dot(terms_ref[here, :], place).astype(bf16)
        else:
            extra = dot(terms_ref[:, here].T, place[0:TERM_ROWS, :])
            extra = (extra + total).astype(bf16)
        key = key_ref[here, :]
        keys[0][here, :] = jnp.where(lane < 64, key, extra)
        keys[1][here, :] = jnp.where(lane < 64, extra, key)
        return carry

    lax.fori_loop(first, rows // K_TILE, fill, 0)


def query_tiles(q_ref, terms_ref, place, here, scaling):
    lane = lax.broadcasted_iota(jnp.int32, (Q_TILE, LANES), 1)
    extra = dot(terms_ref[here, :], place).astype(bf16)
    query = (q_ref[here, :].astype(f32) * scaling).astype(bf16)
    return jnp.where(lane < 64, query, extra), jnp.where(lane < 64, extra, query)


def attend_kernel(local_heads, own, ranges_ref, q_ref, k_ref, v_ref, t_query_ref, t_key_ref,
                  begin_ref, *refs):
    if own:
        acc_out_ref, state_out_ref, key0, key1, values, acc0, acc1 = refs
    else:
        acc_in_ref, state_in_ref, o_ref, lse_ref, key0, key1, values, acc0, acc1 = refs
    pair = pl.program_id(0)
    rows = q_ref.shape[0]
    base = rows if own else 0
    keys, accs = (key0, key1), (acc0, acc1)
    first, _ = key_range(ranges_ref, 0, rows, own)
    fill_keys(pair, local_heads, own, first, k_ref, t_key_ref, keys)

    def turn(n, carry):
        values[:, tile_of(n, K_TILE)] = v_ref[tile_of(n, K_TILE), :].T
        return carry

    lax.fori_loop(first, rows // K_TILE, turn, 0)
    place = placing(pair, local_heads, QUERY)

    def query_loop(tile, carry):
        here = tile_of(tile, Q_TILE)
        queries = query_tiles(q_ref, t_query_ref, place, here, 64**-0.5)
        begin_row = begin_ref[0:1, here]
        if own:
            low = jnp.full((1, Q_TILE), FAR, f32)
            zero = jnp.zeros((1, Q_TILE), f32)
            state = (low, zero, low, zero)
            for acc in accs:
                acc[...] = jnp.zeros_like(acc)
        else:
            state = tuple(state_in_ref[n : n + 1, here] for n in range(4))
            for h in range(2):
                accs[h][...] = acc_in_ref[64 * h : 64 * (h + 1), here]

        def step(masked, number, state):
            there = tile_of(number, K_TILE)
            fresh = []
            if masked:
                allowed = allowed_pairs(base + number * K_TILE, tile, rows, begin_row)
            for h in range(2):
                largest, total = state[2 * h], state[2 * h + 1]
                scores = dot(keys[h][there, :], queries[h], NT)
                if masked:
                    scores = jnp.where(allowed, scores, FAR)
                now = jnp.maximum(largest, jnp.max(scores, axis=0, keepdims=True))
                fade = jnp.exp(largest - now)
                weights = jnp.exp(scores - now)
                total = total * fade + jnp.sum(weights, axis=0, keepdims=True)
                accs[h][...] = accs[h][...] * fade + dot(
                    values[64 * h : 64 * (h + 1), there], weights.astype(bf16)
                )
                fresh += [now, total]
            return tuple(fresh)

        state = key_loops(ranges_ref, tile, rows, own, step, state)
        if own:
            for h in range(2):
                acc_out_ref[64 * h : 64 * (h + 1), here] = accs[h][...]
            for n in range(4):
                state_out_ref[n : n + 1, here] = state[n]
        else:
            mixed = jnp.concatenate(
                [accs[h][...] * (1.0 / state[2 * h + 1]) for h in range(2)], axis=0
            )
            o_ref[here, :] = mixed.T.astype(bf16)
            for h in range(2):
                lse_ref[h : h + 1, here] = state[2 * h] + jnp.log(state[2 * h + 1])
        return carry

    lax.fori_loop(0, rows // Q_TILE, query_loop, 0)


def lane_block(rows, offset):
    return pl.BlockSpec((rows, LANES), lambda p, *_: (0, offset + p))


def fixed(shape):
    return pl.BlockSpec(shape, lambda p, *_: (0, 0))


def pair_block(height, rows):
    return pl.BlockSpec((height, rows), lambda p, *_: (p, 0))


def attend(own, ranges, query, key_value, terms, key_terms, begins, local_heads, so_far=()):
    rows = query.shape[0]
    pairs = local_heads // 2
    running_specs = [pair_block(LANES, rows), pair_block(8, rows)]
    running_shape = (
        jax.ShapeDtypeStruct((LANES * pairs, rows), f32),
        jax.ShapeDtypeStruct((8 * pairs, rows), f32),
    )
    final_specs = [lane_block(rows, 0), pair_block(8, rows)]
    final_shape = (
        jax.ShapeDtypeStruct((rows, pairs * LANES), bf16),
        jax.ShapeDtypeStruct((8 * pairs, rows), f32),
    )
    return pl.pallas_call(
        functools.partial(attend_kernel, local_heads, own),
        grid_spec=pltpu.PrefetchScalarGridSpec(
            num_scalar_prefetch=1,
            grid=(pairs,),
            in_specs=[
                lane_block(rows, 0),
                lane_block(rows, 0),
                lane_block(rows, pairs),
                fixed((rows, LANES)),
                fixed((rows, LANES) if own else (TERM_ROWS, rows)),
                fixed((8, rows)),
            ]
            + ([] if own else running_specs),
            out_specs=running_specs if own else final_specs,
            scratch_shapes=[
                pltpu.VMEM((rows, LANES), bf16),
                pltpu.VMEM((rows, LANES), bf16),
                pltpu.VMEM((LANES, rows), bf16),
                pltpu.VMEM((64, Q_TILE), f32),
                pltpu.VMEM((64, Q_TILE), f32),
            ],
        ),
        out_shape=running_shape if own else final_shape,
        cost_estimate=pl.CostEstimate(
            flops=40_000_000_000 if own else 10_000_000_000,
            transcendentals=20_000_000,
            bytes_accessed=12_000_000,
        ),
        name="attend_own" if own else "attend_prev",
    )(ranges, query, key_value, key_value, terms, key_terms, begins, *so_far)


def attend_back_kernel(local_heads, own, ranges_ref, q_ref, k_ref, v_ref, t_query_ref, t_key_ref,
                       begin_ref, grad_ref, o_ref, lse_ref, *refs):
    if own:
        dq_in_ref, decay_in_ref, dq_ref, dk_ref, dv_ref, decay_ref = refs[:6]
    else:
        dq_ref, row_decay_ref, dkv_ref, decay_ref = refs[:4]
        dk_ref, dv_ref = dkv_ref.at[0], dkv_ref.at[1]
    key0, key1, key_t0, key_t1, dk0, dk1, dv, dq0, dq1 = refs[-9:]
    pair = pl.program_id(0)
    rows = q_ref.shape[0]
    base = rows if own else 0
    keys, keys_t, dks, dqs = (key0, key1), (key_t0, key_t1), (dk0, dk1), (dq0, dq1)
    first, _ = key_range(ranges_ref, 0, rows, own)
    fill_keys(pair, local_heads, own, first, k_ref, t_key_ref, keys)

    def turn(n, carry):
        here = tile_of(n, K_TILE)
        for h in range(2):
            keys_t[h][:, here] = keys[h][here, :].T
        return carry

    lax.fori_loop(first, rows // K_TILE, turn, 0)
    for ref in (dk0, dk1, dv):
        ref[...] = jnp.zeros_like(ref)
    place = placing(pair, local_heads, QUERY)
    lane = lax.broadcasted_iota(jnp.int32, (Q_TILE, LANES), 1)
    pick_row = lax.broadcasted_iota(jnp.int32, (8, LANES), 0)
    pick_lane = lax.broadcasted_iota(jnp.int32, (8, LANES), 1)
    pick = jnp.where((pick_lane // 64) == pick_row, 1.0, 0.0)
    sums_ref = decay_ref if own else row_decay_ref

    @pl.when(pair == 0)
    def _():
        if own:
            decay_ref[...] = decay_in_ref[...]
        else:
            decay_ref[...] = jnp.zeros_like(decay_ref)
            row_decay_ref[...] = jnp.zeros_like(row_decay_ref)

    def query_tile(tile):
        here = tile_of(tile, Q_TILE)
        queries = query_tiles(q_ref, t_query_ref, place, here, 64**-0.5)
        begin_row = begin_ref[0:1, here]
        grad = grad_ref[here, :]
        nothing = jnp.zeros_like(grad)
        grads = (jnp.where(lane < 64, grad, nothing), jnp.where(lane < 64, nothing, grad))
        product = grad.astype(f32) * o_ref[here, :].astype(f32)
        inner = dot(pick, product, NT, precision=lax.Precision.HIGHEST)
        for dq in dqs:
            dq[...] = jnp.zeros_like(dq)

        def step(masked, number, state):
            there = tile_of(number, K_TILE)
            if masked:
                allowed = allowed_pairs(base + number * K_TILE, tile, rows, begin_row)
            value = v_ref[there, :]
            value_part = 0.0
            for h in range(2):
                scores = dot(keys[h][there, :], queries[h], NT)
                prob = jnp.exp(scores - lse_ref[h : h + 1, here])
                if masked:
                    prob = jnp.where(allowed, prob, 0.0)
                grad_prob = dot(value, grads[h], NT)
                grad_score = (prob * (grad_prob - inner[h : h + 1, :])).astype(bf16)
                value_part = value_part + dot(prob.astype(bf16), grads[h])
                dks[h][there, :] += dot(grad_score, queries[h])
                dqs[h][...] += dot(keys_t[h][:, there], grad_score)
            dv[there, :] += value_part
            return state

        key_loops(ranges_ref, tile, rows, own, step, 0)
        turned = [dq[...].T for dq in dqs]
        dq_tile = jnp.where(lane < 64, turned[0], turned[1]) * 64**-0.5
        if own:
            dq_tile = dq_tile + dq_in_ref[here, :]
        dq_ref[here, :] = dq_tile.astype(dq_ref.dtype)
        sums = sums_ref[here, :]
        sums = sums + jnp.where(lane == 2 * pair, turned[0][:, 64:65], 0.0)
        sums = sums + jnp.where(lane == 2 * pair + 1, turned[1][:, 0:1], 0.0)
        sums_ref[here, :] = sums

    def query_loop(tile, carry):
        if own:
            query_tile(tile)
        else:
            reaches = key_range(ranges_ref, tile, rows, own)[0] < rows // K_TILE
            pl.when(reaches)(lambda: query_tile(tile))

            @pl.when(jnp.logical_not(reaches))
            def _():
                dq_ref[tile_of(tile, Q_TILE), :] = jnp.zeros((Q_TILE, LANES), dq_ref.dtype)

        return carry

    lax.fori_loop(0, rows // Q_TILE, query_loop, 0)
    sign = -1.0 if own else 1.0

    def finish(n, carry):
        here = tile_of(n, Q_TILE)
        left, right = dk0[here, :], dk1[here, :]
        dk_ref[here, :] = jnp.where(lane < 64, left, right).astype(dk_ref.dtype)
        dv_ref[here, :] = dv[here, :].astype(dv_ref.dtype)
        decay = decay_ref[here, :]
        decay = decay + jnp.where(lane == 2 * pair, sign * left[:, 67:68], 0.0)
        decay = decay + jnp.where(lane == 2 * pair + 1, sign * right[:, 3:4], 0.0)
        decay_ref[here, :] = decay
        return carry

    lax.fori_loop(0, rows // Q_TILE, finish, 0)


def attend_back(
    own, ranges, query, key_value, terms, key_terms, begins, grad, mixed, lse, local_heads,
    so_far=(),
):
    rows = query.shape[0]
    pairs = local_heads // 2
    wide = jax.ShapeDtypeStruct((rows, pairs * LANES), f32)
    sums = jax.ShapeDtypeStruct((rows, LANES), f32)
    if own:
        out_specs = [lane_block(rows, 0)] * 3 + [fixed((rows, LANES))]
        out_shape = (jax.ShapeDtypeStruct(wide.shape, bf16), wide, wide, sums)
    else:
        both = pl.BlockSpec((2, rows, LANES), lambda p, *_: (0, 0, p))
        out_specs = [lane_block(rows, 0), fixed((rows, LANES)), both, fixed((rows, LANES))]
        out_shape = (
            wide, sums, jax.ShapeDtypeStruct((2, rows, pairs * LANES), bf16), sums,
        )
    return pl.pallas_call(
        functools.partial(attend_back_kernel, local_heads, own),
        grid_spec=pltpu.PrefetchScalarGridSpec(
            num_scalar_prefetch=1,
            grid=(pairs,),
            in_specs=[
                lane_block(rows, 0),
                lane_block(rows, 0),
                lane_block(rows, pairs),
                fixed((rows, LANES)),
                fixed((rows, LANES) if own else (TERM_ROWS, rows)),
                fixed((8, rows)),
                lane_block(rows, 0),
                lane_block(rows, 0),
                pair_block(8, rows),
            ]
            + ([lane_block(rows, 0), fixed((rows, LANES))] if own else []),
            out_specs=out_specs,
            scratch_shapes=[
                pltpu.VMEM((rows, LANES), bf16),
                pltpu.VMEM((rows, LANES), bf16),
                pltpu.VMEM((LANES, rows), bf16),
                pltpu.VMEM((LANES, rows), bf16),
                pltpu.VMEM((rows, LANES), f32),
                pltpu.VMEM((rows, LANES), f32),
                pltpu.VMEM((rows, LANES), f32),
                pltpu.VMEM((LANES, Q_TILE), f32),
                pltpu.VMEM((LANES, Q_TILE), f32),
            ],
        ),
        out_shape=out_shape,
        cost_estimate=pl.CostEstimate(
            flops=20_000_000_000 if own else 10_000_000_000,
            transcendentals=20_000_000,
            bytes_accessed=25_000_000,
        ),
        name="attend_back_own" if own else "attend_back_prev",
    )(
        ranges, query, key_value, key_value, terms, key_terms, begins, grad, mixed, lse, *so_far
    )


PIECES = 4


def partners():
    me = lax.axis_index("head")
    near = me + 1 - 2 * (me % 2)
    far = (me + 2) % 4
    cross = (near + 2) % 4
    return me, near, far, cross


def signal(other):
    pl.semaphore_signal(
        pltpu.get_barrier_semaphore(), inc=1, device_id=other, device_id_type=pl.DeviceIdType.MESH
    )


def greet(others):
    for other in others:
        signal(other)
    pl.semaphore_wait(pltpu.get_barrier_semaphore(), len(others))


def remote(source, target, send, receive, other):
    return pltpu.make_async_remote_copy(
        src_ref=source,
        dst_ref=target,
        send_sem=send,
        recv_sem=receive,
        device_id=other,
        device_id_type=pl.DeviceIdType.MESH,
    )


def on_head(index):
    return {"head": index}


def on_blk(index):
    return {"blk": index}


def piece_at(ref, slot, piece, size):
    span = size // PIECES
    return ref.at[pl.ds(pl.multiple_of(slot * size + piece * span, span), span), :]


class Slots:
    def __init__(self, by_device):
        me, near, far, cross = partners()
        if by_device:
            self.own = self.sent_near = self.sent_far = me
            self.near, self.far, self.cross = near, far, cross
            self.passed = far
        else:
            self.own, self.sent_near, self.sent_far = 3, 2, 1
            self.near, self.far, self.cross = 2, 1, 0
            self.passed = 0


def spread_piece(source, all_ref, size, sems, piece, slots):
    me, near, far, _ = partners()
    far_send, far_recv, near_send, near_recv, _, _, own = sems
    copies = (
        remote(source, piece_at(all_ref, slots.sent_far, piece, size), far_send.at[piece],
               far_recv.at[piece], on_head(far)),
        remote(source, piece_at(all_ref, slots.sent_near, piece, size), near_send.at[piece],
               near_recv.at[piece], on_head(near)),
        pltpu.make_async_copy(source, piece_at(all_ref, slots.own, piece, size), own.at[piece]),
    )
    for copy in copies:
        copy.start()
    return copies


def hand_on(all_ref, size, sems, sent, slots):
    me, near, far, cross = partners()
    far_send, far_recv, near_send, near_recv, on_send, on_recv, own = sems
    passed = []
    for piece in range(PIECES):
        there = piece_at(all_ref, slots.far, piece, size)
        remote(there, there, far_send.at[piece], far_recv.at[piece], on_head(far)).wait_recv()
        copy = remote(
            there, piece_at(all_ref, slots.passed, piece, size), on_send.at[piece],
            on_recv.at[piece], on_head(near),
        )
        copy.start()
        passed.append(copy)

    def finish():
        for piece in range(PIECES):
            to_far, to_near, local = sent[piece]
            to_far.wait_send()
            to_near.wait_send()
            local.wait()
            passed[piece].wait_send()
            there = piece_at(all_ref, slots.near, piece, size)
            remote(there, there, near_send.at[piece], near_recv.at[piece], on_head(near)).wait_recv()
            there = piece_at(all_ref, slots.cross, piece, size)
            remote(there, there, on_send.at[piece], on_recv.at[piece], on_head(near)).wait_recv()

    return finish


def gather_sems():
    return [pltpu.SemaphoreType.DMA((PIECES,)) for _ in range(7)]


def blk_peers():
    here = lax.axis_index("blk")
    half = lax.axis_size("blk") // 2
    low, high = here % 2, here // 2
    partner = here + 1 - 2 * low
    after = [((high + t) % half) * 2 + low for t in range(half)]
    return here, partner, after


class Line:
    def __init__(self, block_of, kinds, sems):
        self.block_of, self.kinds = block_of, kinds
        self.pair_send, self.pair_recv, self.up_send, self.up_recv, self.down_send, self.down_recv = sems
        here = lax.axis_index("blk")
        self.half = lax.axis_size("blk") // 2
        self.low, self.high = here % 2, here // 2
        self.partner = here + 1 - 2 * self.low
        self.has_up, self.has_down = self.high < self.half - 1, self.high > 0

    def greet(self, others):
        greet_sum = len(others) + 1
        for other in others + [on_blk(self.partner)]:
            signal(other)
        pl.when(self.has_up)(lambda: signal(on_blk(self.at(self.high + 1))))
        pl.when(self.has_down)(lambda: signal(on_blk(self.at(self.high - 1))))
        ends = (self.high == 0).astype(jnp.int32) + (self.high == self.half - 1).astype(jnp.int32)
        pl.semaphore_wait(pltpu.get_barrier_semaphore(), greet_sum + 2 - ends)

    def at(self, high):
        return high * 2 + self.low

    def pair_copy(self, kind, high, low):
        block = self.block_of(kind, high * 2 + low)
        return remote(
            block, block, self.pair_send.at[kind, high], self.pair_recv.at[kind, high],
            on_blk(self.partner),
        )

    def up_copy(self, kind, high):
        block = self.block_of(kind, self.at(high))
        return remote(
            block, block, self.up_send.at[kind, high], self.up_recv.at[kind, high],
            on_blk(self.at(jnp.minimum(self.high + 1, self.half - 1))),
        )

    def down_copy(self, kind, high):
        block = self.block_of(kind, self.at(high))
        return remote(
            block, block, self.down_send.at[kind, high], self.down_recv.at[kind, high],
            on_blk(self.at(jnp.maximum(self.high - 1, 0))),
        )

    def launch(self, kind):
        self.pair_copy(kind, self.high, self.low).start()
        pl.when(self.has_up)(lambda: self.up_copy(kind, self.high).start())
        pl.when(self.has_down)(lambda: self.down_copy(kind, self.high).start())

    def step(self, t):
        for kind in range(self.kinds):
            below, above = self.high - t, self.high + t

            @pl.when(below >= 0)
            def _():
                self.up_copy(kind, below).wait_recv()
                self.pair_copy(kind, below, self.low).start()
                pl.when(self.has_up)(lambda: self.up_copy(kind, below).start())

            @pl.when(above < self.half)
            def _():
                self.down_copy(kind, above).wait_recv()
                self.pair_copy(kind, above, self.low).start()
                pl.when(self.has_down)(lambda: self.down_copy(kind, above).start())

    def finish(self):
        for kind in range(self.kinds):

            def wait(high, carry):
                self.pair_copy(kind, high, self.low).wait_send()
                self.pair_copy(kind, high, 1 - self.low).wait_recv()

                @pl.when((high <= self.high) & self.has_up)
                def _():
                    self.up_copy(kind, high).wait_send()

                @pl.when((high >= self.high) & self.has_down)
                def _():
                    self.down_copy(kind, high).wait_send()

                return carry

            lax.fori_loop(0, self.half, wait, 0)


def gather_first_kernel(before, after, *refs):
    small_ref, weight_refs = refs[0], refs[1 : 1 + before + after]
    tokens_ref, cotangent_ref, pack_all, tokens_all, cotangent_all, pack_ref = refs[
        1 + before + after : 7 + before + after
    ]
    sems = refs[7 + before + after :]
    groups = pack_ref.shape[0]
    start = 0
    for n, ref in enumerate(weight_refs):
        if n == before:
            pack_ref[:, :, start : start + LANES] = small_ref[...]
            start += LANES
        wide = ref.shape[1] // groups
        for group in range(groups):
            pack_ref[group, :, start : start + wide] = ref[
                :, group * wide : (group + 1) * wide
            ].astype(bf16)
        start += wide
    swap_send, swap_recv, swap_own = sems[:3]
    token_sems, cotangent_sems = sems[9:16], sems[16:23]
    me, near, far, cross = partners()
    sources = (me, near, far, cross)
    line = Line(lambda kind, blk: pack_all.at[blk, sources[kind]], 4, sems[3:9])
    here = lax.axis_index("blk")
    line.greet([on_head(near), on_head(far), on_head(cross)])
    swaps = [pltpu.make_async_copy(pack_ref.at[me], pack_all.at[here, me], swap_own)]
    for kind, other in enumerate((near, far, cross)):
        swaps.append(
            remote(
                pack_ref.at[other],
                pack_all.at[here, me],
                swap_send.at[kind],
                swap_recv.at[kind],
                on_head(other),
            )
        )
    for swap in swaps:
        swap.start()
    size = tokens_ref.shape[0]
    span = size // PIECES

    def spread_all(ref, all_ref, some, slots):
        return [
            spread_piece(ref.at[pl.ds(piece * span, span), :], all_ref, size, some, piece, slots)
            for piece in range(PIECES)
        ]

    by_device, crossing = Slots(True), Slots(False)
    tokens_sent = spread_all(tokens_ref, tokens_all, token_sems, by_device)
    swaps[0].wait()
    line.launch(0)
    for kind, source in enumerate((near, far, cross)):
        block = pack_all.at[here, source]
        remote(
            block, block, swap_send.at[kind], swap_recv.at[kind], on_head(source)
        ).wait_recv()
        line.launch(kind + 1)
    cotangent_sent = spread_all(cotangent_ref, cotangent_all, cotangent_sems, crossing)
    for t in range(1, line.half):
        line.step(t)
    finish_tokens = hand_on(tokens_all, size, token_sems, tokens_sent, by_device)
    finish_cotangent = hand_on(cotangent_all, size, cotangent_sems, cotangent_sent, crossing)
    for swap in swaps[1:]:
        swap.wait_send()
    line.finish()
    finish_tokens()
    finish_cotangent()


def gather_first(before, small, after, tokens, cotangent, number):
    groups, share, _ = small.shape
    weights = [*before, *after]
    columns = LANES + sum(weight.shape[1] // groups for weight in weights)
    peers = lax.axis_size("blk")
    rows, width = tokens.shape
    whole = jax.ShapeDtypeStruct((groups * rows, width), bf16)
    vmem, anywhere = pl.BlockSpec(memory_space=pltpu.VMEM), pl.BlockSpec(memory_space=pl.ANY)
    all_pack, all_tokens, all_cotangent = pl.pallas_call(
        functools.partial(gather_first_kernel, len(before), len(after)),
        in_specs=[vmem] * (3 + len(weights)),
        out_specs=[anywhere] * 3,
        out_shape=[jax.ShapeDtypeStruct((peers, groups, share, columns), bf16), whole, whole],
        scratch_shapes=[
            pltpu.VMEM((groups, share, columns), bf16),
            pltpu.SemaphoreType.DMA((3,)),
            pltpu.SemaphoreType.DMA((3,)),
            pltpu.SemaphoreType.DMA,
        ]
        + [pltpu.SemaphoreType.DMA((4, peers // 2)) for _ in range(6)]
        + gather_sems()
        + gather_sems(),
        compiler_params=pltpu.CompilerParams(collective_id=number, has_side_effects=True),
        cost_estimate=pl.CostEstimate(
            flops=70_000_000_000, transcendentals=0, bytes_accessed=30_000_000
        ),
        name="gather_first",
    )(small, *weights, tokens, cotangent)
    return all_pack.reshape(peers * groups * share, columns), all_tokens, all_cotangent


class Sum:
    def __init__(self, part_ref, buffers, sems, size, by_device):
        self.part_ref, self.size, self.span = part_ref, size, size // PIECES
        self.slots = Slots(by_device)
        self.near_buf, self.turn_buf, self.far_buf = buffers
        self.near_send, self.near_recv, self.far_send, self.far_recv = sems
        self.near_copies, self.far_copies = [], []

    def piece(self, n):
        return slice(n * self.span, (n + 1) * self.span)

    def start(self):
        me, near, far, cross = partners()
        for which, shard in ((0, self.slots.cross), (1, self.slots.near)):
            for n in range(PIECES):
                copy = remote(
                    piece_at(self.part_ref, shard, n, self.size),
                    self.near_buf.at[which, pl.ds(n * self.span, self.span), :],
                    self.near_send.at[which, n],
                    self.near_recv.at[which, n],
                    on_head(near),
                )
                copy.start()
                self.near_copies.append(copy)

    def turn(self):
        me, near, far, cross = partners()
        for n in range(PIECES):
            here = self.piece(n)
            self.near_copies[n].wait_recv()
            self.turn_buf[here, :] = (
                piece_at(self.part_ref, self.slots.far, n, self.size)[...].astype(f32)
                + self.near_buf[0, here, :].astype(f32)
            ).astype(bf16)
            copy = remote(
                self.turn_buf.at[pl.ds(n * self.span, self.span), :],
                self.far_buf.at[pl.ds(n * self.span, self.span), :],
                self.far_send.at[n],
                self.far_recv.at[n],
                on_head(far),
            )
            copy.start()
            self.far_copies.append(copy)

    def total(self, n):
        self.near_copies[PIECES + n].wait_recv()
        self.far_copies[n].wait_recv()
        here = self.piece(n)
        return (
            piece_at(self.part_ref, self.slots.own, n, self.size)[...].astype(f32)
            + self.near_buf[1, here, :].astype(f32)
            + self.far_buf[here, :].astype(f32)
        )

    def finish(self):
        for copy in self.near_copies + self.far_copies:
            copy.wait_send()


def sum_buffers(size, width):
    return [
        pltpu.VMEM((2, size, width), bf16),
        pltpu.VMEM((size, width), bf16),
        pltpu.VMEM((size, width), bf16),
    ]


def sum_sems():
    return [
        pltpu.SemaphoreType.DMA((2, PIECES)),
        pltpu.SemaphoreType.DMA((2, PIECES)),
        pltpu.SemaphoreType.DMA((PIECES,)),
        pltpu.SemaphoreType.DMA((PIECES,)),
    ]


def exchange_kernel(local, extras, summed, weights, *refs):
    part_ref, extra_refs = refs[0], refs[1 : 1 + extras]
    refs = refs[1 + extras :]
    if weights:
        mine_ref, refs = refs[0], refs[1:]
    out_ref, all_ref, refs = refs[0], refs[1], refs[2:]
    if weights:
        weight_ref, refs = refs[0], refs[1:]
    payload, sems = refs[0], refs[1:]
    size = out_ref.shape[0]
    span = size // PIECES
    _, near, far, _ = partners()
    if weights:
        kinds = mine_ref.shape[0]
        line = Line(lambda kind, blk: weight_ref.at[blk, kind], kinds, sems[-7:-1])
        own = pltpu.make_async_copy(mine_ref, weight_ref.at[lax.axis_index("blk")], sems[-1])
        own.start()
        line.greet([on_head(near), on_head(far)])
    else:
        greet([on_head(near), on_head(far)])
    slots = Slots(summed)
    if not summed:
        shares = Sum(part_ref, sems[7:10], sems[10:14], size, True)
        shares.start()
    if weights:
        own.wait()
        for kind in range(kinds):
            line.launch(kind)
    if not summed:
        shares.turn()
    sent = []
    for piece in range(PIECES):
        if weights and piece != 2:
            hop = {0: 1, 1: 2, 3: 3}[piece]
            for t in range(hop, line.half if piece == 3 else min(hop + 1, line.half)):
                line.step(t)
        here = slice(piece * span, (piece + 1) * span)
        total = part_ref[here, :] if summed else shares.total(piece)
        result, share = local(total, here, *extra_refs)
        out_ref[here, :] = result.astype(out_ref.dtype)
        payload[here, :] = share.astype(bf16)
        source = payload.at[pl.ds(piece * span, span), :]
        sent.append(spread_piece(source, all_ref, size, sems[:7], piece, slots))
    hand_on(all_ref, size, sems[:7], sent, slots)()
    if not summed:
        shares.finish()
    if weights:
        line.finish()


def exchange(local, part, extras, summed, number, name, mine=None):
    rows, width = part.shape
    size = rows if summed else rows // 4
    vmem, anywhere = pl.BlockSpec(memory_space=pltpu.VMEM), pl.BlockSpec(memory_space=pl.ANY)
    weights = mine is not None
    inputs = [part, *extras]
    out_specs = [vmem, anywhere]
    out_shape = [
        jax.ShapeDtypeStruct((size, width), f32),
        jax.ShapeDtypeStruct((4 * size, width), bf16),
    ]
    scratch = [pltpu.VMEM((size, width), bf16)] + gather_sems()
    if not summed:
        scratch += sum_buffers(size, width) + sum_sems()
    if weights:
        peers = lax.axis_size("blk")
        inputs.append(mine)
        out_specs.append(anywhere)
        out_shape.append(jax.ShapeDtypeStruct((peers,) + mine.shape, bf16))
        scratch += [pltpu.SemaphoreType.DMA((mine.shape[0], peers // 2)) for _ in range(6)]
        scratch.append(pltpu.SemaphoreType.DMA)
    return pl.pallas_call(
        functools.partial(exchange_kernel, local, len(extras), summed, weights),
        in_specs=[vmem] * len(inputs),
        out_specs=out_specs,
        out_shape=out_shape,
        scratch_shapes=scratch,
        compiler_params=pltpu.CompilerParams(collective_id=number, has_side_effects=True),
        cost_estimate=pl.CostEstimate(
            flops=10_000_000_000 if summed else 70_000_000_000,
            transcendentals=0,
            bytes_accessed=16_000_000,
        ),
        name=name,
    )(*inputs)


def column_chunks(width):
    count = max(width // 512, 1)
    first = width - 512 * (count - 1)
    return [(0, first)] + [(first + 512 * n, 512) for n in range(count - 1)]


def finish_last_kernel(grads_ref, weight_ref, grad_ref, output_grad_ref, second_ref,
                       grad_middle_ref, tokens_ref, gain_ref, weights_ref, output_ref,
                       second_out_ref, tokens_grad_ref, first_ref, *refs):
    buffers = (refs[0:3], refs[3:6])
    first_buffers = refs[6:9]
    pair_send, pair_recv, line_send, line_recv, swap_send, swap_recv = refs[9:15]
    first_sems = refs[15:19]
    me, near, far, cross = partners()
    others = (near, far, cross)
    here, partner, after = blk_peers()
    steps = len(after)
    greet(
        [on_head(other) for other in others]
        + [on_blk(partner)]
        + [on_blk(peer) for peer in after[1:]]
    )
    size = tokens_grad_ref.shape[0]
    first = Sum(first_ref, first_buffers, first_sems, size, True)
    chunks = []
    for ref, out_ref, some in (
        (grad_ref, weights_ref, buffers[0]), (output_grad_ref, output_ref, buffers[1])
    ):
        for start, wide in column_chunks(ref.shape[3]):
            chunks.append((ref, out_ref, some, pl.ds(start, wide)))
    groups = grad_ref.shape[1]
    sent = []
    for c, (ref, _, (pair_buf, _, _), at) in enumerate(chunks):
        for t in list(range(1, steps)) + [0]:
            copy = remote(
                ref.at[after[t] + partner - here, :, :, at],
                pair_buf.at[t, :, :, at],
                pair_send.at[c, t],
                pair_recv.at[c, t],
                on_blk(partner),
            )
            copy.start()
            sent.append(copy)

    def swap(source_ref, out_ref, c):
        for kind, other in enumerate(others):
            copy = remote(
                source_ref.at[other], out_ref.at[me], swap_send.at[c, kind],
                swap_recv.at[c, kind], on_head(other),
            )
            copy.start()
            sent.append(copy)

    swap(second_ref, second_out_ref, len(chunks))

    def add_up(c):
        ref, out_ref, (pair_buf, line_buf, row_buf), at = chunks[c]
        block = pair_buf.at[0, :, :, at]
        remote(block, block, pair_send.at[c, 0], pair_recv.at[c, 0], on_blk(partner)).wait_recv()
        for t in range(1, steps):
            block = line_buf.at[t, :, :, at]
            remote(
                block, block, line_send.at[c, t], line_recv.at[c, t], on_blk(after[t])
            ).wait_recv()

        def add_all(group, carry):
            total = ref[here, group, :, at].astype(f32) + pair_buf[0, group, :, at].astype(f32)
            for t in range(1, steps):
                total = total + line_buf[t, group, :, at].astype(f32)
            row_buf[group, :, at] = total.astype(bf16)
            return carry

        lax.fori_loop(0, groups, add_all, 0)
        out_ref[me, :, at] = row_buf[me, :, at]
        swap(row_buf.at[:, :, at], out_ref.at[:, :, at], c)

    across = grads_ref.shape[1]
    tiles = first_ref.shape[0] // 256

    def multiply(n, carry):
        rows = tile_of(n, 256)
        first_ref[rows, :] = dot(grads_ref[rows, :], weight_ref[:, :across], NT).astype(bf16)
        return carry

    lax.fori_loop(0, tiles // 2, multiply, 0)
    for c, (ref, _, (pair_buf, line_buf, _), at) in enumerate(chunks):
        for t in range(1, steps):
            block = pair_buf.at[t, :, :, at]
            remote(
                block, block, pair_send.at[c, t], pair_recv.at[c, t], on_blk(partner)
            ).wait_recv()

            def add(group, carry):
                pair_buf[t, group, :, at] = (
                    ref[after[t], group, :, at].astype(f32)
                    + pair_buf[t, group, :, at].astype(f32)
                ).astype(bf16)
                return carry

            lax.fori_loop(0, groups, add, 0)
            copy = remote(
                block, line_buf.at[t, :, :, at], line_send.at[c, t], line_recv.at[c, t],
                on_blk(after[t]),
            )
            copy.start()
            sent.append(copy)
        if c == 0:
            lax.fori_loop(tiles // 2, tiles, multiply, 0)
            first.start()
        else:
            if c == 1:
                first.turn()
            add_up(c - 1)
    for piece in range(PIECES):
        rows = first.piece(piece)
        tokens_grad_ref[rows, :], _ = after_first(
            first.total(piece), rows, grad_middle_ref, tokens_ref, gain_ref
        )
    add_up(len(chunks) - 1)
    second_out_ref[me] = second_ref[me]
    for c in range(len(chunks) + 1):
        if c < len(chunks):
            _, out_ref, _, at = chunks[c]
            out_ref = out_ref.at[:, :, at]
        else:
            out_ref = second_out_ref
        for kind, other in enumerate(others):
            block = out_ref.at[other]
            remote(
                block, block, swap_send.at[c, kind], swap_recv.at[c, kind], on_head(other)
            ).wait_recv()
    for copy in sent:
        copy.wait_send()
    first.finish()


def finish_last(grads, first, grad, output_grad, second, groups, grad_middle, tokens, gain, number):
    peers = lax.axis_size("blk")
    share = grad.shape[0] // (peers * groups)
    rows, width = tokens.shape
    vmem = pl.BlockSpec(memory_space=pltpu.VMEM)
    half = peers // 2
    widths = (grad.shape[1], output_grad.shape[1])
    chunks = sum(len(column_chunks(width)) for width in widths)

    def blocks(columns):
        return [pltpu.VMEM((half, groups, share, columns), bf16) for _ in range(2)] + [
            pltpu.VMEM((groups, share, columns), bf16)
        ]

    return pl.pallas_call(
        finish_last_kernel,
        in_specs=[vmem] * 8,
        out_specs=[vmem] * 4,
        out_shape=[
            jax.ShapeDtypeStruct((groups, share, columns), bf16)
            for columns in widths + (second.shape[1],)
        ]
        + [jax.ShapeDtypeStruct((rows, width), f32)],
        scratch_shapes=[pltpu.VMEM((4 * rows, width), bf16)]
        + blocks(widths[0])
        + blocks(widths[1])
        + sum_buffers(rows, width)
        + [pltpu.SemaphoreType.DMA((chunks, half)) for _ in range(4)]
        + [pltpu.SemaphoreType.DMA((chunks + 1, 3)) for _ in range(2)]
        + sum_sems(),
        compiler_params=pltpu.CompilerParams(
            collective_id=number, has_side_effects=True, vmem_limit_bytes=60 << 20
        ),
        cost_estimate=pl.CostEstimate(
            flops=80_000_000_000, transcendentals=0, bytes_accessed=40_000_000
        ),
        name="finish_last",
    )(
        grads,
        first,
        grad.reshape(peers, groups, share, widths[0]),
        output_grad.reshape(peers, groups, share, widths[1]),
        second.reshape(groups, share, second.shape[1]),
        grad_middle, tokens, gain,
    )


def inverse_rms(value):
    return lax.rsqrt(jnp.mean(value * value, axis=1, keepdims=True) + epsilon)


def through_norm(grad, value):
    factor = inverse_rms(value)
    normed = value * factor
    return factor * (grad - normed * jnp.mean(grad * normed, axis=1, keepdims=True))


def after_attention(total, here, tokens_ref, gain_ref):
    middle = tokens_ref[here, :].astype(f32) + total
    return middle, middle * inverse_rms(middle) * gain_ref[0:1, :]


def after_hidden(total, here, cotangent_ref, middle_ref, gain_ref):
    grad = cotangent_ref[here, :].astype(f32) + through_norm(
        total * gain_ref[0:1, :], middle_ref[here, :]
    )
    return grad, grad


def after_first(total, here, grad_ref, tokens_ref, gain_ref):
    grad = grad_ref[here, :] + through_norm(
        total * gain_ref[0:1, :], tokens_ref[here, :].astype(f32)
    )
    return grad, None


FEED_TILE = 256
FEED_COLUMNS = 512


def feed_kernel(input_ref, cotangent_ref, weight_ref, down_weight_ref, down_ref, grad_ref, total_ref,
                acts, turned0, turned1, stage, near_buf, far_buf, near_send, near_recv, far_send, far_recv):
    step = pl.program_id(0)
    hidden_width = down_weight_ref.shape[1]
    size = total_ref.shape[0]
    per = size // FEED_TILE
    tiles = 4 * per
    _, near, far, _ = partners()

    @pl.when(step == 0)
    def _():
        greet([on_head(near), on_head(far)])

    def to_near(which, piece):
        return remote(
            stage.at[which * per + piece],
            near_buf.at[which, piece],
            near_send.at[which, piece],
            near_recv.at[which, piece],
            on_head(near),
        )

    def to_far(piece):
        return remote(
            near_buf.at[0, piece], far_buf.at[piece], far_send.at[piece], far_recv.at[piece],
            on_head(far),
        )

    @pl.when(step < tiles)
    def _():
        here = tile_of(step, FEED_TILE)
        inputs, cotangent = input_ref[...], cotangent_ref[...]
        turned0[:, here] = inputs.T
        turned1[:, here] = cotangent.T
        gate_at, up_at, down_at = (
            slice(n * hidden_width, (n + 1) * hidden_width) for n in range(3)
        )
        gate = dot(inputs, weight_ref[:, gate_at])
        up = dot(inputs, weight_ref[:, up_at])
        grad_hidden = dot(cotangent, down_weight_ref[...])
        opening = jax.nn.sigmoid(gate)
        active = gate * opening
        hidden = (active * up).astype(bf16)
        grad_gate = (grad_hidden * up * opening * (1.0 + gate * (1.0 - opening))).astype(bf16)
        grad_up = (grad_hidden * active).astype(bf16)
        acts[here, gate_at] = grad_gate
        acts[here, up_at] = grad_up
        acts[here, down_at] = hidden
        down_ref[...] = dot(hidden, down_weight_ref[...], NT).astype(bf16)
        back = dot(grad_gate, weight_ref[:, gate_at], NT) + dot(
            grad_up, weight_ref[:, up_at], NT
        )
        for piece in range(per):
            for which, first in ((0, 0), (1, 2 * per)):

                @pl.when(step == first + piece)
                def _():
                    stage[which * per + piece] = back.astype(bf16)
                    to_near(which, piece).start()

            @pl.when(step == per + piece)
            def _():
                to_near(0, piece).wait_recv()
                near_buf[0, piece] = (back + near_buf[0, piece].astype(f32)).astype(bf16)
                to_far(piece).start()

            @pl.when(step == 3 * per + piece)
            def _():
                total_ref[piece * FEED_TILE : (piece + 1) * FEED_TILE, :] = back

    @pl.when(step >= tiles)
    def _():
        at = tile_of(step - tiles, FEED_COLUMNS)
        from_input = (step - tiles) * FEED_COLUMNS < 2 * hidden_width

        @pl.when(from_input)
        def _():
            grad_ref[...] = dot(turned0[...], acts[:, at]).astype(bf16)

        @pl.when(jnp.logical_not(from_input))
        def _():
            grad_ref[...] = dot(turned1[...], acts[:, at]).astype(bf16)

    @pl.when(step == pl.num_programs(0) - 1)
    def _():
        for piece in range(per):
            here = slice(piece * FEED_TILE, (piece + 1) * FEED_TILE)
            to_near(1, piece).wait_recv()
            to_far(piece).wait_recv()
            total_ref[here, :] += near_buf[1, piece].astype(f32) + far_buf[piece].astype(f32)
            to_near(0, piece).wait_send()
            to_near(1, piece).wait_send()
            to_far(piece).wait_send()


def feed(inputs, cotangent, weight, down_weight, number):
    rows, width = inputs.shape
    columns = weight.shape[1] + down_weight.shape[1]
    size = rows // 4
    tiles, per = rows // FEED_TILE, size // FEED_TILE
    tile = pl.BlockSpec((FEED_TILE, width), lambda n: (jnp.minimum(n, tiles - 1), 0))

    def whole(shape):
        return pl.BlockSpec(shape, lambda n: (0, 0), pipeline_mode=pl.Buffered(1))

    return pl.pallas_call(
        feed_kernel,
        grid=(tiles + columns // FEED_COLUMNS,),
        in_specs=[tile, tile, whole(weight.shape), whole(down_weight.shape)],
        out_specs=[
            tile,
            pl.BlockSpec((width, FEED_COLUMNS), lambda n: (0, jnp.maximum(n - tiles, 0))),
            whole((size, width)),
        ],
        out_shape=[
            jax.ShapeDtypeStruct((rows, width), bf16),
            jax.ShapeDtypeStruct((width, columns), bf16),
            jax.ShapeDtypeStruct((size, width), f32),
        ],
        scratch_shapes=[
            pltpu.VMEM((rows, columns), bf16),
            pltpu.VMEM((width, rows), bf16),
            pltpu.VMEM((width, rows), bf16),
            pltpu.VMEM((2 * per, FEED_TILE, width), bf16),
            pltpu.VMEM((2, per, FEED_TILE, width), bf16),
            pltpu.VMEM((per, FEED_TILE, width), bf16),
            pltpu.SemaphoreType.DMA((2, per)),
            pltpu.SemaphoreType.DMA((2, per)),
            pltpu.SemaphoreType.DMA((per,)),
            pltpu.SemaphoreType.DMA((per,)),
        ],
        compiler_params=pltpu.CompilerParams(
            collective_id=number, has_side_effects=True, vmem_limit_bytes=63 << 20
        ),
        cost_estimate=pl.CostEstimate(
            flops=6 * rows * width * columns, transcendentals=rows * columns // 3,
            bytes_accessed=45_000_000,
        ),
        name="feed",
    )(inputs, cotangent, weight, down_weight)


def over_tokens(operand, other_side):
    return lax.dot_general(
        operand, other_side, (((0,), (0,)), ((), ())), preferred_element_type=f32
    )


def sent_columns(pieces, groups):
    packed = jnp.concatenate(
        [piece.reshape(piece.shape[0], groups, -1) for piece in pieces], axis=2
    )
    mine = lax.all_to_all(packed, "head", split_axis=1, concat_axis=0, tiled=True)
    return mine.reshape(mine.shape[0], mine.shape[2])


def all_rows(mine):
    return lax.all_gather(mine, "blk", axis=0, tiled=True)


def row_sums(grad):
    return lax.psum_scatter(grad, "blk", scatter_dimension=0, tiled=True)


def crossing_sum(part):
    cross, far, near, own = (piece.astype(f32) for piece in jnp.split(part, 4))
    members = range(lax.axis_size("head"))
    got = lax.ppermute(
        jnp.concatenate([cross, near]).astype(bf16), "head",
        [(n, n + 1 - 2 * (n % 2)) for n in members],
    )
    of_far, of_own = jnp.split(got.astype(f32), 2)
    back = lax.ppermute(
        (far + of_far).astype(bf16), "head", [(n, (n + 2) % 4) for n in members]
    )
    return own + of_own + back.astype(f32)


def body(
    tokens,
    segment,
    norm1_gain,
    w_query,
    w_key,
    w_value,
    w_gate_out,
    w_forget,
    forget_bias,
    w_output,
    norm2_gain,
    w_gate,
    w_up,
    w_down,
    cotangent,
):
    token_rows, model_width = tokens.shape
    groups = lax.axis_size("head")
    head_count = forget_bias.shape[0]
    local_heads = head_count // groups
    local_width = model_width // groups
    hidden_width = w_gate.shape[1] // groups
    rows = token_rows * groups
    share = w_query.shape[0]
    group = lax.axis_index("head")

    low = lambda array: array.astype(bf16)
    spread = lambda gain: jnp.broadcast_to(low(gain)[:, None, None], (share, groups, 1))
    forget_low = low(w_forget).reshape(share, groups, local_heads)
    rest = LANES - local_heads - 2
    small = jnp.concatenate(
        [forget_low, spread(norm1_gain), spread(norm2_gain), jnp.zeros((share, groups, rest), bf16)],
        axis=2,
    )
    first, tokens_all, cotangent_all = gather_first(
        (w_key, w_value), jnp.swapaxes(small, 0, 1), (w_query, w_gate_out, w_output), tokens,
        cotangent, 0,
    )
    kv_width = 2 * local_width + LANES
    output_weight = first[:, kv_width + 2 * local_width :]

    def gain_rows(column):
        gain = first[:, 2 * local_width + local_heads + column].astype(f32)
        return jnp.broadcast_to(gain[None, :], (8, model_width))

    gain1, gain2 = gain_rows(0), gain_rows(1)
    bias = lax.dynamic_slice_in_dim(forget_bias, group * local_heads, local_heads, 0)
    bias = jnp.broadcast_to(jnp.pad(bias, (0, LANES - local_heads))[None, :], (8, LANES))
    input1, key_value, terms, turned_terms, forget = project(
        tokens_all, gain1, first, bias, 2 * local_width, local_heads
    )
    earlier_kv = passed_along(key_value, "blk", 1)
    earlier_terms = passed_along(turned_terms, "blk", 1)
    query = dot(input1, first[:, kv_width : kv_width + local_width]).astype(bf16)
    gate_raw = dot(
        input1, first[:, kv_width + local_width : kv_width + 2 * local_width]
    )

    segment_plus = segment + 1
    earlier_segment = passed_along(segment_plus, "blk", 1)
    window = jnp.concatenate([earlier_segment, segment_plus])
    begins = jnp.sum(
        (window[:, None] < segment_plus[None, :]).astype(jnp.int32), axis=0
    )
    tiles = begins.reshape(rows // Q_TILE, Q_TILE)
    ranges = jnp.stack([tiles[:, 0] // K_TILE, (tiles[:, -1] + K_TILE - 1) // K_TILE])
    begins = jnp.broadcast_to(begins[None, :], (8, rows))

    so_far = attend(True, ranges, query, key_value, terms, terms, begins, local_heads)
    later = lax.optimization_barrier((w_gate, w_up, w_down, key_value))
    mine = sent_columns([low(weight) for weight in later[:3]], groups)
    mine, earlier_kv, earlier_terms, so_far, gate_raw = lax.optimization_barrier(
        (mine, earlier_kv, earlier_terms, so_far, gate_raw)
    )
    second = all_rows(mine[:, : 2 * hidden_width])
    mine_down = mine[:, 2 * hidden_width :].reshape(groups, share, hidden_width)
    attended, lse = attend(
        False, ranges, query, earlier_kv, terms, earlier_terms, begins, local_heads, so_far
    )
    opened = jax.nn.sigmoid(gate_raw)
    attended_wide = attended.astype(f32)
    gated = (opened * attended_wide).astype(bf16)
    branch = dot(gated, output_weight, NT).astype(bf16)
    middle, input2, down_weight = exchange(
        after_attention, branch, [tokens, gain2], False, 1, "exchange_middle", mine_down
    )
    down_weight = down_weight.reshape(model_width, hidden_width)
    down, second_grad, grad_input2 = feed(input2, cotangent_all, second, down_weight, 4)
    second_part = row_sums(second_grad)
    grad_middle, grad_branch = exchange(
        after_hidden, grad_input2, [cotangent, middle, gain2], True, 2, "exchange_hidden"
    )

    down, grad_branch = lax.optimization_barrier((down, grad_branch))
    result = (middle + crossing_sum(down)).astype(bf16)
    grad_gated = dot(grad_branch, output_weight)
    grad_attended = (grad_gated * opened).astype(bf16)
    grad_gate_pre = (grad_gated * attended_wide * opened * (1.0 - opened)).astype(bf16)
    dq_prev, rows_prev, dkv_prev, decay_prev = attend_back(
        False, ranges, query, earlier_kv, terms, earlier_terms, begins, grad_attended, attended,
        lse, local_heads,
    )
    dkv_later = passed_along(dkv_prev, "blk", -1)
    decay_later = passed_along(decay_prev[:, :8], "blk", -1)
    decay_later = jnp.pad(decay_later, ((0, 0), (0, LANES - 8)))
    dq, dk_own, dv_own, decay_own = attend_back(
        True, ranges, query, key_value, terms, terms, begins, grad_attended, attended,
        lse, local_heads, (dq_prev, rows_prev),
    )
    dk = (dk_own + dkv_later[0].astype(f32)).astype(bf16)
    dv = (dv_own + dkv_later[1].astype(f32)).astype(bf16)
    logf_grad = decay_back(decay_own, decay_later)
    forget_grad = jnp.where(
        jnp.arange(LANES)[None, :] < local_heads, logf_grad * jax.nn.sigmoid(-forget), 0.0
    ).astype(bf16)
    grads = jnp.concatenate([dk, dv, forget_grad, dq, grad_gate_pre], axis=1)
    first_grad = over_tokens(input1, grads)
    bias_part = jnp.sum(forget_grad.astype(f32), axis=0)
    row = jnp.arange(model_width)[:, None] % share
    column = jnp.arange(kv_width + 2 * local_width)[None, :]
    spread_bias = jnp.sum(
        jnp.where(row == jnp.arange(LANES)[None, :], bias_part[None, :], 0.0), axis=1, keepdims=True
    )
    first_grad = jnp.where(
        column == 2 * local_width + local_heads, spread_bias, first_grad
    ).astype(bf16)
    output_grad = over_tokens(grad_branch, gated).astype(bf16)
    first_sum, output_sum, second_sum, tokens_grad = finish_last(
        grads, first, first_grad, output_grad, second_part, groups, grad_middle, tokens, gain1, 3
    )
    first_sum, output_sum, second_sum = (
        jnp.swapaxes(array, 0, 1).astype(f32) for array in (first_sum, output_sum, second_sum)
    )

    def columns(array, start, width):
        return array[:, :, start : start + width].reshape(share, groups * width)

    key_sum, value_sum = (columns(first_sum, n * local_width, local_width) for n in range(2))
    forget_sum = columns(first_sum, 2 * local_width, local_heads)
    bias_total = first_sum[:local_heads, :, 2 * local_width + local_heads].T.reshape(head_count)
    query_sum, gate_out_sum = (
        columns(first_sum, kv_width + n * local_width, local_width) for n in range(2)
    )
    output_total = columns(output_sum, 0, local_width)
    gate_sum, up_sum, down_sum = (
        columns(second_sum, n * hidden_width, hidden_width) for n in range(3)
    )

    def along(weight, grad):
        return jnp.sum(low(weight).astype(f32) * grad, axis=1)

    gain1_total = (
        along(w_query, query_sum)
        + along(w_key, key_sum)
        + along(w_value, value_sum)
        + along(w_gate_out, gate_out_sum)
        + along(w_forget, forget_sum)
    ) / low(norm1_gain).astype(f32)
    gain2_total = (along(w_gate, gate_sum) + along(w_up, up_sum)) / low(norm2_gain).astype(f32)
    return (
        result,
        tokens_grad,
        gain1_total,
        query_sum,
        key_sum,
        value_sum,
        gate_out_sum,
        forget_sum,
        bias_total,
        output_total,
        gain2_total,
        gate_sum,
        up_sum,
        down_sum,
    )


def solution(mesh):
    both = ("blk", "head")
    matrix, vector = P(both, None), P(both)
    return jax.shard_map(
        body,
        mesh=mesh,
        in_specs=(
            matrix, P("blk"), vector, matrix, matrix, matrix, matrix, matrix, P(), matrix, vector,
            matrix, matrix, matrix, matrix,
        ),
        out_specs=(
            matrix, matrix, vector, matrix, matrix, matrix, matrix, matrix, P(), matrix, vector,
            matrix, matrix, matrix,
        ),
        check_vma=False,
    )
```

```python
import functools

import jax
import jax.numpy as jnp
from jax import lax
from jax.experimental import pallas as pl
from jax.experimental.pallas import tpu as pltpu
from jax.sharding import PartitionSpec as P

epsilon = 1e-06
LANES = 128
Q_TILE = 512
K_TILE = 512
FAR = -1e30
NT = (((1,), (1,)), ((), ()))
NN = (((1,), (0,)), ((), ()))
bf16 = jnp.bfloat16
f32 = jnp.float32


def dot(a, b, dims=NN, **kw):
    return lax.dot_general(a, b, dims, preferred_element_type=f32, **kw)


def passed_along(array, axis, by):
    peers = lax.axis_size(axis)
    pairs = [(i, i + by) for i in range(peers) if 0 <= i + by < peers]
    return lax.ppermute(array, axis, pairs)


def split3(value):
    high = value.astype(bf16)
    rest = value - high.astype(f32)
    mid = rest.astype(bf16)
    low = (rest - mid.astype(f32)).astype(bf16)
    return high, mid, low


def running(value_of, steps, rows, upper):
    place = lax.broadcasted_iota(jnp.int32, (rows, rows), 0)
    other = lax.broadcasted_iota(jnp.int32, (rows, rows), 1)
    tri = jnp.where((other >= place) if upper else (other <= place), 1.0, 0.0).astype(bf16)
    outs = [None] * steps
    carry = jnp.zeros((1, LANES), f32)
    order = range(steps - 1, -1, -1) if upper else range(steps)
    for n in order:
        block = value_of(n)
        total = sum(dot(tri, part) for part in split3(block)) + carry
        outs[n] = total
        carry = total[0:1] if upper else total[rows - 1 : rows]
    return outs, carry


PROJECT_TILE = 256
TERM_ROWS = 32


def project_kernel(local_heads, tokens_ref, gain_ref, weight_ref, bias_ref, input_ref, out_ref,
                   terms_ref, turned_ref, forget_ref, carry_ref):
    rows = tokens_ref.shape[0]
    wide = weight_ref.shape[1] - LANES

    @pl.when(pl.program_id(0) == 0)
    def _():
        carry_ref[...] = jnp.zeros_like(carry_ref)

    tokens = tokens_ref[...].astype(f32)
    input1 = (tokens * inverse_rms(tokens) * gain_ref[0:1, :]).astype(bf16)
    input_ref[...] = input1
    raw = dot(input1, weight_ref[...])
    out_ref[...] = raw[:, :wide].astype(bf16)
    forget = (raw[:, wide:] + bias_ref[0:1, :]).astype(bf16).astype(f32)
    forget_ref[...] = forget
    lane = lax.broadcasted_iota(jnp.int32, (rows, LANES), 1)
    logf = jnp.minimum(forget, 0.0) - jnp.log1p(jnp.exp(-jnp.abs(forget)))
    logf = jnp.where(lane < local_heads, logf, 0.0)
    place = lax.broadcasted_iota(jnp.int32, (rows, rows), 0)
    other = lax.broadcasted_iota(jnp.int32, (rows, rows), 1)
    tri = jnp.where(other <= place, 1.0, 0.0).astype(bf16)
    sums = sum(dot(tri, part) for part in split3(logf)) + carry_ref[0:1, :]
    carry_ref[0:1, :] = sums[rows - 1 : rows, :]
    high, mid, low = split3(sums)
    terms = (
        high.astype(f32)
        + pltpu.roll(mid.astype(f32), local_heads, 1)
        + pltpu.roll(low.astype(f32), 2 * local_heads, 1)
        + jnp.where(lane == 3 * local_heads, 1.0, 0.0)
    ).astype(bf16)
    terms_ref[...] = terms
    turned_ref[...] = terms.T[0:TERM_ROWS, :]


def project(tokens, gain, weight, bias, wide, local_heads):
    rows, width = tokens.shape

    def tile(columns):
        return pl.BlockSpec((PROJECT_TILE, columns), lambda n: (n, 0))

    def whole(*shape):
        return pl.BlockSpec(shape, lambda n: (0, 0))

    return pl.pallas_call(
        functools.partial(project_kernel, local_heads),
        grid=(rows // PROJECT_TILE,),
        in_specs=[tile(width), whole(8, width), whole(width, wide + LANES), whole(8, LANES)],
        out_specs=[
            tile(width),
            tile(wide),
            tile(LANES),
            pl.BlockSpec((TERM_ROWS, PROJECT_TILE), lambda n: (0, n)),
            tile(LANES),
        ],
        out_shape=[
            jax.ShapeDtypeStruct((rows, width), bf16),
            jax.ShapeDtypeStruct((rows, wide), bf16),
            jax.ShapeDtypeStruct((rows, LANES), bf16),
            jax.ShapeDtypeStruct((TERM_ROWS, rows), bf16),
            jax.ShapeDtypeStruct((rows, LANES), f32),
        ],
        scratch_shapes=[pltpu.VMEM((8, LANES), f32)],
        cost_estimate=pl.CostEstimate(
            flops=2 * rows * width * (wide + LANES), transcendentals=rows * LANES,
            bytes_accessed=20_000_000,
        ),
        name="project",
    )(tokens, gain, weight, bias)


def decay_back_kernel(own_ref, halo_ref, out_ref):
    rows = 256
    steps = own_ref.shape[0] // rows
    own, _ = running(lambda n: own_ref[n * rows : (n + 1) * rows, :], steps, rows, True)
    halo, _ = running(lambda n: halo_ref[n * rows : (n + 1) * rows, :], steps, rows, False)
    for n in range(steps):
        part = slice(n * rows, (n + 1) * rows)
        out_ref[part, :] = own[n] + (halo[n] - halo_ref[part, :])


def decay_back(own, halo):
    return pl.pallas_call(
        decay_back_kernel,
        out_shape=jax.ShapeDtypeStruct(own.shape, f32),
        name="decay_back",
    )(own, halo)


QUERY, KEY, TOTAL = range(3)


def placing(pair, local_heads, role):
    row = lax.broadcasted_iota(jnp.int32, (LANES, LANES), 0)
    col = lax.broadcasted_iota(jnp.int32, (LANES, LANES), 1)
    head = jnp.where(col < 64, 2 * pair + 1, 2 * pair)
    spot = jnp.where(col < 64, col, col - 64)
    term = spot - 3 * role
    is_term = (term >= 0) & (term < 3) & (row == term * local_heads + head)
    if role == QUERY:
        ones = (spot >= 3) & (spot < 9)
    else:
        ones = (spot < 3) & (role == KEY)
    is_one = ones & (row == 3 * local_heads)
    sign = -1.0 if role == KEY else 1.0
    return (jnp.where(is_term, sign, 0.0) + jnp.where(is_one, 1.0, 0.0)).astype(bf16)


def allowed_pairs(first_key, query_tile, rows, begin_row):
    shape = (K_TILE, Q_TILE)
    key_place = first_key + lax.broadcasted_iota(jnp.int32, shape, 0)
    query_place = rows + query_tile * Q_TILE + lax.broadcasted_iota(jnp.int32, shape, 1)
    return (key_place >= begin_row) & (key_place <= query_place)


def key_range(ranges_ref, query_tile, rows, own):
    count = rows // K_TILE
    base = count if own else 0
    first = jnp.clip(ranges_ref[0, query_tile] - base, 0, count)
    full = jnp.clip(ranges_ref[1, query_tile] - base, first, count)
    return first, full


def key_loops(ranges_ref, query_tile, rows, own, step, carry):
    first, full = key_range(ranges_ref, query_tile, rows, own)
    inside = query_tile * (Q_TILE // K_TILE) if own else rows // K_TILE
    full = jnp.minimum(full, inside)
    carry = lax.fori_loop(first, full, functools.partial(step, True), carry)
    carry = lax.fori_loop(full, inside, functools.partial(step, False), carry)
    if own:
        carry = lax.fori_loop(
            inside, inside + Q_TILE // K_TILE, functools.partial(step, True), carry
        )
    return carry


def tile_of(number, size):
    return pl.ds(pl.multiple_of(number * size, size), size)


def fill_keys(pair, local_heads, own, first, key_ref, terms_ref, keys):
    place = placing(pair, local_heads, KEY)
    lane = lax.broadcasted_iota(jnp.int32, (K_TILE, LANES), 1)
    rows = key_ref.shape[0]
    if not own:
        last = terms_ref[:, rows - LANES : rows].T
        total = dot(last, placing(pair, local_heads, TOTAL)[0:TERM_ROWS, :])[LANES - 1 : LANES, :]

    def fill(n, carry):
        here = tile_of(n, K_TILE)
        if own:
            extra = dot(terms_ref[here, :], place).astype(bf16)
        else:
            extra = dot(terms_ref[:, here].T, place[0:TERM_ROWS, :])
            extra = (extra + total).astype(bf16)
        key = key_ref[here, :]
        keys[0][here, :] = jnp.where(lane < 64, key, extra)
        keys[1][here, :] = jnp.where(lane < 64, extra, key)
        return carry

    lax.fori_loop(first, rows // K_TILE, fill, 0)


def query_tiles(q_ref, terms_ref, place, here, scaling):
    lane = lax.broadcasted_iota(jnp.int32, (Q_TILE, LANES), 1)
    extra = dot(terms_ref[here, :], place).astype(bf16)
    query = (q_ref[here, :].astype(f32) * scaling).astype(bf16)
    return jnp.where(lane < 64, query, extra), jnp.where(lane < 64, extra, query)


def attend_kernel(local_heads, own, ranges_ref, q_ref, k_ref, v_ref, t_query_ref, t_key_ref,
                  begin_ref, *refs):
    if own:
        acc_out_ref, state_out_ref, key0, key1, values, acc0, acc1 = refs
    else:
        acc_in_ref, state_in_ref, o_ref, lse_ref, key0, key1, values, acc0, acc1 = refs
    pair = pl.program_id(0)
    rows = q_ref.shape[0]
    base = rows if own else 0
    keys, accs = (key0, key1), (acc0, acc1)
    first, _ = key_range(ranges_ref, 0, rows, own)
    fill_keys(pair, local_heads, own, first, k_ref, t_key_ref, keys)

    def turn(n, carry):
        values[:, tile_of(n, K_TILE)] = v_ref[tile_of(n, K_TILE), :].T
        return carry

    lax.fori_loop(first, rows // K_TILE, turn, 0)
    place = placing(pair, local_heads, QUERY)

    def query_loop(tile, carry):
        here = tile_of(tile, Q_TILE)
        queries = query_tiles(q_ref, t_query_ref, place, here, 64**-0.5)
        begin_row = begin_ref[0:1, here]
        if own:
            low = jnp.full((1, Q_TILE), FAR, f32)
            zero = jnp.zeros((1, Q_TILE), f32)
            state = (low, zero, low, zero)
            for acc in accs:
                acc[...] = jnp.zeros_like(acc)
        else:
            state = tuple(state_in_ref[n : n + 1, here] for n in range(4))
            for h in range(2):
                accs[h][...] = acc_in_ref[64 * h : 64 * (h + 1), here]

        def step(masked, number, state):
            there = tile_of(number, K_TILE)
            fresh = []
            if masked:
                allowed = allowed_pairs(base + number * K_TILE, tile, rows, begin_row)
            for h in range(2):
                largest, total = state[2 * h], state[2 * h + 1]
                scores = dot(keys[h][there, :], queries[h], NT)
                if masked:
                    scores = jnp.where(allowed, scores, FAR)
                now = jnp.maximum(largest, jnp.max(scores, axis=0, keepdims=True))
                fade = jnp.exp(largest - now)
                weights = jnp.exp(scores - now)
                total = total * fade + jnp.sum(weights, axis=0, keepdims=True)
                accs[h][...] = accs[h][...] * fade + dot(
                    values[64 * h : 64 * (h + 1), there], weights.astype(bf16)
                )
                fresh += [now, total]
            return tuple(fresh)

        state = key_loops(ranges_ref, tile, rows, own, step, state)
        if own:
            for h in range(2):
                acc_out_ref[64 * h : 64 * (h + 1), here] = accs[h][...]
            for n in range(4):
                state_out_ref[n : n + 1, here] = state[n]
        else:
            mixed = jnp.concatenate(
                [accs[h][...] * (1.0 / state[2 * h + 1]) for h in range(2)], axis=0
            )
            o_ref[here, :] = mixed.T.astype(bf16)
            for h in range(2):
                lse_ref[h : h + 1, here] = state[2 * h] + jnp.log(state[2 * h + 1])
        return carry

    lax.fori_loop(0, rows // Q_TILE, query_loop, 0)


def lane_block(rows, offset):
    return pl.BlockSpec((rows, LANES), lambda p, *_: (0, offset + p))


def fixed(shape):
    return pl.BlockSpec(shape, lambda p, *_: (0, 0))


def pair_block(height, rows):
    return pl.BlockSpec((height, rows), lambda p, *_: (p, 0))


def attend(own, ranges, query, key_value, terms, key_terms, begins, local_heads, so_far=()):
    rows = query.shape[0]
    pairs = local_heads // 2
    running_specs = [pair_block(LANES, rows), pair_block(8, rows)]
    running_shape = (
        jax.ShapeDtypeStruct((LANES * pairs, rows), f32),
        jax.ShapeDtypeStruct((8 * pairs, rows), f32),
    )
    final_specs = [lane_block(rows, 0), pair_block(8, rows)]
    final_shape = (
        jax.ShapeDtypeStruct((rows, pairs * LANES), bf16),
        jax.ShapeDtypeStruct((8 * pairs, rows), f32),
    )
    return pl.pallas_call(
        functools.partial(attend_kernel, local_heads, own),
        grid_spec=pltpu.PrefetchScalarGridSpec(
            num_scalar_prefetch=1,
            grid=(pairs,),
            in_specs=[
                lane_block(rows, 0),
                lane_block(rows, 0),
                lane_block(rows, pairs),
                fixed((rows, LANES)),
                fixed((rows, LANES) if own else (TERM_ROWS, rows)),
                fixed((8, rows)),
            ]
            + ([] if own else running_specs),
            out_specs=running_specs if own else final_specs,
            scratch_shapes=[
                pltpu.VMEM((rows, LANES), bf16),
                pltpu.VMEM((rows, LANES), bf16),
                pltpu.VMEM((LANES, rows), bf16),
                pltpu.VMEM((64, Q_TILE), f32),
                pltpu.VMEM((64, Q_TILE), f32),
            ],
        ),
        out_shape=running_shape if own else final_shape,
        cost_estimate=pl.CostEstimate(
            flops=40_000_000_000 if own else 10_000_000_000,
            transcendentals=20_000_000,
            bytes_accessed=12_000_000,
        ),
        name="attend_own" if own else "attend_prev",
    )(ranges, query, key_value, key_value, terms, key_terms, begins, *so_far)


def attend_back_kernel(local_heads, own, ranges_ref, q_ref, k_ref, v_ref, t_query_ref, t_key_ref,
                       begin_ref, grad_ref, o_ref, lse_ref, *refs):
    if own:
        dq_in_ref, decay_in_ref, dq_ref, dk_ref, dv_ref, decay_ref = refs[:6]
    else:
        dq_ref, row_decay_ref, dkv_ref, decay_ref = refs[:4]
        dk_ref, dv_ref = dkv_ref.at[0], dkv_ref.at[1]
    key0, key1, key_t0, key_t1, dk0, dk1, dv, dq0, dq1 = refs[-9:]
    pair = pl.program_id(0)
    rows = q_ref.shape[0]
    base = rows if own else 0
    keys, keys_t, dks, dqs = (key0, key1), (key_t0, key_t1), (dk0, dk1), (dq0, dq1)
    first, _ = key_range(ranges_ref, 0, rows, own)
    fill_keys(pair, local_heads, own, first, k_ref, t_key_ref, keys)

    def turn(n, carry):
        here = tile_of(n, K_TILE)
        for h in range(2):
            keys_t[h][:, here] = keys[h][here, :].T
        return carry

    lax.fori_loop(first, rows // K_TILE, turn, 0)
    for ref in (dk0, dk1, dv):
        ref[...] = jnp.zeros_like(ref)
    place = placing(pair, local_heads, QUERY)
    lane = lax.broadcasted_iota(jnp.int32, (Q_TILE, LANES), 1)
    pick_row = lax.broadcasted_iota(jnp.int32, (8, LANES), 0)
    pick_lane = lax.broadcasted_iota(jnp.int32, (8, LANES), 1)
    pick = jnp.where((pick_lane // 64) == pick_row, 1.0, 0.0)
    sums_ref = decay_ref if own else row_decay_ref

    @pl.when(pair == 0)
    def _():
        if own:
            decay_ref[...] = decay_in_ref[...]
        else:
            decay_ref[...] = jnp.zeros_like(decay_ref)
            row_decay_ref[...] = jnp.zeros_like(row_decay_ref)

    def query_tile(tile):
        here = tile_of(tile, Q_TILE)
        queries = query_tiles(q_ref, t_query_ref, place, here, 64**-0.5)
        begin_row = begin_ref[0:1, here]
        grad = grad_ref[here, :]
        nothing = jnp.zeros_like(grad)
        grads = (jnp.where(lane < 64, grad, nothing), jnp.where(lane < 64, nothing, grad))
        product = grad.astype(f32) * o_ref[here, :].astype(f32)
        inner = dot(pick, product, NT, precision=lax.Precision.HIGHEST)
        for dq in dqs:
            dq[...] = jnp.zeros_like(dq)

        def step(masked, number, state):
            there = tile_of(number, K_TILE)
            if masked:
                allowed = allowed_pairs(base + number * K_TILE, tile, rows, begin_row)
            value = v_ref[there, :]
            value_part = 0.0
            for h in range(2):
                scores = dot(keys[h][there, :], queries[h], NT)
                prob = jnp.exp(scores - lse_ref[h : h + 1, here])
                if masked:
                    prob = jnp.where(allowed, prob, 0.0)
                grad_prob = dot(value, grads[h], NT)
                grad_score = (prob * (grad_prob - inner[h : h + 1, :])).astype(bf16)
                value_part = value_part + dot(prob.astype(bf16), grads[h])
                dks[h][there, :] += dot(grad_score, queries[h])
                dqs[h][...] += dot(keys_t[h][:, there], grad_score)
            dv[there, :] += value_part
            return state

        key_loops(ranges_ref, tile, rows, own, step, 0)
        turned = [dq[...].T for dq in dqs]
        dq_tile = jnp.where(lane < 64, turned[0], turned[1]) * 64**-0.5
        if own:
            dq_tile = dq_tile + dq_in_ref[here, :]
        dq_ref[here, :] = dq_tile.astype(dq_ref.dtype)
        sums = sums_ref[here, :]
        sums = sums + jnp.where(lane == 2 * pair, turned[0][:, 64:65], 0.0)
        sums = sums + jnp.where(lane == 2 * pair + 1, turned[1][:, 0:1], 0.0)
        sums_ref[here, :] = sums

    def query_loop(tile, carry):
        if own:
            query_tile(tile)
        else:
            reaches = key_range(ranges_ref, tile, rows, own)[0] < rows // K_TILE
            pl.when(reaches)(lambda: query_tile(tile))

            @pl.when(jnp.logical_not(reaches))
            def _():
                dq_ref[tile_of(tile, Q_TILE), :] = jnp.zeros((Q_TILE, LANES), dq_ref.dtype)

        return carry

    lax.fori_loop(0, rows // Q_TILE, query_loop, 0)
    sign = -1.0 if own else 1.0

    def finish(n, carry):
        here = tile_of(n, Q_TILE)
        left, right = dk0[here, :], dk1[here, :]
        dk_ref[here, :] = jnp.where(lane < 64, left, right).astype(dk_ref.dtype)
        dv_ref[here, :] = dv[here, :].astype(dv_ref.dtype)
        decay = decay_ref[here, :]
        decay = decay + jnp.where(lane == 2 * pair, sign * left[:, 67:68], 0.0)
        decay = decay + jnp.where(lane == 2 * pair + 1, sign * right[:, 3:4], 0.0)
        decay_ref[here, :] = decay
        return carry

    lax.fori_loop(0, rows // Q_TILE, finish, 0)


def attend_back(
    own, ranges, query, key_value, terms, key_terms, begins, grad, mixed, lse, local_heads,
    so_far=(),
):
    rows = query.shape[0]
    pairs = local_heads // 2
    wide = jax.ShapeDtypeStruct((rows, pairs * LANES), f32)
    sums = jax.ShapeDtypeStruct((rows, LANES), f32)
    if own:
        out_specs = [lane_block(rows, 0)] * 3 + [fixed((rows, LANES))]
        out_shape = (jax.ShapeDtypeStruct(wide.shape, bf16), wide, wide, sums)
    else:
        both = pl.BlockSpec((2, rows, LANES), lambda p, *_: (0, 0, p))
        out_specs = [lane_block(rows, 0), fixed((rows, LANES)), both, fixed((rows, LANES))]
        out_shape = (
            wide, sums, jax.ShapeDtypeStruct((2, rows, pairs * LANES), bf16), sums,
        )
    return pl.pallas_call(
        functools.partial(attend_back_kernel, local_heads, own),
        grid_spec=pltpu.PrefetchScalarGridSpec(
            num_scalar_prefetch=1,
            grid=(pairs,),
            in_specs=[
                lane_block(rows, 0),
                lane_block(rows, 0),
                lane_block(rows, pairs),
                fixed((rows, LANES)),
                fixed((rows, LANES) if own else (TERM_ROWS, rows)),
                fixed((8, rows)),
                lane_block(rows, 0),
                lane_block(rows, 0),
                pair_block(8, rows),
            ]
            + ([lane_block(rows, 0), fixed((rows, LANES))] if own else []),
            out_specs=out_specs,
            scratch_shapes=[
                pltpu.VMEM((rows, LANES), bf16),
                pltpu.VMEM((rows, LANES), bf16),
                pltpu.VMEM((LANES, rows), bf16),
                pltpu.VMEM((LANES, rows), bf16),
                pltpu.VMEM((rows, LANES), f32),
                pltpu.VMEM((rows, LANES), f32),
                pltpu.VMEM((rows, LANES), f32),
                pltpu.VMEM((LANES, Q_TILE), f32),
                pltpu.VMEM((LANES, Q_TILE), f32),
            ],
        ),
        out_shape=out_shape,
        cost_estimate=pl.CostEstimate(
            flops=20_000_000_000 if own else 10_000_000_000,
            transcendentals=20_000_000,
            bytes_accessed=25_000_000,
        ),
        name="attend_back_own" if own else "attend_back_prev",
    )(
        ranges, query, key_value, key_value, terms, key_terms, begins, grad, mixed, lse, *so_far
    )


PIECES = 4


def partners():
    me = lax.axis_index("head")
    near = me + 1 - 2 * (me % 2)
    far = (me + 2) % 4
    cross = (near + 2) % 4
    return me, near, far, cross


def signal(other):
    pl.semaphore_signal(
        pltpu.get_barrier_semaphore(), inc=1, device_id=other, device_id_type=pl.DeviceIdType.MESH
    )


def greet(others):
    for other in others:
        signal(other)
    pl.semaphore_wait(pltpu.get_barrier_semaphore(), len(others))


def remote(source, target, send, receive, other):
    return pltpu.make_async_remote_copy(
        src_ref=source,
        dst_ref=target,
        send_sem=send,
        recv_sem=receive,
        device_id=other,
        device_id_type=pl.DeviceIdType.MESH,
    )


def on_head(index):
    return {"head": index}


def on_blk(index):
    return {"blk": index}


def piece_at(ref, slot, piece, size):
    span = size // PIECES
    return ref.at[pl.ds(pl.multiple_of(slot * size + piece * span, span), span), :]


class Slots:
    def __init__(self, by_device):
        me, near, far, cross = partners()
        if by_device:
            self.own = self.sent_near = self.sent_far = me
            self.near, self.far, self.cross = near, far, cross
            self.passed = far
        else:
            self.own, self.sent_near, self.sent_far = 3, 2, 1
            self.near, self.far, self.cross = 2, 1, 0
            self.passed = 0


def spread_piece(source, all_ref, size, sems, piece, slots):
    me, near, far, _ = partners()
    far_send, far_recv, near_send, near_recv, _, _, own = sems
    copies = (
        remote(source, piece_at(all_ref, slots.sent_far, piece, size), far_send.at[piece],
               far_recv.at[piece], on_head(far)),
        remote(source, piece_at(all_ref, slots.sent_near, piece, size), near_send.at[piece],
               near_recv.at[piece], on_head(near)),
        pltpu.make_async_copy(source, piece_at(all_ref, slots.own, piece, size), own.at[piece]),
    )
    for copy in copies:
        copy.start()
    return copies


def hand_on(all_ref, size, sems, sent, slots):
    me, near, far, cross = partners()
    far_send, far_recv, near_send, near_recv, on_send, on_recv, own = sems
    passed = []
    for piece in range(PIECES):
        there = piece_at(all_ref, slots.far, piece, size)
        remote(there, there, far_send.at[piece], far_recv.at[piece], on_head(far)).wait_recv()
        copy = remote(
            there, piece_at(all_ref, slots.passed, piece, size), on_send.at[piece],
            on_recv.at[piece], on_head(near),
        )
        copy.start()
        passed.append(copy)

    def finish():
        for piece in range(PIECES):
            to_far, to_near, local = sent[piece]
            to_far.wait_send()
            to_near.wait_send()
            local.wait()
            passed[piece].wait_send()
            there = piece_at(all_ref, slots.near, piece, size)
            remote(there, there, near_send.at[piece], near_recv.at[piece], on_head(near)).wait_recv()
            there = piece_at(all_ref, slots.cross, piece, size)
            remote(there, there, on_send.at[piece], on_recv.at[piece], on_head(near)).wait_recv()

    return finish


def gather_sems():
    return [pltpu.SemaphoreType.DMA((PIECES,)) for _ in range(7)]


def blk_peers():
    here = lax.axis_index("blk")
    half = lax.axis_size("blk") // 2
    low, high = here % 2, here // 2
    partner = here + 1 - 2 * low
    after = [((high + t) % half) * 2 + low for t in range(half)]
    return here, partner, after


class Line:
    def __init__(self, block_of, kinds, sems):
        self.block_of, self.kinds = block_of, kinds
        self.pair_send, self.pair_recv, self.up_send, self.up_recv, self.down_send, self.down_recv = sems
        here = lax.axis_index("blk")
        self.half = lax.axis_size("blk") // 2
        self.low, self.high = here % 2, here // 2
        self.partner = here + 1 - 2 * self.low
        self.has_up, self.has_down = self.high < self.half - 1, self.high > 0

    def greet(self, others):
        greet_sum = len(others) + 1
        for other in others + [on_blk(self.partner)]:
            signal(other)
        pl.when(self.has_up)(lambda: signal(on_blk(self.at(self.high + 1))))
        pl.when(self.has_down)(lambda: signal(on_blk(self.at(self.high - 1))))
        ends = (self.high == 0).astype(jnp.int32) + (self.high == self.half - 1).astype(jnp.int32)
        pl.semaphore_wait(pltpu.get_barrier_semaphore(), greet_sum + 2 - ends)

    def at(self, high):
        return high * 2 + self.low

    def pair_copy(self, kind, high, low):
        block = self.block_of(kind, high * 2 + low)
        return remote(
            block, block, self.pair_send.at[kind, high], self.pair_recv.at[kind, high],
            on_blk(self.partner),
        )

    def up_copy(self, kind, high):
        block = self.block_of(kind, self.at(high))
        return remote(
            block, block, self.up_send.at[kind, high], self.up_recv.at[kind, high],
            on_blk(self.at(jnp.minimum(self.high + 1, self.half - 1))),
        )

    def down_copy(self, kind, high):
        block = self.block_of(kind, self.at(high))
        return remote(
            block, block, self.down_send.at[kind, high], self.down_recv.at[kind, high],
            on_blk(self.at(jnp.maximum(self.high - 1, 0))),
        )

    def launch(self, kind):
        self.pair_copy(kind, self.high, self.low).start()
        pl.when(self.has_up)(lambda: self.up_copy(kind, self.high).start())
        pl.when(self.has_down)(lambda: self.down_copy(kind, self.high).start())

    def step(self, t):
        for kind in range(self.kinds):
            below, above = self.high - t, self.high + t

            @pl.when(below >= 0)
            def _():
                self.up_copy(kind, below).wait_recv()
                self.pair_copy(kind, below, self.low).start()
                pl.when(self.has_up)(lambda: self.up_copy(kind, below).start())

            @pl.when(above < self.half)
            def _():
                self.down_copy(kind, above).wait_recv()
                self.pair_copy(kind, above, self.low).start()
                pl.when(self.has_down)(lambda: self.down_copy(kind, above).start())

    def finish(self):
        for kind in range(self.kinds):

            def wait(high, carry):
                self.pair_copy(kind, high, self.low).wait_send()
                self.pair_copy(kind, high, 1 - self.low).wait_recv()

                @pl.when((high <= self.high) & self.has_up)
                def _():
                    self.up_copy(kind, high).wait_send()

                @pl.when((high >= self.high) & self.has_down)
                def _():
                    self.down_copy(kind, high).wait_send()

                return carry

            lax.fori_loop(0, self.half, wait, 0)


def gather_first_kernel(before, after, *refs):
    small_ref, weight_refs = refs[0], refs[1 : 1 + before + after]
    tokens_ref, cotangent_ref, pack_all, tokens_all, cotangent_all, pack_ref = refs[
        1 + before + after : 7 + before + after
    ]
    sems = refs[7 + before + after :]
    groups = pack_ref.shape[0]
    start = 0
    for n, ref in enumerate(weight_refs):
        if n == before:
            pack_ref[:, :, start : start + LANES] = small_ref[...]
            start += LANES
        wide = ref.shape[1] // groups
        for group in range(groups):
            pack_ref[group, :, start : start + wide] = ref[
                :, group * wide : (group + 1) * wide
            ].astype(bf16)
        start += wide
    swap_send, swap_recv, swap_own = sems[:3]
    token_sems, cotangent_sems = sems[9:16], sems[16:23]
    me, near, far, cross = partners()
    sources = (me, near, far, cross)
    line = Line(lambda kind, blk: pack_all.at[blk, sources[kind]], 4, sems[3:9])
    here = lax.axis_index("blk")
    line.greet([on_head(near), on_head(far), on_head(cross)])
    swaps = [pltpu.make_async_copy(pack_ref.at[me], pack_all.at[here, me], swap_own)]
    for kind, other in enumerate((near, far, cross)):
        swaps.append(
            remote(
                pack_ref.at[other],
                pack_all.at[here, me],
                swap_send.at[kind],
                swap_recv.at[kind],
                on_head(other),
            )
        )
    for swap in swaps:
        swap.start()
    size = tokens_ref.shape[0]
    span = size // PIECES

    def spread_all(ref, all_ref, some, slots):
        return [
            spread_piece(ref.at[pl.ds(piece * span, span), :], all_ref, size, some, piece, slots)
            for piece in range(PIECES)
        ]

    by_device, crossing = Slots(True), Slots(False)
    tokens_sent = spread_all(tokens_ref, tokens_all, token_sems, by_device)
    swaps[0].wait()
    line.launch(0)
    for kind, source in enumerate((near, far, cross)):
        block = pack_all.at[here, source]
        remote(
            block, block, swap_send.at[kind], swap_recv.at[kind], on_head(source)
        ).wait_recv()
        line.launch(kind + 1)
    cotangent_sent = spread_all(cotangent_ref, cotangent_all, cotangent_sems, crossing)
    for t in range(1, line.half):
        line.step(t)
        if t == min(2, line.half - 1):
            finish_tokens = hand_on(tokens_all, size, token_sems, tokens_sent, by_device)
    finish_cotangent = hand_on(cotangent_all, size, cotangent_sems, cotangent_sent, crossing)
    for swap in swaps[1:]:
        swap.wait_send()
    line.finish()
    finish_tokens()
    finish_cotangent()


def gather_first(before, small, after, tokens, cotangent, number):
    groups, share, _ = small.shape
    weights = [*before, *after]
    columns = LANES + sum(weight.shape[1] // groups for weight in weights)
    peers = lax.axis_size("blk")
    rows, width = tokens.shape
    whole = jax.ShapeDtypeStruct((groups * rows, width), bf16)
    vmem, anywhere = pl.BlockSpec(memory_space=pltpu.VMEM), pl.BlockSpec(memory_space=pl.ANY)
    all_pack, all_tokens, all_cotangent = pl.pallas_call(
        functools.partial(gather_first_kernel, len(before), len(after)),
        in_specs=[vmem] * (3 + len(weights)),
        out_specs=[anywhere] * 3,
        out_shape=[jax.ShapeDtypeStruct((peers, groups, share, columns), bf16), whole, whole],
        scratch_shapes=[
            pltpu.VMEM((groups, share, columns), bf16),
            pltpu.SemaphoreType.DMA((3,)),
            pltpu.SemaphoreType.DMA((3,)),
            pltpu.SemaphoreType.DMA,
        ]
        + [pltpu.SemaphoreType.DMA((4, peers // 2)) for _ in range(6)]
        + gather_sems()
        + gather_sems(),
        compiler_params=pltpu.CompilerParams(collective_id=number, has_side_effects=True),
        cost_estimate=pl.CostEstimate(
            flops=70_000_000_000, transcendentals=0, bytes_accessed=30_000_000
        ),
        name="gather_first",
    )(small, *weights, tokens, cotangent)
    return all_pack.reshape(peers * groups * share, columns), all_tokens, all_cotangent


class Sum:
    def __init__(self, part_ref, buffers, sems, size, by_device):
        self.part_ref, self.size, self.span = part_ref, size, size // PIECES
        self.slots = Slots(by_device)
        self.near_buf, self.turn_buf, self.far_buf = buffers
        self.near_send, self.near_recv, self.far_send, self.far_recv = sems
        self.near_copies, self.far_copies = [], []

    def piece(self, n):
        return slice(n * self.span, (n + 1) * self.span)

    def start(self):
        me, near, far, cross = partners()
        for which, shard in ((0, self.slots.cross), (1, self.slots.near)):
            for n in range(PIECES):
                copy = remote(
                    piece_at(self.part_ref, shard, n, self.size),
                    self.near_buf.at[which, pl.ds(n * self.span, self.span), :],
                    self.near_send.at[which, n],
                    self.near_recv.at[which, n],
                    on_head(near),
                )
                copy.start()
                self.near_copies.append(copy)

    def turn(self):
        me, near, far, cross = partners()
        for n in range(PIECES):
            here = self.piece(n)
            self.near_copies[n].wait_recv()
            self.turn_buf[here, :] = (
                piece_at(self.part_ref, self.slots.far, n, self.size)[...].astype(f32)
                + self.near_buf[0, here, :].astype(f32)
            ).astype(bf16)
            copy = remote(
                self.turn_buf.at[pl.ds(n * self.span, self.span), :],
                self.far_buf.at[pl.ds(n * self.span, self.span), :],
                self.far_send.at[n],
                self.far_recv.at[n],
                on_head(far),
            )
            copy.start()
            self.far_copies.append(copy)

    def total(self, n):
        self.near_copies[PIECES + n].wait_recv()
        self.far_copies[n].wait_recv()
        here = self.piece(n)
        return (
            piece_at(self.part_ref, self.slots.own, n, self.size)[...].astype(f32)
            + self.near_buf[1, here, :].astype(f32)
            + self.far_buf[here, :].astype(f32)
        )

    def finish(self):
        for copy in self.near_copies + self.far_copies:
            copy.wait_send()


def sum_buffers(size, width):
    return [
        pltpu.VMEM((2, size, width), bf16),
        pltpu.VMEM((size, width), bf16),
        pltpu.VMEM((size, width), bf16),
    ]


def sum_sems():
    return [
        pltpu.SemaphoreType.DMA((2, PIECES)),
        pltpu.SemaphoreType.DMA((2, PIECES)),
        pltpu.SemaphoreType.DMA((PIECES,)),
        pltpu.SemaphoreType.DMA((PIECES,)),
    ]


def exchange_kernel(local, extras, summed, weights, *refs):
    part_ref, extra_refs = refs[0], refs[1 : 1 + extras]
    refs = refs[1 + extras :]
    if weights:
        mine_ref, refs = refs[0], refs[1:]
    out_ref, all_ref, refs = refs[0], refs[1], refs[2:]
    if weights:
        weight_ref, refs = refs[0], refs[1:]
    payload, sems = refs[0], refs[1:]
    size = out_ref.shape[0]
    span = size // PIECES
    _, near, far, _ = partners()
    if weights:
        kinds = mine_ref.shape[0]
        line = Line(lambda kind, blk: weight_ref.at[blk, kind], kinds, sems[-7:-1])
        own = pltpu.make_async_copy(mine_ref, weight_ref.at[lax.axis_index("blk")], sems[-1])
        own.start()
        line.greet([on_head(near), on_head(far)])
    else:
        greet([on_head(near), on_head(far)])
    slots = Slots(summed)
    if not summed:
        shares = Sum(part_ref, sems[7:10], sems[10:14], size, True)
        shares.start()
    if weights:
        own.wait()
        for kind in range(kinds):
            line.launch(kind)
    if not summed:
        shares.turn()
    sent = []
    for piece in range(PIECES):
        if weights and piece != 2:
            hop = {0: 1, 1: 2, 3: 3}[piece]
            for t in range(hop, line.half if piece == 3 else min(hop + 1, line.half)):
                line.step(t)
        here = slice(piece * span, (piece + 1) * span)
        total = part_ref[here, :] if summed else shares.total(piece)
        result, share = local(total, here, *extra_refs)
        out_ref[here, :] = result.astype(out_ref.dtype)
        payload[here, :] = share.astype(bf16)
        source = payload.at[pl.ds(piece * span, span), :]
        sent.append(spread_piece(source, all_ref, size, sems[:7], piece, slots))
    hand_on(all_ref, size, sems[:7], sent, slots)()
    if not summed:
        shares.finish()
    if weights:
        line.finish()


def exchange(local, part, extras, summed, number, name, mine=None):
    rows, width = part.shape
    size = rows if summed else rows // 4
    vmem, anywhere = pl.BlockSpec(memory_space=pltpu.VMEM), pl.BlockSpec(memory_space=pl.ANY)
    weights = mine is not None
    inputs = [part, *extras]
    out_specs = [vmem, anywhere]
    out_shape = [
        jax.ShapeDtypeStruct((size, width), f32),
        jax.ShapeDtypeStruct((4 * size, width), bf16),
    ]
    scratch = [pltpu.VMEM((size, width), bf16)] + gather_sems()
    if not summed:
        scratch += sum_buffers(size, width) + sum_sems()
    if weights:
        peers = lax.axis_size("blk")
        inputs.append(mine)
        out_specs.append(anywhere)
        out_shape.append(jax.ShapeDtypeStruct((peers,) + mine.shape, bf16))
        scratch += [pltpu.SemaphoreType.DMA((mine.shape[0], peers // 2)) for _ in range(6)]
        scratch.append(pltpu.SemaphoreType.DMA)
    return pl.pallas_call(
        functools.partial(exchange_kernel, local, len(extras), summed, weights),
        in_specs=[vmem] * len(inputs),
        out_specs=out_specs,
        out_shape=out_shape,
        scratch_shapes=scratch,
        compiler_params=pltpu.CompilerParams(collective_id=number, has_side_effects=True),
        cost_estimate=pl.CostEstimate(
            flops=10_000_000_000 if summed else 70_000_000_000,
            transcendentals=0,
            bytes_accessed=16_000_000,
        ),
        name=name,
    )(*inputs)


def column_chunks(width):
    count = max(width // 512, 1)
    first = width - 512 * (count - 1)
    return [(0, first)] + [(first + 512 * n, 512) for n in range(count - 1)]


def finish_last_kernel(grads_ref, weight_ref, grad_ref, output_grad_ref, second_ref,
                       grad_middle_ref, tokens_ref, gain_ref, weights_ref, output_ref,
                       second_out_ref, tokens_grad_ref, first_ref, *refs):
    buffers = (refs[0:3], refs[3:6])
    first_buffers = refs[6:9]
    pair_send, pair_recv, line_send, line_recv, swap_send, swap_recv = refs[9:15]
    first_sems = refs[15:19]
    me, near, far, cross = partners()
    others = (near, far, cross)
    here, partner, after = blk_peers()
    steps = len(after)
    greet(
        [on_head(other) for other in others]
        + [on_blk(partner)]
        + [on_blk(peer) for peer in after[1:]]
    )
    size = tokens_grad_ref.shape[0]
    first = Sum(first_ref, first_buffers, first_sems, size, True)
    chunks = []
    for ref, out_ref, some in (
        (grad_ref, weights_ref, buffers[0]), (output_grad_ref, output_ref, buffers[1])
    ):
        for start, wide in column_chunks(ref.shape[3]):
            chunks.append((ref, out_ref, some, pl.ds(start, wide)))
    groups = grad_ref.shape[1]
    sent = []
    for c, (ref, _, (pair_buf, _, _), at) in enumerate(chunks):
        for t in list(range(1, steps)) + [0]:
            copy = remote(
                ref.at[after[t] + partner - here, :, :, at],
                pair_buf.at[t, :, :, at],
                pair_send.at[c, t],
                pair_recv.at[c, t],
                on_blk(partner),
            )
            copy.start()
            sent.append(copy)

    def swap(source_ref, out_ref, c):
        for kind, other in enumerate(others):
            copy = remote(
                source_ref.at[other], out_ref.at[me], swap_send.at[c, kind],
                swap_recv.at[c, kind], on_head(other),
            )
            copy.start()
            sent.append(copy)

    swap(second_ref, second_out_ref, len(chunks))

    def add_up(c):
        ref, out_ref, (pair_buf, line_buf, row_buf), at = chunks[c]
        block = pair_buf.at[0, :, :, at]
        remote(block, block, pair_send.at[c, 0], pair_recv.at[c, 0], on_blk(partner)).wait_recv()
        for t in range(1, steps):
            block = line_buf.at[t, :, :, at]
            remote(
                block, block, line_send.at[c, t], line_recv.at[c, t], on_blk(after[t])
            ).wait_recv()

        def add_all(group, carry):
            total = ref[here, group, :, at].astype(f32) + pair_buf[0, group, :, at].astype(f32)
            for t in range(1, steps):
                total = total + line_buf[t, group, :, at].astype(f32)
            row_buf[group, :, at] = total.astype(bf16)
            return carry

        lax.fori_loop(0, groups, add_all, 0)
        out_ref[me, :, at] = row_buf[me, :, at]
        swap(row_buf.at[:, :, at], out_ref.at[:, :, at], c)

    across = grads_ref.shape[1]
    tiles = first_ref.shape[0] // 256

    def multiply(n, carry):
        rows = tile_of(n, 256)
        first_ref[rows, :] = dot(grads_ref[rows, :], weight_ref[:, :across], NT).astype(bf16)
        return carry

    lax.fori_loop(0, tiles // 2, multiply, 0)
    for c, (ref, _, (pair_buf, line_buf, _), at) in enumerate(chunks):
        for t in range(1, steps):
            block = pair_buf.at[t, :, :, at]
            remote(
                block, block, pair_send.at[c, t], pair_recv.at[c, t], on_blk(partner)
            ).wait_recv()

            def add(group, carry):
                pair_buf[t, group, :, at] = (
                    ref[after[t], group, :, at].astype(f32)
                    + pair_buf[t, group, :, at].astype(f32)
                ).astype(bf16)
                return carry

            lax.fori_loop(0, groups, add, 0)
            copy = remote(
                block, line_buf.at[t, :, :, at], line_send.at[c, t], line_recv.at[c, t],
                on_blk(after[t]),
            )
            copy.start()
            sent.append(copy)
        if c == 0:
            lax.fori_loop(tiles // 2, tiles, multiply, 0)
            first.start()
        else:
            if c == 1:
                first.turn()
            add_up(c - 1)
    for piece in range(PIECES):
        rows = first.piece(piece)
        tokens_grad_ref[rows, :], _ = after_first(
            first.total(piece), rows, grad_middle_ref, tokens_ref, gain_ref
        )
    add_up(len(chunks) - 1)
    second_out_ref[me] = second_ref[me]
    for c in range(len(chunks) + 1):
        if c < len(chunks):
            _, out_ref, _, at = chunks[c]
            out_ref = out_ref.at[:, :, at]
        else:
            out_ref = second_out_ref
        for kind, other in enumerate(others):
            block = out_ref.at[other]
            remote(
                block, block, swap_send.at[c, kind], swap_recv.at[c, kind], on_head(other)
            ).wait_recv()
    for copy in sent:
        copy.wait_send()
    first.finish()


def finish_last(grads, first, grad, output_grad, second, groups, grad_middle, tokens, gain, number):
    peers = lax.axis_size("blk")
    share = grad.shape[0] // (peers * groups)
    rows, width = tokens.shape
    vmem = pl.BlockSpec(memory_space=pltpu.VMEM)
    half = peers // 2
    widths = (grad.shape[1], output_grad.shape[1])
    chunks = sum(len(column_chunks(width)) for width in widths)

    def blocks(columns):
        return [pltpu.VMEM((half, groups, share, columns), bf16) for _ in range(2)] + [
            pltpu.VMEM((groups, share, columns), bf16)
        ]

    return pl.pallas_call(
        finish_last_kernel,
        in_specs=[vmem] * 8,
        out_specs=[vmem] * 4,
        out_shape=[
            jax.ShapeDtypeStruct((groups, share, columns), bf16)
            for columns in widths + (second.shape[1],)
        ]
        + [jax.ShapeDtypeStruct((rows, width), f32)],
        scratch_shapes=[pltpu.VMEM((4 * rows, width), bf16)]
        + blocks(widths[0])
        + blocks(widths[1])
        + sum_buffers(rows, width)
        + [pltpu.SemaphoreType.DMA((chunks, half)) for _ in range(4)]
        + [pltpu.SemaphoreType.DMA((chunks + 1, 3)) for _ in range(2)]
        + sum_sems(),
        compiler_params=pltpu.CompilerParams(
            collective_id=number, has_side_effects=True, vmem_limit_bytes=60 << 20
        ),
        cost_estimate=pl.CostEstimate(
            flops=80_000_000_000, transcendentals=0, bytes_accessed=40_000_000
        ),
        name="finish_last",
    )(
        grads,
        first,
        grad.reshape(peers, groups, share, widths[0]),
        output_grad.reshape(peers, groups, share, widths[1]),
        second.reshape(groups, share, second.shape[1]),
        grad_middle, tokens, gain,
    )


def inverse_rms(value):
    return lax.rsqrt(jnp.mean(value * value, axis=1, keepdims=True) + epsilon)


def through_norm(grad, value):
    factor = inverse_rms(value)
    normed = value * factor
    return factor * (grad - normed * jnp.mean(grad * normed, axis=1, keepdims=True))


def after_attention(total, here, tokens_ref, gain_ref):
    middle = tokens_ref[here, :].astype(f32) + total
    return middle, middle * inverse_rms(middle) * gain_ref[0:1, :]


def after_hidden(total, here, cotangent_ref, middle_ref, gain_ref):
    grad = cotangent_ref[here, :].astype(f32) + through_norm(
        total * gain_ref[0:1, :], middle_ref[here, :]
    )
    return grad, grad


def after_first(total, here, grad_ref, tokens_ref, gain_ref):
    grad = grad_ref[here, :] + through_norm(
        total * gain_ref[0:1, :], tokens_ref[here, :].astype(f32)
    )
    return grad, None


FEED_TILE = 256
FEED_COLUMNS = 512


def feed_kernel(input_ref, cotangent_ref, weight_ref, down_weight_ref, down_ref, grad_ref, total_ref,
                acts, turned0, turned1, stage, near_buf, far_buf, near_send, near_recv, far_send, far_recv):
    step = pl.program_id(0)
    hidden_width = down_weight_ref.shape[1]
    size = total_ref.shape[0]
    per = size // FEED_TILE
    tiles = 4 * per
    _, near, far, _ = partners()

    @pl.when(step == 0)
    def _():
        greet([on_head(near), on_head(far)])

    def to_near(which, piece):
        return remote(
            stage.at[which * per + piece],
            near_buf.at[which, piece],
            near_send.at[which, piece],
            near_recv.at[which, piece],
            on_head(near),
        )

    def to_far(piece):
        return remote(
            near_buf.at[0, piece], far_buf.at[piece], far_send.at[piece], far_recv.at[piece],
            on_head(far),
        )

    @pl.when(step < tiles)
    def _():
        here = tile_of(step, FEED_TILE)
        inputs, cotangent = input_ref[...], cotangent_ref[...]
        turned0[:, here] = inputs.T
        turned1[:, here] = cotangent.T
        gate_at, up_at, down_at = (
            slice(n * hidden_width, (n + 1) * hidden_width) for n in range(3)
        )
        gate = dot(inputs, weight_ref[:, gate_at])
        up = dot(inputs, weight_ref[:, up_at])
        grad_hidden = dot(cotangent, down_weight_ref[...])
        opening = jax.nn.sigmoid(gate)
        active = gate * opening
        hidden = (active * up).astype(bf16)
        grad_gate = (grad_hidden * up * opening * (1.0 + gate * (1.0 - opening))).astype(bf16)
        grad_up = (grad_hidden * active).astype(bf16)
        acts[here, gate_at] = grad_gate
        acts[here, up_at] = grad_up
        acts[here, down_at] = hidden
        down_ref[...] = dot(hidden, down_weight_ref[...], NT).astype(bf16)
        back = dot(grad_gate, weight_ref[:, gate_at], NT) + dot(
            grad_up, weight_ref[:, up_at], NT
        )
        for piece in range(per):
            for which, first in ((0, 0), (1, 2 * per)):

                @pl.when(step == first + piece)
                def _():
                    stage[which * per + piece] = back.astype(bf16)
                    to_near(which, piece).start()

            @pl.when(step == per + piece)
            def _():
                to_near(0, piece).wait_recv()
                near_buf[0, piece] = (back + near_buf[0, piece].astype(f32)).astype(bf16)
                to_far(piece).start()

            @pl.when(step == 3 * per + piece)
            def _():
                total_ref[piece * FEED_TILE : (piece + 1) * FEED_TILE, :] = back

    @pl.when(step >= tiles)
    def _():
        at = tile_of(step - tiles, FEED_COLUMNS)
        from_input = (step - tiles) * FEED_COLUMNS < 2 * hidden_width

        @pl.when(from_input)
        def _():
            grad_ref[...] = dot(turned0[...], acts[:, at]).astype(bf16)

        @pl.when(jnp.logical_not(from_input))
        def _():
            grad_ref[...] = dot(turned1[...], acts[:, at]).astype(bf16)

    @pl.when(step == pl.num_programs(0) - 1)
    def _():
        for piece in range(per):
            here = slice(piece * FEED_TILE, (piece + 1) * FEED_TILE)
            to_near(1, piece).wait_recv()
            to_far(piece).wait_recv()
            total_ref[here, :] += near_buf[1, piece].astype(f32) + far_buf[piece].astype(f32)
            to_near(0, piece).wait_send()
            to_near(1, piece).wait_send()
            to_far(piece).wait_send()


def feed(inputs, cotangent, weight, down_weight, number):
    rows, width = inputs.shape
    columns = weight.shape[1] + down_weight.shape[1]
    size = rows // 4
    tiles, per = rows // FEED_TILE, size // FEED_TILE
    tile = pl.BlockSpec((FEED_TILE, width), lambda n: (jnp.minimum(n, tiles - 1), 0))

    def whole(shape):
        return pl.BlockSpec(shape, lambda n: (0, 0), pipeline_mode=pl.Buffered(1))

    return pl.pallas_call(
        feed_kernel,
        grid=(tiles + columns // FEED_COLUMNS,),
        in_specs=[tile, tile, whole(weight.shape), whole(down_weight.shape)],
        out_specs=[
            tile,
            pl.BlockSpec((width, FEED_COLUMNS), lambda n: (0, jnp.maximum(n - tiles, 0))),
            whole((size, width)),
        ],
        out_shape=[
            jax.ShapeDtypeStruct((rows, width), bf16),
            jax.ShapeDtypeStruct((width, columns), bf16),
            jax.ShapeDtypeStruct((size, width), f32),
        ],
        scratch_shapes=[
            pltpu.VMEM((rows, columns), bf16),
            pltpu.VMEM((width, rows), bf16),
            pltpu.VMEM((width, rows), bf16),
            pltpu.VMEM((2 * per, FEED_TILE, width), bf16),
            pltpu.VMEM((2, per, FEED_TILE, width), bf16),
            pltpu.VMEM((per, FEED_TILE, width), bf16),
            pltpu.SemaphoreType.DMA((2, per)),
            pltpu.SemaphoreType.DMA((2, per)),
            pltpu.SemaphoreType.DMA((per,)),
            pltpu.SemaphoreType.DMA((per,)),
        ],
        compiler_params=pltpu.CompilerParams(
            collective_id=number, has_side_effects=True, vmem_limit_bytes=63 << 20
        ),
        cost_estimate=pl.CostEstimate(
            flops=6 * rows * width * columns, transcendentals=rows * columns // 3,
            bytes_accessed=45_000_000,
        ),
        name="feed",
    )(inputs, cotangent, weight, down_weight)


def over_tokens(operand, other_side):
    return lax.dot_general(
        operand, other_side, (((0,), (0,)), ((), ())), preferred_element_type=f32
    )


def sent_columns(pieces, groups):
    packed = jnp.concatenate(
        [piece.reshape(piece.shape[0], groups, -1) for piece in pieces], axis=2
    )
    mine = lax.all_to_all(packed, "head", split_axis=1, concat_axis=0, tiled=True)
    return mine.reshape(mine.shape[0], mine.shape[2])


def all_rows(mine):
    return lax.all_gather(mine, "blk", axis=0, tiled=True)


def row_sums(grad):
    return lax.psum_scatter(grad, "blk", scatter_dimension=0, tiled=True)


def crossing_sum(part):
    cross, far, near, own = (piece.astype(f32) for piece in jnp.split(part, 4))
    members = range(lax.axis_size("head"))
    got = lax.ppermute(
        jnp.concatenate([cross, near]).astype(bf16), "head",
        [(n, n + 1 - 2 * (n % 2)) for n in members],
    )
    of_far, of_own = jnp.split(got.astype(f32), 2)
    back = lax.ppermute(
        (far + of_far).astype(bf16), "head", [(n, (n + 2) % 4) for n in members]
    )
    return own + of_own + back.astype(f32)


def body(
    tokens,
    segment,
    norm1_gain,
    w_query,
    w_key,
    w_value,
    w_gate_out,
    w_forget,
    forget_bias,
    w_output,
    norm2_gain,
    w_gate,
    w_up,
    w_down,
    cotangent,
):
    token_rows, model_width = tokens.shape
    groups = lax.axis_size("head")
    head_count = forget_bias.shape[0]
    local_heads = head_count // groups
    local_width = model_width // groups
    hidden_width = w_gate.shape[1] // groups
    rows = token_rows * groups
    share = w_query.shape[0]
    group = lax.axis_index("head")

    low = lambda array: array.astype(bf16)
    spread = lambda gain: jnp.broadcast_to(low(gain)[:, None, None], (share, groups, 1))
    forget_low = low(w_forget).reshape(share, groups, local_heads)
    rest = LANES - local_heads - 2
    small = jnp.concatenate(
        [forget_low, spread(norm1_gain), spread(norm2_gain), jnp.zeros((share, groups, rest), bf16)],
        axis=2,
    )
    first, tokens_all, cotangent_all = gather_first(
        (w_key, w_value), jnp.swapaxes(small, 0, 1), (w_query, w_gate_out, w_output), tokens,
        cotangent, 0,
    )
    kv_width = 2 * local_width + LANES
    output_weight = first[:, kv_width + 2 * local_width :]

    def gain_rows(column):
        gain = first[:, 2 * local_width + local_heads + column].astype(f32)
        return jnp.broadcast_to(gain[None, :], (8, model_width))

    gain1, gain2 = gain_rows(0), gain_rows(1)
    bias = lax.dynamic_slice_in_dim(forget_bias, group * local_heads, local_heads, 0)
    bias = jnp.broadcast_to(jnp.pad(bias, (0, LANES - local_heads))[None, :], (8, LANES))
    input1, key_value, terms, turned_terms, forget = project(
        tokens_all, gain1, first, bias, 2 * local_width, local_heads
    )
    earlier_kv = passed_along(key_value, "blk", 1)
    earlier_terms = passed_along(turned_terms, "blk", 1)
    query = dot(input1, first[:, kv_width : kv_width + local_width]).astype(bf16)
    gate_raw = dot(
        input1, first[:, kv_width + local_width : kv_width + 2 * local_width]
    )

    segment_plus = segment + 1
    earlier_segment = passed_along(segment_plus, "blk", 1)
    window = jnp.concatenate([earlier_segment, segment_plus])
    begins = jnp.sum(
        (window[:, None] < segment_plus[None, :]).astype(jnp.int32), axis=0
    )
    tiles = begins.reshape(rows // Q_TILE, Q_TILE)
    ranges = jnp.stack([tiles[:, 0] // K_TILE, (tiles[:, -1] + K_TILE - 1) // K_TILE])
    begins = jnp.broadcast_to(begins[None, :], (8, rows))

    so_far = attend(True, ranges, query, key_value, terms, terms, begins, local_heads)
    later = lax.optimization_barrier((w_gate, w_up, w_down, key_value))
    mine = sent_columns([low(weight) for weight in later[:3]], groups)
    mine, earlier_kv, earlier_terms, so_far, gate_raw = lax.optimization_barrier(
        (mine, earlier_kv, earlier_terms, so_far, gate_raw)
    )
    down_weight = all_rows(mine[:, 2 * hidden_width :])
    mine_second = mine[:, : 2 * hidden_width].reshape(groups, share, 2 * hidden_width)
    attended, lse = attend(
        False, ranges, query, earlier_kv, terms, earlier_terms, begins, local_heads, so_far
    )
    opened = jax.nn.sigmoid(gate_raw)
    attended_wide = attended.astype(f32)
    gated = (opened * attended_wide).astype(bf16)
    branch = dot(gated, output_weight, NT).astype(bf16)
    middle, input2, second = exchange(
        after_attention, branch, [tokens, gain2], False, 1, "exchange_middle", mine_second
    )
    second = second.reshape(model_width, 2 * hidden_width)
    down, second_grad, grad_input2 = feed(input2, cotangent_all, second, down_weight, 4)
    second_part = row_sums(second_grad)
    grad_middle, grad_branch = exchange(
        after_hidden, grad_input2, [cotangent, middle, gain2], True, 2, "exchange_hidden"
    )

    down, grad_branch = lax.optimization_barrier((down, grad_branch))
    result = (middle + crossing_sum(down)).astype(bf16)
    grad_gated = dot(grad_branch, output_weight)
    grad_attended = (grad_gated * opened).astype(bf16)
    grad_gate_pre = (grad_gated * attended_wide * opened * (1.0 - opened)).astype(bf16)
    dq_prev, rows_prev, dkv_prev, decay_prev = attend_back(
        False, ranges, query, earlier_kv, terms, earlier_terms, begins, grad_attended, attended,
        lse, local_heads,
    )
    dkv_later = passed_along(dkv_prev, "blk", -1)
    decay_later = passed_along(decay_prev[:, :8], "blk", -1)
    decay_later = jnp.pad(decay_later, ((0, 0), (0, LANES - 8)))
    dq, dk_own, dv_own, decay_own = attend_back(
        True, ranges, query, key_value, terms, terms, begins, grad_attended, attended,
        lse, local_heads, (dq_prev, rows_prev),
    )
    dk = (dk_own + dkv_later[0].astype(f32)).astype(bf16)
    dv = (dv_own + dkv_later[1].astype(f32)).astype(bf16)
    logf_grad = decay_back(decay_own, decay_later)
    forget_grad = jnp.where(
        jnp.arange(LANES)[None, :] < local_heads, logf_grad * jax.nn.sigmoid(-forget), 0.0
    ).astype(bf16)
    grads = jnp.concatenate([dk, dv, forget_grad, dq, grad_gate_pre], axis=1)
    first_grad = over_tokens(input1, grads)
    bias_part = jnp.sum(forget_grad.astype(f32), axis=0)
    row = jnp.arange(model_width)[:, None] % share
    column = jnp.arange(kv_width + 2 * local_width)[None, :]
    spread_bias = jnp.sum(
        jnp.where(row == jnp.arange(LANES)[None, :], bias_part[None, :], 0.0), axis=1, keepdims=True
    )
    first_grad = jnp.where(
        column == 2 * local_width + local_heads, spread_bias, first_grad
    ).astype(bf16)
    output_grad = over_tokens(grad_branch, gated).astype(bf16)
    first_sum, output_sum, second_sum, tokens_grad = finish_last(
        grads, first, first_grad, output_grad, second_part, groups, grad_middle, tokens, gain1, 3
    )
    first_sum, output_sum, second_sum = (
        jnp.swapaxes(array, 0, 1).astype(f32) for array in (first_sum, output_sum, second_sum)
    )

    def columns(array, start, width):
        return array[:, :, start : start + width].reshape(share, groups * width)

    key_sum, value_sum = (columns(first_sum, n * local_width, local_width) for n in range(2))
    forget_sum = columns(first_sum, 2 * local_width, local_heads)
    bias_total = first_sum[:local_heads, :, 2 * local_width + local_heads].T.reshape(head_count)
    query_sum, gate_out_sum = (
        columns(first_sum, kv_width + n * local_width, local_width) for n in range(2)
    )
    output_total = columns(output_sum, 0, local_width)
    gate_sum, up_sum, down_sum = (
        columns(second_sum, n * hidden_width, hidden_width) for n in range(3)
    )

    def along(weight, grad):
        return jnp.sum(low(weight).astype(f32) * grad, axis=1)

    gain1_total = (
        along(w_query, query_sum)
        + along(w_key, key_sum)
        + along(w_value, value_sum)
        + along(w_gate_out, gate_out_sum)
        + along(w_forget, forget_sum)
    ) / low(norm1_gain).astype(f32)
    gain2_total = (along(w_gate, gate_sum) + along(w_up, up_sum)) / low(norm2_gain).astype(f32)
    return (
        result,
        tokens_grad,
        gain1_total,
        query_sum,
        key_sum,
        value_sum,
        gate_out_sum,
        forget_sum,
        bias_total,
        output_total,
        gain2_total,
        gate_sum,
        up_sum,
        down_sum,
    )


def solution(mesh):
    both = ("blk", "head")
    matrix, vector = P(both, None), P(both)
    return jax.shard_map(
        body,
        mesh=mesh,
        in_specs=(
            matrix, P("blk"), vector, matrix, matrix, matrix, matrix, matrix, P(), matrix, vector,
            matrix, matrix, matrix, matrix,
        ),
        out_specs=(
            matrix, matrix, vector, matrix, matrix, matrix, matrix, matrix, P(), matrix, vector,
            matrix, matrix, matrix,
        ),
        check_vma=False,
    )
```

```python
import functools

import jax
import jax.numpy as jnp
from jax import lax
from jax.experimental import pallas as pl
from jax.experimental.pallas import tpu as pltpu
from jax.sharding import PartitionSpec as P

epsilon = 1e-06
LANES = 128
Q_TILE = 512
K_TILE = 512
FAR = -1e30
NT = (((1,), (1,)), ((), ()))
NN = (((1,), (0,)), ((), ()))
bf16 = jnp.bfloat16
f32 = jnp.float32


def dot(a, b, dims=NN, **kw):
    return lax.dot_general(a, b, dims, preferred_element_type=f32, **kw)


def passed_along(array, axis, by):
    peers = lax.axis_size(axis)
    pairs = [(i, i + by) for i in range(peers) if 0 <= i + by < peers]
    return lax.ppermute(array, axis, pairs)


def split3(value):
    high = value.astype(bf16)
    rest = value - high.astype(f32)
    mid = rest.astype(bf16)
    low = (rest - mid.astype(f32)).astype(bf16)
    return high, mid, low


def running(value_of, steps, rows, upper):
    place = lax.broadcasted_iota(jnp.int32, (rows, rows), 0)
    other = lax.broadcasted_iota(jnp.int32, (rows, rows), 1)
    tri = jnp.where((other >= place) if upper else (other <= place), 1.0, 0.0).astype(bf16)
    outs = [None] * steps
    carry = jnp.zeros((1, LANES), f32)
    order = range(steps - 1, -1, -1) if upper else range(steps)
    for n in order:
        block = value_of(n)
        total = sum(dot(tri, part) for part in split3(block)) + carry
        outs[n] = total
        carry = total[0:1] if upper else total[rows - 1 : rows]
    return outs, carry


PROJECT_TILE = 512
TERM_ROWS = 32


def project_kernel(local_heads, tokens_ref, gain_ref, weight_ref, bias_ref, input_ref, out_ref,
                   terms_ref, turned_ref, forget_ref, carry_ref):
    rows = tokens_ref.shape[0]
    wide = weight_ref.shape[1] - LANES

    @pl.when(pl.program_id(0) == 0)
    def _():
        carry_ref[...] = jnp.zeros_like(carry_ref)

    tokens = tokens_ref[...].astype(f32)
    input1 = (tokens * inverse_rms(tokens) * gain_ref[0:1, :]).astype(bf16)
    input_ref[...] = input1
    raw = dot(input1, weight_ref[...])
    out_ref[...] = raw[:, :wide].astype(bf16)
    forget = (raw[:, wide:] + bias_ref[0:1, :]).astype(bf16).astype(f32)
    forget_ref[...] = forget
    lane = lax.broadcasted_iota(jnp.int32, (rows, LANES), 1)
    logf = jnp.minimum(forget, 0.0) - jnp.log1p(jnp.exp(-jnp.abs(forget)))
    logf = jnp.where(lane < local_heads, logf, 0.0)
    place = lax.broadcasted_iota(jnp.int32, (rows, rows), 0)
    other = lax.broadcasted_iota(jnp.int32, (rows, rows), 1)
    tri = jnp.where(other <= place, 1.0, 0.0).astype(bf16)
    sums = sum(dot(tri, part) for part in split3(logf)) + carry_ref[0:1, :]
    carry_ref[0:1, :] = sums[rows - 1 : rows, :]
    high, mid, low = split3(sums)
    terms = (
        high.astype(f32)
        + pltpu.roll(mid.astype(f32), local_heads, 1)
        + pltpu.roll(low.astype(f32), 2 * local_heads, 1)
        + jnp.where(lane == 3 * local_heads, 1.0, 0.0)
    ).astype(bf16)
    terms_ref[...] = terms
    turned_ref[...] = terms.T[0:TERM_ROWS, :]


def project(tokens, gain, weight, bias, wide, local_heads):
    rows, width = tokens.shape

    def tile(columns):
        return pl.BlockSpec((PROJECT_TILE, columns), lambda n: (n, 0))

    def whole(*shape):
        return pl.BlockSpec(shape, lambda n: (0, 0))

    return pl.pallas_call(
        functools.partial(project_kernel, local_heads),
        grid=(rows // PROJECT_TILE,),
        in_specs=[tile(width), whole(8, width), whole(width, wide + LANES), whole(8, LANES)],
        out_specs=[
            tile(width),
            tile(wide),
            tile(LANES),
            pl.BlockSpec((TERM_ROWS, PROJECT_TILE), lambda n: (0, n)),
            tile(LANES),
        ],
        out_shape=[
            jax.ShapeDtypeStruct((rows, width), bf16),
            jax.ShapeDtypeStruct((rows, wide), bf16),
            jax.ShapeDtypeStruct((rows, LANES), bf16),
            jax.ShapeDtypeStruct((TERM_ROWS, rows), bf16),
            jax.ShapeDtypeStruct((rows, LANES), f32),
        ],
        scratch_shapes=[pltpu.VMEM((8, LANES), f32)],
        cost_estimate=pl.CostEstimate(
            flops=2 * rows * width * (wide + LANES), transcendentals=rows * LANES,
            bytes_accessed=20_000_000,
        ),
        name="project",
    )(tokens, gain, weight, bias)


def decay_back_kernel(own_ref, halo_ref, out_ref):
    rows = 256
    steps = own_ref.shape[0] // rows
    own, _ = running(lambda n: own_ref[n * rows : (n + 1) * rows, :], steps, rows, True)
    halo, _ = running(lambda n: halo_ref[n * rows : (n + 1) * rows, :], steps, rows, False)
    for n in range(steps):
        part = slice(n * rows, (n + 1) * rows)
        out_ref[part, :] = own[n] + (halo[n] - halo_ref[part, :])


def decay_back(own, halo):
    return pl.pallas_call(
        decay_back_kernel,
        out_shape=jax.ShapeDtypeStruct(own.shape, f32),
        name="decay_back",
    )(own, halo)


QUERY, KEY, TOTAL = range(3)


def placing(pair, local_heads, role):
    row = lax.broadcasted_iota(jnp.int32, (LANES, LANES), 0)
    col = lax.broadcasted_iota(jnp.int32, (LANES, LANES), 1)
    head = jnp.where(col < 64, 2 * pair + 1, 2 * pair)
    spot = jnp.where(col < 64, col, col - 64)
    term = spot - 3 * role
    is_term = (term >= 0) & (term < 3) & (row == term * local_heads + head)
    if role == QUERY:
        ones = (spot >= 3) & (spot < 9)
    else:
        ones = (spot < 3) & (role == KEY)
    is_one = ones & (row == 3 * local_heads)
    sign = -1.0 if role == KEY else 1.0
    return (jnp.where(is_term, sign, 0.0) + jnp.where(is_one, 1.0, 0.0)).astype(bf16)


def allowed_pairs(first_key, query_tile, rows, begin_row):
    shape = (K_TILE, Q_TILE)
    key_place = first_key + lax.broadcasted_iota(jnp.int32, shape, 0)
    query_place = rows + query_tile * Q_TILE + lax.broadcasted_iota(jnp.int32, shape, 1)
    return (key_place >= begin_row) & (key_place <= query_place)


def key_range(ranges_ref, query_tile, rows, own):
    count = rows // K_TILE
    base = count if own else 0
    first = jnp.clip(ranges_ref[0, query_tile] - base, 0, count)
    full = jnp.clip(ranges_ref[1, query_tile] - base, first, count)
    return first, full


def key_loops(ranges_ref, query_tile, rows, own, step, carry):
    first, full = key_range(ranges_ref, query_tile, rows, own)
    inside = query_tile * (Q_TILE // K_TILE) if own else rows // K_TILE
    full = jnp.minimum(full, inside)
    carry = lax.fori_loop(first, full, functools.partial(step, True), carry)
    carry = lax.fori_loop(full, inside, functools.partial(step, False), carry)
    if own:
        carry = lax.fori_loop(
            inside, inside + Q_TILE // K_TILE, functools.partial(step, True), carry
        )
    return carry


def tile_of(number, size):
    return pl.ds(pl.multiple_of(number * size, size), size)


def fill_keys(pair, local_heads, own, first, key_ref, terms_ref, keys):
    place = placing(pair, local_heads, KEY)
    lane = lax.broadcasted_iota(jnp.int32, (K_TILE, LANES), 1)
    rows = key_ref.shape[0]
    if not own:
        last = terms_ref[:, rows - LANES : rows].T
        total = dot(last, placing(pair, local_heads, TOTAL)[0:TERM_ROWS, :])[LANES - 1 : LANES, :]

    def fill(n, carry):
        here = tile_of(n, K_TILE)
        if own:
            extra = dot(terms_ref[here, :], place).astype(bf16)
        else:
            extra = dot(terms_ref[:, here].T, place[0:TERM_ROWS, :])
            extra = (extra + total).astype(bf16)
        key = key_ref[here, :]
        keys[0][here, :] = jnp.where(lane < 64, key, extra)
        keys[1][here, :] = jnp.where(lane < 64, extra, key)
        return carry

    lax.fori_loop(first, rows // K_TILE, fill, 0)


def query_tiles(q_ref, terms_ref, place, here, scaling):
    lane = lax.broadcasted_iota(jnp.int32, (Q_TILE, LANES), 1)
    extra = dot(terms_ref[here, :], place).astype(bf16)
    query = (q_ref[here, :].astype(f32) * scaling).astype(bf16)
    return jnp.where(lane < 64, query, extra), jnp.where(lane < 64, extra, query)


def attend_kernel(local_heads, own, ranges_ref, q_ref, k_ref, v_ref, t_query_ref, t_key_ref,
                  begin_ref, *refs):
    if own:
        acc_out_ref, state_out_ref, key0, key1, values, acc0, acc1 = refs
    else:
        acc_in_ref, state_in_ref, o_ref, lse_ref, key0, key1, values, acc0, acc1 = refs
    pair = pl.program_id(0)
    rows = q_ref.shape[0]
    base = rows if own else 0
    keys, accs = (key0, key1), (acc0, acc1)
    first, _ = key_range(ranges_ref, 0, rows, own)
    fill_keys(pair, local_heads, own, first, k_ref, t_key_ref, keys)

    def turn(n, carry):
        values[:, tile_of(n, K_TILE)] = v_ref[tile_of(n, K_TILE), :].T
        return carry

    lax.fori_loop(first, rows // K_TILE, turn, 0)
    place = placing(pair, local_heads, QUERY)

    def query_loop(tile, carry):
        here = tile_of(tile, Q_TILE)
        queries = query_tiles(q_ref, t_query_ref, place, here, 64**-0.5)
        begin_row = begin_ref[0:1, here]
        if own:
            low = jnp.full((1, Q_TILE), FAR, f32)
            zero = jnp.zeros((1, Q_TILE), f32)
            state = (low, zero, low, zero)
            for acc in accs:
                acc[...] = jnp.zeros_like(acc)
        else:
            state = tuple(state_in_ref[n : n + 1, here] for n in range(4))
            for h in range(2):
                accs[h][...] = acc_in_ref[64 * h : 64 * (h + 1), here]

        def step(masked, number, state):
            there = tile_of(number, K_TILE)
            fresh = []
            if masked:
                allowed = allowed_pairs(base + number * K_TILE, tile, rows, begin_row)
            for h in range(2):
                largest, total = state[2 * h], state[2 * h + 1]
                scores = dot(keys[h][there, :], queries[h], NT)
                if masked:
                    scores = jnp.where(allowed, scores, FAR)
                now = jnp.maximum(largest, jnp.max(scores, axis=0, keepdims=True))
                fade = jnp.exp(largest - now)
                weights = jnp.exp(scores - now)
                total = total * fade + jnp.sum(weights, axis=0, keepdims=True)
                accs[h][...] = accs[h][...] * fade + dot(
                    values[64 * h : 64 * (h + 1), there], weights.astype(bf16)
                )
                fresh += [now, total]
            return tuple(fresh)

        state = key_loops(ranges_ref, tile, rows, own, step, state)
        if own:
            for h in range(2):
                acc_out_ref[64 * h : 64 * (h + 1), here] = accs[h][...]
            for n in range(4):
                state_out_ref[n : n + 1, here] = state[n]
        else:
            mixed = jnp.concatenate(
                [accs[h][...] * (1.0 / state[2 * h + 1]) for h in range(2)], axis=0
            )
            o_ref[here, :] = mixed.T.astype(bf16)
            for h in range(2):
                lse_ref[h : h + 1, here] = state[2 * h] + jnp.log(state[2 * h + 1])
        return carry

    lax.fori_loop(0, rows // Q_TILE, query_loop, 0)


def lane_block(rows, offset):
    return pl.BlockSpec((rows, LANES), lambda p, *_: (0, offset + p))


def fixed(shape):
    return pl.BlockSpec(shape, lambda p, *_: (0, 0))


def pair_block(height, rows):
    return pl.BlockSpec((height, rows), lambda p, *_: (p, 0))


def attend(own, ranges, query, key_value, terms, key_terms, begins, local_heads, so_far=()):
    rows = query.shape[0]
    pairs = local_heads // 2
    running_specs = [pair_block(LANES, rows), pair_block(8, rows)]
    running_shape = (
        jax.ShapeDtypeStruct((LANES * pairs, rows), f32),
        jax.ShapeDtypeStruct((8 * pairs, rows), f32),
    )
    final_specs = [lane_block(rows, 0), pair_block(8, rows)]
    final_shape = (
        jax.ShapeDtypeStruct((rows, pairs * LANES), bf16),
        jax.ShapeDtypeStruct((8 * pairs, rows), f32),
    )
    return pl.pallas_call(
        functools.partial(attend_kernel, local_heads, own),
        grid_spec=pltpu.PrefetchScalarGridSpec(
            num_scalar_prefetch=1,
            grid=(pairs,),
            in_specs=[
                lane_block(rows, 0),
                lane_block(rows, 0),
                lane_block(rows, pairs),
                fixed((rows, LANES)),
                fixed((rows, LANES) if own else (TERM_ROWS, rows)),
                fixed((8, rows)),
            ]
            + ([] if own else running_specs),
            out_specs=running_specs if own else final_specs,
            scratch_shapes=[
                pltpu.VMEM((rows, LANES), bf16),
                pltpu.VMEM((rows, LANES), bf16),
                pltpu.VMEM((LANES, rows), bf16),
                pltpu.VMEM((64, Q_TILE), f32),
                pltpu.VMEM((64, Q_TILE), f32),
            ],
        ),
        out_shape=running_shape if own else final_shape,
        cost_estimate=pl.CostEstimate(
            flops=40_000_000_000 if own else 10_000_000_000,
            transcendentals=20_000_000,
            bytes_accessed=12_000_000,
        ),
        name="attend_own" if own else "attend_prev",
    )(ranges, query, key_value, key_value, terms, key_terms, begins, *so_far)


def attend_back_kernel(local_heads, own, ranges_ref, q_ref, k_ref, v_ref, t_query_ref, t_key_ref,
                       begin_ref, grad_ref, o_ref, lse_ref, *refs):
    if own:
        dq_in_ref, decay_in_ref, dq_ref, dk_ref, dv_ref, decay_ref = refs[:6]
    else:
        dq_ref, row_decay_ref, dkv_ref, decay_ref = refs[:4]
        dk_ref, dv_ref = dkv_ref.at[0], dkv_ref.at[1]
    key0, key1, key_t0, key_t1, dk0, dk1, dv, dq0, dq1 = refs[-9:]
    pair = pl.program_id(0)
    rows = q_ref.shape[0]
    base = rows if own else 0
    keys, keys_t, dks, dqs = (key0, key1), (key_t0, key_t1), (dk0, dk1), (dq0, dq1)
    first, _ = key_range(ranges_ref, 0, rows, own)
    fill_keys(pair, local_heads, own, first, k_ref, t_key_ref, keys)

    def turn(n, carry):
        here = tile_of(n, K_TILE)
        for h in range(2):
            keys_t[h][:, here] = keys[h][here, :].T
        return carry

    lax.fori_loop(first, rows // K_TILE, turn, 0)
    for ref in (dk0, dk1, dv):
        ref[...] = jnp.zeros_like(ref)
    place = placing(pair, local_heads, QUERY)
    lane = lax.broadcasted_iota(jnp.int32, (Q_TILE, LANES), 1)
    pick_row = lax.broadcasted_iota(jnp.int32, (8, LANES), 0)
    pick_lane = lax.broadcasted_iota(jnp.int32, (8, LANES), 1)
    pick = jnp.where((pick_lane // 64) == pick_row, 1.0, 0.0)
    sums_ref = decay_ref if own else row_decay_ref

    @pl.when(pair == 0)
    def _():
        if own:
            decay_ref[...] = decay_in_ref[...]
        else:
            decay_ref[...] = jnp.zeros_like(decay_ref)
            row_decay_ref[...] = jnp.zeros_like(row_decay_ref)

    def query_tile(tile):
        here = tile_of(tile, Q_TILE)
        queries = query_tiles(q_ref, t_query_ref, place, here, 64**-0.5)
        begin_row = begin_ref[0:1, here]
        grad = grad_ref[here, :]
        nothing = jnp.zeros_like(grad)
        grads = (jnp.where(lane < 64, grad, nothing), jnp.where(lane < 64, nothing, grad))
        product = grad.astype(f32) * o_ref[here, :].astype(f32)
        inner = dot(pick, product, NT, precision=lax.Precision.HIGHEST)
        for dq in dqs:
            dq[...] = jnp.zeros_like(dq)

        def step(masked, number, state):
            there = tile_of(number, K_TILE)
            if masked:
                allowed = allowed_pairs(base + number * K_TILE, tile, rows, begin_row)
            value = v_ref[there, :]
            value_part = 0.0
            for h in range(2):
                scores = dot(keys[h][there, :], queries[h], NT)
                prob = jnp.exp(scores - lse_ref[h : h + 1, here])
                if masked:
                    prob = jnp.where(allowed, prob, 0.0)
                grad_prob = dot(value, grads[h], NT)
                grad_score = (prob * (grad_prob - inner[h : h + 1, :])).astype(bf16)
                value_part = value_part + dot(prob.astype(bf16), grads[h])
                dks[h][there, :] += dot(grad_score, queries[h])
                dqs[h][...] += dot(keys_t[h][:, there], grad_score)
            dv[there, :] += value_part
            return state

        key_loops(ranges_ref, tile, rows, own, step, 0)
        turned = [dq[...].T for dq in dqs]
        dq_tile = jnp.where(lane < 64, turned[0], turned[1]) * 64**-0.5
        if own:
            dq_tile = dq_tile + dq_in_ref[here, :]
        dq_ref[here, :] = dq_tile.astype(dq_ref.dtype)
        sums = sums_ref[here, :]
        sums = sums + jnp.where(lane == 2 * pair, turned[0][:, 64:65], 0.0)
        sums = sums + jnp.where(lane == 2 * pair + 1, turned[1][:, 0:1], 0.0)
        sums_ref[here, :] = sums

    def query_loop(tile, carry):
        if own:
            query_tile(tile)
        else:
            reaches = key_range(ranges_ref, tile, rows, own)[0] < rows // K_TILE
            pl.when(reaches)(lambda: query_tile(tile))

            @pl.when(jnp.logical_not(reaches))
            def _():
                dq_ref[tile_of(tile, Q_TILE), :] = jnp.zeros((Q_TILE, LANES), dq_ref.dtype)

        return carry

    lax.fori_loop(0, rows // Q_TILE, query_loop, 0)
    sign = -1.0 if own else 1.0

    def finish(n, carry):
        here = tile_of(n, Q_TILE)
        left, right = dk0[here, :], dk1[here, :]
        dk_ref[here, :] = jnp.where(lane < 64, left, right).astype(dk_ref.dtype)
        dv_ref[here, :] = dv[here, :].astype(dv_ref.dtype)
        decay = decay_ref[here, :]
        decay = decay + jnp.where(lane == 2 * pair, sign * left[:, 67:68], 0.0)
        decay = decay + jnp.where(lane == 2 * pair + 1, sign * right[:, 3:4], 0.0)
        decay_ref[here, :] = decay
        return carry

    lax.fori_loop(0, rows // Q_TILE, finish, 0)


def attend_back(
    own, ranges, query, key_value, terms, key_terms, begins, grad, mixed, lse, local_heads,
    so_far=(),
):
    rows = query.shape[0]
    pairs = local_heads // 2
    wide = jax.ShapeDtypeStruct((rows, pairs * LANES), f32)
    sums = jax.ShapeDtypeStruct((rows, LANES), f32)
    if own:
        out_specs = [lane_block(rows, 0)] * 3 + [fixed((rows, LANES))]
        out_shape = (jax.ShapeDtypeStruct(wide.shape, bf16), wide, wide, sums)
    else:
        both = pl.BlockSpec((2, rows, LANES), lambda p, *_: (0, 0, p))
        out_specs = [lane_block(rows, 0), fixed((rows, LANES)), both, fixed((rows, LANES))]
        out_shape = (
            wide, sums, jax.ShapeDtypeStruct((2, rows, pairs * LANES), bf16), sums,
        )
    return pl.pallas_call(
        functools.partial(attend_back_kernel, local_heads, own),
        grid_spec=pltpu.PrefetchScalarGridSpec(
            num_scalar_prefetch=1,
            grid=(pairs,),
            in_specs=[
                lane_block(rows, 0),
                lane_block(rows, 0),
                lane_block(rows, pairs),
                fixed((rows, LANES)),
                fixed((rows, LANES) if own else (TERM_ROWS, rows)),
                fixed((8, rows)),
                lane_block(rows, 0),
                lane_block(rows, 0),
                pair_block(8, rows),
            ]
            + ([lane_block(rows, 0), fixed((rows, LANES))] if own else []),
            out_specs=out_specs,
            scratch_shapes=[
                pltpu.VMEM((rows, LANES), bf16),
                pltpu.VMEM((rows, LANES), bf16),
                pltpu.VMEM((LANES, rows), bf16),
                pltpu.VMEM((LANES, rows), bf16),
                pltpu.VMEM((rows, LANES), f32),
                pltpu.VMEM((rows, LANES), f32),
                pltpu.VMEM((rows, LANES), f32),
                pltpu.VMEM((LANES, Q_TILE), f32),
                pltpu.VMEM((LANES, Q_TILE), f32),
            ],
        ),
        out_shape=out_shape,
        cost_estimate=pl.CostEstimate(
            flops=20_000_000_000 if own else 10_000_000_000,
            transcendentals=20_000_000,
            bytes_accessed=25_000_000,
        ),
        name="attend_back_own" if own else "attend_back_prev",
    )(
        ranges, query, key_value, key_value, terms, key_terms, begins, grad, mixed, lse, *so_far
    )


PIECES = 4


def partners():
    me = lax.axis_index("head")
    near = me + 1 - 2 * (me % 2)
    far = (me + 2) % 4
    cross = (near + 2) % 4
    return me, near, far, cross


def signal(other):
    pl.semaphore_signal(
        pltpu.get_barrier_semaphore(), inc=1, device_id=other, device_id_type=pl.DeviceIdType.MESH
    )


def greet(others):
    for other in others:
        signal(other)
    pl.semaphore_wait(pltpu.get_barrier_semaphore(), len(others))


def remote(source, target, send, receive, other):
    return pltpu.make_async_remote_copy(
        src_ref=source,
        dst_ref=target,
        send_sem=send,
        recv_sem=receive,
        device_id=other,
        device_id_type=pl.DeviceIdType.MESH,
    )


def on_head(index):
    return {"head": index}


def on_blk(index):
    return {"blk": index}


def piece_at(ref, slot, piece, size):
    span = size // PIECES
    return ref.at[pl.ds(pl.multiple_of(slot * size + piece * span, span), span), :]


class Slots:
    def __init__(self, by_device):
        me, near, far, cross = partners()
        if by_device:
            self.own = self.sent_near = self.sent_far = me
            self.near, self.far, self.cross = near, far, cross
            self.passed = far
        else:
            self.own, self.sent_near, self.sent_far = 3, 2, 1
            self.near, self.far, self.cross = 2, 1, 0
            self.passed = 0


def spread_piece(source, all_ref, size, sems, piece, slots):
    me, near, far, _ = partners()
    far_send, far_recv, near_send, near_recv, _, _, own = sems
    copies = (
        remote(source, piece_at(all_ref, slots.sent_far, piece, size), far_send.at[piece],
               far_recv.at[piece], on_head(far)),
        remote(source, piece_at(all_ref, slots.sent_near, piece, size), near_send.at[piece],
               near_recv.at[piece], on_head(near)),
        pltpu.make_async_copy(source, piece_at(all_ref, slots.own, piece, size), own.at[piece]),
    )
    for copy in copies:
        copy.start()
    return copies


def hand_on(all_ref, size, sems, sent, slots):
    me, near, far, cross = partners()
    far_send, far_recv, near_send, near_recv, on_send, on_recv, own = sems
    passed = []
    for piece in range(PIECES):
        there = piece_at(all_ref, slots.far, piece, size)
        remote(there, there, far_send.at[piece], far_recv.at[piece], on_head(far)).wait_recv()
        copy = remote(
            there, piece_at(all_ref, slots.passed, piece, size), on_send.at[piece],
            on_recv.at[piece], on_head(near),
        )
        copy.start()
        passed.append(copy)

    def finish():
        for piece in range(PIECES):
            to_far, to_near, local = sent[piece]
            to_far.wait_send()
            to_near.wait_send()
            local.wait()
            passed[piece].wait_send()
            there = piece_at(all_ref, slots.near, piece, size)
            remote(there, there, near_send.at[piece], near_recv.at[piece], on_head(near)).wait_recv()
            there = piece_at(all_ref, slots.cross, piece, size)
            remote(there, there, on_send.at[piece], on_recv.at[piece], on_head(near)).wait_recv()

    return finish


def gather_sems():
    return [pltpu.SemaphoreType.DMA((PIECES,)) for _ in range(7)]


def blk_peers():
    here = lax.axis_index("blk")
    half = lax.axis_size("blk") // 2
    low, high = here % 2, here // 2
    partner = here + 1 - 2 * low
    after = [((high + t) % half) * 2 + low for t in range(half)]
    return here, partner, after


class Line:
    def __init__(self, block_of, kinds, sems):
        self.block_of, self.kinds = block_of, kinds
        self.pair_send, self.pair_recv, self.up_send, self.up_recv, self.down_send, self.down_recv = sems
        here = lax.axis_index("blk")
        self.half = lax.axis_size("blk") // 2
        self.low, self.high = here % 2, here // 2
        self.partner = here + 1 - 2 * self.low
        self.has_up, self.has_down = self.high < self.half - 1, self.high > 0

    def greet(self, others):
        greet_sum = len(others) + 1
        for other in others + [on_blk(self.partner)]:
            signal(other)
        pl.when(self.has_up)(lambda: signal(on_blk(self.at(self.high + 1))))
        pl.when(self.has_down)(lambda: signal(on_blk(self.at(self.high - 1))))
        ends = (self.high == 0).astype(jnp.int32) + (self.high == self.half - 1).astype(jnp.int32)
        pl.semaphore_wait(pltpu.get_barrier_semaphore(), greet_sum + 2 - ends)

    def at(self, high):
        return high * 2 + self.low

    def pair_copy(self, kind, high, low):
        block = self.block_of(kind, high * 2 + low)
        return remote(
            block, block, self.pair_send.at[kind, high], self.pair_recv.at[kind, high],
            on_blk(self.partner),
        )

    def up_copy(self, kind, high):
        block = self.block_of(kind, self.at(high))
        return remote(
            block, block, self.up_send.at[kind, high], self.up_recv.at[kind, high],
            on_blk(self.at(jnp.minimum(self.high + 1, self.half - 1))),
        )

    def down_copy(self, kind, high):
        block = self.block_of(kind, self.at(high))
        return remote(
            block, block, self.down_send.at[kind, high], self.down_recv.at[kind, high],
            on_blk(self.at(jnp.maximum(self.high - 1, 0))),
        )

    def launch(self, kind):
        self.pair_copy(kind, self.high, self.low).start()
        pl.when(self.has_up)(lambda: self.up_copy(kind, self.high).start())
        pl.when(self.has_down)(lambda: self.down_copy(kind, self.high).start())

    def step(self, t):
        for kind in range(self.kinds):
            below, above = self.high - t, self.high + t

            @pl.when(below >= 0)
            def _():
                self.up_copy(kind, below).wait_recv()
                self.pair_copy(kind, below, self.low).start()
                pl.when(self.has_up)(lambda: self.up_copy(kind, below).start())

            @pl.when(above < self.half)
            def _():
                self.down_copy(kind, above).wait_recv()
                self.pair_copy(kind, above, self.low).start()
                pl.when(self.has_down)(lambda: self.down_copy(kind, above).start())

    def finish(self):
        for kind in range(self.kinds):

            def wait(high, carry):
                self.pair_copy(kind, high, self.low).wait_send()
                self.pair_copy(kind, high, 1 - self.low).wait_recv()

                @pl.when((high <= self.high) & self.has_up)
                def _():
                    self.up_copy(kind, high).wait_send()

                @pl.when((high >= self.high) & self.has_down)
                def _():
                    self.down_copy(kind, high).wait_send()

                return carry

            lax.fori_loop(0, self.half, wait, 0)


def gather_first_kernel(before, after, *refs):
    small_ref, weight_refs = refs[0], refs[1 : 1 + before + after]
    tokens_ref, cotangent_ref, pack_all, tokens_all, cotangent_all, pack_ref = refs[
        1 + before + after : 7 + before + after
    ]
    sems = refs[7 + before + after :]
    groups = pack_ref.shape[0]
    start = 0
    for n, ref in enumerate(weight_refs):
        if n == before:
            pack_ref[:, :, start : start + LANES] = small_ref[...]
            start += LANES
        wide = ref.shape[1] // groups
        for group in range(groups):
            pack_ref[group, :, start : start + wide] = ref[
                :, group * wide : (group + 1) * wide
            ].astype(bf16)
        start += wide
    swap_send, swap_recv, swap_own = sems[:3]
    token_sems, cotangent_sems = sems[9:16], sems[16:23]
    me, near, far, cross = partners()
    sources = (me, near, far, cross)
    line = Line(lambda kind, blk: pack_all.at[blk, sources[kind]], 4, sems[3:9])
    here = lax.axis_index("blk")
    line.greet([on_head(near), on_head(far), on_head(cross)])
    swaps = [pltpu.make_async_copy(pack_ref.at[me], pack_all.at[here, me], swap_own)]
    for kind, other in enumerate((near, far, cross)):
        swaps.append(
            remote(
                pack_ref.at[other],
                pack_all.at[here, me],
                swap_send.at[kind],
                swap_recv.at[kind],
                on_head(other),
            )
        )
    for swap in swaps:
        swap.start()
    size = tokens_ref.shape[0]
    span = size // PIECES

    def spread_all(ref, all_ref, some, slots):
        return [
            spread_piece(ref.at[pl.ds(piece * span, span), :], all_ref, size, some, piece, slots)
            for piece in range(PIECES)
        ]

    by_device, crossing = Slots(True), Slots(False)
    tokens_sent = spread_all(tokens_ref, tokens_all, token_sems, by_device)
    swaps[0].wait()
    line.launch(0)
    for kind, source in enumerate((near, far, cross)):
        block = pack_all.at[here, source]
        remote(
            block, block, swap_send.at[kind], swap_recv.at[kind], on_head(source)
        ).wait_recv()
        line.launch(kind + 1)
    cotangent_sent = spread_all(cotangent_ref, cotangent_all, cotangent_sems, crossing)
    for t in range(1, line.half):
        line.step(t)
        if t == min(2, line.half - 1):
            finish_tokens = hand_on(tokens_all, size, token_sems, tokens_sent, by_device)
    finish_cotangent = hand_on(cotangent_all, size, cotangent_sems, cotangent_sent, crossing)
    for swap in swaps[1:]:
        swap.wait_send()
    line.finish()
    finish_tokens()
    finish_cotangent()


def gather_first(before, small, after, tokens, cotangent, number):
    groups, share, _ = small.shape
    weights = [*before, *after]
    columns = LANES + sum(weight.shape[1] // groups for weight in weights)
    peers = lax.axis_size("blk")
    rows, width = tokens.shape
    whole = jax.ShapeDtypeStruct((groups * rows, width), bf16)
    vmem, anywhere = pl.BlockSpec(memory_space=pltpu.VMEM), pl.BlockSpec(memory_space=pl.ANY)
    all_pack, all_tokens, all_cotangent = pl.pallas_call(
        functools.partial(gather_first_kernel, len(before), len(after)),
        in_specs=[vmem] * (3 + len(weights)),
        out_specs=[anywhere] * 3,
        out_shape=[jax.ShapeDtypeStruct((peers, groups, share, columns), bf16), whole, whole],
        scratch_shapes=[
            pltpu.VMEM((groups, share, columns), bf16),
            pltpu.SemaphoreType.DMA((3,)),
            pltpu.SemaphoreType.DMA((3,)),
            pltpu.SemaphoreType.DMA,
        ]
        + [pltpu.SemaphoreType.DMA((4, peers // 2)) for _ in range(6)]
        + gather_sems()
        + gather_sems(),
        compiler_params=pltpu.CompilerParams(collective_id=number, has_side_effects=True),
        cost_estimate=pl.CostEstimate(
            flops=70_000_000_000, transcendentals=0, bytes_accessed=30_000_000
        ),
        name="gather_first",
    )(small, *weights, tokens, cotangent)
    return all_pack.reshape(peers * groups * share, columns), all_tokens, all_cotangent


class Sum:
    def __init__(self, part_ref, buffers, sems, size, by_device):
        self.part_ref, self.size, self.span = part_ref, size, size // PIECES
        self.slots = Slots(by_device)
        self.near_buf, self.turn_buf, self.far_buf = buffers
        self.near_send, self.near_recv, self.far_send, self.far_recv = sems
        self.near_copies, self.far_copies = [], []

    def piece(self, n):
        return slice(n * self.span, (n + 1) * self.span)

    def start(self):
        me, near, far, cross = partners()
        for which, shard in ((0, self.slots.cross), (1, self.slots.near)):
            for n in range(PIECES):
                copy = remote(
                    piece_at(self.part_ref, shard, n, self.size),
                    self.near_buf.at[which, pl.ds(n * self.span, self.span), :],
                    self.near_send.at[which, n],
                    self.near_recv.at[which, n],
                    on_head(near),
                )
                copy.start()
                self.near_copies.append(copy)

    def turn(self):
        me, near, far, cross = partners()
        for n in range(PIECES):
            here = self.piece(n)
            self.near_copies[n].wait_recv()
            self.turn_buf[here, :] = (
                piece_at(self.part_ref, self.slots.far, n, self.size)[...].astype(f32)
                + self.near_buf[0, here, :].astype(f32)
            ).astype(bf16)
            copy = remote(
                self.turn_buf.at[pl.ds(n * self.span, self.span), :],
                self.far_buf.at[pl.ds(n * self.span, self.span), :],
                self.far_send.at[n],
                self.far_recv.at[n],
                on_head(far),
            )
            copy.start()
            self.far_copies.append(copy)

    def total(self, n):
        self.near_copies[PIECES + n].wait_recv()
        self.far_copies[n].wait_recv()
        here = self.piece(n)
        return (
            piece_at(self.part_ref, self.slots.own, n, self.size)[...].astype(f32)
            + self.near_buf[1, here, :].astype(f32)
            + self.far_buf[here, :].astype(f32)
        )

    def finish(self):
        for copy in self.near_copies + self.far_copies:
            copy.wait_send()


def sum_buffers(size, width):
    return [
        pltpu.VMEM((2, size, width), bf16),
        pltpu.VMEM((size, width), bf16),
        pltpu.VMEM((size, width), bf16),
    ]


def sum_sems():
    return [
        pltpu.SemaphoreType.DMA((2, PIECES)),
        pltpu.SemaphoreType.DMA((2, PIECES)),
        pltpu.SemaphoreType.DMA((PIECES,)),
        pltpu.SemaphoreType.DMA((PIECES,)),
    ]


def exchange_kernel(local, extras, summed, weights, *refs):
    part_ref, extra_refs = refs[0], refs[1 : 1 + extras]
    refs = refs[1 + extras :]
    if weights:
        mine_ref, refs = refs[0], refs[1:]
    out_ref, all_ref, refs = refs[0], refs[1], refs[2:]
    if weights:
        weight_ref, refs = refs[0], refs[1:]
    payload, sems = refs[0], refs[1:]
    size = out_ref.shape[0]
    span = size // PIECES
    _, near, far, _ = partners()
    if weights:
        kinds = mine_ref.shape[0]
        line = Line(lambda kind, blk: weight_ref.at[blk, kind], kinds, sems[-7:-1])
        own = pltpu.make_async_copy(mine_ref, weight_ref.at[lax.axis_index("blk")], sems[-1])
        own.start()
        line.greet([on_head(near), on_head(far)])
    else:
        greet([on_head(near), on_head(far)])
    slots = Slots(summed)
    if not summed:
        shares = Sum(part_ref, sems[7:10], sems[10:14], size, True)
        shares.start()
    if weights:
        own.wait()
        for kind in range(kinds):
            line.launch(kind)
    if not summed:
        shares.turn()
    sent = []
    for piece in range(PIECES):
        if weights and piece != 2:
            hop = {0: 1, 1: 2, 3: 3}[piece]
            for t in range(hop, line.half if piece == 3 else min(hop + 1, line.half)):
                line.step(t)
        here = slice(piece * span, (piece + 1) * span)
        total = part_ref[here, :] if summed else shares.total(piece)
        result, share = local(total, here, *extra_refs)
        out_ref[here, :] = result.astype(out_ref.dtype)
        payload[here, :] = share.astype(bf16)
        source = payload.at[pl.ds(piece * span, span), :]
        sent.append(spread_piece(source, all_ref, size, sems[:7], piece, slots))
    hand_on(all_ref, size, sems[:7], sent, slots)()
    if not summed:
        shares.finish()
    if weights:
        line.finish()


def exchange(local, part, extras, summed, number, name, mine=None):
    rows, width = part.shape
    size = rows if summed else rows // 4
    vmem, anywhere = pl.BlockSpec(memory_space=pltpu.VMEM), pl.BlockSpec(memory_space=pl.ANY)
    weights = mine is not None
    inputs = [part, *extras]
    out_specs = [vmem, anywhere]
    out_shape = [
        jax.ShapeDtypeStruct((size, width), f32),
        jax.ShapeDtypeStruct((4 * size, width), bf16),
    ]
    scratch = [pltpu.VMEM((size, width), bf16)] + gather_sems()
    if not summed:
        scratch += sum_buffers(size, width) + sum_sems()
    if weights:
        peers = lax.axis_size("blk")
        inputs.append(mine)
        out_specs.append(anywhere)
        out_shape.append(jax.ShapeDtypeStruct((peers,) + mine.shape, bf16))
        scratch += [pltpu.SemaphoreType.DMA((mine.shape[0], peers // 2)) for _ in range(6)]
        scratch.append(pltpu.SemaphoreType.DMA)
    return pl.pallas_call(
        functools.partial(exchange_kernel, local, len(extras), summed, weights),
        in_specs=[vmem] * len(inputs),
        out_specs=out_specs,
        out_shape=out_shape,
        scratch_shapes=scratch,
        compiler_params=pltpu.CompilerParams(collective_id=number, has_side_effects=True),
        cost_estimate=pl.CostEstimate(
            flops=10_000_000_000 if summed else 70_000_000_000,
            transcendentals=0,
            bytes_accessed=16_000_000,
        ),
        name=name,
    )(*inputs)


def column_chunks(width):
    count = max(width // 512, 1)
    first = width - 512 * (count - 1)
    return [(0, first)] + [(first + 512 * n, 512) for n in range(count - 1)]


def finish_last_kernel(grads_ref, weight_ref, grad_ref, output_grad_ref, second_ref,
                       grad_middle_ref, tokens_ref, gain_ref, weights_ref, output_ref,
                       second_out_ref, tokens_grad_ref, first_ref, *refs):
    buffers = (refs[0:3], refs[3:6])
    first_buffers = refs[6:9]
    pair_send, pair_recv, line_send, line_recv, swap_send, swap_recv = refs[9:15]
    first_sems = refs[15:19]
    me, near, far, cross = partners()
    others = (near, far, cross)
    here, partner, after = blk_peers()
    steps = len(after)
    greet(
        [on_head(other) for other in others]
        + [on_blk(partner)]
        + [on_blk(peer) for peer in after[1:]]
    )
    size = tokens_grad_ref.shape[0]
    first = Sum(first_ref, first_buffers, first_sems, size, True)
    chunks = []
    for ref, out_ref, some in (
        (grad_ref, weights_ref, buffers[0]), (output_grad_ref, output_ref, buffers[1])
    ):
        for start, wide in column_chunks(ref.shape[3]):
            chunks.append((ref, out_ref, some, pl.ds(start, wide)))
    groups = grad_ref.shape[1]
    sent = []
    for c, (ref, _, (pair_buf, _, _), at) in enumerate(chunks):
        for t in list(range(1, steps)) + [0]:
            copy = remote(
                ref.at[after[t] + partner - here, :, :, at],
                pair_buf.at[t, :, :, at],
                pair_send.at[c, t],
                pair_recv.at[c, t],
                on_blk(partner),
            )
            copy.start()
            sent.append(copy)

    def swap(source_ref, out_ref, c):
        for kind, other in enumerate(others):
            copy = remote(
                source_ref.at[other], out_ref.at[me], swap_send.at[c, kind],
                swap_recv.at[c, kind], on_head(other),
            )
            copy.start()
            sent.append(copy)

    swap(second_ref, second_out_ref, len(chunks))

    def add_up(c):
        ref, out_ref, (pair_buf, line_buf, row_buf), at = chunks[c]
        block = pair_buf.at[0, :, :, at]
        remote(block, block, pair_send.at[c, 0], pair_recv.at[c, 0], on_blk(partner)).wait_recv()
        for t in range(1, steps):
            block = line_buf.at[t, :, :, at]
            remote(
                block, block, line_send.at[c, t], line_recv.at[c, t], on_blk(after[t])
            ).wait_recv()

        def add_all(group, carry):
            total = ref[here, group, :, at].astype(f32) + pair_buf[0, group, :, at].astype(f32)
            for t in range(1, steps):
                total = total + line_buf[t, group, :, at].astype(f32)
            row_buf[group, :, at] = total.astype(bf16)
            return carry

        lax.fori_loop(0, groups, add_all, 0)
        out_ref[me, :, at] = row_buf[me, :, at]
        swap(row_buf.at[:, :, at], out_ref.at[:, :, at], c)

    across = grads_ref.shape[1]
    tiles = first_ref.shape[0] // 256

    def multiply(n, carry):
        rows = tile_of(n, 256)
        first_ref[rows, :] = dot(grads_ref[rows, :], weight_ref[:, :across], NT).astype(bf16)
        return carry

    lax.fori_loop(0, tiles // 2, multiply, 0)
    for c, (ref, _, (pair_buf, line_buf, _), at) in enumerate(chunks):
        for t in range(1, steps):
            block = pair_buf.at[t, :, :, at]
            remote(
                block, block, pair_send.at[c, t], pair_recv.at[c, t], on_blk(partner)
            ).wait_recv()

            def add(group, carry):
                pair_buf[t, group, :, at] = (
                    ref[after[t], group, :, at].astype(f32)
                    + pair_buf[t, group, :, at].astype(f32)
                ).astype(bf16)
                return carry

            lax.fori_loop(0, groups, add, 0)
            copy = remote(
                block, line_buf.at[t, :, :, at], line_send.at[c, t], line_recv.at[c, t],
                on_blk(after[t]),
            )
            copy.start()
            sent.append(copy)
        if c == 0:
            lax.fori_loop(tiles // 2, tiles, multiply, 0)
            first.start()
        else:
            if c == 1:
                first.turn()
            add_up(c - 1)
    for piece in range(PIECES):
        rows = first.piece(piece)
        tokens_grad_ref[rows, :], _ = after_first(
            first.total(piece), rows, grad_middle_ref, tokens_ref, gain_ref
        )
    add_up(len(chunks) - 1)
    second_out_ref[me] = second_ref[me]
    for c in range(len(chunks) + 1):
        if c < len(chunks):
            _, out_ref, _, at = chunks[c]
            out_ref = out_ref.at[:, :, at]
        else:
            out_ref = second_out_ref
        for kind, other in enumerate(others):
            block = out_ref.at[other]
            remote(
                block, block, swap_send.at[c, kind], swap_recv.at[c, kind], on_head(other)
            ).wait_recv()
    for copy in sent:
        copy.wait_send()
    first.finish()


def finish_last(grads, first, grad, output_grad, second, groups, grad_middle, tokens, gain, number):
    peers = lax.axis_size("blk")
    share = grad.shape[0] // (peers * groups)
    rows, width = tokens.shape
    vmem = pl.BlockSpec(memory_space=pltpu.VMEM)
    half = peers // 2
    widths = (grad.shape[1], output_grad.shape[1])
    chunks = sum(len(column_chunks(width)) for width in widths)

    def blocks(columns):
        return [pltpu.VMEM((half, groups, share, columns), bf16) for _ in range(2)] + [
            pltpu.VMEM((groups, share, columns), bf16)
        ]

    return pl.pallas_call(
        finish_last_kernel,
        in_specs=[vmem] * 8,
        out_specs=[vmem] * 4,
        out_shape=[
            jax.ShapeDtypeStruct((groups, share, columns), bf16)
            for columns in widths + (second.shape[1],)
        ]
        + [jax.ShapeDtypeStruct((rows, width), f32)],
        scratch_shapes=[pltpu.VMEM((4 * rows, width), bf16)]
        + blocks(widths[0])
        + blocks(widths[1])
        + sum_buffers(rows, width)
        + [pltpu.SemaphoreType.DMA((chunks, half)) for _ in range(4)]
        + [pltpu.SemaphoreType.DMA((chunks + 1, 3)) for _ in range(2)]
        + sum_sems(),
        compiler_params=pltpu.CompilerParams(
            collective_id=number, has_side_effects=True, vmem_limit_bytes=60 << 20
        ),
        cost_estimate=pl.CostEstimate(
            flops=80_000_000_000, transcendentals=0, bytes_accessed=40_000_000
        ),
        name="finish_last",
    )(
        grads,
        first,
        grad.reshape(peers, groups, share, widths[0]),
        output_grad.reshape(peers, groups, share, widths[1]),
        second.reshape(groups, share, second.shape[1]),
        grad_middle, tokens, gain,
    )


def inverse_rms(value):
    return lax.rsqrt(jnp.mean(value * value, axis=1, keepdims=True) + epsilon)


def through_norm(grad, value):
    factor = inverse_rms(value)
    normed = value * factor
    return factor * (grad - normed * jnp.mean(grad * normed, axis=1, keepdims=True))


def after_attention(total, here, tokens_ref, gain_ref):
    middle = tokens_ref[here, :].astype(f32) + total
    return middle, middle * inverse_rms(middle) * gain_ref[0:1, :]


def after_hidden(total, here, cotangent_ref, middle_ref, gain_ref):
    grad = cotangent_ref[here, :].astype(f32) + through_norm(
        total * gain_ref[0:1, :], middle_ref[here, :]
    )
    return grad, grad


def after_first(total, here, grad_ref, tokens_ref, gain_ref):
    grad = grad_ref[here, :] + through_norm(
        total * gain_ref[0:1, :], tokens_ref[here, :].astype(f32)
    )
    return grad, None


FEED_TILE = 256
FEED_COLUMNS = 1024


def feed_kernel(input_ref, cotangent_ref, weight_ref, down_weight_ref, down_ref, grad_ref, total_ref,
                acts, turned0, turned1, stage, near_buf, far_buf, near_send, near_recv, far_send, far_recv):
    step = pl.program_id(0)
    hidden_width = down_weight_ref.shape[1]
    size = total_ref.shape[0]
    per = size // FEED_TILE
    tiles = 4 * per
    _, near, far, _ = partners()

    @pl.when(step == 0)
    def _():
        greet([on_head(near), on_head(far)])

    def to_near(which, piece):
        return remote(
            stage.at[which * per + piece],
            near_buf.at[which, piece],
            near_send.at[which, piece],
            near_recv.at[which, piece],
            on_head(near),
        )

    def to_far(piece):
        return remote(
            near_buf.at[0, piece], far_buf.at[piece], far_send.at[piece], far_recv.at[piece],
            on_head(far),
        )

    @pl.when(step < tiles)
    def _():
        here = tile_of(step, FEED_TILE)
        inputs, cotangent = input_ref[...], cotangent_ref[...]
        turned0[:, here] = inputs.T
        turned1[:, here] = cotangent.T
        gate_at, up_at, down_at = (
            slice(n * hidden_width, (n + 1) * hidden_width) for n in range(3)
        )
        gate = dot(inputs, weight_ref[:, gate_at])
        up = dot(inputs, weight_ref[:, up_at])
        grad_hidden = dot(cotangent, down_weight_ref[...])
        opening = 0.5 * jnp.tanh(0.5 * gate) + 0.5
        active = gate * opening
        hidden = (active * up).astype(bf16)
        grad_gate = (grad_hidden * up * opening * (1.0 + gate * (1.0 - opening))).astype(bf16)
        grad_up = (grad_hidden * active).astype(bf16)
        acts[here, gate_at] = grad_gate
        acts[here, up_at] = grad_up
        acts[here, down_at] = hidden
        down_ref[...] = dot(hidden, down_weight_ref[...], NT).astype(bf16)
        back = dot(grad_gate, weight_ref[:, gate_at], NT) + dot(
            grad_up, weight_ref[:, up_at], NT
        )
        for piece in range(per):
            for which, first in ((0, 0), (1, 2 * per)):

                @pl.when(step == first + piece)
                def _():
                    stage[which * per + piece] = back.astype(bf16)
                    to_near(which, piece).start()

            @pl.when(step == per + piece)
            def _():
                to_near(0, piece).wait_recv()
                near_buf[0, piece] = (back + near_buf[0, piece].astype(f32)).astype(bf16)
                to_far(piece).start()

            @pl.when(step == 3 * per + piece)
            def _():
                total_ref[piece * FEED_TILE : (piece + 1) * FEED_TILE, :] = back

    @pl.when(step >= tiles)
    def _():
        at = tile_of(step - tiles, FEED_COLUMNS)
        from_input = (step - tiles) * FEED_COLUMNS < 2 * hidden_width

        @pl.when(from_input)
        def _():
            grad_ref[...] = dot(turned0[...], acts[:, at]).astype(bf16)

        @pl.when(jnp.logical_not(from_input))
        def _():
            grad_ref[...] = dot(turned1[...], acts[:, at]).astype(bf16)

    @pl.when(step == pl.num_programs(0) - 1)
    def _():
        for piece in range(per):
            here = slice(piece * FEED_TILE, (piece + 1) * FEED_TILE)
            to_near(1, piece).wait_recv()
            to_far(piece).wait_recv()
            total_ref[here, :] += near_buf[1, piece].astype(f32) + far_buf[piece].astype(f32)
            to_near(0, piece).wait_send()
            to_near(1, piece).wait_send()
            to_far(piece).wait_send()


def feed(inputs, cotangent, weight, down_weight, number):
    rows, width = inputs.shape
    columns = weight.shape[1] + down_weight.shape[1]
    size = rows // 4
    tiles, per = rows // FEED_TILE, size // FEED_TILE
    tile = pl.BlockSpec((FEED_TILE, width), lambda n: (jnp.minimum(n, tiles - 1), 0))

    def whole(shape):
        return pl.BlockSpec(shape, lambda n: (0, 0), pipeline_mode=pl.Buffered(1))

    return pl.pallas_call(
        feed_kernel,
        grid=(tiles + columns // FEED_COLUMNS,),
        in_specs=[tile, tile, whole(weight.shape), whole(down_weight.shape)],
        out_specs=[
            tile,
            pl.BlockSpec((width, FEED_COLUMNS), lambda n: (0, jnp.maximum(n - tiles, 0))),
            whole((size, width)),
        ],
        out_shape=[
            jax.ShapeDtypeStruct((rows, width), bf16),
            jax.ShapeDtypeStruct((width, columns), bf16),
            jax.ShapeDtypeStruct((size, width), f32),
        ],
        scratch_shapes=[
            pltpu.VMEM((rows, columns), bf16),
            pltpu.VMEM((width, rows), bf16),
            pltpu.VMEM((width, rows), bf16),
            pltpu.VMEM((2 * per, FEED_TILE, width), bf16),
            pltpu.VMEM((2, per, FEED_TILE, width), bf16),
            pltpu.VMEM((per, FEED_TILE, width), bf16),
            pltpu.SemaphoreType.DMA((2, per)),
            pltpu.SemaphoreType.DMA((2, per)),
            pltpu.SemaphoreType.DMA((per,)),
            pltpu.SemaphoreType.DMA((per,)),
        ],
        compiler_params=pltpu.CompilerParams(
            collective_id=number, has_side_effects=True, vmem_limit_bytes=63 << 20
        ),
        cost_estimate=pl.CostEstimate(
            flops=6 * rows * width * columns, transcendentals=rows * columns // 3,
            bytes_accessed=45_000_000,
        ),
        name="feed",
    )(inputs, cotangent, weight, down_weight)


def over_tokens(operand, other_side):
    return lax.dot_general(
        operand, other_side, (((0,), (0,)), ((), ())), preferred_element_type=f32
    )


def sent_columns(pieces, groups):
    packed = jnp.concatenate(
        [piece.reshape(piece.shape[0], groups, -1) for piece in pieces], axis=2
    )
    mine = lax.all_to_all(packed, "head", split_axis=1, concat_axis=0, tiled=True)
    return mine.reshape(mine.shape[0], mine.shape[2])


def all_rows(mine):
    return lax.all_gather(mine, "blk", axis=0, tiled=True)


def row_sums(grad):
    return lax.psum_scatter(grad, "blk", scatter_dimension=0, tiled=True)


def crossing_sum(part):
    cross, far, near, own = (piece.astype(f32) for piece in jnp.split(part, 4))
    members = range(lax.axis_size("head"))
    got = lax.ppermute(
        jnp.concatenate([cross, near]).astype(bf16), "head",
        [(n, n + 1 - 2 * (n % 2)) for n in members],
    )
    of_far, of_own = jnp.split(got.astype(f32), 2)
    back = lax.ppermute(
        (far + of_far).astype(bf16), "head", [(n, (n + 2) % 4) for n in members]
    )
    return own + of_own + back.astype(f32)


def body(
    tokens,
    segment,
    norm1_gain,
    w_query,
    w_key,
    w_value,
    w_gate_out,
    w_forget,
    forget_bias,
    w_output,
    norm2_gain,
    w_gate,
    w_up,
    w_down,
    cotangent,
):
    token_rows, model_width = tokens.shape
    groups = lax.axis_size("head")
    head_count = forget_bias.shape[0]
    local_heads = head_count // groups
    local_width = model_width // groups
    hidden_width = w_gate.shape[1] // groups
    rows = token_rows * groups
    share = w_query.shape[0]
    group = lax.axis_index("head")

    low = lambda array: array.astype(bf16)
    spread = lambda gain: jnp.broadcast_to(low(gain)[:, None, None], (share, groups, 1))
    forget_low = low(w_forget).reshape(share, groups, local_heads)
    rest = LANES - local_heads - 2
    small = jnp.concatenate(
        [forget_low, spread(norm1_gain), spread(norm2_gain), jnp.zeros((share, groups, rest), bf16)],
        axis=2,
    )
    first, tokens_all, cotangent_all = gather_first(
        (w_key, w_value), jnp.swapaxes(small, 0, 1), (w_query, w_gate_out, w_output), tokens,
        cotangent, 0,
    )
    kv_width = 2 * local_width + LANES
    output_weight = first[:, kv_width + 2 * local_width :]

    def gain_rows(column):
        gain = first[:, 2 * local_width + local_heads + column].astype(f32)
        return jnp.broadcast_to(gain[None, :], (8, model_width))

    gain1, gain2 = gain_rows(0), gain_rows(1)
    bias = lax.dynamic_slice_in_dim(forget_bias, group * local_heads, local_heads, 0)
    bias = jnp.broadcast_to(jnp.pad(bias, (0, LANES - local_heads))[None, :], (8, LANES))
    input1, key_value, terms, turned_terms, forget = project(
        tokens_all, gain1, first, bias, 2 * local_width, local_heads
    )
    earlier_kv = passed_along(key_value, "blk", 1)
    earlier_terms = passed_along(turned_terms, "blk", 1)
    query = dot(input1, first[:, kv_width : kv_width + local_width]).astype(bf16)
    gate_raw = dot(
        input1, first[:, kv_width + local_width : kv_width + 2 * local_width]
    )

    segment_plus = segment + 1
    earlier_segment = passed_along(segment_plus, "blk", 1)
    window = jnp.concatenate([earlier_segment, segment_plus])
    begins = jnp.sum(
        (window[:, None] < segment_plus[None, :]).astype(jnp.int32), axis=0
    )
    tiles = begins.reshape(rows // Q_TILE, Q_TILE)
    ranges = jnp.stack([tiles[:, 0] // K_TILE, (tiles[:, -1] + K_TILE - 1) // K_TILE])
    begins = jnp.broadcast_to(begins[None, :], (8, rows))

    so_far = attend(True, ranges, query, key_value, terms, terms, begins, local_heads)
    later = lax.optimization_barrier((w_gate, w_up, w_down, key_value))
    mine = sent_columns([low(weight) for weight in later[:3]], groups)
    mine, earlier_kv, earlier_terms, so_far, gate_raw = lax.optimization_barrier(
        (mine, earlier_kv, earlier_terms, so_far, gate_raw)
    )
    down_weight = all_rows(mine[:, 2 * hidden_width :])
    mine_second = mine[:, : 2 * hidden_width].reshape(groups, share, 2 * hidden_width)
    attended, lse = attend(
        False, ranges, query, earlier_kv, terms, earlier_terms, begins, local_heads, so_far
    )
    opened = jax.nn.sigmoid(gate_raw)
    attended_wide = attended.astype(f32)
    gated = (opened * attended_wide).astype(bf16)
    branch = dot(gated, output_weight, NT).astype(bf16)
    middle, input2, second = exchange(
        after_attention, branch, [tokens, gain2], False, 1, "exchange_middle", mine_second
    )
    second = second.reshape(model_width, 2 * hidden_width)
    down, second_grad, grad_input2 = feed(input2, cotangent_all, second, down_weight, 4)
    second_part = row_sums(second_grad)
    grad_middle, grad_branch = exchange(
        after_hidden, grad_input2, [cotangent, middle, gain2], True, 2, "exchange_hidden"
    )

    down, grad_branch = lax.optimization_barrier((down, grad_branch))
    result = (middle + crossing_sum(down)).astype(bf16)
    grad_gated = dot(grad_branch, output_weight)
    grad_attended = (grad_gated * opened).astype(bf16)
    grad_gate_pre = (grad_gated * attended_wide * opened * (1.0 - opened)).astype(bf16)
    dq_prev, rows_prev, dkv_prev, decay_prev = attend_back(
        False, ranges, query, earlier_kv, terms, earlier_terms, begins, grad_attended, attended,
        lse, local_heads,
    )
    dkv_later = passed_along(dkv_prev, "blk", -1)
    decay_later = passed_along(decay_prev[:, :8], "blk", -1)
    decay_later = jnp.pad(decay_later, ((0, 0), (0, LANES - 8)))
    dq, dk_own, dv_own, decay_own = attend_back(
        True, ranges, query, key_value, terms, terms, begins, grad_attended, attended,
        lse, local_heads, (dq_prev, rows_prev),
    )
    dk = (dk_own + dkv_later[0].astype(f32)).astype(bf16)
    dv = (dv_own + dkv_later[1].astype(f32)).astype(bf16)
    logf_grad = decay_back(decay_own, decay_later)
    forget_grad = jnp.where(
        jnp.arange(LANES)[None, :] < local_heads, logf_grad * jax.nn.sigmoid(-forget), 0.0
    ).astype(bf16)
    grads = jnp.concatenate([dk, dv, forget_grad, dq, grad_gate_pre], axis=1)
    first_grad = over_tokens(input1, grads)
    bias_part = jnp.sum(forget_grad.astype(f32), axis=0)
    row = jnp.arange(model_width)[:, None] % share
    column = jnp.arange(kv_width + 2 * local_width)[None, :]
    spread_bias = jnp.sum(
        jnp.where(row == jnp.arange(LANES)[None, :], bias_part[None, :], 0.0), axis=1, keepdims=True
    )
    first_grad = jnp.where(
        column == 2 * local_width + local_heads, spread_bias, first_grad
    ).astype(bf16)
    output_grad = over_tokens(grad_branch, gated).astype(bf16)
    first_sum, output_sum, second_sum, tokens_grad = finish_last(
        grads, first, first_grad, output_grad, second_part, groups, grad_middle, tokens, gain1, 3
    )
    first_sum, output_sum, second_sum = (
        jnp.swapaxes(array, 0, 1).astype(f32) for array in (first_sum, output_sum, second_sum)
    )

    def columns(array, start, width):
        return array[:, :, start : start + width].reshape(share, groups * width)

    key_sum, value_sum = (columns(first_sum, n * local_width, local_width) for n in range(2))
    forget_sum = columns(first_sum, 2 * local_width, local_heads)
    bias_total = first_sum[:local_heads, :, 2 * local_width + local_heads].T.reshape(head_count)
    query_sum, gate_out_sum = (
        columns(first_sum, kv_width + n * local_width, local_width) for n in range(2)
    )
    output_total = columns(output_sum, 0, local_width)
    gate_sum, up_sum, down_sum = (
        columns(second_sum, n * hidden_width, hidden_width) for n in range(3)
    )

    def along(weight, grad):
        return jnp.sum(low(weight).astype(f32) * grad, axis=1)

    gain1_total = (
        along(w_query, query_sum)
        + along(w_key, key_sum)
        + along(w_value, value_sum)
        + along(w_gate_out, gate_out_sum)
        + along(w_forget, forget_sum)
    ) / low(norm1_gain).astype(f32)
    gain2_total = (along(w_gate, gate_sum) + along(w_up, up_sum)) / low(norm2_gain).astype(f32)
    return (
        result,
        tokens_grad,
        gain1_total,
        query_sum,
        key_sum,
        value_sum,
        gate_out_sum,
        forget_sum,
        bias_total,
        output_total,
        gain2_total,
        gate_sum,
        up_sum,
        down_sum,
    )


def solution(mesh):
    both = ("blk", "head")
    matrix, vector = P(both, None), P(both)
    return jax.shard_map(
        body,
        mesh=mesh,
        in_specs=(
            matrix, P("blk"), vector, matrix, matrix, matrix, matrix, matrix, P(), matrix, vector,
            matrix, matrix, matrix, matrix,
        ),
        out_specs=(
            matrix, matrix, vector, matrix, matrix, matrix, matrix, matrix, P(), matrix, vector,
            matrix, matrix, matrix,
        ),
        check_vma=False,
    )
```

```python
import functools

import jax
import jax.numpy as jnp
from jax import lax
from jax.experimental import pallas as pl
from jax.experimental.pallas import tpu as pltpu
from jax.sharding import PartitionSpec as P

epsilon = 1e-06
LANES = 128
Q_TILE = 512
K_TILE = 512
FAR = -1e30
NT = (((1,), (1,)), ((), ()))
NN = (((1,), (0,)), ((), ()))
bf16 = jnp.bfloat16
f32 = jnp.float32


def dot(a, b, dims=NN, **kw):
    return lax.dot_general(a, b, dims, preferred_element_type=f32, **kw)


def passed_along(array, axis, by):
    peers = lax.axis_size(axis)
    pairs = [(i, i + by) for i in range(peers) if 0 <= i + by < peers]
    return lax.ppermute(array, axis, pairs)


def split3(value):
    high = value.astype(bf16)
    rest = value - high.astype(f32)
    mid = rest.astype(bf16)
    low = (rest - mid.astype(f32)).astype(bf16)
    return high, mid, low


def running(value_of, steps, rows, upper):
    place = lax.broadcasted_iota(jnp.int32, (rows, rows), 0)
    other = lax.broadcasted_iota(jnp.int32, (rows, rows), 1)
    tri = jnp.where((other >= place) if upper else (other <= place), 1.0, 0.0).astype(bf16)
    outs = [None] * steps
    carry = jnp.zeros((1, LANES), f32)
    order = range(steps - 1, -1, -1) if upper else range(steps)
    for n in order:
        block = value_of(n)
        total = sum(dot(tri, part) for part in split3(block)) + carry
        outs[n] = total
        carry = total[0:1] if upper else total[rows - 1 : rows]
    return outs, carry


PROJECT_TILE = 512
TERM_ROWS = 32


def project_kernel(local_heads, tokens_ref, gain_ref, weight_ref, bias_ref, input_ref, out_ref,
                   terms_ref, turned_ref, forget_ref, carry_ref):
    rows = tokens_ref.shape[0]
    wide = weight_ref.shape[1] - LANES

    @pl.when(pl.program_id(0) == 0)
    def _():
        carry_ref[...] = jnp.zeros_like(carry_ref)

    tokens = tokens_ref[...].astype(f32)
    input1 = (tokens * inverse_rms(tokens) * gain_ref[0:1, :]).astype(bf16)
    input_ref[...] = input1
    raw = dot(input1, weight_ref[...])
    out_ref[...] = raw[:, :wide].astype(bf16)
    forget = (raw[:, wide:] + bias_ref[0:1, :]).astype(bf16).astype(f32)
    forget_ref[...] = forget
    lane = lax.broadcasted_iota(jnp.int32, (rows, LANES), 1)
    logf = jnp.minimum(forget, 0.0) - jnp.log1p(jnp.exp(-jnp.abs(forget)))
    logf = jnp.where(lane < local_heads, logf, 0.0)
    place = lax.broadcasted_iota(jnp.int32, (rows, rows), 0)
    other = lax.broadcasted_iota(jnp.int32, (rows, rows), 1)
    tri = jnp.where(other <= place, 1.0, 0.0).astype(bf16)
    sums = sum(dot(tri, part) for part in split3(logf)) + carry_ref[0:1, :]
    carry_ref[0:1, :] = sums[rows - 1 : rows, :]
    high, mid, low = split3(sums)
    terms = (
        high.astype(f32)
        + pltpu.roll(mid.astype(f32), local_heads, 1)
        + pltpu.roll(low.astype(f32), 2 * local_heads, 1)
        + jnp.where(lane == 3 * local_heads, 1.0, 0.0)
    ).astype(bf16)
    terms_ref[...] = terms
    turned_ref[...] = terms.T[0:TERM_ROWS, :]


def project(tokens, gain, weight, bias, wide, local_heads):
    rows, width = tokens.shape

    def tile(columns):
        return pl.BlockSpec((PROJECT_TILE, columns), lambda n: (n, 0))

    def whole(*shape):
        return pl.BlockSpec(shape, lambda n: (0, 0))

    return pl.pallas_call(
        functools.partial(project_kernel, local_heads),
        grid=(rows // PROJECT_TILE,),
        in_specs=[tile(width), whole(8, width), whole(width, wide + LANES), whole(8, LANES)],
        out_specs=[
            tile(width),
            tile(wide),
            tile(LANES),
            pl.BlockSpec((TERM_ROWS, PROJECT_TILE), lambda n: (0, n)),
            tile(LANES),
        ],
        out_shape=[
            jax.ShapeDtypeStruct((rows, width), bf16),
            jax.ShapeDtypeStruct((rows, wide), bf16),
            jax.ShapeDtypeStruct((rows, LANES), bf16),
            jax.ShapeDtypeStruct((TERM_ROWS, rows), bf16),
            jax.ShapeDtypeStruct((rows, LANES), f32),
        ],
        scratch_shapes=[pltpu.VMEM((8, LANES), f32)],
        cost_estimate=pl.CostEstimate(
            flops=2 * rows * width * (wide + LANES), transcendentals=rows * LANES,
            bytes_accessed=20_000_000,
        ),
        name="project",
    )(tokens, gain, weight, bias)


def decay_back_kernel(own_ref, halo_ref, out_ref):
    rows = 256
    steps = own_ref.shape[0] // rows
    own, _ = running(lambda n: own_ref[n * rows : (n + 1) * rows, :], steps, rows, True)
    halo, _ = running(lambda n: halo_ref[n * rows : (n + 1) * rows, :], steps, rows, False)
    for n in range(steps):
        part = slice(n * rows, (n + 1) * rows)
        out_ref[part, :] = own[n] + (halo[n] - halo_ref[part, :])


def decay_back(own, halo):
    return pl.pallas_call(
        decay_back_kernel,
        out_shape=jax.ShapeDtypeStruct(own.shape, f32),
        name="decay_back",
    )(own, halo)


QUERY, KEY, TOTAL = range(3)


def placing(pair, local_heads, role):
    row = lax.broadcasted_iota(jnp.int32, (LANES, LANES), 0)
    col = lax.broadcasted_iota(jnp.int32, (LANES, LANES), 1)
    head = jnp.where(col < 64, 2 * pair + 1, 2 * pair)
    spot = jnp.where(col < 64, col, col - 64)
    term = spot - 3 * role
    is_term = (term >= 0) & (term < 3) & (row == term * local_heads + head)
    if role == QUERY:
        ones = (spot >= 3) & (spot < 9)
    else:
        ones = (spot < 3) & (role == KEY)
    is_one = ones & (row == 3 * local_heads)
    sign = -1.0 if role == KEY else 1.0
    return (jnp.where(is_term, sign, 0.0) + jnp.where(is_one, 1.0, 0.0)).astype(bf16)


def allowed_pairs(first_key, query_tile, rows, begin_row):
    shape = (K_TILE, Q_TILE)
    key_place = first_key + lax.broadcasted_iota(jnp.int32, shape, 0)
    query_place = rows + query_tile * Q_TILE + lax.broadcasted_iota(jnp.int32, shape, 1)
    return (key_place >= begin_row) & (key_place <= query_place)


def key_range(ranges_ref, query_tile, rows, own):
    count = rows // K_TILE
    base = count if own else 0
    first = jnp.clip(ranges_ref[0, query_tile] - base, 0, count)
    full = jnp.clip(ranges_ref[1, query_tile] - base, first, count)
    return first, full


def key_loops(ranges_ref, query_tile, rows, own, step, carry):
    first, full = key_range(ranges_ref, query_tile, rows, own)
    inside = query_tile * (Q_TILE // K_TILE) if own else rows // K_TILE
    full = jnp.minimum(full, inside)
    carry = lax.fori_loop(first, full, functools.partial(step, True), carry)
    carry = lax.fori_loop(full, inside, functools.partial(step, False), carry)
    if own:
        carry = lax.fori_loop(
            inside, inside + Q_TILE // K_TILE, functools.partial(step, True), carry
        )
    return carry


def tile_of(number, size):
    return pl.ds(pl.multiple_of(number * size, size), size)


def fill_keys(pair, local_heads, own, first, key_ref, terms_ref, keys):
    place = placing(pair, local_heads, KEY)
    lane = lax.broadcasted_iota(jnp.int32, (K_TILE, LANES), 1)
    rows = key_ref.shape[0]
    if not own:
        last = terms_ref[:, rows - LANES : rows].T
        total = dot(last, placing(pair, local_heads, TOTAL)[0:TERM_ROWS, :])[LANES - 1 : LANES, :]

    def fill(n, carry):
        here = tile_of(n, K_TILE)
        if own:
            extra = dot(terms_ref[here, :], place).astype(bf16)
        else:
            extra = dot(terms_ref[:, here].T, place[0:TERM_ROWS, :])
            extra = (extra + total).astype(bf16)
        key = key_ref[here, :]
        keys[0][here, :] = jnp.where(lane < 64, key, extra)
        keys[1][here, :] = jnp.where(lane < 64, extra, key)
        return carry

    lax.fori_loop(first, rows // K_TILE, fill, 0)


def query_tiles(q_ref, terms_ref, place, here, scaling):
    lane = lax.broadcasted_iota(jnp.int32, (Q_TILE, LANES), 1)
    extra = dot(terms_ref[here, :], place).astype(bf16)
    query = (q_ref[here, :].astype(f32) * scaling).astype(bf16)
    return jnp.where(lane < 64, query, extra), jnp.where(lane < 64, extra, query)


def attend_kernel(local_heads, own, ranges_ref, q_ref, k_ref, v_ref, t_query_ref, t_key_ref,
                  begin_ref, *refs):
    if own:
        acc_out_ref, state_out_ref, key0, key1, values, acc0, acc1 = refs
    else:
        acc_in_ref, state_in_ref, o_ref, lse_ref, key0, key1, values, acc0, acc1 = refs
    pair = pl.program_id(0)
    rows = q_ref.shape[0]
    base = rows if own else 0
    keys, accs = (key0, key1), (acc0, acc1)
    first, _ = key_range(ranges_ref, 0, rows, own)
    fill_keys(pair, local_heads, own, first, k_ref, t_key_ref, keys)

    def turn(n, carry):
        values[:, tile_of(n, K_TILE)] = v_ref[tile_of(n, K_TILE), :].T
        return carry

    lax.fori_loop(first, rows // K_TILE, turn, 0)
    place = placing(pair, local_heads, QUERY)

    def query_loop(tile, carry):
        here = tile_of(tile, Q_TILE)
        queries = query_tiles(q_ref, t_query_ref, place, here, 64**-0.5)
        begin_row = begin_ref[0:1, here]
        if own:
            low = jnp.full((1, Q_TILE), FAR, f32)
            zero = jnp.zeros((1, Q_TILE), f32)
            state = (low, zero, low, zero)
            for acc in accs:
                acc[...] = jnp.zeros_like(acc)
        else:
            state = tuple(state_in_ref[n : n + 1, here] for n in range(4))
            for h in range(2):
                accs[h][...] = acc_in_ref[64 * h : 64 * (h + 1), here]

        def step(masked, number, state):
            there = tile_of(number, K_TILE)
            fresh = []
            if masked:
                allowed = allowed_pairs(base + number * K_TILE, tile, rows, begin_row)
            for h in range(2):
                largest, total = state[2 * h], state[2 * h + 1]
                scores = dot(keys[h][there, :], queries[h], NT)
                if masked:
                    scores = jnp.where(allowed, scores, FAR)
                now = jnp.maximum(largest, jnp.max(scores, axis=0, keepdims=True))
                fade = jnp.exp(largest - now)
                weights = jnp.exp(scores - now)
                total = total * fade + jnp.sum(weights, axis=0, keepdims=True)
                accs[h][...] = accs[h][...] * fade + dot(
                    values[64 * h : 64 * (h + 1), there], weights.astype(bf16)
                )
                fresh += [now, total]
            return tuple(fresh)

        state = key_loops(ranges_ref, tile, rows, own, step, state)
        if own:
            for h in range(2):
                acc_out_ref[64 * h : 64 * (h + 1), here] = accs[h][...]
            for n in range(4):
                state_out_ref[n : n + 1, here] = state[n]
        else:
            mixed = jnp.concatenate(
                [accs[h][...] * (1.0 / state[2 * h + 1]) for h in range(2)], axis=0
            )
            o_ref[here, :] = mixed.T.astype(bf16)
            for h in range(2):
                lse_ref[h : h + 1, here] = state[2 * h] + jnp.log(state[2 * h + 1])
        return carry

    lax.fori_loop(0, rows // Q_TILE, query_loop, 0)


def lane_block(rows, offset):
    return pl.BlockSpec((rows, LANES), lambda p, *_: (0, offset + p))


def fixed(shape):
    return pl.BlockSpec(shape, lambda p, *_: (0, 0))


def pair_block(height, rows):
    return pl.BlockSpec((height, rows), lambda p, *_: (p, 0))


def attend(own, ranges, query, key_value, terms, key_terms, begins, local_heads, so_far=()):
    rows = query.shape[0]
    pairs = local_heads // 2
    running_specs = [pair_block(LANES, rows), pair_block(8, rows)]
    running_shape = (
        jax.ShapeDtypeStruct((LANES * pairs, rows), f32),
        jax.ShapeDtypeStruct((8 * pairs, rows), f32),
    )
    final_specs = [lane_block(rows, 0), pair_block(8, rows)]
    final_shape = (
        jax.ShapeDtypeStruct((rows, pairs * LANES), bf16),
        jax.ShapeDtypeStruct((8 * pairs, rows), f32),
    )
    return pl.pallas_call(
        functools.partial(attend_kernel, local_heads, own),
        grid_spec=pltpu.PrefetchScalarGridSpec(
            num_scalar_prefetch=1,
            grid=(pairs,),
            in_specs=[
                lane_block(rows, 0),
                lane_block(rows, 0),
                lane_block(rows, pairs),
                fixed((rows, LANES)),
                fixed((rows, LANES) if own else (TERM_ROWS, rows)),
                fixed((8, rows)),
            ]
            + ([] if own else running_specs),
            out_specs=running_specs if own else final_specs,
            scratch_shapes=[
                pltpu.VMEM((rows, LANES), bf16),
                pltpu.VMEM((rows, LANES), bf16),
                pltpu.VMEM((LANES, rows), bf16),
                pltpu.VMEM((64, Q_TILE), f32),
                pltpu.VMEM((64, Q_TILE), f32),
            ],
        ),
        out_shape=running_shape if own else final_shape,
        cost_estimate=pl.CostEstimate(
            flops=40_000_000_000 if own else 10_000_000_000,
            transcendentals=20_000_000,
            bytes_accessed=12_000_000,
        ),
        name="attend_own" if own else "attend_prev",
    )(ranges, query, key_value, key_value, terms, key_terms, begins, *so_far)


def attend_back_kernel(local_heads, own, ranges_ref, q_ref, k_ref, v_ref, t_query_ref, t_key_ref,
                       begin_ref, grad_ref, o_ref, lse_ref, *refs):
    if own:
        dq_in_ref, decay_in_ref, dq_ref, dk_ref, dv_ref, decay_ref = refs[:6]
    else:
        dq_ref, row_decay_ref, dkv_ref, decay_ref = refs[:4]
        dk_ref, dv_ref = dkv_ref.at[0], dkv_ref.at[1]
    key0, key1, key_t0, key_t1, dk0, dk1, dv, dq0, dq1 = refs[-9:]
    pair = pl.program_id(0)
    rows = q_ref.shape[0]
    base = rows if own else 0
    keys, keys_t, dks, dqs = (key0, key1), (key_t0, key_t1), (dk0, dk1), (dq0, dq1)
    first, _ = key_range(ranges_ref, 0, rows, own)
    fill_keys(pair, local_heads, own, first, k_ref, t_key_ref, keys)

    def turn(n, carry):
        here = tile_of(n, K_TILE)
        for h in range(2):
            keys_t[h][:, here] = keys[h][here, :].T
        return carry

    lax.fori_loop(first, rows // K_TILE, turn, 0)
    for ref in (dk0, dk1, dv):
        ref[...] = jnp.zeros_like(ref)
    place = placing(pair, local_heads, QUERY)
    lane = lax.broadcasted_iota(jnp.int32, (Q_TILE, LANES), 1)
    pick_row = lax.broadcasted_iota(jnp.int32, (8, LANES), 0)
    pick_lane = lax.broadcasted_iota(jnp.int32, (8, LANES), 1)
    pick = jnp.where((pick_lane // 64) == pick_row, 1.0, 0.0)
    sums_ref = decay_ref if own else row_decay_ref

    @pl.when(pair == 0)
    def _():
        if own:
            decay_ref[...] = decay_in_ref[...]
        else:
            decay_ref[...] = jnp.zeros_like(decay_ref)
            row_decay_ref[...] = jnp.zeros_like(row_decay_ref)

    def query_tile(tile):
        here = tile_of(tile, Q_TILE)
        queries = query_tiles(q_ref, t_query_ref, place, here, 64**-0.5)
        begin_row = begin_ref[0:1, here]
        grad = grad_ref[here, :]
        nothing = jnp.zeros_like(grad)
        grads = (jnp.where(lane < 64, grad, nothing), jnp.where(lane < 64, nothing, grad))
        product = grad.astype(f32) * o_ref[here, :].astype(f32)
        inner = dot(pick, product, NT, precision=lax.Precision.HIGHEST)
        for dq in dqs:
            dq[...] = jnp.zeros_like(dq)

        def step(masked, number, state):
            there = tile_of(number, K_TILE)
            if masked:
                allowed = allowed_pairs(base + number * K_TILE, tile, rows, begin_row)
            value = v_ref[there, :]
            value_part = 0.0
            for h in range(2):
                scores = dot(keys[h][there, :], queries[h], NT)
                prob = jnp.exp(scores - lse_ref[h : h + 1, here])
                if masked:
                    prob = jnp.where(allowed, prob, 0.0)
                grad_prob = dot(value, grads[h], NT)
                grad_score = (prob * (grad_prob - inner[h : h + 1, :])).astype(bf16)
                value_part = value_part + dot(prob.astype(bf16), grads[h])
                dks[h][there, :] += dot(grad_score, queries[h])
                dqs[h][...] += dot(keys_t[h][:, there], grad_score)
            dv[there, :] += value_part
            return state

        key_loops(ranges_ref, tile, rows, own, step, 0)
        turned = [dq[...].T for dq in dqs]
        dq_tile = jnp.where(lane < 64, turned[0], turned[1]) * 64**-0.5
        if own:
            dq_tile = dq_tile + dq_in_ref[here, :]
        dq_ref[here, :] = dq_tile.astype(dq_ref.dtype)
        sums = sums_ref[here, :]
        sums = sums + jnp.where(lane == 2 * pair, turned[0][:, 64:65], 0.0)
        sums = sums + jnp.where(lane == 2 * pair + 1, turned[1][:, 0:1], 0.0)
        sums_ref[here, :] = sums

    def query_loop(tile, carry):
        if own:
            query_tile(tile)
        else:
            reaches = key_range(ranges_ref, tile, rows, own)[0] < rows // K_TILE
            pl.when(reaches)(lambda: query_tile(tile))

            @pl.when(jnp.logical_not(reaches))
            def _():
                dq_ref[tile_of(tile, Q_TILE), :] = jnp.zeros((Q_TILE, LANES), dq_ref.dtype)

        return carry

    lax.fori_loop(0, rows // Q_TILE, query_loop, 0)
    sign = -1.0 if own else 1.0

    def finish(n, carry):
        here = tile_of(n, Q_TILE)
        left, right = dk0[here, :], dk1[here, :]
        dk_ref[here, :] = jnp.where(lane < 64, left, right).astype(dk_ref.dtype)
        dv_ref[here, :] = dv[here, :].astype(dv_ref.dtype)
        decay = decay_ref[here, :]
        decay = decay + jnp.where(lane == 2 * pair, sign * left[:, 67:68], 0.0)
        decay = decay + jnp.where(lane == 2 * pair + 1, sign * right[:, 3:4], 0.0)
        decay_ref[here, :] = decay
        return carry

    lax.fori_loop(0, rows // Q_TILE, finish, 0)


def attend_back(
    own, ranges, query, key_value, terms, key_terms, begins, grad, mixed, lse, local_heads,
    so_far=(),
):
    rows = query.shape[0]
    pairs = local_heads // 2
    wide = jax.ShapeDtypeStruct((rows, pairs * LANES), f32)
    sums = jax.ShapeDtypeStruct((rows, LANES), f32)
    if own:
        out_specs = [lane_block(rows, 0)] * 3 + [fixed((rows, LANES))]
        out_shape = (jax.ShapeDtypeStruct(wide.shape, bf16), wide, wide, sums)
    else:
        both = pl.BlockSpec((2, rows, LANES), lambda p, *_: (0, 0, p))
        out_specs = [lane_block(rows, 0), fixed((rows, LANES)), both, fixed((rows, LANES))]
        out_shape = (
            wide, sums, jax.ShapeDtypeStruct((2, rows, pairs * LANES), bf16), sums,
        )
    return pl.pallas_call(
        functools.partial(attend_back_kernel, local_heads, own),
        grid_spec=pltpu.PrefetchScalarGridSpec(
            num_scalar_prefetch=1,
            grid=(pairs,),
            in_specs=[
                lane_block(rows, 0),
                lane_block(rows, 0),
                lane_block(rows, pairs),
                fixed((rows, LANES)),
                fixed((rows, LANES) if own else (TERM_ROWS, rows)),
                fixed((8, rows)),
                lane_block(rows, 0),
                lane_block(rows, 0),
                pair_block(8, rows),
            ]
            + ([lane_block(rows, 0), fixed((rows, LANES))] if own else []),
            out_specs=out_specs,
            scratch_shapes=[
                pltpu.VMEM((rows, LANES), bf16),
                pltpu.VMEM((rows, LANES), bf16),
                pltpu.VMEM((LANES, rows), bf16),
                pltpu.VMEM((LANES, rows), bf16),
                pltpu.VMEM((rows, LANES), f32),
                pltpu.VMEM((rows, LANES), f32),
                pltpu.VMEM((rows, LANES), f32),
                pltpu.VMEM((LANES, Q_TILE), f32),
                pltpu.VMEM((LANES, Q_TILE), f32),
            ],
        ),
        out_shape=out_shape,
        cost_estimate=pl.CostEstimate(
            flops=20_000_000_000 if own else 10_000_000_000,
            transcendentals=20_000_000,
            bytes_accessed=25_000_000,
        ),
        name="attend_back_own" if own else "attend_back_prev",
    )(
        ranges, query, key_value, key_value, terms, key_terms, begins, grad, mixed, lse, *so_far
    )


PIECES = 4


def partners():
    me = lax.axis_index("head")
    near = me + 1 - 2 * (me % 2)
    far = (me + 2) % 4
    cross = (near + 2) % 4
    return me, near, far, cross


def signal(other):
    pl.semaphore_signal(
        pltpu.get_barrier_semaphore(), inc=1, device_id=other, device_id_type=pl.DeviceIdType.MESH
    )


def greet(others):
    for other in others:
        signal(other)
    pl.semaphore_wait(pltpu.get_barrier_semaphore(), len(others))


def remote(source, target, send, receive, other):
    return pltpu.make_async_remote_copy(
        src_ref=source,
        dst_ref=target,
        send_sem=send,
        recv_sem=receive,
        device_id=other,
        device_id_type=pl.DeviceIdType.MESH,
    )


def on_head(index):
    return {"head": index}


def on_blk(index):
    return {"blk": index}


def piece_at(ref, slot, piece, size):
    span = size // PIECES
    return ref.at[pl.ds(pl.multiple_of(slot * size + piece * span, span), span), :]


class Slots:
    def __init__(self, by_device):
        me, near, far, cross = partners()
        if by_device:
            self.own = self.sent_near = self.sent_far = me
            self.near, self.far, self.cross = near, far, cross
            self.passed = far
        else:
            self.own, self.sent_near, self.sent_far = 3, 2, 1
            self.near, self.far, self.cross = 2, 1, 0
            self.passed = 0


def spread_piece(source, all_ref, size, sems, piece, slots):
    me, near, far, _ = partners()
    far_send, far_recv, near_send, near_recv, _, _, own = sems
    copies = (
        remote(source, piece_at(all_ref, slots.sent_far, piece, size), far_send.at[piece],
               far_recv.at[piece], on_head(far)),
        remote(source, piece_at(all_ref, slots.sent_near, piece, size), near_send.at[piece],
               near_recv.at[piece], on_head(near)),
        pltpu.make_async_copy(source, piece_at(all_ref, slots.own, piece, size), own.at[piece]),
    )
    for copy in copies:
        copy.start()
    return copies


def hand_on(all_ref, size, sems, sent, slots):
    me, near, far, cross = partners()
    far_send, far_recv, near_send, near_recv, on_send, on_recv, own = sems
    passed = []
    for piece in range(PIECES):
        there = piece_at(all_ref, slots.far, piece, size)
        remote(there, there, far_send.at[piece], far_recv.at[piece], on_head(far)).wait_recv()
        copy = remote(
            there, piece_at(all_ref, slots.passed, piece, size), on_send.at[piece],
            on_recv.at[piece], on_head(near),
        )
        copy.start()
        passed.append(copy)

    def finish():
        for piece in range(PIECES):
            to_far, to_near, local = sent[piece]
            to_far.wait_send()
            to_near.wait_send()
            local.wait()
            passed[piece].wait_send()
            there = piece_at(all_ref, slots.near, piece, size)
            remote(there, there, near_send.at[piece], near_recv.at[piece], on_head(near)).wait_recv()
            there = piece_at(all_ref, slots.cross, piece, size)
            remote(there, there, on_send.at[piece], on_recv.at[piece], on_head(near)).wait_recv()

    return finish


def gather_sems():
    return [pltpu.SemaphoreType.DMA((PIECES,)) for _ in range(7)]


def blk_peers():
    here = lax.axis_index("blk")
    half = lax.axis_size("blk") // 2
    low, high = here % 2, here // 2
    partner = here + 1 - 2 * low
    after = [((high + t) % half) * 2 + low for t in range(half)]
    return here, partner, after


class Line:
    def __init__(self, block_of, kinds, sems):
        self.block_of, self.kinds = block_of, kinds
        self.pair_send, self.pair_recv, self.up_send, self.up_recv, self.down_send, self.down_recv = sems
        here = lax.axis_index("blk")
        self.half = lax.axis_size("blk") // 2
        self.low, self.high = here % 2, here // 2
        self.partner = here + 1 - 2 * self.low
        self.has_up, self.has_down = self.high < self.half - 1, self.high > 0

    def greet(self, others):
        greet_sum = len(others) + 1
        for other in others + [on_blk(self.partner)]:
            signal(other)
        pl.when(self.has_up)(lambda: signal(on_blk(self.at(self.high + 1))))
        pl.when(self.has_down)(lambda: signal(on_blk(self.at(self.high - 1))))
        ends = (self.high == 0).astype(jnp.int32) + (self.high == self.half - 1).astype(jnp.int32)
        pl.semaphore_wait(pltpu.get_barrier_semaphore(), greet_sum + 2 - ends)

    def at(self, high):
        return high * 2 + self.low

    def pair_copy(self, kind, high, low):
        block = self.block_of(kind, high * 2 + low)
        return remote(
            block, block, self.pair_send.at[kind, high], self.pair_recv.at[kind, high],
            on_blk(self.partner),
        )

    def up_copy(self, kind, high):
        block = self.block_of(kind, self.at(high))
        return remote(
            block, block, self.up_send.at[kind, high], self.up_recv.at[kind, high],
            on_blk(self.at(jnp.minimum(self.high + 1, self.half - 1))),
        )

    def down_copy(self, kind, high):
        block = self.block_of(kind, self.at(high))
        return remote(
            block, block, self.down_send.at[kind, high], self.down_recv.at[kind, high],
            on_blk(self.at(jnp.maximum(self.high - 1, 0))),
        )

    def launch(self, kind):
        self.pair_copy(kind, self.high, self.low).start()
        pl.when(self.has_up)(lambda: self.up_copy(kind, self.high).start())
        pl.when(self.has_down)(lambda: self.down_copy(kind, self.high).start())

    def step(self, t):
        for kind in range(self.kinds):
            below, above = self.high - t, self.high + t

            @pl.when(below >= 0)
            def _():
                self.up_copy(kind, below).wait_recv()
                self.pair_copy(kind, below, self.low).start()
                pl.when(self.has_up)(lambda: self.up_copy(kind, below).start())

            @pl.when(above < self.half)
            def _():
                self.down_copy(kind, above).wait_recv()
                self.pair_copy(kind, above, self.low).start()
                pl.when(self.has_down)(lambda: self.down_copy(kind, above).start())

    def finish(self):
        for kind in range(self.kinds):

            def wait(high, carry):
                self.pair_copy(kind, high, self.low).wait_send()
                self.pair_copy(kind, high, 1 - self.low).wait_recv()

                @pl.when((high <= self.high) & self.has_up)
                def _():
                    self.up_copy(kind, high).wait_send()

                @pl.when((high >= self.high) & self.has_down)
                def _():
                    self.down_copy(kind, high).wait_send()

                return carry

            lax.fori_loop(0, self.half, wait, 0)


def gather_first_kernel(before, after, *refs):
    small_ref, weight_refs = refs[0], refs[1 : 1 + before + after]
    tokens_ref, cotangent_ref, pack_all, tokens_all, cotangent_all, pack_ref = refs[
        1 + before + after : 7 + before + after
    ]
    sems = refs[7 + before + after :]
    groups = pack_ref.shape[0]
    start = 0
    for n, ref in enumerate(weight_refs):
        if n == before:
            pack_ref[:, :, start : start + LANES] = small_ref[...]
            start += LANES
        wide = ref.shape[1] // groups
        for group in range(groups):
            pack_ref[group, :, start : start + wide] = ref[
                :, group * wide : (group + 1) * wide
            ].astype(bf16)
        start += wide
    swap_send, swap_recv, swap_own = sems[:3]
    token_sems, cotangent_sems = sems[9:16], sems[16:23]
    me, near, far, cross = partners()
    sources = (me, near, far, cross)
    line = Line(lambda kind, blk: pack_all.at[blk, sources[kind]], 4, sems[3:9])
    here = lax.axis_index("blk")
    line.greet([on_head(near), on_head(far), on_head(cross)])
    swaps = [pltpu.make_async_copy(pack_ref.at[me], pack_all.at[here, me], swap_own)]
    for kind, other in enumerate((near, far, cross)):
        swaps.append(
            remote(
                pack_ref.at[other],
                pack_all.at[here, me],
                swap_send.at[kind],
                swap_recv.at[kind],
                on_head(other),
            )
        )
    for swap in swaps:
        swap.start()
    size = tokens_ref.shape[0]
    span = size // PIECES

    def spread_all(ref, all_ref, some, slots):
        return [
            spread_piece(ref.at[pl.ds(piece * span, span), :], all_ref, size, some, piece, slots)
            for piece in range(PIECES)
        ]

    by_device, crossing = Slots(True), Slots(False)
    tokens_sent = spread_all(tokens_ref, tokens_all, token_sems, by_device)
    swaps[0].wait()
    line.launch(0)
    for kind, source in enumerate((near, far, cross)):
        block = pack_all.at[here, source]
        remote(
            block, block, swap_send.at[kind], swap_recv.at[kind], on_head(source)
        ).wait_recv()
        line.launch(kind + 1)
    cotangent_sent = spread_all(cotangent_ref, cotangent_all, cotangent_sems, crossing)
    for t in range(1, line.half):
        line.step(t)
        if t == min(2, line.half - 1):
            finish_tokens = hand_on(tokens_all, size, token_sems, tokens_sent, by_device)
    finish_cotangent = hand_on(cotangent_all, size, cotangent_sems, cotangent_sent, crossing)
    for swap in swaps[1:]:
        swap.wait_send()
    line.finish()
    finish_tokens()
    finish_cotangent()


def gather_first(before, small, after, tokens, cotangent, number):
    groups, share, _ = small.shape
    weights = [*before, *after]
    columns = LANES + sum(weight.shape[1] // groups for weight in weights)
    peers = lax.axis_size("blk")
    rows, width = tokens.shape
    whole = jax.ShapeDtypeStruct((groups * rows, width), bf16)
    vmem, anywhere = pl.BlockSpec(memory_space=pltpu.VMEM), pl.BlockSpec(memory_space=pl.ANY)
    all_pack, all_tokens, all_cotangent = pl.pallas_call(
        functools.partial(gather_first_kernel, len(before), len(after)),
        in_specs=[vmem] * (3 + len(weights)),
        out_specs=[anywhere] * 3,
        out_shape=[jax.ShapeDtypeStruct((peers, groups, share, columns), bf16), whole, whole],
        scratch_shapes=[
            pltpu.VMEM((groups, share, columns), bf16),
            pltpu.SemaphoreType.DMA((3,)),
            pltpu.SemaphoreType.DMA((3,)),
            pltpu.SemaphoreType.DMA,
        ]
        + [pltpu.SemaphoreType.DMA((4, peers // 2)) for _ in range(6)]
        + gather_sems()
        + gather_sems(),
        compiler_params=pltpu.CompilerParams(collective_id=number, has_side_effects=True),
        cost_estimate=pl.CostEstimate(
            flops=70_000_000_000, transcendentals=0, bytes_accessed=30_000_000
        ),
        name="gather_first",
    )(small, *weights, tokens, cotangent)
    return all_pack.reshape(peers * groups * share, columns), all_tokens, all_cotangent


class Sum:
    def __init__(self, part_ref, buffers, sems, size, by_device):
        self.part_ref, self.size, self.span = part_ref, size, size // PIECES
        self.slots = Slots(by_device)
        self.near_buf, self.turn_buf, self.far_buf = buffers
        self.near_send, self.near_recv, self.far_send, self.far_recv = sems
        self.near_copies, self.far_copies = [], []

    def piece(self, n):
        return slice(n * self.span, (n + 1) * self.span)

    def start(self):
        me, near, far, cross = partners()
        for which, shard in ((0, self.slots.cross), (1, self.slots.near)):
            for n in range(PIECES):
                copy = remote(
                    piece_at(self.part_ref, shard, n, self.size),
                    self.near_buf.at[which, pl.ds(n * self.span, self.span), :],
                    self.near_send.at[which, n],
                    self.near_recv.at[which, n],
                    on_head(near),
                )
                copy.start()
                self.near_copies.append(copy)

    def turn(self):
        me, near, far, cross = partners()
        for n in range(PIECES):
            here = self.piece(n)
            self.near_copies[n].wait_recv()
            self.turn_buf[here, :] = (
                piece_at(self.part_ref, self.slots.far, n, self.size)[...].astype(f32)
                + self.near_buf[0, here, :].astype(f32)
            ).astype(bf16)
            copy = remote(
                self.turn_buf.at[pl.ds(n * self.span, self.span), :],
                self.far_buf.at[pl.ds(n * self.span, self.span), :],
                self.far_send.at[n],
                self.far_recv.at[n],
                on_head(far),
            )
            copy.start()
            self.far_copies.append(copy)

    def total(self, n):
        self.near_copies[PIECES + n].wait_recv()
        self.far_copies[n].wait_recv()
        here = self.piece(n)
        return (
            piece_at(self.part_ref, self.slots.own, n, self.size)[...].astype(f32)
            + self.near_buf[1, here, :].astype(f32)
            + self.far_buf[here, :].astype(f32)
        )

    def finish(self):
        for copy in self.near_copies + self.far_copies:
            copy.wait_send()


def sum_buffers(size, width):
    return [
        pltpu.VMEM((2, size, width), bf16),
        pltpu.VMEM((size, width), bf16),
        pltpu.VMEM((size, width), bf16),
    ]


def sum_sems():
    return [
        pltpu.SemaphoreType.DMA((2, PIECES)),
        pltpu.SemaphoreType.DMA((2, PIECES)),
        pltpu.SemaphoreType.DMA((PIECES,)),
        pltpu.SemaphoreType.DMA((PIECES,)),
    ]


def exchange_kernel(local, extras, summed, weights, *refs):
    part_ref, extra_refs = refs[0], refs[1 : 1 + extras]
    refs = refs[1 + extras :]
    if weights:
        mine_ref, refs = refs[0], refs[1:]
    out_ref, all_ref, refs = refs[0], refs[1], refs[2:]
    if weights:
        weight_ref, refs = refs[0], refs[1:]
    payload, sems = refs[0], refs[1:]
    size = out_ref.shape[0]
    span = size // PIECES
    _, near, far, _ = partners()
    if weights:
        kinds = mine_ref.shape[0]
        line = Line(lambda kind, blk: weight_ref.at[blk, kind], kinds, sems[-7:-1])
        own = pltpu.make_async_copy(mine_ref, weight_ref.at[lax.axis_index("blk")], sems[-1])
        own.start()
        line.greet([on_head(near), on_head(far)])
    else:
        greet([on_head(near), on_head(far)])
    slots = Slots(summed)
    if not summed:
        shares = Sum(part_ref, sems[7:10], sems[10:14], size, True)
        shares.start()
    if weights:
        own.wait()
        for kind in range(kinds):
            line.launch(kind)
    if not summed:
        shares.turn()
    sent = []
    for piece in range(PIECES):
        if weights and piece != 2:
            hop = {0: 1, 1: 2, 3: 3}[piece]
            for t in range(hop, line.half if piece == 3 else min(hop + 1, line.half)):
                line.step(t)
        here = slice(piece * span, (piece + 1) * span)
        total = part_ref[here, :] if summed else shares.total(piece)
        result, share = local(total, here, *extra_refs)
        out_ref[here, :] = result.astype(out_ref.dtype)
        payload[here, :] = share.astype(bf16)
        source = payload.at[pl.ds(piece * span, span), :]
        sent.append(spread_piece(source, all_ref, size, sems[:7], piece, slots))
    hand_on(all_ref, size, sems[:7], sent, slots)()
    if not summed:
        shares.finish()
    if weights:
        line.finish()


def exchange(local, part, extras, summed, number, name, mine=None):
    rows, width = part.shape
    size = rows if summed else rows // 4
    vmem, anywhere = pl.BlockSpec(memory_space=pltpu.VMEM), pl.BlockSpec(memory_space=pl.ANY)
    weights = mine is not None
    inputs = [part, *extras]
    out_specs = [vmem, anywhere]
    out_shape = [
        jax.ShapeDtypeStruct((size, width), f32),
        jax.ShapeDtypeStruct((4 * size, width), bf16),
    ]
    scratch = [pltpu.VMEM((size, width), bf16)] + gather_sems()
    if not summed:
        scratch += sum_buffers(size, width) + sum_sems()
    if weights:
        peers = lax.axis_size("blk")
        inputs.append(mine)
        out_specs.append(anywhere)
        out_shape.append(jax.ShapeDtypeStruct((peers,) + mine.shape, bf16))
        scratch += [pltpu.SemaphoreType.DMA((mine.shape[0], peers // 2)) for _ in range(6)]
        scratch.append(pltpu.SemaphoreType.DMA)
    return pl.pallas_call(
        functools.partial(exchange_kernel, local, len(extras), summed, weights),
        in_specs=[vmem] * len(inputs),
        out_specs=out_specs,
        out_shape=out_shape,
        scratch_shapes=scratch,
        compiler_params=pltpu.CompilerParams(collective_id=number, has_side_effects=True),
        cost_estimate=pl.CostEstimate(
            flops=10_000_000_000 if summed else 70_000_000_000,
            transcendentals=0,
            bytes_accessed=16_000_000,
        ),
        name=name,
    )(*inputs)


def column_chunks(width):
    count = max(width // 512, 1)
    first = width - 512 * (count - 1)
    return [(0, first)] + [(first + 512 * n, 512) for n in range(count - 1)]


def finish_last_kernel(grads_ref, weight_ref, grad_ref, output_grad_ref, second_ref,
                       grad_middle_ref, tokens_ref, gain_ref, weights_ref, output_ref,
                       second_out_ref, tokens_grad_ref, first_ref, *refs):
    buffers = (refs[0:3], refs[3:6])
    first_buffers = refs[6:9]
    pair_send, pair_recv, line_send, line_recv, swap_send, swap_recv = refs[9:15]
    first_sems = refs[15:19]
    me, near, far, cross = partners()
    others = (near, far, cross)
    here, partner, after = blk_peers()
    steps = len(after)
    greet(
        [on_head(other) for other in others]
        + [on_blk(partner)]
        + [on_blk(peer) for peer in after[1:]]
    )
    size = tokens_grad_ref.shape[0]
    first = Sum(first_ref, first_buffers, first_sems, size, True)
    chunks = []
    for ref, out_ref, some in (
        (grad_ref, weights_ref, buffers[0]), (output_grad_ref, output_ref, buffers[1])
    ):
        for start, wide in column_chunks(ref.shape[3]):
            chunks.append((ref, out_ref, some, pl.ds(start, wide)))
    groups = grad_ref.shape[1]
    sent = []
    for c, (ref, _, (pair_buf, _, _), at) in enumerate(chunks):
        for t in list(range(1, steps)) + [0]:
            copy = remote(
                ref.at[after[t] + partner - here, :, :, at],
                pair_buf.at[t, :, :, at],
                pair_send.at[c, t],
                pair_recv.at[c, t],
                on_blk(partner),
            )
            copy.start()
            sent.append(copy)

    def swap(source_ref, out_ref, c):
        for kind, other in enumerate(others):
            copy = remote(
                source_ref.at[other], out_ref.at[me], swap_send.at[c, kind],
                swap_recv.at[c, kind], on_head(other),
            )
            copy.start()
            sent.append(copy)

    swap(second_ref, second_out_ref, len(chunks))

    def add_up(c):
        ref, out_ref, (pair_buf, line_buf, row_buf), at = chunks[c]
        block = pair_buf.at[0, :, :, at]
        remote(block, block, pair_send.at[c, 0], pair_recv.at[c, 0], on_blk(partner)).wait_recv()
        for t in range(1, steps):
            block = line_buf.at[t, :, :, at]
            remote(
                block, block, line_send.at[c, t], line_recv.at[c, t], on_blk(after[t])
            ).wait_recv()

        def add_all(group, carry):
            total = ref[here, group, :, at].astype(f32) + pair_buf[0, group, :, at].astype(f32)
            for t in range(1, steps):
                total = total + line_buf[t, group, :, at].astype(f32)
            row_buf[group, :, at] = total.astype(bf16)
            return carry

        lax.fori_loop(0, groups, add_all, 0)
        out_ref[me, :, at] = row_buf[me, :, at]
        swap(row_buf.at[:, :, at], out_ref.at[:, :, at], c)

    across = grads_ref.shape[1]
    tiles = first_ref.shape[0] // 256

    def multiply(n, carry):
        rows = tile_of(n, 256)
        first_ref[rows, :] = dot(grads_ref[rows, :], weight_ref[:, :across], NT).astype(bf16)
        return carry

    lax.fori_loop(0, tiles // 2, multiply, 0)
    for c, (ref, _, (pair_buf, line_buf, _), at) in enumerate(chunks):
        for t in range(1, steps):
            block = pair_buf.at[t, :, :, at]
            remote(
                block, block, pair_send.at[c, t], pair_recv.at[c, t], on_blk(partner)
            ).wait_recv()

            def add(group, carry):
                pair_buf[t, group, :, at] = (
                    ref[after[t], group, :, at].astype(f32)
                    + pair_buf[t, group, :, at].astype(f32)
                ).astype(bf16)
                return carry

            lax.fori_loop(0, groups, add, 0)
            copy = remote(
                block, line_buf.at[t, :, :, at], line_send.at[c, t], line_recv.at[c, t],
                on_blk(after[t]),
            )
            copy.start()
            sent.append(copy)
        if c == 0:
            lax.fori_loop(tiles // 2, tiles, multiply, 0)
            first.start()
        else:
            if c == 1:
                first.turn()
            add_up(c - 1)
    for piece in range(PIECES):
        rows = first.piece(piece)
        tokens_grad_ref[rows, :], _ = after_first(
            first.total(piece), rows, grad_middle_ref, tokens_ref, gain_ref
        )
    add_up(len(chunks) - 1)
    second_out_ref[me] = second_ref[me]
    for c in range(len(chunks) + 1):
        if c < len(chunks):
            _, out_ref, _, at = chunks[c]
            out_ref = out_ref.at[:, :, at]
        else:
            out_ref = second_out_ref
        for kind, other in enumerate(others):
            block = out_ref.at[other]
            remote(
                block, block, swap_send.at[c, kind], swap_recv.at[c, kind], on_head(other)
            ).wait_recv()
    for copy in sent:
        copy.wait_send()
    first.finish()


def finish_last(grads, first, grad, output_grad, second, groups, grad_middle, tokens, gain, number):
    peers = lax.axis_size("blk")
    share = grad.shape[0] // (peers * groups)
    rows, width = tokens.shape
    vmem = pl.BlockSpec(memory_space=pltpu.VMEM)
    half = peers // 2
    widths = (grad.shape[1], output_grad.shape[1])
    chunks = sum(len(column_chunks(width)) for width in widths)

    def blocks(columns):
        return [pltpu.VMEM((half, groups, share, columns), bf16) for _ in range(2)] + [
            pltpu.VMEM((groups, share, columns), bf16)
        ]

    return pl.pallas_call(
        finish_last_kernel,
        in_specs=[vmem] * 8,
        out_specs=[vmem] * 4,
        out_shape=[
            jax.ShapeDtypeStruct((groups, share, columns), bf16)
            for columns in widths + (second.shape[1],)
        ]
        + [jax.ShapeDtypeStruct((rows, width), f32)],
        scratch_shapes=[pltpu.VMEM((4 * rows, width), bf16)]
        + blocks(widths[0])
        + blocks(widths[1])
        + sum_buffers(rows, width)
        + [pltpu.SemaphoreType.DMA((chunks, half)) for _ in range(4)]
        + [pltpu.SemaphoreType.DMA((chunks + 1, 3)) for _ in range(2)]
        + sum_sems(),
        compiler_params=pltpu.CompilerParams(
            collective_id=number, has_side_effects=True, vmem_limit_bytes=60 << 20
        ),
        cost_estimate=pl.CostEstimate(
            flops=80_000_000_000, transcendentals=0, bytes_accessed=40_000_000
        ),
        name="finish_last",
    )(
        grads,
        first,
        grad.reshape(peers, groups, share, widths[0]),
        output_grad.reshape(peers, groups, share, widths[1]),
        second.reshape(groups, share, second.shape[1]),
        grad_middle, tokens, gain,
    )


def inverse_rms(value):
    return lax.rsqrt(jnp.mean(value * value, axis=1, keepdims=True) + epsilon)


def through_norm(grad, value):
    factor = inverse_rms(value)
    normed = value * factor
    return factor * (grad - normed * jnp.mean(grad * normed, axis=1, keepdims=True))


def after_attention(total, here, tokens_ref, gain_ref):
    middle = tokens_ref[here, :].astype(f32) + total
    return middle, middle * inverse_rms(middle) * gain_ref[0:1, :]


def after_hidden(total, here, cotangent_ref, middle_ref, gain_ref):
    grad = cotangent_ref[here, :].astype(f32) + through_norm(
        total * gain_ref[0:1, :], middle_ref[here, :]
    )
    return grad, grad


def after_first(total, here, grad_ref, tokens_ref, gain_ref):
    grad = grad_ref[here, :] + through_norm(
        total * gain_ref[0:1, :], tokens_ref[here, :].astype(f32)
    )
    return grad, None


FEED_TILE = 256
FEED_COLUMNS = 1024


def feed_kernel(input_ref, cotangent_ref, weight_ref, down_weight_ref, down_ref, grad_ref, total_ref,
                acts, turned0, turned1, stage, near_buf, far_buf, near_send, near_recv, far_send, far_recv):
    step = pl.program_id(0)
    hidden_width = down_weight_ref.shape[1]
    size = total_ref.shape[0]
    per = size // FEED_TILE
    tiles = 4 * per
    _, near, far, _ = partners()

    @pl.when(step == 0)
    def _():
        greet([on_head(near), on_head(far)])

    def to_near(which, piece):
        return remote(
            stage.at[which * per + piece],
            near_buf.at[which, piece],
            near_send.at[which, piece],
            near_recv.at[which, piece],
            on_head(near),
        )

    def to_far(piece):
        return remote(
            near_buf.at[0, piece], far_buf.at[piece], far_send.at[piece], far_recv.at[piece],
            on_head(far),
        )

    @pl.when(step < tiles)
    def _():
        here = tile_of(step, FEED_TILE)
        inputs, cotangent = input_ref[...], cotangent_ref[...]
        turned0[:, here] = inputs.T
        turned1[:, here] = cotangent.T
        gate_at, up_at, down_at = (
            slice(n * hidden_width, (n + 1) * hidden_width) for n in range(3)
        )
        gate = dot(inputs, weight_ref[:, gate_at])
        up = dot(inputs, weight_ref[:, up_at])
        grad_hidden = dot(cotangent, down_weight_ref[...])
        opening = 0.5 * jnp.tanh(0.5 * gate) + 0.5
        active = gate * opening
        hidden = (active * up).astype(bf16)
        grad_gate = (grad_hidden * up * opening * (1.0 + gate * (1.0 - opening))).astype(bf16)
        grad_up = (grad_hidden * active).astype(bf16)
        acts[here, gate_at] = grad_gate
        acts[here, up_at] = grad_up
        acts[here, down_at] = hidden
        down_ref[...] = dot(hidden, down_weight_ref[...], NT).astype(bf16)
        back = dot(grad_gate, weight_ref[:, gate_at], NT) + dot(
            grad_up, weight_ref[:, up_at], NT
        )
        for piece in range(per):
            for which, first in ((0, 0), (1, 2 * per)):

                @pl.when(step == first + piece)
                def _():
                    stage[which * per + piece] = back.astype(bf16)
                    to_near(which, piece).start()

            @pl.when(step == per + piece)
            def _():
                to_near(0, piece).wait_recv()
                near_buf[0, piece] = (back + near_buf[0, piece].astype(f32)).astype(bf16)
                to_far(piece).start()

            @pl.when(step == 3 * per + piece)
            def _():
                total_ref[piece * FEED_TILE : (piece + 1) * FEED_TILE, :] = back

    @pl.when(step >= tiles)
    def _():
        at = tile_of(step - tiles, FEED_COLUMNS)
        from_input = (step - tiles) * FEED_COLUMNS < 2 * hidden_width

        @pl.when(from_input)
        def _():
            grad_ref[...] = dot(turned0[...], acts[:, at]).astype(bf16)

        @pl.when(jnp.logical_not(from_input))
        def _():
            grad_ref[...] = dot(turned1[...], acts[:, at]).astype(bf16)

    @pl.when(step == pl.num_programs(0) - 1)
    def _():
        for piece in range(per):
            here = slice(piece * FEED_TILE, (piece + 1) * FEED_TILE)
            to_near(1, piece).wait_recv()
            to_far(piece).wait_recv()
            total_ref[here, :] += near_buf[1, piece].astype(f32) + far_buf[piece].astype(f32)
            to_near(0, piece).wait_send()
            to_near(1, piece).wait_send()
            to_far(piece).wait_send()


def feed(inputs, cotangent, weight, down_weight, number):
    rows, width = inputs.shape
    columns = weight.shape[1] + down_weight.shape[1]
    size = rows // 4
    tiles, per = rows // FEED_TILE, size // FEED_TILE
    tile = pl.BlockSpec((FEED_TILE, width), lambda n: (jnp.minimum(n, tiles - 1), 0))

    def whole(shape):
        return pl.BlockSpec(shape, lambda n: (0, 0), pipeline_mode=pl.Buffered(1))

    return pl.pallas_call(
        feed_kernel,
        grid=(tiles + columns // FEED_COLUMNS,),
        in_specs=[tile, tile, whole(weight.shape), whole(down_weight.shape)],
        out_specs=[
            tile,
            pl.BlockSpec((width, FEED_COLUMNS), lambda n: (0, jnp.maximum(n - tiles, 0))),
            whole((size, width)),
        ],
        out_shape=[
            jax.ShapeDtypeStruct((rows, width), bf16),
            jax.ShapeDtypeStruct((width, columns), bf16),
            jax.ShapeDtypeStruct((size, width), f32),
        ],
        scratch_shapes=[
            pltpu.VMEM((rows, columns), bf16),
            pltpu.VMEM((width, rows), bf16),
            pltpu.VMEM((width, rows), bf16),
            pltpu.VMEM((2 * per, FEED_TILE, width), bf16),
            pltpu.VMEM((2, per, FEED_TILE, width), bf16),
            pltpu.VMEM((per, FEED_TILE, width), bf16),
            pltpu.SemaphoreType.DMA((2, per)),
            pltpu.SemaphoreType.DMA((2, per)),
            pltpu.SemaphoreType.DMA((per,)),
            pltpu.SemaphoreType.DMA((per,)),
        ],
        compiler_params=pltpu.CompilerParams(
            collective_id=number, has_side_effects=True, vmem_limit_bytes=63 << 20
        ),
        cost_estimate=pl.CostEstimate(
            flops=6 * rows * width * columns, transcendentals=rows * columns // 3,
            bytes_accessed=45_000_000,
        ),
        name="feed",
    )(inputs, cotangent, weight, down_weight)


def over_tokens(operand, other_side):
    return lax.dot_general(
        operand, other_side, (((0,), (0,)), ((), ())), preferred_element_type=f32
    )


def sent_columns(pieces, groups):
    packed = jnp.concatenate(
        [piece.reshape(piece.shape[0], groups, -1) for piece in pieces], axis=2
    )
    mine = lax.all_to_all(packed, "head", split_axis=1, concat_axis=0, tiled=True)
    return mine.reshape(mine.shape[0], mine.shape[2])


def all_rows(mine):
    return lax.all_gather(mine, "blk", axis=0, tiled=True)


def row_sums(grad):
    return lax.psum_scatter(grad, "blk", scatter_dimension=0, tiled=True)


def crossing_sum(part):
    cross, far, near, own = (piece.astype(f32) for piece in jnp.split(part, 4))
    members = range(lax.axis_size("head"))
    got = lax.ppermute(
        jnp.concatenate([cross, near]).astype(bf16), "head",
        [(n, n + 1 - 2 * (n % 2)) for n in members],
    )
    of_far, of_own = jnp.split(got.astype(f32), 2)
    back = lax.ppermute(
        (far + of_far).astype(bf16), "head", [(n, (n + 2) % 4) for n in members]
    )
    return own + of_own + back.astype(f32)


def body(
    tokens,
    segment,
    norm1_gain,
    w_query,
    w_key,
    w_value,
    w_gate_out,
    w_forget,
    forget_bias,
    w_output,
    norm2_gain,
    w_gate,
    w_up,
    w_down,
    cotangent,
):
    token_rows, model_width = tokens.shape
    groups = lax.axis_size("head")
    head_count = forget_bias.shape[0]
    local_heads = head_count // groups
    local_width = model_width // groups
    hidden_width = w_gate.shape[1] // groups
    rows = token_rows * groups
    share = w_query.shape[0]
    group = lax.axis_index("head")

    low = lambda array: array.astype(bf16)
    spread = lambda gain: jnp.broadcast_to(low(gain)[:, None, None], (share, groups, 1))
    forget_low = low(w_forget).reshape(share, groups, local_heads)
    rest = LANES - local_heads - 2
    small = jnp.concatenate(
        [forget_low, spread(norm1_gain), spread(norm2_gain), jnp.zeros((share, groups, rest), bf16)],
        axis=2,
    )
    first, tokens_all, cotangent_all = gather_first(
        (w_key, w_value), jnp.swapaxes(small, 0, 1), (w_query, w_gate_out, w_output), tokens,
        cotangent, 0,
    )
    kv_width = 2 * local_width + LANES
    output_weight = first[:, kv_width + 2 * local_width :]

    def gain_rows(column):
        gain = first[:, 2 * local_width + local_heads + column].astype(f32)
        return jnp.broadcast_to(gain[None, :], (8, model_width))

    gain1, gain2 = gain_rows(0), gain_rows(1)
    bias = lax.dynamic_slice_in_dim(forget_bias, group * local_heads, local_heads, 0)
    bias = jnp.broadcast_to(jnp.pad(bias, (0, LANES - local_heads))[None, :], (8, LANES))
    input1, key_value, terms, turned_terms, forget = project(
        tokens_all, gain1, first, bias, 2 * local_width, local_heads
    )
    earlier_kv = passed_along(key_value, "blk", 1)
    earlier_terms = passed_along(turned_terms, "blk", 1)
    query_gate = lax.optimization_barrier(
        dot(input1, first[:, kv_width : kv_width + 2 * local_width])
    )
    query, gate_raw = query_gate[:, :local_width].astype(bf16), query_gate[:, local_width:]

    segment_plus = segment + 1
    earlier_segment = passed_along(segment_plus, "blk", 1)
    window = jnp.concatenate([earlier_segment, segment_plus])
    begins = jnp.sum(
        (window[:, None] < segment_plus[None, :]).astype(jnp.int32), axis=0
    )
    tiles = begins.reshape(rows // Q_TILE, Q_TILE)
    ranges = jnp.stack([tiles[:, 0] // K_TILE, (tiles[:, -1] + K_TILE - 1) // K_TILE])
    begins = jnp.broadcast_to(begins[None, :], (8, rows))

    so_far = attend(True, ranges, query, key_value, terms, terms, begins, local_heads)
    later = lax.optimization_barrier((w_gate, w_up, w_down, key_value))
    mine = sent_columns([low(weight) for weight in later[:3]], groups)
    mine, earlier_kv, earlier_terms, so_far, gate_raw = lax.optimization_barrier(
        (mine, earlier_kv, earlier_terms, so_far, gate_raw)
    )
    down_weight = all_rows(mine[:, 2 * hidden_width :])
    mine_second = mine[:, : 2 * hidden_width].reshape(groups, share, 2 * hidden_width)
    attended, lse = attend(
        False, ranges, query, earlier_kv, terms, earlier_terms, begins, local_heads, so_far
    )
    opened = jax.nn.sigmoid(gate_raw)
    attended_wide = attended.astype(f32)
    gated = (opened * attended_wide).astype(bf16)
    branch = dot(gated, output_weight, NT).astype(bf16)
    middle, input2, second = exchange(
        after_attention, branch, [tokens, gain2], False, 1, "exchange_middle", mine_second
    )
    second = second.reshape(model_width, 2 * hidden_width)
    down, second_grad, grad_input2 = feed(input2, cotangent_all, second, down_weight, 4)
    second_part = row_sums(second_grad)
    grad_middle, grad_branch = exchange(
        after_hidden, grad_input2, [cotangent, middle, gain2], True, 2, "exchange_hidden"
    )

    down, grad_branch = lax.optimization_barrier((down, grad_branch))
    result = (middle + crossing_sum(down)).astype(bf16)
    grad_gated = dot(grad_branch, output_weight)
    grad_attended = (grad_gated * opened).astype(bf16)
    grad_gate_pre = (grad_gated * attended_wide * opened * (1.0 - opened)).astype(bf16)
    dq_prev, rows_prev, dkv_prev, decay_prev = attend_back(
        False, ranges, query, earlier_kv, terms, earlier_terms, begins, grad_attended, attended,
        lse, local_heads,
    )
    dkv_later = passed_along(dkv_prev, "blk", -1)
    decay_later = passed_along(decay_prev[:, :8], "blk", -1)
    decay_later = jnp.pad(decay_later, ((0, 0), (0, LANES - 8)))
    dq, dk_own, dv_own, decay_own = attend_back(
        True, ranges, query, key_value, terms, terms, begins, grad_attended, attended,
        lse, local_heads, (dq_prev, rows_prev),
    )
    dk = (dk_own + dkv_later[0].astype(f32)).astype(bf16)
    dv = (dv_own + dkv_later[1].astype(f32)).astype(bf16)
    logf_grad = decay_back(decay_own, decay_later)
    forget_grad = jnp.where(
        jnp.arange(LANES)[None, :] < local_heads, logf_grad * jax.nn.sigmoid(-forget), 0.0
    ).astype(bf16)
    grads = jnp.concatenate([dk, dv, forget_grad, dq, grad_gate_pre], axis=1)
    first_grad = over_tokens(input1, grads)
    bias_part = jnp.sum(forget_grad.astype(f32), axis=0)
    row = jnp.arange(model_width)[:, None] % share
    column = jnp.arange(kv_width + 2 * local_width)[None, :]
    spread_bias = jnp.sum(
        jnp.where(row == jnp.arange(LANES)[None, :], bias_part[None, :], 0.0), axis=1, keepdims=True
    )
    first_grad = jnp.where(
        column == 2 * local_width + local_heads, spread_bias, first_grad
    ).astype(bf16)
    output_grad = over_tokens(grad_branch, gated).astype(bf16)
    first_sum, output_sum, second_sum, tokens_grad = finish_last(
        grads, first, first_grad, output_grad, second_part, groups, grad_middle, tokens, gain1, 3
    )
    first_sum, output_sum, second_sum = (
        jnp.swapaxes(array, 0, 1).astype(f32) for array in (first_sum, output_sum, second_sum)
    )

    def columns(array, start, width):
        return array[:, :, start : start + width].reshape(share, groups * width)

    key_sum, value_sum = (columns(first_sum, n * local_width, local_width) for n in range(2))
    forget_sum = columns(first_sum, 2 * local_width, local_heads)
    bias_total = first_sum[:local_heads, :, 2 * local_width + local_heads].T.reshape(head_count)
    query_sum, gate_out_sum = (
        columns(first_sum, kv_width + n * local_width, local_width) for n in range(2)
    )
    output_total = columns(output_sum, 0, local_width)
    gate_sum, up_sum, down_sum = (
        columns(second_sum, n * hidden_width, hidden_width) for n in range(3)
    )

    def along(weight, grad):
        return jnp.sum(low(weight).astype(f32) * grad, axis=1)

    gain1_total = (
        along(w_query, query_sum)
        + along(w_key, key_sum)
        + along(w_value, value_sum)
        + along(w_gate_out, gate_out_sum)
        + along(w_forget, forget_sum)
    ) / low(norm1_gain).astype(f32)
    gain2_total = (along(w_gate, gate_sum) + along(w_up, up_sum)) / low(norm2_gain).astype(f32)
    return (
        result,
        tokens_grad,
        gain1_total,
        query_sum,
        key_sum,
        value_sum,
        gate_out_sum,
        forget_sum,
        bias_total,
        output_total,
        gain2_total,
        gate_sum,
        up_sum,
        down_sum,
    )


def solution(mesh):
    both = ("blk", "head")
    matrix, vector = P(both, None), P(both)
    return jax.shard_map(
        body,
        mesh=mesh,
        in_specs=(
            matrix, P("blk"), vector, matrix, matrix, matrix, matrix, matrix, P(), matrix, vector,
            matrix, matrix, matrix, matrix,
        ),
        out_specs=(
            matrix, matrix, vector, matrix, matrix, matrix, matrix, matrix, P(), matrix, vector,
            matrix, matrix, matrix,
        ),
        check_vma=False,
    )
```
